128 devices in a mesh: row: 16 (over z, x_lo, core), col: 8 (over y, x_hi).
Axes of the slice: x: 4 (x_hi: 2, x_lo: 2; x = x_hi * 2 + x_lo), y: 4, z: 4, core: 2. Of those that a mesh axis runs over, the one named last changes fastest.
Arguments:
- stored: float32 [16, 16, 8, 2, 128, 128], P('col', 'row'), may hold values from -1.2 to 1.2
- tile_rows: int32 [16, 8], replicated, may hold values from 0 to 63, as said below
- offsets: int32 [16, 16, 2], replicated, may hold values from 0 to 63, as said below
- kept_rows: int32 [16, 16, 32], P('col', 'row'), may hold values from 0 to 63, as said below
- kept_cols: int32 [16, 16, 32], P('col', 'row'), may hold values from 0 to 63, as said below
- kept_count: int32 [16, 16], P('col', 'row'), may hold values from 8 to 32, as said below
Outputs:
- kept_blocks: float32 [16, 16, 32, 128, 128], P('col', 'row')
The draws below stay inside these ranges and needn't reach their ends.
Inputs may be any that keep to these rules, and one draw needn't show every extreme that they name: Every list is increasing and is the set of block rows a with (a AND m) equal to one value of the grid row, for one bit mask m with log2(8) bits set, the same for all grid rows; the tiles of grid column Y have their occupied block columns in tile_rows[Y]. A XOR offsets[X, Y, r] lies in tile_rows[Y] for every a in tile_rows[X]. `kept_rows`: within a tile the kept (row, column) pairs are distinct; rows lie in tile_rows[I] and columns in tile_rows[J], also in slots past the count. `kept_cols`: paired with kept_rows slot by slot. `kept_count`: tiles whose grid row and column differ by at most one, cyclically, keep 32 blocks.
All inputs are finite; a program needn't handle non-finite values.
Results may differ from the reference program's by a relative error of at most 0.0003.
Values sent between devices are 32-bit elements; how exact they have to be, the bound alone decides.
A program may use at most 192 MiB of HBM per device.

```python
import jax
import jax.numpy as jnp
from jax import lax

BS = 128
TB = 64
ACTIVE = 8
HALF = 2
KEPT = 32
GRID = 16


def layout(key):
    key_mask, key_rows, key_offsets, key_kept, key_count = jax.random.split(jax.random.fold_in(key, 11), 5)
    log_tile = TB.bit_length() - 1
    zero_bits = log_tile - (ACTIVE.bit_length() - 1)
    bit_order = jax.random.permutation(key_mask, log_tile)[:zero_bits].astype(jnp.int32)
    zero_mask = jnp.sum(jnp.left_shift(jnp.int32(1), bit_order)).astype(jnp.int32)
    parity = jnp.bitwise_and(jax.random.randint(key_rows, (GRID,), 0, TB, dtype=jnp.int32), zero_mask)
    parity = parity.at[0].set(zero_mask).at[1].set(0)
    all_rows = jnp.arange(TB, dtype=jnp.int32)
    member = jnp.bitwise_and(all_rows[None, :], zero_mask) == parity[:, None]
    scores = jnp.where(member, all_rows[None, :], all_rows[None, :] + TB)
    tile_rows = jnp.argsort(scores, axis=1, stable=True)[:, :ACTIVE].astype(jnp.int32)
    raw_offsets = jax.random.randint(key_offsets, (GRID, GRID, HALF), 0, TB, dtype=jnp.int32)
    parity_diff = jnp.bitwise_xor(parity[:, None], parity[None, :])[:, :, None]
    free_mask = jnp.bitwise_xor(jnp.int32(TB - 1), zero_mask)
    offsets = jnp.bitwise_or(jnp.bitwise_and(raw_offsets, free_mask), parity_diff)
    offsets = offsets.at[0, 1, 0].set(TB - 1).at[0, 0, 0].set(0).astype(jnp.int32)
    cells = ACTIVE * ACTIVE
    kept_scores = jax.random.randint(key_kept, (GRID, GRID, cells), 0, 2 ** 20, dtype=jnp.int32) * cells
    kept_scores = kept_scores + jnp.arange(cells, dtype=jnp.int32)
    chosen = jnp.argsort(kept_scores, axis=-1, stable=True)[..., :KEPT].astype(jnp.int32)
    row_pick = chosen // ACTIVE
    col_pick = chosen % ACTIVE
    grid_index = jnp.arange(GRID, dtype=jnp.int32)
    kept_rows = tile_rows[grid_index[:, None, None], row_pick].astype(jnp.int32)
    kept_cols = tile_rows[grid_index[None, :, None], col_pick].astype(jnp.int32)
    counts = jax.random.randint(key_count, (GRID, GRID), KEPT // 4, KEPT + 1, dtype=jnp.int32)
    distance = (grid_index[:, None] - grid_index[None, :]) % GRID
    is_near = (distance <= 1) | (distance >= GRID - 1)
    counts = jnp.where(is_near, KEPT, counts).astype(jnp.int32)
    return (tile_rows, offsets, kept_rows, kept_cols, counts)


def draw_tile_rows(key, part):
    return layout(key)[0]


def draw_offsets(key, part):
    return layout(key)[1]


def draw_kept_rows(key, part):
    return layout(key)[2]


def draw_kept_cols(key, part):
    return layout(key)[3]


def draw_kept_count(key, part):
    return layout(key)[4]


def shard_levels(own_key, extent, cuts, smallest, largest):
    loudness, own = 1.0, jax.random.fold_in(own_key, 6)
    for dim, parts in cuts:
        heights = jnp.exp(jax.random.uniform(jax.random.fold_in(own, dim), (parts,), jnp.float32, smallest / len(cuts), largest / len(cuts)))
        loudness = loudness * jnp.repeat(heights, extent[dim] // parts).reshape([-1 if axis == dim else 1 for axis in range(len(extent))])
    return loudness


def centred(stream_key, shape, width, reach, cuts=(), kind=jnp.bfloat16):
    gain = shard_levels(stream_key, shape, cuts, -0.22, 0.18) if cuts else 1.0
    array = jax.random.normal(stream_key, shape, jnp.float32) * width * gain
    return jnp.minimum(jnp.maximum(array, -reach), reach).astype(kind)


def setup_inputs(seed: int = 0) -> dict:
    key_of = jax.random.split(jax.random.key(seed), 7)
    stored = centred(key_of[0], (GRID, GRID, ACTIVE, HALF, BS, BS), 0.2, 1.2, ((0, 8), (1, 16)), jnp.float32)
    tile_rows = draw_tile_rows(jax.random.fold_in(key_of[6], 71), 0)
    offsets = draw_offsets(jax.random.fold_in(key_of[6], 71), 0)
    kept_rows = draw_kept_rows(jax.random.fold_in(key_of[6], 71), 0)
    kept_cols = draw_kept_cols(jax.random.fold_in(key_of[6], 71), 0)
    kept_count = draw_kept_count(jax.random.fold_in(key_of[6], 71), 0)
    return {"stored": stored, "tile_rows": tile_rows, "offsets": offsets, "kept_rows": kept_rows, "kept_cols": kept_cols, "kept_count": kept_count}


def rank_in(row_list, lookup_keys):
    positions = jnp.arange(row_list.shape[0], dtype=jnp.int32)
    matches = row_list == lookup_keys[..., None]
    return jnp.sum(jnp.where(matches, positions, 0), -1).astype(jnp.int32)


def tile_cols(tile_rows, offsets, tile_x, tile_y):
    offsets_both = jnp.concatenate([offsets[tile_x, tile_y], offsets[tile_y, tile_x]])
    return jnp.bitwise_xor(tile_rows[tile_x][:, None], offsets_both[None, :])


def assemble(own_half, mirror, tile_rows, offsets, tile_x, tile_y):
    half_slots = own_half.shape[1]
    mirror_rows = jnp.bitwise_xor(tile_rows[tile_x][:, None], offsets[tile_y, tile_x][None, :])
    position = rank_in(tile_rows[tile_y], mirror_rows)
    picked = mirror[position, jnp.arange(half_slots, dtype=jnp.int32)[None, :]]
    return jnp.concatenate([own_half, jnp.swapaxes(picked, -1, -2)], 1)


def lane_terms(vals_a, vals_b, cols_a, cols_b, rows_i, rows_k, want_rows, want_cols, live_count):
    kept_slots = want_rows.shape[0]
    block_size = vals_a.shape[-1]
    is_live = jnp.arange(kept_slots, dtype=jnp.int32) < live_count
    position = rank_in(rows_k, cols_a)
    summed = jnp.zeros((kept_slots, block_size * block_size), jnp.float32)
    for slot in range(vals_a.shape[1]):
        picked = vals_b[position[:, slot]]
        picked_cols = cols_b[position[:, slot]]
        products = jnp.einsum('eij,ebjk->ebik', vals_a[:, slot], picked, precision=lax.Precision.HIGHEST)
        weights = ((rows_i[None, :, None] == want_rows[:, None, None])
                   & (picked_cols[None] == want_cols[:, None, None])
                   & is_live[:, None, None]).astype(jnp.float32)
        summed = summed + jnp.dot(weights.reshape(kept_slots, -1), products.reshape(-1, block_size * block_size),
                                  precision=lax.Precision.HIGHEST)
    return summed.reshape(kept_slots, block_size, block_size)


def reference(stored, tile_rows, offsets, kept_rows, kept_cols, kept_count):
    def entries(tile_x, tile_y):
        return assemble(stored[tile_x, tile_y], stored[tile_y, tile_x], tile_rows, offsets, tile_x, tile_y)

    def one_tile(flat_index):
        tile_i = flat_index // GRID
        tile_j = flat_index % GRID
        summed = jnp.zeros((KEPT, BS, BS), jnp.float32)
        for step_index in range(2):
            tile_k = (tile_i + tile_j + step_index) % GRID
            summed = summed + lane_terms(entries(tile_i, tile_k), entries(tile_k, tile_j),
                                         tile_cols(tile_rows, offsets, tile_i, tile_k),
                                         tile_cols(tile_rows, offsets, tile_k, tile_j),
                                         tile_rows[tile_i], tile_rows[tile_k],
                                         kept_rows[tile_i, tile_j], kept_cols[tile_i, tile_j],
                                         kept_count[tile_i, tile_j])
        return summed

    result = lax.map(one_tile, jnp.arange(GRID * GRID, dtype=jnp.int32))
    return result.reshape(GRID, GRID, KEPT, BS, BS)
```

```python
import jax
import jax.numpy as jnp
import numpy as np
from jax import lax
from jax.experimental import pallas as pl
from jax.experimental.pallas import tpu as pltpu
from jax.sharding import PartitionSpec as P

MESH = pl.DeviceIdType.MESH
CHUNKS = 4
SLOTS = 16
SENDS = [
    [32, 5, 8, 408576, 525313, 525345, 525377, 525409, 656898, 407553, 408608, 656930, 657410, 656962, 657442, 656994, 787971, 407585, 788003, 657474, 408640, 788035, 788067, 407617, 919044, 657506, 919076, 408672, 919108, 407649, 919140, 1865731, 1865763, 1865795, 1865827],
    [36, 4, 9, 655360, 786433, 655392, 786465, 655424, 786497, 655456, 786529, 276480, 918018, 276512, 818178, 1558530, 918050, 788995, 918082, 818210, 918114, 789027, 1558562, 276544, 1558594, 789059, 818242, 789091, 276576, 932865, 818274, 932897, 1558626, 1557505, 932929, 932961, 1557537, 1557569, 1557601],
    [52, 8, 14, 263169, 281090, 281122, 281154, 624640, 802816, 309763, 281186, 263201, 624672, 263233, 263265, 309795, 393216, 393248, 624704, 393280, 309827, 1314308, 802848, 393312, 1314340, 624736, 1314372, 309859, 1314404, 2066949, 802880, 701444, 2067974, 802912, 701476, 2066981, 1576455, 2068006, 701508, 2067013, 1576487, 1721348, 1852423, 1576519, 1721380, 701540, 2068038, 1576551, 2067045, 1852455, 1721412, 2068070, 1852487, 1721444, 1852519],
    [80, 9, 14, 494592, 1050624, 279553, 1181697, 1050656, 1181729, 1050688, 1181761, 1050720, 1181793, 494624, 279585, 1313283, 494656, 699909, 279617, 494688, 279649, 1313315, 699941, 756737, 1313347, 673284, 673316, 756769, 1313379, 673348, 699973, 673380, 933893, 1065478, 1343493, 756801, 1066498, 1343525, 933925, 756833, 1065510, 804868, 1343557, 1066530, 1805315, 835079, 933957, 835111, 804900, 1869320, 830472, 1065542, 831016, 1066562, 804932, 831048, 700005, 933989, 1805347, 804964, 1868840, 835143, 1065574, 1049601, 831080, 1066594, 1616902, 1049633, 1747970, 1868872, 1049665, 1805379, 835175, 1616934, 1049697, 1748002, 1343589, 1805411, 1616966, 1868904, 1748034, 1616998, 1748066],
    [56, 10, 14, 658432, 612867, 1184771, 790018, 658464, 1185315, 1185347, 790050, 1150976, 658496, 612387, 1185379, 1544193, 612419, 1675266, 1151008, 790082, 658528, 1544225, 612451, 1675298, 790114, 1151040, 526337, 526369, 1544257, 526401, 1675330, 1563140, 526433, 1151072, 1676805, 1563172, 1823238, 1676837, 1562119, 1676869, 1693192, 1544289, 1823270, 1563204, 1675362, 1562151, 1676901, 1693224, 1709577, 1709609, 1823302, 1562183, 1709641, 1563236, 1693256, 1709673, 1823334, 1562215, 1693288],
    [52, 9, 14, 294912, 1314816, 365569, 1445889, 1314848, 1445921, 1314880, 1445953, 1314912, 1445985, 365601, 294944, 365633, 365665, 558594, 530950, 558626, 294976, 558658, 295008, 1300995, 558690, 793093, 1344515, 1694212, 530982, 557060, 793125, 531014, 1301027, 1344547, 793157, 531046, 557604, 1693732, 1345091, 1824263, 557636, 1300547, 793189, 1708552, 1345123, 1693764, 557668, 1708584, 1824295, 1708616, 1300579, 1708648, 1693796, 1824327, 1824359],
    [40, 8, 14, 464896, 397313, 464928, 397345, 464960, 397377, 464992, 397409, 1315840, 1989122, 1315872, 925189, 925221, 1645060, 1646086, 794115, 1360901, 794147, 1315904, 794179, 925253, 1645092, 1315936, 1646118, 794211, 1858055, 925285, 1989154, 1858087, 1360933, 1645124, 1646150, 1858119, 1360965, 1645156, 1989186, 1646182, 1858151, 1360997, 1989218],
    [48, 6, 14, 311296, 1054720, 1185793, 1054752, 1185825, 1054784, 1185857, 1054816, 1185889, 465921, 713729, 984578, 465953, 713761, 1446913, 465985, 713793, 459267, 466017, 713825, 1317381, 311328, 311360, 459299, 1317413, 810500, 1383424, 1317445, 810532, 311392, 459331, 1514498, 1446945, 1317477, 810564, 1383456, 459363, 810596, 1515042, 1446977, 1383488, 1515074, 984098, 984130, 1383520, 1447009, 1515106, 984162],
    [44, 7, 14, 466944, 466976, 467008, 467040, 715268, 926724, 927268, 927300, 861185, 714788, 927332, 1434115, 975362, 714820, 1238533, 1189382, 661505, 661537, 975394, 714852, 1238565, 661569, 975426, 1189414, 1238597, 661601, 975458, 1189446, 2025478, 1238629, 1317890, 2025510, 1189478, 1317922, 861217, 2025542, 861249, 1434147, 2025574, 861281, 1317954, 1434179, 1317986, 1434211],
    [44, 7, 14, 925696, 269313, 1056769, 925728, 1056801, 925760, 1056833, 925792, 1056865, 453122, 269345, 453154, 269377, 453186, 269409, 582656, 453218, 582688, 582720, 1830403, 582752, 1108484, 1319430, 860161, 797189, 1830435, 1108516, 1319462, 797221, 1108548, 797253, 1108580, 1319494, 797285, 1319526, 2024454, 1830467, 2024486, 860193, 2024518, 1830499, 860225, 860257, 2024550],
    [36, 7, 14, 271360, 271392, 271424, 271456, 532481, 532513, 667141, 532545, 536067, 532577, 667173, 667205, 1206788, 536099, 1337858, 962054, 536131, 1484800, 536163, 1484832, 1206820, 962086, 1484864, 667237, 1337890, 962118, 1206852, 1337922, 1484896, 1206884, 962150, 1152005, 1152037, 1337954, 1152069, 1152101],
    [40, 4, 14, 927744, 306177, 1058817, 927776, 1058849, 927808, 1058881, 927840, 1058913, 306209, 947715, 1190402, 947747, 1190434, 947779, 1190466, 306241, 625667, 1190498, 306273, 625699, 437248, 437280, 1057793, 437312, 625731, 437344, 947811, 1057825, 1019907, 625763, 1057857, 1485826, 1057889, 1485858, 1019939, 1485890, 1019971, 1020003, 1485922],
    [52, 6, 14, 360448, 438273, 665601, 1601536, 360480, 438305, 686594, 930818, 360512, 665633, 438337, 360544, 438369, 686626, 930850, 1093632, 665665, 686658, 930882, 686690, 930914, 1225219, 1357316, 1995780, 1093664, 1601568, 1225251, 1996324, 1473029, 1324037, 665697, 1356836, 1473061, 1324069, 1093696, 1601600, 1715203, 1225283, 1473093, 1324101, 1357380, 1995844, 1093728, 1715235, 1601632, 1225315, 1715267, 1357412, 1473125, 1324133, 1715299, 1995876],
    [52, 7, 14, 798720, 404481, 929793, 798752, 929825, 798784, 929857, 798816, 929889, 293378, 404513, 1454598, 293410, 404545, 1454630, 293442, 404577, 293474, 556547, 1340416, 753664, 556579, 963585, 540164, 556611, 540196, 540228, 556643, 1210885, 1340448, 963617, 1342468, 1210917, 540260, 753696, 1342500, 1340480, 963649, 1210949, 753728, 1062917, 1342532, 753760, 1342564, 1210981, 963681, 1062949, 1454662, 1062981, 1454694, 1063013, 1340512],
    [24, 4, 12, 275456, 275488, 671234, 275520, 275552, 802307, 274433, 671266, 274465, 274497, 802339, 274529, 671298, 802371, 1164290, 671330, 1426435, 802403, 1164322, 1426467, 1164354, 1426499, 1164386, 1426531],
    [28, 5, 9, 538624, 669697, 538656, 669729, 538688, 669761, 538720, 669793, 406529, 801282, 406561, 801314, 377856, 801346, 377888, 406593, 801378, 377920, 932356, 377952, 406625, 932388, 932420, 1163779, 932452, 1163811, 1163843, 1163875],
    [60, 10, 12, 262144, 396289, 396321, 1328642, 262176, 1328674, 396353, 1328706, 685056, 262208, 1328738, 396385, 685088, 262240, 685120, 1444357, 1445380, 685152, 946691, 1397255, 1444389, 1560578, 1208321, 1445412, 1528328, 946723, 1397287, 1208353, 1528360, 1560610, 946755, 1444421, 1397319, 1208385, 1706505, 1590281, 1528392, 1560642, 946787, 1820672, 1706537, 1590313, 1208417, 1445444, 1472006, 1820704, 1560674, 1397351, 1472038, 1820736, 1706569, 1590345, 1444453, 1820768, 1528424, 1472070, 1445476, 1706601, 1590377, 1472102],
    [64, 10, 15, 291841, 1458697, 395779, 394241, 291873, 291905, 675332, 395811, 291937, 554498, 394273, 774663, 395843, 774695, 554530, 394305, 395875, 513541, 554562, 1574921, 675364, 513573, 394337, 1327622, 513605, 554594, 1327654, 675396, 513637, 1429510, 1327686, 1707012, 675428, 1034240, 1327718, 524288, 1429542, 1034272, 774727, 1660424, 524320, 524352, 1707044, 1034304, 774759, 1660456, 524384, 1429574, 1034336, 1575465, 1458217, 1429606, 1460227, 1707076, 1660488, 1575497, 1458249, 1460259, 1460291, 1460323, 1660520, 1575529, 1458281, 1707108],
    [56, 7, 12, 293888, 293920, 293952, 1068547, 935426, 293984, 1199620, 1427456, 1068579, 935458, 454659, 1199652, 586756, 1068611, 1211393, 1821697, 1427488, 1211425, 1821729, 1199684, 1068643, 935490, 1427520, 1330694, 2054147, 1199716, 935522, 1196033, 1211457, 1821761, 1461765, 1330726, 1196065, 1461797, 454691, 1330758, 1427552, 2054179, 586788, 1461829, 1330790, 1461861, 1196097, 1211489, 1633283, 454723, 586820, 2054211, 1633315, 1821793, 1196129, 454755, 1633347, 586852, 2054243, 1633379],
    [68, 8, 12, 1197056, 379905, 1329670, 379937, 676354, 1067010, 379969, 380001, 1198597, 938500, 1428480, 949248, 936451, 1067554, 675874, 439301, 936483, 938532, 1067586, 949280, 1198629, 675906, 936515, 1428512, 439333, 936547, 938564, 1067618, 1198661, 675938, 439365, 1198693, 938596, 1329702, 1329734, 439397, 1870852, 1329766, 1870884, 1428544, 949312, 832518, 1197088, 962563, 949344, 832550, 1197120, 962595, 1428576, 832582, 1473537, 1764871, 2069510, 1870916, 1197152, 1473569, 962627, 2069542, 1764903, 832614, 1473601, 2069574, 1473633, 1764935, 962659, 1870948, 2069606, 1764967],
    [52, 9, 16, 410624, 410656, 1036288, 410688, 1036320, 920577, 1036352, 410720, 920609, 1036384, 1415688, 803841, 298498, 803873, 298530, 528899, 803905, 298562, 1201670, 528931, 803937, 298594, 1201702, 528963, 1547266, 1201734, 920641, 1201766, 1677829, 920673, 528995, 1940999, 2072068, 1413120, 1415720, 1413152, 1547298, 1677861, 1941031, 2072100, 1413184, 1415752, 1413216, 1547330, 1677893, 1941063, 2072132, 1415784, 1547362, 1677925, 1941095, 2072164],
    [52, 9, 16, 805888, 381953, 541697, 381985, 615939, 384514, 382017, 615971, 267266, 541729, 382049, 616003, 384546, 1331719, 267298, 541761, 267842, 384066, 1200645, 541793, 267874, 384098, 616035, 1200677, 805920, 805952, 805984, 1202692, 1200709, 1333251, 1202724, 1333283, 1331751, 1200741, 1202756, 1593864, 1331783, 1926662, 1331815, 1333315, 1202788, 1593896, 1333347, 1926694, 1593928, 1926726, 2000901, 2000933, 1593960, 2000965, 2000997, 1926758],
    [40, 7, 16, 411648, 542721, 411680, 708101, 542753, 1069056, 1203716, 411712, 1203748, 808451, 708133, 1069088, 1203780, 542785, 808483, 411744, 839170, 708165, 1069120, 1680386, 1680930, 838690, 542817, 1203812, 1680962, 838722, 808515, 708197, 1069152, 839266, 1680482, 808547, 2018308, 1332742, 1332774, 2018340, 1332806, 2018372, 1332838, 2018404],
    [64, 9, 16, 613376, 282625, 282657, 482818, 680453, 282689, 282721, 482850, 676864, 940547, 940579, 482882, 676896, 482914, 680485, 1127942, 614916, 1071108, 613408, 1071652, 940611, 614436, 613440, 614980, 1071172, 940643, 676928, 936961, 936993, 1127974, 1071716, 613472, 937025, 614500, 937057, 676960, 1755139, 1128006, 1886210, 1128038, 680517, 1793025, 680549, 1755171, 1886242, 1597959, 1793057, 1755203, 1597991, 729091, 1886274, 1726984, 1598023, 729123, 1793089, 1727016, 1598055, 729155, 1727048, 1755235, 1727080, 729187, 1886306, 1793121],
    [44, 7, 16, 352256, 352288, 352320, 545792, 545824, 545856, 545888, 352352, 806913, 1205763, 806945, 1205795, 806977, 1022979, 1205827, 483329, 807009, 1205859, 1581570, 1681924, 1023011, 483361, 1023043, 1712132, 1023075, 483393, 1682950, 483425, 1681956, 1581602, 1682982, 1712164, 1401349, 1581634, 1681988, 1712196, 1401381, 1683014, 1682020, 1581666, 1712228, 1401413, 1683046, 1401445],
    [52, 9, 16, 414721, 942597, 629251, 414753, 402946, 942629, 414785, 289284, 402978, 414817, 289316, 416768, 1813506, 289348, 416800, 629283, 629315, 289380, 1204744, 942661, 942693, 403010, 629347, 1073670, 403042, 1599491, 1204776, 416832, 1896456, 416864, 1073702, 1862151, 1599523, 1862183, 1204808, 1073734, 1371142, 1073766, 1371174, 1599555, 1813538, 1896488, 1204840, 1371206, 1813570, 1862215, 1599587, 1371238, 1896520, 1813602, 1862247, 1896552],
    [40, 5, 16, 285696, 285728, 285760, 993281, 1338883, 285792, 993313, 546817, 644099, 570884, 644643, 1338403, 570916, 546849, 993345, 890370, 546881, 890402, 1338947, 644163, 1335296, 644707, 1338467, 1467396, 570948, 1335328, 890434, 546913, 890466, 570980, 1894400, 993377, 1467428, 1894432, 1335360, 1467460, 1894464, 1335392, 1894496, 1467492],
    [60, 10, 16, 680960, 715776, 680992, 773635, 555524, 425477, 1075720, 846849, 2012168, 555556, 681024, 425509, 681056, 555588, 715808, 904710, 425541, 846881, 555620, 773667, 425573, 715840, 1466369, 813575, 813607, 846913, 1075752, 813639, 1466401, 1334273, 904742, 1438210, 715872, 1438242, 813671, 1334305, 846945, 1438274, 1334337, 1438306, 1468937, 1075784, 1882121, 773699, 1882665, 1468457, 904774, 2012200, 1075816, 1334369, 773731, 1466433, 1469001, 1466465, 904806, 1469033, 1882185, 2012232, 1882217, 2012264],
    [76, 12, 16, 418816, 512514, 506371, 418848, 643588, 512546, 506403, 716800, 418880, 847873, 506435, 716832, 418912, 643620, 847905, 506467, 716864, 417793, 417825, 847937, 507397, 1486848, 716896, 417857, 507429, 847969, 417889, 1716227, 507461, 1488898, 512578, 1078791, 643652, 1585670, 512610, 1209865, 507493, 1078823, 965636, 643684, 1486880, 1751560, 1209897, 1585702, 1228298, 1078855, 1488930, 1716259, 1209929, 965668, 1078887, 1751592, 1486912, 1209961, 1691658, 1228330, 1488962, 1603083, 1585734, 1716291, 965700, 1691690, 1603115, 1751624, 1228362, 1486944, 1488994, 1603147, 1585766, 1691722, 965732, 1716323, 1603179, 1751656, 1228394, 1691754],
    [36, 7, 16, 308224, 324609, 308256, 549889, 324641, 308288, 324673, 376323, 308320, 549921, 324705, 424450, 376355, 424482, 549953, 424514, 376387, 424546, 549985, 1604100, 376419, 1735173, 1717251, 1604132, 1735205, 1717283, 1604164, 1735237, 1995270, 1717315, 1604196, 1735269, 1995302, 1995334, 1717347, 1995366],
    [32, 6, 15, 420864, 290816, 419841, 510466, 290848, 510498, 420896, 510530, 290880, 419873, 510562, 511493, 420928, 290912, 419905, 511525, 420960, 1077764, 419937, 1077796, 511557, 1619969, 1077828, 511589, 1620001, 1691139, 1077860, 1691171, 1691203, 1620033, 1691235, 1620065],
    [48, 10, 12, 642048, 552961, 814081, 552993, 814113, 553025, 817670, 903684, 948743, 553057, 672258, 1341961, 814145, 817702, 903716, 948775, 1339907, 672290, 1341993, 814177, 642080, 903748, 1339939, 1079816, 672322, 642112, 1079848, 817734, 1339971, 903780, 672354, 948807, 642144, 1342025, 1079880, 817766, 1340003, 948839, 1470464, 1079912, 816645, 1342057, 1470496, 816677, 1470528, 816709, 1470560, 816741],
    [44, 7, 12, 266240, 698369, 567810, 266272, 266304, 567842, 266336, 698401, 698433, 567874, 567906, 698465, 1476099, 1607172, 1476131, 572419, 457732, 1607204, 572451, 1476163, 457764, 572483, 1607236, 1053697, 573027, 1475683, 457796, 1053729, 1607268, 1359365, 1053761, 1490438, 457828, 1359397, 1053793, 2011136, 2011168, 1490470, 2011200, 1359429, 2011232, 1490502, 1359461, 1490534],
    [64, 11, 15, 307201, 307233, 307265, 821763, 307297, 719364, 364544, 821795, 719396, 821827, 660994, 1214468, 719428, 364576, 457221, 1214500, 588294, 821859, 661026, 457253, 661058, 1214532, 364608, 950793, 588326, 457285, 661090, 364640, 1081866, 588358, 1215076, 457317, 659457, 1099271, 950825, 659489, 588390, 831488, 441353, 718948, 659521, 326666, 1081898, 441385, 950857, 326698, 1099303, 831520, 659553, 441417, 1081930, 441961, 950377, 326730, 831552, 1184264, 1099335, 1081962, 1184296, 326762, 831584, 1184328, 1099367, 1184360],
    [44, 9, 16, 264192, 264224, 444931, 264256, 444963, 264288, 444995, 496641, 440320, 445027, 496673, 496705, 2028034, 440352, 1022468, 496737, 2028066, 689156, 1022500, 820741, 440384, 689188, 1022532, 820773, 2028098, 689220, 1740295, 440416, 820805, 689764, 1740327, 820837, 1022052, 1740359, 1740391, 1284614, 1284646, 2017800, 1284678, 1284710, 2017832, 2017864, 2017896, 2028130],
    [60, 11, 16, 310272, 310304, 310336, 310368, 527361, 527393, 571393, 527425, 527457, 1608198, 1503746, 571425, 1608230, 1503778, 1182720, 1503810, 1182752, 1477124, 571457, 1477156, 1182784, 456195, 1345539, 1182816, 456227, 1345571, 456259, 1345603, 571489, 456291, 1477188, 1345635, 1856007, 1857032, 1987081, 1477220, 1988106, 1856039, 1887749, 1857064, 1987113, 1608262, 2043914, 2044458, 1987626, 1608294, 1887781, 1856071, 1857096, 2044490, 1987145, 1987658, 1887813, 1503842, 1887845, 1856103, 1857128, 2044522, 1987177, 1987690],
    [52, 8, 12, 790528, 1086981, 955908, 601602, 601634, 955940, 1052673, 601666, 955972, 1087013, 601698, 956004, 790560, 1087045, 1087077, 425985, 953859, 1052705, 426017, 1349126, 1349158, 1215490, 748550, 1349190, 1346564, 790592, 953891, 426049, 748582, 1052737, 1349222, 1215522, 1346596, 790624, 953923, 426081, 748614, 1215554, 1480199, 1346628, 688128, 953955, 1052769, 748646, 688160, 1215586, 1480231, 1346660, 1480263, 688192, 1480295, 688224],
    [44, 7, 12, 1085954, 921600, 1085986, 1743364, 1347588, 1086018, 922625, 1213440, 1743396, 1347620, 1086050, 1217027, 1743428, 1347652, 1217059, 921632, 1217091, 1213472, 1217123, 1348196, 1084418, 922657, 1213504, 921664, 1084450, 922689, 1213536, 1479174, 1084482, 1479206, 921696, 819201, 1084514, 1479238, 819233, 922721, 1479270, 2005509, 819265, 2005541, 2005573, 819297, 1742948, 2005605],
    [40, 7, 16, 559104, 398337, 1234434, 1481730, 559136, 692740, 559168, 398369, 559200, 398401, 1482274, 710149, 398433, 1482306, 1482338, 692772, 1233954, 2075139, 692804, 1233986, 692836, 1234018, 1576960, 1627654, 2075171, 710181, 1217542, 1576992, 1627686, 1217574, 710213, 1218118, 710245, 1218150, 1577024, 1627206, 1577056, 1627238, 2075203, 2075235],
    [68, 11, 16, 629760, 690177, 760833, 317954, 629792, 690209, 760865, 316931, 317986, 629824, 316963, 318018, 690241, 760897, 316995, 629856, 317027, 318050, 690273, 760929, 2020874, 1945092, 841222, 1945124, 429056, 429088, 429120, 1577985, 429152, 1945156, 841254, 1088005, 1088037, 1088069, 841286, 1578017, 1088101, 841318, 2020906, 1219079, 1774088, 1757192, 1875976, 1889801, 1480713, 1219111, 1757736, 1876008, 1219143, 1773608, 1889833, 1480745, 1219175, 1578049, 2020938, 1757768, 1876040, 1889865, 1480777, 1578081, 1757800, 1876072, 1773640, 1945188, 1889897, 1480809, 1773672, 2020970],
    [52, 8, 16, 430080, 1024000, 631298, 430112, 631330, 433667, 433699, 430144, 631362, 433731, 631394, 1615364, 433763, 1615396, 430176, 1615428, 1615460, 1024032, 1024064, 952321, 603137, 603169, 952353, 603201, 603233, 952385, 1024096, 952417, 1725441, 2023942, 908292, 1613319, 1417217, 1250821, 1417249, 908324, 1613351, 1250853, 1725473, 1417281, 908356, 2023974, 1250885, 1417313, 908388, 1250917, 1613383, 1725505, 2024006, 1613415, 1725537, 2024038],
    [64, 12, 16, 732160, 732192, 300033, 300065, 595458, 893953, 300097, 961032, 514565, 1092105, 595490, 732224, 645638, 1090051, 961064, 595522, 1090083, 893985, 1092137, 732256, 300129, 1614346, 595554, 1090115, 431104, 1505803, 1744907, 1090147, 431136, 514597, 961096, 431168, 645670, 431200, 514629, 894017, 1092169, 988676, 645702, 1614378, 988708, 514661, 1745451, 988740, 894049, 645734, 988772, 987655, 2028554, 1614410, 1505323, 987687, 1745483, 961128, 987719, 1505355, 987751, 1092201, 2028586, 1614442, 1505899, 1745003, 2028618, 2028650],
    [52, 10, 16, 563200, 2053637, 1223685, 1093124, 1093156, 600064, 697858, 1922052, 1224229, 1224261, 828931, 702983, 1093188, 704008, 600096, 563232, 697890, 600128, 563264, 828963, 703015, 563296, 697922, 704040, 828995, 1093220, 697954, 1355270, 829027, 703047, 1224293, 1355302, 823297, 600160, 823329, 1355334, 823361, 1452553, 704072, 1452585, 1355366, 823393, 1922084, 2053157, 703079, 1452617, 704104, 1922116, 2053189, 1452649, 1922148, 2053221],
    [48, 8, 16, 323074, 323106, 1356293, 323138, 323170, 708608, 1356325, 708640, 610819, 610851, 1354244, 610883, 1354276, 1356357, 708672, 825345, 1354308, 708704, 825377, 1354340, 610915, 825409, 1125377, 825441, 1880582, 1125409, 957440, 1096708, 1880614, 1125441, 957472, 1125473, 1502727, 1649664, 957504, 1880646, 1649696, 957536, 1649728, 1502759, 1096740, 1649760, 1356389, 1502791, 1880678, 1096772, 1502823, 1096804],
    [48, 8, 16, 368640, 301057, 368672, 265730, 368704, 265762, 368736, 265794, 265826, 403972, 301089, 301121, 301153, 404004, 995328, 404036, 404068, 1241088, 1634821, 1126401, 1025025, 995360, 1750534, 1126433, 1025057, 1241120, 1881607, 995392, 1025089, 1126465, 1634853, 1750566, 995424, 1025121, 1241152, 1881639, 1126497, 1918467, 1750598, 1634885, 1881671, 1241184, 1918499, 1750630, 1918531, 1881703, 1634917, 1918563],
    [44, 7, 16, 303105, 303137, 303169, 303201, 472065, 472097, 472129, 472161, 435200, 759298, 435232, 435264, 759330, 435296, 945154, 965123, 724992, 945186, 759362, 725024, 945218, 1242112, 725056, 759394, 725088, 1897988, 1618437, 945250, 965155, 1749510, 965187, 965219, 1618469, 1242144, 1749542, 1898020, 1618501, 1242176, 1749574, 1898052, 1618533, 1749606, 1242208, 1898084],
    [28, 6, 15, 325633, 305152, 325665, 325697, 305184, 325729, 849920, 1095170, 305216, 1488387, 1619460, 1243653, 305248, 1095202, 1488419, 1619492, 1095234, 849952, 1488451, 1243685, 849984, 1619524, 1243717, 1095266, 1488483, 850016, 1619556, 1243749],
    [40, 7, 12, 775168, 279042, 833538, 279074, 833570, 436225, 279106, 833602, 279138, 833634, 436257, 775200, 850945, 436289, 1113605, 436321, 829440, 829472, 850977, 1358342, 829504, 1358374, 775232, 1096195, 829536, 775264, 1113637, 1227268, 1096227, 1227300, 851009, 1358406, 1096259, 1113669, 1227332, 1096291, 1227364, 1358438, 851041, 1113701],
    [44, 7, 12, 451584, 451616, 451648, 451680, 596993, 837123, 719875, 597025, 597057, 837155, 597089, 837187, 968196, 968228, 968260, 837219, 968292, 1710597, 1580550, 1710629, 1237506, 719907, 1368065, 1237538, 1368097, 1580582, 1237570, 1710661, 719939, 1368129, 1237602, 1368161, 719971, 1580614, 1375237, 1710693, 1506310, 1375269, 1580646, 1506342, 1375301, 1506374, 1375333, 1506406],
    [44, 6, 15, 295937, 295969, 296001, 296033, 707074, 707106, 967171, 1098244, 707138, 967203, 588804, 967235, 1098276, 998403, 967267, 874496, 975873, 874528, 874560, 975905, 998435, 874592, 1098308, 707170, 975937, 1082368, 1082400, 1447940, 1098340, 975969, 1082432, 1447972, 998467, 1082464, 998499, 588836, 1448004, 588868, 1448036, 588900, 1893893, 1893925, 1893957, 1893989],
    [68, 10, 16, 281600, 296960, 321537, 296992, 321569, 1232386, 297024, 321601, 1232418, 297056, 321633, 1232450, 1232482, 281632, 865797, 846342, 281664, 865829, 846374, 619522, 281696, 619554, 846406, 865861, 619586, 619618, 1869825, 1492487, 809475, 846438, 1754632, 1923072, 1661953, 1885705, 865893, 809507, 1869857, 1492519, 991748, 1923104, 809539, 1661985, 1754664, 1885737, 809571, 1895424, 1869889, 1923136, 991780, 1662017, 1492551, 1072132, 1895456, 1754696, 1072164, 1072708, 1885769, 1923168, 1072740, 1895488, 991300, 1662049, 1869921, 1492583, 991332, 1895520, 1754728, 1885801],
    [60, 9, 16, 543745, 416258, 416290, 416322, 733701, 1361925, 578051, 578083, 584705, 543777, 578115, 578147, 543809, 1362469, 733221, 584737, 543841, 730114, 548356, 1624584, 1493510, 584769, 730146, 548388, 1773063, 416354, 733765, 1361989, 584801, 548420, 1493542, 548452, 1624616, 673792, 585728, 1493574, 730178, 673824, 1362533, 1773095, 1924097, 673856, 1493606, 730210, 673888, 585760, 733285, 1389574, 1389606, 1924129, 1773127, 585792, 1624648, 1389638, 1924161, 1389670, 1773159, 1624680, 585824, 1924193],
    [64, 9, 16, 427008, 323585, 564739, 323617, 323649, 564771, 413696, 427040, 1350150, 323681, 413728, 562690, 432644, 413760, 432676, 427072, 413792, 564803, 544769, 1625091, 432708, 544801, 564835, 427104, 544833, 432740, 544865, 562722, 562754, 1625123, 562786, 1009157, 1758727, 717824, 1625155, 1874951, 1009189, 1465347, 2006536, 1009221, 1350182, 1465379, 1536003, 1009253, 1625187, 1758759, 717856, 1874983, 2006568, 1465411, 1350214, 1536035, 1465443, 1758791, 717888, 1536067, 1875015, 2006600, 1350246, 1536099, 1758823, 717920, 1875047, 2006632],
    [52, 9, 16, 283649, 283681, 529408, 1612295, 283713, 529440, 283745, 1626632, 751107, 529472, 751139, 1233412, 529504, 1495558, 1233444, 956420, 1233476, 1233508, 1873928, 956452, 751171, 878596, 956484, 956516, 1235461, 1495590, 751203, 1235493, 1495622, 849410, 1612327, 1235525, 1495654, 1235557, 878628, 1612359, 1667078, 849442, 878660, 1874472, 1626152, 1667110, 878692, 1874504, 1626184, 1626728, 1667142, 849474, 1612391, 1667174, 1874024, 849506],
    [44, 6, 12, 515073, 448002, 973826, 515105, 448034, 1105411, 973858, 974402, 442369, 515137, 1105443, 974434, 447554, 1105475, 442401, 515169, 447586, 1105507, 442433, 1236484, 1824768, 1236516, 442465, 704512, 1775620, 1236548, 778243, 778275, 1824800, 704544, 1236580, 1775652, 1367557, 778307, 1367589, 1367621, 1824832, 704576, 1775684, 1367653, 778339, 704608, 1824864, 1775716],
    [40, 7, 12, 973315, 646660, 1496067, 973347, 574464, 842242, 646692, 842274, 574496, 842306, 842338, 973379, 973411, 574528, 646724, 646756, 1496099, 1104389, 1366534, 574560, 1366566, 1694720, 1104421, 1825793, 1104453, 835585, 1104485, 1694752, 1825825, 1496131, 835617, 1366598, 1496163, 1366630, 1694784, 1825857, 835649, 835681, 1694816, 1825889],
    [60, 11, 16, 647168, 312320, 312352, 647200, 312384, 312416, 443393, 443425, 443457, 647232, 443489, 859651, 1491463, 647264, 1369606, 859683, 1369638, 910850, 1369670, 910882, 859715, 1369702, 1360392, 1491495, 1360424, 859747, 923648, 910914, 923680, 923712, 1360456, 923744, 1631753, 1491527, 910946, 2007557, 1171972, 1762826, 1711105, 1631785, 1826817, 1172004, 1762858, 2007589, 1631817, 1360488, 1711137, 1826849, 1762890, 1491559, 2007621, 1631849, 1172036, 1711169, 1762922, 1826881, 2007653, 1172068, 1711201, 1826913],
    [52, 10, 16, 584195, 517121, 304642, 584227, 304674, 858628, 584259, 517153, 304706, 584291, 531457, 304738, 1229318, 284672, 531489, 284704, 517185, 531521, 1229350, 284736, 531553, 858660, 284768, 1230345, 977413, 517217, 858692, 977445, 977477, 858724, 977509, 1370118, 1501703, 1499656, 1370150, 1230377, 1244168, 1499688, 1501735, 1370694, 1228870, 1499720, 1244200, 1501767, 1499752, 1230409, 1244232, 1370726, 1228902, 1501799, 1230441, 1244264],
    [76, 12, 16, 486400, 313345, 486432, 1109506, 313377, 481795, 1109538, 313409, 792068, 939010, 1109570, 313441, 481827, 1362944, 1109602, 481859, 1362976, 486464, 481891, 1474564, 1363008, 1475108, 486496, 744965, 791588, 792132, 1270278, 951815, 744997, 951847, 951879, 745029, 1363040, 951911, 1223176, 745061, 792164, 1240585, 1223208, 1212938, 1792004, 1240617, 939042, 1212970, 1595392, 1400331, 1223240, 1240649, 939074, 1792036, 939106, 1989633, 1213002, 1240681, 1400363, 1270310, 1595424, 1943553, 1792068, 1989665, 1474628, 1270342, 1595456, 1400395, 1223272, 1213034, 1792100, 1989697, 1595488, 1400427, 1943585, 1989729, 1474660, 1270374, 1943617, 1943649],
    [44, 8, 16, 446465, 446497, 743938, 446529, 1632771, 743970, 446561, 578560, 1737731, 744002, 970246, 1138694, 979460, 1632803, 578592, 1737763, 744034, 578624, 970278, 578656, 1632835, 876037, 1632867, 979492, 876069, 970310, 979524, 979556, 1763847, 876101, 1763879, 876133, 1138726, 970342, 1763911, 1534977, 1763943, 1535009, 1737795, 1138758, 1535041, 1737827, 1138790, 1535073],
    [48, 5, 16, 971776, 980482, 980514, 487424, 980546, 487456, 980578, 487488, 487520, 1273857, 1273889, 631808, 560130, 1273921, 560162, 1273953, 631840, 502785, 502817, 631872, 560194, 631904, 970753, 502849, 502881, 1635844, 1497088, 971808, 560226, 1739267, 1497120, 970785, 971840, 2070532, 1635876, 1497152, 2070564, 1497184, 970817, 1739299, 971872, 1635908, 1739331, 2070596, 970849, 1739363, 1635940, 2070628],
    [40, 7, 16, 357377, 340993, 357409, 341025, 357441, 341057, 357473, 341089, 318464, 318496, 318528, 1372676, 318560, 734208, 734240, 734272, 1226242, 1110531, 1226274, 1110563, 1110595, 1110627, 734304, 1899013, 2045446, 1939460, 1372708, 1226306, 1939492, 1899045, 1226338, 1372740, 2045478, 1939524, 1899077, 1372772, 2045510, 1939556, 1899109, 2045542],
    [40, 6, 15, 342017, 342049, 342081, 342113, 565762, 565794, 565826, 565858, 581632, 581664, 581696, 581728, 579584, 579616, 1111555, 1504772, 579648, 1783808, 1766917, 579680, 1111587, 1504804, 710657, 1766949, 710689, 1111619, 710721, 1783840, 1504836, 710753, 1766981, 1432576, 1111651, 1432608, 1432640, 1783872, 1504868, 1432672, 1767013, 1783904],
    [36, 6, 12, 580609, 580641, 343041, 343073, 343105, 343137, 1636868, 1767941, 580673, 580705, 843776, 843808, 843840, 843872, 777216, 1112578, 1892353, 1374723, 777248, 1112610, 1374755, 777280, 1636900, 1892385, 1767973, 1112642, 777312, 1374787, 1636932, 1768005, 1892417, 1112674, 1374819, 1636964, 1768037, 1892449],
    [32, 5, 12, 335872, 335904, 335936, 335968, 727041, 1115650, 727073, 1115682, 727105, 1115714, 728579, 795649, 1115746, 605186, 605218, 728611, 795681, 727137, 728643, 1776640, 605250, 728675, 605282, 1508868, 795713, 1776672, 1508900, 795745, 1508932, 1776704, 1508964, 1776736],
    [52, 8, 15, 334849, 334881, 334913, 334945, 336896, 663553, 706055, 336928, 663585, 336960, 663617, 336992, 663649, 1006083, 599041, 599073, 794627, 1623040, 1006115, 1006147, 852485, 1006179, 1114630, 752130, 752162, 599105, 752194, 794659, 852517, 1772036, 599137, 1114662, 2033666, 752226, 794691, 852549, 1772068, 1623072, 1114694, 2033698, 794723, 706087, 706119, 852581, 1114726, 1623104, 706151, 1772100, 2033730, 1772132, 2033762, 1623136],
    [40, 6, 16, 428032, 428064, 428096, 428128, 477698, 477730, 1598979, 1379331, 477762, 1531904, 477794, 598016, 1531936, 575489, 1531968, 575521, 1532000, 575553, 575585, 1379875, 598048, 598080, 1598499, 598112, 1639940, 1379907, 1771013, 1639972, 1771045, 1386496, 1598531, 1386528, 1379939, 1640004, 1386560, 1771077, 1386592, 1640036, 1771109, 1598563],
    [56, 9, 16, 314369, 488962, 854018, 314401, 488994, 854050, 314433, 489026, 854082, 314465, 1477632, 489058, 854114, 1608705, 1477664, 1608737, 1477696, 1608769, 1477728, 1116679, 1608801, 1729543, 882180, 731136, 1511941, 1730087, 1116199, 882212, 731168, 882244, 731200, 882276, 1658371, 731232, 2060806, 1551364, 1511973, 1116743, 1658403, 1512005, 1551396, 1551428, 1729607, 1658435, 1512037, 1551460, 1116775, 1509896, 1509928, 2060838, 1509960, 1658467, 1509992, 1729639, 2060870, 2060902],
    [48, 8, 16, 299008, 299040, 299072, 299104, 1091078, 602627, 958467, 593410, 602659, 1091110, 593442, 593474, 1353220, 593506, 602691, 862209, 1091142, 602723, 1650688, 862241, 958499, 1353252, 862273, 1548288, 958531, 1353284, 1548320, 862305, 1644039, 1091174, 824321, 1644071, 824353, 1154565, 1548352, 1644103, 1154597, 1650720, 1644135, 958563, 1154629, 1548384, 824385, 1353316, 1154661, 1650752, 824417, 1650784],
    [60, 10, 16, 339968, 470017, 340000, 470049, 340032, 470081, 1463296, 340064, 1351173, 1027587, 1118211, 1222152, 827906, 1251844, 1118755, 470113, 1118787, 1222184, 1118819, 1484294, 827938, 1251876, 1027107, 1222216, 1027139, 1484326, 1249799, 827970, 1249831, 1251908, 1679360, 1800199, 1249863, 1251940, 1351205, 1811457, 1249895, 1484358, 1380873, 1679392, 1027171, 1351237, 1811489, 1380905, 1800231, 1222248, 1679424, 828002, 1380937, 1463328, 1811521, 1800263, 1380969, 1463360, 1679456, 1811553, 1484390, 1463392, 1800295, 1351269],
    [60, 11, 16, 473088, 268288, 677889, 268320, 333314, 473120, 268352, 333346, 268384, 333378, 473152, 333410, 1661443, 990725, 1121798, 473184, 677921, 990757, 844803, 990789, 1381895, 1245190, 845347, 1512968, 677953, 1660963, 845379, 1121830, 845411, 990821, 1381927, 1121862, 1513000, 677985, 1660995, 1121894, 1107460, 1245222, 1107492, 1381959, 1252874, 1513032, 1107524, 1523209, 1245254, 1252906, 1661027, 1252938, 1107556, 1252970, 1381991, 1302528, 1513064, 1523241, 1302560, 1245286, 1523273, 1302592, 1302624, 1523305],
    [48, 7, 16, 648193, 735233, 735265, 1055744, 648225, 735297, 663044, 1269251, 1187330, 648257, 735329, 1448961, 1513990, 1055776, 663076, 663108, 474112, 1187362, 1269283, 663140, 474144, 648289, 474176, 1514022, 474208, 1448993, 1106437, 1514054, 1106469, 1269315, 1391622, 1106501, 1514086, 1106533, 1055808, 1269347, 1391654, 1695744, 1187394, 1695776, 1391686, 1449025, 1055840, 1695808, 1187426, 1449057, 1391718, 1695840],
    [44, 8, 12, 401408, 270850, 270882, 270914, 400899, 270946, 327681, 400931, 401440, 327713, 400963, 401472, 327745, 400995, 401504, 327777, 1123844, 1449985, 1254918, 1827841, 1450017, 1123876, 1123908, 1123940, 1450049, 1129472, 1517063, 1129504, 1827873, 1450081, 1129536, 1517095, 1129568, 1385989, 1827905, 1254950, 1386021, 1254982, 1386053, 1517127, 1255014, 1386085, 1517159, 1827937],
    [48, 7, 12, 469507, 1253379, 1253923, 1122818, 1253955, 1122850, 1122882, 469027, 1122914, 1187840, 1516038, 469059, 867328, 1384964, 1319937, 867360, 1384996, 1187872, 469603, 1253475, 867392, 1319969, 399362, 399394, 1187904, 1507329, 399426, 1780229, 399458, 1385028, 867424, 1385060, 1320001, 1260545, 1187936, 1507361, 1260577, 1320033, 1260609, 1780261, 1507393, 1516070, 1516102, 1260641, 1780293, 1516134, 1780325, 1507425],
    [48, 8, 16, 370688, 370720, 370752, 1083907, 370784, 691714, 878087, 649217, 691746, 878119, 616964, 691778, 649249, 878151, 649281, 649313, 1083939, 992258, 616996, 617028, 752641, 1083971, 992290, 2057734, 1518598, 992322, 992866, 1519142, 752673, 745989, 1387525, 1519174, 1084003, 617060, 746021, 1387557, 746053, 1387589, 752705, 746085, 1387621, 878183, 1519206, 691298, 2057254, 752737, 2057286, 2057318],
    [64, 10, 16, 330752, 328705, 1124869, 330784, 484867, 328737, 1124901, 330816, 484899, 328769, 330848, 484931, 328801, 1925639, 764928, 484963, 1664005, 1124933, 1795593, 896001, 2056708, 1124965, 764960, 1255942, 1925671, 896033, 1664037, 695810, 1795625, 695842, 1255974, 1519623, 695874, 1781769, 2056740, 764992, 695906, 1256006, 1256038, 896065, 1519655, 765024, 1781801, 896097, 748040, 2001926, 1925703, 748072, 1519687, 1664069, 1795657, 1781833, 2001958, 748104, 2056772, 748136, 2001990, 1925735, 1519719, 1664101, 1782377, 2002022, 1795177, 2056804],
    [44, 6, 16, 356352, 373761, 1521154, 356384, 373793, 1521186, 356416, 373825, 1521218, 356448, 373857, 1521250, 371712, 1652229, 371744, 822274, 822306, 371776, 371808, 1652261, 1351680, 1652293, 1552384, 1552416, 1351712, 1765892, 1552448, 1929731, 1552480, 1765924, 1652325, 822338, 1351744, 1929763, 822370, 1942533, 1351776, 1942565, 1765956, 1942597, 1929795, 1942629, 1765988, 1929827],
    [64, 11, 16, 331777, 331809, 331841, 331873, 370178, 463872, 370210, 463904, 370242, 370274, 463936, 897025, 463968, 1522182, 897057, 1373699, 897089, 864772, 969224, 1652744, 1482752, 864804, 1522214, 1100295, 1745921, 864836, 1522246, 897121, 864868, 1231369, 1156613, 969256, 1482784, 1373731, 1156645, 1745953, 1652776, 1100327, 1156677, 1231401, 969288, 1652808, 1389066, 1156709, 1100359, 1389098, 2072583, 1231433, 1482816, 1373763, 2072615, 1745985, 1522278, 1389130, 969320, 2072647, 1482848, 1100391, 1746017, 1373795, 1389162, 2072679, 1231465, 1652840],
    [36, 7, 15, 333824, 358401, 333856, 358433, 333888, 358465, 333920, 358497, 1120772, 386562, 996867, 386594, 620544, 1120804, 386626, 1259013, 386658, 996899, 1120836, 620576, 1259045, 996931, 620608, 1259077, 1120868, 996963, 620640, 1259109, 1907206, 1931268, 1931300, 1907238, 1931332, 1907270, 1931364, 1907302],
    [60, 10, 12, 319488, 359425, 989185, 319520, 359457, 319552, 359489, 319584, 359521, 989217, 1391111, 1128964, 989249, 1260038, 1128996, 1391143, 1260070, 573955, 997379, 573987, 997411, 721926, 574019, 997443, 1260102, 574051, 997475, 1434630, 1129028, 989281, 1391175, 721958, 1129060, 1382400, 1434662, 721990, 1260134, 1382432, 1382464, 1391207, 1382496, 1697289, 1908226, 1434694, 722022, 1697321, 2039301, 1908258, 1697353, 1376776, 2039333, 1908290, 1376808, 1376840, 1376872, 1434726, 2039365, 1908322, 1697385, 2039397],
    [36, 7, 12, 349184, 273409, 273441, 349216, 273473, 273505, 349248, 1191427, 721412, 983040, 349280, 721444, 1191459, 1000965, 983072, 1000997, 1394182, 721476, 1134593, 1191491, 1134625, 1394214, 983104, 1001029, 1733122, 721508, 1134657, 1134689, 1394246, 1733154, 983136, 1191523, 1733186, 1001061, 1394278, 1733218],
    [32, 7, 15, 459776, 459808, 611329, 1133058, 459840, 611361, 459872, 611393, 1377281, 1246724, 611425, 1395203, 1131013, 1133090, 1395235, 1131045, 1133122, 1246756, 1395267, 1393158, 1133154, 1377313, 1131077, 1395299, 1393190, 1246788, 1377345, 1131109, 1393222, 1246820, 1377377, 1393254],
    [52, 8, 16, 390658, 871426, 390690, 871458, 758276, 390722, 871490, 837632, 350209, 390754, 871522, 1247232, 350241, 837664, 1132037, 350273, 1378305, 350305, 837696, 700931, 1787398, 1247264, 700963, 758308, 1132069, 700995, 837728, 1787430, 1378337, 701027, 985607, 758340, 985639, 941056, 985671, 758372, 2055168, 941088, 1132101, 1247296, 941120, 1378369, 2055200, 1787462, 941152, 1132133, 985703, 1247328, 2055232, 1378401, 1787494, 2055264],
    [32, 6, 16, 351233, 351265, 351297, 351329, 576512, 576544, 1641473, 1510915, 1510947, 576576, 1526274, 1657348, 576608, 1788421, 1526306, 1494017, 1494049, 1657380, 1641505, 1494081, 1788453, 1526338, 1494113, 1657412, 1510979, 1788485, 1526370, 1657444, 1641537, 1788517, 1511011, 1641569],
    [56, 9, 16, 315392, 353280, 315424, 1398279, 315456, 338945, 856578, 353312, 315488, 1398311, 338977, 353344, 1398343, 1363969, 339009, 353376, 339041, 1364001, 856610, 568835, 1267204, 568867, 1267236, 1364033, 856642, 568899, 1267268, 1265157, 568931, 1910784, 1265189, 1267300, 1364065, 876545, 999428, 769542, 999460, 769574, 999492, 769606, 1529352, 769638, 856674, 999524, 1529384, 1398375, 1910816, 876577, 1265221, 1529416, 1529448, 876609, 1265253, 876641, 1910848, 1910880],
    [48, 9, 16, 1137154, 1268228, 1266183, 606725, 1119747, 1137186, 1268260, 1364993, 607750, 606757, 1119779, 1266215, 607782, 1137218, 1365025, 606789, 1268292, 607814, 1365057, 1119811, 1459720, 1911809, 1266247, 606821, 1137250, 2009095, 1459752, 617473, 607846, 617505, 1266279, 617537, 1268324, 617569, 1459784, 879616, 1459816, 879648, 1365089, 1119843, 1911841, 879680, 2009127, 879712, 1911873, 2009159, 1911905, 2009191],
    [56, 10, 16, 445440, 445472, 534024, 445504, 1102849, 742915, 454148, 873989, 354304, 742947, 354336, 445536, 1007106, 874021, 354368, 1007138, 742979, 354400, 1007170, 454180, 874053, 1007202, 485377, 1138183, 665097, 812034, 485409, 743011, 485441, 454212, 874085, 485473, 534056, 454244, 1138215, 665129, 534088, 1138247, 812066, 1138279, 665161, 1239558, 534120, 1464320, 812098, 1239590, 812130, 1239622, 665193, 1239654, 1464352, 1464384, 1102881, 1464416, 1102913, 1102945],
    [52, 7, 16, 1011712, 355329, 679426, 355361, 355393, 355425, 1100800, 679458, 1011744, 1399301, 1008131, 1530374, 1011776, 1399333, 1100832, 679490, 978436, 1640451, 1530406, 1399365, 1902598, 679522, 1901573, 978468, 1530438, 1399397, 978500, 1530470, 1727488, 1008163, 1858561, 978532, 1640483, 1901605, 1902630, 1727520, 1011808, 1008195, 1858593, 1901637, 1100864, 1640515, 1727552, 1902662, 1858625, 1901669, 1727584, 1100896, 1008227, 1858657, 1640547, 1902694],
    [64, 11, 16, 1012736, 468482, 468514, 880641, 468546, 548864, 548896, 1781256, 1012768, 548928, 880673, 1530888, 468578, 1012800, 863747, 1140228, 1649159, 2042377, 1140260, 863779, 1140292, 1697792, 1517572, 1402374, 880705, 863811, 548960, 863843, 1140324, 1697824, 1781288, 1697856, 1012832, 1070597, 1517604, 1697888, 1530920, 2043402, 880737, 1649191, 2026506, 1517636, 1070629, 2042409, 1402406, 2027050, 2042922, 1649223, 1531464, 1402438, 1780808, 1070661, 2042441, 1402470, 1517668, 2027082, 2042954, 1649255, 1531496, 1070693, 1780840, 2042473, 2027114, 2042986],
    [36, 8, 16, 1042432, 287745, 287777, 338436, 1042464, 287809, 338468, 287841, 338500, 1143809, 1663494, 561667, 1663526, 1141250, 1141282, 1663558, 561699, 561731, 338532, 561763, 1143841, 1042496, 1888773, 1042528, 1141314, 1141346, 1794567, 1143873, 1888805, 1794599, 1794631, 1663590, 1143905, 1794663, 1888837, 1888869],
    [44, 7, 12, 780288, 781313, 1011202, 780320, 1011234, 747012, 1011266, 1011298, 1142275, 781345, 780352, 1142307, 1142339, 781377, 780384, 1142371, 1404422, 1145857, 781409, 747044, 747076, 1145889, 747108, 1145921, 1533445, 1272837, 1404454, 1273381, 1798146, 1532965, 1145953, 1404486, 1408000, 1273413, 1798178, 1408032, 1532997, 1273445, 1408064, 1404518, 1798210, 1408096, 1533029, 1798242],
    [60, 7, 12, 490497, 619011, 1009667, 1010211, 750082, 490529, 1756162, 618531, 490561, 1756706, 1010243, 1714176, 749602, 1756738, 490593, 1714208, 1010275, 1714240, 618563, 1014784, 749634, 618595, 750178, 1436672, 1272324, 1014816, 1272356, 1567745, 1270788, 693252, 1272388, 1403397, 693284, 1270820, 1272420, 1403429, 1436704, 1014848, 1270852, 1534470, 693316, 1270884, 1567777, 1534502, 1436736, 693348, 954374, 1567809, 1403461, 1436768, 1014880, 1534534, 1567841, 1403493, 954406, 954438, 1534566, 954470, 1756258, 1714272],
    [56, 8, 16, 389120, 1550855, 1668103, 389152, 389184, 1419780, 839684, 389216, 724482, 1537542, 1044481, 2076165, 1257987, 1044513, 1419812, 724514, 1537574, 738305, 2076197, 738337, 1044545, 1668647, 1550375, 1044577, 1419844, 1668679, 724546, 811014, 1101829, 811046, 1537606, 738369, 839716, 1550407, 811078, 2076229, 724578, 738401, 1258019, 1101861, 1537638, 839748, 1668711, 811110, 1419876, 1550439, 1258051, 1101893, 1117190, 1117222, 839780, 1258083, 1117254, 1117286, 1102437, 2075749],
    [56, 10, 16, 345089, 450050, 450082, 1143299, 345121, 1143331, 1014279, 1143363, 345153, 1143395, 765952, 914433, 591879, 345185, 723464, 914465, 1783301, 450114, 1405444, 450146, 1405476, 765984, 1405508, 1144840, 1405540, 592423, 347136, 766016, 723496, 914497, 766048, 347168, 914529, 1013799, 1144872, 592455, 347200, 1013831, 1336838, 1145416, 723016, 347232, 1336870, 1014375, 591975, 1145448, 723048, 1783333, 1336902, 1336934, 1783365, 1783397, 2035209, 2035241, 2035273, 2035305],
    [36, 7, 15, 346113, 346145, 346177, 346209, 519168, 519200, 1406467, 519232, 519264, 590851, 650754, 1406499, 590883, 650786, 1406531, 650818, 590915, 650850, 1406563, 590947, 1993729, 1305092, 1799685, 1305124, 1799717, 1993761, 1993793, 1305156, 1799749, 1920518, 1799781, 1305188, 1920550, 1920582, 1993825, 1920614],
    [72, 11, 12, 1003520, 388097, 475651, 388129, 388161, 1005060, 1003552, 388193, 1003584, 475683, 1005092, 475715, 475747, 1174018, 1276421, 1174050, 1005124, 1174082, 1407494, 852997, 1174114, 869895, 1538055, 1876994, 1669640, 1005156, 1276453, 589830, 868360, 1877026, 1407526, 912384, 853029, 869927, 1538087, 589862, 912416, 868904, 1669160, 1276485, 1877058, 1003616, 853061, 1407558, 869959, 1538119, 589894, 868936, 1669192, 1788929, 1276517, 912448, 853093, 1407590, 2051593, 589926, 869991, 1538151, 1788961, 912480, 868968, 1669224, 1524234, 2051625, 1788993, 1877090, 1524266, 2051657, 1524298, 1789025, 1524330, 2051689],
    [40, 7, 12, 495616, 363520, 799745, 363552, 799777, 363584, 495648, 363616, 755713, 888322, 888354, 755745, 888386, 1148420, 495680, 669187, 1672710, 755777, 1148452, 1148484, 888418, 1148516, 669219, 755809, 495712, 669251, 1672742, 1280517, 1280549, 669283, 1672774, 1937410, 1937442, 1672806, 1280581, 799809, 1937474, 799841, 1280613, 1937506],
    [52, 8, 15, 1016322, 626689, 1016354, 391684, 538115, 1016386, 391716, 538147, 569344, 1016418, 391748, 569376, 569408, 391780, 1018881, 569440, 522757, 626721, 1018913, 522789, 538179, 1524736, 1278471, 522821, 538211, 1569794, 626753, 1018945, 522853, 668166, 1278503, 668198, 1524768, 1569826, 626785, 1018977, 668230, 888832, 1278535, 888864, 888896, 1424386, 1524800, 888928, 1569858, 1278567, 1424418, 668262, 1424450, 1524832, 1569890, 1424482],
    [48, 10, 16, 329728, 608257, 329760, 624130, 329792, 624162, 329824, 624194, 759808, 624226, 1412613, 608289, 759840, 755203, 608321, 755235, 1412645, 755267, 759872, 608353, 755299, 1690116, 759904, 1412677, 1803782, 1733637, 1934855, 1690148, 1412709, 1803814, 1733669, 1934887, 1690180, 1674761, 1543688, 1674793, 1803846, 1543720, 1934919, 1690212, 1543752, 1803878, 1674825, 1934951, 1543784, 1733701, 1674857, 1733733],
    [52, 9, 16, 366593, 410115, 366625, 410147, 366657, 410179, 366689, 410211, 461825, 344578, 890880, 461857, 344610, 461889, 344642, 890912, 461921, 344674, 1248256, 1262086, 1059846, 1248288, 1263108, 1248320, 890944, 1248352, 1584647, 1060390, 1560069, 1655815, 1261606, 890976, 1263140, 1560101, 1584679, 1060422, 1655847, 1261638, 1560133, 1263172, 1584711, 1935880, 1935912, 1060454, 1560165, 1655879, 1261670, 1935944, 1263204, 1935976, 1584743, 1655911],
    [48, 8, 16, 462848, 367616, 367648, 593921, 367680, 367712, 1283589, 406019, 1076229, 497665, 462880, 537092, 497697, 406051, 593953, 497729, 497761, 462912, 537124, 593985, 1810432, 1541639, 406083, 462944, 1076773, 1283109, 1810464, 594017, 1810496, 1283653, 537156, 1541671, 1076293, 920066, 406115, 1283685, 1541703, 1545734, 537188, 1545766, 1076325, 920098, 1545798, 1541735, 1545830, 920130, 920162, 1810528],
    [60, 9, 16, 499713, 499745, 551428, 499777, 551460, 499809, 892928, 413187, 892960, 413219, 1546758, 413251, 892992, 413283, 1809409, 1282565, 478214, 1546790, 478246, 893024, 1809441, 1282597, 551492, 1809473, 1136130, 1136162, 1282629, 551524, 1136194, 1001991, 1051650, 1002023, 1282661, 1051682, 1002055, 1051714, 478790, 1052258, 1002087, 1774593, 1135714, 478822, 1219584, 2050053, 1546310, 1774625, 1219616, 2069000, 2050085, 2069032, 1774657, 1219648, 1774689, 2069064, 2050117, 1546342, 2069096, 1809505, 2050149, 1219680],
    [48, 8, 16, 501760, 501792, 628226, 501824, 628258, 501856, 943621, 1285635, 761857, 1416710, 694272, 1285667, 1074182, 1285699, 761889, 943653, 1416742, 1285731, 761921, 1074214, 761953, 1462791, 628290, 943685, 1416774, 694304, 628322, 1021444, 1021476, 1416806, 1021508, 694336, 1021540, 1074246, 1414149, 694368, 1414181, 1414213, 943717, 1414245, 1462823, 1431559, 1074278, 1431591, 1462855, 1431623, 1432167, 1462375],
    [52, 9, 16, 302081, 1724932, 1594885, 302113, 726531, 302145, 1724964, 726563, 632833, 302177, 1563653, 1594917, 632865, 632897, 726595, 826368, 632929, 1153543, 726627, 763904, 826400, 1153575, 1153607, 1153639, 763936, 826432, 763968, 764000, 826464, 1903623, 1089030, 1089062, 1903655, 2019842, 1808904, 1089094, 1808936, 1563685, 2019874, 1724996, 1903687, 1808968, 1089126, 1564229, 1594437, 1809000, 2019906, 1725028, 1564261, 1594469, 1903719, 2019938],
    [48, 8, 16, 1026049, 696321, 994823, 634880, 434691, 499204, 434723, 499236, 434755, 892418, 634912, 434787, 499268, 1418758, 499300, 1287685, 1418790, 634944, 1287717, 892450, 1418822, 994855, 1287749, 1287781, 892482, 1418854, 711685, 892514, 634976, 994887, 711717, 711749, 696353, 1026081, 696385, 1912838, 711781, 1913861, 994919, 1026113, 696417, 1912870, 1913893, 1026145, 1912902, 1913925, 1912934, 1913957],
    [44, 9, 16, 635904, 766977, 635936, 767009, 895490, 1256966, 471555, 635968, 471587, 471619, 1256998, 471651, 767041, 636000, 1158145, 767073, 895522, 1596933, 1155591, 1158177, 1286664, 895554, 1257030, 1155623, 1596965, 1286696, 1155655, 1596997, 1257062, 1286728, 1155687, 1158209, 1286760, 895586, 2008065, 1597029, 2008097, 1158241, 1812996, 2008129, 1813028, 1813060, 1813092, 2008161],
    [44, 8, 16, 636928, 272384, 503809, 518658, 272416, 1420807, 518690, 636960, 272448, 518722, 272480, 286722, 518754, 501251, 636992, 2061319, 286754, 501283, 501315, 286786, 501347, 637024, 503841, 286818, 503873, 503905, 1289733, 1549828, 1549860, 1549892, 1289765, 1420839, 1289797, 1549924, 1289829, 2061351, 1420871, 1744390, 1420903, 2061383, 1744422, 1744454, 1744486, 2061415],
    [60, 9, 16, 899073, 899105, 1288711, 1930247, 899137, 797696, 928769, 899169, 1729029, 1713670, 637952, 1860098, 1157635, 1698822, 1860614, 637984, 797728, 1157667, 1991172, 638016, 928801, 1729061, 1288743, 1713702, 638048, 1992200, 1157699, 1860130, 1288775, 1157731, 1930279, 797760, 1731585, 1860646, 1991204, 928833, 1713734, 797792, 1992232, 1729093, 1698854, 1860162, 1288807, 1731617, 928865, 1930311, 1698886, 1860678, 1731649, 1991236, 1699430, 1992264, 1731681, 1729125, 1860194, 1713254, 1930343, 1860710, 1991268, 1992296],
    [68, 7, 12, 1060864, 1031168, 1160707, 1293313, 634372, 1323009, 1031200, 1422853, 1293345, 1029634, 634404, 1029666, 1060896, 855044, 1029698, 622593, 1323041, 1553926, 1160739, 1029730, 1422885, 1160771, 1553958, 1060928, 622625, 1553990, 1031232, 609283, 622657, 1160803, 1422917, 855076, 1323073, 622689, 1730565, 1422949, 1220612, 1554022, 1409024, 609315, 1293377, 1060960, 634436, 855108, 609347, 634468, 1992707, 1323105, 1220644, 609379, 1220676, 1730597, 1220708, 1031264, 855140, 1409056, 1992739, 1730629, 1904644, 1409088, 1992771, 1730661, 1904676, 1409120, 1293409, 1904708, 1992803, 1904740],
    [60, 7, 12, 361472, 1028610, 1191936, 361504, 1159683, 361536, 1028642, 1290756, 361568, 1555457, 1061889, 1159715, 1028674, 739331, 1421829, 1159747, 1028706, 460802, 1159779, 739363, 1290788, 1421861, 739395, 1191968, 986116, 1290820, 739427, 1274885, 1061921, 460834, 1421893, 1555489, 1192000, 986148, 1290852, 1061953, 1421925, 460866, 1863174, 1192032, 986180, 1274917, 460898, 1061985, 1555521, 1863206, 1540097, 986212, 1540129, 1863238, 1274949, 2035717, 1274981, 1540161, 1863270, 2035749, 1540193, 1555553, 2035781, 2035813],
    [48, 10, 15, 362496, 392193, 651780, 362528, 392225, 362560, 521734, 392257, 651812, 362592, 392289, 521766, 372740, 372772, 651844, 535042, 372804, 1291270, 521798, 373348, 651364, 1291302, 521830, 887299, 535074, 1616391, 1291334, 535106, 1291366, 1878537, 535138, 740869, 887331, 887363, 1453576, 740901, 1616423, 887395, 1453608, 740933, 1453640, 740965, 1878569, 1453672, 1616455, 1878601, 1616487, 1878633],
    [68, 12, 12, 783360, 1686025, 1192961, 783392, 493569, 783424, 1686057, 493601, 493633, 493665, 1554950, 1192993, 1307140, 1423364, 783456, 1018370, 1307172, 1423396, 1321990, 1307204, 1423428, 1018402, 1554982, 1307236, 1193025, 2010632, 1423460, 1831431, 1686089, 1018434, 1322022, 1700873, 1832459, 1018466, 1879557, 1831463, 1148928, 1322566, 1554502, 1700905, 1150467, 1879589, 1148960, 1817098, 1832491, 1150499, 1831495, 1148992, 1193057, 1700937, 1150531, 1817130, 1149024, 1832523, 1555046, 1322086, 1831527, 1150563, 1817162, 2010664, 1879621, 1701481, 1685609, 1817194, 1832555, 2010696, 1879653, 2010728],
    [40, 7, 9, 508928, 640001, 508960, 640033, 508992, 640065, 509024, 640097, 771587, 641024, 902661, 277505, 641056, 277537, 771619, 277569, 641088, 277601, 641120, 1194498, 1325059, 771651, 902693, 1064452, 1194530, 771683, 902725, 1033734, 1325091, 1033766, 1064484, 902757, 1194562, 1033798, 1325123, 1064516, 1194594, 1033830, 1325155, 1064548],
    [12, 3, 12, 378881, 378913, 378945, 378977, 772096, 772128, 1032706, 772160, 1032738, 1032770, 772192, 1032802],
    [64, 8, 14, 380928, 551936, 1035264, 1166337, 1035296, 1166369, 1035328, 1166401, 1035360, 1166433, 1263616, 380960, 493058, 380992, 493090, 381024, 493122, 770563, 493154, 687105, 492036, 551968, 886277, 1297413, 1263648, 492068, 552000, 886309, 1297445, 492100, 552032, 886341, 1297477, 492132, 1804289, 687137, 886373, 1297509, 687169, 1146883, 770595, 1263680, 687201, 1080839, 1410566, 1080871, 1146915, 770627, 1263712, 1804321, 1410598, 1146947, 1080903, 1804353, 1410630, 1147491, 1080935, 770147, 1410662, 1804385, 1295366, 1295398, 1295430, 1295462],
    [52, 7, 14, 1296900, 683009, 1919493, 1002496, 1133569, 541186, 905216, 683041, 1165827, 541218, 541250, 1002528, 683073, 1165859, 1673220, 1133601, 541282, 683105, 1396230, 1919525, 1936385, 1296932, 1278979, 1165891, 1673252, 1002560, 905248, 1133633, 1296964, 1279011, 1396262, 1165923, 1207296, 1002592, 1936417, 1673284, 1133665, 1279043, 1296996, 1207328, 905280, 1919557, 1936449, 1279075, 1396294, 1207360, 905312, 1673316, 1919589, 1207392, 1396326, 1936481],
    [40, 7, 14, 348160, 1168384, 1299457, 1168416, 1299489, 1168448, 1299521, 1168480, 1299553, 1542659, 348192, 1281540, 348224, 1411586, 1542691, 1806853, 348256, 1431046, 776192, 1281572, 479233, 1411618, 479265, 1806885, 479297, 1411650, 479329, 1411682, 1542723, 1281604, 776224, 1542755, 1281636, 1431078, 776256, 776288, 1806917, 1431110, 1431142, 1806949],
    [44, 8, 14, 382976, 1298949, 383008, 480257, 383040, 383072, 480289, 1807874, 1527300, 1167364, 480321, 1167908, 480353, 1298981, 1938947, 1807906, 1167940, 907265, 1167972, 1789957, 1938979, 1526820, 1807938, 1659398, 907297, 1791495, 1659430, 907329, 1789989, 1299013, 1299045, 1791527, 907361, 1526852, 1659462, 1790021, 1939011, 1791559, 1659494, 1807970, 1790053, 1791591, 1526884, 1939043],
    [44, 5, 14, 385024, 1039360, 1170433, 1039392, 1170465, 1039424, 1170497, 1039456, 1170529, 1302018, 595969, 857090, 1302050, 1302082, 385056, 1302114, 596001, 385088, 857122, 596033, 385120, 596065, 857154, 906755, 842752, 1037828, 906787, 857186, 842784, 1037860, 1642499, 906819, 2036740, 1642531, 1037892, 906851, 2036772, 1037924, 1642563, 842816, 842848, 2036804, 1642595, 2036836],
    [40, 7, 14, 516097, 448512, 516129, 448544, 448576, 516161, 448608, 516193, 1038853, 1678850, 1906182, 1169414, 1579523, 1038885, 1565188, 1906214, 1169446, 1678882, 1038917, 1579555, 1906246, 1169478, 1678914, 2037765, 1038949, 1565220, 1498113, 1170022, 1579587, 1498145, 1678946, 1905766, 1579619, 1565252, 1498177, 2037797, 1498209, 2037829, 1565284, 2037861],
    [60, 6, 14, 1041408, 1172481, 1041440, 1172513, 1041472, 1172545, 1041504, 1172577, 604160, 450561, 604192, 604224, 450593, 604256, 450625, 866818, 450657, 1942020, 712704, 712736, 712768, 736771, 866850, 1566720, 712800, 980994, 1630210, 1566752, 736803, 866882, 1761283, 1566784, 736835, 866914, 982019, 1304069, 1566816, 736867, 1942052, 1304101, 1630242, 981026, 1761315, 1914885, 982051, 1942084, 1304133, 1630274, 981058, 1761347, 1914917, 982083, 981090, 1304165, 982115, 1942116, 1630306, 1914949, 1761379, 1914981],
    [32, 7, 14, 387072, 320513, 387104, 320545, 387136, 320577, 387168, 320609, 763396, 911361, 911393, 911425, 763428, 909826, 763460, 909858, 2074115, 909890, 909922, 911457, 1040902, 1040934, 763492, 1500677, 1500709, 1040966, 2074147, 1500741, 2074179, 1040998, 1500773, 2074211],
    [60, 10, 14, 944128, 1043456, 1174529, 1043488, 1174561, 1043520, 1174593, 1043552, 1174625, 1306114, 621569, 489987, 1306146, 490019, 1306178, 1306210, 913408, 621601, 490051, 566274, 566306, 913440, 621633, 490083, 944160, 913472, 621665, 566338, 884231, 566370, 944192, 913504, 779784, 779816, 884263, 1451524, 779848, 779880, 1582087, 944224, 1566217, 884295, 1321477, 1451556, 1566249, 1582119, 884327, 1321509, 1451588, 1566281, 1582151, 1451620, 1321541, 1582183, 1321573, 1539590, 1566313, 1539622, 1539654, 1539686],
    [48, 7, 14, 520192, 290306, 520224, 290338, 520256, 290370, 520288, 290402, 682499, 782339, 1469440, 1175553, 782883, 1600513, 682019, 1436164, 1175585, 1436196, 782915, 1469472, 1436228, 1600545, 1436260, 682051, 1175617, 782947, 959492, 1469504, 959524, 1600577, 1175649, 682083, 959556, 1829382, 959588, 1829414, 1469536, 1746950, 1583621, 1600609, 1746982, 1829446, 1583653, 1829478, 1747014, 1583685, 1583717, 1747046],
    [84, 11, 14, 421888, 1176576, 1307649, 1176608, 1307681, 1176640, 1307713, 1176672, 1307745, 505346, 374786, 1439235, 505378, 374818, 1439267, 421920, 505410, 374850, 1439299, 505442, 374882, 1439331, 421952, 870916, 768003, 741893, 768035, 421984, 870948, 768067, 741925, 768099, 684033, 1030149, 870980, 684065, 900615, 684097, 871012, 684129, 741957, 1292806, 1162760, 1030181, 737801, 741989, 900647, 882694, 737833, 872970, 1292838, 873002, 1276936, 1162792, 1030213, 873034, 900679, 873066, 737865, 882726, 1292870, 1177600, 1162824, 1030245, 1921030, 1276968, 900711, 737897, 882758, 2052104, 1277000, 1921062, 883302, 1292390, 1277544, 1162344, 1177632, 1177664, 2052136, 1921094, 1177696, 2052168, 1921126, 2052200],
    [48, 8, 14, 523264, 1700357, 422913, 1569282, 1569314, 476675, 422945, 1569346, 1569378, 422977, 1700389, 523296, 476707, 423009, 1700421, 523328, 476739, 523360, 1161734, 898054, 815620, 898598, 815652, 476771, 898630, 815684, 1700453, 815716, 1161254, 898662, 1863685, 654337, 654369, 654401, 1161286, 1865223, 654433, 1863717, 1865255, 1161318, 1863749, 1865287, 1947650, 1947682, 1863781, 1865319, 1947714, 1947746],
    [28, 4, 9, 785408, 916481, 785440, 916513, 785472, 916545, 785504, 916577, 376832, 507905, 376864, 507937, 376896, 652802, 652834, 1048067, 652866, 1048099, 652898, 1048131, 507969, 376928, 1048163, 508001, 1045507, 1045539, 1045571, 1045603],
    [44, 5, 8, 1456128, 653312, 653344, 653376, 653408, 784898, 915971, 784930, 784962, 638977, 784994, 1455106, 1586179, 639009, 916003, 916035, 1016834, 884739, 916067, 639041, 1016866, 884771, 1455138, 1047044, 639073, 1016898, 901120, 1586211, 1047076, 884803, 1047108, 1455170, 901152, 1016930, 1047140, 884835, 1586243, 901184, 1455202, 1586275, 901216, 1456160, 1456192, 1456224],
]
ROLES = [
    [0, 0, 5, 1, 6, 6, 7, 4, 0, 0, 1, 5, 2, 3],
    [0, 4, 6, 5, 2, 7, 8, 3, 1, 1, 7, 2, 3, 8],
    [0, 5, 8, 10, 9, 6, 4, 7, 11, 11, 13, 12, 2, 3],
    [0, 3, 5, 6, 10, 12, 8, 2, 11, 11, 9, 7, 4, 13],
    [0, 2, 10, 13, 11, 5, 3, 9, 6, 6, 8, 7, 4, 12],
    [0, 8, 10, 6, 9, 13, 11, 5, 7, 7, 4, 3, 2, 12],
    [0, 4, 8, 10, 9, 6, 5, 3, 13, 13, 12, 11, 2, 7],
    [0, 5, 3, 10, 7, 6, 2, 9, 12, 12, 8, 13, 11, 4],
    [0, 2, 7, 10, 8, 5, 4, 6, 3, 3, 11, 9, 13, 12],
    [0, 6, 2, 4, 7, 9, 8, 5, 10, 10, 12, 11, 3, 13],
    [0, 11, 7, 9, 8, 6, 5, 3, 10, 10, 12, 13, 2, 4],
    [0, 2, 8, 13, 5, 4, 3, 12, 9, 9, 6, 10, 7, 11],
    [0, 3, 6, 11, 7, 4, 2, 5, 8, 8, 10, 9, 13, 12],
    [0, 6, 2, 5, 7, 10, 3, 4, 8, 8, 12, 11, 13, 9],
    [0, 8, 4, 6, 5, 7, 3, 2, 9, 9, 10, 11, 0, 8],
    [0, 2, 3, 3, 6, 5, 7, 7, 8, 8, 0, 2, 1, 4],
    [5, 5, 11, 9, 4, 4, 10, 2, 0, 6, 1, 3, 8, 7],
    [9, 12, 3, 7, 6, 10, 4, 5, 1, 2, 14, 13, 8, 11],
    [11, 2, 10, 7, 9, 6, 4, 5, 2, 11, 7, 10, 8, 3],
    [6, 3, 8, 2, 9, 11, 7, 4, 10, 5, 11, 9, 4, 7],
    [8, 5, 9, 10, 2, 7, 6, 12, 3, 11, 4, 13, 15, 14],
    [5, 7, 4, 10, 9, 8, 3, 6, 2, 12, 11, 13, 15, 14],
    [9, 6, 7, 13, 10, 3, 4, 8, 15, 14, 5, 2, 11, 12],
    [3, 8, 2, 7, 9, 4, 10, 5, 12, 6, 13, 15, 14, 11],
    [10, 12, 7, 8, 11, 5, 3, 9, 4, 2, 6, 13, 15, 14],
    [5, 6, 3, 7, 9, 8, 4, 11, 2, 14, 13, 12, 15, 10],
    [12, 14, 6, 8, 2, 4, 3, 11, 10, 9, 15, 13, 7, 5],
    [7, 8, 3, 4, 10, 9, 6, 5, 13, 14, 11, 15, 12, 2],
    [2, 8, 11, 15, 4, 10, 9, 7, 3, 6, 5, 14, 12, 13],
    [12, 6, 5, 11, 9, 8, 2, 4, 3, 14, 10, 13, 7, 15],
    [13, 14, 8, 6, 3, 12, 10, 7, 2, 9, 5, 11, 0, 4],
    [8, 6, 2, 2, 9, 7, 11, 11, 4, 10, 0, 5, 1, 3],
    [5, 5, 7, 3, 6, 6, 8, 4, 0, 10, 1, 2, 11, 9],
    [9, 11, 5, 3, 10, 12, 6, 4, 1, 14, 8, 13, 2, 7],
    [4, 6, 10, 11, 5, 9, 7, 12, 2, 13, 14, 15, 3, 8],
    [3, 4, 7, 9, 13, 6, 8, 10, 14, 2, 11, 15, 12, 5],
    [3, 2, 9, 11, 8, 4, 6, 7, 2, 3, 11, 9, 10, 5],
    [3, 6, 8, 4, 10, 11, 9, 5, 7, 2, 11, 10, 5, 9],
    [4, 13, 9, 8, 6, 15, 2, 11, 3, 10, 14, 7, 5, 12],
    [7, 5, 8, 12, 11, 9, 10, 3, 15, 4, 6, 14, 2, 13],
    [14, 7, 8, 12, 2, 3, 4, 13, 9, 10, 5, 11, 15, 6],
    [3, 10, 5, 8, 12, 11, 6, 9, 15, 13, 4, 7, 2, 14],
    [2, 7, 6, 10, 3, 8, 5, 4, 14, 12, 15, 13, 11, 9],
    [10, 4, 12, 5, 9, 8, 13, 6, 15, 14, 3, 11, 2, 7],
    [15, 10, 6, 12, 2, 14, 7, 13, 8, 9, 3, 4, 11, 5],
    [13, 5, 11, 8, 14, 6, 12, 3, 7, 10, 2, 15, 9, 4],
    [3, 2, 6, 10, 4, 7, 9, 8, 11, 13, 12, 14, 0, 5],
    [2, 6, 10, 10, 4, 3, 11, 11, 7, 9, 0, 8, 1, 5],
    [5, 5, 8, 3, 6, 6, 7, 4, 0, 9, 1, 2, 11, 10],
    [4, 6, 2, 13, 3, 7, 11, 14, 1, 8, 12, 10, 9, 5],
    [5, 8, 11, 10, 7, 9, 2, 12, 3, 15, 4, 13, 6, 14],
    [6, 5, 10, 3, 9, 8, 12, 13, 2, 14, 4, 15, 11, 7],
    [6, 4, 9, 12, 3, 8, 7, 11, 2, 14, 10, 5, 15, 13],
    [4, 8, 7, 5, 13, 6, 11, 3, 10, 12, 14, 9, 2, 15],
    [11, 9, 6, 8, 7, 2, 5, 3, 9, 11, 8, 6, 10, 4],
    [2, 5, 9, 6, 10, 8, 4, 11, 7, 3, 8, 10, 11, 4],
    [4, 12, 6, 11, 14, 13, 10, 9, 5, 15, 3, 2, 8, 7],
    [10, 8, 3, 6, 13, 12, 7, 5, 2, 11, 4, 15, 14, 9],
    [4, 10, 9, 12, 11, 7, 2, 13, 3, 8, 5, 15, 14, 6],
    [9, 3, 14, 12, 8, 7, 4, 13, 2, 11, 5, 10, 6, 15],
    [15, 3, 4, 10, 7, 11, 2, 8, 5, 12, 6, 14, 9, 13],
    [12, 4, 5, 8, 7, 3, 13, 11, 2, 14, 9, 15, 10, 6],
    [14, 3, 10, 8, 5, 4, 13, 12, 6, 9, 2, 11, 0, 7],
    [3, 2, 10, 10, 5, 4, 11, 11, 6, 8, 0, 9, 1, 7],
    [10, 10, 6, 2, 11, 11, 8, 4, 0, 3, 1, 9, 7, 5],
    [5, 8, 4, 12, 6, 11, 2, 13, 1, 7, 3, 14, 10, 9],
    [13, 4, 6, 11, 15, 5, 3, 8, 9, 12, 10, 14, 2, 7],
    [2, 8, 5, 6, 10, 7, 4, 15, 12, 13, 9, 14, 3, 11],
    [11, 14, 8, 10, 2, 15, 7, 9, 3, 13, 4, 5, 6, 12],
    [3, 9, 2, 11, 12, 7, 10, 4, 13, 5, 6, 14, 8, 15],
    [2, 8, 10, 11, 7, 9, 5, 6, 14, 13, 4, 15, 3, 12],
    [9, 6, 13, 5, 7, 8, 2, 11, 15, 14, 10, 4, 3, 12],
    [2, 3, 8, 11, 10, 6, 7, 5, 3, 2, 11, 8, 9, 4],
    [2, 6, 8, 3, 11, 10, 5, 7, 9, 4, 10, 11, 7, 5],
    [10, 3, 5, 9, 13, 2, 6, 8, 12, 15, 7, 11, 4, 14],
    [10, 6, 4, 7, 11, 5, 3, 9, 13, 15, 12, 2, 8, 14],
    [12, 11, 2, 6, 15, 13, 5, 10, 7, 4, 8, 14, 9, 3],
    [11, 4, 7, 6, 12, 10, 9, 8, 3, 15, 5, 14, 2, 13],
    [3, 11, 7, 10, 5, 12, 8, 9, 13, 6, 2, 14, 0, 4],
    [3, 7, 8, 8, 4, 6, 9, 9, 2, 5, 0, 10, 1, 11],
    [11, 11, 10, 6, 3, 3, 8, 5, 0, 4, 1, 7, 2, 9],
    [6, 10, 8, 13, 5, 7, 2, 3, 1, 4, 11, 14, 12, 9],
    [5, 6, 11, 12, 8, 10, 2, 13, 3, 7, 4, 15, 9, 14],
    [2, 4, 9, 14, 6, 5, 13, 15, 12, 3, 7, 11, 8, 10],
    [5, 14, 7, 9, 6, 15, 8, 4, 2, 12, 3, 13, 10, 11],
    [10, 7, 2, 5, 11, 9, 4, 6, 3, 13, 14, 15, 8, 12],
    [8, 3, 7, 10, 9, 5, 2, 11, 12, 13, 4, 6, 15, 14],
    [8, 5, 15, 3, 7, 6, 2, 11, 9, 10, 4, 12, 13, 14],
    [9, 7, 4, 12, 10, 8, 6, 13, 2, 11, 3, 5, 14, 15],
    [8, 6, 2, 5, 10, 7, 9, 11, 4, 14, 12, 15, 13, 3],
    [8, 4, 11, 10, 9, 5, 3, 6, 4, 8, 10, 11, 7, 2],
    [6, 5, 7, 3, 8, 10, 2, 11, 9, 4, 10, 8, 11, 2],
    [13, 4, 7, 10, 5, 11, 6, 8, 3, 14, 9, 12, 2, 15],
    [12, 4, 7, 10, 11, 3, 8, 13, 2, 5, 14, 15, 6, 9],
    [7, 3, 10, 9, 8, 5, 12, 11, 4, 14, 2, 13, 0, 6],
    [6, 5, 10, 10, 8, 7, 3, 3, 2, 11, 0, 4, 1, 9],
    [10, 10, 7, 4, 11, 11, 9, 6, 0, 2, 1, 5, 3, 8],
    [2, 8, 4, 13, 7, 12, 5, 14, 1, 11, 6, 9, 3, 10],
    [2, 6, 8, 14, 3, 7, 5, 9, 10, 11, 13, 12, 4, 15],
    [11, 8, 2, 6, 10, 12, 7, 4, 14, 9, 3, 13, 5, 15],
    [3, 14, 6, 15, 4, 7, 5, 9, 8, 12, 11, 2, 10, 13],
    [11, 8, 10, 7, 9, 5, 4, 6, 2, 12, 15, 3, 13, 14],
    [5, 4, 6, 8, 2, 11, 3, 13, 10, 12, 14, 15, 7, 9],
    [10, 7, 2, 6, 9, 8, 13, 3, 11, 14, 4, 15, 5, 12],
    [13, 2, 6, 8, 3, 4, 5, 9, 7, 11, 10, 12, 14, 15],
    [10, 7, 3, 4, 9, 8, 11, 2, 6, 13, 12, 14, 15, 5],
    [3, 13, 5, 8, 4, 6, 7, 9, 10, 15, 14, 11, 2, 12],
    [9, 3, 4, 2, 10, 7, 8, 11, 14, 15, 5, 12, 6, 13],
    [4, 11, 9, 7, 10, 6, 3, 5, 11, 4, 7, 9, 8, 2],
    [4, 2, 7, 3, 8, 10, 9, 6, 11, 5, 10, 8, 6, 9],
    [4, 2, 10, 11, 6, 8, 12, 13, 7, 9, 14, 5, 0, 3],
    [4, 6, 7, 7, 9, 10, 11, 11, 5, 8, 0, 3, 1, 2],
    [2, 2, 6, 3, 4, 4, 1, 7, 0, 5, 1, 7, 8, 8],
    [7, 5, 3, 6, 4, 2, 1, 9, 1, 9, 8, 10, 11, 11],
    [4, 3, 5, 8, 2, 6, 1, 9, 12, 13, 11, 7, 10, 10],
    [9, 3, 7, 5, 8, 4, 1, 6, 11, 12, 10, 13, 2, 2],
    [2, 3, 6, 8, 12, 4, 1, 9, 7, 5, 10, 11, 13, 13],
    [10, 4, 8, 6, 9, 5, 1, 7, 2, 3, 11, 12, 13, 13],
    [5, 3, 2, 8, 6, 4, 1, 7, 10, 11, 9, 12, 13, 13],
    [9, 6, 7, 10, 8, 5, 1, 4, 11, 2, 12, 3, 13, 13],
    [2, 8, 5, 6, 3, 11, 1, 7, 4, 9, 13, 12, 10, 10],
    [9, 2, 7, 11, 8, 6, 1, 5, 3, 4, 10, 13, 12, 12],
    [11, 9, 2, 10, 6, 8, 1, 13, 3, 12, 4, 7, 5, 5],
    [9, 4, 7, 3, 8, 6, 1, 2, 12, 13, 10, 5, 11, 11],
    [6, 5, 3, 11, 8, 10, 1, 12, 2, 4, 7, 9, 13, 13],
    [10, 2, 8, 4, 9, 5, 1, 7, 6, 3, 11, 12, 13, 13],
    [8, 2, 6, 5, 7, 3, 1, 4, 2, 8, 5, 6, 0, 0],
    [3, 2, 5, 5, 6, 0, 1, 1, 7, 4, 0, 6, 1, 1],
]


def fill_table(tbl, me, lo, hi):
    if hi - lo == 1:
        head = SENDS[lo]
        for place, word in enumerate(head):
            tbl[place] = jnp.int32(word)
        return
    mid = (lo + hi) // 2
    lax.cond(
        me < mid,
        lambda: fill_table(tbl, me, lo, mid),
        lambda: fill_table(tbl, me, mid, hi),
    )


def spread_kernel(stored_ref, slots_ref, tbl, own_sem, send_sem, recv_sem):
    rows_per = stored_ref.shape[2] // CHUNKS
    row_count = lax.axis_size("row")
    me = lax.axis_index("col") * row_count + lax.axis_index("row")
    fill_table(tbl, me, 0, len(SENDS))
    own = [
        pltpu.make_async_copy(stored_ref.at[lane, 0], slots_ref.at[lane], own_sem.at[lane])
        for lane in range(2)
    ]
    for copy in own:
        copy.start()

    def hop(source, target, slot, chunk, place):
        return pltpu.make_async_remote_copy(
            src_ref=source,
            dst_ref=slots_ref.at[slot, pl.ds(chunk * rows_per, rows_per)],
            send_sem=send_sem.at[place],
            recv_sem=recv_sem.at[slot, chunk],
            device_id={"col": target // row_count, "row": lax.rem(target, row_count)},
            device_id_type=MESH,
        )

    def arrival(slot, chunk):
        piece = slots_ref.at[slot, pl.ds(chunk * rows_per, rows_per)]
        hop(piece, me, slot, chunk, 0).wait_recv()

    sends = tbl[0]

    @pl.loop(0, sends)
    def _(place):
        word = tbl[3 + place]
        slot = word & 31
        chunk = (word >> 5) & 15
        target = (word >> 10) & 127
        landing = word >> 17

        @pl.when(((word >> 9) & 1) == 1)
        def _():
            arrival(slot, chunk)

        @pl.when(slot < 2)
        def _():
            piece = stored_ref.at[slot, 0, pl.ds(chunk * rows_per, rows_per)]
            hop(piece, target, landing, chunk, place).start()

        @pl.when(slot >= 2)
        def _():
            piece = slots_ref.at[slot, pl.ds(chunk * rows_per, rows_per)]
            hop(piece, target, landing, chunk, place).start()

    @pl.loop(tbl[1], tbl[2])
    def _(slot):
        for chunk in range(CHUNKS):
            arrival(slot, chunk)

    @pl.loop(0, sends)
    def _(place):
        piece = slots_ref.at[0, pl.ds(0, rows_per)]
        hop(piece, me, 0, 0, place).wait_send()

    for copy in own:
        copy.wait()


def spread(stored):
    return pl.pallas_call(
        spread_kernel,
        out_shape=jax.ShapeDtypeStruct((SLOTS,) + stored.shape[2:], jnp.float32),
        in_specs=[pl.BlockSpec(memory_space=pl.ANY)],
        out_specs=pl.BlockSpec(memory_space=pl.ANY),
        scratch_shapes=[
            pltpu.SMEM((max(len(entry) for entry in SENDS),), jnp.int32),
            pltpu.SemaphoreType.DMA((2,)),
            pltpu.SemaphoreType.DMA((max(entry[0] for entry in SENDS),)),
            pltpu.SemaphoreType.DMA((SLOTS, CHUNKS)),
        ],
        compiler_params=pltpu.CompilerParams(has_side_effects=True),
        name="spread",
    )(stored)


def rank_in(row_list, lookup_keys):
    positions = jnp.arange(row_list.shape[0], dtype=jnp.int32)
    matches = row_list == lookup_keys[..., None]
    return jnp.sum(jnp.where(matches, positions, 0), -1)


def tile_cols(tile_rows, offsets, tile_x, tile_y):
    offsets_both = jnp.concatenate([offsets[tile_x, tile_y], offsets[tile_y, tile_x]])
    return jnp.bitwise_xor(tile_rows[tile_x][:, None], offsets_both[None, :])


def assemble(own_half, mirror, tile_rows, offsets, tile_x, tile_y):
    half_slots = own_half.shape[1]
    mirror_rows = jnp.bitwise_xor(tile_rows[tile_x][:, None], offsets[tile_y, tile_x][None, :])
    position = rank_in(tile_rows[tile_y], mirror_rows)
    picked = mirror[position, jnp.arange(half_slots, dtype=jnp.int32)[None, :]]
    return jnp.concatenate([own_half, jnp.swapaxes(picked, -1, -2)], 1)


def lane_terms(vals_a, vals_b, cols_a, cols_b, rows_i, rows_k, want_rows, want_cols, live_count):
    kept_slots = want_rows.shape[0]
    block_size = vals_a.shape[-1]
    is_live = jnp.arange(kept_slots, dtype=jnp.int32) < live_count
    position = rank_in(rows_k, cols_a)
    summed = jnp.zeros((kept_slots, block_size * block_size), jnp.float32)
    for slot in range(vals_a.shape[1]):
        picked = vals_b[position[:, slot]]
        picked_cols = cols_b[position[:, slot]]
        products = jnp.einsum(
            "eij,ebjk->ebik", vals_a[:, slot], picked, precision=lax.Precision.HIGHEST
        )
        weights = (
            (rows_i[None, :, None] == want_rows[:, None, None])
            & (picked_cols[None] == want_cols[:, None, None])
            & is_live[:, None, None]
        ).astype(jnp.float32)
        summed = summed + jnp.dot(
            weights.reshape(kept_slots, -1),
            products.reshape(-1, block_size * block_size),
            precision=lax.Precision.HIGHEST,
        )
    return summed.reshape(kept_slots, block_size, block_size)


def local(stored, tile_rows, offsets, kept_rows, kept_cols, kept_count):
    grid_size = lax.axis_size("row")
    row_id = lax.axis_index("row")
    col_id = lax.axis_index("col")
    me = col_id * grid_size + row_id
    lane_count = stored.shape[0]
    slots = spread(stored)
    roles = jnp.asarray(np.array(ROLES, np.int32))[me]
    results = []
    for lane in range(lane_count):
        tile_i = col_id * lane_count + lane
        summed = jnp.zeros((kept_rows.shape[-1],) + stored.shape[-2:], jnp.float32)
        for step in range(2):
            tile_k = (tile_i + row_id + step) % grid_size
            left = 2 * (2 * lane + step)
            right = 8 + 2 * (lane + step)
            vals_a = assemble(slots[roles[left]], slots[roles[left + 1]], tile_rows, offsets, tile_i, tile_k)
            vals_b = assemble(slots[roles[right]], slots[roles[right + 1]], tile_rows, offsets, tile_k, row_id)
            summed = summed + lane_terms(
                vals_a, vals_b,
                tile_cols(tile_rows, offsets, tile_i, tile_k),
                tile_cols(tile_rows, offsets, tile_k, row_id),
                tile_rows[tile_i], tile_rows[tile_k],
                kept_rows[lane, 0], kept_cols[lane, 0], kept_count[lane, 0],
            )
        results.append(summed)
    return jnp.stack(results)[:, None]


def solution(mesh):
    in_specs = (
        P("col", "row", None, None, None, None),
        P(),
        P(),
        P("col", "row", None),
        P("col", "row", None),
        P("col", "row"),
    )
    out_specs = P("col", "row", None, None, None)
    return jax.shard_map(local, mesh=mesh, in_specs=in_specs, out_specs=out_specs, check_vma=False)
```

```python
import jax
import jax.numpy as jnp
import numpy as np
from jax import lax
from jax.experimental import pallas as pl
from jax.experimental.pallas import tpu as pltpu
from jax.sharding import PartitionSpec as P

MESH = pl.DeviceIdType.MESH
CHUNKS = 2
SLOTS = 21
SENDS = [
    [32, 12, 16, 539648, 1442817, 1442849, 427523, 527363, 361986, 362018, 790020, 427555, 527395, 1574408, 790052, 2070025, 1213958, 1022469, 1213990, 1022501, 1016327, 801793, 1016359, 1574440, 1329161, 539680, 1147402, 1704970, 1329705, 1705514, 801825, 1146922, 2197003, 2069545, 2197035],
    [32, 11, 14, 1572864, 1703937, 1572896, 1703969, 886275, 948741, 886307, 1821701, 1966600, 1868295, 1323526, 1835014, 948773, 932865, 1323558, 1835046, 852484, 1868327, 1410054, 1821733, 1966632, 852516, 932897, 1476105, 931840, 1410086, 1476137, 2000394, 1444354, 931872, 2000426, 1444386],
    [32, 12, 18, 278528, 1673216, 278560, 1969672, 412162, 409091, 1804804, 409123, 412194, 560645, 787457, 1838598, 1083911, 787489, 560677, 1310720, 1673248, 1908233, 1310752, 1838630, 1983496, 1969704, 1083943, 1804836, 2114566, 1983528, 1871370, 1908265, 1150475, 2114598, 1150507, 1871402],
    [36, 12, 17, 1574912, 656385, 1705985, 1574944, 1706017, 1543168, 1674241, 411140, 675331, 437766, 542213, 411172, 2067976, 1837064, 670210, 675363, 656417, 670242, 437798, 542245, 1064960, 1064992, 2066953, 1327623, 1837608, 1543200, 1327655, 1740298, 1674273, 2113542, 1117707, 2066985, 1117739, 2067496, 2113574, 1740330],
    [30, 12, 20, 364544, 1483777, 1050625, 364576, 400900, 524802, 400932, 524834, 630275, 1282049, 630307, 794117, 794149, 2330626, 1282081, 983559, 1938954, 1206792, 1050657, 983591, 1483809, 1206824, 1059337, 2330658, 2349579, 1059369, 1938986, 2349611, 1449478, 1449510],
    [42, 13, 15, 532480, 1576960, 393217, 1708033, 1576992, 1708065, 557570, 557602, 393249, 758275, 532512, 1839620, 758307, 786436, 1839652, 951299, 1676289, 786468, 951331, 918528, 1970695, 918560, 924165, 1970727, 1055238, 1807882, 1181193, 1562633, 1606152, 1676321, 1181225, 1562665, 924197, 1312267, 1807914, 1055270, 1312299, 2494988, 1606184, 2495020, 1380358, 1380390],
    [20, 9, 17, 267264, 267296, 529409, 529441, 547330, 547362, 564740, 1187334, 564772, 1360902, 1185283, 1187366, 1185315, 1693189, 2300423, 1360934, 2170376, 1693221, 2300455, 2170408],
    [34, 8, 15, 272384, 1185792, 465921, 1316865, 1185824, 1316897, 272416, 465953, 1201666, 728579, 1201698, 1335299, 728611, 657410, 1065984, 657442, 1579527, 583174, 1181702, 1448453, 941572, 583206, 1448485, 941604, 1645568, 1335331, 1677317, 1066016, 1446913, 1579559, 1446945, 1181734, 1645600, 1677349],
    [34, 11, 20, 528384, 698884, 528416, 890376, 1451526, 799234, 535554, 696326, 536098, 682499, 698916, 1123329, 798754, 682531, 792577, 696870, 1451046, 1183752, 1615370, 1324042, 1184296, 792609, 889896, 1841671, 1123361, 1580549, 1842697, 1615402, 1324074, 2301952, 1841703, 2301984, 1580581, 1842729],
    [28, 10, 16, 322560, 1449984, 499713, 1581057, 1450016, 1581089, 435715, 322592, 659457, 435747, 659489, 525826, 921600, 499745, 921632, 525858, 2368008, 666118, 1516036, 2484745, 2236935, 1811973, 666150, 1516068, 2236967, 1812005, 2368040, 2484777],
    [20, 9, 16, 436224, 276481, 276513, 1319936, 436256, 1319968, 1862147, 1237506, 1617413, 1237538, 1289732, 1289764, 2386438, 1617445, 1715719, 1862179, 2386470, 1977864, 1715751, 1977896],
    [36, 12, 17, 1189888, 402433, 1320961, 1189920, 1320993, 402465, 806912, 408066, 1223680, 408098, 811523, 806944, 801285, 1354753, 801317, 2125322, 1153540, 811555, 1223712, 1354785, 2256391, 1974792, 1728520, 1153572, 1974824, 1728552, 1583625, 2141707, 1583657, 2256900, 2258438, 2125354, 2256932, 2141739, 2258470, 2256423],
    [32, 11, 17, 1748992, 273408, 360448, 1056769, 273440, 360480, 308739, 1882626, 308771, 1880065, 1056801, 1455624, 1188359, 2142726, 1424900, 1017353, 1586185, 1188391, 1424932, 1455656, 1080842, 1017385, 1586217, 1442309, 1749024, 1080874, 1442341, 1880097, 2258953, 2258985, 2142758, 1882658],
    [36, 11, 18, 293888, 1454080, 262145, 1585153, 1454112, 1585185, 293920, 262177, 1342978, 394242, 1343010, 817669, 2012161, 394274, 1716739, 788998, 949251, 917504, 817701, 1716771, 917536, 949283, 789030, 2143753, 671239, 671271, 2012193, 2029066, 1866759, 1980936, 2143785, 2112004, 1866791, 2029098, 1980968, 2112036],
    [18, 8, 17, 795138, 668672, 1864195, 795170, 668704, 554502, 554534, 1191937, 835077, 1864227, 1191969, 835109, 2109956, 2109988, 1820167, 1195015, 1195559, 1819687],
    [24, 9, 11, 1062912, 275457, 1193985, 1062944, 1194017, 1458692, 377856, 275489, 1849864, 377888, 571907, 571939, 1456646, 1847810, 1328647, 1458724, 1280006, 1847842, 1587717, 1280550, 1456166, 1587749, 1328679, 1849896],
    [40, 14, 18, 816128, 526336, 1721861, 1048576, 638976, 423426, 639008, 806406, 1051649, 573956, 526368, 806438, 1721893, 573988, 663043, 423458, 979463, 663075, 1048608, 816160, 1051681, 1819147, 1968652, 979495, 1822725, 1855492, 1339912, 2183690, 1819179, 1787401, 1470465, 1339944, 2183722, 2100749, 1822757, 1968684, 1470497, 1787433, 1855524, 2100781],
    [38, 13, 17, 507904, 263169, 507936, 395778, 263201, 395810, 1078273, 905733, 1884680, 808451, 1049600, 644612, 808483, 1330180, 644644, 905765, 1365510, 1199623, 1365542, 1049632, 1078305, 1558026, 2099723, 1982475, 1199655, 1851913, 2230796, 2244620, 1330212, 2115586, 1851945, 1884712, 1558058, 2115618, 2099755, 1982507, 2230828, 2244652],
    [34, 12, 17, 1589248, 424961, 424993, 1077764, 1461252, 1604608, 673283, 646658, 646690, 642565, 1461796, 642597, 871942, 673315, 969223, 1820672, 1592840, 969255, 1952769, 1077284, 1592872, 1723915, 871974, 1854986, 1604640, 1723947, 1590273, 2149897, 1855018, 1820704, 1589280, 1952801, 2149929, 1590305],
    [34, 11, 16, 510976, 511008, 1591810, 1591842, 577027, 1735681, 655362, 676356, 577059, 818694, 1722374, 655394, 676388, 1722918, 804357, 818214, 804389, 1985034, 1315846, 2279943, 1459200, 2083841, 1853961, 1315878, 1720321, 1735713, 1853993, 2182664, 2279975, 1985066, 1459232, 2083873, 2182696, 1720353],
    [36, 11, 18, 279552, 279584, 265217, 348674, 513026, 265249, 348706, 872966, 513058, 774144, 809475, 872998, 775684, 933892, 892421, 934436, 892453, 1167880, 809507, 774176, 1314314, 1463306, 775204, 1332745, 1197057, 1167912, 1332777, 1691649, 1314346, 1463338, 1197089, 1446407, 2201607, 1691681, 1446439, 2201639],
    [24, 9, 18, 381953, 398850, 802816, 381985, 398882, 802848, 907780, 1707009, 1462791, 907812, 1071619, 934913, 1462823, 1071651, 934945, 1707041, 2184710, 2000903, 1333765, 1593864, 1333797, 1593896, 2184742, 2000935],
    [32, 11, 17, 542721, 413186, 544768, 1203715, 413218, 544800, 542753, 1203747, 936452, 839174, 936484, 664582, 839206, 1460224, 1231368, 664614, 1075200, 1460256, 1231400, 2232839, 1075232, 1232394, 1724423, 2232871, 1725957, 1232426, 2103817, 1724455, 2578432, 1725989, 2578464, 2103849],
    [26, 9, 17, 482304, 282625, 1464836, 282657, 420354, 482336, 420386, 1595909, 939008, 936964, 533508, 1464868, 1595941, 1204739, 533540, 1204771, 939040, 936996, 1070598, 1070630, 1985537, 1858056, 1985569, 1858088, 1493511, 1493543],
    [28, 11, 19, 414720, 483328, 414752, 502274, 483360, 502306, 582147, 909828, 1157640, 582179, 909860, 1025541, 685575, 1331201, 1726469, 685607, 1499657, 1157672, 1308166, 1400833, 1025573, 1331233, 1726501, 1308198, 1400865, 1499689, 2155018, 2155050],
    [28, 10, 16, 547840, 289282, 615425, 289314, 547872, 676865, 1023491, 1466371, 946692, 1466915, 1599492, 676897, 615457, 1023011, 1597958, 946724, 1599524, 1597990, 1209864, 1859592, 1993223, 1991177, 1445381, 1993255, 1209896, 1859624, 1445413, 1991209],
    [30, 10, 20, 286720, 423937, 286752, 415745, 926212, 366082, 415777, 366114, 423969, 584195, 1334272, 926244, 681478, 805381, 584227, 681510, 805413, 1763328, 1334304, 1210372, 1601031, 1763360, 2086916, 1601063, 1210404, 1895944, 2086948, 1895976, 1467913, 1467945],
    [38, 10, 19, 781313, 584704, 649731, 1337347, 293378, 548865, 649763, 1337379, 293410, 781345, 548897, 584736, 1465345, 812032, 1174022, 1468422, 1198081, 796167, 812064, 1174054, 1633281, 1193480, 1730568, 1468454, 1465377, 1198113, 1731112, 1208837, 1633313, 796199, 1205769, 1193000, 2127877, 1208869, 1205801, 2127909, 1845764, 1845796],
    [40, 13, 18, 287744, 287776, 643587, 637442, 585728, 1340932, 418817, 667650, 637474, 585760, 418849, 667682, 900613, 1340964, 849415, 687622, 900645, 1619971, 980488, 643619, 1182724, 687654, 1182756, 849447, 1752070, 2332680, 980520, 1896449, 2275849, 1996298, 1620003, 2127371, 1490444, 1996330, 2332712, 1896481, 2127403, 1490476, 2275881, 1752102],
    [22, 10, 18, 325632, 324609, 325664, 324641, 1473027, 1733122, 1196548, 1406469, 1733154, 1196580, 1866246, 943105, 1406501, 1852935, 1997320, 943137, 1473059, 1866278, 1852967, 1997352, 2290185, 2290217],
    [30, 10, 18, 421888, 420865, 274433, 420897, 274465, 1338368, 421920, 622082, 622114, 1338400, 1061380, 1141251, 947719, 1474053, 1061412, 1474085, 1068033, 1296902, 947751, 1141283, 1296934, 1068065, 1506825, 1062408, 1297408, 1506857, 1062440, 1297440, 2018307, 2018339],
    [24, 10, 15, 379905, 552960, 1341955, 379937, 673792, 1341987, 673824, 552992, 1469441, 292356, 701958, 292388, 1732101, 1469473, 1603074, 701990, 1732133, 1604104, 1734151, 1735177, 1603106, 1604136, 1735209, 1734183],
    [38, 13, 18, 266240, 1353729, 266272, 430595, 443906, 313860, 430627, 443938, 313892, 660997, 1351174, 1613827, 661029, 1249284, 966152, 853511, 1613859, 1228298, 966184, 1349129, 853543, 1353761, 1349161, 851468, 1868812, 1577985, 1228330, 1578017, 1351206, 1249316, 2263563, 851500, 1868844, 2535424, 2001929, 2263595, 2535456, 2001961],
    [34, 13, 16, 458752, 307201, 458784, 1737220, 307233, 831488, 962564, 562690, 831520, 1737252, 719368, 562722, 792070, 591365, 962596, 1477127, 591397, 1085961, 850442, 792102, 570375, 1477159, 1085993, 719400, 1314817, 570407, 850474, 1314849, 1487363, 1487395, 2261516, 2130443, 2130475, 2261548],
    [24, 9, 18, 264192, 309248, 264224, 1082883, 331266, 309280, 1179649, 331298, 1345029, 593412, 1082915, 593444, 1345061, 1216006, 1379847, 1179681, 1216038, 1379879, 1738248, 1738280, 2249734, 1094657, 1094689, 2249766],
    [26, 9, 16, 671744, 440321, 658433, 671776, 658465, 440353, 1575936, 441344, 2159109, 1575968, 441376, 1739268, 1101314, 1608198, 1200643, 1608230, 1200675, 1739300, 1101346, 2249224, 1870343, 1111046, 1870375, 1111078, 2159141, 2249256],
    [34, 11, 17, 397313, 1347079, 397345, 1480194, 2101248, 594435, 1612803, 1480226, 594467, 1477634, 957957, 1612835, 1611270, 988676, 1081344, 988708, 1743369, 957989, 1240584, 1081376, 1611302, 1240616, 1643525, 2185224, 2101280, 1347111, 1606657, 1643557, 1743401, 2185256, 1873418, 1606689, 1477666, 1873450],
    [30, 11, 15, 558080, 843266, 1478658, 558112, 1610245, 1479202, 1119747, 875012, 922628, 875044, 922660, 1741318, 1610277, 2363392, 842786, 1343489, 1119779, 1709057, 1744392, 1872391, 2267657, 1741350, 1343521, 2003466, 1872423, 2363424, 2003498, 1709089, 1744424, 2267689],
    [24, 11, 19, 428032, 366592, 366624, 300546, 841219, 300578, 399361, 399393, 428064, 823813, 925190, 841251, 1252872, 824836, 990727, 823845, 990759, 824868, 925222, 1742346, 1252904, 1742378, 2150921, 2150953],
    [36, 12, 16, 690177, 712195, 690209, 1874442, 535042, 1234438, 822272, 535074, 961028, 840197, 712227, 1416192, 822304, 961060, 1234470, 1612297, 1547265, 840229, 1481224, 2019337, 1840129, 1481256, 1416224, 2020362, 2136587, 1612329, 2151943, 1547297, 1840161, 1874474, 2282507, 2019369, 2136619, 2020394, 2151975, 2282539],
    [24, 9, 20, 954368, 269313, 269345, 431618, 1745922, 700416, 431650, 1745954, 692740, 846341, 700448, 826886, 846373, 1024001, 692772, 826918, 954400, 1024033, 981507, 981539, 1223176, 1223208, 1748487, 1748519],
    [36, 13, 19, 438273, 438305, 1712642, 454147, 601088, 1712674, 595460, 454179, 601120, 439813, 595492, 561670, 439845, 561702, 1092103, 950274, 987656, 1351688, 950306, 1092135, 2269708, 1483274, 955392, 987688, 1351720, 1355782, 1485321, 1483306, 955424, 1355814, 964107, 1636361, 1485353, 964139, 2269740, 1636393],
    [38, 13, 18, 301056, 860161, 301088, 697858, 1486346, 962053, 697890, 694273, 828932, 828964, 1108483, 731136, 1103366, 1092614, 694305, 962085, 731168, 1103398, 1092646, 860193, 970757, 1745415, 1363975, 970789, 1108515, 1893900, 1714697, 1745447, 1359368, 1486378, 1364007, 1714729, 1893932, 1359400, 2315274, 2013707, 2315306, 2013739],
    [22, 7, 18, 338945, 338977, 1664000, 1251843, 1846789, 1219584, 1780736, 1780768, 1349633, 1189378, 1191428, 1251875, 1219616, 1349665, 1191460, 1664032, 1189410, 1878534, 1846821, 1620998, 1878566, 1621030],
    [38, 12, 21, 1650688, 425984, 457728, 426016, 457760, 396802, 471555, 396834, 471587, 819201, 1226246, 864773, 762881, 799750, 704007, 1781761, 1226278, 864805, 762913, 819233, 704039, 2073603, 799782, 1650720, 958984, 1212419, 1781793, 1915396, 959016, 1212451, 1375754, 1375786, 928265, 2010635, 928297, 2073635, 2010667, 1915428],
    [24, 9, 18, 1242112, 565249, 588801, 588833, 798210, 588291, 565281, 798242, 1618437, 1090560, 588323, 1782785, 1751558, 1090592, 1112580, 1618469, 1112612, 1242144, 1782817, 2273799, 1751590, 2404872, 2273831, 2404904],
    [18, 8, 18, 305152, 303105, 305184, 454657, 303137, 1619458, 454689, 1750531, 1357316, 1357348, 1619490, 998917, 2667015, 1750563, 998949, 1128966, 1128998, 2667047],
    [24, 11, 14, 567297, 567329, 1106434, 829440, 1096195, 829472, 604676, 1227269, 1096227, 661509, 1358342, 662053, 604708, 1226789, 1358374, 1106466, 2216455, 1489416, 1489448, 1955337, 1637898, 2216487, 1637930, 1955369],
    [24, 10, 17, 409601, 710146, 688128, 451584, 409633, 451616, 688160, 559620, 710178, 848390, 714245, 559652, 848422, 1100291, 1100323, 2272775, 714277, 1492489, 1363464, 1106945, 1492521, 1106977, 1363496, 2272807],
    [28, 9, 15, 295936, 295968, 1360386, 1360418, 825859, 820225, 820257, 838148, 825891, 1710599, 1490951, 838180, 1491495, 1972226, 975873, 1710119, 1362437, 2146824, 1362469, 975905, 1113090, 1711112, 1113122, 1972258, 2146856, 1711144, 2024966, 2024998],
    [30, 12, 19, 326656, 318465, 1214465, 326688, 318497, 1214497, 705026, 705058, 678403, 678435, 1067008, 2054144, 1067040, 1623559, 1105412, 1475081, 1236485, 1072648, 1475113, 1072680, 1521158, 1105444, 1728010, 2054176, 1521190, 1728042, 1236517, 1754635, 1623591, 1754667],
    [34, 11, 17, 281600, 281632, 489986, 543745, 490018, 1624579, 543777, 581124, 1624611, 1755653, 581156, 977921, 1012741, 1013285, 1104392, 1277446, 2017286, 1755173, 977953, 2120706, 1277478, 2017318, 2322436, 1622535, 2186241, 1622567, 1104424, 1609225, 1609257, 2186273, 2120738, 2411018, 2411050, 2322468],
    [32, 11, 17, 319488, 319520, 1494530, 455681, 455713, 563715, 937984, 1627657, 563747, 1494562, 1069057, 956932, 938016, 956964, 1069089, 1089029, 1496582, 1791495, 1089061, 2005001, 1858562, 1496614, 1875464, 2421258, 1791527, 1627689, 2006018, 2005033, 1858594, 1875496, 2421290, 2006050],
    [28, 11, 18, 283649, 283681, 302594, 1495042, 545792, 302626, 1495074, 842245, 545824, 580100, 1626627, 1626659, 580132, 1135112, 842277, 1135144, 1218055, 1368586, 1497606, 2053130, 1218087, 1368618, 2398211, 1497638, 2160137, 2053162, 2398243, 2160169],
    [30, 10, 16, 550912, 312321, 613891, 1629187, 312353, 448002, 550944, 613923, 1760774, 448034, 1629219, 1217028, 1137157, 1825793, 1086470, 1137189, 1760806, 1217060, 1989128, 2015232, 1086502, 1594376, 1825825, 1348103, 1891849, 1989160, 1348135, 2015264, 1594408, 1891881],
    [38, 12, 15, 321537, 434176, 810498, 321569, 434208, 777731, 790529, 1370114, 790561, 777763, 578052, 1366533, 810530, 578084, 967680, 967712, 2087937, 1366565, 1757702, 1268736, 1268768, 1628680, 1370146, 1759753, 2317314, 1889285, 1757734, 1890826, 1628712, 2317346, 1759785, 2087969, 1889317, 2021899, 1900039, 1890858, 1900071, 2021931],
    [34, 12, 19, 516096, 587266, 574464, 516128, 587298, 1088003, 574496, 572932, 702981, 1369606, 1302529, 572964, 703013, 2056715, 1631753, 834055, 1302561, 2157579, 1369638, 2029572, 1088035, 1631785, 1879562, 1098753, 910856, 834087, 910888, 1911819, 2158123, 1879594, 1098785, 2056235, 2029604, 1911851],
    [26, 10, 16, 386049, 566786, 1317889, 566818, 453123, 386081, 453155, 679936, 679968, 705537, 2025989, 705569, 1761798, 1097728, 2270729, 1097760, 2157063, 2026021, 1761830, 2157095, 1885700, 2417160, 1317921, 1885732, 2417192, 2270761],
    [36, 13, 17, 486400, 486432, 720386, 707585, 2027019, 2316803, 720418, 1008132, 1762821, 1138182, 1764874, 707617, 1058313, 1008164, 1661448, 2252804, 1138214, 1090055, 1090087, 2119680, 1887232, 1058345, 1762853, 1764906, 1989633, 1844231, 2027051, 2119712, 1887264, 1661480, 1989665, 2316835, 2420236, 1844263, 2252836, 2420268],
    [28, 11, 19, 314369, 1500674, 314401, 1400324, 878592, 1232896, 711171, 945670, 814597, 711203, 814629, 878624, 945702, 1500706, 1207816, 1894921, 1400356, 2552327, 1207848, 1894953, 1232928, 1797121, 1797153, 1892874, 2531338, 1892906, 2531370, 2552359],
    [28, 12, 20, 356352, 316417, 356384, 316449, 541186, 578560, 1374723, 541218, 578592, 1404929, 2011652, 1404961, 2122249, 965130, 1374755, 1373704, 1630726, 2384395, 2011684, 1373736, 1630758, 1888773, 2122281, 2132487, 1888805, 965162, 2132519, 2384427],
    [30, 9, 17, 474112, 311297, 297474, 311329, 297506, 575488, 488449, 474144, 1634819, 488481, 1505796, 919556, 1634851, 1336837, 952325, 1765895, 575520, 1336869, 1881090, 952357, 920100, 2274822, 1765927, 953347, 1881122, 953379, 1505316, 2028040, 2274854, 2028072],
    [26, 9, 17, 448512, 569345, 569377, 1488386, 448544, 785409, 785441, 689667, 715778, 706561, 689699, 716322, 1487906, 1504773, 1432068, 1432100, 706593, 1635846, 1244679, 1713155, 1244711, 1897992, 1504805, 1635878, 1713187, 1898024],
    [22, 9, 15, 280576, 324098, 280608, 449537, 324130, 717315, 449569, 717347, 843776, 1502210, 843808, 970245, 1766916, 1502242, 970277, 1899014, 1767943, 1766948, 2161160, 1767975, 1899046, 2161192],
    [20, 9, 16, 598016, 334848, 334880, 346626, 346658, 598048, 724993, 725025, 1920517, 2462211, 1381892, 1920549, 1382919, 1381924, 1257990, 1382951, 2462243, 1902088, 1258022, 1902120],
    [28, 9, 15, 294912, 294944, 1376771, 463362, 602112, 929793, 596993, 463394, 597025, 602144, 929825, 867331, 1376803, 723460, 1507845, 723492, 1254401, 867363, 735750, 1769478, 1507877, 735782, 1769510, 1254433, 2165255, 2427400, 2165287, 2427432],
    [28, 9, 19, 444416, 442369, 1274370, 444448, 442401, 600064, 837124, 1345536, 600096, 2181122, 1638919, 1345568, 837156, 858113, 1293829, 1657350, 858145, 1293861, 1508872, 1753095, 1638951, 1657382, 1513987, 1274402, 1753127, 1514019, 2181154, 1508904],
    [26, 9, 17, 297985, 1142785, 298017, 429056, 605184, 429088, 605216, 2051586, 1284098, 1247749, 1142817, 1284642, 1247781, 1640967, 1509894, 1948677, 2051106, 1509926, 1799683, 1948709, 1903112, 1640999, 2464260, 1903144, 1799715, 2464292],
    [30, 11, 20, 368640, 368672, 466945, 693249, 466977, 350723, 762372, 350755, 762404, 859653, 693281, 1222150, 859685, 2437634, 1222182, 2447881, 2134016, 1546759, 926725, 2138632, 1546791, 926757, 2037769, 2134048, 2138664, 2038313, 2579978, 2447401, 2580010, 2437666],
    [44, 15, 18, 340992, 299009, 341024, 470017, 299041, 1245698, 470049, 1245730, 960003, 727556, 960035, 727588, 1151496, 2306049, 1122822, 1169927, 2334720, 1122854, 989701, 1169959, 1151528, 1385997, 2297869, 989733, 2036235, 1511946, 1511978, 2400267, 1942028, 2464780, 1942060, 1517070, 2428942, 2036267, 2431497, 2334752, 1386029, 2297901, 2400299, 1517102, 2428974, 2464812, 2306081, 2431529],
    [26, 12, 19, 268288, 342016, 413697, 268320, 342048, 2037250, 413729, 2168323, 2037282, 1171972, 2168355, 1510920, 1172004, 1384966, 1387015, 1383946, 1510952, 2052617, 2052649, 1515019, 1384998, 1387047, 1383978, 1785349, 1515051, 1785381],
    [30, 10, 17, 337920, 744963, 475650, 531457, 779265, 337952, 592388, 531489, 744995, 475682, 592420, 985605, 869379, 985637, 1055744, 1776134, 1944071, 869411, 1055776, 1615878, 1907208, 1776166, 779297, 1392137, 1907240, 1944103, 1522696, 1615910, 1392169, 1522728],
    [38, 12, 18, 332800, 343040, 459777, 332832, 343072, 664068, 1221122, 1843200, 1221154, 459809, 1648133, 1404422, 664100, 2073095, 1648165, 1125383, 1156617, 1642498, 1353224, 1125927, 2105345, 1353256, 1770501, 1843232, 1388035, 1156649, 1388067, 1910283, 1404454, 1642530, 2105377, 2041354, 1910315, 2072615, 2075650, 2041386, 1770533, 2075682],
    [30, 12, 16, 304128, 271361, 354305, 304160, 271393, 1026562, 732675, 354337, 732707, 1909256, 1026594, 1403396, 1646596, 1778181, 1647140, 2171401, 2040327, 1402916, 2139658, 1778213, 2172933, 1909288, 2435590, 2040359, 2171433, 2172965, 2401803, 2435622, 2139690, 2401835],
    [30, 11, 19, 306177, 306209, 473089, 614915, 473121, 614947, 736770, 1779208, 599556, 736802, 1771523, 599588, 1288192, 1010181, 1650182, 1288224, 1747465, 1010213, 1650214, 1158146, 1158178, 2034183, 1779240, 2187270, 1784330, 1771555, 2034215, 1747497, 2187302, 1784362],
    [32, 12, 17, 371713, 749058, 371745, 749090, 1271299, 1518084, 764928, 1518116, 764960, 747013, 1120775, 747045, 1139208, 1120807, 1139240, 568841, 1084934, 1780234, 1271331, 2057220, 1780266, 568873, 1911307, 1942531, 1911339, 2449414, 1084966, 2188298, 1942563, 2057252, 2449446, 2188330],
    [24, 11, 19, 372736, 335872, 372768, 335904, 468483, 468515, 898049, 991750, 863746, 1253893, 863778, 898081, 1094151, 991782, 1094183, 1253925, 992772, 1914378, 2454024, 992804, 1654281, 1914410, 1654313, 2454056],
    [38, 13, 16, 359425, 1520130, 589824, 359457, 1520162, 893444, 619520, 589856, 619552, 827907, 893476, 827939, 821250, 1159169, 1287686, 821282, 1407493, 1159201, 1522185, 1287718, 1904641, 1407525, 1913351, 2007040, 1913383, 1549834, 2008065, 1904673, 1367560, 1260043, 1549866, 2007072, 1260075, 2175500, 2008097, 2175532, 1522217, 1367592],
    [18, 6, 16, 333824, 487425, 603650, 487457, 751616, 333856, 603682, 751648, 722435, 722467, 1402373, 1260549, 1539075, 1402405, 1260581, 1539107, 2169348, 2169380],
    [26, 9, 14, 460800, 310272, 460832, 310304, 464897, 638466, 638498, 464929, 866821, 997894, 862724, 866853, 1408001, 1238017, 862756, 997926, 1408033, 1390083, 1390115, 1391112, 1777159, 1958918, 1777191, 1391144, 1238049, 1958950],
    [20, 8, 16, 836099, 1900544, 520706, 742400, 520738, 836131, 742432, 873473, 873505, 967172, 1394181, 967204, 1525254, 2296327, 1900576, 1394213, 1568772, 1525286, 1568804, 2296359],
    [26, 10, 17, 328704, 480257, 328736, 1133058, 480289, 1377281, 1131012, 1264131, 1131044, 1919493, 1116681, 2312712, 1262087, 1133090, 1452039, 1264163, 1230342, 1262119, 1230374, 1452071, 1919525, 1860617, 1116713, 2312744, 1377313, 1860649],
    [22, 7, 20, 285696, 1014785, 285728, 481281, 481313, 1886208, 1038850, 1378305, 1038882, 2055168, 1886240, 1014817, 737795, 2055200, 1378337, 2032134, 2148868, 737827, 1393157, 2148900, 1393189, 2032166],
    [38, 12, 18, 880640, 351233, 445954, 351265, 479748, 678912, 445986, 479780, 678944, 880672, 2574859, 1537026, 876037, 1625088, 876069, 1756161, 2165761, 1395206, 1246729, 1625120, 1421832, 1787912, 1305604, 1537058, 1756193, 1305636, 1399303, 1395238, 1421864, 1787944, 1399335, 1246761, 2443786, 2144771, 2443818, 2165793, 2144803, 2574891],
    [36, 12, 19, 446464, 344579, 446496, 344611, 1529350, 1529382, 1008640, 708609, 606727, 1007108, 1270282, 1659914, 708641, 606759, 1007140, 1102345, 1429513, 1532929, 1531394, 1102377, 1008672, 1660458, 1531426, 1429545, 1269802, 1916934, 1037832, 1532961, 830981, 1037864, 2041856, 1824267, 2041888, 1916966, 1824299, 831013],
    [30, 11, 18, 352256, 352288, 743939, 484353, 464386, 464418, 1645060, 876548, 743971, 971777, 484385, 1790471, 1006085, 971809, 1645092, 876580, 1006117, 1255431, 1256966, 1658886, 1256998, 1658918, 1790503, 2048522, 1758728, 1255463, 1758760, 2180617, 2048554, 2180649],
    [40, 13, 20, 284672, 317441, 284704, 317473, 748037, 616962, 1793026, 1014276, 1924611, 616994, 1793058, 857092, 1924643, 748069, 857636, 1013796, 1142279, 1267208, 1775115, 1142311, 870924, 1397772, 1774089, 1272326, 1639432, 1272358, 1527817, 1774121, 1534976, 1267240, 1533953, 1775147, 1535008, 1527849, 1533985, 870956, 1397804, 1639464, 2445834, 2445866],
    [36, 13, 20, 347136, 355329, 315393, 347168, 355361, 315425, 715269, 596484, 417282, 1501699, 1923594, 417314, 1432580, 596516, 1432612, 1004038, 715301, 1265160, 1792008, 1004070, 1792552, 608775, 999434, 1695241, 1264680, 1923626, 1695273, 1501731, 608807, 1596416, 1906188, 999466, 2289163, 1596448, 1906220, 2289195],
    [26, 11, 19, 1073152, 617986, 1649157, 1795077, 618018, 881664, 1274881, 610820, 881696, 610852, 993799, 1795621, 845318, 730627, 1648677, 1073184, 1274913, 993831, 730659, 1987080, 1519114, 1519146, 845350, 2009609, 1987112, 2009641],
    [32, 13, 17, 911360, 357377, 357409, 1124870, 911392, 1925644, 880131, 2173955, 880163, 861700, 1532424, 1857033, 2304008, 861732, 1561093, 1136130, 1124902, 1794571, 1532456, 1136162, 1435146, 2320903, 2320935, 1561125, 2042891, 1794603, 1925676, 1435178, 2304040, 1857065, 2042923, 2173987],
    [30, 12, 19, 490497, 1828354, 912385, 490529, 847365, 1666566, 1239556, 912417, 726531, 726563, 1140232, 1435648, 847397, 1666598, 1435680, 1140264, 1239588, 1926663, 1875971, 1801216, 2318858, 1928715, 1876003, 1926695, 1632777, 1801248, 1928747, 1632809, 2318890, 1828386],
    [38, 12, 15, 337411, 1665027, 353797, 1796101, 337443, 1144832, 1043457, 1927684, 1665059, 1796645, 1145857, 1005063, 1927716, 353317, 2189834, 972804, 1012226, 1043489, 2058758, 1144864, 2058790, 1698313, 977416, 1012258, 1145889, 977448, 1005095, 1960960, 1698345, 972836, 2060291, 1371145, 2451979, 1960992, 2189866, 1371177, 2452011, 2060323],
    [28, 10, 20, 345088, 505857, 745990, 505889, 878088, 345120, 733698, 2035204, 1372681, 1241092, 1669635, 746022, 607233, 733730, 782336, 607265, 1266181, 782368, 1266213, 1961985, 878120, 1669667, 1962017, 1241636, 1945095, 2034724, 1372713, 1945127],
    [36, 12, 16, 358914, 390145, 476161, 718341, 358946, 390177, 517636, 476193, 517668, 724489, 1667081, 718373, 2337291, 1929227, 2075143, 1536007, 865795, 1263112, 1798666, 1133568, 724521, 1536551, 1667113, 865827, 986122, 1798698, 1503241, 1929771, 1133600, 986154, 1263144, 1931782, 2074663, 1931814, 2336811, 1503273],
    [42, 15, 18, 388096, 914433, 750083, 388128, 457218, 750115, 1932808, 457250, 485892, 2092034, 1243655, 485924, 1144326, 1437196, 1273349, 1144358, 1000456, 1932840, 1993729, 1243687, 914465, 1003017, 984587, 1273381, 1000488, 1003049, 1668107, 984619, 1437228, 1662477, 2092066, 1930762, 1115662, 1395713, 1662509, 1668139, 1115694, 1395745, 1993761, 2313216, 2313248, 1930794],
    [32, 14, 16, 609281, 751106, 650240, 2062851, 609313, 477187, 2062883, 1011206, 650272, 740868, 751138, 740900, 2193925, 477219, 1768972, 2193957, 1109511, 739848, 1389065, 1011238, 1567242, 1109543, 1567274, 2325003, 1114117, 739880, 1786381, 2325035, 1389097, 1786413, 1769004, 1114149],
    [24, 9, 14, 495616, 495106, 495648, 1541636, 406529, 495138, 1672709, 1544194, 1541668, 406561, 1803782, 1672741, 1149447, 1803814, 1544226, 1411073, 1952264, 1149479, 2110470, 1952296, 1411105, 2110502, 2460163, 2460195],
    [36, 11, 17, 887809, 405505, 405537, 364034, 626688, 995845, 364066, 626720, 903686, 1998853, 920581, 897539, 995877, 920613, 1937410, 903718, 931332, 897571, 887841, 1409545, 904711, 1224704, 2068481, 904743, 1224736, 931364, 1998885, 1937442, 1917952, 1409577, 1979912, 2083338, 2068513, 1979944, 2083370, 1917984],
    [28, 11, 20, 497664, 329728, 327681, 329760, 1046019, 327713, 497696, 493058, 493090, 854532, 1148421, 854564, 1934339, 1641991, 1046051, 1148453, 1805832, 855558, 1934371, 855590, 1936906, 1689097, 1642023, 1805864, 1991686, 1936938, 1689129, 1991718],
    [26, 9, 17, 759809, 1524227, 1772544, 667138, 2049542, 1903617, 759841, 667170, 691716, 1542661, 720897, 1176581, 691748, 1415168, 1542693, 720929, 1415200, 1176613, 1524259, 1772576, 1903649, 2329095, 2329127, 2215432, 2049574, 2215464],
    [28, 9, 20, 331776, 367616, 270851, 367648, 1118726, 755202, 270883, 331808, 760833, 1283588, 2166785, 1283620, 755234, 1564165, 1318913, 760865, 1039880, 1678341, 1564197, 1679360, 1512967, 1678373, 1679392, 1118758, 1039912, 1318945, 1512999, 2166817],
    [30, 9, 17, 373761, 373793, 1675782, 631808, 891394, 635395, 1053188, 1166342, 891426, 635427, 2298881, 631840, 1053220, 1940481, 1035781, 1413125, 1810433, 1035813, 1413157, 1481728, 1166886, 1675302, 1940513, 1810465, 2334215, 2200072, 2334247, 2200104, 1481760, 2298913],
    [34, 13, 19, 432128, 628227, 514562, 1248772, 550405, 763905, 514594, 432160, 763937, 625158, 628259, 894976, 550437, 625190, 1545737, 895008, 783879, 783911, 1414149, 1074698, 1809418, 1248804, 1414181, 1545769, 1425928, 2072075, 1074730, 1809450, 2072107, 2039308, 1425960, 2198536, 2198568, 2039340],
    [34, 12, 19, 370689, 433153, 370721, 626179, 1808901, 1939975, 530946, 433185, 2086404, 530978, 695296, 626211, 1806857, 1419264, 695328, 1808933, 1017863, 1940007, 1219080, 1292292, 1419296, 1292836, 1017895, 1806889, 1219112, 1313286, 2118154, 1957387, 2118667, 1957419, 1313318, 2118186, 2085924, 2118699],
    [26, 10, 19, 502784, 888832, 340482, 502816, 340514, 633857, 729603, 633889, 1019905, 729635, 908804, 888864, 1568262, 1019937, 996871, 908836, 1682952, 1021445, 996903, 2108937, 1021477, 1568294, 2076672, 1682984, 2076704, 2108969],
    [36, 13, 16, 504833, 504865, 766976, 1548804, 813056, 767008, 1417733, 2043908, 813088, 766466, 896001, 766498, 896033, 1417765, 1028611, 1126918, 1548836, 1813000, 1028643, 1126950, 1029639, 2206217, 1876993, 1029671, 1291786, 1813032, 1291818, 1877025, 2204171, 2206249, 2560001, 2204203, 2043940, 2466316, 2560033, 2466348],
    [30, 11, 19, 403456, 374785, 374817, 469507, 768000, 469539, 768032, 370178, 1154567, 403488, 370210, 894470, 1584644, 894502, 1423877, 1154599, 1305097, 1059849, 1551882, 1305129, 1059881, 1584676, 1551914, 1423909, 1960456, 1960488, 2191370, 1680389, 1680421, 2191402],
    [34, 11, 17, 519682, 404995, 628739, 521217, 519714, 405027, 628771, 521249, 1550852, 928769, 942597, 699392, 1550884, 942629, 1162240, 928801, 1162272, 1434120, 1582082, 1681929, 1434152, 1686532, 1681961, 1582114, 1598983, 699424, 1947649, 2468362, 1686564, 1730054, 1947681, 2468394, 1599015, 1730086],
    [34, 11, 16, 506880, 391682, 506912, 391714, 401923, 1422339, 401955, 1422371, 753665, 833028, 734725, 753697, 734757, 1555457, 1978369, 1553928, 1685001, 1259015, 1155080, 833060, 1816074, 2242054, 1553960, 1685033, 1155112, 2254858, 1671168, 1555489, 1978401, 1259047, 2255402, 1815594, 1671200, 2242086],
    [32, 10, 15, 536576, 536608, 472578, 1552899, 622592, 472610, 461827, 1552931, 899588, 1683973, 1815046, 899620, 622624, 1684005, 461859, 1815078, 1817601, 1717249, 886790, 1946120, 886822, 1653257, 1946152, 1802241, 1717281, 1652231, 1817633, 1652263, 1802273, 2044937, 1653289, 2044969],
    [38, 15, 20, 493568, 538624, 633347, 2079747, 504322, 633379, 2079779, 504354, 389637, 538656, 1322502, 389669, 1047553, 493600, 1047585, 1290245, 2046472, 1718795, 1127946, 797191, 1290277, 1097225, 2095104, 1097257, 1127978, 797223, 2095136, 1947150, 2271756, 1718827, 2140685, 1322534, 1947182, 2591236, 2140717, 2591268, 2046504, 2271788],
    [40, 15, 17, 654337, 278019, 1699843, 363010, 278051, 1699875, 363042, 756736, 654369, 755713, 1827332, 1325573, 913928, 2078728, 756768, 1027593, 1832458, 2209802, 755745, 1325605, 2603531, 1027625, 913960, 2078760, 2210346, 1453575, 1963019, 2094605, 2207246, 1831978, 2603563, 1963051, 1019398, 1827364, 1019430, 1453607, 2094637, 2061836, 2207278, 2061868],
    [30, 11, 15, 1033216, 1164289, 1033248, 1164321, 1063937, 769538, 815622, 769570, 1281541, 772096, 772128, 815654, 1165827, 1132039, 1412102, 1165859, 1281573, 1559044, 1412134, 1559076, 1132071, 1295881, 1437701, 1295913, 1655306, 1437733, 1063969, 1655338, 1326600, 1326632],
    [16, 7, 14, 378880, 641025, 378912, 1556994, 641057, 1557026, 738820, 1554947, 1687555, 1688099, 1950214, 738852, 1935877, 1554467, 1935909, 1950246],
    [36, 10, 16, 382976, 1428480, 522241, 491521, 1559553, 1428512, 1559585, 653826, 1690626, 383008, 491553, 624132, 522273, 2065410, 653858, 1690658, 1001472, 624164, 509443, 885255, 509475, 1278469, 1001504, 915976, 885287, 916008, 1079301, 1278501, 1540617, 1294345, 1079333, 1540649, 1294377, 1426950, 2065442, 1426982],
    [28, 10, 17, 478208, 512001, 381442, 478240, 1657858, 381474, 512033, 1179139, 1788929, 1179171, 1427972, 1657890, 1428004, 944128, 1300480, 1163781, 1656328, 944160, 1300512, 1788961, 1163813, 1690118, 1526279, 1690150, 1526311, 2050569, 2050601, 1656360],
    [30, 12, 17, 1299456, 1430529, 1299488, 1430561, 901635, 770562, 770594, 741377, 776192, 901667, 1285638, 776224, 741409, 2203144, 1921024, 1562119, 1285670, 771593, 1562151, 1814026, 1921056, 771625, 2198020, 1988107, 2593285, 2203176, 2198052, 2593317, 1814058, 1988139],
    [20, 9, 16, 515072, 349185, 497154, 349217, 499203, 515104, 497186, 499235, 2071045, 1955841, 1955873, 2071077, 1922566, 1954311, 1922598, 2201092, 2085384, 1954343, 2085416, 2201124],
    [36, 12, 18, 518144, 1170432, 1301505, 1170464, 1301537, 518176, 611329, 1054214, 683522, 1670145, 611361, 1042951, 683554, 856581, 940547, 1397252, 1042983, 856613, 1268234, 1054246, 1298434, 940579, 1268266, 1397284, 1298466, 906760, 1152007, 1234944, 1309195, 906792, 1152039, 1309227, 1168905, 1670177, 1168937, 1234976],
    [22, 8, 16, 385025, 612867, 1693699, 385057, 780288, 1527298, 1825284, 1040901, 612899, 780320, 1693731, 1825316, 1040933, 973825, 2218503, 1202694, 1250308, 1250340, 973857, 1202726, 2218535, 1527330],
    [34, 11, 15, 387072, 1041408, 1172481, 1041440, 1172513, 387104, 631299, 418308, 451074, 418340, 451106, 631331, 713223, 1161733, 1303557, 994822, 1662982, 1304101, 994854, 713255, 975368, 1121281, 975400, 1161253, 2023424, 1121313, 1129993, 1176074, 2285569, 1663014, 1176106, 1130025, 2023456, 2285601],
    [16, 7, 15, 320513, 320545, 501250, 501282, 1418757, 1174528, 1565188, 1174560, 1565220, 1828865, 1418789, 1420803, 1696262, 1828897, 1696294, 1420835],
    [40, 15, 19, 1698816, 1309697, 1829889, 1698848, 1829921, 647683, 523778, 647715, 523810, 778757, 753158, 778789, 753190, 1309729, 1076743, 1440768, 759304, 1036804, 1076775, 1440800, 759336, 1036836, 1538569, 1538601, 1566220, 2516992, 2063885, 1697291, 2499086, 1976842, 2063917, 1975302, 1566252, 2499118, 1498117, 2517024, 1697323, 1975334, 1976874, 1498149],
    [36, 12, 16, 651264, 384000, 289793, 2448901, 384032, 289825, 645636, 2091012, 552454, 916995, 917027, 645668, 2091044, 552486, 651296, 1530378, 2353162, 2124290, 1047048, 2222088, 1958411, 1286663, 1863177, 1047080, 2222120, 1177602, 1530410, 2353194, 1178146, 1286695, 2386944, 2123810, 1958443, 1863209, 2448933, 2386976],
    [36, 12, 16, 290816, 1438720, 1569793, 1438752, 1569825, 1701380, 290848, 684033, 2340868, 684065, 1031683, 640514, 1031715, 1030661, 1701412, 1964032, 1160197, 1030693, 640546, 868870, 2340900, 1964064, 1160229, 868902, 1686023, 1602058, 1229320, 1686055, 1229352, 1817097, 1602090, 2314249, 1817129, 2211339, 2211371, 2314281],
    [28, 10, 16, 392192, 375809, 1831430, 392224, 375841, 636418, 2471942, 636450, 1995271, 784385, 1032707, 1472004, 784417, 2126344, 2093064, 1110533, 1864705, 1032739, 1472036, 1110565, 2472486, 1830950, 1995303, 2126376, 2093096, 1864737, 2585097, 2585129],
    [24, 10, 16, 376832, 1571840, 1702913, 1571872, 1702945, 376864, 556547, 619010, 555524, 509953, 619042, 556579, 509985, 555556, 1834501, 1834533, 1211910, 1211942, 1800711, 1800743, 1307144, 982537, 1307176, 982569],
    [36, 11, 14, 1439744, 1439776, 1702404, 884233, 1571330, 621059, 1571362, 621091, 883206, 652292, 1702436, 1034242, 537600, 686600, 883238, 1833479, 652324, 537632, 773121, 686632, 1278983, 1833511, 1034274, 902144, 884265, 648709, 1276426, 773153, 648741, 1848327, 1276458, 1279015, 1044490, 1044522, 1848359, 902176],
]
ROLES = [
    [0, 0, 12, 1, 13, 13, 14, 15, 0, 0, 1, 12, 8, 10],
    [0, 11, 13, 12, 6, 8, 5, 2, 1, 1, 8, 6, 2, 5],
    [0, 4, 12, 14, 13, 11, 8, 6, 15, 15, 17, 16, 2, 3],
    [0, 8, 7, 6, 15, 14, 4, 3, 16, 16, 12, 2, 5, 13],
    [0, 2, 12, 19, 13, 10, 14, 15, 16, 16, 3, 18, 11, 17],
    [0, 12, 2, 5, 4, 7, 11, 6, 13, 13, 8, 9, 3, 14],
    [0, 7, 9, 11, 10, 8, 6, 12, 14, 14, 15, 13, 2, 16],
    [0, 5, 3, 12, 9, 7, 6, 14, 11, 11, 8, 13, 4, 10],
    [0, 5, 11, 17, 12, 9, 6, 18, 14, 14, 16, 13, 19, 15],
    [0, 7, 10, 14, 11, 8, 3, 6, 2, 2, 15, 9, 13, 12],
    [0, 13, 9, 12, 10, 5, 8, 7, 15, 15, 14, 11, 3, 6],
    [0, 9, 2, 4, 15, 13, 5, 6, 16, 16, 14, 12, 7, 10],
    [0, 6, 11, 13, 12, 3, 9, 8, 14, 14, 15, 4, 5, 16],
    [0, 3, 5, 8, 12, 11, 2, 7, 13, 13, 16, 14, 17, 15],
    [0, 15, 8, 14, 9, 12, 11, 7, 10, 10, 13, 16, 0, 15],
    [0, 8, 4, 4, 6, 9, 7, 7, 10, 10, 0, 8, 1, 5],
    [12, 12, 15, 17, 13, 13, 14, 5, 0, 2, 1, 8, 16, 10],
    [11, 12, 2, 5, 9, 13, 7, 4, 1, 14, 16, 15, 6, 3],
    [16, 3, 13, 10, 14, 15, 4, 12, 3, 16, 10, 13, 8, 11],
    [6, 14, 13, 12, 11, 2, 15, 4, 10, 9, 2, 11, 4, 15],
    [4, 14, 11, 12, 2, 5, 10, 9, 7, 13, 8, 16, 17, 15],
    [7, 8, 3, 13, 11, 10, 5, 12, 2, 16, 17, 9, 14, 15],
    [8, 5, 11, 14, 10, 15, 3, 12, 4, 9, 6, 13, 2, 16],
    [4, 8, 10, 2, 9, 5, 11, 3, 7, 13, 12, 15, 14, 16],
    [2, 17, 12, 15, 4, 9, 11, 14, 8, 13, 18, 7, 6, 16],
    [6, 9, 2, 11, 3, 8, 7, 4, 12, 14, 5, 15, 13, 10],
    [2, 9, 11, 13, 15, 12, 10, 7, 14, 18, 5, 17, 19, 16],
    [6, 8, 10, 5, 3, 12, 11, 13, 17, 16, 18, 15, 2, 14],
    [3, 9, 4, 13, 12, 6, 11, 10, 2, 15, 5, 16, 14, 17],
    [10, 2, 6, 3, 16, 15, 8, 7, 14, 11, 12, 13, 4, 17],
    [14, 11, 13, 12, 15, 7, 10, 5, 6, 8, 17, 4, 0, 16],
    [9, 8, 12, 12, 3, 11, 13, 13, 10, 14, 0, 4, 1, 5],
    [8, 8, 13, 17, 10, 10, 16, 12, 0, 15, 1, 14, 5, 4],
    [4, 12, 8, 13, 11, 14, 10, 7, 1, 3, 2, 9, 6, 15],
    [3, 8, 12, 14, 5, 11, 13, 6, 4, 16, 9, 15, 10, 17],
    [6, 7, 10, 8, 4, 9, 15, 11, 14, 5, 3, 13, 2, 12],
    [7, 16, 14, 12, 15, 2, 6, 10, 16, 7, 12, 14, 13, 11],
    [7, 5, 2, 6, 12, 14, 13, 9, 11, 10, 14, 12, 9, 13],
    [2, 4, 12, 11, 10, 17, 14, 16, 7, 9, 18, 15, 3, 13],
    [9, 8, 12, 4, 10, 11, 7, 6, 15, 14, 5, 2, 3, 13],
    [12, 13, 10, 17, 4, 6, 2, 11, 16, 9, 18, 15, 14, 19],
    [8, 12, 5, 9, 13, 10, 6, 7, 14, 15, 18, 16, 4, 17],
    [2, 11, 6, 14, 4, 8, 10, 5, 17, 16, 13, 15, 3, 9],
    [8, 6, 3, 13, 11, 7, 14, 15, 17, 16, 9, 4, 10, 12],
    [19, 8, 6, 17, 2, 11, 18, 12, 13, 16, 14, 9, 15, 20],
    [9, 7, 12, 10, 8, 5, 13, 6, 15, 2, 11, 16, 14, 17],
    [2, 4, 8, 10, 3, 13, 11, 9, 12, 17, 14, 16, 0, 15],
    [3, 6, 7, 7, 8, 5, 9, 9, 11, 13, 0, 12, 1, 10],
    [15, 15, 11, 10, 12, 12, 16, 9, 0, 5, 1, 14, 6, 13],
    [7, 2, 4, 12, 8, 11, 5, 13, 1, 9, 3, 10, 6, 14],
    [6, 7, 18, 15, 10, 11, 13, 12, 3, 9, 8, 17, 14, 16],
    [10, 6, 14, 4, 5, 3, 2, 11, 8, 9, 12, 15, 13, 16],
    [16, 4, 9, 12, 8, 2, 11, 6, 3, 13, 5, 15, 10, 14],
    [12, 3, 4, 6, 2, 11, 5, 14, 7, 13, 17, 15, 9, 16],
    [4, 11, 12, 14, 6, 10, 13, 15, 11, 4, 14, 12, 9, 3],
    [8, 10, 12, 14, 9, 11, 3, 7, 5, 13, 11, 9, 7, 3],
    [7, 4, 6, 13, 5, 3, 18, 9, 15, 14, 17, 8, 16, 12],
    [10, 6, 3, 5, 8, 12, 7, 13, 2, 9, 11, 14, 4, 15],
    [3, 15, 12, 14, 16, 5, 10, 11, 8, 7, 6, 9, 13, 4],
    [18, 9, 11, 14, 13, 15, 7, 17, 3, 6, 4, 8, 12, 16],
    [2, 7, 8, 13, 19, 16, 12, 15, 4, 10, 14, 17, 5, 18],
    [10, 7, 4, 11, 3, 8, 14, 12, 2, 6, 9, 15, 13, 16],
    [11, 5, 14, 13, 8, 6, 16, 7, 4, 12, 10, 9, 0, 15],
    [6, 7, 11, 11, 8, 9, 5, 5, 10, 12, 0, 13, 1, 14],
    [9, 9, 13, 10, 6, 6, 11, 8, 0, 12, 1, 7, 14, 15],
    [6, 3, 7, 8, 5, 14, 11, 4, 1, 13, 2, 9, 10, 12],
    [16, 18, 12, 9, 8, 5, 11, 14, 15, 13, 10, 17, 2, 6],
    [7, 5, 15, 9, 6, 8, 10, 3, 16, 11, 13, 12, 14, 2],
    [12, 8, 11, 15, 14, 19, 17, 18, 2, 4, 16, 7, 6, 13],
    [10, 11, 15, 5, 13, 14, 16, 4, 17, 12, 6, 8, 3, 7],
    [2, 7, 11, 14, 3, 5, 13, 10, 16, 4, 12, 18, 15, 17],
    [11, 8, 2, 5, 6, 10, 4, 14, 9, 13, 12, 15, 3, 16],
    [4, 17, 15, 14, 16, 5, 10, 11, 17, 4, 14, 15, 13, 12],
    [7, 8, 4, 5, 15, 14, 13, 6, 12, 9, 14, 15, 6, 13],
    [4, 16, 6, 14, 8, 18, 13, 11, 3, 7, 17, 12, 5, 15],
    [12, 11, 6, 8, 10, 4, 3, 5, 7, 14, 13, 15, 2, 16],
    [2, 6, 11, 14, 17, 3, 10, 16, 12, 18, 13, 15, 5, 8],
    [2, 7, 4, 11, 14, 12, 15, 9, 13, 3, 10, 8, 6, 5],
    [2, 9, 6, 10, 12, 11, 7, 5, 8, 4, 14, 15, 0, 13],
    [5, 8, 2, 2, 6, 9, 12, 12, 7, 10, 0, 11, 1, 13],
    [13, 13, 9, 5, 10, 10, 8, 6, 0, 15, 1, 14, 12, 11],
    [7, 10, 2, 5, 4, 11, 3, 8, 1, 16, 14, 12, 15, 13],
    [8, 14, 13, 10, 9, 17, 18, 19, 16, 12, 2, 11, 7, 15],
    [8, 6, 17, 7, 10, 11, 4, 5, 14, 15, 3, 16, 13, 12],
    [17, 18, 10, 13, 3, 7, 12, 6, 14, 11, 5, 8, 16, 15],
    [12, 7, 5, 10, 6, 11, 3, 9, 2, 14, 13, 17, 16, 15],
    [7, 12, 2, 13, 5, 8, 3, 14, 18, 17, 16, 6, 19, 15],
    [13, 8, 15, 7, 14, 10, 2, 18, 5, 19, 3, 17, 11, 16],
    [7, 4, 5, 11, 15, 12, 13, 14, 3, 17, 10, 16, 8, 18],
    [13, 8, 7, 14, 11, 12, 3, 2, 4, 6, 15, 16, 5, 9],
    [17, 7, 14, 16, 15, 13, 11, 6, 7, 17, 16, 14, 12, 18],
    [4, 10, 11, 3, 14, 12, 2, 13, 5, 6, 12, 14, 13, 2],
    [17, 15, 14, 11, 7, 5, 12, 13, 2, 18, 10, 16, 4, 19],
    [11, 7, 6, 12, 9, 10, 2, 8, 3, 14, 4, 15, 5, 13],
    [14, 11, 16, 17, 2, 6, 15, 8, 5, 4, 12, 13, 0, 9],
    [5, 11, 13, 13, 3, 14, 8, 8, 10, 15, 0, 6, 1, 4],
    [12, 12, 4, 5, 13, 13, 10, 6, 0, 2, 1, 7, 9, 11],
    [11, 12, 14, 16, 9, 13, 8, 3, 1, 2, 15, 7, 4, 6],
    [3, 19, 11, 17, 5, 2, 10, 8, 14, 16, 18, 15, 12, 13],
    [5, 7, 16, 3, 14, 13, 6, 2, 10, 9, 11, 15, 12, 8],
    [3, 11, 4, 12, 15, 14, 16, 10, 2, 17, 9, 18, 19, 13],
    [9, 6, 4, 2, 8, 5, 10, 11, 12, 14, 13, 15, 3, 16],
    [3, 6, 10, 14, 5, 9, 13, 11, 15, 18, 17, 7, 2, 16],
    [13, 7, 2, 17, 5, 15, 14, 18, 3, 6, 10, 16, 11, 12],
    [12, 5, 11, 10, 13, 14, 18, 16, 15, 2, 7, 17, 4, 6],
    [4, 5, 6, 8, 12, 11, 2, 9, 15, 14, 7, 13, 3, 10],
    [6, 13, 10, 12, 2, 16, 11, 18, 7, 14, 15, 17, 9, 8],
    [11, 9, 3, 15, 4, 10, 6, 12, 13, 14, 5, 16, 2, 7],
    [15, 2, 12, 13, 11, 8, 3, 10, 2, 15, 13, 12, 14, 9],
    [5, 6, 12, 8, 10, 13, 14, 4, 11, 3, 13, 10, 4, 14],
    [5, 7, 15, 3, 14, 6, 19, 16, 13, 12, 18, 17, 0, 4],
    [8, 15, 3, 3, 11, 10, 13, 13, 7, 16, 0, 6, 1, 2],
    [2, 2, 14, 12, 8, 8, 1, 11, 0, 9, 1, 11, 13, 13],
    [6, 3, 7, 9, 8, 2, 1, 10, 1, 10, 13, 12, 11, 11],
    [5, 9, 2, 12, 4, 6, 1, 10, 14, 11, 15, 8, 13, 13],
    [12, 6, 10, 9, 11, 4, 1, 2, 13, 16, 3, 14, 15, 15],
    [9, 4, 15, 7, 3, 2, 1, 14, 5, 6, 12, 13, 16, 16],
    [8, 11, 9, 13, 10, 7, 1, 6, 2, 4, 12, 15, 14, 14],
    [5, 10, 12, 16, 14, 8, 1, 13, 3, 17, 11, 6, 15, 15],
    [3, 7, 8, 10, 9, 4, 1, 5, 14, 11, 12, 13, 15, 15],
    [4, 8, 5, 11, 2, 7, 1, 12, 3, 14, 9, 10, 13, 13],
    [9, 4, 7, 11, 8, 6, 1, 12, 2, 5, 10, 14, 13, 13],
    [2, 12, 16, 17, 13, 11, 1, 15, 9, 14, 18, 6, 10, 10],
    [8, 10, 12, 2, 13, 4, 1, 9, 3, 15, 14, 6, 7, 7],
    [7, 9, 4, 13, 11, 3, 1, 15, 5, 2, 14, 6, 12, 12],
    [12, 6, 10, 7, 11, 8, 1, 4, 2, 3, 13, 14, 15, 15],
    [14, 15, 11, 13, 5, 12, 1, 10, 15, 14, 13, 11, 0, 0],
    [2, 7, 11, 11, 12, 0, 1, 1, 4, 13, 0, 12, 1, 1],
]


def fill_table(tbl, me, lo, hi):
    if hi - lo == 1:
        head = SENDS[lo]
        for place, word in enumerate(head):
            tbl[place] = jnp.int32(word)
        return
    mid = (lo + hi) // 2
    lax.cond(
        me < mid,
        lambda: fill_table(tbl, me, lo, mid),
        lambda: fill_table(tbl, me, mid, hi),
    )


def spread_kernel(stored_ref, slots_ref, tbl, own_sem, send_sem, recv_sem):
    rows_per = stored_ref.shape[2] // CHUNKS
    row_count = lax.axis_size("row")
    me = lax.axis_index("col") * row_count + lax.axis_index("row")
    fill_table(tbl, me, 0, len(SENDS))
    own = [
        pltpu.make_async_copy(stored_ref.at[lane, 0], slots_ref.at[lane], own_sem.at[lane])
        for lane in range(2)
    ]
    for copy in own:
        copy.start()

    def hop(source, target, slot, chunk, place):
        return pltpu.make_async_remote_copy(
            src_ref=source,
            dst_ref=slots_ref.at[slot, pl.ds(chunk * rows_per, rows_per)],
            send_sem=send_sem.at[place],
            recv_sem=recv_sem.at[slot, chunk],
            device_id={"col": target // row_count, "row": lax.rem(target, row_count)},
            device_id_type=MESH,
        )

    def arrival(slot, chunk):
        piece = slots_ref.at[slot, pl.ds(chunk * rows_per, rows_per)]
        hop(piece, me, slot, chunk, 0).wait_recv()

    sends = tbl[0]

    @pl.loop(0, sends)
    def _(place):
        word = tbl[3 + place]
        slot = word & 31
        chunk = (word >> 5) & 15
        target = (word >> 10) & 127
        landing = word >> 17

        @pl.when(((word >> 9) & 1) == 1)
        def _():
            arrival(slot, chunk)

        @pl.when(slot < 2)
        def _():
            piece = stored_ref.at[slot, 0, pl.ds(chunk * rows_per, rows_per)]
            hop(piece, target, landing, chunk, place).start()

        @pl.when(slot >= 2)
        def _():
            piece = slots_ref.at[slot, pl.ds(chunk * rows_per, rows_per)]
            hop(piece, target, landing, chunk, place).start()

    @pl.loop(tbl[1], tbl[2])
    def _(slot):
        for chunk in range(CHUNKS):
            arrival(slot, chunk)

    @pl.loop(0, sends)
    def _(place):
        piece = slots_ref.at[0, pl.ds(0, rows_per)]
        hop(piece, me, 0, 0, place).wait_send()

    for copy in own:
        copy.wait()


def spread(stored):
    return pl.pallas_call(
        spread_kernel,
        out_shape=jax.ShapeDtypeStruct((SLOTS,) + stored.shape[2:], jnp.float32),
        in_specs=[pl.BlockSpec(memory_space=pl.ANY)],
        out_specs=pl.BlockSpec(memory_space=pl.ANY),
        scratch_shapes=[
            pltpu.SMEM((max(len(entry) for entry in SENDS),), jnp.int32),
            pltpu.SemaphoreType.DMA((2,)),
            pltpu.SemaphoreType.DMA((max(entry[0] for entry in SENDS),)),
            pltpu.SemaphoreType.DMA((SLOTS, CHUNKS)),
        ],
        compiler_params=pltpu.CompilerParams(has_side_effects=True),
        name="spread",
    )(stored)


def split(value):
    high = value.astype(jnp.bfloat16)
    return high, (value - high.astype(jnp.float32)).astype(jnp.bfloat16)


def multiply_kernel(
    slots_ref, roles_ref, rows_ref, offs_ref, krow_ref, kcol_ref, kcnt_ref, out_ref,
    raw, left, right, done, in_sem, out_sem,
):
    grid = lax.axis_size("row")
    tile_j = lax.axis_index("row")
    col_id = lax.axis_index("col")
    me = col_id * grid + tile_j
    tiles = raw.shape[0]
    active = raw.shape[1]
    half = raw.shape[2]
    block = raw.shape[-1]
    kept = krow_ref.shape[-1]

    def load(place):
        return pltpu.make_async_copy(
            slots_ref.at[roles_ref[me, place]], raw.at[place], in_sem.at[place]
        )

    for place in range(tiles):
        load(place).start()

    first = rows_ref[0, 0]
    bits = [rows_ref[0, 1] ^ first, rows_ref[0, 2] ^ first, rows_ref[0, 4] ^ first]

    def rank(value):
        return sum(
            jnp.where((value & bit) != 0, jnp.int32(1 << place), jnp.int32(0))
            for place, bit in enumerate(bits)
        )

    def shifts(tile_x, tile_y):
        both = ((tile_x, tile_y), (tile_y, tile_x))
        return [rank(offs_ref[x, y, slot]) for x, y in both for slot in range(half)]

    tile_is = [col_id * 2 + lane for lane in range(2)]
    tile_ks = [lax.rem(tile_is[0] + tile_j + place, grid) for place in range(3)]
    left_shifts = [
        [shifts(tile_is[lane], tile_ks[lane + step]) for step in range(2)] for lane in range(2)
    ]

    for place in range(3):
        load(8 + 2 * place).wait()
        load(9 + 2 * place).wait()
        own, mirror = raw.at[8 + 2 * place], raw.at[9 + 2 * place]
        moves = shifts(tile_ks[place], tile_j)

        @pl.loop(0, active)
        def _(row):
            for slot in range(half):
                mirror[row, slot] = mirror[row, slot].T

        def entry(slot, row):
            if slot < half:
                return own.at[row, slot]
            return mirror.at[row ^ moves[slot], slot - half]

        alive = []
        for slot in range(2 * half):
            same = [moves[slot] == moves[before] for before in range(slot)]
            taken = jnp.bool_(False)
            for before in range(slot):
                join = same[before] & alive[before] & jnp.logical_not(taken)
                taken = taken | same[before]

                @pl.when(join)
                def _():
                    @pl.loop(0, active)
                    def _(row):
                        into = entry(before, row)
                        into[...] = into[...] + entry(slot, row)[...]

            alive.append(jnp.logical_not(taken))

        for shift in range(active):
            used = moves[0] == shift
            for slot in range(1, 2 * half):
                used = used | (moves[slot] == shift)

            @pl.when(jnp.logical_not(used))
            def _():
                @pl.loop(0, active)
                def _(row):
                    right[place, row, row ^ shift] = jnp.zeros((block, 2 * block), jnp.bfloat16)

        for slot in range(2 * half):
            @pl.when(alive[slot])
            def _():
                @pl.loop(0, active)
                def _(row):
                    high, low = split(entry(slot, row)[...])
                    column = row ^ moves[slot]
                    right[place, row, column, :, :block] = high
                    right[place, row, column, :, block:] = low

    for place in range(4):
        load(2 * place).wait()
        load(2 * place + 1).wait()

        @pl.loop(0, active)
        def _(row):
            for slot in range(half):
                high, low = split(raw[2 * place, row, slot])
                left[place, row, slot, :block] = high
                left[place, row, slot, block:] = low
                high, low = split(raw[2 * place + 1, row, slot].T)
                left[place, row, half + slot, :block] = high
                left[place, row, half + slot, block:] = low

    for lane in range(2):
        count = kcnt_ref[lane, 0]

        @pl.loop(0, kept)
        def _(item):
            @pl.when(item < count)
            def _():
                row = rank(krow_ref[lane, 0, item])
                column = rank(kcol_ref[lane, 0, item])
                lefts, rights = [], []
                for step in range(2):
                    for slot in range(2 * half):
                        middle = row ^ left_shifts[lane][step][slot]
                        source = row if slot < half else middle
                        lefts.append(left[2 * lane + step, source, slot])
                        rights.append(right[lane + step, middle, column])
                total = jnp.dot(
                    jnp.concatenate(lefts, 1),
                    jnp.concatenate(rights, 0),
                    preferred_element_type=jnp.float32,
                )
                total = total[:block] + total[block:]
                done[lane, item] = total[:, :block] + total[:, block:]

            @pl.when(item >= count)
            def _():
                done[lane, item] = jnp.zeros((block, block), jnp.float32)

        pltpu.make_async_copy(done.at[lane], out_ref.at[lane, 0], out_sem.at[lane]).start()

    for lane in range(2):
        pltpu.make_async_copy(done.at[lane], out_ref.at[lane, 0], out_sem.at[lane]).wait()


def multiply(slots, roles, tile_rows, offsets, kept_rows, kept_cols, kept_count):
    block = slots.shape[-1]
    active, half = slots.shape[1:3]
    lanes, _, kept = kept_rows.shape
    tiles = roles.shape[-1]
    smem = pl.BlockSpec(memory_space=pltpu.SMEM)
    return pl.pallas_call(
        multiply_kernel,
        out_shape=jax.ShapeDtypeStruct((lanes, 1, kept, block, block), jnp.float32),
        in_specs=[pl.BlockSpec(memory_space=pl.ANY)] + [smem] * 6,
        out_specs=pl.BlockSpec(memory_space=pl.ANY),
        scratch_shapes=[
            pltpu.VMEM((tiles, active, half, block, block), jnp.float32),
            pltpu.VMEM((4, active, 2 * half, 2 * block, block), jnp.bfloat16),
            pltpu.VMEM((3, active, active, block, 2 * block), jnp.bfloat16),
            pltpu.VMEM((lanes, kept, block, block), jnp.float32),
            pltpu.SemaphoreType.DMA((tiles,)),
            pltpu.SemaphoreType.DMA((lanes,)),
        ],
        compiler_params=pltpu.CompilerParams(vmem_limit_bytes=56 << 20),
        name="multiply",
    )(slots, roles, tile_rows, offsets, kept_rows, kept_cols, kept_count)


def local(stored, tile_rows, offsets, kept_rows, kept_cols, kept_count):
    slots = spread(stored)
    roles = jnp.asarray(np.array(ROLES, np.int32))
    return multiply(slots, roles, tile_rows, offsets, kept_rows, kept_cols, kept_count)


def solution(mesh):
    in_specs = (
        P("col", "row", None, None, None, None),
        P(),
        P(),
        P("col", "row", None),
        P("col", "row", None),
        P("col", "row"),
    )
    out_specs = P("col", "row", None, None, None)
    return jax.shard_map(local, mesh=mesh, in_specs=in_specs, out_specs=out_specs, check_vma=False)
```

```python
import jax
import jax.numpy as jnp
import numpy as np
from jax import lax
from jax.experimental import pallas as pl
from jax.experimental.pallas import tpu as pltpu
from jax.sharding import PartitionSpec as P

MESH = pl.DeviceIdType.MESH
CHUNKS = 4
SLOTS = 32
SENDS = [
    [2242561, 1187840, 1187904, 1187968, 1188032, 270337, 270401, 1851906, 270465, 2242625, 270529, 688648, 1450505, 1982473, 2242689, 688712, 1450569, 2244616, 2242753, 688776, 1450633, 1982537, 662026, 688840, 1450697, 2244680, 662090, 2523661, 1982601, 2523725, 2244744, 1982665, 3160592, 2523789, 2244808, 3160656, 958993, 1851970, 3160720, 2916883, 2236435, 1852034, 3160784, 2523853, 2237011, 1852098, 1456660, 2916435, 2237075, 3031564, 1456724, 2916499, 926214, 3031628, 662154, 2917075, 2236627, 3031692, 1456788, 1344018, 3031756, 662218, 959057, 1327630, 1456852, 1344082, 1327694, 2628118, 959121, 1327758, 2759192, 1344146, 1057287, 1327822, 2628182, 959185, 926278, 1720847, 2759256, 1344210, 1057351, 1720911, 2628246, 1737237, 926342, 1720975, 2759320, 1745431, 1057415, 1721039, 2628310, 1737301, 926406, 1729035, 2759384, 1745495, 1057479, 1729099, 1737365, 1729163, 1745559, 1729227, 1737429, 1745623],
    [2326529, 262144, 262208, 262272, 262336, 393217, 393281, 1992201, 393345, 2326593, 393409, 1992265, 2326657, 535051, 524804, 1992329, 2326721, 535115, 2516493, 2851330, 2501134, 2516557, 2851394, 2501198, 2516621, 2851458, 2501262, 655877, 1966608, 2516685, 2851522, 2501326, 524868, 1992393, 2334724, 2763279, 524932, 2376708, 1966672, 2334788, 655941, 2763343, 524996, 3040272, 2334852, 656005, 2763407, 1966736, 2376772, 2334916, 656069, 535179, 3040336, 3375113, 2763471, 1966800, 2376836, 2728460, 535243, 3040400, 2859530, 1051154, 2376900, 3375177, 1051218, 3040464, 2728524, 1051282, 1066513, 2859594, 1051346, 1459731, 3375241, 1313300, 1066577, 2728588, 1321494, 1459795, 2859658, 1313364, 1066641, 3375305, 1321558, 1459859, 2728652, 1313428, 1066705, 2859722, 1321622, 1459923, 1810965, 1313492, 1811029, 1321686, 1811093, 1811157],
    [2258944, 2237440, 1859585, 1859649, 1859713, 1859777, 1990656, 1990720, 1990784, 2237504, 2513410, 1990848, 2513474, 534019, 2646542, 2513538, 534083, 287247, 2513602, 795663, 2408976, 418321, 2775043, 787473, 2409040, 287311, 549394, 2259008, 795727, 713236, 418385, 680455, 2775107, 787537, 2409104, 287375, 549458, 2259072, 795791, 2802197, 3039253, 418449, 2775683, 787601, 2802261, 3039317, 287439, 549522, 2259136, 795855, 942614, 2802325, 3039381, 418513, 2775747, 787665, 2802389, 3039445, 2646606, 549586, 3299342, 2237568, 2646670, 3430931, 533635, 2646734, 3299406, 2237632, 1098263, 3430995, 533699, 942678, 1098327, 680519, 3299470, 1180690, 942742, 2409168, 680583, 3431059, 1180754, 1098391, 680647, 3299534, 1180818, 942806, 3457560, 1335818, 3431123, 1180882, 3457624, 1335882, 1341447, 1582090, 3457688, 1335946, 1604102, 1844246, 3457752, 1336010, 1341511, 1582154, 1098455, 1597965, 1604166, 1844310, 713300, 1598029, 1341575, 1582218, 713364, 1598093, 1604230, 1844374, 713428, 1598157, 1341639, 1582282, 1604294, 1844438],
    [401409, 278528, 278592, 278656, 278720, 409601, 409665, 409729, 533006, 409793, 2640401, 541200, 1712144, 672274, 2902547, 541264, 1712208, 639508, 672338, 2902611, 541328, 1712272, 672402, 2902675, 541392, 1712336, 672466, 2902739, 533070, 2220565, 1064981, 533134, 3303942, 2220629, 1065045, 533198, 3304006, 2220693, 1065109, 2490902, 3304070, 2220757, 1065173, 2490966, 3304134, 2867735, 2491030, 2640465, 2744840, 786959, 2640529, 2744904, 2491094, 2640593, 2744968, 2499081, 1460762, 2745032, 2499145, 1075736, 3129881, 2499209, 1591835, 3129945, 2499273, 1460826, 2867799, 917522, 1591899, 3130009, 787023, 1075800, 2867863, 917586, 1460890, 3130073, 787087, 1075864, 2867927, 917650, 1591963, 639572, 787151, 1460954, 639636, 917714, 1075928, 639700, 401473, 1592027, 1557020, 401537, 1557084, 401601, 1557148, 1557212],
    [301056, 1884160, 1900545, 1875968, 2007041, 1876032, 2007105, 1876096, 2007169, 1876160, 2015746, 563201, 1900609, 2007233, 1884224, 2687491, 2406916, 2015810, 2687555, 2406980, 1884288, 1900673, 2407044, 2015874, 2687619, 834055, 1884352, 1900737, 834119, 2015938, 2687683, 834183, 2671119, 834247, 3080720, 2671183, 2407108, 3080784, 1095683, 2671247, 3080848, 2531860, 2671311, 1350149, 2826770, 301120, 844309, 3080912, 2531924, 975374, 1358358, 2826834, 563265, 967185, 2826898, 2531988, 1095747, 1229335, 2826962, 844373, 1350213, 3342356, 2532052, 975438, 1358422, 3342420, 1221130, 301184, 967249, 3342484, 563329, 1229399, 3342548, 1221194, 844437, 1095811, 1647123, 975502, 1350277, 1647187, 1221258, 1358486, 967313, 1647251, 301248, 1229463, 1647315, 1221322, 844501, 563393, 1095875, 975566, 1350341, 967377, 1358550, 1229527],
    [1179649, 294912, 294976, 295040, 295104, 425985, 426049, 426113, 1179713, 426177, 2394640, 1179777, 2394704, 1179841, 2402819, 2680337, 819716, 1974798, 2787332, 2811410, 819780, 2105871, 2787396, 2680401, 819844, 1974862, 2787460, 2811474, 819908, 2105935, 2787524, 2680465, 1974926, 2402883, 2811538, 2105999, 2402947, 2680529, 1974990, 2394768, 3065350, 2106063, 1212935, 2403011, 3065414, 2368005, 3065478, 2394832, 2368069, 3065542, 3312148, 2368133, 2811602, 3189269, 2368197, 1631763, 3312212, 2629632, 1631827, 3189333, 2892290, 1754646, 3312276, 2629696, 1212999, 1754710, 3189397, 2892354, 1754774, 3312340, 2629760, 1213063, 1631891, 3189461, 2892418, 1754838, 2629824, 1213127, 1631955, 2892482],
    [1892352, 1892416, 1892480, 1892544, 2023425, 2023489, 2546178, 2187266, 2023553, 2023617, 2532878, 2547726, 2546242, 2187330, 2926095, 2546306, 2187394, 2532942, 2547790, 2546370, 2187458, 2679313, 3187729, 2679377, 2842639, 719376, 3187793, 2548366, 2843215, 719440, 2679441, 3187857, 2679505, 2843279, 3187921, 2548430, 3104782, 2532494, 2843343, 719504, 2532558, 3104846, 973331, 2925647, 3104910, 1235476, 2925711, 3104974, 1112599, 2925775, 1008146, 1628694, 951319, 1139221, 973395, 1213976, 1008210, 1235540, 959504, 1139285, 1106440, 1112663, 1222169, 1008274, 1106504, 1628758, 951383, 1139349, 973459, 1214040, 1008338, 1106568, 1235604, 959568, 1139413, 2021914, 1222233, 2021978, 951959, 1112215, 1214104, 2022042, 959632, 1106632, 1628822, 1222297, 973523, 952023, 1235668, 1214168, 1112279, 960208, 719056, 1222361, 2022106, 1628886],
    [2418688, 303105, 2252801, 311297, 311361, 311425, 311489, 442368, 442432, 442496, 434702, 2514958, 2418752, 442560, 2515534, 2418816, 565775, 2146834, 2515598, 2418880, 565839, 2146898, 2515662, 565903, 322064, 573954, 565967, 2777617, 322128, 574018, 434254, 2777681, 584212, 574082, 705045, 434318, 2777745, 3336213, 705109, 434382, 2777809, 322192, 574146, 2146962, 2540054, 2252865, 2654723, 322256, 2147026, 2933271, 303169, 2252929, 3983896, 2540118, 2252993, 2654787, 3983960, 705173, 303233, 3432470, 3984024, 2933335, 3563543, 2654851, 3984088, 705237, 836121, 303297, 3432534, 3336277, 2540182, 836185, 3563607, 3336341, 2654915, 2933399, 836249, 3432598, 3336405, 2924569, 2540246, 836313, 3563671, 2924633, 584276, 2933463, 3432662, 2924697, 1755674, 1360393, 3563735, 2924761, 1755738, 1360457, 1466899, 1482770, 584340, 1360521, 1466963, 1613845, 1755802, 1360585, 1467027, 1482834, 584404, 1467091, 1613909, 1755866, 1482898, 1613973, 1482962, 1614037],
    [2308096, 1916929, 1908737, 1908801, 1908865, 1908929, 2039808, 2039872, 2458114, 2039936, 2308160, 1916993, 2040000, 2458178, 2308224, 1917057, 2458242, 2308288, 2441745, 2564628, 2458306, 1917121, 2701845, 2564692, 3113490, 2441809, 858640, 3113554, 737301, 2701909, 2564756, 2204174, 2441873, 866835, 2204238, 737365, 2701973, 2564820, 3113618, 2441937, 858704, 2204302, 737429, 2702037, 2204366, 737493, 866899, 3113682, 858768, 746007, 2596884, 866963, 746071, 1253912, 2596948, 3356696, 746135, 1253976, 2597012, 3356760, 746199, 1254040, 2597076, 1270287, 3356824, 1254104, 3356888, 1393174, 1270351, 1653273, 1653337, 1663514, 1653401, 1393238, 858832, 1663578, 1270415, 867027, 1653465, 1393302, 1663642, 1270479, 1393366, 1663706],
    [2557953, 1867777, 327680, 327744, 327808, 327872, 458753, 458817, 458881, 2558017, 1867841, 458945, 2844177, 2163216, 2558081, 2269200, 2844241, 2425347, 2556434, 2558145, 2400274, 2974723, 590340, 2163280, 2697730, 2269264, 3105796, 2425411, 2556498, 2828288, 2400338, 2974787, 590404, 2163344, 2828352, 2269328, 3105860, 2556562, 2697794, 2400402, 2844305, 2425475, 2163408, 2828416, 2269392, 2974851, 590468, 2556626, 2828480, 2400466, 3105924, 2785807, 2697858, 2844369, 2425539, 2785871, 3090958, 2974915, 590532, 2785935, 3091022, 3105988, 1867905, 2697922, 1795605, 2785999, 3091086, 1795669, 3091150, 1867969, 1795733, 3475987, 1795797, 3607060, 1507851, 1656342, 3476051, 1507915, 1918487, 3607124, 1507979, 1656406, 3476115, 1508043, 1918551, 3607188, 1656470, 1638924, 3476179, 1918615, 1638988, 3607252, 1656534, 1639052, 1918679, 1639116],
    [1925120, 2056193, 1925184, 2056257, 1925248, 2056321, 1925312, 2056385, 1950222, 2557455, 352271, 2318350, 1950286, 2318414, 1950350, 2318478, 2712081, 2849298, 2211857, 2950675, 483346, 3212306, 1950414, 2980372, 2318542, 2605584, 3111445, 2950739, 483922, 3212370, 2980436, 614917, 3111509, 2950803, 483986, 3212434, 2980500, 614981, 3111573, 2950867, 484050, 3212498, 2980564, 615045, 3111637, 3737111, 352847, 615109, 2212433, 2711633, 2848850, 3737175, 2212497, 2711697, 2848914, 2557007, 352911, 2212561, 2711761, 2848978, 3737239, 2605648, 3373590, 2557071, 352975, 2605712, 3373654, 3737303, 2605776, 3373718, 2557135, 3367451, 3504155, 1771033, 3367515, 3504219, 2033178, 3367579, 3504283, 1771097, 3367643, 3504347, 2033242, 3373782, 1771161, 2062872, 2033306, 2062936, 1771225, 2063000, 2033370, 2063064],
    [354304, 335873, 344064, 475137, 344128, 475201, 344192, 475265, 344256, 467470, 354368, 475329, 354432, 598543, 320017, 606738, 467534, 354496, 320081, 606802, 2968080, 598607, 320145, 2968144, 335937, 582164, 467598, 2968208, 320209, 2968272, 598671, 870933, 336001, 606866, 870997, 467662, 868886, 606930, 871061, 598735, 868950, 871125, 336065, 869014, 1010199, 3211795, 869078, 1263630, 3211859, 1131032, 1262085, 582228, 1402881, 3211923, 1131096, 1262149, 582292, 1010263, 3211987, 1131160, 1262213, 582356, 1263694, 2957334, 1131224, 1262277, 1402945, 3088402, 1010327, 2957398, 1263758, 3088466, 1524235, 1491481, 1403009, 2957462, 1524299, 1491545, 1010391, 3088530, 1524363, 1491609, 1263822, 2957526, 1524427, 1491673, 1403073, 3088594, 1761818, 1777688, 1761882, 1777752, 1761946, 1777816, 1762010, 1777880],
    [2070528, 1941504, 2072577, 1941568, 2072641, 1941632, 2072705, 1311234, 1687554, 1941696, 2070592, 2072769, 369168, 1311298, 2081297, 2332688, 500243, 1843730, 2081361, 2070656, 500307, 1843794, 2081425, 2070720, 500371, 1843858, 2081489, 2341390, 500435, 1843922, 1958415, 2472468, 762375, 1687618, 2097171, 2341454, 762439, 2097235, 1958479, 2472532, 762503, 1688194, 2097299, 2341518, 762567, 2097363, 1958543, 2472596, 1155608, 369232, 1688258, 2621447, 2332752, 1155672, 369296, 2621511, 1958607, 2332816, 1155736, 369360, 1310850, 647701, 2332880, 1155800, 2621575, 778264, 2341582, 1310914, 647765, 2472660, 2621639, 778328, 2884119, 647829, 3146243, 778392, 2884183, 647893, 3146307, 778456, 909849, 2884247, 3146371, 1294870, 909913, 2884311, 3146435, 1294934, 909977, 1294998, 910041, 1295062],
    [370689, 2089985, 2031617, 360448, 360512, 360576, 360640, 491521, 491585, 491649, 494094, 2293774, 2090049, 491713, 625167, 2818063, 2090113, 494158, 2293838, 2090177, 771587, 625231, 2818127, 2294414, 370753, 1041922, 493710, 771651, 2818703, 2294478, 771715, 624783, 2818767, 370817, 1033733, 1026576, 2031681, 1033797, 1304081, 1026640, 2031745, 493774, 1304145, 2031809, 1304209, 1026704, 1376786, 1304273, 1026768, 1376850, 624847, 1041986, 1376914, 1409556, 1411603, 1033861, 1376978, 1540629, 1042050, 1673236, 771779, 1550357, 1409620, 1411667, 1033925, 1540693, 1042114, 1673300, 1550421, 1409684, 1411731, 1671691, 1540757, 1673364, 1671755, 1550485, 1671819, 1409748, 1411795, 1671883, 1540821, 370881, 1802765, 1673428, 1802829, 1550549, 1802893, 1802957],
    [1302528, 1302592, 1302656, 1302720, 1433601, 1433665, 2459138, 1433729, 1433793, 2349571, 2459202, 2349635, 2459266, 803341, 2349699, 385551, 2459330, 2506767, 2349763, 385615, 2852366, 516612, 2506831, 385679, 2852430, 2506895, 2873872, 385743, 2852494, 2506959, 2852558, 3136018, 2900497, 2351122, 3376660, 3136082, 3170835, 2351186, 3376724, 803405, 3376788, 3136146, 2351250, 1287692, 803469, 3376852, 3136210, 2900561, 2351314, 1418773, 2900625, 2873936, 1287756, 803533, 2874000, 1287820, 2900689, 2874064, 1287884, 3170899, 1440278, 1549847, 3170963, 1549911, 1440342, 3171027, 1418837, 1549975, 1440406, 1418901, 1440470, 1550039, 1418965, 516676, 516740, 516804],
    [2195457, 376832, 376896, 376960, 377024, 507905, 507969, 508033, 2589193, 508097, 2589257, 2589321, 2589385, 2869772, 1016330, 2869836, 1016394, 2869900, 1016458, 2869964, 2974223, 1016522, 903694, 2974287, 2195521, 2877968, 2974351, 2195585, 2878032, 2974415, 2195649, 2878096, 999954, 1286667, 2878160, 877075, 1278477, 649748, 1286731, 649812, 901636, 877139, 1278541, 1427985, 1163781, 1286795, 649876, 1401366, 901700, 1278605, 649940, 1000018, 1163845, 1286859, 1401430, 911893, 901764, 1278669, 1428049, 1000082, 1163909, 903758, 877203, 901828, 1401494, 911957, 1163973, 1428113, 1000146, 903822, 877267, 1425927, 1401558, 912021, 1425991, 1428177, 1426055, 903886, 1426119, 912085],
    [1448960, 1975296, 1975360, 1975424, 1975488, 2106369, 2106433, 1852940, 2106497, 1449024, 2106561, 681486, 1449088, 2795023, 681550, 1449152, 2795087, 681614, 531984, 2655761, 664593, 681678, 532048, 2655825, 664657, 1853004, 532112, 2655889, 664721, 1853068, 532176, 2795151, 1058323, 1853132, 1973267, 2655953, 664785, 1058387, 2508301, 1973331, 2795215, 1058451, 2508365, 1973395, 3319302, 1058515, 2508429, 1973459, 3319366, 2508493, 2366999, 3319430, 935442, 2367063, 3319494, 935506, 2367127, 1082902, 935570, 1082966, 935634, 2367191, 1083030, 1083094, 1328665, 3022345, 1319945, 1451033, 1877524, 1328729, 3022409, 1320009, 1451097, 1877588, 1328793, 3022473, 1320073, 1451161, 1877652, 1328857, 3022537, 1320137, 1451225, 1877716, 1056282, 1738264, 1056346, 1869333, 1056410, 1738328, 1056474, 1869397, 1738392, 1869461, 1738456, 1869525],
    [369665, 1573888, 1573952, 1574016, 1574080, 1704961, 1705025, 2384399, 1705089, 369729, 1705153, 263697, 2384463, 394754, 369793, 263761, 2384527, 525842, 369857, 656899, 2384591, 2729491, 525906, 934416, 2729555, 2895366, 394818, 811527, 2360327, 2729619, 656963, 811591, 2360391, 2729683, 919060, 2895430, 2360967, 811143, 2982929, 536085, 2361031, 811207, 3507716, 919124, 2895494, 1050121, 1073161, 3638287, 919188, 536149, 1050185, 1073225, 2982993, 919252, 2895558, 525970, 1073801, 1049737, 3507780, 3288598, 394882, 1073865, 1049801, 3638351, 3419671, 263825, 934480, 657027, 2983057, 3419735, 526034, 934544, 3507844, 3419799, 263889, 934608, 394946, 3638415, 3419863, 657091, 1196050, 2983121, 3550744, 1458178, 3507908, 3288662, 1589251, 3638479, 3550808, 1196114, 1680404, 3288726, 1458242, 1942544, 3550872, 1589315, 1680468, 3288790, 1196178, 1942608, 3550936, 1458306, 1680532, 536213, 1589379, 1942672, 536277, 1196242, 1680596, 1458370, 1942736, 1589443],
    [285696, 1598464, 1729537, 1598528, 1729601, 1598592, 1729665, 1442316, 1598656, 556033, 1729729, 419330, 1442380, 687629, 2254350, 419394, 1442444, 678926, 812548, 1442508, 818188, 714255, 812612, 663566, 285760, 419458, 687693, 812676, 556097, 664142, 2253902, 419522, 678990, 664206, 2253966, 1107472, 818252, 664270, 2254030, 714319, 679054, 795155, 714383, 1334802, 795219, 714447, 1211411, 795283, 3204625, 1334866, 795347, 3204689, 1211475, 943623, 3204753, 1334930, 943687, 3204817, 285824, 943751, 1623573, 812740, 687757, 943815, 1107536, 1211539, 1205768, 1623637, 1336841, 556161, 1467915, 1107600, 1336905, 818316, 1205832, 1623701, 1336969, 1334994, 1467979, 1107664, 1337033, 679118, 1205896, 1623765, 285888, 1468043, 1893908, 687821, 1205960, 2024982, 1211603, 1468107, 1893972, 556225, 2025046, 818380, 1894036, 2025110, 1894100, 2025174],
    [271360, 377856, 1590273, 1590337, 1590401, 1590465, 1721344, 1721408, 1721472, 2369036, 517645, 1721536, 2387470, 402445, 517709, 2387534, 411140, 2369100, 517773, 673285, 2649093, 411204, 271424, 779792, 673349, 2780164, 411268, 910865, 402509, 673413, 804371, 2649157, 411332, 2491411, 2868754, 673477, 804435, 2780228, 2491475, 2868818, 804499, 2649221, 2491539, 2868882, 804563, 2780292, 2491603, 2868946, 2649285, 910929, 2369164, 2780356, 910993, 271488, 2387598, 911057, 402573, 2387662, 2369228, 779856, 1068564, 271552, 779920, 1330710, 403149, 779984, 1207832, 3409423, 517325, 1338901, 3409487, 377920, 1068628, 3409551, 377984, 1330774, 3409615, 378048, 1207896, 1713687, 1434636, 1338965, 1442817, 1565697, 1068692, 1713751, 1434700, 1330838, 1442881, 1565761, 1207960, 1713815, 1434764, 1339029, 1442945, 1565825, 1068756, 1713879, 1434828, 1330902, 1443009, 1565889, 1208024, 1339093],
    [302080, 2139136, 2139200, 2139264, 2139328, 2270209, 2270273, 2270337, 2145808, 2270401, 312850, 2426370, 572945, 312914, 2426434, 302144, 312978, 2426498, 2145872, 313042, 2426562, 573009, 2942483, 304147, 302208, 992789, 2934275, 566806, 697879, 2530836, 3343896, 3073046, 304723, 2530900, 2942035, 566870, 697943, 2145936, 992853, 3073110, 304787, 573073, 3343960, 2942099, 566934, 698007, 2530964, 984601, 3073174, 304851, 302272, 992917, 3073750, 566486, 698071, 2146000, 3344024, 2942163, 573137, 1377819, 3195927, 2531028, 992981, 2934339, 3194372, 828936, 3344088, 3195991, 3324951, 829000, 984665, 2934403, 1353226, 1484316, 3194436, 829064, 1377883, 3196055, 1353290, 1484380, 3325015, 829128, 984729, 2934467, 1353354, 1484444, 3194500, 1377947, 3196119, 1353418, 1484508, 3325079, 984793, 1885722, 3194564, 1378011, 2016284, 3325143, 1885786, 1743873, 2016348, 1743937, 1885850, 1744001, 2016412, 1744065, 1885914, 2016476],
    [1836032, 2130944, 2262017, 2131008, 2262081, 2131072, 2262145, 2286096, 2131136, 1836096, 2262209, 427538, 2286160, 1836160, 427602, 2286224, 1836224, 2797075, 427666, 2286288, 926721, 3059222, 427730, 2810389, 926785, 3182100, 689687, 2810453, 926849, 3452440, 820739, 2940951, 926913, 3452504, 689751, 3072018, 1189393, 3452568, 820803, 2941015, 1189457, 3452632, 689815, 2810517, 1189521, 2797139, 820867, 3072082, 1189585, 3182164, 689879, 2810581, 3023875, 3714585, 820931, 2941079, 3023939, 3059286, 3072146, 3024003, 3714649, 2941143, 3024067, 2797203, 3072210, 3277840, 3059350, 1237530, 3277904, 3714713, 1237594, 3277968, 3182228, 1237658, 3278032, 2797267, 1237722, 1311763, 1607182, 3059414, 1311827, 1607246, 3714777, 1499675, 1311891, 1607310, 3182292, 1499739, 1311955, 1607374, 1499803, 1499867],
    [2581504, 1998849, 2155521, 2155585, 2155649, 2155713, 2286592, 2286656, 2285072, 2286720, 2581568, 1998913, 2286784, 2285136, 2581632, 1998977, 2285200, 2581696, 1999041, 583170, 2549267, 2285264, 2573314, 2261522, 583234, 2549331, 2678289, 2573378, 696852, 583298, 2549395, 2678353, 2573442, 2261586, 583362, 2549459, 2678417, 845315, 2573506, 2261650, 845379, 2678481, 3097620, 2261714, 845443, 712214, 3367953, 1081366, 845507, 842772, 696916, 3097684, 1104914, 696980, 3097748, 842836, 697044, 3097812, 1236503, 3368017, 1236567, 3368081, 1104978, 3368145, 1236631, 3359763, 1090072, 1375256, 3359827, 1081942, 711766, 3359891, 1090136, 1762828, 1375320, 3359955, 1082006, 711830, 2057749, 1090200, 1762892, 842900, 2057813, 1082070, 1105042, 2057877, 1090264, 1762956, 1375384, 2057941, 1236695, 1763020, 711894, 842964, 1105106, 1375448],
    [287745, 295937, 1887233, 2147329, 2147393, 2147457, 2147521, 2278400, 2278464, 2278528, 550416, 296001, 1887297, 2278592, 550480, 296065, 1887361, 550544, 296129, 1887425, 3057169, 550608, 323090, 435200, 2647556, 323154, 3057233, 2909699, 445971, 435264, 2647620, 446035, 837142, 3057297, 3337238, 2909763, 435328, 2647684, 323218, 968215, 3057361, 3171351, 446099, 837206, 1099272, 435392, 3337302, 2909827, 968279, 3171415, 3573253, 446163, 837270, 3337366, 2647748, 3573317, 968343, 3171479, 3573381, 323282, 968407, 1361432, 2909891, 3573445, 3337942, 836822, 1361496, 3171543, 1091092, 1361560, 1197073, 1615381, 1361624, 1197137, 1745944, 1197201, 1091156, 1099336, 1197265, 1615445, 287809, 1746008, 1099400, 287873, 1091220, 287937, 1615509, 1099464, 1746072, 1091284, 1615573, 1746136],
    [2171904, 2171968, 2172032, 2172096, 2302977, 2303041, 2303105, 2303169, 607760, 336912, 597521, 2598418, 878099, 730644, 2440707, 2598482, 2835972, 2440771, 2598546, 2966548, 597585, 869909, 2598610, 861718, 2440835, 1017368, 869973, 990743, 870037, 3245078, 861782, 2440899, 1123865, 1017432, 2836036, 990807, 2967124, 3245142, 861846, 730196, 3087898, 337488, 1017496, 2836100, 3087962, 337552, 1123929, 2967188, 3245206, 861910, 730260, 3088026, 337616, 1017560, 2836164, 3088090, 1262617, 3245270, 730836, 1252891, 1123993, 2966740, 3777561, 1383965, 3777625, 1525276, 1252955, 607312, 3777689, 1384029, 1124057, 1262681, 3777753, 990871, 1525340, 1253019, 878163, 597649, 607376, 1384093, 1262745, 990935, 1525404, 1253083, 878227, 597713, 870101, 1384157, 607440, 1262809, 1525468, 878291],
    [2393088, 2567169, 2829840, 2393152, 2179601, 329234, 2295315, 2393216, 2960402, 2310163, 2819587, 2295379, 2829904, 2393280, 2703363, 722436, 2295443, 2524176, 2829968, 2834436, 2819651, 2295507, 329298, 2917377, 2960466, 2703427, 722500, 3081749, 2524240, 2830032, 2834500, 2819715, 3081813, 329362, 2917441, 2960530, 2703491, 722564, 3081877, 2524304, 3485204, 853511, 2834564, 2819779, 3081941, 329426, 2917505, 2960594, 2703555, 722628, 2524368, 2567233, 2834628, 2917569, 3485268, 853575, 2310227, 2567297, 3441685, 2310291, 3441749, 3485332, 2310355, 1115658, 2567361, 3441813, 853639, 2179665, 1246731, 3441877, 3485396, 2179729, 1115722, 1344529, 3746833, 2179793, 1246795, 1344593, 3746897, 853703, 3620885, 1115786, 1344657, 3746961, 3620949, 1246859, 1344721, 3747025, 3621013, 1115850, 3476487, 3621077, 1246923, 3476551, 3498518, 3476615, 3498582, 3476679, 3498646, 3498710, 1786391, 1786455, 1786519, 1786583],
    [2186240, 1958913, 2188288, 2188352, 2188416, 2188480, 2319361, 2319425, 2319489, 2186304, 1958977, 2319553, 2186368, 1959041, 615939, 1959105, 2325507, 2949650, 616003, 2606608, 2325571, 1009157, 2448389, 2606672, 2695700, 1139732, 1009221, 2579987, 2606736, 852501, 1140308, 1009285, 2580051, 2606800, 2695252, 1140372, 616067, 2325635, 2695316, 1140436, 1009349, 2448453, 2695380, 2614807, 616131, 2325699, 991766, 2580115, 2614871, 852565, 2448517, 2614935, 2949714, 2580179, 2614999, 2949778, 2448581, 2949842, 3112465, 1516056, 3112529, 1516120, 3112593, 1516184, 2876953, 3112657, 1516248, 2877017, 2186432, 991830, 2877081, 852629, 2877145, 991894, 852693, 991958],
    [355328, 320513, 2434049, 2180097, 2180161, 2180225, 2180289, 452112, 459792, 355392, 2311699, 452176, 459856, 355456, 2311763, 452240, 355520, 2434113, 2311827, 2575379, 459920, 452304, 2311891, 2575443, 443921, 2434177, 2715158, 459984, 443985, 2977303, 444049, 2434241, 2715222, 3474449, 444113, 2977367, 3474513, 1238546, 2575507, 3474577, 1369620, 2715286, 3474641, 320577, 1000986, 2977431, 1385472, 1238610, 2575571, 1369684, 1517080, 2715350, 1385536, 320641, 2977495, 1238674, 1517144, 1394189, 1001050, 1527321, 1385600, 1369748, 1394253, 1527385, 320705, 1517208, 1394317, 1001114, 1527449, 1385664, 1238738, 1394381, 1001178, 1527513, 1369812, 1517272, 1788944, 1909786, 1797121, 2041365, 2049551, 1789008, 1909850, 2049615, 1797185, 2041429, 2049679, 1789072, 1909914, 2049743, 1797249, 2041493, 1789136, 1909978, 1797313, 2041557],
    [2204672, 2335745, 2204736, 2335809, 2204800, 2335873, 2221584, 2204864, 2335937, 501265, 2221648, 2098706, 2211330, 501329, 2221712, 2098770, 2211394, 501393, 2221776, 2098834, 2211458, 501457, 2737169, 2098898, 2473492, 2860548, 2737233, 2762261, 2604036, 2860612, 2737297, 2762325, 2604100, 2860676, 2737361, 2762389, 2604164, 2860740, 1164819, 2893319, 2604228, 763414, 1295382, 894487, 3016217, 2211522, 1025562, 1557530, 894551, 3016281, 2473556, 1156635, 1688603, 894615, 3016345, 2473620, 763478, 1295446, 894679, 3154967, 2473684, 1025626, 1557594, 3016409, 3382808, 1156699, 1688667, 2893383, 3382872, 763542, 1164883, 3155031, 3382936, 1025690, 1295510, 2893447, 3383000, 1156763, 1557658, 3155095, 763606, 1688731, 2893511, 1025754, 1164947, 3155159, 1156827, 1295574, 2762453, 1811979, 1557722, 1812043, 1688795, 1812107, 1165011, 1812171],
    [2163713, 2329601, 2196480, 2196544, 2196608, 2196672, 468496, 2329665, 1819138, 2589698, 362002, 599569, 2329729, 1695762, 2590274, 362066, 468560, 2329793, 1695826, 2590338, 362130, 363536, 599633, 1695890, 2590402, 362194, 363600, 468624, 1695954, 363664, 599697, 2474517, 468688, 363728, 2474581, 3517971, 599761, 1818690, 3518035, 2163777, 2474645, 3518099, 2163841, 1818754, 3518163, 2163905, 2474709, 887825, 1254934, 1818818, 887889, 1648152, 2875930, 1279002, 887953, 1779225, 2875994, 1279066, 888017, 1254998, 2998787, 1410587, 1648216, 3910683, 2876058, 1279130, 1779289, 1551900, 2998851, 1410651, 1255062, 3910747, 2876122, 1279194, 1648280, 1551964, 2998915, 1410715, 1779353, 3910811, 2998979, 1410779, 1255126, 3910875, 1040916, 1672716, 1648344, 1552028, 1040980, 1803790, 1779417, 1552092, 1041044, 1672780, 1041108, 1803854, 1171991, 1672844, 1934863, 1172055, 1803918, 1934927, 1172119, 1672908, 1934991, 1172183, 1803982, 1935055],
    [1432576, 1860609, 2064385, 1696768, 1827841, 1696832, 1827905, 1696896, 1827969, 1696960, 1695247, 1860673, 2064449, 1828033, 386562, 1695311, 1860737, 2064513, 1695375, 1860801, 2064577, 1695439, 2227730, 2778643, 2227794, 893460, 2778707, 2227858, 893524, 2778771, 1173013, 2227922, 3244053, 2778835, 1173077, 2481680, 3244117, 2639383, 1173141, 2620945, 3244181, 2639447, 1173205, 1432640, 3244245, 2639511, 2481744, 1417750, 2639575, 2621009, 1417814, 1432704, 893588, 2481808, 893652, 2621073, 1432768, 1417878, 2481872, 1417942, 386626, 2621137, 1548813, 386690, 1548877, 386754, 1548941, 1549005, 1679886, 1679950, 1680014, 1680078],
    [2466817, 484353, 2081792, 2081856, 2081920, 2081984, 2212865, 2212929, 2212993, 476685, 2466881, 2213057, 2608654, 476749, 2466945, 2739728, 509443, 738320, 2467009, 2739792, 509507, 738384, 624140, 640529, 2739856, 509571, 738448, 624204, 640593, 2739920, 624268, 476813, 519698, 902662, 738512, 624332, 519762, 3114511, 476877, 2608718, 3114575, 1401868, 519826, 3114639, 1532945, 519890, 3114703, 1664516, 2608782, 1426953, 902726, 1401932, 3515396, 2608846, 1427017, 902790, 484417, 3515972, 640657, 912915, 1427081, 902854, 1132052, 3646481, 912979, 1427145, 1132116, 3516036, 640721, 913043, 3646545, 1533009, 913107, 1664068, 3516100, 509635, 1401996, 3646609, 484481, 3646673, 1560085, 1132180, 1541637, 1560149, 1533073, 1541701, 1560213, 1541765, 1664132, 1560277, 1402060, 1541829, 2073600, 484545, 2073664, 1132244, 2073728, 1533137, 2073792, 1664196],
    [1048576, 2377729, 1976320, 1976384, 1976448, 1976512, 2001420, 1048640, 2377793, 2001484, 1048704, 2779650, 2001548, 1048768, 543246, 2001612, 1835533, 543310, 2533906, 1835597, 543374, 666131, 2533970, 1835661, 543438, 666195, 2534034, 1835725, 2779714, 2534098, 2228225, 2779778, 3058193, 2779842, 2359315, 3058257, 2228289, 2377857, 3058321, 2377921, 2359379, 928277, 666259, 3058385, 2228353, 1198612, 928341, 666323, 3181071, 2359443, 1198676, 928405, 3181135, 2228417, 1198740, 928469, 3181199, 2359507, 1198804, 3181263, 2752533, 1468950, 1190408, 3574288, 1469014, 3015174, 1190472, 3574352, 2752597, 1853975, 1190536, 3574416, 3015238, 1854039, 1190600, 3574480, 2752661, 1993240, 3015302, 1993304, 2752725, 1469078, 3015366, 1854103, 1993368, 1469142, 1854167, 1993432],
    [2240512, 362497, 1574913, 1574977, 1575041, 1575105, 1705984, 1706048, 1706112, 2240576, 362561, 1706176, 2240640, 362625, 395778, 2240704, 2721794, 2518531, 395842, 2721858, 2764803, 544273, 395906, 2721922, 2765379, 2903570, 395970, 2721986, 397843, 544337, 362689, 2765443, 2903634, 3254799, 2896404, 2903698, 3254863, 2896468, 544401, 526854, 3254927, 657941, 2896532, 2903762, 526918, 3254991, 658005, 2896596, 544465, 526982, 3377158, 658069, 2518083, 2765507, 527046, 3377222, 397907, 2518147, 920072, 3377286, 658133, 2518211, 397971, 920136, 3377350, 3697672, 398035, 920200, 1542144, 3697736, 1192471, 920264, 1935888, 3697800, 1182232, 3639320, 3697864, 1192535, 1182296, 3639384, 1854998, 1192599, 1182360, 3639448, 1855062, 1192663, 1182424, 3639512, 1855126, 1542208, 1855190, 1935952, 1986073, 1542272, 1986137, 1936016, 1986201, 1542336, 1986265, 1936080, 2066453, 2066517, 2066581, 2066645],
    [2121728, 2123777, 2123841, 2123905, 2123969, 2254848, 2254912, 1838608, 2254976, 2121792, 2255040, 2681362, 1838672, 2121856, 2681426, 1838736, 2121920, 3197459, 1838800, 2376209, 2910742, 3197523, 265238, 2908161, 2910806, 3197587, 265302, 2376273, 2910870, 3197651, 265366, 2908225, 2910934, 3721751, 265430, 2376337, 3721815, 2625028, 2908289, 3721879, 2625092, 2376401, 3721943, 527896, 2908353, 2681490, 527960, 1204240, 2681554, 528024, 1204304, 1239573, 813577, 528088, 1204368, 1239637, 813641, 2625156, 1204432, 1501722, 813705, 2625220, 944650, 3162116, 1501786, 813769, 1052185, 944714, 3162180, 1239701, 944778, 1584660, 3162244, 1501850, 944842, 1052249, 3162308, 1862157, 1239765, 1584724, 1862221, 1501914, 1052313, 1862285, 1584788, 1862349, 1052377, 1584852],
    [1959937, 2115585, 2115649, 2115713, 2115777, 2246656, 2246720, 2107920, 2246784, 1960001, 2246848, 281107, 403986, 411666, 2222609, 412242, 2370050, 2222673, 3043860, 2770964, 412306, 403538, 2222737, 2904597, 2771540, 412370, 2370114, 1960065, 3043412, 2771604, 674327, 403602, 3131415, 3043476, 2771668, 674391, 2370178, 3131479, 3437059, 674455, 403666, 3131543, 3437123, 674519, 2370242, 3131607, 2904661, 805381, 2754583, 3655685, 2904725, 936474, 805445, 2754647, 3655749, 2904789, 805509, 2754711, 3655813, 936538, 3437187, 805573, 2754775, 3655877, 936602, 3043540, 2107984, 3140121, 936666, 3437251, 281171, 2108048, 3140185, 3559958, 281235, 2108112, 3140249, 3560022, 281299, 3287059, 3140313, 3560086, 3287123, 2222801, 3560150, 3287187, 1960129, 3830296, 3287251, 1042432, 3830360, 1714202, 1042496, 3830424, 1714266, 1042560, 3830488, 1714330, 1042624, 1714394, 1566741, 1566805, 1566869, 1566933],
    [557056, 1615873, 1615937, 1616001, 1616065, 1746944, 1747008, 1747072, 557120, 1747136, 2673166, 557184, 2009616, 2935301, 436740, 950799, 2009680, 3065860, 436804, 950863, 2009744, 2935365, 950927, 723476, 2009808, 3065924, 950991, 2796053, 2959381, 567814, 707090, 557248, 2796117, 2959445, 2673230, 827408, 2796181, 2959509, 707154, 436868, 827472, 2796245, 2959573, 567878, 3065988, 436932, 827536, 723540, 567942, 3066052, 827600, 723604, 2935429, 3047953, 723668, 2935493, 3048017, 568006, 3344919, 2673294, 3048081, 3344983, 1362456, 3048145, 3345047, 1362520, 1475084, 3345111, 1362584, 1605633, 1649178, 707218, 1352205, 1649242, 1362648, 1475148, 1649306, 2673358, 1605697, 1649370, 707282, 1352269, 3738139, 1894931, 1485322, 1475212, 3738203, 2026006, 1485386, 1605761, 3738267, 1894995, 1485450, 1352333, 3738331, 2026070, 1485514, 1475276, 2042393, 1895059, 1605825, 2042457, 2026134, 1352397, 2042521, 1895123, 2042585, 2026198],
    [2404352, 264193, 1607680, 1738753, 1607744, 1738817, 1607808, 1738881, 1607872, 2404416, 272908, 1738945, 2420238, 297474, 428046, 2404480, 272972, 2404544, 273036, 2525712, 273100, 438288, 2944529, 2656273, 264257, 3060242, 2944593, 2525776, 2656337, 264321, 438352, 2944657, 2656401, 264385, 3191316, 2944721, 2656465, 796672, 3191380, 585238, 796736, 3191444, 585302, 796800, 3191508, 2420302, 428110, 796864, 1094163, 2420366, 2525840, 428174, 1059343, 1094227, 585366, 1059407, 1094291, 585430, 2525904, 1059471, 1094355, 952838, 1059535, 1085975, 297538, 3156493, 1083912, 1086039, 1109528, 952902, 3156557, 1083976, 1086103, 297602, 3156621, 1084040, 1086167, 1109592, 952966, 3156685, 1084104, 438416, 297666, 1443858, 1214985, 438480, 1109656, 953030, 428750, 1845781, 1215049, 3452949, 2419918, 1477130, 1444434, 1215113, 3059794, 1109720, 1477194, 1845845, 1215177, 3453013, 1477258, 1444498, 3059858, 1477322, 1845909, 3453077, 1444562, 3059922, 1845973, 3453141],
    [2156545, 2156609, 2156673, 2156737, 2287616, 2287680, 2417168, 2287744, 2287808, 2417232, 2574867, 306690, 451090, 2574931, 306754, 451154, 2943510, 485909, 691715, 451218, 3074583, 3099161, 452633, 691779, 451282, 2943574, 3230232, 699930, 2417296, 3074647, 3230296, 699994, 2417360, 715269, 3099225, 452697, 830469, 3064337, 1002012, 691843, 3194902, 715333, 1002076, 453273, 830533, 3325975, 3074711, 1002140, 700058, 977438, 3064401, 3074775, 453337, 1002204, 1215518, 977502, 3194966, 2943638, 3098777, 1215582, 977566, 3326039, 1108488, 2943702, 3098841, 1215646, 977630, 3064465, 1108552, 2574995, 1215710, 1108616, 3195030, 1370634, 3230360, 1477640, 1108680, 3326103, 1370698, 2575059, 1747978, 3064529, 1370762, 3230424, 1477704, 3195094, 715397, 3885595, 1748042, 3326167, 1370826, 3885659, 1477768, 1753620, 3885723, 306818, 1630749, 715461, 3885787, 1748106, 1753684, 485973, 830597, 1630813, 486037, 691907, 1753748, 486101, 1477832, 1630877, 306882, 1753812, 1748170, 1630941, 830661, 700122],
    [2385921, 2148353, 2148417, 2148481, 2148545, 2279424, 2279488, 2132496, 2279552, 2385985, 2279616, 2421265, 2542098, 2132560, 313875, 2386049, 2421329, 2542162, 2132624, 313939, 2386113, 2804244, 2421393, 2542226, 2132688, 444949, 3041297, 2804308, 2421457, 2542290, 821269, 445013, 3041361, 2936852, 3459586, 2926594, 445077, 3041425, 2936916, 3459650, 2926658, 3041489, 848408, 821333, 681984, 848472, 821397, 682048, 838150, 848536, 3459714, 2926722, 682112, 848600, 3459778, 2926786, 314003, 682176, 838214, 1241106, 969242, 445141, 821461, 3295250, 1372697, 969306, 314067, 698387, 3295314, 2804372, 2936980, 838278, 969370, 960538, 3295378, 2804436, 2937044, 838342, 969434, 698451, 3295442, 1241170, 960602, 1337878, 1372761, 698515, 1600023, 1241234, 960666, 1337942, 1888795, 698579, 1600087, 1888859, 960730, 1338006, 1888923, 1600151, 1372825, 1338070, 1241298, 1600215, 1372889, 1888987],
    [2467840, 2170881, 2172928, 2172992, 2173056, 2173120, 2467904, 2433552, 2312721, 2566675, 2467968, 2170945, 2844691, 2566739, 2468032, 2433616, 2844755, 2566803, 2983937, 2171009, 2844819, 2566867, 2984001, 2433680, 2844883, 469507, 2984065, 2171073, 2312785, 469571, 2984129, 2433744, 2312849, 469635, 3115542, 983570, 2312913, 469699, 3246096, 1114644, 3115606, 983634, 3246160, 1114708, 879127, 3246224, 1122840, 3754008, 3115670, 1122904, 3754072, 3246288, 983698, 3754648, 3516949, 1114772, 1124889, 1525785, 3115734, 1122456, 1124953, 1525849, 3648006, 983762, 1125017, 1525913, 3517013, 1114836, 1125081, 3754712, 3648070, 1122520, 1525977, 3517077, 1796634, 3648134, 1927707, 3517141, 1796698, 3648198, 1770012, 879191, 1770076, 1927771, 1770140, 1796762, 1770204, 879255, 1927835, 1796826, 879319, 1927899],
    [305152, 1773569, 2164737, 2164801, 2164865, 2164929, 2295808, 2295872, 2295936, 690704, 1773633, 2296000, 330257, 1773697, 2140177, 330321, 690768, 1773761, 330385, 2568208, 2140241, 2820610, 330449, 2568272, 2664450, 2820674, 880148, 2951188, 2568848, 2664514, 2820738, 2846229, 2568912, 2664578, 2820802, 2846293, 2664642, 2961938, 854532, 880212, 2951252, 690320, 3223556, 854596, 2846357, 2140305, 3223620, 854660, 2846421, 690384, 3223684, 854724, 880276, 2951316, 2140369, 3223748, 1265174, 829441, 2962002, 1265238, 305216, 2962066, 880340, 2951380, 829505, 2962130, 1265302, 1380883, 305280, 3493384, 1380947, 829569, 3493448, 1381011, 305344, 3493512, 1381075, 829633, 1903116, 3886092, 1389079, 1345554, 1903180, 3886156, 1389143, 1345618, 1903244, 3886220, 1389207, 1345682, 1903308, 3886284, 1389271, 1345746, 3493576, 1265366, 2051608, 2051672, 2034191, 2051736, 2034255, 2051800, 2034319, 2034383],
    [2189313, 2189377, 2189441, 2189505, 2320384, 2320448, 2320512, 2320576, 2581008, 2581072, 3091985, 2713617, 2607634, 2975762, 2581136, 470547, 3107348, 2581200, 2559509, 3107412, 2965524, 2559573, 3107476, 2965588, 2559637, 772613, 3107540, 2965652, 2714193, 2559701, 616984, 3394073, 2965716, 2714257, 2821654, 617048, 3228183, 748038, 2714321, 2821718, 3394137, 3228247, 748102, 3091537, 3631623, 3394201, 3235847, 748166, 2821782, 3631687, 3009051, 3235911, 748230, 3091601, 3631751, 2607698, 2975826, 3235975, 1141256, 2821846, 3631815, 772677, 1272348, 3236039, 1141320, 3091665, 3009115, 1272412, 3228311, 1141384, 470611, 2607762, 1272476, 2975890, 3228375, 1141448, 470675, 780811, 1531928, 1519130, 617112, 3009179, 1531992, 470739, 780875, 1532056, 1519194, 617176, 3394265, 1272540, 2976466, 1532120, 1912349, 2607314, 1654812, 1912413, 3009243, 1654876, 1912477, 1305102, 2058254, 1654940, 1519258, 1305166, 2058318, 1655004, 1912541, 772741, 2058894, 1519322, 1304718, 2058958, 780939, 772805, 1304782, 781003],
    [2549761, 2445313, 2435600, 2549825, 2445377, 346642, 2435664, 2847234, 2812433, 477715, 337939, 2847298, 2812497, 477779, 338003, 2847362, 2812561, 2837013, 477843, 338067, 2847426, 3205141, 2837077, 477907, 338131, 3205205, 2445441, 2837141, 608771, 600600, 3205269, 2445505, 2837205, 600664, 3205333, 741393, 3492377, 600728, 741457, 2549889, 3492441, 600792, 741521, 2812625, 3492505, 346706, 2435728, 741585, 2549953, 3492569, 346770, 2435792, 1099776, 3231744, 346834, 3222043, 1099840, 3231808, 3222107, 1099904, 3231872, 3222171, 1099968, 3231936, 3222235, 1397268, 3598874, 1517586, 1397332, 3598938, 1779737, 1397396, 3599002, 1517650, 1397460, 1886743, 1779801, 1790486, 1886807, 1517714, 1790550, 1886871, 1779865, 1790614, 3599066, 1517778, 1790678, 1886935, 1779929, 608835, 608899, 608963],
    [1933312, 2344960, 1968129, 2205696, 2205760, 2205824, 2205888, 2336769, 2336833, 2336897, 1933376, 2345024, 2230800, 2336961, 2730514, 2345088, 2720273, 2361362, 2730578, 2345152, 2720337, 2361426, 2730642, 1933440, 2738690, 2361490, 2730706, 641556, 2720401, 2361554, 2992662, 1933504, 2230864, 641620, 2992726, 2230928, 641684, 2720465, 2992790, 2230992, 641748, 2466325, 2992854, 2738754, 1968193, 2466389, 2738818, 1968257, 2466453, 3385880, 2738882, 1968321, 2466517, 3786774, 2885656, 3385944, 3786838, 2885720, 3386008, 3786902, 2885784, 3025431, 3786966, 3386072, 2885848, 3271187, 3025495, 3271251, 1419787, 3025559, 3271315, 1813006, 3025623, 3271379, 1559065, 1452570, 1559129, 1452634, 1559193, 1452698, 1559257, 1452762, 1419851, 1436187, 1813070, 1436251, 1419915, 1436315, 1813134, 1436379, 1419979, 1813198],
    [372737, 2304001, 1960961, 2197504, 2197568, 2197632, 2197696, 2328577, 2328641, 2328705, 2732560, 2354192, 2304065, 2328769, 2354768, 2863633, 2304129, 2863697, 1961025, 2304193, 2354832, 460800, 2863761, 460864, 2863825, 1961089, 3256850, 2354896, 460928, 3256914, 460992, 1961153, 985104, 2732112, 3009536, 3256978, 3009600, 1247763, 756230, 887320, 3082264, 2732176, 3009664, 1018375, 887384, 3082328, 3257042, 3009728, 756294, 1018439, 887448, 3082392, 2732240, 781844, 887512, 3082456, 1413654, 781908, 756358, 1018503, 1413718, 781972, 1640983, 1018567, 1413782, 782036, 1255957, 756422, 985168, 1413846, 1166874, 1806873, 1247827, 1806937, 1641047, 1429019, 372801, 1256021, 1166938, 985232, 1807001, 1429083, 372865, 1247891, 1167002, 1807065, 1641111, 1429147, 372929, 1256085, 1167066, 985296, 1429211, 1247955, 1641175, 1256149],
    [1697792, 1697856, 1697920, 1697984, 1828865, 1828929, 2731535, 1828993, 1829057, 2648593, 2731599, 2648657, 2731663, 2648721, 2731727, 2648785, 2985490, 551443, 2343444, 2484244, 2985554, 387605, 3172373, 2736644, 518148, 2985618, 387669, 3172437, 2736708, 518212, 2985682, 387733, 3172501, 2736772, 518276, 3509783, 387797, 3172565, 2482710, 518852, 3509847, 1067545, 2736324, 2484820, 3509911, 2342996, 2484884, 3509975, 1067609, 2343060, 2484948, 3649040, 1067673, 2343124, 3649104, 1329692, 3007000, 3649168, 1329756, 2482774, 3649232, 1329820, 3007064, 1420827, 1329884, 2482838, 1420891, 1731101, 3007128, 1420955, 551507, 2482902, 1421019, 1731165, 3007192, 1936922, 1731229, 1174027, 2076190, 551571, 1174091, 1936986, 1067737, 1174155, 2076254, 1731293, 1174219, 1937050, 551635, 2076318, 1937114, 2076382],
    [2451457, 2459649, 2082816, 2082880, 2082944, 2083008, 2583052, 2459713, 379406, 2583116, 2459777, 379470, 2583180, 2459841, 2355727, 510480, 501776, 2583244, 510544, 632846, 3238413, 512529, 510608, 501840, 3238477, 512593, 379534, 632910, 3238541, 501904, 3238605, 2880019, 632974, 2451521, 2880083, 2451585, 2880147, 1280532, 3524628, 2451649, 1034773, 2880211, 1157141, 3525204, 1132544, 1034837, 1157205, 1132608, 1034901, 1280084, 1132672, 913942, 1034965, 1157269, 1132736, 2355791, 1165828, 1280660, 3524756, 1296919, 1534482, 1165892, 2355855, 1288215, 3525332, 1296983, 1534546, 914006, 1288279, 1297047, 1788440, 1165956, 2355919, 1288343, 1297111, 1788504, 1166020, 1157333, 510672, 1534610, 914070, 1288407, 379598, 1788568, 501968, 1690119, 1534674, 512657, 633038, 1690183, 1788632, 512721, 1280212, 1690247, 914134, 1690311],
    [2378752, 2272256, 1967628, 2378816, 2272320, 1967692, 2272384, 2641421, 2229774, 2272448, 2641485, 2229838, 2641549, 2927617, 2229902, 2641613, 2927681, 1967756, 273937, 2378880, 2927745, 2229966, 2378944, 2927809, 1967820, 3313154, 3173388, 2754064, 274001, 3313218, 3173452, 667154, 2885139, 798211, 3313282, 3173516, 3157524, 929301, 2885203, 3313346, 3173580, 3157588, 929365, 2885267, 274065, 674834, 1084943, 929429, 2885331, 936981, 3706372, 929493, 3146772, 1060357, 1191446, 3706436, 1199126, 798275, 3146836, 1322502, 1191510, 3706500, 1592337, 667218, 2754128, 1060421, 798339, 674898, 3706564, 1191574, 3157652, 798403, 3146900, 1322566, 1191638, 937045, 1085007, 3157716, 667282, 2754192, 1060485, 274129, 1085071, 1199190, 1322630, 3146964, 1085135, 1592401, 667346, 2754256, 1060549, 1879575, 674962, 1322694, 1879639, 937109, 1879703, 1199254, 1879767, 1592465, 675026, 937173, 1199318, 1592529],
    [2468865, 1575937, 1576001, 1576065, 1576129, 1707008, 1707072, 1707136, 2468929, 1707200, 2373136, 2509329, 1969679, 2468993, 2509393, 1969743, 2100755, 2469057, 2635284, 2509457, 2854418, 2635348, 2509521, 2100819, 2854482, 2635412, 419859, 2854546, 2373200, 419923, 2100883, 2854610, 2635476, 419987, 1969807, 626197, 2373264, 3434514, 1969871, 2100947, 626261, 2373328, 420051, 626325, 2889238, 3434578, 626389, 2889302, 3434642, 1158160, 2889366, 3434706, 1158224, 2889430, 3426319, 1158288, 398873, 3426383, 1158352, 3426447, 1281560, 3426511, 1412115, 1722389, 1805847, 1722453, 1314315, 1281624, 1062427, 1722517, 1314379, 1412179, 398937, 1722581, 1314443, 1805911, 1062491, 1985050, 1314507, 1281688, 399001, 1985114, 1412243, 1062555, 1985178, 1805975, 399065, 1985242, 1281752, 1062619, 1412307, 1806039],
    [279552, 1837056, 2018304, 2124801, 2124865, 2124929, 2124993, 279616, 1837120, 2280976, 2018368, 1837184, 542225, 1837248, 542289, 2281040, 2492948, 2804756, 279680, 2493012, 2804820, 542353, 421379, 2805396, 279744, 2631683, 421443, 2018432, 2631747, 2115076, 552470, 421507, 2631811, 2281104, 2245654, 421571, 2805460, 2631875, 2115140, 552534, 2492564, 2018496, 2245718, 552598, 2492628, 2281168, 2245782, 789010, 2115204, 3198466, 552662, 789074, 2245846, 3198530, 789138, 2115268, 3198594, 789202, 542417, 3198658, 978453, 3016705, 1074192, 1076747, 3016769, 1074256, 1371667, 1076811, 1469965, 978517, 3016833, 1074320, 1076875, 1470029, 3016897, 1074384, 1371731, 1076939, 1470093, 978581, 1583639, 1470157, 1583703, 1371795, 1863182, 978645, 1583767, 1863246, 1583831, 1371859, 1863310, 1863374],
    [2108416, 2116609, 2116673, 2116737, 2116801, 2247680, 2247744, 2512400, 2247808, 2501633, 2247872, 2512464, 2108480, 380433, 2512528, 2501697, 380497, 2512592, 2108544, 380561, 2782225, 2501761, 3132948, 2782289, 2108608, 2878997, 2782353, 2501825, 3133012, 816658, 2493456, 2879061, 816722, 2493520, 3133076, 3034648, 2782929, 2493584, 2879125, 3034712, 3167256, 2493648, 3133140, 3034776, 3167320, 658966, 2879189, 3034840, 3167384, 789521, 3403283, 3167448, 659030, 3403347, 1463835, 789585, 3403411, 1594903, 659094, 3403475, 1463899, 789649, 1175068, 1594967, 659158, 1175132, 1463963, 789713, 1175196, 1595031, 1445401, 1175260, 816786, 1846810, 380113, 1464027, 1445465, 1567769, 1595095, 1846874, 1567833, 816850, 1445529, 1567897, 1846938, 1568473, 1445081, 1847002],
    [2401280, 2296832, 2141185, 2141249, 2141313, 2141377, 2149904, 2401344, 2296896, 2403858, 2682387, 2401408, 2296960, 2403922, 2682451, 2401472, 2297024, 2682515, 2428436, 558081, 2682579, 2428500, 3048977, 437781, 2149968, 2428564, 558145, 2150032, 2428628, 3049041, 568856, 2150096, 986647, 558209, 437845, 576533, 986711, 3049105, 437909, 576597, 2952729, 558273, 437973, 576661, 2952793, 3049169, 962074, 576725, 3449879, 3083290, 962138, 3329538, 3449943, 3083354, 568920, 1224200, 3329602, 2403986, 2952857, 3450519, 1355273, 962202, 3329666, 3450583, 3083418, 1355337, 2404050, 3329730, 2952921, 3704342, 1355401, 1486365, 969757, 962266, 3704406, 3083482, 1355465, 1362968, 986263, 3704470, 1486429, 969821, 1224264, 986327, 3704534, 1486493, 1363032, 1224328, 1773083, 3580946, 568984, 1486557, 969885, 1224392, 3581010, 2035228, 1363096, 1773147, 3581074, 969949, 3581138, 2035292, 1773211, 2000414, 1363672, 568536, 2035356, 2000478, 1773275, 2000542, 2035420, 2000606],
    [2370561, 2132992, 2133056, 2133120, 2133184, 2264065, 2264129, 2264193, 2370625, 2264257, 2536977, 2657297, 2370689, 2537041, 2657361, 2370753, 2537105, 3328531, 2657425, 429075, 2764304, 2537169, 576020, 2657489, 560148, 2764368, 2798612, 576084, 3051030, 560212, 2764432, 2798676, 3328595, 3051094, 429139, 2764496, 3060758, 846361, 822297, 3051158, 560788, 396824, 953882, 2798740, 3328659, 3051222, 429203, 3025946, 953946, 3060822, 846425, 822361, 560852, 3026010, 954010, 2798804, 3328723, 429267, 3026074, 954074, 3060886, 846489, 822425, 3026138, 3060950, 846553, 822489, 396888, 1086997, 1231368, 3575323, 1346568, 396952, 1619479, 1231432, 3575387, 1346632, 397016, 1349148, 575636, 3575451, 1347208, 920603, 1087061, 1230984, 3575515, 1183250, 1619543, 1493533, 1608733, 1347272, 920667, 1349212, 1493597, 1608797, 1740300, 1183314, 1087125, 2017292, 1609373, 1871390, 920731, 1619607, 1632286, 1609437, 1183378, 1349276, 1493149, 1740364, 920795, 1087189, 2017356, 1871454, 1183442, 1619671, 1632350, 1349340, 2017932, 1739916, 1632926, 1871006, 575700, 1231048, 1740492, 1493213, 1871582, 2017484, 1632478],
    [2409472, 1869825, 1633281, 1633345, 1633409, 1633473, 1764352, 1764416, 1764480, 2409536, 2263564, 1764544, 2313741, 2158095, 2409600, 2263628, 2313805, 2551313, 2672144, 1869889, 2313869, 2158159, 2409664, 2263692, 2313933, 2551377, 574995, 1869953, 617998, 3075605, 2263756, 706066, 347157, 3075669, 1870017, 976404, 347221, 3075733, 454147, 2672208, 871958, 2158223, 454211, 2672272, 872022, 2551441, 2672336, 872086, 2918916, 715780, 3075797, 575059, 872150, 2918980, 715844, 2158287, 454275, 706130, 347285, 2919044, 715908, 2551505, 976468, 347349, 2919108, 715972, 3468823, 454339, 1500183, 1403919, 1092121, 3468887, 1500247, 1534993, 1092185, 3468951, 575123, 1658392, 1092249, 3469015, 706194, 618062, 1092313, 1240582, 1500311, 1403983, 1223194, 1240646, 976532, 1535057, 1223258, 1240710, 575187, 1658456, 1223322, 1240774, 706258, 618126, 1223386, 1500375, 1404047, 976596, 1535121, 1658520, 618190, 1404111, 1535185, 1658584],
    [2290688, 2395137, 1625088, 1625152, 1625216, 1625280, 1756161, 1756225, 2256396, 1756289, 2290752, 2395201, 1756353, 2256460, 2290816, 2534927, 2412049, 2256524, 2290880, 2665489, 2543124, 2412113, 412692, 2674197, 2665553, 2814977, 2543188, 2674261, 412756, 2815041, 2534991, 2543252, 2412177, 412820, 314882, 2665617, 2815105, 2543316, 2674325, 412884, 314946, 2815169, 2535055, 2412241, 2256588, 841239, 2665681, 3304973, 972304, 2535119, 3305037, 980504, 3444246, 708100, 315010, 3305101, 980568, 3444310, 708164, 3305165, 980632, 2395265, 2674389, 806425, 980696, 3444374, 814097, 2395329, 3331590, 708228, 1461786, 3331654, 3444438, 708292, 315074, 1461850, 3331718, 3968530, 1461914, 3331782, 1617422, 1101319, 1461978, 1898003, 3976213, 1232392, 1494538, 1600533, 841303, 3968594, 1101383, 806489, 972368, 1617486, 1232456, 1494602, 814161, 1898067, 3976277, 1101447, 1600597, 841367, 3968658, 1232520, 1494666, 806553, 972432, 1617550, 1101511, 814225, 1898131, 3976341, 1232584, 1494730, 1600661, 841431, 3968722, 806617, 972496, 1617614, 814289, 1898195, 3976405, 1600725],
    [2599936, 2565121, 2173953, 2174017, 2174081, 2174145, 2565185, 2592272, 2565249, 2592336, 2565313, 2592400, 2444802, 2827264, 2592464, 2444866, 2827328, 3255812, 2444930, 601618, 2827392, 3255876, 2444994, 601682, 732691, 2827456, 3255940, 609298, 601746, 732755, 3256004, 2958352, 609362, 601810, 732819, 3640849, 2958416, 609426, 863751, 732883, 3640913, 2958480, 609490, 994836, 863815, 1125909, 2600000, 2958544, 1002517, 1256982, 1125973, 3640977, 3605508, 1133590, 994900, 1257046, 2600064, 3868166, 1395732, 1126037, 3641041, 3605572, 3100184, 1387544, 994964, 2600128, 3868230, 3100248, 1387608, 1257110, 1126101, 3771411, 3605636, 3100312, 1387672, 995028, 3771475, 3868294, 3100376, 1387736, 1257174, 3771539, 3605700, 1133654, 3771603, 3868358, 1002581, 863879, 1902105, 1945111, 1395796, 863943, 1902169, 1945175, 1133718, 1902233, 2067994, 1002645, 1902297, 2068058, 1395860, 2068122, 1133782, 1945239, 1002709, 2068186, 1395924, 1945303],
    [2526208, 2438145, 2165761, 2165825, 2165889, 2165953, 2526272, 2438209, 2443795, 2526336, 2438273, 2705940, 2526400, 2438337, 2706004, 462338, 2962966, 2788882, 2706068, 3225109, 3190288, 2706132, 724483, 3225173, 3190352, 3360789, 2963030, 2788946, 3500034, 3225237, 2789010, 3360853, 2963094, 2789074, 3360917, 1117722, 462402, 3225301, 3190416, 3622938, 2963158, 3190480, 2443859, 462466, 4002835, 1093137, 3500098, 1117786, 4002899, 1093201, 3623002, 462530, 4003475, 1093265, 2443411, 1117850, 1521175, 3836948, 3500162, 4003539, 1093329, 3623066, 1117914, 1521239, 3837012, 3360981, 724547, 3880476, 3837076, 2443475, 724611, 3880540, 3837140, 3500226, 3880604, 2002457, 3623130, 724675, 3880668, 2002521, 1919515, 1904140, 1521303, 2002585, 1919579, 1904204, 1521367, 2002649, 1919643, 1904268, 1919707, 1904332, 2050584, 2050648, 2050712, 2050776],
    [2450433, 2092033, 2190336, 2190400, 2190464, 2190528, 2092097, 2713104, 2450497, 2092161, 2092225, 2713168, 2450561, 2616336, 2616400, 2713232, 592402, 486931, 2450625, 2616464, 592466, 749076, 486995, 2617040, 3236884, 592530, 3140627, 2712784, 731669, 1011202, 749140, 3140691, 3236948, 592594, 1011266, 1142294, 650769, 3213334, 3229190, 1142358, 650833, 3213398, 3229254, 1142422, 487059, 3140755, 3213462, 3229318, 1142486, 650897, 3213526, 3229382, 749204, 650961, 3237012, 1011330, 749268, 1273353, 487123, 3140819, 3237076, 1011394, 1273417, 1387031, 1772056, 1273481, 1787417, 1666571, 1772120, 1306138, 1926683, 1666635, 1387095, 1306202, 1666699, 1911324, 1306266, 1787481, 1666763, 731733, 1822237, 1926747, 1772184, 1822301, 1928718, 1911388, 1822365, 1928782, 1787545, 731797, 1822429, 1928846, 1926811, 1387159, 1306330, 1928910, 1911452, 1273545, 1787609, 1772248, 1926875, 731861, 1911516, 1387223],
    [357376, 2305024, 2026497, 2182145, 2182209, 2182273, 2182337, 611856, 2288656, 2305088, 611920, 2288720, 339473, 611984, 593426, 2026561, 2288784, 612048, 593490, 357440, 593554, 2026625, 2288848, 357504, 593618, 357568, 2026689, 855571, 478740, 2716692, 3206658, 339537, 740886, 3109910, 3206722, 855635, 478804, 3241478, 3206786, 339601, 740950, 2716756, 3206850, 2305152, 3109974, 339665, 846867, 478868, 3241542, 846931, 855699, 741014, 2716820, 2305216, 846995, 3110038, 847571, 855251, 3231256, 478932, 3241606, 838674, 3345432, 3231320, 741078, 2716884, 838738, 3345496, 3231384, 3110102, 838802, 3345560, 3231448, 3241670, 838866, 3345624, 1405953, 1650199, 1406017, 1650263, 1406081, 1650327, 1406145, 1650391, 2043413, 2043477, 2043541, 2043605],
    [1977345, 2206720, 2206784, 2206848, 2206912, 2337793, 2337857, 2223632, 2337921, 1977409, 2337985, 372241, 2223696, 2632721, 2862611, 2223760, 372305, 2632785, 2721300, 2993172, 2862675, 2223824, 372369, 2632849, 2721364, 2993236, 2862739, 2870291, 372433, 2632913, 2721428, 2993300, 503317, 2870355, 2862803, 1977473, 2721492, 2993364, 503381, 2870419, 1977537, 2991639, 503445, 2870483, 2362898, 3253782, 634392, 503509, 3264002, 2755603, 3253846, 765444, 3264066, 2755667, 3384857, 634456, 896538, 765508, 3264130, 1027611, 2755731, 2991703, 896602, 765572, 3264194, 1027675, 2755795, 634520, 3384921, 896666, 765636, 642075, 3017752, 2991767, 896730, 1027739, 642139, 2362962, 634584, 3253910, 642203, 3017816, 3384985, 1027803, 642267, 2363026, 2991831, 3394577, 3017880, 3253974, 3394641, 2363090, 3385049, 3394705, 3017944, 3394769, 1715740, 1690650, 1715804, 1952789, 1715868, 1690714, 1715932, 1952853, 1690778, 2065949, 1952917, 2066013, 1690842, 2066077, 1952981, 2066141],
    [2593793, 2436097, 2198528, 2198592, 2198656, 2198720, 2698768, 2593857, 2091539, 2460691, 2698832, 2593921, 2698896, 2593985, 2353686, 2698960, 2733585, 2353750, 2733649, 2436161, 3000855, 2733713, 2436225, 2615832, 2733777, 2436289, 495129, 2615896, 3353625, 2995732, 2615960, 2995796, 2690578, 495193, 757274, 2616024, 3353689, 2995860, 757338, 3000919, 2995924, 2690642, 495257, 757402, 3000983, 3353753, 758800, 2461267, 757466, 2091091, 2690706, 3388949, 495321, 1019400, 3001047, 3353817, 758864, 1019464, 2461331, 2091155, 2690770, 3389013, 1150473, 1019528, 3917850, 758928, 1248795, 1150537, 1019592, 2461395, 2091219, 3389077, 1248859, 1150601, 3917914, 758992, 1248923, 1150665, 1674762, 3917978, 3389141, 1248987, 1674826, 3918042, 1781278, 1674890, 2353814, 1781342, 1674954, 2353878, 1821213, 1781406, 1952284, 1781470, 1821277, 1952348, 1821341, 1952412, 1821405, 1952476],
    [2343936, 2509825, 1698816, 1698880, 1698944, 1699008, 1829889, 1829953, 1830017, 2475535, 2509889, 1830081, 2591248, 2475599, 2509953, 2591312, 2475663, 2510017, 2591376, 2772498, 2475727, 388610, 2591440, 2772562, 2344000, 388674, 764436, 2772626, 2344064, 388738, 764500, 2772690, 2344128, 895511, 3042324, 3130901, 764564, 3042388, 3130965, 895575, 3042452, 3131029, 1149464, 3566616, 3131093, 895639, 3567192, 2745360, 1149016, 3567256, 2745424, 895703, 3567320, 2745488, 3508740, 1043973, 3043028, 2745552, 3508804, 1044037, 1723921, 3508868, 1044101, 1723985, 3508932, 1044165, 1724049, 1944089, 1724113, 1944153, 1732115, 1149080, 1994262, 1944217, 1732179, 1149144, 1994326, 388802, 764116, 1732243, 1944281, 1994390, 1732307, 1994454],
    [2321408, 2216961, 2083840, 2083904, 2083968, 2084032, 2453004, 2217025, 2723341, 2346511, 2453068, 2487311, 2723405, 2477584, 2346575, 2453132, 2487375, 2723469, 2477648, 2346639, 2453196, 2487439, 2723533, 2477712, 2346703, 2487503, 2583553, 3386897, 2477776, 3001875, 2610192, 2321472, 3247630, 3001939, 2610256, 2583617, 3386961, 3002003, 2610320, 2321536, 3247694, 3002067, 2610384, 2583681, 3387025, 2321600, 2217089, 3247758, 2583745, 2217153, 3387089, 3011603, 3108355, 3247822, 511512, 3011667, 3108419, 1289749, 3011731, 3108483, 1289813, 3011795, 3108547, 904729, 1035782, 1289877, 3362322, 904793, 1035846, 1289941, 3624468, 904857, 1035910, 1543703, 3755032, 904921, 1035974, 1682966, 511576, 3362386, 1297928, 1813529, 511640, 3624532, 1297992, 1543767, 511704, 3755096, 1298056, 1683030, 3362450, 1298120, 1813593, 3624596, 1543831, 3755160, 1683094, 3362514, 1813657, 3624660, 1543895, 3755224, 1683158, 1813721],
    [2379776, 2265089, 1978369, 1978433, 1978497, 1978561, 2109440, 2109504, 2099724, 2109568, 2379840, 2265153, 2109632, 2503184, 2099788, 2379904, 2265217, 2503248, 2238993, 2379968, 2265281, 2503312, 2239057, 422415, 2527244, 2239121, 2527308, 807438, 2239185, 2527884, 553490, 2099340, 2527948, 946709, 2099404, 3052045, 422479, 2623504, 3297795, 3052109, 2623568, 3052173, 946773, 2623632, 3052237, 807502, 2503376, 2623696, 692755, 553554, 2894356, 422543, 692819, 2894420, 692883, 946837, 2894484, 692947, 807566, 2894548, 3297859, 1216527, 3297923, 1347605, 3148311, 3289111, 3297987, 1216591, 3148375, 3289175, 1323529, 1724950, 1347669, 3148439, 3289239, 1323593, 1725014, 1216655, 3148503, 3289303, 1323657, 1725078, 1347733, 1323721, 1217231, 553618, 1725142, 1348309, 422095, 946389, 807630, 553682],
    [2504704, 2388993, 1576961, 1577025, 1577089, 1577153, 1708032, 1708096, 1708160, 2636303, 2389057, 1708224, 2593296, 2504768, 2389121, 2593360, 2636367, 2389185, 2593424, 3036160, 2504832, 2593488, 3036224, 2636431, 3379732, 3036288, 2504896, 3379796, 266755, 3036352, 2636495, 3379860, 266819, 3029525, 3044355, 3379924, 266883, 3029589, 3044419, 1020435, 266947, 3029653, 3044483, 1151510, 3291158, 3044547, 1151574, 3291222, 3307026, 3641879, 3291798, 3307090, 3641943, 791047, 922136, 3291862, 3307154, 3772440, 1053192, 922200, 3029717, 3307218, 3772504, 791111, 922264, 2497041, 1725460, 3772568, 1053256, 922328, 2497105, 1471511, 3642007, 791175, 2497169, 1725524, 3772632, 1053320, 2497233, 1471575, 3642071, 791239, 1725588, 1020499, 1053384, 1471639, 1151126, 1725652, 1020563, 1471703, 1151190, 1020627, 2069017, 2069081, 2069145, 2069209],
    [2516992, 2412544, 2125825, 2125889, 2125953, 2126017, 2412608, 289296, 2110993, 2519570, 2412672, 289360, 2111057, 2650643, 2519634, 2412736, 289424, 291331, 2111121, 2650707, 2519698, 2912788, 2805761, 289488, 2111185, 2650771, 2519762, 2912852, 2805825, 3033107, 2766357, 2650835, 2912916, 2805889, 3033171, 2766421, 2912980, 2805953, 3033235, 2766485, 684567, 815640, 3076119, 3033299, 2766549, 684631, 3076183, 3164178, 2757652, 684695, 3076247, 3164242, 2757716, 1110553, 3164306, 2757780, 684759, 3076311, 3164370, 1208840, 2757844, 815704, 1503250, 2517056, 291395, 3552790, 815768, 1503314, 2517120, 1208904, 3552854, 815832, 1503378, 2517184, 1339913, 3552918, 1503442, 1206289, 1339977, 3552982, 1206353, 1495579, 291459, 3683352, 1206417, 1110617, 1340041, 3683416, 1206481, 1110681, 1208968, 3683480, 1110745, 291523, 3683544, 1495643, 1340105, 1455642, 1495707, 1209032, 1455706, 1495771, 1455770, 1455834],
    [1961985, 2117633, 2117697, 2117761, 2117825, 2248704, 2248768, 2232848, 2248832, 1962049, 2248896, 283153, 2232912, 1962113, 2652691, 283217, 2232976, 1962177, 2652755, 2233040, 2871313, 545301, 2652819, 274453, 2871377, 676376, 3037719, 536600, 2617344, 676440, 2652883, 938521, 528916, 2617408, 676504, 3037783, 283281, 536664, 2871441, 676568, 3037847, 283345, 528980, 2871505, 545365, 3168794, 3027464, 2617472, 545429, 3168858, 938585, 3027528, 2617536, 545493, 3027592, 3011094, 938649, 3027656, 3142162, 938713, 274517, 3011158, 3168922, 274581, 3142226, 3562011, 536728, 3011222, 3562075, 529044, 3142290, 3562139, 274645, 3011286, 3037911, 1593884, 1454108, 3142354, 3562203, 1593948, 1454172, 3403801, 3168986, 1594012, 1454236, 3403865, 1735197, 1594076, 536792, 3403929, 1735261, 529108, 3403993, 1735325, 1856015, 1454300, 1735389, 1856079, 1856143, 1856207],
    [1878016, 1904640, 2142208, 2142272, 2142336, 2142400, 2166785, 559632, 446993, 2043920, 559696, 447057, 307730, 1904704, 2271250, 447121, 307794, 2166849, 2271314, 447185, 307858, 2043984, 2271378, 3068435, 307922, 1904768, 2271442, 709140, 2166913, 559760, 3199509, 2044048, 559824, 3199573, 1878080, 1904832, 3199637, 700931, 1878144, 2166977, 3199701, 700995, 832024, 2044112, 3049496, 3068499, 701059, 832088, 3346946, 3049560, 3068563, 832152, 856599, 3049624, 3068627, 1225221, 832216, 987155, 3049688, 1634838, 1225285, 1618457, 856663, 3442713, 709204, 1225349, 1618521, 987219, 3442777, 1634902, 1880583, 1618585, 1225413, 856727, 3442841, 3731976, 1880647, 1618649, 987283, 3442905, 3732040, 1880711, 1878208, 3347010, 3732104, 1880775, 1353729, 3347074, 3732168, 701123, 1353793, 3347138, 1896986, 856791, 1353857, 1897050, 987347, 1353921, 1897114, 709268, 1634966, 1897178, 709332, 1635030],
    [2101248, 2398208, 2134017, 2134081, 2134145, 2134209, 2101312, 2398272, 2422290, 2101376, 2398336, 2422354, 2626067, 2923028, 2422418, 2626131, 2923092, 2422482, 406037, 2923156, 406101, 2923220, 718358, 2398400, 406165, 710167, 3447299, 406229, 718422, 3447363, 2626195, 561688, 718486, 2799640, 2101440, 561752, 718550, 2799704, 2626259, 561816, 2799768, 3158545, 561880, 2799832, 3158609, 3339784, 3062279, 3158673, 3339848, 823818, 3062343, 3158737, 3339912, 823882, 3062407, 3019280, 3339976, 823946, 3062471, 3019344, 3577872, 3019408, 3577936, 3019472, 1716761, 3578000, 1716825, 3578064, 824010, 1716889, 3447427, 1716953, 3447491, 2020890, 710231, 2020954, 710295, 2021018, 710359, 2021082],
    [2584577, 2158593, 2158657, 2158721, 2158785, 2289664, 2289728, 2405904, 2410512, 2289792, 2584641, 2289856, 2790930, 2411088, 2584705, 2790994, 2411152, 2584769, 324099, 586242, 2405456, 2411216, 2839059, 324163, 2791058, 3590147, 2839123, 324227, 3590211, 2405520, 2839187, 324291, 2791122, 3590275, 2839251, 717335, 3590339, 2405584, 3371026, 833044, 3852311, 3502613, 979480, 3183640, 3467793, 3371090, 979544, 3183704, 3467857, 3502677, 979608, 3183768, 3467921, 3371154, 979672, 3183832, 3467985, 3502741, 717399, 833108, 3852375, 3371218, 717463, 833172, 3852439, 3502805, 717527, 833236, 3852503, 3756553, 2012694, 3756617, 1624601, 2012758, 3756681, 2012822, 3756745, 1765900, 1624665, 2012886, 1658905, 586306, 1763866, 1667089, 586370, 1763930, 1658969, 586434, 1624729, 1667153, 1763994, 1659033, 1624793, 1667217, 1765964, 1764058, 1659097, 1766028, 1667281, 1766092],
    [2414592, 2387969, 2150401, 2150465, 2150529, 2150593, 2535952, 2414656, 2388033, 2536016, 2642449, 2414720, 2536080, 2642513, 2414784, 2536144, 3078161, 2642577, 578067, 2929155, 3078225, 2642641, 569363, 3078289, 3166740, 2929219, 3078353, 2388097, 2929283, 842258, 2388161, 840213, 2929347, 842322, 971286, 1102360, 3322374, 842386, 971350, 578131, 3322438, 842450, 3166804, 840277, 3322502, 3734039, 3166868, 578195, 1364488, 3322566, 3864600, 3166932, 840341, 1486869, 3734103, 971414, 578259, 1102424, 1749014, 3864664, 971478, 840405, 1102488, 569427, 3734167, 1331737, 1102552, 1486933, 3864728, 1462810, 1749078, 3734231, 1462874, 1757723, 2011163, 3864792, 1331801, 1364552, 569491, 1890844, 1462938, 1757787, 2011227, 1364616, 1890908, 1331865, 1364680, 1486997, 1890972, 1463002, 1757851, 2011291, 1891036, 1749142, 1331929, 1757915, 569555, 1487061, 2011355, 1749206],
    [2426880, 2461696, 1650689, 1650753, 1650817, 1650881, 2461760, 2689548, 2576910, 2426944, 2461824, 2707981, 2461888, 2689612, 348688, 2427008, 3117068, 2708045, 2689676, 3248129, 2576974, 2830867, 2427072, 3117132, 348752, 2830931, 2689740, 3248193, 2708109, 2830995, 3117196, 1116687, 2577038, 2831059, 3248257, 862227, 3093014, 348816, 3117260, 993302, 3093078, 2708173, 3248321, 1378839, 3093142, 471556, 2577102, 1421845, 993366, 3093206, 602629, 348880, 1421909, 1378903, 471620, 3363345, 1421973, 1509913, 602693, 3494424, 733702, 1422037, 1116751, 471684, 3363409, 864775, 1675794, 862291, 602757, 3494488, 733766, 993430, 1946138, 995848, 471748, 3363473, 864839, 1126922, 1675858, 1378967, 995912, 602821, 3494552, 733830, 1126986, 1946202, 1116815, 995976, 3363537, 864903, 1127050, 1675922, 862355, 996040, 3494616, 1127114, 1509977, 1946266, 1929748, 1675986, 1510041, 2060306, 993494, 1946330, 1929812, 733894, 1510105, 2060370, 864967, 1379031, 1929876, 1116879, 2060434, 862419, 1929940, 2060498],
    [2061312, 2439169, 2273281, 1642496, 1642560, 1642624, 1642688, 2061376, 2570764, 2273345, 2036237, 2570828, 2273409, 2454541, 2036301, 2439233, 2798094, 2454605, 2036365, 2429455, 2061440, 2570892, 2798158, 2036429, 2439297, 2798222, 2454669, 2691603, 2061504, 2570956, 2798286, 2822676, 2429519, 2691667, 735252, 2273473, 2454733, 2822740, 2691731, 2847763, 735316, 430093, 2822804, 2691795, 2978831, 735380, 430157, 2822868, 2429583, 2847827, 735444, 430221, 463362, 963096, 2978895, 2439361, 2847891, 963160, 3086865, 2429647, 963224, 2978959, 3086929, 2847955, 963288, 3086993, 2979023, 954903, 3087057, 1136150, 1645074, 954967, 1136214, 1776153, 955031, 1136278, 1645138, 955095, 1136342, 1776217, 430285, 463426, 1479184, 1645202, 463490, 1776281, 2003477, 463554, 1511946, 1479248, 1645266, 1512010, 1776345, 2003541, 1512074, 1479312, 2045967, 1512138, 2046031, 2003605, 1479376, 2046095, 2046159, 2003669],
    [2478080, 2181121, 2191361, 2191425, 2191489, 2191553, 2322432, 2322496, 2322560, 2181185, 2740752, 2322624, 2692626, 356370, 2181249, 2740816, 2692690, 356434, 2181313, 2740880, 619027, 463891, 2740944, 750100, 734228, 2478144, 881154, 865282, 739861, 2478208, 750164, 734292, 3369494, 2478272, 619091, 463955, 3369558, 357010, 3133969, 881218, 2692242, 3369622, 357074, 3134033, 750228, 2692306, 3369686, 1143300, 3134097, 619155, 3741189, 739925, 1143364, 3134161, 881282, 3741253, 739989, 3527191, 750292, 3741317, 740053, 3527255, 619219, 3741381, 1405464, 1143428, 3527319, 881346, 1250328, 1405528, 1143492, 1395225, 1250392, 1405592, 3527383, 1250456, 1405656, 1561114, 1657371, 1250520, 1536522, 1692188, 1665565, 1512452, 1536586, 1395289, 1692252, 1512516, 1536650, 1561178, 1657435, 865346, 1536714, 1692316, 1665629, 734356, 1395353, 1561242, 1798670, 1512580, 1692380, 1657499, 1798734, 464019, 1561306, 1665693, 1798798, 865410, 1395417, 1798862, 734420, 1657563, 1512644, 1665757, 464083, 865474],
    [489472, 2183169, 2183233, 2183297, 2183361, 2314240, 2314304, 1913360, 2314368, 620545, 2314432, 315922, 1913424, 2587153, 2552340, 1913488, 2587217, 2675221, 1913552, 489536, 2675285, 2699795, 620609, 2970134, 2675349, 2699859, 2587281, 2970198, 2813974, 2699923, 489600, 2970262, 2675413, 2699987, 620673, 2970326, 479767, 2552404, 339991, 2587345, 872984, 479831, 2814038, 1004057, 593945, 489664, 2552468, 725530, 620737, 873048, 479895, 2814102, 1135131, 594521, 1003609, 2552532, 725594, 873112, 2814166, 1004185, 594073, 479959, 3469336, 725658, 873176, 3469400, 1004249, 594137, 3469464, 1135195, 725722, 3469528, 340055, 315986, 1135259, 340119, 316050, 340183, 316114, 1135323, 1519643, 2019868, 1519707, 2019932, 1519771, 2019996, 1519835, 2020060],
    [1970176, 2347009, 2207744, 2207808, 2207872, 2207936, 2338817, 2338881, 2599440, 2338945, 2494480, 2347073, 2339009, 2861585, 2495056, 2347137, 2598992, 2495120, 2347201, 2994707, 2852883, 389650, 2495184, 2994771, 2852947, 389714, 2756625, 2994835, 2853011, 389778, 1970240, 2994899, 2853075, 389842, 2757201, 3123734, 1970304, 2748432, 3123798, 2748496, 2757265, 2861137, 1970368, 2748560, 2599056, 2748624, 2757329, 897543, 3123862, 930327, 905239, 1159688, 2861201, 1061400, 1167384, 1159752, 2599120, 930391, 905303, 1683978, 3123926, 1061464, 1167448, 1684042, 2861265, 930455, 905367, 1684106, 1804820, 1061528, 1167512, 1684170, 1681945, 930519, 905431, 2075163, 1061592, 1167576, 1804884, 1307157, 1314834, 1682009, 1438236, 1847834, 2075227, 1307221, 1314898, 897607, 1804948, 1438300, 1847898, 1159816, 1682073, 1307285, 1314962, 897671, 2075291, 1438364, 1847962, 1159880, 1805012, 1307349, 1315026, 897735, 1682137, 1438428, 1848026, 2075355],
    [366593, 1963009, 2199552, 2199616, 2199680, 2199744, 2330625, 2330689, 2330753, 2356752, 366657, 2330817, 2356816, 366721, 2175508, 2986515, 364564, 1963073, 366785, 2437653, 2986579, 495637, 2209808, 2356880, 2437717, 2986643, 495701, 2209872, 1963137, 2437781, 2986707, 495765, 2603523, 2356944, 332310, 496341, 2603587, 1963201, 2953751, 889368, 2603651, 2618387, 2953815, 889432, 2209936, 2618451, 2953879, 365140, 2603715, 2618515, 2953943, 889496, 2210000, 2618579, 3355140, 365204, 2865176, 2880535, 3355204, 889560, 2865240, 2880599, 3355268, 1282570, 365268, 2865304, 2880663, 2437333, 1282634, 2865368, 2880727, 3355332, 1282698, 1546769, 1177106, 2175060, 1282762, 1546833, 1177170, 2175124, 1546897, 1177234, 2175188, 1546961, 1177298, 332374, 332438, 332502],
    [2213888, 1699840, 1699904, 1699968, 1700032, 1830913, 1830977, 2471439, 1831041, 2213952, 1831105, 414225, 2093584, 2471503, 2476049, 2781714, 2987540, 2476625, 3174420, 2987604, 2476689, 3174484, 2987668, 2476753, 3174548, 2987732, 2214016, 3174612, 2471567, 2214080, 2781778, 2471631, 3262480, 2781842, 3642386, 2746901, 2781906, 3642450, 2746965, 1069590, 2093648, 3642514, 3262544, 520709, 413777, 2093712, 3642578, 3262608, 1069654, 2093776, 3257875, 3262672, 1200667, 651782, 3257939, 2747029, 1200731, 782856, 3258003, 2747093, 413841, 651846, 3258067, 4049433, 1200795, 782920, 1553943, 4049497, 1069718, 651910, 1554007, 4049561, 520773, 413905, 782984, 1554071, 4049625, 520837, 1200859, 651974, 1554135, 520901, 1069782, 783048, 1947160, 1994775, 2078234, 1994839, 1947224, 1994903, 2078298, 1994967, 1947288, 1569293, 1987100, 2078362, 1569357, 1987164, 1947352, 1569421, 1987228, 2078426, 1569485, 1987292],
    [2453504, 2469889, 2095105, 2084864, 2084928, 2084992, 2085056, 2601484, 2715660, 2095169, 2609678, 2601548, 2715724, 2095233, 2609742, 2601612, 2715788, 2095297, 2609806, 2601676, 2715852, 2619920, 2609870, 2453568, 3125773, 2619984, 381457, 2453632, 3125837, 2620048, 2453696, 3125901, 2620112, 610835, 3013122, 3125965, 610899, 2469953, 1047058, 3265044, 3013186, 3633166, 2470017, 643605, 3265108, 3764245, 2470081, 1047122, 643669, 3265172, 1290257, 610963, 3013250, 643733, 3265236, 611027, 1047186, 643797, 1552918, 1036310, 3764309, 3013314, 1815063, 1298455, 3633230, 1047250, 1552982, 1036374, 3764373, 3405844, 1815127, 1298519, 381521, 3405908, 3633294, 2077208, 1429528, 1036950, 3764437, 3405972, 381585, 1290321, 1299095, 3406036, 3633358, 2077272, 1429592, 1037014, 1825295, 381649, 1290385, 1299159, 1825359, 1552534, 2052633, 1430168, 1825423, 2076824, 2052697, 1825487, 1814679, 2052761, 1430232, 1290449, 2052825, 2076888, 1552598, 1814743],
    [2397184, 2239489, 1979392, 1979456, 1979520, 1979584, 2381324, 2239553, 2659340, 275982, 2774541, 2239617, 2659916, 276046, 2774605, 2239681, 2659980, 2774669, 2660044, 2231823, 2774733, 2397248, 407056, 2380876, 2397312, 407120, 2380940, 2397376, 2231887, 2381004, 693249, 405010, 276110, 947729, 693313, 545806, 693377, 2231951, 538131, 676880, 693441, 405074, 669204, 538195, 807955, 2887189, 1095190, 407184, 939028, 2887253, 1095254, 538259, 947793, 2887317, 1095318, 276174, 545870, 669268, 2887381, 1095382, 407248, 676944, 669332, 2232015, 1611288, 538323, 808019, 1453591, 1611352, 800260, 939092, 1453655, 669396, 1611416, 800324, 947857, 1453719, 1742361, 800388, 545934, 1453783, 1742425, 800452, 677008, 405138, 1193479, 1742489, 808083, 405202, 1324553, 1611480, 939156, 1193543, 1586699, 1742553, 947921, 1324617, 1586763, 545998, 1193607, 1586827, 677072, 1324681, 1586891, 808147, 1193671, 939220, 1324745],
    [1577985, 1578049, 1578113, 1578177, 1709056, 1709120, 2511375, 1709184, 1709248, 2511439, 2511503, 2375184, 2602513, 2511567, 1711121, 2602577, 3305489, 1711185, 2602641, 2233876, 3035156, 1711249, 2602705, 2233940, 3035220, 1711313, 3380757, 267285, 2364950, 2234004, 3035284, 2375248, 3511318, 267861, 3305553, 2375312, 3773975, 267925, 2365014, 2234068, 3035348, 2375376, 3511382, 267989, 3305617, 3380309, 2365078, 3305681, 3774039, 3568146, 3511446, 2365142, 3568210, 3380373, 3568274, 2629147, 3774103, 3151386, 3568338, 3511510, 2898970, 3151450, 3699219, 2899034, 3380437, 3151514, 3699283, 2899098, 3774167, 3151578, 3699347, 1676824, 2899162, 3699411, 2629211, 1938972, 1864217, 2629275, 1676888, 1864281, 2629339, 1939036, 1864345, 1676952, 1864409, 1939100, 1677016, 1939164],
    [281600, 316417, 1839105, 2126849, 2126913, 2126977, 2127041, 2257920, 2257984, 2258048, 281664, 456208, 2363408, 2258112, 281728, 1839169, 456272, 281792, 2363472, 456336, 579093, 290321, 1839233, 2911766, 579157, 2363536, 2911830, 579221, 1839297, 2911894, 579285, 2364112, 2911958, 667669, 455888, 3200531, 3436055, 799250, 3200595, 3436119, 667733, 3200659, 3436183, 799314, 3200723, 3436247, 667797, 683540, 799378, 316481, 2888217, 316545, 945168, 2888281, 290385, 316609, 1340938, 2888345, 1635864, 683604, 1341002, 2888409, 1766400, 945232, 1341066, 1635928, 667861, 290449, 1341130, 1585690, 1766464, 683668, 1585754, 1635992, 945296, 1766528, 290513, 799442, 1585818, 1636056, 683732, 1766592, 945360, 1585882],
    [2094080, 1997825, 2118657, 2118721, 2118785, 2118849, 2249728, 2249792, 2249856, 2225680, 1997889, 2249920, 2242065, 2225744, 1997953, 2242129, 2643475, 2225808, 1998017, 2242193, 2905620, 2784256, 2225872, 2242257, 2905684, 2784320, 2094144, 2897426, 2905748, 2784384, 2094208, 3028483, 2905812, 2784448, 2094272, 2897490, 2741268, 3046417, 3028547, 2643539, 2741332, 3046481, 2897554, 2741396, 3046545, 3028611, 2643603, 2741460, 3046609, 2897618, 2514453, 2749459, 3028675, 2643667, 2514517, 2749523, 3421698, 1070600, 2514581, 2749587, 3421762, 1201673, 2514645, 2749651, 3421826, 1070664, 3266070, 3421890, 1201737, 3266134, 3282436, 1070728, 3266198, 3282500, 1201801, 3266262, 3282564, 1070792, 1570327, 3282628, 1857036, 1201865, 1570391, 1447448, 1570455, 1447512, 1857100, 1570519, 1447576, 1857164, 1447640, 1717785, 1857228, 1717849, 1717913, 1717977],
    [297984, 340993, 2143232, 2143296, 2143360, 2143424, 2545168, 298048, 341057, 308754, 2545232, 298112, 2823697, 439828, 447508, 298176, 2823761, 439892, 447572, 2919957, 2823825, 439956, 447636, 2920021, 2823889, 440020, 447700, 3320833, 3216899, 570884, 308818, 2545296, 2920085, 3216963, 308882, 2545360, 3320897, 3217027, 308946, 3069442, 2920149, 3217091, 964101, 3069506, 3749399, 3320961, 964165, 3069570, 3749463, 3321025, 964229, 3069634, 3583512, 3749527, 964293, 1496598, 3583576, 341121, 1758226, 3583640, 3749591, 1504793, 3583704, 341185, 1488393, 1504857, 4133888, 3845651, 1496662, 4133952, 3845715, 1758290, 4134016, 3845779, 1504921, 4134080, 3845843, 1496726, 1905685, 2010129, 1758354, 1905749, 2010193, 570948, 1504985, 1905813, 2010257, 571012, 1496790, 1905877, 2010321, 571076, 1758418, 1488457, 1488521, 1488585],
    [2281473, 2135040, 2135104, 2135168, 2135232, 2266113, 2266177, 2266241, 2281537, 2266305, 300561, 2543633, 2268690, 1971218, 300625, 2543697, 2922003, 300689, 2543761, 2922067, 300753, 2543825, 2922131, 2268754, 1971282, 2281601, 2922195, 2281665, 3159573, 2661397, 3207187, 2661973, 1971858, 1233430, 3159125, 2268306, 1233494, 2662037, 1971922, 824838, 1233558, 3159189, 2268370, 1233622, 3159765, 2661589, 3207251, 3315225, 3290137, 835096, 3207315, 3315289, 3290201, 835160, 3207379, 3315353, 3290265, 835224, 824902, 3330576, 3315417, 3290329, 835288, 824966, 3600916, 1480218, 661001, 1489946, 825030, 3330640, 1480282, 791558, 1490010, 3600980, 1480346, 931341, 1490074, 3330704, 1480410, 661065, 1490138, 3601044, 791622, 1752590, 3330768, 931405, 1752654, 3601108, 661129, 2028055, 791686, 1752718, 2028119, 931469, 2028183, 661193, 1752782, 2028247, 791750, 931533],
    [349184, 1895425, 2159616, 2159680, 2159744, 2159808, 2667024, 349248, 1895489, 325122, 2667088, 2184721, 2812945, 2667152, 2184785, 2813009, 2667216, 1895553, 2184849, 2658834, 2577923, 2813073, 587268, 2920981, 2935812, 2577987, 587332, 2658898, 2935876, 2578051, 587396, 2921045, 2935940, 2578115, 587460, 2658962, 2936004, 2184913, 2921109, 2971156, 1895617, 849432, 2659026, 3101720, 2813137, 849496, 2921173, 3101784, 3066896, 849560, 1356310, 3101848, 3066960, 849624, 1356374, 3101912, 3067024, 325186, 1356438, 3067088, 2971220, 3470873, 3444761, 325250, 3460627, 2971284, 3470937, 3444825, 325314, 3460691, 2971348, 3471001, 3444889, 1266707, 3460755, 3471065, 3444953, 1266771, 3460819, 1356502, 1266835, 1502229, 1741335, 349312, 1502293, 1741399, 1266899, 1502357, 1741463, 349376, 1502421, 1741527, 1537025, 1537089, 1537153, 1537217],
    [2151424, 2151488, 2151552, 2151616, 2282497, 2282561, 2528784, 2415632, 2520080, 2282625, 2282689, 2651665, 2528848, 2415696, 2676227, 2651729, 2416272, 3052547, 2807315, 2651793, 2416336, 3053123, 2675779, 2807379, 588817, 2651857, 2528400, 2676355, 2807443, 720405, 3052675, 2913299, 2807507, 588881, 2520144, 2528464, 3192338, 720469, 2913363, 3192402, 588945, 2520208, 2676419, 720533, 3052739, 2913427, 3192466, 589009, 2520272, 1103367, 3298311, 3192530, 720597, 1234455, 1103431, 1225751, 3298375, 1365512, 1103495, 3298439, 1218068, 1627672, 1103559, 1367577, 1750040, 3298503, 1234519, 1367641, 1225815, 2913491, 1365576, 1244698, 3429384, 1881113, 1627736, 1244762, 3429448, 1750104, 1234583, 1367705, 1225879, 1603094, 1365640, 1244826, 3429512, 1881177, 1627800, 1367769, 1750168, 1603158, 1234647, 1244890, 1225943, 1603222, 1365704, 3429576, 1881241, 1627864, 1750232, 1603286, 1881305, 1218132, 1218196, 1218260],
    [2462720, 2176000, 2176064, 2176128, 2176192, 2307073, 2307137, 2192912, 2307201, 2462784, 2307265, 331282, 2569234, 2192976, 2856465, 331346, 2569298, 2193040, 2856529, 2700819, 472596, 331410, 2569362, 2193104, 603669, 2462848, 2700883, 472660, 331474, 2569426, 742420, 603733, 2856593, 2700947, 3222547, 603797, 742484, 2462912, 2701011, 3222611, 603861, 1012757, 2856657, 3222675, 1012821, 1160193, 3616280, 1012885, 1160257, 3616344, 1012949, 1160321, 472724, 3616408, 742548, 1160385, 472788, 3616472, 742612, 3126290, 996892, 3214875, 1004572, 3126354, 996956, 3214939, 1127966, 3363870, 3126418, 997020, 3215003, 1128030, 3363934, 3126482, 997084, 3215067, 1128094, 3363998, 1021465, 1652233, 3222739, 1004636, 1685018, 1652297, 1379862, 1783327, 3364574, 1127646, 1021529, 1652361, 1510935, 1783391, 1397791, 1685082, 1652425, 1642013, 1783455, 1397855, 1021593, 1379926, 1783519, 1004700, 1685146, 1510999, 1397919, 1021657, 1642077, 1004764, 1685210, 1379990, 1397983, 1511063, 1642141, 1380054, 1511127, 1642205],
    [1915905, 2167808, 2167872, 2167936, 2168000, 2298881, 2298945, 2299009, 2178576, 2299073, 487938, 332802, 2178640, 2668051, 488002, 332866, 1915969, 2668115, 2178704, 2954773, 562708, 1916033, 2954837, 2668179, 1012246, 3085847, 726038, 2178768, 2929687, 3109400, 3085911, 857112, 1916097, 2929751, 3109464, 3085975, 857176, 2956818, 2929815, 1012310, 3086039, 726102, 2956882, 2929879, 3109528, 857240, 2956946, 2954901, 2668243, 1012374, 726166, 2957010, 3322902, 1274396, 988188, 857816, 3358225, 3322966, 3109080, 988764, 726742, 3358289, 3323030, 1273948, 988828, 3358353, 3323094, 1266185, 1119241, 333442, 3358417, 2954965, 3454491, 1266249, 1119305, 988892, 1391637, 1381898, 3454555, 1527818, 333506, 1391701, 3454619, 1266313, 1119369, 1391765, 1381962, 3454683, 1527882, 1391829, 562772, 1274012, 1119945, 1644061, 1785369, 1382026, 562836, 1921053, 1644125, 1785433, 562900, 1921117, 1644189, 1785497, 1382090, 2004506, 1921181, 1644253, 1785561, 2004570, 1921245, 2004634, 1527946, 2004698, 487554, 1265865, 1011926, 1528010, 1274076, 487618],
    [390144, 1668097, 1668161, 1668225, 1668289, 1799168, 1799232, 1799296, 390208, 1799360, 2298382, 488962, 2323470, 390272, 2298446, 489026, 2323534, 620036, 390336, 2306576, 750608, 2324110, 620100, 513548, 2706961, 2306640, 750672, 620164, 513612, 2297998, 2838034, 751248, 2585618, 620228, 513676, 882181, 2707025, 2306192, 2586194, 513740, 882245, 2969107, 2586258, 652813, 2969171, 2586322, 652877, 2969235, 3215893, 652941, 2969299, 2306768, 750800, 653005, 2707089, 3215957, 906767, 882309, 2707153, 3216021, 2324174, 1299457, 882373, 3239444, 2298062, 906831, 3239508, 3216085, 1299521, 1118744, 3239572, 906895, 1118808, 3239636, 1299585, 1118872, 2837586, 1144328, 906959, 1118936, 2837650, 1144392, 1299649, 1258009, 2837714, 1275401, 1144456, 1823762, 1258073, 1920535, 1275465, 1144520, 1823826, 1258137, 1920599, 1275529, 1823890, 1258201, 1920663, 489090, 1823954, 1920727, 1275593, 2059798, 489154, 2059862, 2059926, 2059990],
    [621568, 1659904, 1659968, 1660032, 1660096, 1790977, 1791041, 1791105, 753164, 1791169, 2561550, 480770, 753228, 2053648, 2684433, 2561614, 753292, 2053712, 2684497, 2561678, 753356, 2053776, 2684561, 2561742, 613392, 2053840, 3356175, 613456, 2938387, 3347973, 480834, 613520, 2938451, 3479058, 480898, 613584, 873991, 2938515, 3356239, 480962, 621632, 874055, 2938579, 3348037, 621696, 874119, 3077652, 3479122, 621760, 874183, 1111575, 3356303, 2972673, 3208728, 3348101, 2972737, 3077716, 3479186, 2972801, 1111639, 1390106, 2972865, 3208792, 3356367, 3243545, 3077780, 1390170, 3243609, 1111703, 3348165, 3243673, 3208856, 1390234, 1531405, 3077844, 3479250, 3243737, 1111767, 1390298, 1531469, 3208920, 2037269, 1793564, 2684625, 2045462, 1793628, 2029083, 2037333, 1793692, 2029147, 2045526, 1793756, 2029211, 2037397, 1529355, 1531533, 2029275, 2045590, 1529419, 1531597, 2037461, 1529483, 2045654, 1529547],
    [1840128, 2208768, 2208832, 2208896, 2208960, 2339841, 2339905, 2348560, 2339969, 1840192, 2340033, 374290, 2479635, 504851, 2503698, 374354, 2479699, 504915, 2503762, 3124756, 636437, 2479763, 504979, 2102801, 3124820, 767510, 636501, 2479827, 505043, 2102865, 3116054, 767574, 374418, 2348624, 2503826, 3124884, 767638, 636565, 2348688, 1840256, 3124948, 767702, 374482, 2348752, 2503890, 3378712, 1029144, 636629, 644117, 2496023, 3116118, 644181, 2496087, 3378776, 1029208, 1291803, 644245, 2102929, 3116182, 1291867, 644309, 2496151, 3378840, 1029272, 1291931, 1168411, 1840320, 3116246, 1291995, 3134981, 2102993, 3378904, 1029336, 1561622, 2496215, 3780124, 3135045, 529409, 3780188, 1692690, 529473, 3780252, 3135109, 529537, 4042266, 1168475, 529601, 4042330, 3135173, 1053716, 3780316, 1561686, 1316381, 4042394, 1692754, 1053780, 4042458, 1168539, 1316445, 3903001, 1561750, 1053844, 3903065, 1692818, 1316509, 3903129, 1168603, 1053908, 3903193, 1561814, 1316573, 1692882],
    [2202625, 2215937, 2200576, 2200640, 2200704, 2200768, 2331649, 2331713, 2331777, 2224656, 2202689, 2331841, 2224720, 2202753, 2831890, 2224784, 2202817, 2831954, 2224848, 2857984, 595475, 2858048, 2486801, 366086, 497172, 595539, 2858112, 2486865, 497236, 3487253, 2858176, 2486929, 497300, 595603, 2735124, 2486993, 497364, 2832018, 2735188, 2216001, 366150, 628232, 3618326, 2735252, 2216065, 628296, 3618390, 2735316, 2216129, 366214, 628360, 3618454, 2866182, 3657736, 628424, 3618518, 2866246, 3657800, 366278, 2832082, 2866310, 3657864, 3487317, 2866374, 3657928, 3487381, 3273241, 1285136, 3487445, 3789316, 1416209, 1152522, 1914392, 3273305, 1285200, 1152586, 1283595, 1914456, 3789380, 1416273, 1152650, 1283659, 1914520, 3273369, 1285264, 1152714, 1283723, 1914584, 3789444, 1416337, 1283787, 595667, 3273433, 1285328, 3789508, 1416401, 1954327, 1954391, 1954455, 1954519],
    [291840, 2214912, 1700865, 1700929, 1700993, 1701057, 1831936, 1832000, 1832064, 291904, 2214976, 1832128, 2855440, 291968, 2215040, 2855504, 292032, 2215104, 504338, 2485777, 554511, 504402, 2747393, 554575, 504466, 521731, 2747457, 554639, 504530, 521795, 2747521, 554703, 635411, 521859, 3175427, 2485841, 635475, 521923, 3175491, 2485905, 635539, 3175555, 2485969, 635603, 3175619, 3272213, 783894, 3510788, 1078289, 2747585, 783958, 3510852, 773652, 1209345, 784022, 2855568, 914950, 773716, 1078353, 784086, 3510916, 1046025, 773780, 1209409, 2855632, 915014, 773844, 1078417, 3510980, 1046089, 1209473, 3272277, 1937943, 915078, 1078481, 3272341, 1938007, 1046153, 1209537, 3272405, 1938071, 915142, 1734146, 1437208, 1046217, 1437272, 1864726, 1938135, 1734210, 1437336, 1437400, 1864790, 1734274, 1864854, 1734338, 1864918],
    [1922048, 1309697, 2085889, 2085953, 2086017, 2086081, 1922112, 1309761, 2725378, 1922176, 1309825, 2725442, 2315792, 1309889, 898578, 2096128, 2315856, 2725506, 2096192, 2315920, 2725570, 2096256, 2315984, 3249678, 2709009, 2096320, 898642, 2709073, 2219532, 3249742, 2709137, 2219596, 898706, 775699, 2709201, 2219660, 3249806, 775763, 1922240, 2219724, 898770, 775827, 3372051, 2752013, 3249870, 775891, 3503631, 2752077, 3905028, 1037845, 3372115, 2752141, 3905092, 1037909, 3503695, 2752205, 3905156, 1037973, 3372179, 3905220, 1038037, 3503759, 1414678, 3014152, 3372243, 1545233, 3014216, 3503823, 3014280, 1807892, 3765269, 1414742, 3014344, 3765333, 1545297, 1955339, 3765397, 1807956, 1955403, 3765461, 1414806, 1955467, 1545361, 1955531, 1808020, 1414870, 1545425, 1808084],
    [432128, 2381824, 1980416, 1980480, 1980544, 1980608, 2111489, 2111553, 2372108, 2111617, 2381888, 309260, 2111681, 276994, 2372172, 2381952, 309324, 408067, 2634255, 2382016, 571407, 2634319, 686605, 571471, 2634383, 309900, 686669, 2634447, 686733, 571535, 2371724, 309964, 686797, 2371788, 948225, 571599, 408131, 1088004, 948289, 659984, 277058, 948353, 1218573, 660048, 408195, 1088068, 948417, 660112, 277122, 1202693, 432192, 660176, 408259, 1202757, 1218637, 277186, 1088132, 1333777, 432256, 1464846, 1333841, 1218701, 1088196, 1202821, 1184274, 1743379, 1464910, 1184338, 1202885, 1743443, 1184402, 1718793, 1333905, 1743507, 1184466, 1718857, 1743571, 1464974, 1446420, 1849877, 1718921, 2005013, 1865749, 1446484, 1718985, 1333969, 432320, 1849941, 2005077, 1865813, 1446548, 1218765, 1465038, 1850005, 2005141, 1865877, 1446612, 2005717, 1865941, 1849557],
    [1939456, 1318913, 1579008, 1710081, 1579072, 1710145, 1579136, 1710209, 1579200, 1581583, 1939520, 1710273, 2653713, 1573395, 1939584, 2653777, 1704468, 1939648, 2653841, 1573459, 2464277, 2653905, 1704532, 2595346, 810500, 1573523, 2464341, 1072662, 1704596, 2595410, 1573587, 2464405, 1704660, 2595474, 2252311, 1581647, 2464469, 924184, 3177496, 2595538, 1318977, 924248, 3177560, 1581711, 924312, 3177624, 2996761, 1319041, 924376, 3177688, 2996825, 1581775, 2252375, 2996889, 1319105, 2252439, 2996953, 2761232, 1596939, 2761296, 2252503, 1055244, 2761360, 1597003, 1055308, 2761424, 1597067, 1055372, 1597131, 1055436, 1072726, 810564, 1072790, 810628, 1072854, 810692],
    [2291712, 2256896, 2127873, 2127937, 2128001, 2128065, 2256960, 449040, 293394, 2773010, 580113, 2113028, 293458, 424467, 555012, 2773074, 2291776, 2636819, 293522, 424531, 555588, 2773138, 449104, 2636883, 293586, 424595, 555652, 2773202, 580177, 2636947, 555716, 424659, 2291840, 2257024, 2637011, 817685, 2257088, 449168, 2112580, 1077265, 580241, 2112644, 817749, 2291904, 1077329, 2112708, 449232, 1077393, 2235413, 817813, 580305, 1077457, 2235477, 981527, 3428884, 2235541, 817877, 1243672, 3428948, 2235605, 1079817, 981591, 3429012, 1064473, 1079881, 1243736, 3429076, 1195546, 981655, 1470480, 1326614, 1759771, 1470544, 1064537, 1602076, 1759835, 1195610, 1079945, 1759899, 1733149, 1326678, 1602140, 1243800, 1064601, 1080009, 981719, 1733213, 1195674, 1473038, 1602204, 1759963, 1326742, 1473102, 1243864, 1470608, 1064665, 1473166, 1733277, 1195738, 1473230, 1602268, 1326806, 1470672, 1733341],
    [2119680, 2250753, 2119744, 2250817, 2119808, 2250881, 1972752, 2119872, 2250945, 285202, 1972816, 416273, 2357779, 2114050, 1972880, 2114114, 2357843, 1972944, 2638356, 2357907, 2897937, 2114178, 2742805, 2644485, 800786, 2768901, 3004951, 2644549, 2768965, 2882070, 932377, 2644613, 677913, 416337, 2769029, 3267098, 2898001, 2644677, 809499, 2769093, 3267162, 2898577, 940551, 415889, 3301383, 3267226, 1071644, 1194011, 940615, 285266, 3267290, 3301447, 1325084, 940679, 678489, 416465, 3301511, 3005015, 2898129, 940743, 809563, 3301575, 2742869, 800850, 2114242, 2882134, 931929, 285330, 3695128, 3005079, 1071708, 1194075, 678553, 3695192, 2742933, 1071772, 1325148, 809627, 3695256, 2882198, 1071836, 800914, 2357971, 3695320, 931993, 285394, 2638420, 3005143, 1194139, 678617, 2638484, 2742997, 1325212, 809691, 2638548, 2882262, 800978, 932057, 1194203, 1325276],
    [333824, 299008, 325632, 2144257, 2144321, 2144385, 2144449, 2275328, 2275392, 2275456, 325696, 465424, 2396176, 2275520, 325760, 465488, 2396240, 325824, 465552, 2396304, 2538004, 587777, 465616, 2396368, 2538068, 2789396, 727569, 587841, 2538132, 2789460, 727633, 587905, 2538196, 2789524, 727697, 587969, 2789588, 3201558, 727761, 989714, 3201622, 3183127, 1120792, 3201686, 3183191, 989778, 3201750, 3183255, 3332114, 1120856, 3183319, 3332178, 333888, 3314201, 989842, 3332242, 3314265, 3332818, 1120920, 3314329, 333952, 3463184, 3314393, 989394, 299072, 3463248, 1120984, 299136, 3463312, 334016, 299200, 3463376, 1767957, 1907227, 1610259, 2030106, 1907291, 1871873, 1768021, 1907355, 1610323, 2030170, 1907419, 1871937, 1768085, 1610387, 2030234, 1872001, 1768149, 1610451, 2030298, 1872065],
    [2373632, 2138112, 2136065, 2136129, 2136193, 2136257, 2267136, 2267200, 2267264, 2373696, 2138176, 2267328, 2767377, 2138240, 694786, 2767441, 2138304, 2547203, 694850, 2129922, 2767505, 2555410, 825860, 2373760, 2392068, 2555474, 825924, 2129986, 2767569, 2555538, 694914, 2373824, 2392132, 2547267, 956935, 825988, 2103827, 2130050, 2685959, 694978, 2103891, 2392196, 2817542, 956999, 826052, 2103955, 2130114, 2686023, 2104019, 2392260, 2547331, 957063, 2662928, 2686087, 2794004, 2547395, 957127, 2662992, 2686151, 2794068, 3079701, 2365974, 2663056, 3079765, 2366038, 2794132, 2817606, 2366102, 2663120, 3079829, 2366166, 2794196, 2817670, 3079893, 2817734, 2555602, 1874447, 1768983, 1874511, 1769047, 1874575, 1769111, 1874639, 1769175],
    [1883136, 2455553, 2160640, 2160704, 2160768, 2160832, 1883200, 2455617, 2423314, 1883264, 2455681, 455187, 457219, 2423378, 2407427, 2455745, 2683412, 2947588, 2423442, 2538500, 2718224, 455251, 2423506, 1883328, 2718288, 455315, 457283, 2407491, 2718352, 455379, 2947652, 2538564, 2718416, 2945557, 2800658, 3241984, 2945621, 457347, 2407555, 3242048, 2683476, 2947716, 1006104, 2538628, 2683540, 2800722, 1006168, 2683604, 457411, 1006232, 2407619, 3602952, 2945685, 2947780, 1006296, 2538692, 2945749, 2800786, 3242112, 3603016, 3338248, 2800850, 3242176, 3338312, 3063302, 1661457, 3603080, 3338376, 3063366, 1661521, 1626646, 1374746, 3063430, 1661585, 3603144, 3461146, 1374810, 3063494, 1661649, 3461210, 1374874, 3456537, 3233810, 3461274, 1374938, 3448343, 3233874, 3461338, 1899022, 3456601, 3233938, 3338440, 1899086, 3448407, 3234002, 1626710, 1899150, 3456665, 1626774, 1899214, 3448471, 1626838, 3456729, 3448535],
    [2154497, 2152449, 2152513, 2152577, 2152641, 2283520, 2283584, 2283648, 2154561, 2283712, 440849, 317457, 2277890, 2277954, 2783763, 2807827, 2278018, 3045908, 2938900, 702998, 318033, 2278082, 3045972, 2938964, 440401, 3070487, 711172, 2154625, 3438596, 2808403, 3184663, 3070551, 711236, 2154689, 3438660, 2939540, 3184727, 318097, 3070615, 711300, 3203072, 3438724, 440465, 3070679, 711364, 3203136, 3438788, 2808467, 3184791, 3203200, 2783315, 2939604, 3184855, 318161, 3203264, 3045524, 2808531, 440529, 3334167, 2783379, 1227288, 3334231, 3045588, 1366534, 1489435, 1497628, 3334295, 2783443, 1620506, 3334359, 3692550, 1366598, 1751068, 1497692, 3465744, 3824149, 1227352, 3465808, 3692614, 1366662, 1489499, 1497756, 3465872, 3824213, 1620570, 3465936, 3692678, 1366726, 1751132, 1497820, 1622557, 3824277, 703062, 1368594, 3692742, 1227416, 1622621, 3824341, 1489563, 1368658, 1997337, 1620634, 1622685, 1997401, 1751196, 1368722, 1997465, 703126, 1622749, 1997529, 1227480, 1368786, 1489627, 1620698, 1751260, 703190],
    [497664, 358400, 1781761, 2177024, 2177088, 2177152, 2177216, 1781825, 506384, 751632, 760337, 1781889, 752208, 760401, 1781953, 752272, 760465, 2560016, 752336, 358464, 760529, 2560080, 358528, 2726404, 2560144, 473605, 358592, 2726468, 2560208, 604691, 473669, 3084288, 2856979, 743425, 473733, 3084352, 2726532, 743489, 604755, 997909, 473797, 3084416, 2857043, 743553, 604819, 997973, 3084480, 2857107, 743617, 604883, 998037, 1267733, 3478019, 2726596, 1128982, 1145364, 3119126, 3478083, 998101, 1129046, 1407511, 3119190, 3478147, 1530392, 3478211, 2857171, 1249810, 1267797, 505936, 1249874, 1145428, 506000, 1129110, 1391116, 1249938, 1530456, 3119254, 1129174, 1522189, 1250002, 1407575, 3119318, 1391180, 1267861, 506064, 1522253, 1145492, 497728, 1391244, 1407639, 497792, 1522317, 1530520, 497856, 1391308, 1267925, 1522381, 1145556, 1530584, 1407703],
    [2301952, 2168833, 2168897, 2168961, 2169025, 2299904, 2299968, 2529808, 2300032, 2302016, 2300096, 2063890, 2431505, 2660369, 2302080, 2194963, 2431569, 2660433, 2302144, 596482, 2195027, 2431633, 2660497, 720915, 596546, 2063954, 2431697, 2660561, 729106, 596610, 2195091, 965140, 720979, 596674, 2064018, 2668546, 729170, 2195155, 965204, 721043, 2850309, 2668610, 1245717, 2850373, 965268, 860695, 2850437, 2668674, 860759, 2850501, 965332, 729234, 2064082, 2668738, 860823, 1006613, 2930711, 721107, 1408536, 2930775, 1384472, 1138201, 2930839, 1245781, 1006677, 2931415, 3473946, 1138265, 2529872, 3474010, 1408600, 2529936, 3474074, 1007253, 2530000, 3474138, 1138329, 2013718, 1384536, 1408664, 2013782, 1245333, 1007317, 2013846, 1384600, 1138393, 2013910, 1245397, 1408728, 729298, 1384664, 860375],
    [2169856, 1964033, 2193408, 2324481, 2193472, 2324545, 2193536, 2324609, 2193600, 2169920, 1964097, 2324673, 2169984, 1964161, 2170048, 1964225, 2978323, 2571794, 776720, 2978387, 605203, 776784, 2978451, 605267, 776848, 2978515, 605331, 776912, 3240468, 2571858, 1169937, 3101188, 2571922, 1170001, 3240532, 1014277, 2571986, 1170065, 3101252, 1014341, 605395, 1170129, 3240596, 1014405, 3218951, 3143680, 3101316, 1014469, 3219015, 3143744, 3240660, 3219079, 3143808, 3101380, 1276426, 3219143, 3143872, 3625493, 1276490, 1515031, 3887638, 1276554, 1515095, 3625557, 1276618, 1538572, 3349516, 3887702, 1538636, 3349580, 3625621, 1538700, 3349644, 3887766, 1931791, 1538764, 3349708, 3625685, 1931855, 3529240, 1515159, 3887830, 1931919, 3529304, 1515223, 1931983, 3529368, 3529432],
    [2048001, 2185217, 2185281, 2185345, 2185409, 2316288, 2316352, 2316416, 2449936, 2316480, 2677250, 342546, 2447362, 2450000, 342610, 2816517, 2572293, 342674, 2816581, 481811, 2572357, 342738, 2816645, 481875, 2572421, 2562580, 2816709, 612372, 2572485, 3340821, 2832403, 612948, 2447938, 2450064, 2676802, 2562132, 613012, 2448002, 481939, 2450128, 2676866, 2562196, 613076, 2448066, 3097105, 2676930, 2562260, 875032, 3097169, 1104406, 2955288, 875096, 482003, 2048065, 850455, 2955352, 3097233, 1104470, 3226116, 2048129, 850519, 2832467, 3097297, 1104534, 3226180, 2048193, 850583, 2955928, 874648, 3358739, 1104598, 2955992, 874712, 3490307, 850647, 2832531, 3358803, 1923609, 3340885, 3226244, 3490371, 1923673, 3340949, 2832595, 3358867, 1923737, 3341013, 3226308, 3490435, 2038298, 3358931, 1783833, 3490499, 2038362, 1794048, 1783897, 1794112, 1923801, 2038426, 1794176, 1783961, 1794240, 2038490, 1784025],
    [268289, 382977, 1685504, 1685568, 1685632, 1685696, 1816577, 1816641, 1816705, 399884, 645132, 1816769, 2724366, 375298, 530959, 2480653, 2724430, 375362, 531023, 645708, 2724494, 375426, 768517, 539153, 2611205, 2724558, 375490, 768581, 531087, 2611269, 627218, 768645, 531151, 2611333, 758291, 768709, 2611397, 399436, 627282, 268353, 383041, 766484, 400012, 2480717, 758355, 645260, 268417, 1028629, 400076, 383105, 766548, 268481, 2480781, 1028693, 539217, 645324, 627346, 539281, 383169, 1030664, 1544727, 539345, 2480845, 1544791, 3274754, 1587728, 1292809, 1030728, 758419, 3274818, 1587792, 1292873, 766612, 1423883, 3274882, 1587856, 1292937, 1030792, 1028757, 1423947, 3274946, 1587920, 1293001, 1544855, 1424011, 1956374, 1316864, 1030856, 627410, 1424075, 1570816, 1447949, 758483, 1956438, 1316928, 1544919, 1570880, 1448013, 766676, 1956502, 1316992, 1028821, 1570944, 1448077, 1956566, 1317056, 1571008, 1448141],
    [622592, 1677312, 1808385, 1677376, 1808449, 1677440, 1808513, 1572364, 1677504, 753676, 1808577, 1572428, 885261, 2202126, 629251, 1572492, 630785, 891396, 1825796, 2982415, 891460, 1825860, 2982479, 891524, 2693648, 1021968, 1825924, 2982543, 891588, 2693712, 1022032, 1825988, 2982607, 2202190, 2824723, 1572556, 1024014, 2202254, 2824787, 777230, 753740, 2202318, 2824851, 777294, 622656, 2693776, 1022096, 777358, 1147412, 2824915, 777422, 1147476, 2693840, 1022160, 908308, 885325, 1251861, 908372, 630849, 1382929, 908948, 1024078, 1415688, 1514002, 909012, 753804, 1260054, 622720, 1415752, 1251925, 629315, 1147028, 1382993, 629379, 885389, 1415816, 1514066, 630913, 1260118, 1024142, 1415880, 1251989, 629443, 753868, 1383057, 622784, 1514130, 1147092, 1260182, 885453, 1252053, 630977, 1383121, 1024206, 1514194, 1260246],
    [2390016, 637952, 1701889, 1701953, 1702017, 1702081, 1832960, 1833024, 1833088, 638016, 547343, 1833152, 391682, 547407, 2596368, 2226691, 522756, 547471, 2596432, 2226755, 653842, 547535, 2596496, 2226819, 522820, 2906641, 2596560, 3002899, 2750981, 2989061, 3307536, 3002963, 2751045, 2989125, 3569667, 3003027, 2751109, 2906705, 2989189, 3003091, 2751173, 2390080, 2989253, 774677, 391746, 915976, 891912, 3307600, 3396120, 653906, 916040, 891976, 3569731, 522884, 3396184, 916104, 2906769, 892040, 391810, 3396248, 916168, 892104, 2390144, 2226883, 653970, 3396312, 638080, 3307664, 1178137, 522948, 1045014, 638144, 3569795, 1178201, 391874, 1176084, 2906833, 1424388, 1178265, 654034, 774741, 2390208, 1555458, 1178329, 774805, 1686546, 3307728, 774869, 1424452, 3569859, 1045078, 1555522, 1857561, 1176148, 1686610, 1857625, 1045142, 1424516, 1857689, 1176212, 1555586, 1857753, 1823258, 1989143, 1686674, 1823322, 1989207, 1424580, 1823386, 1989271, 1555650, 1823450, 1989335, 1686738, 1045206, 1176276],
    [1564673, 2086912, 2086976, 2087040, 2087104, 2217985, 2218049, 1948172, 2218113, 1564737, 2218177, 2578959, 637454, 1564801, 2579023, 637518, 1564865, 2579087, 637582, 1827344, 2579151, 637646, 1827408, 907794, 2840594, 1038867, 1948236, 2088979, 2972165, 1038931, 1948300, 2089043, 907858, 2840658, 1038995, 1948364, 2089107, 2972229, 1039059, 2734605, 2089171, 907922, 2840722, 2734669, 1827472, 907986, 2840786, 1300999, 2734733, 2613255, 2972293, 2734797, 770577, 2972357, 1301063, 1153043, 2613319, 3103254, 1432087, 1161239, 1032725, 3103318, 1301127, 1153107, 1432151, 1827536, 3103382, 1432215, 1161303, 2613383, 3103446, 1301191, 1153171, 1432279, 2613447, 1669656, 1161367, 770641, 2054681, 1153235, 1032789, 2054745, 1161431, 770705, 2054809, 1554964, 1032853, 2054873, 1555028, 770769, 1669720, 1555092, 1032917, 1669784, 1555156, 1669848],
    [2128896, 277504, 277568, 277632, 277696, 408577, 408641, 408705, 2391561, 408769, 1588747, 2391625, 433676, 1850380, 1588811, 2391689, 1588875, 2391753, 1588939, 949770, 2670093, 671236, 949834, 2670157, 671300, 949898, 2670221, 671364, 949962, 2670285, 671428, 2128960, 2627086, 695823, 2129024, 695887, 2129088, 3020304, 1850956, 433228, 2645007, 1851020, 695951, 2645071, 2627150, 1851084, 1097234, 2645135, 2627214, 933383, 1097298, 2645711, 3020368, 933447, 1097362, 1342993, 2627278, 933511, 1359380, 1727499, 3020432, 433292, 1343057, 3020496, 695503, 1727563, 923155, 1613335, 1343121, 1185301, 1613399, 1727627, 923219, 933575, 1359444, 1343185, 1185365, 1613463, 1727691, 923283, 1359508, 1185429, 1613527, 923347, 1097426, 1185493, 1359572, 1848854, 433356, 1848918, 1848982, 1849046],
    [1186817, 1186881, 1186945, 1187009, 1317888, 1317952, 2521602, 1318016, 1318080, 2500099, 2521666, 2500163, 2521730, 2727439, 2500227, 269828, 2914308, 1031696, 2500291, 400913, 2521794, 663059, 2341905, 2631188, 269892, 3176467, 2727503, 2622994, 400977, 2914372, 2341969, 2631252, 269956, 2914436, 794118, 2727567, 2631316, 401041, 3701261, 2342033, 2631380, 270020, 2914500, 1031760, 663123, 2623058, 401105, 3176531, 2342097, 663187, 2623122, 3176595, 1031824, 663251, 2623186, 3176659, 1031888, 3701325, 2727631, 3701389, 3701453, 1595916, 3128854, 1726990, 3128918, 1210901, 3128982, 1595980, 3129046, 1727054, 1210965, 1596044, 1727118, 794182, 1211029, 794246, 1596108, 794310, 1727182, 1211093],
    [283648, 1841153, 293888, 293952, 294016, 294080, 424961, 425025, 2031118, 425089, 422926, 1841217, 425153, 2293263, 423502, 1841281, 2293327, 423566, 1841345, 2293391, 793091, 423630, 2293455, 670212, 685071, 2030670, 283712, 670276, 2030734, 670340, 685135, 2030798, 415248, 1063431, 1063495, 283776, 1080841, 2234377, 685199, 1080905, 2234441, 283840, 1113617, 1080969, 2234505, 415312, 1081033, 2234569, 685263, 3071508, 1332754, 793155, 3071572, 1332818, 793219, 3071636, 1332882, 1063559, 3071700, 1332946, 793283, 1506835, 1186325, 1474060, 1113681, 1186389, 415376, 1506899, 1186453, 1474124, 415440, 1113745, 1186517, 1474188, 1506963, 1988118, 1604630, 1063623, 1474252, 1996311, 1113809, 1735703, 670404, 1988182, 1507027, 1604694, 1996375, 1735767, 1988246, 1604758, 1996439, 1735831, 1988310, 1604822, 1996503, 1735895],
    [1440769, 1858560, 1858624, 1858688, 1858752, 1989633, 1989697, 1580546, 1989761, 1702914, 1989825, 2123267, 417296, 540174, 1703490, 1984015, 548370, 2244115, 1834513, 2384914, 548434, 540238, 1834577, 2384978, 548498, 2244179, 1834641, 2385042, 548562, 540302, 1834705, 2385106, 941575, 2244243, 2088470, 1984079, 941639, 540366, 1440833, 1984143, 941703, 2244307, 1703554, 1984207, 941767, 1580098, 1440897, 2123331, 417360, 1580162, 1703618, 2123395, 417424, 1580226, 1440961, 1465880, 2123459, 417488, 924696, 2088534, 1465944, 2770453, 924760, 2088598, 1466008, 2770517, 924824, 2088662, 1466072, 2770581, 2891289, 2882567, 2770645, 2891353, 2882631, 2901527, 2891417, 2882695, 2901591, 2891481, 2882759, 2901655, 924888, 3144720, 2901719, 1457684, 3144784, 1457748, 3144848, 1457812, 3144912, 1457876],
    [2274304, 1899520, 310272, 441345, 310336, 441409, 310400, 441473, 310464, 2274368, 450062, 441537, 2309648, 2274432, 450126, 2309712, 2274496, 450190, 2309776, 431105, 450254, 2309840, 581135, 431169, 728594, 581199, 431233, 867857, 581263, 431297, 728658, 581327, 701454, 728722, 704019, 1899584, 701518, 3096084, 704083, 1899648, 955925, 3096148, 1899712, 955989, 728786, 2809346, 701582, 3096212, 704147, 2939923, 956053, 1121814, 2809410, 1357335, 3096276, 966152, 2939987, 701646, 1121878, 966216, 2809474, 956117, 867921, 704211, 966280, 2940051, 1121942, 966344, 2809538, 867985, 2940115, 1873433, 1122006, 1621017, 1629720, 1873497, 868049, 1621081, 1629784, 1357399, 1629848, 1873561, 1777178, 1621145, 1629912, 1357463, 1873625, 1777242, 1621209, 1357527, 1777306, 1777370],
    [1874945, 1875009, 1875073, 1875137, 2006016, 2006080, 2006144, 2006208, 2663950, 1981454, 2554383, 2664014, 1981518, 2685457, 2664078, 1981582, 2685521, 2786834, 2554447, 3180051, 2685585, 3209744, 2664142, 1981646, 2554511, 2786898, 2685649, 3180115, 2554575, 2104853, 3311124, 2923541, 564758, 3471876, 2786962, 2767894, 564822, 3209808, 3180179, 2767958, 564886, 3471940, 2104917, 3311188, 2923605, 564950, 3209872, 2787026, 2768022, 3472004, 3180243, 2768086, 3209936, 2104981, 3311252, 1220105, 2923669, 3472068, 2105045, 3311316, 1220169, 2923733, 1476119, 1505816, 1220233, 3185687, 1476183, 1636889, 1220297, 3185751, 1482251, 1476247, 1505880, 3185815, 1482315, 1476311, 1636953, 3185879, 1482379, 1505944, 2008602, 1482443, 1637017, 1506008, 2008666, 1637081, 2008730, 2008794],
    [1932288, 2413569, 326657, 326721, 326785, 326849, 457728, 457792, 457856, 1932352, 2413633, 457920, 1932416, 2553359, 2791953, 2162194, 1932480, 2553423, 3054083, 2162258, 2317838, 2553487, 3054147, 2162322, 2317902, 2553551, 2424339, 3054211, 2162386, 2317966, 2413697, 3054275, 851460, 2318030, 2413761, 3315716, 851524, 2718739, 2946576, 3315780, 851588, 2710546, 2946640, 2424403, 3315844, 851652, 2718803, 2946704, 3315908, 2710610, 2946768, 2792017, 1242644, 2710674, 2792081, 1373201, 2710738, 2424467, 2792145, 1242708, 2718867, 1481237, 1373265, 2719443, 2424019, 1612311, 1242772, 1882646, 1373329, 1481301, 1242836, 1612375, 1373393, 1882710, 1889816, 1481365, 1889880, 1612439, 1889944, 1882774, 1890008, 1481429, 1612503, 1882838],
    [2417664, 2137089, 1891328, 1891392, 1891456, 1891520, 2022401, 2022465, 2260482, 2022529, 2417728, 2137153, 2022593, 318990, 2260546, 2541059, 2137217, 2260610, 2541123, 2137281, 2260674, 2541187, 2399232, 2915342, 2541251, 2399296, 2121234, 2803215, 2399360, 2417792, 2399424, 2803279, 2932241, 2803343, 2932305, 2121298, 2803407, 2932369, 319054, 2915406, 2417856, 2932433, 974343, 319118, 2915470, 3055125, 1230352, 974407, 319182, 2915534, 1230416, 1088527, 3309076, 1492502, 1088591, 3309140, 1492566, 1088655, 3309204, 1492630, 1088719, 3309268, 1351187, 1230480, 974471, 1498647, 2121362, 3316759, 1492694, 974535, 1498711, 2121426, 3316823, 1230544, 3055189, 1498775, 3316887, 3055253, 1498839, 3316951, 3055317, 1351251, 1760781, 1351315, 1760845, 1351379, 1760909, 1760973],
    [351232, 2429952, 343041, 343105, 343169, 343233, 474112, 474176, 474240, 2430016, 482830, 474304, 1949201, 2046993, 2430080, 482894, 1949265, 2047057, 2430144, 482958, 630288, 3094018, 483022, 630352, 3094082, 744975, 630416, 3094146, 351296, 630480, 3094210, 745039, 736773, 1949329, 2047121, 351360, 3609615, 1949393, 2047185, 3609679, 745103, 998918, 736837, 3120661, 2964501, 1130006, 351424, 3609743, 736901, 3120725, 2964565, 1130070, 745167, 3609807, 3120789, 2964629, 1130134, 2841622, 3871745, 3120853, 2964693, 1130198, 1259031, 2841686, 736965, 3251736, 1259095, 2841750, 3251800, 2841814, 3871809, 3251864, 1259159, 1269267, 3251928, 1539602, 3871873, 1259223, 1269331, 1539666, 3871937, 3513881, 1775124, 1269395, 3513945, 1775188, 1539730, 3514009, 1775252, 1269459, 3514073, 1775316, 1539794, 998982, 999046, 999110],
    [2014209, 1907712, 1907776, 1907840, 1907904, 2038785, 2038849, 2038913, 2276866, 2038977, 2688526, 882702, 2432014, 2276930, 591376, 350224, 2563088, 2014273, 466449, 350800, 2696209, 2563152, 2276994, 466513, 883278, 2696273, 2432078, 2014337, 2694674, 466577, 2709522, 2696337, 2563728, 2277058, 2694738, 466641, 2709586, 2696401, 2432654, 2014401, 590928, 350352, 2563792, 2792975, 2694802, 2709650, 2688078, 2432718, 2793039, 590992, 882830, 2793103, 2694866, 2709714, 2688142, 2793167, 1137175, 591056, 826901, 1399320, 2688206, 957972, 1399384, 3089942, 1228314, 1399448, 3090006, 1228378, 1399512, 3090070, 1228442, 1792539, 3090134, 1228506, 1508889, 1800217, 1646090, 826965, 1137239, 1639955, 1646154, 958036, 1792603, 1508953, 1646218, 958100, 1800281, 1640019, 1646282, 827029, 1137303, 1509017, 827093, 1792667, 1640083, 958164, 1800345, 1509081, 1137367, 1640147, 1792731, 350416, 1800409, 882894],
    [1178624, 1930241, 359424, 359488, 359552, 359616, 490497, 490561, 490625, 1178688, 1930305, 490689, 1178752, 1930369, 1015299, 1178816, 1930433, 1015363, 2446339, 1965582, 1015427, 2446403, 1965646, 1015491, 2446467, 1965710, 2963986, 2446531, 1965774, 3095044, 2840081, 2350607, 3095108, 2840145, 2350671, 3095172, 2840209, 2350735, 3095236, 2840273, 2350799, 2964050, 3233299, 2743810, 3217940, 3233363, 2874885, 3218004, 1277462, 3233427, 3005441, 3487766, 1277526, 3233491, 2743874, 3487830, 1277590, 3634704, 2874949, 3487894, 1277654, 3634768, 3005505, 3487958, 3634832, 2743938, 2964114, 2875013, 2964178, 3005569, 3634896, 3218068, 2744002, 3218132, 2875077, 1915413, 3005633, 1915477, 1801741, 1915541, 1801805, 1915605, 1801869, 1801933],
    [353280, 2153472, 2300929, 1924096, 2055169, 1924160, 2055233, 1924224, 2055297, 1924288, 345602, 2153536, 2300993, 2055361, 2442756, 335374, 2153600, 335438, 2153664, 746497, 2704902, 335502, 2704966, 335566, 2705030, 2301057, 2705094, 2301121, 876040, 2825733, 345666, 2825797, 1271314, 982547, 2825861, 3499540, 982611, 2442820, 2825925, 2948629, 3489297, 2442884, 2948693, 3489361, 2442948, 2948757, 3489425, 3499604, 2948821, 3489489, 1271378, 982675, 1261072, 3499668, 982739, 1523215, 3499732, 3202583, 1400344, 1653784, 353344, 3202647, 876104, 1400408, 1653848, 746561, 3202711, 1400472, 1261136, 1271442, 3202775, 876168, 1523279, 345730, 1637910, 876232, 1400536, 1653912, 353408, 1637974, 1261200, 746625, 1638038, 1523343, 1271506, 1638102, 1653976, 345794, 1261264, 353472, 1523407, 746689],
    [515072, 375808, 375872, 375936, 376000, 506881, 506945, 507009, 646670, 507073, 1719823, 769552, 646734, 1719887, 769616, 646798, 2506258, 769680, 900627, 646862, 1719951, 2864643, 769744, 900691, 2358288, 1720015, 3118596, 900755, 2358352, 802321, 3118660, 900819, 2358416, 3118724, 1842710, 1162262, 2358480, 3118788, 2506322, 1162838, 2612757, 2864707, 2506386, 1162902, 2612821, 2864771, 2506450, 1162966, 2612885, 2864835, 1842262, 2612949, 890388, 1842326, 1039379, 890452, 1842390, 1039443, 890516, 2498071, 1039507, 1422872, 2760198, 1039571, 1422936, 2498135, 1047567, 1423000, 2760262, 1047631, 1423064, 2498199, 1047695, 1816089, 2760326, 1047759, 1816153, 2498263, 515136, 2070042, 2760390, 1818124, 515200, 2070106, 802385, 1818188, 515264, 2070170, 802449, 1818252, 1816217, 802513, 1818316, 890580, 2070234, 1816281],
    [2327553, 1940480, 1940544, 1940608, 1940672, 2071553, 2071617, 514562, 2071681, 2327617, 2071745, 514626, 2327681, 514690, 2327745, 368142, 499215, 2488335, 493060, 2702864, 368206, 499279, 784398, 632326, 2702928, 499343, 2488399, 754690, 761351, 2702992, 499407, 784462, 885767, 859666, 2488463, 3122705, 2833939, 2488527, 1148419, 2834003, 368270, 784526, 3122769, 3227156, 368334, 784590, 493124, 3227220, 514754, 3122833, 761415, 3227284, 3397635, 885831, 3227348, 1023510, 3398211, 3122897, 761479, 3620373, 1154569, 3398275, 632390, 761543, 3620437, 1023574, 3398339, 754754, 3620501, 1154633, 1308694, 1147971, 3620565, 1023638, 1562633, 493188, 2834067, 1154697, 1308758, 885895, 2834131, 1547799, 1023702, 1693719, 632454, 2703056, 1547863, 1154761, 1693783, 754818, 859730, 1547927, 1562697, 1148035, 859794, 1547991, 1693847, 493252, 859858, 1308822, 885959, 1562761, 632518, 1693911, 754882, 1308886, 1148099, 1562825],
    [1866753, 392192, 392256, 392320, 392384, 523265, 523329, 523393, 2522633, 523457, 2079234, 1866817, 2079298, 382475, 654852, 2522697, 2079362, 382539, 654916, 1866881, 2079426, 382603, 654980, 2522761, 382667, 655044, 1866945, 2522825, 899598, 1203724, 899662, 2872847, 1203788, 899726, 3003921, 2489872, 1203852, 785925, 2988048, 3003985, 2489936, 1203916, 785989, 2988112, 3004049, 2490000, 2383373, 786053, 2988176, 3004113, 2490064, 2383437, 786117, 2988240, 1431060, 2383501, 1284627, 2872911, 916999, 2383565, 1284691, 2872975, 917063, 2776068, 1284755, 2873039, 917127, 2776132, 1284819, 1308181, 917191, 2776196, 899790, 1439254, 2776260, 1431124, 2907658, 1308245, 3038738, 1439318, 2907722, 1431188, 3038802, 1308309, 2907786, 1439382, 3038866, 1431252, 2907850, 1308373, 3038930, 1439446],
    [2333696, 1301505, 1301569, 1301633, 1301697, 384000, 384064, 384128, 2465282, 384192, 884233, 648714, 1564168, 2079752, 884297, 2352652, 1564232, 2079816, 884361, 2352716, 1564296, 2079880, 884425, 2483725, 1564360, 2079944, 1146383, 2483789, 2465346, 2999812, 2457105, 1956881, 2465410, 2483853, 2588176, 1957457, 2465474, 2483917, 2588240, 1957521, 2333760, 2999876, 2588304, 1957585, 2333824, 648778, 2588368, 2333888, 2456657, 2352780, 2997257, 2456721, 648842, 1293838, 2456785, 2352844, 2997321, 2981395, 648906, 1293902, 2981459, 2999940, 2997385, 1146447, 3000004, 1293966, 2981523, 1820181, 2997449, 1146511, 1820245, 1170951, 1294030, 1146575, 1820309, 1171015, 1678866, 2981587, 1820373, 1171079, 1678930, 1662486, 1951255, 1171143, 1678994, 1670676, 1951319, 1679058, 1662550, 1951383, 1809931, 1670740, 1951447, 1809995, 1662614, 1810059, 1670804, 1810123, 1662678, 1670868],
]
LEAVES = [
    [963, 964, 965],
    [963, 966, 967, 968],
    [964, 965, 968, 969, 971, 972],
    [962, 963, 964, 965, 967, 970, 971, 972, 973],
    [966, 968, 969, 971, 972, 973],
    [968, 969, 970, 971, 972, 973],
    [963, 964, 965, 966, 967, 969, 970, 971, 972, 973],
    [964, 965, 966, 967, 968, 970, 971, 972, 973],
    [963, 964, 965, 966, 967, 968, 969, 970, 971, 972, 973],
    [965, 966, 967, 968, 969, 970, 973],
    [962, 963, 964, 966, 967, 968, 969, 970, 971, 972, 973],
    [962, 963, 964, 966, 967, 968, 969, 970, 972, 973],
    [964, 965, 966, 968, 969, 970, 971, 972, 973],
    [964, 966, 967, 968, 969, 970, 972],
    [965, 966, 967, 968, 969, 970, 971],
    [962, 963, 966, 968],
    [962, 963, 964, 965, 967, 968, 970, 971],
    [965, 968, 970, 971, 972, 973, 974],
    [963, 965, 966, 970],
    [962, 963, 966, 967, 968, 969, 970, 971],
    [965, 966, 967, 969, 971, 972, 973, 974, 975],
    [962, 964, 965, 966, 967, 968, 969, 970, 971, 972, 973, 975],
    [964, 965, 966, 967, 968, 969, 970, 971, 973, 974, 975],
    [962, 966, 967, 969, 970, 971, 972, 973, 974, 975],
    [962, 965, 966, 967, 968, 969, 970, 971, 972, 973, 974, 975],
    [962, 965, 966, 968, 969, 972, 973, 974, 975],
    [962, 964, 966, 967, 968, 969, 970, 971, 972, 973, 974, 975],
    [962, 963, 964, 965, 966, 967, 968, 969, 970, 971, 972, 974],
    [963, 965, 966, 968, 969, 970, 972, 973, 974, 975],
    [964, 965, 966, 967, 968, 969, 970, 971, 973],
    [963, 964, 965, 966, 967, 968, 969, 970, 971, 972],
    [962, 967, 968, 970, 971],
    [963, 964, 965, 967, 969, 970, 971],
    [964, 965, 967, 969, 970, 971, 972, 973, 974],
    [962, 963, 965, 966, 967, 968, 971, 972, 974, 975],
    [964, 966, 967, 968, 969, 970, 971, 972, 973, 974, 975],
    [962, 963, 967, 968, 969, 971],
    [963, 964, 965, 967, 971],
    [964, 966, 967, 969, 971, 972, 973, 974, 975],
    [963, 964, 965, 967, 968, 969, 970, 971, 972, 973, 974, 975],
    [962, 964, 965, 967, 968, 969, 970, 971, 972, 973, 974, 975],
    [963, 965, 966, 967, 969, 970, 971, 973, 974],
    [962, 963, 964, 969, 970, 972, 973, 975],
    [964, 965, 966, 967, 968, 969, 970, 971, 972, 973, 974, 975],
    [963, 964, 965, 966, 967, 968, 969, 970, 972, 973, 975],
    [962, 963, 964, 965, 968, 969, 970, 971, 972, 973, 974, 975],
    [962, 963, 965, 966, 967, 968, 969, 970, 972, 973, 974],
    [962, 963, 965, 966, 968, 969, 970, 971],
    [967, 968, 969, 970, 971],
    [962, 963, 964, 965, 966, 967, 968, 969, 970, 972, 973, 974],
    [965, 966, 967, 968, 969, 970, 972, 975],
    [962, 963, 964, 965, 966, 967, 968, 969, 970, 971, 972, 973, 974, 975],
    [963, 964, 965, 966, 967, 970, 971, 972, 973, 974, 975],
    [962, 963, 964, 965, 966, 967, 969, 970, 971, 973, 974, 975],
    [962, 965, 967, 968, 969, 970, 971],
    [963, 965, 969, 971],
    [963, 965, 968, 969, 970, 971, 972, 973, 974, 975],
    [964, 965, 966, 967, 968, 969, 970, 971, 973, 974, 975],
    [963, 964, 965, 967, 968, 970, 972, 973, 975],
    [963, 964, 965, 967, 968, 969, 970, 971, 972, 973, 974, 975],
    [963, 965, 966, 967, 968, 969, 970, 971, 972, 973, 974, 975],
    [962, 963, 964, 965, 966, 967, 971, 972, 973, 974, 975],
    [963, 966, 967, 968, 969, 970, 971, 972, 973, 974],
    [962, 964, 965, 967, 969, 970, 971],
    [962, 964, 965, 966, 967, 968, 970, 971],
    [962, 964, 965, 966, 969, 970, 971, 972, 973, 974],
    [962, 964, 965, 966, 967, 970, 971, 972, 973, 974, 975],
    [962, 963, 964, 965, 966, 967, 969, 970, 971, 972, 973, 974],
    [964, 966, 969, 970, 971, 972, 973, 974, 975],
    [962, 964, 965, 966, 969, 971, 972, 973, 974, 975],
    [964, 965, 966, 967, 968, 970, 971, 973, 974, 975],
    [962, 964, 965, 967, 969, 970, 971, 972, 973, 974, 975],
    [962, 963, 969, 971],
    [963, 964, 965, 966, 967, 968, 969, 971],
    [963, 966, 967, 968, 969, 971, 972, 973, 975],
    [962, 963, 964, 965, 966, 967, 968, 969, 970, 971, 972, 973, 974, 975],
    [962, 963, 964, 965, 966, 969, 971, 972, 973, 974, 975],
    [962, 965, 966, 967, 968, 969, 971, 972, 973, 974, 975],
    [962, 963, 964, 967, 969, 970, 971, 972, 974],
    [963, 964, 965, 966, 967, 968, 969, 970, 971],
    [962, 963, 965, 966, 968, 970],
    [962, 963, 964, 965, 966, 967, 968, 969, 970, 971, 972, 973, 974],
    [962, 963, 964, 965, 966, 967, 968, 969, 971, 972, 973, 974, 975],
    [965, 966, 967, 970, 971, 973, 974, 975],
    [966, 967, 968, 970, 971, 972, 973, 974, 975],
    [962, 963, 964, 965, 967, 968, 970, 971, 972, 975],
    [965, 966, 967, 968, 969, 970, 971, 972, 973, 974, 975],
    [962, 964, 965, 966, 969, 970, 971, 972, 973, 974, 975],
    [962, 963, 964, 965, 966, 967, 968, 970, 971, 972, 973, 974, 975],
    [963, 964, 965, 966, 967, 968, 971, 972, 973, 974, 975],
    [963, 966, 967, 970, 971],
    [963, 964, 966, 968, 969, 970],
    [962, 963, 964, 966, 967, 968, 969, 970, 971, 972, 973, 974, 975],
    [962, 963, 965, 967, 969, 972, 973, 974, 975],
    [965, 967, 968, 970, 971, 972, 973, 974],
    [963, 965, 966, 967, 969, 970],
    [966, 967, 968, 970, 971],
    [962, 963, 965, 966, 967, 968, 969, 970, 973, 974],
    [962, 963, 965, 966, 967, 968, 970, 971, 972, 973, 975],
    [963, 964, 966, 968, 969, 970, 971, 972, 973, 974, 975],
    [962, 963, 964, 965, 966, 967, 968, 969, 970, 971, 972, 973, 974, 975],
    [965, 968, 969, 970, 971, 972, 973, 974],
    [962, 965, 967, 969, 970, 971, 972, 973, 975],
    [963, 965, 967, 968, 969, 970, 971, 972, 973, 974, 975],
    [962, 966, 967, 968, 969, 970, 971, 974, 975],
    [963, 964, 966, 967, 968, 969, 970, 971, 972, 973, 974, 975],
    [962, 963, 966, 968, 969, 971, 973, 974],
    [966, 967, 968, 969, 970, 971, 972, 973, 974, 975],
    [963, 964, 966, 967, 970],
    [962, 965, 966, 967, 969, 970, 971],
    [966, 967, 969, 970, 971, 972, 973, 974],
    [962, 963, 964, 966, 968, 969, 970, 971],
    [962, 963, 965, 966, 968],
    [965, 967, 968, 969, 970, 971],
    [962, 965, 966, 968, 970, 971, 973],
    [964, 965, 966, 968, 969, 970, 971, 972, 973],
    [963, 964, 965, 966, 967, 969, 970, 971, 972, 973],
    [962, 963, 965, 966, 967, 968, 970, 972, 973],
    [962, 965, 966, 967, 968, 969, 970, 971, 972, 973],
    [964, 965, 966, 968, 969, 970, 971, 972],
    [963, 964, 967, 968, 969, 970, 971, 972, 973],
    [963, 964, 965, 966, 967, 968, 969, 971, 972, 973],
    [966, 967, 968, 969, 970, 971, 972],
    [963, 967, 969, 970, 971, 972, 973],
    [962, 965, 967, 968, 969, 970, 971, 973],
    [965, 968, 970, 971, 972, 973],
    [963, 966, 968],
    [963, 965, 966],
]
ROLES = [
    [0, 0, 2, 1, 3, 3, 4, 5, 0, 0, 1, 2, 7, 6],
    [0, 2, 7, 8, 4, 5, 3, 6, 1, 1, 5, 4, 6, 3],
    [0, 5, 2, 7, 3, 6, 13, 10, 9, 9, 12, 11, 4, 8],
    [0, 5, 11, 3, 12, 10, 2, 7, 13, 13, 4, 8, 9, 6],
    [0, 5, 2, 9, 3, 7, 6, 10, 4, 4, 12, 11, 8, 13],
    [0, 7, 3, 13, 4, 9, 2, 12, 10, 10, 5, 6, 8, 11],
    [0, 12, 3, 10, 2, 5, 4, 8, 7, 7, 13, 9, 6, 11],
    [0, 9, 6, 5, 2, 8, 7, 12, 11, 11, 10, 4, 3, 13],
    [0, 10, 2, 12, 3, 13, 4, 11, 7, 7, 5, 8, 6, 9],
    [0, 12, 3, 13, 4, 11, 2, 8, 5, 5, 6, 9, 7, 10],
    [0, 8, 2, 11, 3, 12, 5, 9, 7, 7, 13, 10, 4, 6],
    [0, 11, 3, 7, 4, 5, 9, 8, 12, 12, 13, 6, 2, 10],
    [0, 10, 2, 13, 3, 11, 7, 12, 5, 5, 6, 4, 9, 8],
    [0, 13, 3, 12, 5, 11, 2, 8, 4, 4, 10, 7, 6, 9],
    [0, 5, 2, 10, 3, 8, 6, 4, 11, 11, 7, 9, 0, 5],
    [0, 7, 6, 6, 4, 3, 2, 2, 8, 8, 0, 7, 1, 5],
    [4, 4, 3, 5, 11, 11, 8, 9, 0, 2, 1, 7, 6, 10],
    [2, 3, 11, 8, 9, 10, 7, 5, 1, 4, 12, 13, 14, 6],
    [10, 6, 5, 8, 7, 11, 3, 4, 6, 10, 8, 5, 2, 9],
    [5, 9, 10, 3, 4, 6, 2, 8, 11, 7, 6, 4, 8, 2],
    [5, 13, 6, 8, 2, 14, 10, 12, 3, 11, 4, 7, 15, 9],
    [3, 6, 2, 11, 10, 14, 4, 13, 5, 7, 15, 8, 9, 12],
    [6, 15, 2, 8, 7, 10, 3, 12, 13, 14, 11, 4, 9, 5],
    [4, 8, 3, 15, 6, 13, 2, 5, 12, 14, 11, 9, 7, 10],
    [3, 7, 8, 9, 2, 10, 5, 6, 4, 13, 11, 15, 12, 14],
    [10, 11, 3, 14, 4, 7, 2, 8, 5, 9, 15, 12, 6, 13],
    [6, 7, 5, 10, 4, 9, 3, 15, 14, 12, 11, 13, 2, 8],
    [7, 13, 10, 11, 4, 15, 3, 12, 6, 9, 2, 14, 5, 8],
    [4, 10, 14, 11, 2, 9, 13, 12, 5, 3, 8, 6, 7, 15],
    [15, 13, 8, 5, 14, 12, 2, 7, 3, 4, 9, 11, 6, 10],
    [12, 9, 6, 10, 8, 11, 3, 2, 5, 14, 7, 13, 0, 4],
    [6, 9, 10, 10, 3, 2, 11, 11, 7, 8, 0, 5, 1, 4],
    [9, 9, 4, 3, 2, 2, 7, 8, 0, 5, 1, 10, 6, 11],
    [6, 2, 7, 11, 8, 9, 3, 13, 1, 4, 5, 14, 12, 10],
    [5, 12, 6, 13, 3, 7, 10, 9, 4, 11, 14, 15, 2, 8],
    [5, 14, 10, 15, 7, 6, 11, 12, 3, 13, 9, 8, 2, 4],
    [5, 3, 2, 11, 7, 4, 10, 9, 3, 5, 11, 2, 8, 6],
    [2, 10, 4, 8, 11, 9, 5, 7, 3, 6, 9, 11, 7, 5],
    [3, 12, 8, 6, 2, 7, 10, 5, 11, 4, 15, 9, 13, 14],
    [8, 6, 9, 4, 10, 5, 14, 13, 12, 3, 7, 11, 2, 15],
    [7, 11, 3, 15, 2, 5, 6, 14, 10, 13, 8, 9, 4, 12],
    [3, 15, 2, 14, 4, 12, 11, 8, 6, 9, 5, 7, 10, 13],
    [3, 5, 8, 14, 2, 11, 4, 6, 12, 13, 15, 10, 9, 7],
    [8, 15, 6, 7, 3, 5, 11, 13, 12, 14, 2, 4, 10, 9],
    [6, 15, 11, 7, 2, 10, 14, 5, 3, 12, 4, 13, 8, 9],
    [10, 7, 3, 8, 13, 6, 4, 9, 2, 11, 5, 12, 14, 15],
    [3, 7, 12, 8, 2, 9, 4, 11, 10, 13, 6, 14, 0, 5],
    [7, 4, 10, 10, 3, 8, 11, 11, 2, 6, 0, 9, 1, 5],
    [11, 11, 5, 6, 9, 9, 3, 10, 0, 2, 1, 8, 4, 7],
    [8, 10, 5, 9, 6, 11, 7, 2, 1, 12, 14, 4, 3, 13],
    [5, 9, 3, 14, 7, 12, 13, 11, 15, 6, 4, 8, 2, 10],
    [3, 14, 6, 5, 11, 8, 15, 12, 4, 9, 2, 13, 7, 10],
    [4, 12, 10, 13, 3, 14, 8, 9, 2, 5, 6, 11, 7, 15],
    [8, 12, 11, 4, 9, 10, 3, 5, 15, 2, 6, 13, 7, 14],
    [7, 10, 8, 9, 4, 5, 11, 2, 10, 7, 9, 8, 3, 6],
    [7, 8, 9, 3, 10, 2, 6, 11, 4, 5, 2, 10, 11, 6],
    [4, 11, 3, 14, 6, 8, 7, 5, 2, 9, 12, 10, 13, 15],
    [2, 12, 4, 9, 6, 3, 7, 8, 10, 11, 15, 14, 5, 13],
    [4, 8, 2, 9, 10, 7, 14, 11, 3, 15, 5, 6, 13, 12],
    [7, 9, 10, 3, 14, 12, 11, 4, 6, 8, 2, 5, 13, 15],
    [9, 11, 7, 8, 10, 5, 4, 12, 2, 14, 6, 15, 3, 13],
    [8, 9, 7, 6, 5, 10, 3, 13, 2, 11, 12, 15, 4, 14],
    [4, 12, 7, 9, 14, 6, 2, 5, 8, 3, 10, 13, 0, 11],
    [6, 8, 11, 11, 2, 7, 4, 4, 5, 9, 0, 3, 1, 10],
    [10, 10, 6, 8, 7, 7, 2, 9, 0, 5, 1, 3, 4, 11],
    [7, 8, 2, 11, 3, 10, 4, 14, 1, 13, 5, 12, 6, 9],
    [4, 12, 14, 9, 5, 15, 3, 8, 7, 11, 6, 13, 2, 10],
    [15, 10, 3, 6, 2, 9, 7, 13, 4, 14, 11, 12, 8, 5],
    [9, 12, 5, 3, 10, 15, 7, 6, 2, 11, 14, 8, 13, 4],
    [9, 5, 4, 15, 14, 10, 11, 13, 2, 3, 12, 7, 6, 8],
    [4, 13, 2, 12, 6, 7, 3, 10, 9, 15, 5, 14, 11, 8],
    [4, 13, 11, 7, 2, 8, 5, 6, 12, 14, 9, 15, 3, 10],
    [2, 9, 6, 11, 7, 10, 5, 8, 9, 2, 11, 6, 3, 4],
    [5, 10, 3, 2, 4, 7, 11, 9, 8, 6, 7, 4, 9, 11],
    [7, 3, 4, 14, 8, 13, 2, 10, 6, 15, 9, 11, 5, 12],
    [8, 13, 4, 14, 6, 11, 15, 5, 7, 9, 10, 3, 2, 12],
    [15, 6, 7, 10, 12, 13, 9, 8, 2, 4, 3, 5, 14, 11],
    [6, 12, 11, 9, 10, 8, 13, 15, 2, 14, 4, 5, 3, 7],
    [7, 2, 13, 5, 9, 10, 8, 6, 4, 12, 3, 11, 0, 14],
    [11, 3, 2, 2, 5, 4, 10, 10, 9, 6, 0, 7, 1, 8],
    [8, 8, 11, 7, 10, 10, 4, 9, 0, 5, 1, 6, 2, 3],
    [12, 9, 2, 4, 6, 10, 3, 5, 1, 7, 13, 14, 11, 8],
    [4, 6, 8, 10, 5, 7, 9, 14, 3, 11, 13, 12, 2, 15],
    [8, 10, 2, 13, 9, 12, 4, 14, 11, 7, 3, 6, 5, 15],
    [12, 15, 9, 4, 13, 7, 5, 6, 2, 14, 3, 11, 8, 10],
    [11, 4, 2, 9, 7, 6, 3, 13, 5, 14, 12, 15, 8, 10],
    [13, 9, 4, 10, 3, 12, 2, 8, 5, 11, 15, 6, 14, 7],
    [4, 8, 13, 15, 2, 7, 3, 11, 5, 12, 9, 6, 10, 14],
    [4, 13, 10, 8, 7, 5, 2, 9, 6, 14, 12, 11, 15, 3],
    [10, 9, 13, 7, 2, 12, 4, 3, 8, 14, 11, 6, 5, 15],
    [10, 7, 9, 8, 6, 5, 11, 3, 7, 10, 8, 9, 4, 2],
    [9, 8, 3, 4, 11, 2, 5, 10, 6, 7, 2, 11, 10, 5],
    [13, 12, 8, 2, 7, 10, 4, 9, 5, 6, 3, 15, 11, 14],
    [10, 6, 2, 9, 8, 11, 4, 5, 3, 15, 14, 12, 7, 13],
    [12, 8, 6, 14, 4, 11, 9, 3, 5, 10, 7, 13, 0, 2],
    [6, 11, 2, 2, 7, 3, 4, 4, 8, 9, 0, 10, 1, 5],
    [10, 10, 3, 2, 11, 11, 8, 9, 0, 4, 1, 5, 6, 7],
    [3, 2, 6, 9, 12, 13, 7, 10, 1, 14, 8, 11, 5, 4],
    [2, 6, 4, 14, 5, 8, 7, 9, 13, 15, 11, 10, 3, 12],
    [4, 11, 2, 15, 7, 8, 5, 14, 9, 13, 3, 10, 6, 12],
    [3, 8, 5, 7, 9, 15, 6, 14, 2, 10, 4, 13, 11, 12],
    [2, 7, 3, 11, 4, 15, 5, 13, 8, 6, 9, 10, 12, 14],
    [2, 8, 3, 10, 4, 11, 5, 14, 7, 15, 9, 13, 6, 12],
    [3, 6, 2, 7, 4, 14, 10, 15, 13, 9, 8, 11, 5, 12],
    [2, 10, 5, 12, 3, 11, 4, 13, 9, 14, 6, 7, 15, 8],
    [3, 10, 8, 13, 2, 11, 4, 7, 6, 15, 9, 5, 14, 12],
    [6, 14, 12, 10, 4, 9, 5, 15, 8, 11, 13, 7, 3, 2],
    [11, 9, 2, 8, 7, 14, 5, 12, 15, 10, 3, 13, 4, 6],
    [3, 7, 5, 11, 4, 2, 6, 9, 7, 3, 11, 5, 8, 10],
    [5, 10, 8, 7, 4, 9, 11, 6, 2, 3, 9, 4, 6, 11],
    [10, 7, 8, 9, 5, 13, 2, 4, 12, 6, 14, 11, 0, 3],
    [6, 7, 11, 11, 2, 3, 4, 4, 9, 5, 0, 8, 1, 10],
    [5, 5, 6, 2, 3, 3, 1, 4, 0, 7, 1, 4, 8, 8],
    [6, 4, 2, 7, 3, 5, 1, 10, 1, 10, 8, 11, 9, 9],
    [3, 11, 7, 12, 4, 6, 1, 9, 8, 13, 10, 5, 2, 2],
    [7, 11, 2, 12, 3, 8, 1, 13, 10, 9, 5, 4, 6, 6],
    [3, 6, 8, 9, 4, 7, 1, 11, 2, 5, 13, 12, 10, 10],
    [7, 9, 2, 12, 3, 11, 1, 13, 4, 5, 6, 8, 10, 10],
    [2, 11, 4, 13, 3, 10, 1, 7, 12, 5, 9, 6, 8, 8],
    [6, 13, 3, 12, 2, 7, 1, 9, 8, 10, 4, 11, 5, 5],
    [2, 9, 5, 6, 3, 10, 1, 12, 7, 13, 4, 8, 11, 11],
    [5, 7, 3, 12, 2, 10, 1, 4, 8, 6, 13, 9, 11, 11],
    [2, 10, 3, 13, 5, 12, 1, 6, 7, 9, 8, 4, 11, 11],
    [7, 13, 2, 12, 3, 8, 1, 6, 10, 11, 4, 5, 9, 9],
    [3, 11, 8, 12, 2, 7, 1, 5, 9, 4, 10, 6, 13, 13],
    [9, 13, 2, 4, 3, 7, 1, 6, 5, 8, 10, 11, 12, 12],
    [3, 6, 4, 5, 8, 7, 1, 2, 6, 3, 5, 4, 0, 0],
    [4, 5, 2, 2, 3, 0, 1, 1, 6, 7, 0, 3, 1, 1],
]


def fill_table(table, me, low, high):
    if high - low == 1:
        sends, leaves = SENDS[low], LEAVES[low]
        for place, word in enumerate([len(sends), len(leaves)] + sends + leaves):
            table[place] = jnp.int32(word)
        return
    middle = (low + high) // 2
    lax.cond(
        me < middle,
        lambda: fill_table(table, me, low, middle),
        lambda: fill_table(table, me, middle, high),
    )


def neighbours(col, row):
    x = lax.rem(col, 2) * 2 + lax.rem(row // 2, 2)
    y, z, core = col // 2, row // 4, lax.rem(row, 2)
    found = [(x, y, z, 1 - core)]
    for move in (1, 3):
        for other in range(2):
            found.append((lax.rem(x + move, 4), y, z, other))
            found.append((x, lax.rem(y + move, 4), z, other))
            found.append((x, y, lax.rem(z + move, 4), other))
    return [{"col": y * 2 + x // 2, "row": z * 4 + lax.rem(x, 2) * 2 + core} for x, y, z, core in found]


def spread_kernel(stored_ref, slots_ref, table, own_sem, send_sem, recv_sem):
    rows_per = stored_ref.shape[2] // CHUNKS
    col, row = lax.axis_index("col"), lax.axis_index("row")
    beside = neighbours(col, row)
    sibling = beside[0]

    barrier = pltpu.get_barrier_semaphore()
    for device in beside:
        pl.semaphore_signal(barrier, inc=1, device_id=device, device_id_type=MESH)
    own = [
        pltpu.make_async_copy(stored_ref.at[lane, 0], slots_ref.at[lane], own_sem.at[lane])
        for lane in range(2)
    ]
    for copy in own:
        copy.start()
    fill_table(table, col * lax.axis_size("row") + row, 0, len(SENDS))
    pl.semaphore_wait(barrier, len(beside))

    def hop(source, slot, chunk, place, device):
        return pltpu.make_async_remote_copy(
            src_ref=source,
            dst_ref=slots_ref.at[slot, pl.ds(chunk * rows_per, rows_per)],
            send_sem=send_sem.at[place],
            recv_sem=recv_sem.at[slot, chunk],
            device_id=device,
            device_id_type=MESH,
        )

    def arrival(slot, chunk):
        piece = slots_ref.at[slot, pl.ds(chunk * rows_per, rows_per)]
        hop(piece, slot, chunk, 0, sibling).wait_recv()

    sends = table[0]

    @pl.loop(0, sends)
    def _(place):
        word = table[2 + place]
        slot = word & 63
        chunk = (word >> 6) & 7
        device = {"col": (word >> 10) & 7, "row": (word >> 13) & 15}
        landing = word >> 17

        @pl.when(((word >> 9) & 1) == 1)
        def _():
            arrival(slot, chunk)

        @pl.when(slot < 2)
        def _():
            piece = stored_ref.at[slot, 0, pl.ds(chunk * rows_per, rows_per)]
            hop(piece, landing, chunk, place, device).start()

        @pl.when(slot >= 2)
        def _():
            piece = slots_ref.at[slot, pl.ds(chunk * rows_per, rows_per)]
            hop(piece, landing, chunk, place, device).start()

    @pl.loop(0, table[1])
    def _(place):
        word = table[2 + sends + place]
        for chunk in range(CHUNKS):
            @pl.when(((word >> (6 + chunk)) & 1) == 1)
            def _():
                arrival(word & 63, chunk)

    @pl.loop(0, sends)
    def _(place):
        hop(slots_ref.at[0, pl.ds(0, rows_per)], 0, 0, place, sibling).wait_send()

    for copy in own:
        copy.wait()


def spread(stored):
    most = max(len(sends) for sends in SENDS)
    return pl.pallas_call(
        spread_kernel,
        out_shape=jax.ShapeDtypeStruct((SLOTS,) + stored.shape[2:], jnp.float32),
        in_specs=[pl.BlockSpec(memory_space=pl.ANY)],
        out_specs=pl.BlockSpec(memory_space=pl.ANY),
        scratch_shapes=[
            pltpu.SMEM((2 + most + SLOTS,), jnp.int32),
            pltpu.SemaphoreType.DMA((2,)),
            pltpu.SemaphoreType.DMA((most,)),
            pltpu.SemaphoreType.DMA((SLOTS, CHUNKS)),
        ],
        compiler_params=pltpu.CompilerParams(collective_id=0, has_side_effects=True),
        name="spread",
    )(stored)


def split(value):
    high = value.astype(jnp.bfloat16)
    return high, (value - high.astype(jnp.float32)).astype(jnp.bfloat16)


def multiply_kernel(
    slots_ref, roles_ref, rows_ref, offs_ref, krow_ref, kcol_ref, kcnt_ref, out_ref,
    raw, left, right, done, pairs, pair_count, bucket, bucket_count, facts, in_sem, out_sem,
):
    grid = lax.axis_size("row")
    tile_j = lax.axis_index("row")
    col_id = lax.axis_index("col")
    me = col_id * grid + tile_j
    tiles, active, half = raw.shape[:3]
    block = raw.shape[-1]
    lanes, _, kept = krow_ref.shape
    slots = 2 * half
    steps = 2
    most = steps * slots * slots

    def load(place):
        return pltpu.make_async_copy(
            slots_ref.at[roles_ref[me, place]], raw.at[place], in_sem.at[place]
        )

    for place in range(tiles):
        load(place).start()

    first = rows_ref[0, 0]
    bits = [rows_ref[0, 1] ^ first, rows_ref[0, 2] ^ first, rows_ref[0, 4] ^ first]

    def rank(value):
        return sum(
            jnp.where((value & bit) != 0, jnp.int32(1 << place), jnp.int32(0))
            for place, bit in enumerate(bits)
        )

    def shifts(tile_x, tile_y):
        both = ((tile_x, tile_y), (tile_y, tile_x))
        return [rank(offs_ref[x, y, slot]) for x, y in both for slot in range(half)]

    tile_is = [col_id * lanes + lane for lane in range(lanes)]
    tile_ks = [lax.rem(tile_is[0] + tile_j + place, grid) for place in range(3)]
    right_moves = [shifts(tile_k, tile_j) for tile_k in tile_ks]

    for place in range(lanes * active):
        pair_count[place] = 0
    for lane in range(lanes):
        for step in range(steps):
            left_moves = shifts(tile_is[lane], tile_ks[lane + step])
            for slot in range(slots):
                move = left_moves[slot]
                turn = move if slot >= half else 0
                left_base = (2 * lane + step) * active * slots + slot
                for other in range(slots):
                    apart = move ^ right_moves[lane + step][other]
                    place = lane * active + apart
                    count = pair_count[place]
                    right_base = (lane + step) * active * slots + other
                    reach = move if other < half else apart
                    pairs[place * most + count] = (
                        turn | reach << 3 | left_base << 6 | right_base << 14
                    )
                    pair_count[place] = count + 1

    widest = 4
    room = 2 * lanes * kept
    for place in range(widest + 1):
        bucket_count[place] = 0
    for place in range(lanes * active):
        pair_count[place] = place << 3 | pair_count[place] << 7

    def put(size, word):
        filled = bucket_count[size]
        bucket[size * room + filled] = word
        bucket_count[size] = filled + 1

    for lane in range(lanes):
        count = kcnt_ref[lane, 0]
        together = 8

        @pl.loop(0, kept // together)
        def _(part):
            found = []
            for offset in range(together):
                item = part * together + offset
                row = rank(krow_ref[lane, 0, item])
                place = lane * active + (row ^ rank(kcol_ref[lane, 0, item]))
                found.append(jnp.where(item < count, pair_count[place] | row, 0))
            for offset in range(together):
                item = lane * kept + part * together + offset
                products = found[offset] >> 7
                facts[item] = found[offset] & 127
                begin = jnp.where(products > 0, ((products - 1) & 7) + 1, 0)
                put((begin + 1) >> 1, item | begin << 13)

                @pl.loop(0, (products - begin) >> 3)
                def _(more):
                    put(widest, item | (begin + 8 * more) << 7 | 1 << 12 | 8 << 13)

    left[4 * active * slots] = jnp.zeros((2 * block, block), jnp.bfloat16)

    for place in range(3):
        load(8 + 2 * place).wait()
        load(9 + 2 * place).wait()

        @pl.loop(0, active)
        def _(row):
            for slot in range(slots):
                value = raw[8 + 2 * place + slot // half, row, slot % half]
                high, low = split(value.T if slot >= half else value)
                into = (place * active + row) * slots + slot
                right[into, :, :block] = high
                right[into, :, block:] = low

    for place in range(4):
        load(2 * place).wait()
        load(2 * place + 1).wait()

        @pl.loop(0, active)
        def _(row):
            for slot in range(slots):
                value = raw[2 * place + slot // half, row, slot % half]
                high, low = split(value.T if slot >= half else value)
                into = (place * active + row) * slots + slot
                left[into, :block] = high
                left[into, block:] = low

    def gather(word, size):
        fact = facts[word & 127]
        row = fact & 7
        base = (fact >> 3) * most + ((word >> 7) & 31)
        products = word >> 13
        lefts, rights = [], []
        for place in range(2 * size):
            inside = place < products
            code = pairs[base + jnp.where(inside, place, 0)]
            source = ((code >> 6) & 255) + (row ^ (code & 7)) * slots
            lefts.append(left[jnp.where(inside, source, 4 * active * slots)])
            rights.append(right[(code >> 14) + (row ^ ((code >> 3) & 7)) * slots])
        total = jnp.dot(
            jnp.concatenate(lefts, 1), jnp.concatenate(rights, 0), preferred_element_type=jnp.float32
        )
        total = total[:block] + total[block:]
        return total[:, :block] + total[:, block:]

    def add(word, into, total):
        again = ((word >> 12) & 1) == 1

        @pl.when(again)
        def _():
            done[into] = done[into] + total

        @pl.when(jnp.logical_not(again))
        def _():
            done[into] = total

    @pl.loop(0, bucket_count[0])
    def _(place):
        done[bucket[place] & 127] = jnp.zeros((block, block), jnp.float32)

    for size in range(1, widest + 1):
        count = bucket_count[size]

        @pl.loop(0, (count + 1) >> 1)
        def _(place):
            start = size * room + 2 * place
            one = bucket[start]
            paired = 2 * place + 1 < count
            two = bucket[jnp.where(paired, start + 1, start)]
            total_one = gather(one, size)
            total_two = gather(two, size)
            if size < widest:
                done[one & 127] = total_one
                done[jnp.where(paired, two & 127, lanes * kept)] = total_two
            else:
                add(one, one & 127, total_one)
                add(jnp.where(paired, two, 0), jnp.where(paired, two & 127, lanes * kept), total_two)

    def store(lane):
        return pltpu.make_async_copy(
            done.at[pl.ds(lane * kept, kept)], out_ref.at[lane, 0], out_sem.at[lane]
        )

    for lane in range(lanes):
        store(lane).start()
    for lane in range(lanes):
        store(lane).wait()


def multiply(slots, roles, tile_rows, offsets, kept_rows, kept_cols, kept_count):
    block = slots.shape[-1]
    active, half = slots.shape[1:3]
    lanes, _, kept = kept_rows.shape
    tiles = roles.shape[-1]
    items = lanes * kept
    products = 2 * (2 * half) ** 2
    smem = pl.BlockSpec(memory_space=pltpu.SMEM)
    return pl.pallas_call(
        multiply_kernel,
        out_shape=jax.ShapeDtypeStruct((lanes, 1, kept, block, block), jnp.float32),
        in_specs=[pl.BlockSpec(memory_space=pl.ANY)] + [smem] * 6,
        out_specs=pl.BlockSpec(memory_space=pl.ANY),
        scratch_shapes=[
            pltpu.VMEM((tiles, active, half, block, block), jnp.float32),
            pltpu.VMEM((4 * active * 2 * half + 1, 2 * block, block), jnp.bfloat16),
            pltpu.VMEM((3 * active * 2 * half, block, 2 * block), jnp.bfloat16),
            pltpu.VMEM((items + 1, block, block), jnp.float32),
            pltpu.SMEM((lanes * active * products,), jnp.int32),
            pltpu.SMEM((lanes * active,), jnp.int32),
            pltpu.SMEM((10 * items,), jnp.int32),
            pltpu.SMEM((5,), jnp.int32),
            pltpu.SMEM((items,), jnp.int32),
            pltpu.SemaphoreType.DMA((tiles,)),
            pltpu.SemaphoreType.DMA((lanes,)),
        ],
        compiler_params=pltpu.CompilerParams(vmem_limit_bytes=56 << 20),
        name="multiply",
    )(slots, roles, tile_rows, offsets, kept_rows, kept_cols, kept_count)


def local(stored, tile_rows, offsets, kept_rows, kept_cols, kept_count):
    slots = spread(stored)
    roles = jnp.asarray(np.array(ROLES, np.int32))
    return multiply(slots, roles, tile_rows, offsets, kept_rows, kept_cols, kept_count)


def solution(mesh):
    in_specs = (
        P("col", "row", None, None, None, None),
        P(),
        P(),
        P("col", "row", None),
        P("col", "row", None),
        P("col", "row"),
    )
    out_specs = P("col", "row", None, None, None)
    return jax.shard_map(local, mesh=mesh, in_specs=in_specs, out_specs=out_specs, check_vma=False)
```

```python
import jax
import jax.numpy as jnp
from jax import lax
from jax.experimental import pallas as pl
from jax.experimental.pallas import tpu as pltpu
from jax.sharding import PartitionSpec as P

MESH = pl.DeviceIdType.MESH
CHUNKS = 4
SLOTS = 33
STEPS = [
    [118, 104, 12, 1851457, 9576512, 17965248, 26353664, 34742400, 42213441, 50601985, 58990785, 69222914, 75767937, 84286154, 93094408, 102113993, 1073746818, 1074811906, 111558857, 1075088323, 1074326531, 119675596, 128090827, 135668233, 1076690944, 1073824768, 145113097, 1074105345, 153631301, 160203400, 168435781, 177611401, 187056265, 1074651136, 1075979264, 1076258817, 195172940, 202146504, 211165769, 220610633, 227287558, 237142667, 245766734, 252322437, 261890575, 270287041, 277619334, 287848581, 295862859, 302654149, 312222351, 320618497, 327950918, 338180293, 346194443, 352985605, 362553935, 370950273, 1076540421, 378282694, 388511749, 395084360, 404497103, 413155394, 1077337094, 421665420, 430736016, 438321346, 446831116, 455901776, 463487106, 470161930, 481067536, 489439247, 495327818, 506233552, 514605135, 520493706, 529826449, 539771023, 547756686, 554869332, 564936911, 1075780548, 572922382, 581861971, 590364808, 597178898, 607027923, 615530568, 623254222, 632193555, 638861515, 647510674, 655655505, 664027275, 672676562, 680698516, 691028168, 697842258, 707691155, 714358859, 723270229, 731152913, 741359624, 748436181, 756195860, 764690443, 1075540935, 773601941, 781484753, 792224397, 798767637, 806527700, 817390157, 825244182, 834167309, 842021462, 850944717, 858798806, 867187350],
    [106, 92, 13, 1933440, 10249408, 17039553, 25427969, 33816641, 42205313, 50724992, 59113536, 67502080, 77620809, 85819456, 92668096, 102786697, 109806218, 117713611, 1073743810, 126353924, 1074020352, 136078336, 143360522, 151267851, 161507017, 168526538, 1073782785, 1075897345, 176433803, 186672649, 193692234, 203958924, 211575936, 220701261, 229124684, 236741696, 245998159, 254421518, 262824964, 271164047, 279587470, 285737668, 296379588, 304587405, 1076169669, 313141838, 1074354118, 1075161094, 321939150, 329884367, 338176716, 347104398, 354918925, 363473102, 372270158, 380215823, 388508172, 394789444, 405431364, 413639373, 420358800, 428343940, 438141120, 447374468, 1076482052, 1074932740, 454044306, 463306752, 472933390, 478423627, 489652233, 496125524, 504244816, 514818249, 521291476, 529410768, 539983945, 546457236, 554961489, 562954887, 573538441, 580273749, 588261906, 596509383, 605439701, 614179411, 621685264, 630063687, 638993941, 647733779, 655755798, 663618055, 672548501, 681288339, 1076775943, 689179281, 697452052, 706454227, 1074700232, 1075769352, 714091218, 722864790, 1077091267, 1075540995, 731253462, 739256914, 747899601, 756419158, 764676625],
    [142, 128, 11, 2368512, 8673408, 18636801, 27025537, 35414081, 43802817, 52322304, 60710976, 69099712, 77866048, 86399682, 94265472, 103047758, 111567428, 1073744322, 119953474, 127927364, 1074287555, 136864272, 1074823168, 142893777, 153507970, 161613009, 170181138, 176579206, 185098963, 193225233, 203839490, 211944465, 220512978, 226910726, 235430419, 243557009, 254564943, 262276241, 270844498, 277373587, 285499985, 296507919, 304219217, 312787602, 319316563, 329671172, 338451087, 346031108, 354706126, 363225796, 372005583, 379585732, 388260366, 396780164, 405952590, 414057491, 1073803268, 419848902, 430891732, 438592142, 445538951, 456284302, 463471748, 470180422, 481223188, 489185872, 495870535, 506615822, 514720851, 1076956166, 523166356, 531129040, 540170446, 548275411, 556720724, 564683408, 574118032, 581829779, 590397974, 596664342, 606348480, 616060944, 623952470, 630218838, 639902848, 649615440, 657506966, 663773334, 674781392, 680928327, 1074612165, 691061462, 697327830, 706094215, 714635398, 722526741, 731275928, 739661957, 747766936, 756081237, 764830296, 773216325, 781321304, 789635797, 798646986, 806249159, 815298630, 823665866, 831709783, 840589962, 848192007, 857089031, 865630214, 1074108423, 873652951, 882270936, 889477184, 898761944, 907207191, 916087370, 924211397, 932717642, 940761751, 949379608, 956586176, 965870616, 974185109, 983196170, 990140416, 999826442, 1075436554, 1075717067, 1075995659, 1076279240, 1008394777, 1016472775, 1024874501, 1033560793, 1041791174, 1050158218, 1077336012, 1058726489, 1075260365, 1067115161, 1076588489],
    [102, 88, 9, 1687681, 8790209, 17055936, 25444352, 33833024, 42221696, 50741249, 59129921, 67518593, 76030478, 85573697, 92684481, 103303760, 109707855, 119128257, 126501457, 136858128, 1073741824, 144293889, 152830547, 162024080, 168428175, 176677458, 187189968, 193594063, 201974292, 213019349, 218759695, 228975109, 238184981, 243802830, 254140997, 1073771458, 263350869, 270918341, 278659603, 1076927428, 288516757, 296084101, 303825619, 1075375109, 310895314, 320602771, 327672466, 336077390, 344605393, 353258072, 361243278, 369877590, 1076692931, 378159761, 386812632, 1074094022, 396894210, 403431958, 411978392, 422060098, 430818009, 436879889, 448285338, 455614658, 464372313, 473451098, 480780418, 487318166, 498617050, 503833106, 512630929, 523782682, 529408209, 539869849, 1075678152, 546195992, 554573905, 565035545, 571351057, 579592918, 587604033, 597017303, 604627604, 612769793, 1074385863, 1074932682, 622750299, 629547137, 638960151, 1076525001, 647916059, 654959188, 664693403, 672514647, 1077317579, 681470683, 688513748, 1074714573, 698239644, 706069143, 715016796, 723405532, 731793948, 1075258316, 1076061196],
    [110, 96, 3, 2275456, 10289153, 18931777, 27041984, 35430464, 43819008, 52207744, 60995584, 69263489, 77668930, 1073746754, 86161600, 94445570, 100983503, 1074809795, 109486725, 1074298880, 119715904, 128131205, 134537743, 143041093, 151435458, 161685573, 168092239, 176595461, 186851333, 193258127, 202021585, 210150085, 219191425, 228794565, 235586195, 1073797125, 245440706, 252363475, 260881108, 270606466, 277529171, 286046804, 294306323, 302684753, 313459221, 1075389380, 1075930116, 320117254, 330236501, 338346514, 1076211655, 344373314, 355402453, 363512402, 1076742022, 369664662, 379388033, 386710164, 397066962, 403219030, 412391494, 422511253, 430621330, 436773398, 446496833, 454334598, 464708302, 1074149321, 470328022, 479238145, 488440001, 498262542, 504406666, 513859777, 521583243, 1077310408, 530636801, 537311234, 546644567, 554343057, 565371470, 571810519, 580303563, 590537358, 1077056715, 596976151, 607437456, 613718214, 621847114, 630792792, 640991952, 647411723, 655399105, 666157584, 672473751, 682934864, 688560657, 697901720, 705733130, 714520651, 723173398, 731456024, 739031572, 748339350, 756622040, 764453578, 772192386, 781893718, 1075239946, 789616705, 798671062, 1075784653, 1076580300],
    [114, 100, 13, 1869888, 9568449, 17072193, 25460865, 33849537, 42237953, 50757760, 59146432, 67534848, 77367424, 85065729, 92700736, 103597711, 109609103, 119310528, 127008897, 137283152, 143556688, 1073741824, 152864768, 160563265, 170837520, 177111056, 186515982, 195209859, 204260943, 210272335, 220070542, 229026434, 237815503, 243826895, 253624910, 262318595, 269149713, 279609361, 286163600, 295568078, 304261827, 1073762435, 313443472, 321553105, 327713295, 337815619, 346038402, 355255311, 363496017, 370049744, 379723776, 388941008, 397322963, 403866258, 413147650, 421963778, 431277202, 437420754, 446963907, 456174164, 464831698, 472547985, 479363602, 488906883, 498117140, 506775122, 512917586, 522199618, 1074829826, 531671700, 540328978, 547365058, 556837588, 565503702, 573317830, 579527825, 590645781, 1075371972, 597827648, 605585993, 613082193, 624200277, 631513091, 1075644870, 641001110, 649366229, 657203206, 665233602, 674555414, 681713792, 690399298, 699721302, 707534918, 713745617, 724478611, 732045504, 739803785, 748471895, 758032979, 766255238, 773637783, 783583893, 790896707, 798803671, 808364563, 815301129, 823969303, 1074352075, 1074638791, 832078537, 1076746184, 1075184649, 1074164684, 1077060549, 1076028421, 1076308938, 1076590541],
    [118, 104, 11, 2401280, 10803264, 18669569, 27058305, 35446977, 43835457, 52355072, 60743744, 69132416, 77912256, 86419074, 94298304, 102711887, 111337551, 1073744578, 119855104, 128361666, 1074287555, 136266255, 144891919, 1074823168, 153409664, 161915906, 170345169, 178839761, 187081794, 195754193, 203375311, 212000975, 220505280, 227080784, 237847058, 245555855, 254059648, 260627150, 271401682, 279503505, 287614016, 296417425, 304955986, 310960773, 321446417, 329819269, 338360337, 346899090, 352903877, 363389521, 371762373, 380303441, 388448337, 394846789, 405316677, 411621902, 422002833, 428401157, 438871045, 445184528, 1073797125, 455557137, 461953614, 470713360, 480198799, 487621646, 498549268, 504029719, 512665110, 522936343, 529195671, 537953486, 549255897, 556490903, 1075382214, 562750167, 571385558, 582810137, 590045399, 596304471, 605587091, 615211095, 622364179, 633141913, 640639512, 646874192, 654899920, 665805400, 672040144, 683473497, 1074099143, 690971288, 697206416, 705230992, 716137176, 723027667, 731830938, 741819092, 747546262, 1077000132, 756996826, 766984788, 772712022, 1077275593, 782162458, 792150676, 798000206, 805886606, 815489557, 823166094, 832494170, 840655573, 1076502476, 848856659, 857432725, 1075728330, 865821269, 1074698189, 1075241931, 1076044811, 1076326344],
    [114, 100, 3, 2418688, 10510401, 17080449, 25477120, 33865856, 42254528, 50643008, 59162817, 67551361, 75939841, 86304896, 92963470, 102785025, 109494337, 119859264, 126517838, 136339585, 1073741824, 143294990, 153116865, 159959634, 168461006, 179366594, 187326658, 195356864, 204104194, 211984899, 221309506, 229269570, 237150915, 246475394, 254435458, 262316611, 1073764354, 1075360003, 269370000, 277127169, 288541205, 294535760, 302293185, 313707221, 321938006, 329425027, 338872981, 344236097, 355492566, 364038741, 369935063, 378454680, 386703951, 397469698, 405824150, 1076941764, 411877911, 420397592, 428647119, 439378454, 445432471, 453812879, 462578321, 470598231, 478978575, 487744017, 496421593, 504381972, 514760728, 521587225, 529687121, 539926680, 546226904, 554582736, 565092568, 1074858949, 571392600, 579748368, 590258264, 596951560, 605473369, 613433940, 622239895, 630506056, 638110354, 647127761, 655794263, 664060616, 671664658, 680542868, 689348631, 697877065, 705219282, 714097364, 722903255, 731431625, 739691161, 748331731, 756597257, 765258266, 773497427, 781763209, 790424218, 798663315, 1074353161, 806666888, 815589978, 823829011, 1075151880, 1074127814, 1075979270, 832367322, 1076260807, 1076803530, 1077341131, 1076568012, 1075793869],
    [86, 72, 1, 2064384, 10819648, 18686081, 27074561, 35463233, 43851969, 52762624, 61309570, 69288463, 1073744578, 77928576, 86474818, 1074287555, 94454351, 1074823168, 103094464, 111640770, 120144594, 128417794, 137444048, 145310354, 153059392, 162338881, 170476050, 178225344, 187504769, 195641938, 203391104, 212670657, 220283599, 229351950, 238107216, 245449359, 254640772, 263272976, 271794835, 279806660, 288438928, 1073797316, 296960723, 304945153, 313360388, 322126355, 330137668, 336542231, 347292243, 353180305, 363569806, 371811030, 378485335, 388588182, 395516565, 405512782, 413753878, 420289233, 430678734, 438919766, 445594263, 454115472, 462232081, 1075393479, 470892752, 479148759, 487669776, 496179925, 1076975558, 504447056, 512956949, 521626264, 529734229, 538403544, 546118225, 555180632, 1075160005, 1075962885, 563692116, 572080788, 580469460, 588857876, 1076240333, 1075736522, 1076803528, 1077333964, 597123608, 1074736073, 1076578251],
    [102, 88, 1, 2450624, 10823809, 18776257, 25493632, 33882112, 42270784, 50659520, 59179201, 67567617, 75956353, 86336576, 94709761, 102662145, 109510721, 119734863, 128279552, 136216641, 145304066, 153289423, 1073741824, 161834112, 169771137, 178858690, 186843663, 195461774, 204024450, 212689999, 220398223, 229016270, 237578818, 246244367, 1073764354, 252248771, 262570574, 271395011, 279798991, 285803075, 296124942, 304949315, 313353359, 319357571, 330262033, 338503811, 344523267, 355427921, 363669507, 1075351555, 371761732, 380700740, 388982481, 396927492, 405866500, 414148241, 422093444, 431032452, 438870724, 447809732, 1074841604, 454247956, 462848659, 473106960, 479815381, 488014355, 498272912, 504981013, 513180243, 523438672, 529745620, 538346195, 548604624, 554911380, 564472001, 571688532, 581249089, 1074339783, 1075673032, 588858902, 597494354, 1077261254, 605883026, 614024790, 622660306, 630784588, 639437330, 647579286, 656081485, 664364693, 672858637, 1077011402, 1075979274, 681116300, 1076260805, 689530453, 698024653, 1076793291, 706281996, 714688214, 723190413, 1074713613, 731448012, 1075260361, 1076577292],
    [110, 96, 7, 2447488, 10313793, 18702337, 27091073, 35479745, 43999360, 52387904, 60776640, 69556288, 77553664, 86333440, 1073746883, 1074809794, 1074298880, 94722240, 102621775, 109520400, 120150734, 127787535, 137045586, 145316366, 153207508, 159975121, 170482254, 178373268, 185140881, 195648142, 203538964, 210306577, 218587670, 228811415, 237730325, 245482068, 252249681, 260530902, 271284949, 278782671, 288040466, 294085206, 304308759, 313227925, 321643219, 329983634, 336028310, 346251991, 355170901, 363578009, 371926738, 378232985, 388194903, 395532308, 405521113, 411787481, 422773782, 429086804, 439083667, 445342233, 456328342, 462641300, 472629273, 478896729, 489882838, 496195796, 506192403, 515048534, 521624091, 530440847, 537339536, 546798300, 556515417, 563422744, 571964060, 581689939, 588850263, 598720597, 605381256, 613754584, 622295644, 632274965, 638935752, 647562778, 655850012, 1073795014, 665829525, 672489992, 681117402, 690995413, 697655880, 706283098, 1074599877, 1075140616, 713500240, 722950875, 731456535, 739727963, 748233879, 1075426247, 756505243, 765011159, 1077004234, 773138008, 1074149316, 781526680, 1077306315, 1076012043, 790169242, 1076293580, 797386448, 1076833225, 1076584397],
    [98, 84, 11, 2312320, 8724481, 17121280, 25509952, 34029569, 42418241, 50806913, 59195585, 67453120, 77809856, 84222145, 92618880, 102975552, 109387905, 1073741824, 119752704, 126165057, 134685390, 143222977, 151462478, 160000129, 168346128, 176900815, 185016974, 193677839, 201794062, 210289296, 218702415, 227108929, 235455056, 243867663, 252397647, 260645519, 269699794, 277422287, 286476818, 1073762243, 296428226, 303254098, 313205250, 320031378, 330482387, 1074569156, 336283791, 345055761, 355648019, 361326593, 370221713, 378356295, 387105492, 1075628997, 395387601, 406538773, 414368403, 420553297, 431704725, 437076615, 445825684, 453984790, 464330774, 473647829, 479019719, 489865811, 498813525, 504185351, 512934484, 523051606, 529481814, 1074332679, 538798615, 545833680, 555575895, 563266068, 573383318, 579813526, 589130391, 596959832, 606806658, 614296279, 622125720, 631972418, 1074090954, 1074900994, 638903000, 648880854, 655311062, 664068632, 672875021, 681263821, 1077009353, 1075456972, 689652365, 698040909, 1076524998, 1077318669, 1075241931, 1076044811, 1076326344],
    [106, 92, 9, 1310912, 10330305, 18849984, 27107457, 35627072, 43884609, 52404224, 60799490, 69181568, 77071042, 85827585, 92914318, 101163729, 111254019, 1073746306, 119013442, 1074809731, 127525584, 134718033, 1074298880, 144808131, 152576659, 161079952, 170107525, 178362435, 185049745, 194519635, 203547141, 212049925, 220305539, 226992657, 236462803, 244965968, 253993669, 262125762, 269197831, 278405651, 287432901, 295936581, 304068738, 311140935, 320340098, 1073796101, 328180308, 337764421, 344695495, 354400322, 362283010, 370795024, 378249863, 388741714, 395575296, 1075124231, 403677908, 413261957, 420717141, 430684882, 437518400, 445620884, 455721615, 462660309, 473143958, 479461504, 487563796, 497664591, 504603157, 515087062, 522453137, 531219151, 538157717, 548641302, 556007441, 564773391, 573807190, 581173329, 587842126, 598456850, 606339281, 613008078, 623622802, 631898183, 1075398601, 638173710, 1074110411, 648675463, 655343764, 665452743, 671998487, 682229767, 688898260, 699138261, 705553047, 715915285, 722330327, 732692629, 1075703752, 739107415, 749469781, 1076767684, 756006996, 1076523980, 764395540, 1077055437, 1074722762, 1077355462, 1076061190],
    [110, 96, 11, 1958913, 8759489, 17137665, 25526465, 33914945, 42303617, 50823168, 59211968, 69272270, 75989120, 84379854, 94233729, 101154880, 111608527, 117934734, 127788225, 1073741824, 136774223, 143100430, 152953921, 161939983, 170124480, 176654926, 187105935, 193693903, 203678784, 211877966, 220455936, 227256977, 1073765315, 237043726, 245621888, 252422673, 261325395, 270598286, 277734467, 285977169, 296166096, 302900227, 311527507, 321331856, 328051221, 336454787, 1075352517, 345211539, 354886224, 362136581, 370247827, 380183063, 386631759, 395953865, 404193994, 412320275, 421995024, 1074843591, 429508169, 437356563, 446136970, 455680727, 462283971, 471050776, 1074596169, 479691274, 487817939, 496181974, 505005193, 512993880, 521634378, 531178135, 537766549, 546686149, 1074353162, 556343895, 563463301, 571714264, 580067926, 588891145, 596486741, 605233814, 613264085, 622183493, 630522578, 638683347, 647430676, 655600280, 664502861, 672465490, 679848065, 689668621, 697762388, 705013825, 714834573, 722797074, 1075164104, 730564751, 740000461, 747840022, 755345409, 1077003277, 1074144194, 1075995650, 1076279243, 764740242, 1077338060, 772516561, 781648532, 789284879, 798425812, 1075784644, 1076588486],
    [98, 84, 10, 2589824, 9691137, 18079809, 26468545, 34857089, 43376832, 51765312, 60703426, 68542592, 78087232, 85319680, 95017612, 102646338, 1073744194, 111772812, 1074287555, 120183372, 1074823168, 127811586, 136938572, 142992004, 153737932, 161366146, 170493132, 178903564, 1073803264, 187270156, 195426894, 203678415, 210470477, 220592654, 228844047, 235636429, 244081233, 254925520, 262398607, 269190669, 277635793, 288479888, 295952975, 305235151, 311190033, 322034192, 327911053, 336355985, 347200080, 355566607, 363592274, 371688640, 380920468, 388758162, 397509711, 406086228, 414833301, 422020096, 431252180, 439999189, 447841423, 456417812, 464255698, 471434389, 478536260, 490330645, 496739926, 503702212, 514587154, 521766101, 528867844, 539359886, 547071702, 1076960260, 557439573, 563848854, 1075665861, 572914382, 580486229, 590766679, 597031507, 605791766, 615932439, 622197395, 630817813, 641098391, 1075419078, 646963723, 655751891, 666264279, 672129739, 680917523, 688906891, 1075179464, 697295435, 1076758471, 1074154507, 1074701257, 1076028425, 1076311047, 1077373898],
    [106, 92, 9, 2326721, 8765632, 17154112, 25542784, 33931264, 42451009, 50839553, 59228353, 69435457, 76005505, 86212737, 1073741824, 94601217, 101050891, 110068233, 1073768448, 117951180, 1076408321, 126845513, 134728332, 143376963, 152011465, 159990415, 168413710, 177177225, 185164304, 193448524, 204177994, 210233874, 218718928, 229343946, 235399762, 243884624, 254509578, 260565714, 271286922, 277439120, 288090772, 296206484, 302760643, 313630734, 321776341, 329761492, 336421523, 344703619, 355574350, 361587219, 371976404, 380092948, 386777669, 397517518, 403792598, 413919252, 422036052, 428720645, 437756433, 445866647, 455994005, 463045261, 470639315, 481028180, 488088273, 497936917, 504455766, 512606853, 521765581, 529001106, 538010262, 546030083, 556901006, 1076940803, 563307095, 570813131, 1074862018, 580362897, 590211669, 596853464, 605651469, 612756107, 622019224, 630047429, 639205965, 1075147781, 646433292, 654918351, 664248913, 672359127, 679864907, 688507086, 696861263, 1077251014, 1074383878, 705284238, 713638415, 722690583, 730449998, 739459672, 1074661319, 1074162695, 1076796356, 1075502084, 747463251, 756236824, 764502550, 1075782600, 1076061192],
    [122, 108, 13, 1449152, 10363968, 18752640, 27141312, 35529728, 44049473, 52438209, 60826753, 68959884, 77603841, 85870093, 92546702, 102514380, 111036045, 119291404, 127813197, 134751824, 144457292, 1073750016, 1075865601, 152979149, 162432721, 168436945, 177609792, 185222863, 195986961, 201991185, 211688528, 218907790, 229803668, 235546257, 245505732, 1076396484, 1073792004, 252593232, 263095441, 269100625, 278273152, 1074076613, 285886095, 296649809, 302523920, 312351760, 321537686, 330466900, 336078544, 345906384, 355092182, 364021460, 370157079, 377759310, 388111364, 397035030, 405964308, 411575952, 419702478, 429792400, 438978134, 447783959, 454043223, 462822400, 470435407, 481339095, 487597271, 495199758, 505552004, 512509134, 523282071, 529540247, 538060506, 547494980, 554451982, 565224535, 570957523, 579617870, 588547739, 596123219, 604653071, 613713499, 621289107, 1075406786, 630473946, 638879451, 646454803, 1076202438, 655246544, 664045083, 672022165, 680412304, 689604248, 697443866, 705699545, 714359834, 723420818, 730998362, 739911242, 747642457, 1074385859, 1074926595, 1075212231, 756302938, 765363730, 773465738, 781196953, 789464080, 798656088, 806495898, 815408650, 823017173, 831800474, 840861266, 848963274, 856571477, 1076796426, 865764888, 873348629, 1075761096, 1074738121, 882542296, 890248729, 899581650, 1077114827],
    [126, 112, 12, 2327553, 9962625, 18351169, 26739713, 35128513, 43648000, 52036672, 60973647, 68813952, 77825217, 85591232, 95170068, 100926994, 109855376, 117835283, 128156737, 137244309, 142870098, 151798288, 159909013, 170099841, 179187221, 185074709, 193618435, 201982979, 212567122, 1073750017, 221130325, 227017813, 235561539, 243926083, 254510098, 263073493, 268960981, 277504707, 285869251, 296584719, 304885332, 310773459, 319447683, 327812227, 338527311, 1075859459, 346828500, 353125072, 363693775, 371994260, 378290768, 388859535, 1074831301, 395052743, 404906191, 411961046, 420717776, 428213907, 438460559, 445515286, 454272144, 1075636166, 464142929, 473277975, 478809688, 487327367, 497180687, 504603664, 1076170692, 512765593, 522863121, 529401494, 538158160, 548029137, 556928602, 563586262, 1074617282, 570689234, 581583505, 587990599, 596250136, 607495895, 1075427272, 612632210, 622354643, 630195722, 640814618, 648774802, 655099399, 663896199, 674369178, 682329298, 1077264391, 689061959, 696913560, 708159127, 714629267, 722873947, 733324887, 738592339, 748183635, 755633880, 764282454, 773301334, 781190730, 790249482, 798371547, 806855830, 814745226, 823803978, 833752794, 840410134, 848445447, 857091739, 865076938, 874135754, 882257435, 1073875913, 1074414602, 890912906, 898641625, 1074173901, 907165895, 915418649, 924344339, 932195929, 1075245003, 1076833228, 1076589518],
    [118, 104, 9, 2409600, 8944769, 18375680, 26764416, 35153088, 43541568, 52061377, 60449857, 68838529, 77907136, 84573836, 94004225, 101082754, 111461376, 118128332, 127533571, 134637122, 143156227, 153404480, 160202382, 170157583, 176947215, 184968706, 193756750, 203712143, 210501775, 218686992, 227311310, 237266511, 244056143, 252241488, 260865550, 270821071, 277610703, 285795984, 294288908, 302802629, 310961872, 319454796, 328099462, 1073748932, 336512721, 344352450, 353131663, 1075343362, 363355794, 369911429, 380823060, 386686031, 395495061, 403996301, 412746435, 419980483, 431408854, 438853138, 446300803, 456320660, 461923459, 472407762, 481740374, 487095361, 495740485, 505020995, 515294870, 520643651, 531127890, 537814726, 1076928456, 1075639299, 548595412, 554204161, 562980358, 571482775, 582149716, 588539465, 596794899, 604923462, 613425687, 621987413, 630482633, 1077219334, 638344399, 646735365, 655368791, 666289686, 672425609, 1074874373, 1074375685, 680681171, 688923351, 697222737, 706111051, 714374669, 722388497, 731277003, 738753729, 747554449, 756442635, 764567123, 772982485, 781608587, 789872333, 1076743179, 1074669579, 798934616, 806643209, 814504975, 1076515849, 824100504, 1075218375, 1074192391, 831676051, 840877592, 1076036554, 1073964042, 848592461, 857655000, 865256981],
    [114, 100, 8, 2499585, 8774849, 18367616, 26756288, 35144704, 43533376, 52053121, 60441793, 68830209, 78259852, 84272129, 93996097, 103181839, 111814156, 117819021, 128591436, 134596109, 145256133, 151536837, 162145996, 168281681, 178810501, 185091205, 195437761, 201836241, 212364869, 218645573, 229246478, 235390609, 245788239, 252200453, 262801102, 268944913, 1073745925, 1074818053, 279342735, 286139584, 294504147, 304508623, 311420562, 321266817, 329804805, 336611016, 346441237, 355075662, 361612947, 1076662211, 370036246, 379995861, 386802816, 395167251, 403590742, 412108296, 422708816, 428721747, 437546644, 445662792, 455739022, 462546133, 471101012, 479323157, 487466048, 495865494, 504383112, 514213461, 521266261, 529802253, 1074582536, 1075128328, 538209812, 547767957, 554574848, 565167642, 571363030, 582092432, 590333594, 1076448196, 597053143, 607258320, 615499354, 622096084, 631645249, 640665306, 1074374599, 647646873, 655484053, 664020557, 1076216774, 672812633, 680519186, 689185933, 1073881033, 1075736585, 697978393, 707921424, 713410253, 722882135, 730851026, 739517645, 748047895, 756418200, 763741261, 1077058498, 1075508226, 773476057, 781583960, 789571154, 1077348299, 798379671, 806749912, 814081089, 1074226122, 823526936, 830858369],
    [122, 108, 5, 302272, 10527744, 18916544, 27305024, 35693696, 44213313, 52602049, 61392400, 69379201, 75799616, 86156289, 94971394, 103335568, 111582865, 120137346, 126133780, 136890064, 143042133, 153525841, 162080322, 168076948, 178832976, 184985301, 195469009, 204023490, 210282134, 221300291, 226928277, 237411857, 1073745922, 246228691, 252225110, 262988886, 268871189, 279624725, 288171539, 294168086, 302835410, 311082711, 321726035, 330359956, 336248343, 346891923, 352626388, 363906691, 371899477, 380282458, 389359128, 394831574, 405857492, 411745943, 1074809796, 422225562, 431433350, 439149782, 445300311, 1074310085, 455780058, 464987718, 470066772, 481347267, 489340117, 497722906, 506930694, 514901507, 523549701, 1076412934, 1073815555, 532096198, 537716370, 548977731, 557131480, 565240916, 573226133, 582297240, 590144662, 599047237, 607463000, 613213778, 624213125, 632751322, 638379538, 649640963, 655795850, 666305562, 674292756, 683195587, 689350218, 699860058, 707585046, 716487877, 722904778, 733414554, 741917717, 750304387, 756459018, 765265497, 775472277, 780442752, 1075923978, 1074633675, 790431257, 800638037, 807050305, 1075441607, 815597273, 825803989, 830774272, 840763033, 849274459, 857381889, 866051611, 874159297, 882828955, 890936449, 1076770766, 899606235, 1077307336, 1076273097, 1075759053, 1074213836, 1077106639],
    [106, 92, 13, 2015297, 10224769, 18908160, 27296896, 35685568, 44074048, 52593857, 60982337, 69370881, 77464768, 85901313, 94536833, 103452178, 111330000, 117843473, 128749203, 134620753, 144621761, 153915091, 159786705, 169787521, 179080723, 186827408, 193341073, 204246611, 210273989, 220381712, 228459648, 237670098, 243828293, 253936208, 262013952, 1073750979, 271224466, 277382661, 287179840, 296542277, 304778834, 310937221, 321708229, 328991809, 1075855365, 338485381, 345769153, 353152597, 363865171, 372039685, 1073781700, 378318485, 387712001, 395095765, 406062288, 1075366850, 411872789, 420528662, 430973971, 439922200, 445440663, 456139923, 465088216, 470606423, 481305811, 490253976, 495903449, 506865236, 515419736, 521307656, 529580630, 538347145, 548808404, 557493385, 563528410, 571901449, 582222864, 591047689, 596566681, 605455945, 615777360, 624602185, 629990103, 639010505, 649471636, 1074335753, 658156745, 663914120, 672187094, 682886288, 689079880, 697229913, 1074874315, 708191764, 714523290, 1074113478, 1076481994, 722264599, 730784281, 1074667463, 739689050, 1075734476, 747800264, 756466202, 1076270088, 1075245006, 764461718, 1076835277, 1077114831],
    [106, 92, 9, 2153536, 10970304, 18907265, 27321408, 35709952, 44098688, 52487360, 61006977, 69395649, 77784065, 86467584, 94559952, 102793217, 111338561, 119725584, 127959233, 137061905, 145286869, 153280144, 161513537, 170616529, 178841109, 187204116, 195223120, 204170833, 212395605, 220758740, 229336721, 237436503, 245950101, 254313044, 262882516, 270990871, 279478932, 288048276, 296418902, 304825428, 313196246, 319849048, 329991188, 338362006, 346488471, 355681429, 361948871, 370180760, 380304918, 389235733, 396846144, 405208791, 1073755075, 413195456, 422790229, 428901080, 438789248, 446749824, 1076911042, 454066712, 463526912, 473122005, 481642066, 487644755, 498419218, 504683544, 515196626, 521460952, 531973778, 538500634, 546365139, 555706009, 1075361738, 1077200840, 563142291, 572483289, 1074072517, 580181144, 589260377, 1074348998, 596829767, 605594140, 614262413, 621862419, 631203353, 1073845188, 638772743, 647537308, 656205325, 664329946, 673138395, 1074916300, 1076506571, 680715911, 689480284, 698148429, 706272922, 715081371, 1076780039, 723034844, 731702989, 739564632, 748635675, 1075743757, 756604506, 765412955, 1074717646, 1076041679, 1075275721],
    [122, 108, 9, 295937, 8676545, 18924736, 27313216, 35701760, 44090496, 52610113, 60998785, 69387265, 75908624, 84182145, 94553281, 100986578, 109733585, 117736513, 128380610, 134899345, 142902465, 153546370, 159696387, 168469696, 176842321, 185003732, 193250947, 202024000, 210396689, 218558036, 226805315, 235578368, 245916739, 252112532, 260490901, 269132928, 279471107, 285787734, 296414294, 302434005, 311199376, 321414275, 327861958, 338095618, 344376853, 353142352, 363750598, 369936024, 380824728, 386696208, 397567493, 1073749956, 405589141, 411485781, 419841744, 428639440, 437044952, 447933656, 453395600, 464299539, 1075599490, 470861337, 478725846, 489352406, 495240899, 505963715, 514631379, 1075351555, 522644546, 528893008, 539797139, 548195413, 553935873, 564962899, 571524761, 579520134, 590138389, 598631558, 605332633, 613205592, 624094296, 629433409, 638886937, 646497942, 657124502, 664446682, 674391685, 680576729, 688571974, 699190485, 705995993, 716334661, 1074850759, 722519641, 730514950, 738520658, 749626438, 756852247, 1076428806, 764200472, 775089176, 783180806, 790406807, 797492758, 808119318, 813982849, 823436377, 1073838024, 830795282, 840607322, 850552517, 1077256197, 1075956682, 856092180, 865773082, 872738450, 882681559, 1074409419, 1076786124, 1077057481, 891070039, 899327642, 1075234766, 1074204621, 1074751439],
    [118, 104, 11, 1916097, 10560512, 18949184, 27337856, 35726528, 44246145, 52634689, 61023425, 69024769, 77800449, 86449730, 92882640, 103227074, 109659664, 120004098, 128820754, 134825616, 145170050, 153986706, 1073745922, 162088467, 168371219, 176891605, 186465345, 195929682, 202597972, 210445845, 220019841, 229607108, 235881493, 244000405, 254746115, 263038674, 269436117, 277554773, 288300675, 296715780, 1074807427, 305219077, 313465923, 321881732, 329860819, 336143571, 1073787012, 347020483, 355435588, 363415187, 369697939, 378355345, 1076945797, 389104773, 395413015, 403646038, 414399511, 422659269, 428811990, 437075665, 445875737, 456213573, 462366358, 471015128, 479430297, 487810772, 495920662, 504569432, 512984793, 522798675, 529081427, 540229207, 546407511, 555173078, 562904657, 571704921, 580085268, 588719706, 598949591, 605127895, 1075911622, 612976208, 622274074, 630398488, 641574619, 647710426, 655828186, 666058391, 675128859, 680477845, 689383066, 698033675, 705510929, 717071963, 722945174, 731588299, 739450520, 750626459, 756499542, 765142603, 772899991, 1075406793, 781665302, 790439567, 1076207559, 1075702728, 798189204, 807216847, 1076500429, 815481882, 823993935, 1075201998, 1074182090, 832259226, 840640139, 1077333003, 848249941, 857548303, 1074726927, 865813594, 1074491340],
    [118, 104, 10, 1916928, 10781888, 19344577, 27821584, 36383760, 43860096, 52496066, 61550160, 69764752, 77414592, 86181587, 94438914, 103492752, 110968896, 120358017, 128255508, 136513043, 144770690, 153824976, 162218004, 170689601, 178587284, 186844755, 195102274, 204161172, 212632577, 220671041, 1073747970, 228918868, 237274112, 246104148, 254225409, 262473428, 270730899, 279479504, 288047316, 296168577, 304907457, 312828630, 319368786, 329548864, 337994262, 344534738, 353175238, 363365456, 371548758, 378088978, 1075334085, 386729606, 396657792, 405103254, 411643538, 420283910, 428944921, 438788290, 448168979, 456593051, 463953922, 473334995, 481758811, 490112147, 498680516, 506924571, 514285698, 523666515, 532090587, 538093201, 549012100, 554632776, 563258897, 573005890, 580062876, 1074302919, 588056134, 596813393, 607732292, 613748378, 1074585668, 1075908614, 621979345, 632897540, 638783004, 647048793, 656320085, 665935955, 672958103, 682713107, 689245914, 697239048, 706651861, 716267667, 722669276, 730793608, 739323545, 748455447, 758210771, 1074880459, 764348104, 773621335, 781664792, 789909018, 1075680264, 798787287, 806830744, 815074906, 823209689, 832480917, 840385112, 849258005, 857162456, 865275484, 1075177420, 1076234189, 1074163663, 1076803529, 1077330894, 1073951690, 1077111747],
    [110, 96, 5, 2344000, 10706113, 18965504, 27354304, 35742848, 44131392, 52651073, 61039617, 69428353, 77841600, 85818896, 94594241, 103088850, 111764690, 119784448, 127762000, 136643218, 145319058, 153339008, 161316496, 170197522, 178873362, 185296515, 194870992, 203810513, 212140626, 220816466, 227370693, 237337797, 245753425, 254607891, 260924997, 270892101, 279307793, 288162451, 294479365, 304307201, 312862353, 321716819, 328033925, 338290389, 346389509, 1073743877, 355271379, 363456149, 371416193, 378348052, 388621909, 397246102, 1074295746, 405890583, 413787669, 421747777, 428802584, 439576217, 447577814, 455861401, 462234324, 472999575, 481519129, 487286339, 497384581, 506192921, 512565908, 520840899, 531463702, 537854616, 548136537, 556885719, 565404761, 571172355, 582057171, 588186328, 1076926467, 598572630, 604963416, 615245529, 623994455, 632513753, 640777299, 647358042, 657415191, 1075367880, 663560788, 672523802, 682581079, 689301210, 699497491, 706078362, 1074605001, 716135575, 723198555, 1076450244, 733052051, 739975707, 749690071, 756753115, 765164564, 1074902982, 773530267, 781941844, 790330580, 1077272526, 1075709899, 798719124, 1074163658, 1076798412, 1076029391, 1076298695, 1073960909],
    [106, 92, 12, 328769, 8709249, 17132737, 27346048, 35734528, 44123328, 52511808, 61031425, 69420225, 77808769, 86601424, 92595393, 100992193, 111363137, 120155728, 126281233, 134546433, 145321616, 151447185, 159712385, 168232016, 176647701, 185001553, 195653136, 201786512, 210035713, 218563600, 226979413, 237954646, 243729616, 252145301, 263120406, 271787538, 277311189, 288286422, 296953554, 303001299, 313452182, 1073742790, 322119314, 328298007, 335864897, 345075287, 352773841, 363791882, 372450898, 378629847, 387245200, 1073762186, 395396747, 403795607, 412542612, 423175833, 428951243, 437576784, 444951681, 456730137, 462777408, 471254552, 481231946, 487671371, 495283201, 504809176, 515450457, 1074566085, 521225739, 529493523, 538371668, 548340938, 1074840587, 555017232, 562392129, 574170841, 580217856, 588695128, 598672522, 1074072516, 605383872, 613869268, 622265882, 630156947, 638903504, 647431898, 656230031, 663711315, 672581272, 680986202, 689784527, 698287232, 706047104, 714532372, 723338831, 731841728, 740115983, 748618816, 1074353167, 1075158989, 1075702722, 756483738, 1076508616, 765395968, 1077306316, 1076013001, 1076293582, 1076829123, 1075540935],
    [118, 104, 5, 2630657, 10593344, 18982080, 27370496, 35759232, 44278913, 52667457, 60810960, 69444801, 78128257, 86221825, 92644881, 102753872, 109553234, 120071361, 128040579, 134588113, 144696848, 153724035, 162014273, 169983555, 176531025, 186640016, 195667011, 201959060, 212207251, 220315331, 226862737, 237749330, 245998787, 252290644, 262538835, 269198933, 277595345, 285845204, 294397076, 302753301, 311149649, 319399444, 327951444, 1073750980, 336567877, 344958486, 353092753, 361506004, 370122437, 378512982, 386647057, 395060244, 404864515, 412067542, 420463638, 430547971, 1075855363, 439328471, 445621910, 454280340, 462530264, 472882711, 479708181, 1073779650, 1074851141, 489660055, 496084504, 504611924, 514197203, 523476551, 529900615, 538166292, 548642439, 555066503, 564905682, 571582040, 579314898, 589694483, 598974151, 605398215, 615237138, 621257746, 632528391, 638952455, 648791698, 654812306, 663856792, 1076698054, 1075398663, 674209367, 681158283, 688899158, 697277573, 705406613, 714589333, 723101387, 730831877, 738961109, 747619478, 756655627, 1074378697, 764918872, 773432907, 781173974, 1077267467, 790084632, 798213332, 806861976, 815252565, 823639256, 832029909, 1074670541, 1076523980, 840705561, 1077059530, 1075759048, 849094297, 857482841, 1074210766, 865871577, 1076320207],
    [114, 100, 13, 2329665, 8725697, 18973888, 27362304, 35750976, 44139648, 53325520, 59057153, 68674066, 75858962, 86879888, 92611713, 102490643, 109675539, 120434256, 126166081, 136045267, 143230163, 153988624, 162202832, 169599635, 176784531, 187368464, 195267777, 203801109, 210077266, 218728019, 229311632, 237210753, 1073748930, 245744213, 254477392, 262376449, 270910101, 277186194, 288730708, 294463185, 1075339204, 304464597, 313896660, 319628945, 329900695, 339062420, 344794641, 355066583, 361072338, 372616724, 380438104, 388620823, 395151049, 403803862, 413992664, 1075612615, 422175319, 428705417, 437358102, 447547032, 1074328518, 456122502, 462917201, 472712728, 479715538, 487425545, 496471057, 504440411, 514842694, 520980041, 529343569, 538414225, 1076957193, 548397062, 555058891, 563187350, 571680412, 580378770, 588745937, 596969053, 1074873290, 1073849283, 1075963848, 605544530, 613518934, 622134941, 630972499, 638658075, 649060550, 655435419, 1076236229, 664257049, 672902878, 680601307, 1074677708, 689423065, 697665099, 706457118, 714286684, 722977433, 731219595, 740011614, 747963933, 1074180045, 756531801, 764773899, 773566110, 781518557, 1076810763, 789701210, 798172892, 806478362, 814949916, 823255706, 1075260366, 831644378, 1076590543],
    [94, 80, 7, 1432576, 10380289, 18972865, 26862592, 35251328, 43640000, 52028480, 60548225, 68936705, 77325377, 85318784, 94470273, 102516367, 110879937, 119635969, 127682127, 136183314, 144039104, 153190465, 161236687, 168420994, 177593408, 186402319, 193569300, 201975298, 1073754112, 211803792, 220095553, 229212739, 236969552, 245261441, 252813909, 262038721, 270401170, 279544515, 287301328, 295978643, 304710275, 313288209, 320732882, 1076913219, 329875459, 1076148164, 338454097, 345898578, 353739462, 363087379, 371580566, 1077203909, 378905222, 388253395, 396746454, 404070918, 413951633, 421912086, 429236806, 438584915, 447077974, 1074867206, 455894737, 463461904, 472794245, 479306453, 489571333, 496083477, 504620567, 514737221, 521773079, 529786519, 539903173, 546939031, 554952279, 1076716492, 563716183, 571729623, 1075948490, 579969685, 587834004, 1076478919, 1073876941, 597270743, 604628674, 1074681801, 612999892, 621388372, 629794370, 1075218379, 1074190338, 639100430, 1075514312, 647489230, 655877710, 664266382, 1074486286],
    [114, 100, 5, 2466817, 8873153, 18859137, 27247617, 35636417, 44024897, 52544640, 60933120, 69321792, 76113420, 84379276, 94487744, 101156428, 109528717, 119918287, 126567631, 134710988, 145083983, 151733327, 161850433, 1073752064, 170249743, 1076391937, 177055310, 185287695, 193578704, 203804303, 210453647, 220570753, 227133008, 237883090, 244164302, 253060304, 260687376, 271437394, 277316620, 286614544, 294241936, 304991762, 312845505, 320169104, 330157714, 336438926, 345334864, 355585748, 361875079, 369993230, 377964109, 389140116, 395281472, 403130061, 414305876, 420447360, 428295693, 439471636, 445613248, 453469313, 1076932549, 462278294, 471582408, 478766284, 487556096, 496094741, 505136648, 512320588, 521634949, 1076683718, 529788567, 538691144, 545875084, 555189445, 563343063, 571966469, 580609667, 588369621, 597132357, 605775427, 1075918403, 613674519, 622700049, 631072339, 638701141, 647865937, 656106499, 663604822, 672908936, 681404115, 689931395, 1077241801, 1076200456, 697421461, 705807879, 714974929, 723215555, 1074121674, 1074400266, 731735571, 740262979, 747892311, 756139719, 763847681, 773817539, 781045462, 790472337, 798844563, 806211094, 814859847, 822568001, 832537603, 1074680772, 1074954247, 1073929154, 1075518466, 1075795915],
    [102, 88, 11, 1048576, 10266689, 18753536, 27142272, 35530816, 43919552, 51774156, 60598273, 69888578, 76546176, 85764289, 95054530, 101712064, 110930049, 120482510, 127271564, 136743567, 1073750016, 1075865601, 145385986, 152437324, 161909263, 1076400386, 1074844674, 170551426, 176695955, 185991692, 195603085, 204368462, 210250451, 219152448, 229157453, 237922958, 243804691, 254323213, 262144147, 271477262, 277359187, 287738447, 295698515, 305285840, 312904399, 320864275, 330451472, 338209485, 346030291, 355617360, 361507479, 372419222, 379715735, 1075125188, 389171856, 396886081, 403720786, 411839063, 421658711, 1075399619, 431254040, 1074374597, 438968977, 447916566, 456419928, 464134865, 473082454, 479480405, 487336663, 497689169, 506637014, 513034773, 521415175, 531103873, 1076216774, 1073873926, 540306072, 546712072, 556409361, 563366549, 571747015, 579611159, 589430807, 599026392, 605432392, 614989825, 621824722, 630598344, 639762647, 647252693, 655764104, 665321665, 1074154504, 672156178, 680798855, 688933522, 697576007, 1074699271, 706497108, 1075770313, 714885780, 723274452, 731662868, 1077098443, 1077374922],
    [114, 100, 6, 362689, 9963712, 18352256, 26740736, 35129408, 43649089, 52037761, 60830223, 68815041, 75860033, 85592065, 94384847, 101025921, 111282704, 119550607, 126191617, 136448656, 144716367, 154249231, 1073750017, 161614416, 170684113, 178794512, 187803855, 195168976, 204238481, 210111043, 220737744, 229746767, 235425298, 243796613, 254292112, 263301263, 271347217, 277350981, 285479572, 296716355, 304901713, 310905541, 319033940, 328173568, 336202261, 344477330, 352717443, 363343952, 372213891, 1075868612, 378145429, 389180549, 394791429, 403671232, 1076924421, 411699797, 419974738, 428214787, 439322627, 444863188, 453529298, 461769411, 472877251, 1074839555, 478808789, 489843717, 495717015, 506955927, 511971860, 523398213, 529271383, 540510295, 546452056, 556952773, 562825751, 574064663, 580006424, 588533395, 596380375, 607619287, 613560984, 622087699, 630163584, 1073817538, 638726872, 647253587, 655329344, 664015513, 672419539, 681420880, 689181273, 699420246, 706586768, 1076194246, 714347033, 724586134, 731752464, 739513049, 749751830, 756918480, 1076475847, 766529238, 773818517, 1077266379, 782134874, 790595669, 1074143180, 798912026, 807373013, 1075728333, 1074698186, 815689434, 824150037, 1075235785, 832466586, 1074474952, 1076845518],
    [106, 92, 9, 540736, 10512385, 18901185, 27289729, 35678273, 44198016, 52586560, 60975296, 69354192, 77752320, 86650385, 94519824, 103427793, 111297168, 120515156, 128593553, 136462928, 145680916, 153759313, 159924224, 170846868, 178917011, 185090240, 1073755074, 196012756, 204082771, 210256000, 221170197, 226897108, 237519570, 246336085, 252062868, 262685202, 1076904900, 271501973, 277228564, 287851154, 1073779651, 296667861, 304746003, 313016914, 322226903, 329912019, 1074848709, 338576089, 347392663, 353119830, 363741721, 372558423, 378416153, 388907609, 1075907526, 397855450, 403451606, 414073497, 420768328, 431278615, 436612180, 445931537, 456575578, 462302297, 471097489, 481741466, 487460444, 496263377, 504785482, 515295770, 521022617, 529941016, 538339850, 546891859, 554569436, 563372113, 572057619, 579742937, 588661464, 1074360263, 597060234, 605735451, 613166742, 622215832, 630901403, 638455324, 647654028, 655770200, 664038088, 672721043, 680398492, 689596940, 697723594, 706398811, 713829910, 723151564, 1076737995, 1077271562, 731146760, 739829971, 748317260, 1075710988, 756312712, 765119195, 1074681801, 1075222536, 1075496909, 1074211790, 1076586447],
    [134, 120, 11, 1960129, 10504385, 18892865, 27281409, 35670145, 44189696, 52578432, 60828176, 69355584, 77457537, 86132928, 92555923, 102771344, 109464210, 119916690, 128733780, 136595540, 142887443, 153102928, 159795730, 170248210, 179196501, 186927636, 193219155, 203434704, 210258646, 220973270, 229528277, 237259412, 243550931, 254027795, 260590166, 271304790, 277498583, 288116756, 295979732, 304761346, 312748115, 319310486, 330025110, 338579989, 346704450, 354691219, 361122386, 371574866, 380390105, 388780180, 397036162, 405022931, 411585046, 422299670, 428493399, 439243413, 447498777, 455756482, 464267394, 470174418, 480626898, 1073754114, 487213719, 497832148, 506219097, 512510532, 522987522, 531875908, 1076913091, 537545239, 548303576, 556550809, 562842116, 573319234, 581560849, 590246552, 596396676, 606873794, 615762052, 623800856, 629951172, 640690265, 649316548, 1075871748, 657355352, 665856025, 674482180, 682913795, 691021977, 699001425, 708341975, 716187865, 724167313, 733507735, 739387542, 1073798087, 748546049, 1075384265, 758411395, 764545108, 773711937, 783577155, 789719254, 799664849, 809005079, 814876884, 823388352, 1074618312, 834170967, 840706258, 848554048, 1075686342, 859074755, 865216534, 873719808, 882528794, 890374292, 898885760, 907694810, 915539988, 924313749, 932860570, 940714070, 949479509, 958026330, 1076480972, 966535314, 1074403275, 974645269, 983312402, 991422677, 1075201997, 1000089682, 1074172874, 1074984901, 1077356495, 1076326350],
    [134, 120, 5, 2007168, 10946625, 18393217, 26781889, 35170369, 43558913, 52078720, 60467264, 68856000, 77636172, 86444161, 94021632, 103205379, 109357570, 119579148, 128387073, 137161294, 144613440, 153684559, 161925763, 169779392, 176753361, 185256594, 195076748, 204016335, 210422482, 220110848, 227084817, 235588178, 245408460, 254347791, 260753938, 270836372, 277416593, 287754819, 296002260, 302582353, 1073743363, 1074028547, 312920259, 321167892, 329845391, 335981061, 345033235, 354722388, 363268289, 369535557, 378587731, 386573005, 395258518, 403221190, 411478661, 420530835, 428515917, 437463768, 445164166, 453421765, 464317070, 470721040, 479144534, 1075884037, 487639763, 495886928, 504310294, 512272966, 523037390, 529834517, 538389015, 545827334, 556591630, 562995856, 571943639, 1076943878, 582543876, 588939457, 597232154, 1075643268, 1073832964, 607709252, 613329480, 622493697, 630401560, 1076213703, 641263748, 646228610, 655008269, 664341210, 674818244, 680700553, 689218197, 697510552, 706529945, 713992904, 722774602, 731545729, 739715671, 748603931, 755935880, 764717706, 772711120, 781781594, 790416089, 797223618, 806791883, 815047381, 823601815, 832490203, 839821832, 848603658, 857374785, 865282648, 1077270536, 874302041, 881109570, 890677835, 898278029, 907610778, 1075447810, 1074424834, 916376219, 923970057, 932620811, 940876373, 948906710, 958319195, 965913289, 974563979, 1076792331, 1074718731, 983353881, 991078985, 999598794, 1076563977, 1075008522],
    [106, 92, 8, 264257, 9996352, 18385024, 26773696, 35162112, 43681793, 52070529, 60994188, 68847809, 75761857, 85624897, 94276174, 102937292, 109316225, 119573007, 127830542, 136491596, 142870529, 153127631, 161385166, 170045964, 176564288, 186681999, 194939534, 204124238, 210380943, 220236367, 229174929, 235188752, 243935311, 254332563, 260485714, 269101263, 279768724, 285651474, 294004864, 304777749, 313323092, 319206034, 327821327, 338332309, 346877460, 352760530, 361113600, 371886677, 380169809, 386183824, 394668224, 405441237, 413724369, 422621782, 430844557, 439152340, 447787542, 456010317, 464047635, 473084569, 481176077, 487492229, 497610257, 503624272, 514730701, 1073745859, 521046725, 529460951, 540062358, 546179093, 554601029, 565228246, 571475980, 579766789, 590524953, 1074550724, 1075095556, 596510933, 1076414469, 607302233, 613419084, 624079577, 630196428, 640208595, 648720590, 655362188, 665374291, 673886222, 680396949, 688844439, 699052174, 705562709, 714010199, 721728208, 733262424, 1074339784, 1075671048, 739175959, 750039704, 1076990919, 1074912198, 1075457031, 1076786182, 758428184, 1077314498, 766816984, 1073924043, 1074210761, 1076323274],
    [130, 116, 8, 1884160, 10545153, 18933889, 27322433, 35711169, 44230784, 52619456, 61007872, 69255696, 77785152, 84315714, 92596290, 103211537, 109481666, 117762242, 127976016, 137030163, 144490688, 154308308, 159836372, 169656384, 176769621, 187361939, 196251284, 201779348, 212254867, 221203030, 229805652, 235333716, 245940869, 254757398, 263360020, 268888084, 277146242, 1073743811, 287883973, 296700566, 305696324, 310700546, 321438277, 1074022402, 330255062, 335973378, 344648217, 354992645, 1074308101, 363939865, 371911251, 378440729, 386591449, 397197847, 405883097, 413854419, 420383961, 428534425, 438755985, 447826073, 454093320, 462326937, 470477401, 481084119, 489769049, 496036424, 504532679, 514253393, 1076150727, 523848344, 529590920, 538356872, 547799123, 557402648, 563522568, 572964883, 582568664, 588311240, 596544601, 606126800, 1073813512, 616122968, 622127819, 630361159, 640082641, 1075401673, 647973530, 655682059, 663915527, 672590540, 681624208, 1074894794, 689916442, 698264779, 706144780, 715571411, 723470938, 731024519, 739699340, 749519511, 757025498, 764734027, 773762123, 781642316, 791462487, 1075170316, 797526549, 809012868, 815579264, 822692565, 834178564, 840360594, 847858325, 859344580, 865526290, 1074671620, 874474203, 882174603, 889621634, 899080786, 1077042187, 908028507, 916368523, 924246738, 933194395, 941009992, 949971483, 958311435, 1075754957, 1077341126, 966175944, 1076572111, 1076847566],
    [118, 104, 6, 2386049, 10809537, 18925568, 27445377, 35834049, 44091520, 52480192, 60999681, 69118480, 77645888, 86272001, 94695489, 102942785, 111061712, 120351441, 128249985, 136227472, 145517137, 153415681, 159828499, 169781840, 179071633, 187486804, 193382995, 204130902, 212371601, 221041172, 228878401, 237816407, 243714707, 254314577, 262957585, 271372948, 279759383, 285657811, 296257745, 304927444, 312764609, 321702551, 329811985, 336261271, 344483904, 355257047, 361400339, 369815767, 378038272, 1073755075, 386845337, 394954835, 403370007, 411592832, 1076904898, 420399833, 428509331, 436924503, 445147328, 453954073, 462063827, 473223254, 479357461, 487508569, 495626393, 504165016, 512912085, 521325210, 529180889, 537719320, 546466453, 1073778629, 555010715, 563268186, 571123801, 579793618, 588409429, 598395542, 605342299, 613599962, 621455385, 632606870, 638896667, 647154202, 655140954, 663548632, 1074586567, 673893078, 680839899, 688695450, 1075909576, 699715798, 707447318, 714123355, 724881430, 731408924, 739027162, 747565650, 756574812, 764454939, 772600408, 781740700, 789620891, 797897234, 807168669, 814786779, 823063186, 1074874315, 832072412, 839690266, 849111645, 857500381, 1074113485, 865888797, 1076484042, 1075186636, 1074425801, 1076797390, 1075767238, 1076312004, 1077369807],
    [102, 88, 13, 2328577, 10428481, 18950336, 27338880, 35727360, 44116032, 52775504, 60760257, 69568592, 78080657, 85925889, 94734864, 103246545, 111091841, 119900880, 128412241, 137035840, 145066640, 153578001, 162201728, 170494547, 176630468, 186992656, 195756224, 204049043, 212158608, 220921856, 229214739, 235350532, 245713104, 253987009, 260768402, 269437524, 279152705, 285934162, 1073748931, 294070916, 302991892, 312707201, 319619797, 327625284, 338905622, 344785557, 355837956, 1075334148, 363932248, 370100948, 380995672, 386597586, 397486616, 406014614, 413764307, 420421782, 1074561989, 431041176, 439568982, 448104600, 453976150, 1073796034, 464595672, 473123542, 481659096, 487530710, 495930004, 506824728, 512557589, 522013335, 529473558, 540387396, 546925146, 554500693, 565553348, 1074858954, 572222169, 580330203, 590719108, 597510679, 605784601, 613884507, 622553689, 630950105, 639050267, 1074359238, 647842519, 656116377, 663421458, 1076474823, 672754330, 681281625, 1077004235, 689382043, 698050713, 706562647, 1074144206, 714697434, 1075996616, 723085850, 1076273103, 731605017, 1075763148, 1075261385, 1076852685],
    [118, 104, 13, 296960, 10301569, 18942017, 27330689, 35719169, 44107969, 52627648, 61016064, 69693136, 77793408, 84445392, 94187521, 102959168, 109382289, 120024656, 127742145, 136358033, 142936785, 153579024, 161296449, 169912529, 176491025, 187133584, 195498000, 203466769, 210176578, 218852884, 229052560, 237283394, 243730946, 252407444, 262867541, 270995664, 279226370, 285674114, 294350420, 304810645, 312938576, 321169538, 327617218, 336293588, 346753749, 355283667, 363112642, 1073745922, 369822359, 380595798, 388696597, 397191319, 405615123, 411765335, 422538902, 430745687, 439169619, 445319703, 456093206, 464300055, 472724115, 478874327, 489647830, 495784466, 506243287, 1074808771, 512035409, 523332821, 529339026, 539011153, 546638344, 556887125, 562595856, 573911048, 580192840, 590441493, 596150416, 607465544, 613747400, 624127122, 629704784, 641020104, 647301768, 657550485, 666185864, 672172115, 1074036744, 682847250, 688162944, 1073793988, 697912856, 705857665, 713888466, 724790482, 730892499, 739054162, 749956178, 756058259, 1074338757, 765397516, 773410456, 780437696, 790563532, 798576344, 806389779, 815353432, 822380608, 832506508, 840075265, 849283660, 856852673, 1075401740, 1075162059, 865241153, 1076486089, 1075717066, 1075998669, 1076802510, 1077077958, 1076301767, 1074755535],
    [126, 112, 9, 2189505, 10577985, 18966657, 27486208, 35875008, 44132353, 53030416, 61040768, 69429312, 77589137, 84371601, 94973520, 103105106, 111143633, 117926097, 128528016, 136405523, 144697937, 151480401, 162082512, 169863697, 176646161, 185274068, 195125907, 204458709, 210439828, 1073744834, 220291667, 229337686, 237365334, 243994132, 252406340, 262488594, 271280662, 279308310, 285937236, 296043154, 304835286, 312862934, 319499863, 329597650, 338676245, 344665623, 353200711, 363842197, 369831575, 378366471, 389007957, 395274953, 403386071, 414149144, 420168217, 428959769, 439052950, 447080598, 453995017, 464849944, 472869592, 1074283459, 479029959, 487547482, 496224778, 504326729, 515181784, 521365594, 531589784, 1073779654, 538012313, 547447507, 554559497, 563047049, 573901976, 580086426, 590309976, 1074842633, 596732505, 607898203, 613376154, 622029530, 632622168, 1074605000, 1076458437, 638675673, 646930650, 655222857, 663972378, 672738972, 680356487, 691784219, 697262106, 706293276, 1076992007, 716950235, 722157785, 731450909, 738934873, 747760139, 756624988, 767281819, 772489369, 781782685, 789922319, 798214858, 806948445, 1075435403, 815088207, 823257227, 832114397, 840254159, 848546378, 1075197199, 857288412, 1077298442, 864774660, 873808015, 881715401, 889940676, 898877578, 1074180044, 906717828, 915531979, 1076812804, 1075782605, 1076062158, 923658377, 932309067],
    [106, 92, 9, 313408, 10834112, 18958337, 27347137, 35735617, 44124289, 52898512, 61165568, 67422400, 75844162, 86452880, 92623441, 103344194, 111626770, 117787138, 128395792, 134566609, 145287170, 151341698, 161950288, 168120977, 178841730, 187124370, 193284802, 201675281, 212396226, 1073741826, 220678738, 227093204, 235358420, 243583104, 254103680, 1073769411, 260647444, 268912660, 277828179, 285526016, 294202004, 302467220, 313714833, 321212480, 328141333, 336415382, 344937107, 355657937, 361695829, 369969750, 378491603, 389212177, 394995862, 403524310, 412045843, 422766673, 428804821, 436685396, 448063617, 456486994, 462105110, 470632470, 481617985, 490041490, 497502930, 504826391, 515172545, 523595794, 532105816, 538381015, 548726785, 557150418, 562636884, 574058584, 1076398023, 582437400, 588712535, 599224344, 1074066372, 607603416, 613099734, 624390360, 1076967368, 1077243849, 629876822, 639070209, 1076728774, 649546392, 655297173, 666333336, 672598679, 681013441, 689401985, 698165849, 706179137, 1074912202, 714943129, 723331801, 1075454923, 731720217, 1075990478, 740223514, 748612186, 1074698181, 757000858, 1075235788, 765389530, 1074470861, 1075800015],
    [106, 92, 11, 2082880, 10356865, 18982976, 27371712, 35760128, 44148864, 52668481, 61057153, 69567120, 77834241, 85969024, 94242817, 103000257, 111782417, 119644866, 128174274, 136579089, 145599058, 153199170, 161622723, 170117186, 179153426, 186753666, 195177091, 203409408, 212708050, 220307970, 228731395, 237225986, 1073745922, 246262418, 254124755, 262285891, 270518464, 1074817027, 279282256, 287557762, 295569473, 304448208, 313641042, 320735425, 329613840, 338806994, 346819224, 355707032, 363700950, 371829457, 380749842, 1076396996, 388237521, 397650456, 405643798, 413772369, 420456967, 431081618, 438569041, 447982168, 455451283, 464104081, 470542868, 480512145, 489925336, 497918550, 504343239, 512486036, 522979352, 530948691, 538298967, 548145240, 556638870, 563464919, 573311192, 579594964, 589668883, 598878874, 605407895, 615656026, 621537876, 632433178, 638962199, 649210586, 655338119, 664259221, 672803545, 680503879, 689424981, 1073799115, 1075644423, 1074362314, 697969241, 706079259, 1077252041, 1074653128, 714746521, 722856667, 731523609, 739633819, 748145365, 1076238285, 756533781, 1075207118, 1075491782, 764799579, 1077069775, 1074209733, 1076064204],
    [110, 96, 13, 2304129, 8761537, 18738369, 27363457, 35751937, 44140609, 52529345, 61453008, 69069953, 77801665, 86880913, 94578689, 102624257, 112046801, 119401537, 126167637, 136572096, 145601041, 151333397, 161737856, 168110741, 179671635, 185174552, 195292160, 201665237, 213226003, 218729176, 229583504, 235400914, 246780627, 252283480, 263137872, 271167632, 279178304, 285837976, 296692240, 304984657, 310898194, 321857744, 327675538, 339055251, 346664976, 354625601, 361229906, 370379270, 380219472, 387000320, 394907289, 403777600, 412324564, 422440474, 428943552, 436850201, 445878804, 454109312, 462016217, 471044692, 481626200, 487821972, 496487637, 504859210, 515180568, 521769686, 530042005, 538151558, 546802314, 557123800, 563712662, 571984981, 580356618, 590678168, 597267030, 606989914, 613648966, 622299850, 629518401, 639306331, 648933082, 1073746954, 655592134, 663072897, 672868887, 682487450, 1075069958, 689801806, 697930262, 706202645, 714812055, 1074037703, 723356302, 730451545, 738570241, 748358171, 1073799113, 756910606, 765143639, 773688014, 781920983, 1075646478, 790301403, 798689947, 1074879432, 1075422146, 1075966915, 1077021643, 1074423749, 1076277199, 1076809676, 1074736068, 1076590541],
    [102, 88, 8, 1697857, 10086529, 18475201, 26863617, 35383424, 43771968, 52160512, 60549312, 69618255, 75861071, 85836304, 94784143, 101026959, 111002192, 120295058, 128051921, 137390804, 144695955, 153849362, 161606225, 1073754112, 170945172, 178503761, 187535061, 195291734, 204499540, 212058321, 218860630, 228715025, 237234902, 246442516, 254001169, 260803798, 270789270, 279333391, 285969558, 295944849, 304212113, 312732182, 321276623, 327912470, 336227031, 346787410, 353266392, 363564754, 370043416, 378777178, 386820760, 396214992, 403942938, 411986520, 421380752, 429108954, 436890135, 447865372, 454274714, 462416458, 470960795, 481419932, 489524821, 495971018, 504777309, 514974428, 523079317, 529680987, 539856405, 546302602, 555108893, 565677265, 572515027, 580274909, 590843025, 596634122, 1076908994, 1074830279, 1075371018, 605178395, 615637596, 1075646405, 624397393, 1074611142, 630606493, 639623763, 649563153, 654994007, 664789523, 1073842120, 673165017, 680676059, 689942105, 1074129859, 696937111, 706719257, 1076497356, 715107993, 721784015, 1074423757, 1076279241, 1077342155, 730172431, 1076828100, 1075274702],
    [106, 92, 13, 354368, 10856641, 17131520, 28027468, 36295309, 42322638, 50686080, 61581836, 69849677, 75877006, 84240576, 95136396, 103404045, 111766221, 120302284, 1073752064, 128569549, 1076391937, 136931341, 145074241, 154260047, 162097293, 170240129, 179425999, 187017217, 195913857, 204591759, 212961421, 221079617, 229757455, 238127117, 246245569, 252432978, 262760525, 271681613, 277596675, 285987538, 296847565, 304965633, 311151171, 319541778, 328313038, 339036755, 344705731, 353225236, 364202643, 370510417, 378522117, 387033230, 397757139, 403819222, 411816594, 420465285, 431311379, 437619345, 445999760, 454396433, 462277204, 471312468, 479685141, 487705238, 495831700, 504351429, 513386646, 521497296, 528861710, 538282705, 546794069, 554813974, 1076930500, 562416206, 571460165, 580495382, 588606032, 596363907, 1076154373, 604883668, 1074856963, 613918932, 622160400, 630835913, 638691406, 647457429, 655477334, 1074091975, 664523287, 672778825, 681158742, 689400533, 698077847, 706333193, 714582036, 723243735, 731499145, 739354638, 1075150857, 748409431, 1073865666, 756525204, 765044950, 1075973066, 1074416650, 1074699211, 1075502091, 1075785670, 1076852680],
    [126, 112, 9, 2395137, 10626049, 18754624, 27143360, 35531776, 43920512, 52440257, 60828801, 69619340, 77605889, 86123585, 94932684, 102771777, 111554126, 119950860, 128066753, 136875148, 145116364, 153232513, 159690321, 170282572, 178521744, 184856081, 1073750016, 1075865601, 195710669, 203687504, 210022033, 220876301, 228853456, 235187921, 245771790, 254430797, 260320916, 271320212, 279481356, 287715022, 296373901, 302264020, 313263316, 321424460, 327691862, 338448015, 344206868, 355206164, 363105473, 371601038, 378162772, 386149460, 397149268, 405048385, 411578070, 422866435, 430966483, 440044558, 445132438, 456420995, 463768705, 472122896, 478686742, 489975491, 498075283, 507153550, 515141187, 523634200, 529837655, 1076400131, 1074844675, 537545876, 548800152, 555003607, 564940367, 574262478, 582354520, 588394073, 598494927, 607816782, 615909080, 1075126212, 1075672002, 622079494, 632049167, 639274645, 649070163, 655502873, 664022726, 672681049, 681217557, 691013139, 697446041, 705965702, 714624153, 722732626, 731164311, 739520070, 748440726, 756287122, 764718615, 1076992006, 773336776, 780815380, 789841426, 798658261, 806891144, 815549526, 823396050, 832212565, 1075441605, 840445512, 849103894, 856829657, 865611272, 874007769, 1076759560, 882650827, 1074689991, 891047126, 899427851, 906644692, 1077314505, 1073923081, 916205131, 924339225, 932982411, 1074202635, 1074489290],
    [114, 100, 7, 1576065, 9964737, 18353153, 26872896, 35261632, 43519041, 53063247, 61368399, 68816000, 77204480, 86259408, 94244498, 103311887, 109554834, 119541393, 128202384, 136318481, 145255055, 153718420, 161746453, 170538518, 178261585, 187198159, 195661396, 1073750017, 203689685, 212088336, 220204753, 229215956, 235300945, 245632661, 254031440, 262541016, 271158804, 277244049, 287575637, 296891541, 305376472, 310798545, 322319897, 329886927, 335964177, 347485849, 355486231, 363441295, 372651609, 380218383, 389302938, 397817561, 405147160, 414428184, 422857434, 1075858370, 430585430, 438701720, 447982744, 456411674, 464139926, 472256088, 481537112, 489966170, 495455877, 506083030, 515263059, 521506001, 529010245, 1074305988, 540161045, 547229266, 557206227, 562539602, 570953413, 582104277, 589172434, 599149075, 604482770, 612896261, 624047189, 1075368965, 631115282, 641092243, 646425618, 1075128259, 657476183, 664637148, 674253527, 681414300, 691030679, 698191452, 706579996, 714623643, 723269277, 731221137, 739789339, 1076188106, 748434973, 1074899911, 756386833, 764955355, 773600861, 781552721, 790121051, 798766813, 807028756, 815417492, 1076481993, 1074661324, 1074165702, 823806036, 1077325771, 832194772, 1076818893, 1077085134, 1073962952],
    [114, 100, 3, 1837056, 8668288, 18672705, 27290688, 35679360, 44067840, 52456640, 60976129, 69364929, 77753409, 84165696, 94111936, 102551184, 111307905, 117720064, 127666240, 136105552, 142896660, 152832128, 161271504, 169886740, 176451156, 187042451, 194825744, 203441236, 210005652, 220596947, 228388033, 236995732, 243560148, 254151187, 261942273, 270550228, 279998165, 285492416, 296094291, 303885441, 313552405, 321842389, 328230609, 338167809, 347106901, 355396693, 363333697, 371738116, 1073749955, 380661397, 388892821, 397339797, 403727889, 414116885, 420505169, 430442689, 437284358, 447613013, 453824018, 464012932, 470838918, 479358536, 489687559, 496002705, 504155858, 512782022, 523242055, 529321618, 539510340, 1075606466, 546336326, 556665045, 562875986, 573064900, 1076928516, 1075894278, 581437569, 588407888, 598739591, 605185040, 615385109, 621962448, 632475274, 638742152, 649071303, 655516816, 1075393543, 666029578, 672672470, 682806858, 689073672, 697838166, 707972810, 714615446, 1077241866, 722914839, 732972632, 740060248, 748169750, 756469335, 766527128, 773614744, 781635223, 791692824, 798780440, 806514376, 815189719, 825247448, 832335064, 1076463624, 1074386893, 1075195851, 1076777934, 1074955205, 1073932233, 1076299724, 1074221007],
    [106, 92, 1, 2223104, 10628225, 18893953, 27282625, 35671041, 44059713, 52579328, 60968064, 69752400, 77745344, 86109248, 94514177, 102911040, 111695568, 119663744, 128068673, 136869586, 144829632, 153234625, 160069139, 170929360, 178646673, 184962563, 195581584, 203812433, 213003267, 218517123, 229135888, 237366993, 246557827, 252071491, 262698514, 270921233, 280112195, 1073755074, 285626051, 296253074, 304606936, 313666755, 1076909059, 319452755, 329772568, 338701328, 344618643, 354938456, 363867280, 369784531, 380104344, 389033040, 396916306, 403303506, 414190609, 422868633, 428469458, 439356561, 446199381, 453635090, 464522321, 471365269, 479325337, 489688273, 498365977, 506998484, 512879641, 1075090376, 1074850756, 523531865, 532164244, 538045529, 1076432839, 548697817, 557330004, 563211481, 572028437, 582495764, 587852946, 597579351, 607792790, 613936858, 622745239, 632958486, 639102554, 1074622410, 647910935, 658124374, 664268442, 672691925, 683290326, 689434138, 698242775, 706088146, 1076731852, 714476562, 1075694533, 722865234, 1074407373, 731795023, 1076249545, 1073914830, 739642514, 1076026315, 748572175, 1075525574, 756960975, 765349519, 1077363727],
    [126, 112, 0, 427072, 10816705, 18918528, 27307200, 35695616, 44084288, 52759617, 61507152, 69258769, 77925505, 86673104, 94424721, 103329492, 111479809, 120227472, 127979089, 137014805, 145272468, 153947217, 162170384, 169922257, 179113169, 185238657, 195481175, 204278929, 210404417, 1073750978, 218672857, 229420570, 235458072, 246459995, 252085376, 262999057, 269004441, 279367383, 288295957, 294290625, 302558809, 313175765, 321695386, 327732888, 338210324, 347147476, 353010689, 361279001, 371895957, 380415578, 388419223, 396930644, 403080384, 414256212, 420130396, 430616149, 436923417, 445023232, 456199188, 461950680, 472952539, 481234069, 489596563, 1075860422, 497470999, 504278557, 514895387, 523177045, 531539539, 1074829253, 539799258, 545836632, 556838555, 565251220, 573744346, 580038344, 587918553, 596553373, 607063253, 615818267, 621981192, 629861529, 639053334, 649241626, 655535688, 663415897, 672607830, 682927323, 689090184, 697355293, 706260684, 713993949, 722939542, 733127834, 1075103752, 739298461, 747548253, 1074344903, 756494038, 766420691, 772852957, 781757964, 791979099, 798821906, 1076973508, 806669404, 815312460, 823987858, 833791066, 839961693, 848866956, 859088027, 865930834, 1074633740, 1075701705, 874319570, 883861011, 1076243402, 1076517835, 890556060, 898280604, 907333148, 915057692, 1075492813, 924110556, 931835100, 1077342147, 1076824015, 1074217934],
    [130, 116, 11, 2536640, 10759297, 18910273, 27298817, 35818496, 44076161, 52595904, 60984448, 69372992, 78130832, 86422528, 94407873, 103213586, 109349906, 119967441, 128462416, 136754304, 145156690, 151293010, 161910353, 170405584, 178697280, 187099794, 193236114, 203853329, 212348432, 221026004, 229042898, 235179218, 245796497, 254840386, 262672019, 271357588, 277408258, 288394242, 294162115, 305042965, 313003731, 319604931, 330337922, 338169363, 347387543, 352905282, 361402009, 372281026, 378310234, 388501075, 1073747970, 394848450, 403475994, 411438097, 422483669, 428664922, 436899353, 445419226, 453381265, 464295444, 470738969, 478842457, 1075339204, 487362202, 495324369, 506771159, 512551130, 520785625, 528878673, 540325399, 546236569, 556018753, 565491287, 571402329, 581184705, 590124628, 596568281, 606350337, 615421525, 1075622854, 621996618, 630623306, 638324246, 648976021, 655551178, 664177866, 671649347, 680267478, 689223195, 697092611, 705203203, 713821846, 722777755, 730646595, 738758275, 747376214, 1076937673, 756725340, 1073808387, 764209178, 772935384, 1074088903, 781497947, 792390301, 798231637, 807056924, 817555997, 823561866, 831786197, 840611548, 851110493, 857116170, 865209944, 1074370508, 874165916, 1075171338, 884665053, 890375704, 898938587, 907208714, 915541656, 1074935758, 1077306312, 923986058, 932449429, 1076013005, 940361859, 949226517, 957147290, 1076285381, 965273730, 1074736079, 1076588491],
    [122, 108, 10, 2540608, 10570753, 18410688, 26799232, 35187712, 43576384, 52880908, 60902465, 69658252, 77679809, 86280847, 94563982, 103083151, 111601356, 119622785, 128223951, 136506958, 145026255, 153701376, 161932876, 170166863, 178450126, 186969167, 195644544, 203867328, 212109839, 220392974, 228912143, 237421696, 245976256, 254454288, 262587392, 271273490, 279620240, 286189265, 296439442, 302575108, 313174608, 319874765, 329993810, 338340560, 345040525, 355159762, 361295492, 369920723, 378621461, 386852497, 395086483, 403787477, 412018193, 422899350, 431130774, 437568719, 445730453, 453570244, 462195283, 470609414, 479511631, 487673429, 495749651, 504164038, 514411584, 521201165, 529067588, 537718406, 546620431, 555183246, 1073745924, 565348950, 573893718, 579661382, 588729876, 596567633, 1074812934, 607291926, 615836694, 622118031, 630680654, 641108631, 647457806, 656074328, 666274519, 1075353541, 672616084, 680584781, 691440151, 699723478, 706397849, 715083480, 724732118, 731049673, 739952153, 748637848, 758549079, 764603913, 773506649, 782192152, 789769801, 798445268, 807061209, 1075102664, 1073816584, 815066635, 823324297, 831999572, 840623320, 848621131, 1076196361, 857173198, 865789080, 873787019, 1077261251, 882566168, 891243608, 898952907, 1077004299, 1074408459, 1076780994, 1075742666, 1074188231, 1074733066, 1076062215],
    [126, 112, 13, 2387136, 10661057, 19199169, 26790912, 35179648, 43568320, 51956800, 61107328, 69381185, 77919361, 85642831, 94661632, 102935553, 111473729, 119721488, 128250881, 136490113, 143027216, 151310018, 161664656, 168228430, 176581776, 184987341, 195219024, 204901964, 210433617, 218524752, 228773584, 235861715, 246721615, 252079312, 260492995, 270192143, 279211072, 285931025, 297053199, 302435907, 312135375, 319450642, 327611918, 338996431, 344379011, 354078351, 361393810, 369555150, 380939407, 389451468, 394983057, 403459608, 412145239, 423005708, 428625560, 439783052, 445052558, 453791448, 462081541, 473345686, 479254039, 487345752, 496563867, 504516249, 515288598, 521729563, 529951823, 537308749, 546895579, 555380309, 562474509, 571133637, 1073752004, 580449883, 588672015, 596029069, 604688005, 613338823, 622515732, 630877909, 641117782, 1076122566, 1074834438, 646630981, 656070356, 666283734, 671772370, 1076682757, 681236052, 689598101, 698125906, 705746583, 714902674, 722889935, 730123842, 739956372, 747785945, 756977178, 764046418, 772470481, 782143194, 790261269, 797898259, 807308890, 814665351, 822398466, 831575767, 840731858, 848718991, 856608327, 1075912648, 1075671048, 864472579, 873614937, 881784403, 891195034, 1076988931, 1074645961, 897896066, 907169305, 915338899, 924617746, 1074402306, 1075210242, 932105735, 1076528135, 1074185162, 1073945547, 1075541003],
    [110, 96, 13, 2600064, 10562560, 18951296, 27339968, 35728448, 44248257, 52636737, 61286096, 69414017, 78359760, 86191105, 94588561, 103228944, 111914000, 119754321, 128394832, 137080464, 144920081, 153552403, 162245712, 170086097, 178726032, 187149376, 193408596, 201804884, 212805333, 220703936, 229582421, 237480960, 246359573, 254774998, 1073750980, 262604499, 271552022, 277564951, 286075927, 296158867, 305106518, 1075867589, 311250648, 319761624, 330245781, 338661014, 1076663234, 347033305, 353316440, 363922434, 1074842563, 370380434, 380587545, 386870808, 397477058, 403934930, 414142105, 420294295, 431031362, 437489234, 447696473, 453848663, 463930963, 471043602, 478891159, 487534232, 498140290, 504991323, 512446167, 520957143, 531957342, 538676890, 546131096, 557123102, 563711707, 1074335686, 571296792, 582289118, 589008474, 597388956, 607454878, 614043163, 621227668, 629623956, 639305437, 647728858, 656109276, 664743438, 672859741, 681283098, 1074618312, 688606295, 698297998, 706414237, 714706587, 721890836, 730287124, 740240974, 748357149, 756772380, 765406926, 1075688396, 1077008398, 772222676, 780618964, 1075456973, 1076511687, 789400664, 1073911754, 798715484, 1075234761, 1074210763, 1076328399],
    [122, 108, 9, 2165953, 10554433, 18943105, 27331585, 35851392, 44240064, 52866576, 61158416, 69560336, 77794368, 86182912, 95111891, 103198416, 111744657, 119975568, 128280720, 136910353, 143068802, 153529936, 161835088, 170464849, 176754262, 185011906, 195759831, 204770321, 212408017, 221071446, 227085846, 237702743, 245707920, 254717058, 263014422, 269029078, 279645719, 287650896, 297045137, 304957654, 310972054, 321588887, 329992723, 338900119, 347376721, 355158675, 363148496, 372157634, 377949698, 388713043, 397620439, 405711874, 414387928, 419892802, 431174743, 439266370, 447563926, 1073741826, 456330776, 464729111, 472213712, 481594577, 489885336, 498166357, 507057235, 512790226, 523439704, 1073767364, 529338057, 540611603, 546344466, 555174104, 1075879877, 562892361, 573663765, 582554835, 588287570, 596446857, 607218389, 616109203, 621842066, 630001161, 641537556, 647671444, 655837208, 1075633095, 1075381257, 663817739, 674327189, 683480788, 689745625, 1074089926, 697372235, 706391636, 717034580, 722946136, 730926731, 742200468, 748334292, 756500632, 764481227, 773657621, 782020121, 791898180, 1074631691, 798823637, 807186073, 817064068, 823989397, 832351833, 842229956, 849155157, 857386004, 867395588, 875915289, 884303961, 1075172303, 1074933708, 892692633, 1076775875, 901081305, 1074441160, 1076557773, 1077359566, 1077110730],
    [114, 100, 13, 2092160, 10831041, 18967616, 27356288, 35744768, 44133568, 52653121, 61041857, 69430273, 77589504, 86328449, 94596225, 101051920, 111494145, 117829200, 128271425, 136791056, 142995152, 151383696, 161957008, 168390354, 179007059, 186641600, 195511376, 201944722, 212561555, 220195904, 229065936, 235499090, 246115859, 254406225, 263013523, 1073755074, 269053458, 279775765, 288059091, 294480917, 305088017, 313126545, 321850070, 328035989, 338291729, 346899667, 355272853, 361590357, 372196497, 380235473, 388827221, 395144917, 403435156, 414008339, 422381781, 428601044, 439305425, 447678998, 455951443, 462286551, 472844950, 481248337, 487452183, 1076915140, 498010710, 506815570, 513134105, 1076400071, 1074589640, 523700937, 531981330, 537783895, 548866633, 555314698, 562818644, 573924498, 582421001, 588869194, 596373012, 607478994, 614017049, 622423690, 632767560, 638963417, 647571673, 655978186, 666321928, 672517721, 1076693002, 683084425, 689794573, 699876552, 705556119, 1074357257, 715091470, 723069593, 731737805, 741819528, 748014745, 757034574, 765012057, 773680717, 782200462, 790571544, 798846605, 1076201413, 1074124813, 807366350, 815737560, 1075452942, 1075733452, 824126040, 1076008907, 832514712, 1075233731, 1073943494, 1075017679],
    [106, 92, 2, 2436288, 10415169, 18961601, 27184784, 35990592, 44127297, 52350672, 60904449, 67440338, 75845332, 86978259, 94293584, 102847617, 109399636, 119764052, 128921171, 136236560, 142954132, 153318548, 162475539, 169798657, 178877955, 187641491, 194964673, 201674260, 212694533, 220130433, 226823762, 237860485, 246476305, 251989650, 263026245, 271642257, 277155346, 1073754052, 288192197, 296037504, 305196753, 1076649989, 1075879811, 310988375, 321483971, 329591808, 338751057, 344542871, 353324552, 364309655, 371815555, 378744534, 386485783, 395267656, 406252567, 413758531, 420687446, 1075636166, 428429015, 437210824, 448195799, 455308308, 462630550, 470765192, 481750103, 488862932, 496184854, 1076167688, 504321104, 514772096, 521080533, 529617920, 539937984, 547040792, 556715008, 563172480, 571412117, 579818640, 590269504, 597372568, 605892121, 613372944, 621989077, 1074099138, 630150352, 638766613, 646909525, 656223961, 663835840, 672320597, 1076986828, 681389657, 689001536, 697486485, 705629205, 714533906, 1073860551, 722922578, 731590360, 1074670538, 739699858, 748367448, 1076515790, 1074960335, 756887193, 764865746, 1075239883, 1075525577, 1077365709],
    [126, 112, 12, 1838144, 10595329, 18984065, 27372737, 35761217, 44281024, 52669568, 61058112, 69340752, 77835264, 86232657, 92646481, 102895120, 111283856, 120049347, 128689668, 134851588, 144838352, 151760532, 159894676, 170632772, 176794692, 186387456, 193834645, 202092116, 210226260, 220964484, 227126404, 236719296, 244166165, 252423892, 262655555, 271296196, 277196497, 285846724, 296488530, 1073750339, 1075857412, 303017686, 311143956, 319278292, 327528081, 337382528, 347186757, 352832532, 361082385, 371986130, 380741317, 388222097, 397151890, 405907077, 413650051, 422317586, 431072773, 438815747, 447614017, 1074308101, 453881429, 465020487, 472108241, 481168577, 487435989, 498706072, 505662481, 513126025, 523644041, 532391514, 537915031, 546680521, 557198537, 565814808, 571469527, 580234825, 590752841, 1076151238, 599500442, 605023831, 613789193, 624307209, 1073813513, 632792583, 638578199, 648940673, 655339094, 666347143, 672779349, 682494977, 688893590, 699901639, 706195150, 714722325, 1075407879, 722472665, 1076734923, 730836502, 741975640, 748138126, 756665557, 764415641, 1076484040, 775661082, 781692494, 790219925, 797970009, 809215706, 815246862, 823906003, 831524377, 1075186702, 842639064, 849071699, 1074689997, 859014683, 865979414, 1077315532, 875792027, 882756694, 1074189258, 892569179, 899534038, 909346523, 916311190, 924569107, 932957843, 1074995151, 1075803074],
    [114, 100, 11, 373825, 10587201, 18975937, 27364481, 35752961, 44157456, 50705537, 59059858, 69323344, 78362321, 84225746, 94736085, 103402198, 109546710, 120305169, 128421507, 136908372, 145067541, 153733782, 159878294, 170767381, 178622101, 187288150, 193432662, 204321941, 212176469, 220842518, 226987030, 237876309, 245885655, 252032193, 260386322, 271051415, 279819477, 1073742788, 286101209, 293940818, 304605719, 310752257, 1073761221, 322121416, 329771607, 338409105, 1074308034, 347287048, 355977347, 363574865, 372452936, 379701968, 389649408, 395152921, 406007432, 413256336, 423204032, 1075900424, 428707481, 439946393, 448383512, 456758336, 462261849, 473763401, 481938072, 1076961222, 490312832, 498929161, 507103960, 512726032, 522686019, 532483785, 540526659, 546280592, 556240579, 566038153, 574081219, 580097691, 1075667977, 1076204490, 589794819, 598281876, 607635459, 613651995, 1074911235, 624495833, 632932952, 638555216, 649661529, 657451539, 663983707, 673779220, 682617491, 1075449799, 689149659, 699993113, 707783379, 714052816, 724111060, 732949075, 1074677707, 740232732, 748538394, 757042895, 765398684, 773704346, 1074179020, 782208591, 790564444, 798870234, 1076557773, 807374351, 815730396, 824035930, 832540303, 1077351439, 1075277774],
    [86, 72, 4, 2598913, 10863617, 19156033, 26864704, 35253376, 43641856, 52030656, 61326991, 69487617, 78096577, 86492751, 94873665, 103042177, 111658511, 120039553, 128208065, 134720081, 145386577, 153601743, 1073754112, 160017106, 170247297, 179203795, 185436371, 195552788, 203801793, 212568789, 220578881, 229345813, 1076911042, 235695830, 246269584, 254511765, 263089747, 271435472, 279677525, 286027286, 296978947, 304989712, 1075348355, 311447127, 322144323, 330155600, 338325137, 347310275, 355364499, 364087427, 372141587, 380102292, 387295832, 397045457, 405268180, 412461720, 422211089, 430433876, 437627416, 445664919, 454404824, 464408089, 470263825, 479219223, 487041233, 497962585, 1073793991, 503949906, 1074335689, 514739865, 520980627, 1074618309, 531517145, 537757779, 546328279, 554534931, 1075681228, 562851478, 1075178443, 1076508616, 570927249, 579628630, 1077306308, 1076015050, 587836050, 596224530, 1076815814, 1076299726, 1074222029],
    [110, 96, 11, 2468992, 10605633, 19229889, 27249792, 35638464, 44026880, 52415552, 60935169, 69323969, 77712513, 86355136, 94727169, 102880449, 111266881, 118066704, 128177868, 136670337, 143232592, 153343564, 161836097, 168152578, 176787088, 187124812, 195155073, 1073752064, 201707074, 1076391937, 210341584, 220679820, 228840588, 235261634, 245845516, 254006284, 262515712, 268816002, 279399628, 287681600, 295818241, 1076924418, 303148750, 313347789, 321255107, 328314382, 338513549, 347067988, 355454036, 361868878, 372067853, 380622484, 389008532, 395423374, 405622349, 414176788, 422562836, 431197250, 439439061, 447731412, 456117460, 464751618, 472993365, 1074848195, 480637955, 487312964, 498306242, 506547733, 514192515, 520867524, 531860610, 540102293, 547746883, 554421764, 563432979, 574074511, 579849863, 588500616, 596987475, 607628815, 613404359, 622054920, 630541971, 641183439, 646958663, 655609416, 664096467, 674737743, 680513031, 689163976, 697937425, 706432530, 1075904519, 1073824776, 713805444, 723103377, 731598546, 1074105285, 1074383877, 1074664452, 739880529, 748375634, 756764306, 765308566, 773435089, 1075210182, 782085718, 1076272075, 1075502091, 1075787722, 790474262, 1077374921, 798863062],
    [102, 88, 9, 2510976, 10653889, 18755648, 27144320, 35532800, 43921600, 52842688, 60985409, 69208589, 78008384, 86413836, 94374605, 103174144, 111316993, 119540301, 128357004, 134640273, 1073750016, 1075865601, 144706189, 153260161, 159805969, 170273488, 178688588, 184971857, 195439248, 203854540, 210137809, 220605008, 229281805, 238310030, 245770768, 254709840, 263475918, 271190547, 280007298, 288641614, 296356563, 305173058, 313553476, 321522259, 327955141, 338595984, 347361806, 355076755, 361640518, 371888205, 380662468, 388665485, 397439492, 403452549, 414225090, 420377167, 430608589, 439382660, 1076400132, 1074844676, 448015062, 453784133, 1075129410, 464531670, 472944642, 479490706, 1076711363, 489957974, 495858182, 506474582, 514756816, 521040527, 531900950, 537801350, 548417558, 556699664, 563376850, 573844118, 579744454, 590360726, 597594836, 605319762, 613954056, 1074628614, 621556229, 631149076, 638874130, 647508552, 1074387973, 656314964, 663646735, 672674440, 681480852, 688812751, 697840328, 1075714056, 706499221, 1075463113, 1073906697, 1074198474, 714887893, 723276309, 731664981, 1077359559, 1077110731],
    [98, 84, 11, 2601025, 9965633, 18354369, 26742785, 35131521, 43651072, 52039808, 61094479, 68817088, 78098561, 85594176, 94649039, 103264449, 112088592, 119814671, 128430081, 137254608, 144980623, 154120335, 1073750017, 162420368, 170267218, 178927698, 187929105, 195974736, 204451919, 212760275, 220731924, 228987410, 238523093, 245897940, 252204753, 262542034, 272077333, 279452308, 286291605, 296096402, 305369297, 313145362, 322074308, 327553733, 336073302, 347312721, 355350614, 364017220, 369496581, 381128853, 1075866562, 388504148, 394810385, 403182294, 414167247, 422459606, 431126148, 436736534, 447976081, 456013846, 464680452, 470160005, 481275919, 1076402180, 489306258, 495998679, 503845526, 515347029, 523122838, 529028241, 537268805, 1075377091, 546680850, 1076954117, 556415186, 563115029, 571846738, 581858835, 588624018, 598636115, 605401298, 615413395, 622563928, 630216215, 1074096073, 639341208, 1076200391, 646468689, 656118296, 1073862598, 663778389, 672895704, 1075197896, 680547991, 688944341, 1077302220, 1074958283, 1074716621, 697325143, 1075776458, 1074491342],
    [114, 100, 5, 2517120, 10514625, 18903041, 27291713, 35680385, 44200000, 52588544, 61403664, 69365952, 78014464, 86143104, 94779027, 103313555, 111735376, 119957568, 128333523, 136868051, 145289936, 153512128, 161887827, 170422355, 178844304, 184838673, 195442195, 203976723, 210162262, 218393169, 229652056, 235434072, 246084114, 251947665, 263468631, 271381012, 277113553, 288896708, 294154968, 302436886, 313412245, 321926360, 327709336, 338490068, 346966741, 1073750979, 355480728, 361263640, 369545878, 380521045, 389035032, 397210196, 403466448, 414725700, 419877590, 428894938, 439891588, 447410834, 456018453, 1075859524, 465056772, 472707732, 479226522, 487223942, 495326939, 506131154, 512518160, 520778246, 528881307, 539685458, 546072656, 554332870, 562435611, 1074837445, 571535964, 579889690, 587887174, 595990107, 605057609, 613871763, 621832794, 1077200902, 1074344898, 632567319, 638611977, 647426131, 655124624, 666121879, 672166601, 680587932, 691287767, 697332361, 706146515, 1076972553, 716052121, 722530844, 1074627530, 732829209, 740225758, 1073858503, 749606489, 757002846, 1074143179, 766383833, 772862684, 781588125, 790032403, 1075731400, 798365213, 1075489740, 807334430, 815142493, 824111774, 1076553677, 831919837, 1076309966, 1076844495],
    [126, 112, 13, 1962113, 10506240, 18895040, 27283520, 35672192, 44191937, 52580353, 60822224, 69357697, 77459457, 86134849, 92558034, 102765136, 111538769, 120224404, 127931024, 136704529, 145390292, 153096720, 161870545, 170555988, 178926274, 186511425, 193352341, 204110356, 212480514, 220065985, 226906709, 235426518, 246035074, 254145169, 260461077, 1073754242, 268972246, 280481858, 285627093, 294146646, 302526550, 314036226, 1076913091, 321531970, 330813634, 336089750, 344469654, 355979394, 1075882948, 361255446, 369635350, 380629077, 389438167, 394940631, 405680338, 414183445, 422992535, 428494999, 439743059, 448158231, 453660695, 464400978, 470044754, 481686227, 487477913, 498489943, 503992407, 514732562, 520376338, 532017683, 540695046, 548287122, 554717767, 562319506, 571757083, 582479875, 588141273, 599546588, 605302811, 613700315, 623898837, 632969862, 638988441, 647385738, 657977475, 1076413381, 666524358, 672412315, 680546951, 689197211, 699396245, 705581593, 717249178, 722874393, 731271882, 739529307, 750252227, 758798918, 764817625, 773214794, 1073818630, 783676051, 789467737, 1076709320, 800872988, 806760537, 815157770, 825749571, 1074106313, 834427484, 1074648074, 840183899, 848318983, 857076376, 868244058, 873738459, 881873607, 890630744, 901536412, 1075187719, 907407896, 1074948043, 918575642, 924185304, 935353050, 1076273101, 1075764174, 1075514316, 1074493391],
    [114, 100, 0, 428032, 10293376, 18681920, 25593984, 33870545, 44347601, 52236480, 60984002, 67424849, 77901905, 85790720, 94538370, 101118483, 111751233, 119704066, 126145041, 136622097, 145437200, 153258562, 1073752066, 159838867, 168200256, 178860225, 187748948, 195342993, 201754816, 212414593, 218419345, 229323344, 237800068, 243724883, 254489296, 262965956, 269267653, 277279443, 288043664, 296650949, 302953174, 313578004, 321466369, 330336470, 1076381635, 338744020, 344920597, 355240516, 361542149, 372298388, 378483287, 388794884, 1074049028, 397865091, 403747464, 412267081, 420426391, 430868485, 437170774, 448196675, 454078984, 462598665, 470749781, 481331286, 487371333, 498528451, 504541897, 512692885, 523143237, 529445398, 540471299, 546484873, 556828694, 1076939785, 562868869, 574157325, 579801813, 590252165, 1074600965, 596554390, 607711821, 615549078, 624489165, 630141655, 638879824, 1075668938, 649654925, 655307287, 664045712, 1076210701, 672977496, 680571464, 689746639, 697731265, 706531992, 714126024, 723300879, 731154448, 1076754380, 1077286920, 740086488, 748466767, 756451393, 765252120, 773632655, 781617153, 1075464207, 790549202, 798394497, 1074435019, 807326226, 815040720, 1074976710, 824103506, 1075258318, 832492178, 1076052935],
    [98, 84, 10, 2553024, 10227777, 19175617, 27299841, 35688513, 44077249, 52465793, 61273088, 69507073, 77336577, 86438976, 94672961, 102502529, 111998609, 119812160, 128227457, 137164497, 145406674, 152834241, 162330193, 170143744, 178960978, 187495953, 195309760, 204126738, 212086912, 220656768, 229423827, 238089813, 246069906, 254554704, 262803990, 271751682, 280294979, 288683523, 296532499, 304886480, 313849475, 321698451, 330052112, 338301526, 347403971, 355252819, 1073753091, 362083991, 372415106, 380383888, 387224152, 395638295, 405410454, 414750808, 420778520, 429192791, 439916568, 447484115, 454595225, 462747351, 473086105, 481038419, 489855554, 497815571, 504664728, 515414168, 522981523, 1076643785, 529830616, 1074042822, 540580056, 546443924, 555258393, 1075114951, 565360665, 571609684, 580424281, 590526553, 596775636, 605590233, 615692505, 621941268, 632354517, 640291542, 649131541, 1076958152, 657520277, 1074880460, 666016450, 1075676110, 1073865730, 673109594, 1076236234, 1074689999, 1077322701, 681498266, 1076022212, 689886746, 1074469829, 1075538891, 698275546],
    [114, 100, 10, 2158592, 10547264, 18936000, 27324544, 35844225, 44232897, 52742672, 61296656, 69907472, 77787201, 86175745, 94685776, 103239760, 111851216, 120239760, 128405712, 136891090, 142930626, 153793616, 161960080, 170445458, 176484930, 185160211, 195611218, 204650070, 210326227, 220776978, 226816514, 238065219, 243880531, 254068880, 263370262, 269046419, 280020994, 285799000, 296924822, 304400592, 313479256, 319091330, 330479318, 338741378, 347165204, 1073747970, 355505667, 363907138, 372593286, 380671619, 389073090, 397759174, 403239448, 414758615, 423029393, 430919704, 436794072, 447780547, 456583761, 464867846, 1075339398, 1075885059, 470348440, 481867287, 490138129, 498028696, 507033175, 515304145, 523587654, 532199063, 538495705, 548360408, 1077203909, 555136597, 563278346, 572049945, 582046420, 588575305, 1074857927, 597079701, 605221578, 613993113, 623989396, 630518409, 1074086852, 1073846216, 639022613, 647164490, 655936089, 665932372, 672461321, 680965845, 689107594, 698052633, 706406487, 714404553, 1075169289, 1074400266, 723301914, 731607193, 739961047, 748467930, 756773081, 765126679, 773648974, 782022298, 790327385, 798681239, 1074688971, 807203470, 815576666, 1077061580, 823980750, 832369166, 1076288526, 1075785677, 1076849615],
    [110, 96, 9, 2553857, 10539008, 18927808, 27316352, 35704896, 44462608, 52885633, 61256337, 69628624, 78051521, 86422097, 94818836, 103182992, 111605825, 119976465, 128373332, 136737360, 145545232, 153531089, 161927892, 170685139, 179099792, 187093652, 196235779, 204265680, 212628051, 221042768, 227062293, 235458581, 246567555, 254859858, 260747798, 269144086, 279736979, 288553091, 296661637, 304902675, 313841684, 319476438, 330216133, 338842179, 1073746882, 347273283, 355381765, 364008131, 372439235, 1074812931, 378196566, 388936261, 395072151, 406116500, 1075359749, 412398233, 420401305, 428626455, 439409298, 445174421, 454087322, 462074070, 470733401, 478958295, 490002644, 495637142, 504418842, 512405590, 521065177, 529289815, 1076945860, 540072658, 545837781, 554750682, 563654874, 571396633, 580022939, 590665812, 596169301, 605082202, 613986394, 622228056, 632485891, 638890009, 647131739, 657512978, 663269461, 672297691, 681368092, 689483802, 697463323, 706533980, 713601173, 722891480, 731699932, 1075906505, 1074086858, 739815578, 748057240, 756865692, 1073848262, 764719193, 773222936, 781496537, 1075702727, 789098709, 1076498380, 797618326, 1074687944, 1076795342, 1075235787, 1074477005, 1077372879],
    [142, 128, 9, 2426880, 10842304, 19239105, 26816705, 35205121, 43593793, 51982465, 60502016, 68890816, 77279360, 86339584, 94701760, 103256780, 110833728, 119747214, 128667790, 136644736, 145199628, 153432721, 161690190, 170610766, 178587712, 187142732, 195375697, 203633358, 210055746, 220942542, 229085836, 237709378, 245707281, 253964814, 260387458, 271273998, 279652482, 287674369, 296039121, 302330562, 312832064, 321595586, 329617473, 335884802, 346386560, 355149826, 363171969, 1073745922, 369570371, 378245651, 386730573, 397234770, 403124739, 411930830, 420285069, 430789266, 436810436, 447689239, 454101015, 462394070, 472732370, 478622403, 489763545, 496175631, 504468053, 515330648, 520696324, 529634005, 537733337, 548229650, 554119811, 563188373, 574050968, 580200529, 1074820099, 587805252, 596455943, 607203993, 613495302, 621619353, 632771288, 638554710, 646525572, 657404503, 663827078, 671847123, 683102744, 689252497, 1077189636, 699478553, 706171476, 714183189, 722274829, 730673735, 741290647, 748139163, 756091031, 764891860, 772616839, 781693467, 790057620, 798304273, 1075630021, 1074604037, 806195342, 815223316, 822938317, 831337159, 841954007, 848007763, 857305744, 865142999, 1076447239, 1074375687, 873173651, 882471440, 890440271, 1076742089, 1074143241, 898708166, 909193817, 916026064, 923635726, 932383439, 940651078, 949465691, 957163609, 966742682, 1075991558, 1075223496, 974194775, 983519770, 990876182, 999133262, 1008685658, 1016408273, 1075508170, 1024963291, 1032661017, 1042240218, 1050243664, 1058212495, 1066373782, 1077085131, 1073964043],
    [126, 112, 13, 1799169, 10530945, 18419776, 26808512, 35196928, 43585664, 52771532, 60862465, 68908097, 77533903, 86325836, 94442126, 102855822, 111194177, 119476879, 128793104, 136385038, 144748737, 153441296, 161551054, 170736336, 178353166, 187216589, 195105358, 204290704, 212382285, 220550288, 229184084, 237845072, 245936781, 254104656, 262869525, 270875276, 279491085, 287659216, 296293076, 304429580, 312414799, 320959694, 327979730, 1073752002, 338236052, 347019791, 354357263, 363820180, 369922706, 380310101, 388962511, 397374548, 403477074, 413864661, 422516815, 428773911, 439317716, 445321797, 456071311, 464196245, 473265301, 479236761, 489230868, 498146003, 506426388, 512791065, 523311699, 1076120515, 531985493, 538350296, 545985029, 556866195, 563155527, 572617806, 580293272, 587928261, 598809107, 605098631, 1074304964, 1075111940, 614109722, 624260309, 629871237, 638925006, 647664218, 657814549, 1076429829, 664476369, 672830170, 681276545, 689256526, 697995930, 706442433, 714412617, 722811022, 731076246, 739283545, 747966985, 756890203, 1074086854, 764630742, 772838105, 781259463, 789910217, 798693969, 806573654, 814650007, 823202311, 832387611, 840128022, 848728664, 1073844231, 1074913226, 1075719175, 1076785162, 857553563, 1077060552, 865505816, 873796233, 882580113, 890016274, 1076022281, 899496667, 906924759, 915748878, 923701847, 1074731979, 1075541003, 932911633],
    [126, 112, 5, 2347136, 10579969, 18968705, 27357377, 35745857, 44265536, 52654272, 61042688, 69455872, 77820032, 84219602, 94980817, 101019858, 111636689, 119787712, 128923155, 136923793, 142963218, 153579665, 161730624, 171120194, 178866769, 187134033, 193426069, 204460688, 212809427, 220809745, 229077009, 235369045, 246403664, 255006338, 260534997, 271569616, 277574148, 288306835, 294089237, 305123856, 1073754690, 311128772, 322114562, 327512722, 336187411, 344945350, 353071684, 363804243, 370242119, 378130515, 386626180, 397612226, 403786326, 411398738, 420073683, 1076905988, 428151954, 437340822, 445739655, 453628051, 461706258, 471157272, 479294151, 487322260, 1074299845, 495260754, 504449750, 512848391, 521130649, 1073798151, 529732804, 538003990, 546427546, 555037703, 563694171, 571208276, 580195461, 588860123, 596628185, 605492373, 614156892, 621925082, 630527173, 639191579, 647328331, 655348249, 663950468, 672877276, 680882891, 688902745, 697766933, 706038488, 714437259, 722203156, 1075647432, 730821126, 739710165, 747981464, 756380171, 764539543, 1074878475, 772764230, 781390916, 789924440, 798085722, 806318726, 815076357, 823872028, 831640090, 1075416070, 1074644940, 840250439, 848906907, 856814295, 865408069, 874203804, 881979991, 890704981, 898757143, 1074146249, 907219972, 915141332, 924136583, 1076520910, 1076277199, 932525255, 1076819907, 1077355466, 1076058061],
    [106, 92, 3, 2551873, 8747137, 18960384, 27349056, 35737792, 44126336, 52507152, 59078721, 69660801, 78205650, 86061776, 92887761, 103215105, 111759890, 119616144, 126442129, 136769729, 144781904, 153801364, 159996433, 170578516, 176773713, 185012821, 193679445, 204132884, 210073601, 218567189, 227233813, 237687508, 243628225, 252252886, 260788949, 271143506, 279900224, 286226560, 1073744835, 294064341, 303125079, 313086610, 319780864, 330232000, 336138774, 347009024, 353335360, 361173653, 369840277, 380563584, 386889920, 1074283461, 1073783750, 1075899330, 394859094, 405860358, 414407187, 420024982, 431026310, 439573075, 448205402, 456192198, 464739027, 1076434888, 473371290, 481357894, 489904787, 498536986, 504451735, 515201234, 521326675, 532091610, 538006231, 548755602, 554881171, 563294811, 572084315, 582309970, 588435475, 596849179, 605638683, 613503511, 624252946, 630378707, 638792411, 647581915, 655938201, 664500888, 672608407, 681104089, 689666584, 697774295, 706302619, 714658393, 723221208, 1075139530, 731066523, 739824153, 748386904, 756494423, 1074890695, 764882967, 1074131915, 1077030861, 1076779983, 1075492804, 1077338060, 1075783630, 1076318153],
    [114, 100, 12, 2216064, 10358785, 18985025, 27373697, 35762177, 44150977, 52670464, 61059264, 69447744, 77713600, 85856449, 94613632, 102879232, 111022209, 120031955, 128045120, 136187969, 145730070, 153997909, 162009617, 170896086, 179163861, 187175569, 196061846, 203952849, 212595216, 221227606, 229503703, 237507153, 246254296, 252326610, 262926928, 271419928, 277492242, 288092880, 296192659, 305001111, 311038168, 321751640, 327807507, 336335443, 346523731, 355324437, 361378450, 1073753027, 372083352, 378138707, 386535576, 397912604, 405664343, 411710034, 422021139, 428847817, 439210645, 445255768, 1076388802, 456632988, 462402057, 470552595, 481030800, 490187484, 495956553, 506327575, 512495763, 523741788, 529511049, 537661651, 545910995, 1075874825, 1074582472, 555461211, 562688147, 571084824, 580487828, 588763154, 597307933, 606054937, 613929106, 622473949, 630958747, 639480397, 647483602, 656028317, 1074858955, 664775321, 673034893, 681037906, 689582685, 1074360266, 1076725701, 698331854, 706317012, 714977805, 723374810, 1074128836, 1076238284, 731886094, 740272729, 748532429, 756929050, 1075206157, 765440654, 773425748, 782095002, 790606414, 798993113, 807260762, 1075485710, 1075758022, 815507995, 823757332, 1073952711, 832285403, 1077375951],
    [114, 100, 6, 2044096, 8755265, 18740353, 27365377, 35754113, 44142785, 52531265, 61051072, 69439552, 77828096, 85930112, 92781136, 102626305, 111382656, 117772883, 126335504, 136180929, 145592853, 151360212, 159715987, 168278736, 178123841, 187536085, 193434262, 201659091, 210221712, 220845714, 229479061, 235377366, 245610710, 253883392, 260379155, 271422037, 277320214, 287553558, 295826496, 304033856, 312719510, 320811008, 329897554, 338278612, 347017745, 355063506, 361076737, 372445377, 380229138, 386241172, 396998804, 404878528, 414396565, 419926614, 430159958, 438432896, 447950869, 453351553, 464720001, 472380437, 481923608, 486904340, 497661972, 506401361, 514323605, 520458836, 531216468, 539751448, 548605953, 1073749957, 557421208, 565121681, 570792129, 581432405, 590975704, 597007057, 606598357, 615723221, 624530008, 630560913, 640414872, 649277525, 655856138, 665696776, 674173137, 682357976, 689410634, 699871301, 706058257, 715912280, 1075595207, 722965130, 732805704, 741544001, 1074048964, 748131018, 757971592, 766980101, 1076674570, 774748872, 783757445, 1073817608, 792146117, 798333009, 806818519, 815206935, 1076454338, 823595671, 1075951558, 1077269454, 1074934729, 831984215, 1077045187, 1076267980, 1074452431, 1075253195, 1074748365],
    [118, 104, 10, 2470912, 10768384, 18477057, 26865729, 35254465, 43643009, 52162688, 60551360, 68939776, 78139919, 86619151, 94105664, 102757008, 111694415, 120174223, 128436882, 136442002, 144700112, 151491792, 162025615, 169865744, 176657552, 186929344, 195938901, 203420240, 1073754112, 212448335, 220746447, 229493461, 235270742, 243766352, 254038080, 263047829, 268825302, 279203968, 287945935, 296602133, 305549912, 310875152, 322327256, 330413588, 336194074, 344453636, 355881624, 363968148, 372623963, 378008132, 389435928, 397522644, 406178331, 411562692, 422688340, 431771734, 439732955, 445117060, 456937686, 463844480, 1076910018, 473287323, 1075087364, 478540310, 490491926, 497398848, 503966298, 515273233, 522564800, 532050641, 540391059, 545909402, 554037910, 1074329541, 565989526, 573945363, 579463898, 590770833, 599111251, 606587602, 614592722, 624325201, 632665811, 638957271, 647524560, 1077224387, 656919122, 664924242, 673027676, 681078928, 1075933127, 690473490, 698478610, 1076728777, 705688075, 714454551, 723284633, 1074913222, 731630109, 739242635, 748525276, 756576272, 765184669, 772797131, 782079644, 790393433, 798739165, 806351435, 815633948, 823947993, 1075708874, 1073895435, 1075488712, 832293469, 840283735, 849113625, 857061015, 865628240, 1076285388, 1074726861, 1074228174],
    [130, 116, 11, 2314432, 10858625, 18862273, 27250689, 35639361, 44028033, 52646016, 61583884, 69718670, 77811776, 86749900, 94370447, 103272974, 111366144, 120304268, 128055889, 137065042, 145470028, 1073752064, 153221777, 1076391937, 162230802, 170242113, 178518739, 187396818, 195408065, 203684371, 212324942, 221212750, 228962305, 236976719, 243651092, 254268110, 263442965, 269201428, 280064021, 287308303, 293982868, 302502614, 311144596, 321614482, 329251535, 335925844, 347329109, 355692758, 361476180, 371325649, 380883669, 389132813, 397504725, 403034836, 412080784, 419943062, 431190166, 436973780, 446822929, 453890564, 464630413, 473002069, 481810436, 489796301, 498036878, 1076921283, 505674323, 512610884, 523350605, 531591374, 538170072, 548919364, 555078234, 562549334, 573796438, 580104337, 589560467, 597021402, 605270097, 615477262, 624163417, 630575642, 640930453, 647606362, 657551509, 663999000, 1073800130, 674495193, 679989782, 691236886, 698069016, 705942168, 716438041, 722326212, 731099153, 740119127, 747885144, 758634692, 764269188, 773566552, 782070299, 1075909636, 792189060, 798601434, 807228055, 817101465, 823775814, 832155674, 840790747, 848288336, 857330182, 865456794, 873705681, 882725399, 890231504, 899273414, 907653274, 916288091, 923785744, 932827782, 941338840, 949834455, 1075135494, 1074107335, 958115992, 966619803, 1074915272, 1076246473, 1077300165, 1074433029, 1074715594, 1075518474, 1075802059],
    [126, 112, 12, 2397376, 10368193, 18756609, 27145281, 35533953, 44053696, 52442176, 61232780, 69219456, 78157324, 85996544, 92550798, 103569101, 111711372, 117716494, 128734797, 136877644, 142882382, 153900557, 162043596, 1073750016, 168038031, 1075865601, 176436942, 187455117, 195335168, 201592527, 212497614, 220501056, 226758223, 237909649, 246051854, 254055552, 263466129, 268842515, 279852753, 287995022, 294556673, 305409233, 310785619, 321795601, 329937998, 336499777, 347352081, 352728723, 363738705, 371610700, 378442881, 389295185, 394802836, 405165260, 411997377, 420097680, 428357332, 438719500, 445813905, 453652048, 461780691, 470701586, 479368273, 487206608, 495466068, 503985813, 512644754, 521311249, 529149456, 537802370, 545928917, 554587730, 563516950, 570691087, 579745346, 587871829, 596530898, 605460182, 612906516, 621426197, 630477845, 639276739, 646854338, 655373892, 664425683, 672831107, 680408578, 689059397, 697710214, 706368531, 714774019, 1076403202, 722613893, 731264582, 740054228, 748328515, 1075637251, 756168389, 764819142, 773608468, 781620886, 789722629, 798373382, 807163028, 815175254, 1076692997, 1074351110, 823146180, 831804629, 840078545, 848965271, 856700548, 865358997, 874130967, 881866244, 891049044, 1074632708, 899296855, 907301973, 916074199, 1075439559, 924472467, 932861011, 1076237257, 1074942985, 1075217354, 1073923082, 1074214856, 1077375947],
    [98, 84, 12, 1578113, 9966593, 18355393, 26743873, 35263680, 43652096, 52926159, 60429440, 68817984, 78271184, 86480527, 95048336, 102776465, 111646287, 119412371, 128610449, 136330833, 145200655, 1073750017, 152966867, 162164817, 169885201, 179147923, 186521171, 195719185, 203439825, 212702291, 1075858370, 220075539, 229273809, 237868051, 245907095, 254431824, 263296600, 270933657, 280515154, 288199891, 296492634, 305680914, 311539227, 321404631, 329929232, 336705179, 346570327, 356012690, 361870939, 371736087, 381178578, 387036891, 397570710, 405902872, 1074302915, 411857429, 422680216, 431125206, 439457496, 447094297, 453800597, 465024145, 472260313, 478966485, 490190033, 1074585540, 497426009, 1075649477, 506622486, 515355729, 520909397, 532132881, 1075402695, 539762202, 548565590, 555063006, 564928154, 572019229, 580228766, 590094042, 597185181, 605394462, 1075151817, 1073858507, 613962333, 622835356, 630739677, 639612636, 647909972, 1074145222, 655726174, 1076253640, 664687124, 673166876, 1074966478, 681464468, 689944156, 1076819914, 698241748, 1077357516, 1076589517],
    [94, 80, 1, 281664, 8705217, 18904192, 27292672, 35681472, 44069952, 52589697, 60978369, 69341840, 77755393, 84202625, 94916112, 102921281, 111284240, 117756993, 128470608, 136450768, 142922753, 153635984, 161615952, 168482518, 178801872, 184824022, 193648214, 201879249, 209989718, 218813974, 227044945, 235287187, 243979926, 252210705, 260321302, 268717056, 279761936, 285487254, 294546965, 304927888, 310660288, 321705168, 328101525, 338482256, 344339027, 355923543, 360991872, 1073742787, 369504979, 381089303, 386821717, 394670611, 406255319, 411594385, 420902407, 428880536, 439407680, 445542101, 454456967, 462435032, 473364119, 479751890, 488011335, 495850009, 506516672, 513177287, 521155096, 531682432, 1073760263, 538472082, 547124876, 556848128, 563637778, 572315220, 579875416, 589092500, 597192274, 605869588, 1074307014, 1075640261, 613290649, 622622220, 631035604, 1077219273, 638456537, 647788108, 1074621380, 655233625, 664565452, 1076467724, 1075439567, 1076244427, 1076778958, 1075229634, 1077076936, 1076040650, 1075005389],
    [106, 92, 12, 1997952, 10482880, 18896001, 27284481, 35673153, 44061889, 52581504, 60970048, 69351056, 77747392, 85980160, 94272704, 102913024, 111294032, 119438400, 127923328, 136992338, 144848400, 152992768, 161863363, 170014416, 178640387, 186932948, 195171972, 203806339, 212237829, 220337860, 228972099, 1073748164, 1075341315, 237655570, 245502980, 254014546, 262700757, 268850389, 279057476, 287568914, 296254997, 302404629, 313153170, 322582097, 329512082, 1076399042, 338198165, 344347797, 356136465, 362804288, 371752533, 377902165, 389691089, 397530838, 405175877, 414856849, 422696470, 430341765, 437016201, 447484930, 456250966, 1074327045, 463895749, 472536786, 481039554, 487347785, 497284306, 506224282, 514593858, 523359894, 530865812, 537679561, 548148354, 555079257, 564420116, 571627021, 579475027, 588633625, 598498842, 605181645, 613029523, 622188249, 632053338, 638195411, 647354009, 1076691915, 656694868, 663901837, 671749651, 682385114, 688674313, 697308887, 1073828873, 705844813, 714085911, 1075151885, 722605592, 730994392, 739251799, 1074128844, 1076246471, 747771544, 1077302222, 756160088, 1074963400, 764417687, 1076027338, 1075777487, 1074754502],
    [122, 108, 13, 2403328, 10949824, 18920577, 27309249, 35697729, 44086273, 52892672, 61123648, 67557074, 75805906, 86289536, 95098385, 101242388, 109491220, 119844032, 129046099, 134796948, 143045780, 154046032, 162600595, 168351316, 176600148, 187600592, 196155091, 201905876, 210154708, 221165270, 227063509, 238202003, 246748373, 1073750978, 252360195, 262853845, 268744210, 279885462, 285783573, 296652432, 305468437, 310826002, 319075922, 327726741, 338865683, 347411605, 352769106, 361019026, 369669717, 380808275, 389354581, 394712210, 403486406, 412005895, 422646803, 431140051, 439014485, 445429318, 453948999, 464424464, 472585937, 478852803, 489346197, 495892103, 506377750, 514266240, 521186961, 529184387, 539677717, 546223815, 1075867588, 557519952, 563129937, 1076664327, 571929622, 579646982, 591074320, 596937729, 605214423, 613715073, 623580305, 1075375045, 630642392, 640595542, 648746065, 655920857, 664204374, 674960528, 680823873, 689100375, 698815552, 706252313, 713733699, 722924694, 731428557, 742069456, 748195417, 1076431875, 756471448, 764982925, 773534785, 781749913, 1074623434, 790033622, 797750918, 806925837, 815477889, 823430337, 1076996044, 1076217800, 1074137094, 831706775, 840480333, 849032385, 856730833, 1074420749, 865261079, 874198017, 881896465, 890689112, 1075741643, 899077656, 1073927113, 1074993103, 1075279822],
    [114, 100, 11, 2281473, 10523840, 18912384, 27300864, 35689536, 44209153, 52597953, 60986497, 69390465, 77763649, 86154833, 94910164, 103191633, 109352466, 120115218, 128491219, 136853012, 145135249, 151295570, 162058322, 170434067, 178796116, 187078353, 193238674, 204001426, 212377235, 220206741, 229021201, 235181778, 245944530, 254320211, 262149717, 270716993, 278927061, 287480977, 295882945, 1073748931, 302552665, 312481301, 321035281, 330486288, 337812689, 346568340, 355652176, 361272857, 369933401, 380818128, 1075334082, 1074308036, 386438809, 395099289, 405983888, 411604697, 420265177, 431157910, 437042201, 447935062, 453785096, 462339800, 473101014, 1075893191, 478951048, 489854684, 495894104, 506655254, 515650780, 521059864, 529846811, 540816924, 548574236, 554614424, 563648157, 571790043, 579614280, 590517852, 596950749, 605590749, 613732955, 1074863624, 624702556, 632460956, 639024841, 647534109, 655676059, 666645660, 672448093, 681088093, 1075660741, 689631767, 697177675, 706001949, 714789594, 722343435, 731299337, 739963479, 1074103238, 747509451, 756465289, 765121114, 1073859851, 1074665420, 772551880, 781499549, 790295255, 797840523, 806796873, 815452698, 1075209225, 1076278221, 823849623, 1077082058, 832230042, 1077357518, 1076588495],
    [118, 104, 1, 357569, 10153153, 18936896, 27325632, 35714048, 44102784, 52489744, 59077761, 69505746, 75822786, 86044304, 94590146, 103322323, 111736019, 117765762, 127987280, 136533122, 145422019, 153653843, 162067539, 168097346, 178319056, 186864706, 195596947, 204010643, 210040322, 220515844, 228807682, 1073747970, 237539859, 245953555, 252245701, 262886595, 270847620, 279753222, 286061574, 294188613, 302740672, 312790596, 319460052, 327742981, 336294976, 346345156, 1075335172, 355242709, 361559622, 369686149, 380292101, 386626688, 1074825221, 397080067, 405581894, 411891398, 420673046, 430623941, 439448598, 447411779, 453677588, 462616214, 472566917, 481391766, 489354883, 497857158, 504165510, 512947926, 522898501, 531723478, 1074315267, 1073814534, 539791957, 546502230, 556889174, 563801153, 571118164, 581653571, 588966913, 598512149, 606819331, 614132865, 1075664839, 621449876, 631985283, 638643219, 648843925, 656209496, 665898072, 671446081, 681873938, 688616448, 697363603, 707039890, 714929880, 724618456, 730166273, 740594258, 748484248, 758172824, 764507665, 1075154890, 774680774, 782038552, 791727128, 798062225, 807318167, 814839505, 823192659, 832483927, 840005201, 848358611, 1074656204, 857649687, 1077029837, 866038487, 1076519881, 1076017102, 1077340107, 1076309960, 1076840399],
    [110, 96, 7, 1899521, 10662977, 19158209, 27317248, 35705984, 44094528, 52483264, 61002817, 69391361, 77780097, 86179408, 94663760, 102937729, 111334593, 119733904, 128349713, 136492225, 144899600, 153515729, 161657857, 170065616, 178681425, 184981015, 195624467, 203715600, 212907670, 220790483, 229406420, 1073746882, 238073558, 245956179, 254047376, 263239254, 270335105, 279738004, 288405014, 296287891, 304510609, 310810327, 320666817, 330069524, 1074807748, 335976087, 344905241, 354221121, 363624020, 370193433, 378459801, 386858522, 396653776, 403747993, 412014169, 422597785, 428801626, 1073780678, 437302361, 445568729, 456152281, 462356186, 1075108809, 1075392451, 470988508, 481219804, 487521946, 498226709, 504411353, 513070732, 523260953, 529858130, 537302615, 546625036, 555024082, 564417665, 572298907, 580179660, 588578322, 597971969, 1076716490, 605853403, 613733964, 623924313, 630521490, 1075938316, 638760476, 648991772, 656071708, 665080897, 672315036, 682546332, 689626268, 699553429, 706655832, 716101212, 723180636, 733107925, 1074121678, 739423324, 748346588, 758273621, 1074407371, 1076261832, 765236763, 773764824, 1077055437, 1074719695, 1076574149, 782153240, 790541976, 798791259, 1077370823],
    [138, 124, 11, 2462912, 10564673, 18953409, 27341953, 35730433, 44250240, 52638720, 61027520, 69834256, 77804608, 86445585, 92755667, 103233106, 109393107, 120166096, 128789586, 134698515, 145176082, 151335955, 162109008, 168244930, 179121170, 187512468, 193549845, 203896530, 210318357, 220829328, 229453010, 237843988, 245839506, 254121088, 260789849, 269169753, 279784594, 288175700, 296064000, 304549585, 313341652, 321229888, 327898777, 336278681, 346492561, 355701777, 363933402, 372225044, 378230297, 386610201, 397487642, 406033553, 1073747907, 412169925, 422653594, 431199441, 437335685, 445339353, 456207962, 462107865, 472888468, 478623362, 489098833, 495539925, 503919829, 515085393, 520566274, 529870487, 537351827, 545600659, 556774612, 562509378, 574295560, 580073052, 590435420, 598717524, 1075082182, 1076927490, 607850120, 613627420, 623989788, 632534619, 641404616, 647182044, 657544412, 663303829, 674477595, 683347528, 689125020, 699487388, 705246805, 716420827, 1075630088, 1074857927, 722931286, 731330078, 738808981, 749975195, 756747291, 764884702, 772363349, 780482131, 790082753, 798045765, 806817494, 815216222, 823481374, 1074089924, 832025729, 839988741, 849022107, 857159326, 865424542, 873968705, 1074628613, 882576603, 890590302, 899134465, 907742299, 915756254, 924817112, 932523543, 941061725, 949982872, 1074392012, 957689431, 966227485, 975148568, 1076501455, 1075471310, 982978070, 991393501, 1000314456, 1076003789, 1073932234, 1008144022, 1016559261, 1076312011, 1024798423, 1032279123, 1077374921],
    [126, 112, 12, 2667713, 10556480, 18945024, 27333760, 35722432, 44241921, 52630593, 60898896, 69407937, 78164993, 86185089, 94453392, 103330881, 109531842, 119619280, 128759379, 137172500, 143086082, 153173520, 162313747, 168391172, 179256849, 187479763, 193819224, 201790552, 212811345, 221034131, 227373784, 235345112, 246365905, 254325889, 260928024, 268899352, 279920273, 286037717, 294196935, 302871192, 310842520, 319495826, 327980629, 336402073, 345198791, 355931802, 361438802, 372683930, 378761369, 389486106, 394993362, 406238234, 411899609, 420827675, 428807195, 436936210, 445421077, 453842521, 462647513, 473372250, 479010454, 490124378, 1073745861, 495523335, 504174105, 512970759, 523704026, 529473175, 540456154, 545878724, 554637019, 563027671, 574273180, 580211355, 588190875, 596581911, 1074550723, 607827676, 615323284, 622154331, 630133851, 638393878, 649770524, 657266260, 664490697, 672480340, 683325020, 688461383, 699209428, 705262148, 714423508, 722245269, 1075093961, 1075894532, 730404487, 739987465, 747977876, 756979357, 1075381255, 763843138, 772611670, 782145053, 1074088194, 789794951, 798955085, 806166230, 815699549, 823357465, 832509581, 840252436, 1074365384, 849254109, 1073864651, 856903751, 866064077, 873406039, 881422468, 891229709, 1075712013, 899371081, 1074948044, 906449026, 915632217, 924143835, 932925577, 1076279246, 1077342159, 1076833226, 1076589510],
    [126, 112, 9, 390209, 10056768, 18445440, 26833920, 35222720, 42333377, 52761102, 60650510, 69170703, 75986640, 84276353, 94704206, 102593614, 111113935, 117929552, 126219265, 136786000, 145051345, 152925838, 161445455, 168261136, 178771468, 187117584, 195382929, 203257550, 211777167, 218592912, 229103244, 235501060, 245838032, 254103121, 262633107, 269481024, 279253134, 287657489, 296187603, 303035520, 312807630, 321744532, 329766604, 338759759, 346910292, 353367040, 363278480, 372076244, 378533056, 389091471, 397241876, 405263948, 414257359, 422016531, 429084373, 438957072, 447811599, 454258198, 464122960, 473239763, 480736851, 489901591, 1073743813, 1074028549, 497677456, 503936708, 515182739, 523456151, 531231952, 538136149, 548737043, 554948109, 563301909, 573902931, 580114061, 588591640, 598953687, 604862023, 613676690, 622146264, 632507991, 638547464, 647230994, 655700632, 663965333, 672102024, 680777293, 688486020, 698175001, 706032216, 713913991, 722728530, 1075886022, 730428996, 740118105, 747468295, 756250249, 764663501, 1077202948, 1074863042, 773158410, 782061209, 789411527, 798193353, 806614738, 1075408903, 815101578, 824004313, 831485640, 840136265, 848819406, 857044554, 865300118, 873428552, 882079241, 890762382, 1076988937, 1074650120, 1075718153, 898987722, 907243094, 915928142, 1076515850, 924020438, 932705294, 1075219403, 1074457611, 1076822979, 1073964035],
    [114, 100, 0, 2186240, 10679296, 18437185, 26825857, 35214529, 43602945, 52122624, 60511424, 68899904, 77561484, 86176960, 94065792, 101013186, 111115788, 119731264, 128661007, 134567554, 144670412, 154072590, 162215631, 169836108, 179238478, 185415312, 195526221, 204404366, 212547151, 220691981, 229570254, 1073749955, 1075605507, 235878098, 245560448, 254237825, 262878863, 269547028, 279403585, 285939411, 294475461, 305329686, 312958145, 319493779, 328029765, 338884246, 346512385, 353187344, 361584261, 372438614, 379673664, 386872850, 397235736, 405993174, 413228160, 420549656, 430790296, 439940825, 446782656, 454104216, 464344792, 470873812, 479419925, 487658712, 497899096, 505083537, 512974485, 521213016, 529593940, 538271259, 546256466, 555415249, 563437211, 571422354, 582546969, 588471893, 596317779, 604329538, 616101529, 622026453, 629872147, 638408197, 649655897, 656899725, 1076922373, 664614490, 671438338, 680588948, 690454221, 1074319362, 1074867202, 698300119, 706410065, 714432091, 723334874, 1076717508, 731575825, 739598043, 748500634, 1076203462, 757020183, 1074650056, 1075459080, 764229200, 1077303239, 1075226631, 1076545481, 773281355, 782186071, 1074209738, 790058507, 798832154, 806835915, 815740567, 823613067, 831338192, 1076051979],
    [118, 104, 7, 1840256, 10597504, 18986176, 27374592, 35763264, 44283073, 52671617, 61060161, 68948992, 77837313, 84399826, 92779730, 102503488, 112176851, 118216212, 127669440, 137473621, 143382228, 153892050, 162508435, 168547924, 178525904, 187674195, 193713812, 203691536, 212839955, 220976642, 226997906, 237778066, 246525589, 252425815, 262919874, 268940818, 279720978, 288468693, 294368919, 302503058, 310883922, 321664082, 330411541, 336312023, 344445970, 353220121, 363075152, 370128602, 1073755075, 378506840, 386643479, 395170841, 405018256, 412071578, 422677655, 428725913, 437105817, 447354513, 454014490, 464882755, 470669017, 479048921, 489297617, 495957594, 506563607, 515233308, 522851921, 1076912514, 531991683, 537777753, 546157657, 556406289, 563056152, 573953628, 579343425, 1075874756, 588222104, 599119516, 604771477, 613387992, 624285404, 629937237, 640781399, 648795202, 655103189, 666209283, 673961090, 680268821, 691375299, 698209370, 705172673, 716278999, 723375322, 1074325446, 730338433, 1076167624, 741977622, 747099218, 756659790, 1073838021, 763892737, 775532182, 782095514, 789845595, 1077249993, 800697942, 807261210, 815380174, 823400155, 1074129863, 834252502, 840545934, 848565915, 1076501452, 857323022, 865343003, 1075465230, 1074704330, 1076810703, 1074993099, 1075273677],
    [110, 96, 11, 638017, 10589376, 18977856, 27366528, 35755008, 44274817, 52663489, 61198992, 69440577, 76135617, 86217729, 94975506, 103019074, 111132305, 120526356, 128184962, 136298193, 145692308, 151361237, 162001109, 169852433, 176526869, 187166741, 195018321, 204075542, 210353281, 221189716, 229241494, 235518977, 246018646, 254516352, 263132884, 270791362, 279682240, 287961814, 296459264, 1073744835, 305739288, 312734210, 321625152, 1074290690, 327783944, 339293848, 344299157, 354939029, 361995408, 1075884997, 369727112, 381236952, 386242133, 396882005, 403938832, 411670088, 423179864, 431222792, 437493456, 445224648, 455685778, 1076940743, 464777416, 471047760, 1074593800, 480851538, 489943112, 496352787, 1073830854, 506017490, 514183376, 521518739, 530134682, 540274824, 546684627, 555300378, 564514896, 571850323, 580466266, 589680656, 598719572, 605754971, 613282391, 623885524, 630920859, 639211211, 646836759, 656119498, 665828500, 672863771, 681154187, 688779991, 699382804, 706295514, 714708555, 722334359, 731616778, 739972827, 748262923, 756544025, 1075417099, 764932761, 773321305, 781948490, 790098649, 1074915268, 1076234188, 798725770, 1074162637, 1076532234, 1075240911, 1075787721, 1077374926],
    [118, 104, 11, 291840, 10218624, 18478273, 26866753, 35255425, 43643905, 52163712, 60552192, 68940992, 77327360, 84440655, 94106688, 103518800, 110881856, 117995151, 128684752, 136047808, 143160847, 154112721, 162122753, 168326863, 176682501, 187797509, 1073754112, 193229888, 204197586, 210237125, 221352133, 227276307, 235796116, 243561664, 254529042, 1076911042, 260568645, 271683653, 277608083, 285504640, 296472210, 302511749, 313496209, 321942675, 330026578, 1075349509, 338661905, 344847956, 355200148, 363885587, 371954192, 378271443, 386791124, 397143252, 405828819, 414290053, 420345364, 430697556, 437417622, 447713873, 455863316, 462583382, 472617616, 478934611, 489714771, 497667201, 507220614, 514444481, 521303766, 532386310, 539610177, 546993689, 554807834, 565431322, 572159705, 582718150, 588797057, 597028504, 1074319494, 605139546, 613545481, 624151642, 630879897, 638694042, 647100041, 657706138, 663909910, 1074870212, 1077242823, 672248538, 682872026, 689600089, 700158022, 706237441, 714468952, 1076467658, 723358423, 730986057, 739791937, 748023320, 1075176392, 756912663, 764957889, 773189336, 782078615, 789706441, 798913668, 1075977225, 807244375, 815690756, 1075725251, 824152597, 832468036, 1073909708, 840929941, 849245380, 1074710478, 857707221, 1074210765, 866095701, 1076326347],
    [102, 88, 9, 2053120, 9698369, 18863297, 27251777, 35640449, 44028929, 52934348, 60773568, 68418689, 75880002, 86742082, 94109325, 102716480, 109434562, 120296642, 127663821, 136270976, 142988930, 153851010, 161961615, 169606669, 1073752064, 176543234, 1076391937, 187405314, 195516111, 203161165, 1076924418, 212833870, 220952067, 227802113, 237999758, 246118083, 252968129, 263165646, 271283779, 279182528, 288331278, 1074839811, 296449155, 304348288, 1073821636, 314021511, 321345039, 329514048, 339187207, 347305682, 355204290, 364353223, 371676751, 379845632, 1077240774, 1075939463, 1074383879, 388478476, 397147138, 406287891, 412079123, 423072839, 430701698, 1074666437, 1075469317, 439842451, 445633683, 455587468, 464256066, 473134610, 479319573, 489141836, 497941525, 506689170, 512742995, 521246225, 531854930, 537908947, 546412177, 556662421, 565670995, 571593877, 579966673, 590216917, 599225555, 605673097, 613520977, 621925589, 632159829, 639227401, 647468692, 655479893, 664516112, 672781897, 681023060, 689411604, 697947849, 706459216, 1075746760, 1075233801, 714847888, 723236560, 731354836, 1074212811, 1076848586],
    [114, 100, 13, 292864, 8689728, 18757696, 27146240, 35535040, 43923584, 52443137, 60831873, 69220417, 75790528, 84195980, 94386369, 100940290, 109344832, 117750476, 128070159, 134494786, 142899328, 151304716, 161747664, 168081996, 178936461, 1073750016, 1075865601, 185088721, 195441347, 204102221, 210418319, 220345039, 229267981, 235583695, 243808849, 253898895, 262822605, 269138511, 279064655, 288381009, 294303759, 303208643, 313546961, 1076408261, 319846593, 328636493, 335821506, 345029268, 353400897, 361249425, 372267153, 378968269, 386415121, 396628496, 402930306, 414210065, 420911245, 1076677634, 430183056, 437303892, 445675649, 455348816, 462985811, 470841345, 480653827, 488019981, 498366990, 1074603395, 505819203, 512801492, 523532878, 530985091, 538483219, 548698766, 1076196294, 554701334, 562337792, 573864654, 579867222, 588921544, 597457093, 605592275, 1076988868, 613421718, 622475912, 631011397, 637835456, 646976214, 656030216, 664565893, 672701075, 1074387911, 680923799, 689584712, 697473027, 706508805, 1075452936, 714879637, 722516500, 731798034, 739644119, 746887296, 756964050, 765211349, 772970563, 782129746, 790377045, 798136451, 807295634, 1075729354, 1074959370, 815141463, 823931413, 1075233737, 1073939465, 831918615, 1074231243],
    [94, 80, 11, 1866816, 10328256, 18096257, 26744896, 35133568, 43522240, 51910656, 60430337, 68819009, 77207745, 85752832, 94214272, 101982209, 110762113, 119379968, 127696064, 135536833, 144545856, 152861824, 160702529, 168303107, 177873487, 187144913, 1073750017, 193469059, 203301458, 212703891, 218652244, 228467346, 237476497, 245873237, 253371023, 261258902, 270410450, 279419409, 285761172, 295313935, 304978451, 311590614, 319298115, 329130514, 338532947, 344481300, 354034383, 363305553, 370310678, 378411592, 388479509, 396763856, 403865174, 413532759, 422419155, 428367572, 437131912, 1075865540, 447095440, 1076135874, 455475927, 463864343, 472365717, 480649808, 489030295, 1074056133, 497531605, 506363404, 512236227, 522592784, 1074331651, 529406472, 539917964, 546183880, 1073827848, 556695244, 565083724, 1074902028, 572030542, 1077270477, 1075190730, 1075475401, 580419278, 1077055435, 1074719687, 588807822, 1076568006, 597196302, 1075801102, 605707800, 613816344, 622485080, 630593624, 639262424, 647370968, 656039576, 664148120],
    [118, 104, 11, 2422912, 10776768, 18905089, 27424832, 35813504, 44201984, 52590784, 60848257, 69236929, 75788816, 86571600, 94402625, 103086272, 109343440, 119684819, 126253267, 136640576, 142897232, 153239123, 159807571, 170194944, 179327569, 186793619, 193362067, 204011536, 210006672, 220610260, 227310229, 235305491, 246436561, 254343376, 262290451, 269253205, 279990929, 287897744, 296369237, 302807573, 313545233, 319477905, 329661972, 336362197, 347755090, 353032273, 363478165, 370047576, 381309458, 386586641, 397286488, 403602136, 414864018, 420141265, 430841048, 440029906, 447102548, 455372864, 464395928, 470710424, 482015963, 488927232, 497950232, 504264728, 515570331, 522481792, 530988692, 540736027, 546460247, 1073746884, 556416021, 565901915, 571626007, 1074807747, 581582037, 588700189, 596792023, 1073781702, 1075369925, 604642966, 613997278, 621957783, 629808854, 639031965, 647655962, 654974550, 664197853, 672821850, 680140310, 689896096, 698249759, 1075127240, 1075922887, 705969817, 714529373, 723153626, 1074105289, 731135577, 739826206, 748581599, 756432540, 764992094, 773485210, 781598428, 790559328, 798913119, 1074388941, 1075711946, 806764124, 815323806, 824079007, 1074685902, 1076278210, 831798809, 840890912, 1077082059, 848576217, 857668320, 1077357519, 1076588492, 865484316],
    [130, 116, 11, 2119681, 10508353, 18897089, 27285633, 35805312, 44193792, 52304400, 60971200, 69589585, 77748288, 86262274, 94656514, 102636176, 109468243, 119921361, 128205506, 136599746, 144579152, 151411411, 161864337, 170148418, 178542658, 186522320, 193485332, 203807249, 212091522, 220485762, 227162323, 235428436, 1073743874, 246178386, 254794245, 262945412, 271344274, 279960133, 288111172, 1074293699, 296509970, 305388246, 313277124, 321675986, 330054148, 1076408324, 338584279, 344611480, 353122456, 1076943814, 363749975, 369515027, 378157075, 389178056, 397400773, 403462344, 411711571, 420109016, 431120968, 439343749, 445405256, 454309908, 462051928, 1075388421, 471063129, 481190551, 487479385, 496384089, 503864020, 515103254, 523133463, 529029780, 538196116, 548657814, 556950152, 562845832, 571095699, 579229843, 588143129, 1075929031, 598989398, 607281672, 613177352, 621558296, 629823512, 1075679240, 640828053, 649845274, 655382554, 664025300, 672291339, 682771157, 691788378, 697325658, 706099865, 714365581, 722360473, 733102677, 742120090, 747657370, 755775576, 764566155, 1074919369, 775045653, 784063194, 789600474, 798374617, 806509259, 814635225, 823672841, 831772697, 840587982, 848574548, 856840779, 1077280779, 865616073, 873715929, 882530894, 890648601, 898914829, 907559049, 915658905, 924473998, 931936472, 940858061, 949502025, 958028302, 966023757, 1073890317, 1074172942, 1075242954, 1076301775, 1074753484],
    [106, 92, 10, 333952, 8714432, 17076417, 27310272, 35698752, 44087296, 52476032, 59045888, 67408001, 75963088, 86555346, 94968018, 100989056, 109350913, 120109586, 128522258, 134543424, 142905409, 153664082, 162076754, 168202835, 179231312, 187218578, 195631250, 204397200, 210277013, 218534547, 226957456, 237951184, 1073750979, 243866257, 254728720, 260608725, 1075858372, 271768086, 277254675, 285677648, 296934038, 302420691, 310843408, 322099798, 327752273, 336106069, 347265750, 352918225, 361271829, 1074305991, 369695249, 378329153, 387093079, 395106433, 403643028, 412258839, 420272129, 428808724, 437424855, 445438145, 453974612, 462590615, 470866522, 479140564, 488026843, 496171548, 503650304, 513577088, 521599513, 530004568, 538619920, 1075368907, 546363930, 555520000, 562370752, 571669148, 580336152, 588951760, 596835036, 604313664, 613855835, 622639822, 630651481, 639056536, 647671888, 1074866122, 656194190, 664205977, 672611032, 681349312, 689748558, 1076191181, 697359066, 706130459, 1075689420, 714914318, 722524826, 731558032, 1077267470, 1074671557, 739441244, 748458048, 756462235, 764869337, 1076773826, 1073918918, 1077069769, 1074206671, 1075276744],
    [106, 92, 2, 1867840, 10524865, 18913281, 27302017, 35690561, 44210240, 52598912, 60963536, 69376192, 77365376, 86153216, 94699153, 101095569, 111155922, 119308480, 128490131, 136642065, 143038481, 153499795, 159947394, 169639936, 178821715, 186973905, 193370321, 203569808, 210279106, 220496066, 229153491, 237305425, 243701841, 254163155, 260610562, 270827522, 279484947, 285776450, 295844368, 304382018, 1073741826, 313187973, 319723653, 329660435, 337936514, 346742469, 353278149, 363214931, 371630291, 380436182, 389060822, 396507728, 403610181, 413573267, 422239301, 428775941, 438739027, 1073762309, 446700050, 455793669, 463904787, 472710678, 480254610, 489723926, 497721345, 506265238, 513808978, 523278486, 531407572, 539819606, 548149783, 556832854, 564830401, 573315671, 581607489, 590093015, 598516372, 606870167, 615293460, 1074837449, 623778456, 630644377, 640459348, 648944344, 657490517, 664443532, 674110040, 682270849, 689609292, 699275800, 707822229, 1077202890, 714775052, 722918937, 732987925, 739941068, 748084825, 758153941, 1074598924, 764862169, 1075136462, 1074112459, 1076228040, 1076769743, 1077042119, 1075489734, 1076551629, 1075782595, 1076054980],
    [122, 108, 13, 2324480, 10549377, 18937857, 27326657, 35846208, 44103745, 52623488, 61133520, 69254352, 77789184, 86341840, 94566592, 102809168, 111465104, 119896144, 128241744, 136363152, 145062032, 153403027, 161796624, 170096832, 178568915, 187618001, 195393552, 204405270, 212783761, 220773975, 226949207, 237205632, 246348438, 254726673, 262717079, 268892311, 279148608, 1073742786, 288291542, 296669777, 304660183, 310835415, 321870484, 330234454, 338214423, 344773269, 352778263, 363813396, 369818245, 380812374, 386716373, 395115096, 405756628, 1073763267, 411761221, 422755542, 428659285, 439310932, 445315589, 456309782, 462213653, 472873046, 478870213, 489864342, 498397332, 506427414, 1074825221, 512686662, 523681306, 531951636, 539981974, 546241158, 557497432, 565506260, 573536470, 579664536, 591051928, 599060564, 604961286, 613767377, 621738694, 630641362, 639942227, 647321681, 1074321414, 655162072, 664335003, 674676378, 680876177, 689361426, 699842138, 706041873, 714799627, 723055195, 731954192, 739990233, 1075382215, 747436568, 756470354, 767212568, 773544601, 781908619, 790428174, 798413458, 807714323, 815487577, 823851723, 832371278, 840495643, 851098840, 857430553, 1074091977, 865925838, 874050267, 884391642, 890960459, 899480206, 1075153931, 1074650126, 1075720138, 1076782024, 1076016068, 1077078991, 1076570060, 1076328397],
    [126, 112, 9, 2152641, 10541185, 18929665, 27318337, 35838016, 44226688, 52869776, 61003968, 69392384, 77914705, 86530129, 92592786, 103201360, 111598099, 117891091, 128473809, 134666836, 145144528, 153541267, 159834259, 170416657, 176478930, 187087376, 195484371, 201777363, 212359825, 218421842, 227064018, 237427283, 243720275, 254572755, 1073744834, 260364818, 269261525, 279861846, 288022530, 294050324, 302561362, 313416342, 321577154, 327604948, 336509140, 346970838, 355131522, 361159316, 369924757, 380525078, 388685890, 395090453, 405856919, 414472728, 1074289603, 420395092, 431022615, 439638616, 445823706, 456579611, 464437275, 472676371, 479377946, 490134171, 497991835, 506230931, 512932506, 523688667, 1075348421, 531546331, 539785299, 546486874, 557242971, 565100635, 571767452, 579787485, 588560605, 598794967, 607410904, 613341853, 622114973, 630381278, 640737879, 649353880, 655284765, 664057885, 672324126, 1073796039, 681894033, 691951838, 697227869, 706000989, 715448337, 725506078, 731559966, 739433118, 749002961, 759060638, 765114526, 775217347, 781482524, 790280414, 798153310, 1074869190, 808771587, 817780830, 1076978632, 822655122, 833937539, 840202844, 1075948484, 848214164, 859103299, 865368796, 873379860, 882434777, 890943582, 1076479949, 1074141134, 899211929, 906795605, 915989017, 923318290, 1075214282, 932766297, 1077317577, 1074720716, 1076830155, 1075800015],
    [118, 104, 1, 497664, 8878144, 18550785, 27343040, 35731456, 44120128, 52508800, 61028481, 69417153, 77805633, 84375744, 92912272, 102961296, 111360001, 120011346, 126318720, 134855248, 144904272, 153565714, 159873024, 170236611, 178459152, 184891923, 193411796, 203897490, 210483921, 218855504, 228790992, 235485909, 243743252, 254229202, 262904021, 270209089, 277575696, 285817429, 294074964, 304846933, 312152193, 319518864, 327760533, 336018068, 346886163, 355178645, 361461968, 369441491, 380467218, 388829395, 396728963, 403389060, 414021778, 422680708, 429592769, 436812309, 447576274, 453718614, 464230421, 470104723, 481130578, 489492627, 497392195, 1073745987, 503659091, 512440900, 523343940, 531435603, 538007745, 545995460, 554381846, 565287108, 571562113, 579549700, 587936470, 598841348, 605116481, 1074808836, 613628551, 621490838, 631609347, 638670849, 647182855, 655560914, 666327124, 671725584, 680737351, 1074302917, 689115218, 699881684, 705411665, 714291911, 722669714, 733436052, 738966033, 1074583559, 747835410, 758601748, 764131985, 773675607, 780777680, 790452759, 797415616, 807230103, 814192768, 824007383, 830969920, 1075381186, 840923736, 1073832905, 849312280, 1075950542, 1077013446, 857701080, 1076508619, 866089624, 1077305295, 1075746760, 1075242957, 1076309964, 1076840394],
    [102, 88, 8, 2031616, 10795200, 18946049, 27334785, 35723329, 44112065, 52631616, 61020160, 69408896, 78027280, 85917760, 94574784, 103193168, 111083712, 119766738, 128359120, 136249472, 144932434, 153682452, 161913488, 168648214, 178593872, 187603665, 195657303, 203759824, 212769361, 220823063, 228925456, 237935121, 245989079, 254091408, 263101073, 1073752003, 271154839, 277553878, 287619072, 295927442, 302719574, 312785024, 321093138, 1076124612, 330367642, 337950784, 344808662, 355383318, 363922010, 369826502, 378363542, 1075350466, 388937814, 397476570, 403380870, 412450521, 422492374, 431030810, 436935174, 446004889, 456046742, 464061012, 1074316229, 470489670, 479026262, 1073808390, 489732755, 497615508, 504725017, 514898643, 522781396, 529890905, 540064339, 546374363, 556841491, 563282002, 1074090953, 572299992, 579928667, 589077144, 596705947, 1074896840, 1075705799, 605854296, 613097622, 622795276, 631020056, 638263318, 647928533, 655556754, 664738380, 673094165, 680722450, 689904268, 1077293003, 698260053, 705757723, 715070156, 1076777996, 723425941, 731054290, 1075220429, 1074721742, 1077095375, 1076585418],
    [106, 92, 8, 382976, 10582080, 18970816, 27359232, 35747968, 44252816, 50714688, 61436562, 69418704, 75880576, 86602322, 94584400, 101046464, 111768082, 120135364, 126474897, 136934098, 145301124, 151640657, 162362068, 170466820, 178780161, 185422547, 195632708, 201972241, 1073754116, 212693524, 220413456, 229112001, 1076908995, 237859412, 246488661, 252304081, 263025300, 271654613, 279443585, 1074824130, 288576152, 296820373, 303135239, 312997953, 322130520, 330374677, 336689735, 346945680, 355684888, 364239511, 372448968, 380850904, 387152072, 397794007, 406003336, 414798422, 420706440, 431348311, 439557704, 448352982, 454260808, 464386064, 473112072, 481907350, 487815176, 497940688, 1073797128, 1075391433, 1076451269, 504577625, 515461654, 521501386, 532011543, 537743891, 546520729, 555055690, 565049424, 571298387, 580075033, 588610186, 597285014, 604852883, 613629657, 622164490, 630839318, 1075152906, 1074382790, 639311578, 647983771, 656243278, 664393942, 672865818, 681538075, 689797646, 697399943, 706336854, 714808986, 723481179, 731740814, 739974746, 748647131, 756906702, 764508871, 1074142222, 1075734477, 1076268039, 1074722764, 1077358543, 1076847563],
    [114, 100, 3, 352257, 10573953, 18962497, 27351041, 35739841, 44259392, 52648128, 61036544, 67461313, 77813888, 86448657, 92624913, 102974019, 111876818, 117922002, 128139971, 137042514, 143087698, 153305731, 162331204, 170597010, 176642194, 186860035, 1073743875, 195885700, 203889361, 210065617, 220944965, 229589634, 237828804, 246626882, 252140050, 262887941, 269179475, 280051781, 288160260, 296425490, 302340753, 313219717, 319511187, 330252802, 1074293764, 338753541, 346495121, 352672337, 363551429, 369973972, 380584642, 1076664325, 1075376130, 389085253, 396826705, 403528212, 414138434, 423033366, 431175874, 439435397, 448199318, 456341634, 464863815, 473365206, 481507330, 490029767, 1076963655, 498530902, 504445011, 512449235, 523583495, 531691717, 537999571, 548487173, 556857477, 563550743, 571169299, 581788176, 588315221, 597105367, 607207621, 613735000, 621885459, 630020692, 640508496, 1076450249, 647035413, 655440019, 666189959, 672201429, 680991383, 688741012, 699228816, 705755797, 714815636, 721772673, 731175640, 739981332, 746938433, 1074889674, 756341272, 765147220, 774726352, 1073870795, 781507224, 790043223, 798580928, 807090388, 815357952, 1077290956, 1076256717, 823746688, 1075746766, 1075234760, 832135232, 1074209743, 1076056006],
    [114, 100, 9, 268289, 8902785, 18462721, 26851393, 35371200, 43759616, 52017281, 60536960, 68794561, 78108672, 84154433, 94091328, 103387854, 109427266, 117848589, 128703052, 136942222, 145217600, 151403149, 162107918, 168434192, 176674881, 187273806, 193600208, 204200588, 210219730, 218765904, 229366476, 235508435, 243931792, 254532108, 1073745860, 1074554884, 260682390, 268843597, 277338113, 285840019, 293869761, 302504129, 311276245, 321378496, 328219217, 336171539, 344308226, 354932864, 360978561, 369603218, 378550929, 389020303, 394900054, 405412505, 414185999, 419934802, 428194434, 438967001, 447740623, 453620438, 464132633, 472906319, 479312520, 487953112, 497687129, 504625869, 1076403143, 512867016, 521507352, 528857794, 538179597, 545667277, 1075368962, 555072137, 562672150, 571734093, 579877393, 588364360, 596488853, 605288589, 613432017, 622181065, 630559384, 638720128, 647748247, 655735369, 664113752, 672405644, 681302743, 689289737, 696881747, 706214612, 714217664, 1075130377, 1076983755, 1077251014, 1074392070, 722582024, 730706453, 739514572, 748411479, 1076763656, 1075729349, 755872341, 764934676, 773068812, 780644882, 789846092, 798743063, 1074955203, 1073924042, 1074208778, 1076061187, 806877844, 814880832, 823654996, 831657984],
    [122, 108, 12, 1178816, 8757377, 18454529, 26843329, 35231809, 43620481, 52140032, 60528704, 68917440, 76676096, 84509260, 94083200, 101548685, 110230592, 120273423, 128162512, 134847043, 143366788, 152173696, 160006860, 170866755, 178494032, 185178627, 193698372, 201949836, 210492624, 221198339, 228825744, 235510467, 244416640, 252435600, 263141571, 270768656, 277715653, 285842051, 294378512, 302882832, 1073742851, 313473155, 319135809, 327933008, 338377423, 345342546, 353361486, 363543183, 370245696, 378658450, 388708943, 395287047, 404872199, 414162951, 420297425, 428990162, 437616850, 445463185, 454007495, 463592647, 472883399, 479017489, 487432400, 495967758, 504183377, 512727687, 522312839, 531603591, 537991765, 546282055, 555867207, 565157959, 1074024455, 1074834439, 571808404, 579707024, 588242638, 597236307, 605126656, 613408398, 622402067, 630692361, 638294532, 647093778, 654680257, 1076683714, 664083156, 672635465, 680368709, 688751181, 697424978, 706288275, 714578633, 722311685, 730955968, 739850774, 748133001, 755866245, 763986444, 1075904517, 1073825801, 772872853, 780901060, 789938322, 1074373636, 798571094, 1076219850, 805675009, 815348374, 1074665416, 1075210248, 822968845, 832125654, 840269842, 1076534219, 1075508235, 848370389, 856523469, 1077354438, 1075802118, 865409620, 873308240, 881924629, 890837715, 898963988],
    [130, 116, 8, 2521152, 9157760, 18479233, 26867905, 35256385, 43644929, 52164672, 60553216, 68941952, 78018752, 84655296, 94107840, 101055185, 111016450, 117963395, 126196738, 136870415, 145478226, 151386641, 161348162, 168426003, 176528450, 187202127, 195810002, 201718417, 211679874, 218888789, 227048084, 235248770, 246141586, 252050001, 1073754112, 262011586, 269089363, 277379668, 285580482, 1076903938, 296473106, 302906006, 311425668, 319289923, 327711444, 336436356, 344849110, 353368644, 361495189, 369654292, 378379332, 389403159, 395180630, 403438293, 411810816, 422606993, 431346263, 437123606, 445381141, 454031876, 462265348, 472283136, 481940184, 487062019, 495696960, 506493137, 515494552, 520616643, 529529540, 537763012, 548436049, 1073776644, 1074321411, 557437464, 562690771, 571841619, 581466831, 590991960, 596245139, 605142101, 615021199, 624030425, 631666816, 638827651, 649450135, 655727827, 665876497, 674616023, 682343963, 689338896, 699527705, 705805525, 714766486, 1075386309, 724693657, 732675675, 739670672, 1075138502, 749859417, 756447952, 764656643, 775672349, 781613648, 789691413, 800838237, 806468757, 815429654, 826004125, 831888531, 840595670, 1074634698, 1075696584, 851170013, 858504923, 865761366, 873722394, 882801180, 892059291, 898888410, 907967068, 915651651, 1074931660, 924054170, 933133020, 940940307, 1076262857, 949219930, 958298780, 965983427, 1077324750, 1076555725, 1076824007, 1074226123],
    [110, 96, 8, 1818624, 10336321, 18864193, 27252865, 35641345, 44161216, 52549632, 60807361, 69326976, 77316224, 86096588, 94492736, 102481984, 111262284, 119259328, 128039564, 136428044, 144687297, 151878287, 1073752064, 1076391937, 161856013, 169852929, 178747984, 187021901, 195018881, 1076934594, 203913872, 212187789, 220184641, 229210833, 235911699, 245987857, 254130893, 261052946, 271049364, 277600404, 286243539, 1077211078, 294607442, 1076698053, 1075403781, 304996872, 311285768, 320714753, 328038927, 338158100, 344709140, 353352339, 1075680195, 363297488, 1074906055, 372105928, 378394824, 386906707, 395147983, 405267156, 411818196, 420600470, 429766849, 1073875908, 1074416644, 438794768, 447603272, 453892168, 463321217, 473004629, 480764500, 487315540, 496220686, 506034769, 514712200, 521001096, 529775182, 540113557, 1074693128, 546423320, 555080393, 563206678, 571718350, 581532305, 588497495, 597023241, 605149910, 613661326, 623999701, 630440663, 638966345, 647477270, 657553941, 663863896, 672520841, 680647254, 689420438, 697260690, 1074189321, 705937943, 714586326, 723475033, 730972824, 739752022, 747592402, 756138712, 765418009, 773046935, 782195353, 790584025, 1075259338, 797801039, 1076323275],
    [106, 92, 13, 2260032, 8666113, 17054785, 25443521, 33832065, 42351744, 50740288, 59129024, 69369024, 75906048, 86146176, 92708364, 102923264, 109485708, 1073747969, 118390473, 1075339264, 1075881985, 126262988, 135167625, 143040076, 153490958, 160333321, 170268238, 177110601, 185114191, 195434126, 204111562, 212342416, 220888714, 229686930, 237508304, 246054410, 1076416450, 252616339, 262543054, 271220298, 280018450, 287839824, 294542987, 305184466, 310646421, 319839761, 330350162, 335812181, 345407053, 353418776, 363337232, 370040331, 378584664, 386143957, 395337361, 403750552, 411309589, 420372043, 1074598851, 1074877443, 429143639, 437305048, 445267652, 454458893, 462995030, 471348761, 478821956, 488013517, 495492815, 505034260, 512376452, 521166417, 529284741, 537828947, 546846361, 554319364, 562978507, 1075160068, 571227845, 580138519, 588160531, 596655815, 605453965, 613170757, 622378518, 630732505, 638598791, 646995665, 655113733, 664024791, 672710294, 680541703, 1076222981, 1075719173, 689487574, 697972308, 705707591, 1076774919, 714356375, 721985167, 730767059, 739915476, 747150863, 756561497, 1074430918, 1073923078, 765081236, 1074213832, 1077113864],
    [110, 96, 13, 2390209, 9575552, 17964032, 26352704, 34741440, 43261057, 51649729, 60669442, 68426753, 77887489, 85204033, 93855244, 102612674, 1073746306, 111442049, 1074809795, 119152270, 127777858, 135798412, 144996417, 152706766, 1074305025, 161332354, 169352908, 176846860, 1075372033, 187172496, 194649614, 203792079, 211295820, 218789964, 229115472, 236592718, 245734991, 251928132, 263092292, 271058448, 277094084, 287678095, 296646852, 304613072, 310648324, 321494739, 330201092, 338437841, 344202884, 355367044, 361864852, 371992081, 1075905540, 380116565, 386276886, 394950860, 405257301, 414065686, 420116620, 430546451, 439494290, 447225493, 456292941, 463977621, 472655505, 478551766, 487749710, 496082644, 506734168, 512106134, 523401741, 529636884, 539894998, 546469902, 556375635, 565454360, 570826326, 580024526, 588357204, 599008920, 607287949, 615392406, 623484563, 630356110, 640558166, 648527381, 656940053, 666008269, 673982033, 682082005, 690494677, 697850521, 708060888, 714889815, 724706898, 731404825, 1074089925, 741484242, 748444375, 757440015, 765221527, 1074632646, 773610007, 783427090, 790125145, 1075168200, 798513881, 1073884103, 1076518857, 1075749897, 1076293578, 1076835275, 1077113867],
    [98, 84, 1, 283712, 10229888, 17071232, 25459904, 33848320, 42236992, 50756609, 59145345, 69140174, 75922625, 85727232, 92697806, 101088321, 111083150, 119281856, 126252558, 136248910, 144447552, 151417998, 1073747969, 161414158, 168195150, 178526273, 186914817, 193754831, 202407569, 209998976, 220469377, 1075332034, 227213010, 235828880, 245635265, 252739153, 260723793, 269228226, 277771792, 286005378, 294533827, 302806671, 1073777091, 311326416, 319961797, 328007316, 336336962, 345274067, 353253507, 361526863, 370179793, 378164433, 387070597, 1074319557, 395116052, 403734033, 411718673, 420624453, 428670676, 1074865092, 437000194, 445937235, 454221462, 462837269, 470693891, 479002196, 488003285, 495983319, 504036882, 511988928, 521149079, 529202834, 537547921, 546314775, 554884630, 563500693, 571480663, 579534418, 588396549, 596932115, 605748760, 613316176, 621688899, 1075931079, 630382294, 638998101, 647691992, 654595072, 1076212680, 1077015560, 1077286858, 664469144, 672429715, 681246296, 688682511, 1075212230, 697491030, 1076800457, 1076547531, 1074733004, 1075791821],
    [118, 104, 13, 1588225, 9829569, 18635968, 27024448, 35412992, 43801728, 52321281, 60709953, 69098689, 77070018, 85474433, 94264449, 102917713, 109337681, 1073744322, 119012418, 127417537, 1074287555, 136472273, 142892241, 152566786, 160971841, 170026641, 176446609, 1074829313, 186121346, 193478224, 203580945, 210000913, 220225158, 228588739, 235421392, 245786311, 252075207, 262168134, 270531651, 277364240, 287459023, 294018695, 304111302, 312474627, 319307408, 329671815, 335961607, 346054150, 354688134, 362150913, 1075371014, 371614727, 377904711, 388242438, 396360835, 1075642375, 405169223, 411721429, 421796934, 430440146, 1073834949, 439109332, 445275797, 455351494, 463994514, 472663700, 478830101, 489692691, 497548818, 506218068, 512384597, 523378254, 531103314, 540304405, 548413011, 555089025, 565470357, 1076470729, 573578899, 580254785, 590636117, 598735941, 607133395, 1075957704, 615802069, 623901701, 632430094, 640435732, 649067653, 657596110, 664946255, 674233541, 682761870, 690112015, 697048790, 705977879, 715277967, 722615319, 730603094, 739532439, 747380374, 756309719, 764558551, 773086807, 1074669515, 1076260804, 781335639, 789995084, 798514765, 806100502, 815161036, 823680717, 831667351, 840326796, 848846349, 857103884, 865623693, 1076790284, 1074189325, 1075262410, 1077113866],
    [98, 84, 9, 2405376, 8707200, 17087553, 25476225, 33864897, 42253313, 50773184, 59161728, 67550272, 75815936, 86291520, 92716032, 103068800, 109502095, 117775952, 128234688, 134536384, 145309265, 151568019, 1073747969, 159833615, 170563278, 176627282, 185122387, 193256512, 204117518, 210181778, 218676947, 226942543, 237672078, 243875477, 252231187, 260497103, 271226446, 277429973, 288152787, 294294593, 1075336131, 304692881, 313318419, 319460353, 329858577, 338484307, 345019927, 355024593, 363650195, 370185815, 377822928, 386457236, 394957953, 402988560, 411735233, 420404430, 428285458, 437556953, 445177556, 454106648, 462618326, 470849239, 479272600, 487888473, 495901774, 1074831302, 504438488, 1075632072, 513054233, 521338390, 528817808, 538099274, 546608793, 555286106, 563158616, 571653770, 1075120069, 580058774, 588289687, 596196949, 605208266, 613613142, 621223634, 630373898, 1074089929, 638508174, 1074628618, 646504020, 654892564, 664337946, 671694357, 681115290, 1074381771, 1073886156, 1077048332, 689503962, 1077322690, 697228302, 1076031431, 1076833229, 1076586436],
    [134, 120, 10, 1875073, 10263553, 18652225, 27171840, 35560640, 43949120, 52856386, 60726400, 68984001, 78174735, 86023758, 94799490, 1073746498, 102645456, 1074809795, 111729295, 119840337, 128353474, 136199760, 145414225, 153394833, 1074305025, 161907714, 169754256, 178968721, 186949329, 196117582, 203701906, 212507794, 220911825, 228892177, 236986003, 246062802, 254335567, 263226894, 270572558, 278929107, 287890127, 297043540, 304913941, 312516302, 1075372996, 320872019, 329963537, 338986644, 344628886, 354459278, 363740310, 372570821, 380929748, 388250834, 397736453, 406095380, 413965909, 420257350, 430980697, 439393369, 445685400, 456456837, 464553166, 470589062, 480255507, 489725657, 498399813, 506496142, 1075913733, 512794136, 523255321, 531667993, 537697990, 548993176, 554477079, 564960981, 571514584, 581975705, 590388377, 596418054, 607713496, 613197527, 1076188166, 621453014, 630234712, 640564438, 649656344, 655402523, 663395926, 672308744, 682507350, 691314269, 699988056, 705472151, 715955861, 722116118, 731029064, 741227542, 750034589, 756589725, 764737557, 772972168, 783301849, 791322194, 798532701, 806943386, 1075163079, 814915272, 824458322, 832231964, 839952027, 1076741128, 849009372, 856729179, 866008592, 874052122, 881632855, 1074136009, 892640797, 899195933, 907343957, 916733458, 925539346, 932772442, 941139677, 951360733, 957675669, 965781211, 974452949, 1073893322, 983104218, 1074700235, 1075770316, 1077097484, 991615644, 1000004188, 1077373901],
    [98, 84, 10, 2448513, 10802369, 17103936, 25492672, 33881088, 42269824, 50789441, 59178113, 67566785, 77945921, 86431438, 92732417, 103455362, 111213698, 119635471, 128374350, 137009666, 144768002, 153190095, 161928846, 170695250, 176750211, 1073747969, 186744399, 195483150, 204118722, 211877058, 218945043, 228687503, 237804050, 243858947, 254334676, 262495425, 271358610, 278986306, 286053971, 296049665, 1075331074, 304781378, 310967875, 319608531, 329866243, 338467538, 344522435, 355171989, 363386388, 1073776643, 372546128, 378328723, 388726485, 397842627, 405363843, 413718164, 423008387, 430669397, 438883924, 448174083, 455835157, 463787073, 473339971, 480861379, 488952833, 498375376, 506027075, 514118785, 523541136, 530109520, 539713233, 548706832, 555275280, 564878865, 572045975, 581656145, 589231761, 1074319302, 597211735, 605607056, 615210129, 622377495, 631174353, 639154903, 1074601925, 647550160, 656325334, 664728593, 673102358, 681505873, 689879638, 698268310, 1075664845, 1075163076, 1076753352, 1077031944, 1077299147, 1074177994, 1076286407, 1074996172, 1076063177],
    [98, 84, 7, 2417856, 10271809, 18668737, 27057153, 35445889, 43834433, 52354176, 60742848, 69131264, 77774402, 86689474, 94297152, 1073744194, 103465986, 111328386, 119832208, 1074287555, 128245329, 137020482, 144882882, 153386512, 161799825, 1074829313, 170048514, 178963586, 186965521, 195749009, 203209729, 212106960, 220520145, 229303505, 236764353, 246080529, 253541505, 262438480, 271498964, 280151759, 288276052, 296412241, 305053204, 313706127, 1075364804, 321830548, 330483215, 338861778, 347260495, 355098135, 363781143, 372416082, 379905152, 388652631, 397335639, 403365510, 411885063, 422747666, 430236736, 438984407, 447667415, 453828167, 464690834, 472179712, 478994119, 488162838, 496278607, 506093207, 514776215, 520805894, 529325703, 538502862, 546610319, 1073808391, 554360518, 563668494, 571776207, 580437590, 588553231, 596303430, 605593237, 613992150, 1074091014, 622370325, 630777486, 1075164106, 1077015562, 639147733, 647546518, 1077284808, 1074685897, 655924821, 664331854, 672841427, 1076276165, 681229843, 689618579, 1076555723, 698007123, 1076831180, 1076060109],
    [102, 88, 1, 351296, 10818624, 17120321, 25640064, 34028608, 42417344, 50805760, 59063425, 67452097, 77927424, 84639438, 92617729, 103093440, 109805070, 119870592, 126574287, 135118481, 1073747969, 145831507, 151346176, 160144914, 170997459, 176905871, 185310802, 195903188, 204551699, 210468494, 220699860, 229457556, 238106259, 244022862, 254254228, 263011860, 268786816, 280310913, 287808532, 296566356, 305476609, 311123471, 321363028, 330774039, 336289359, 344833617, 352672960, 364196929, 372350552, 378625236, 389362881, 397516504, 406271703, 412179604, 1075334084, 422682264, 431437463, 437345300, 1074308037, 447847960, 456603223, 462511188, 470523602, 481123397, 490419733, 498441945, 506289349, 515585685, 523607705, 531454981, 540751573, 548773465, 556620933, 565917269, 573939225, 1075893186, 580458128, 588734166, 596491985, 1074866120, 605623888, 613899862, 621518482, 630789840, 639065750, 646823441, 1076184003, 655955472, 664231446, 1073848267, 1075702726, 672882394, 681262298, 1076498380, 1074681801, 689659546, 698039450, 1075228615, 706436634, 714816538, 1076818893, 1077097485, 723213914, 731593818, 1077364682],
    [122, 108, 10, 2014209, 10822721, 18685120, 27073664, 35462208, 43850752, 52370433, 60759105, 69147777, 77511809, 86320321, 94313665, 103242446, 111221966, 119454785, 128263297, 1073744835, 136519313, 1074287554, 145038863, 151616080, 161553934, 170206209, 178175169, 186851025, 195370575, 201947792, 1074829313, 212403794, 220642449, 228793937, 235502288, 245958354, 254196945, 260667920, 271656467, 279362641, 288169495, 296573007, 304922261, 311100439, 321723991, 330127375, 337714766, 344654935, 355376143, 363667159, 369696389, 380721285, 388046478, 394986711, 405707855, 413998743, 421731857, 431053381, 436804677, 445318295, 455523345, 461970949, 472995845, 480839314, 487136965, 498161861, 506005010, 1075363845, 514760399, 522525903, 531454159, 540091987, 548191957, 556080783, 565008527, 573646483, 581746261, 589781006, 598812371, 606912021, 614946894, 621872336, 632200335, 640112782, 647169558, 655793689, 664369748, 672335574, 681138327, 689348185, 697369680, 706158153, 714701524, 722535568, 731455115, 739712649, 748255764, 756457177, 764610134, 773398219, 781655561, 790190295, 798164630, 806952459, 815210185, 823753364, 831954585, 839975952, 1073812489, 848895563, 857299031, 866068056, 1075135499, 1074111430, 874076183, 882845400, 1075957706, 1074672588, 1077048332, 891233816, 1077323716, 899622552, 1076289485, 1075785671, 1076849608],
    [102, 88, 5, 1301632, 10310657, 17136640, 25525440, 33913920, 42302592, 50822209, 59210945, 67599489, 77419585, 85589582, 92765185, 103365136, 109673488, 119362689, 127532686, 136139969, 144309774, 1073747969, 153450193, 161087182, 169729615, 178869906, 186506895, 195647058, 203283983, 1075344323, 1076933635, 212424402, 220593362, 229980819, 237590034, 244415635, 253615823, 262501905, 271923795, 277970003, 286514368, 1077201860, 296056465, 305478355, 311524563, 321256530, 330643987, 336690195, 347035156, 354811026, 1074336709, 363412048, 372201108, 378109008, 387177472, 1074873282, 396719697, 405355152, 411663504, 421919762, 430521040, 436829392, 445897792, 456604360, 464475860, 472505474, 481769992, 489641556, 497802372, 1073848712, 506681045, 515323976, 521633290, 1075964870, 531356868, 540235285, 548878472, 555187850, 564780034, 573789781, 580721366, 1076502471, 590208069, 598955669, 605887062, 615111746, 1075736521, 622664342, 632019972, 639441430, 648928389, 656358039, 664239690, 673832130, 681523927, 689405642, 699128900, 1076792330, 1074718667, 706689623, 716037317, 723466775, 732814341, 1076299724, 1074223053],
    [110, 96, 9, 353408, 10312705, 18701377, 27090113, 35478657, 43998400, 52386880, 60767746, 69164032, 75850816, 85941376, 94322242, 1073744642, 101008514, 1074287555, 111599118, 117923471, 128400527, 134831813, 142951490, 153672901, 159866383, 1074829313, 170343439, 176774661, 185558145, 195485262, 201809615, 212286671, 219244166, 229039822, 235363919, 245840975, 252003330, 262724613, 269172368, 277694151, 287760014, 294215301, 302726736, 310723778, 321444997, 327769669, 336281104, 344802887, 1075367239, 1074593797, 354999365, 361447120, 370238982, 380567058, 387923138, 395798165, 1073831558, 403660489, 414121554, 421477506, 429352661, 437214857, 447676114, 456212052, 461726720, 1075688392, 1077015560, 470875798, 481378004, 488072789, 498007698, 506543636, 513238549, 521207510, 531709588, 538265239, 1077291972, 546373142, 554647057, 563176518, 571432521, 580320984, 588586582, 596985367, 604986889, 613875288, 622411347, 630015111, 1076515849, 638647382, 646921937, 1075225546, 655320129, 664354323, 672482903, 680984088, 689520275, 697123847, 706297555, 713385152, 1076031436, 722927256, 731192534, 739337414, 747585169, 756369111, 764746902, 772760577, 1076824011, 781523990, 789537985, 797916753, 1074227149],
    [102, 88, 13, 1719360, 8903808, 17153024, 25541696, 33930432, 42318976, 50838529, 59227265, 67615937, 77216768, 84540942, 92781633, 102382784, 109706894, 119159936, 126484174, 1073747969, 136060418, 143261262, 152821457, 161226306, 169598545, 178003586, 185186002, 194780866, 202235535, 1075340290, 210351698, 219012687, 229391888, 1076145091, 238393043, 245096081, 254418566, 1076417476, 261078599, 271947411, 279576213, 287972934, 294633159, 305501715, 313130709, 321666768, 330667603, 338296341, 346832528, 353081047, 363462229, 371859142, 1074867270, 378377748, 388488841, 397164112, 403412631, 413654537, 422190086, 428578327, 439500377, 447209161, 454276760, 464666265, 472374857, 1076715529, 479041108, 489832153, 496754193, 1075939275, 1074124744, 504207060, 514997785, 521002703, 529372820, 537796310, 546168335, 554679943, 562796119, 570940416, 579739286, 588234247, 596227730, 605667021, 612883520, 621682198, 1075190791, 1075728332, 631092890, 639221261, 646438080, 655236694, 663992024, 672775821, 1074693061, 681424410, 689552973, 1073924109, 696890898, 706590426, 714323544, 1074475978, 1077113866, 722712088, 731756122],
    [126, 112, 11, 2458689, 10737857, 18717696, 27106368, 35495104, 43883648, 52403393, 60791937, 69180481, 78095874, 86235137, 94346241, 103104068, 111385668, 1073744770, 120038594, 128178305, 1074287555, 136658628, 144940228, 153592962, 161732673, 168271503, 1074829313, 178758722, 187553923, 195772048, 201825999, 210345553, 221226065, 229497027, 237706321, 243768847, 252288657, 263169169, 271439939, 279649425, 285711951, 294231569, 305112081, 313382915, 321592337, 329490052, 336174801, 346683524, 355443921, 363150468, 371432964, 378664975, 389260814, 1075372036, 396704772, 405642834, 413792260, 422815310, 430644433, 439197394, 445774031, 456369806, 464207568, 472751634, 480901316, 489924302, 1075908549, 497761872, 506306194, 512882767, 522552513, 531316240, 538418836, 548010052, 556106753, 563584596, 571603087, 581272705, 588750356, 598865938, 605783107, 613916372, 624031890, 630948995, 638664213, 647601674, 657586258, 664503491, 672611990, 681156234, 689800261, 699529426, 706166486, 714710730, 722982996, 731743237, 739720726, 748265034, 756930634, 765297797, 1074611210, 773275222, 782096586, 790332419, 800399063, 1074108359, 806869012, 815769299, 1075180488, 1077031944, 825564823, 832428170, 840934931, 850730519, 1077307334, 857593866, 866100819, 875896407, 882366612, 891126981, 1076273099, 1075758028, 898711189, 907532500, 916432531, 923876949, 932265685, 1073949645, 1076588489],
    [118, 104, 9, 2070592, 10517697, 17169409, 25558081, 33946817, 42466432, 50855104, 59243520, 67632192, 77568128, 86015105, 92667009, 101308041, 1073749954, 111122432, 119569473, 127899840, 136346625, 143259212, 1075599361, 153247370, 162110027, 168425100, 1075359744, 1076950016, 178887307, 187063436, 193590796, 202112709, 211967562, 218756812, 227392205, 237108814, 244055685, 254172172, 1077218244, 1074359300, 263050318, 271554638, 279051918, 285998597, 296115404, 304993422, 313498126, 319684230, 329382926, 336330309, 346848320, 1076726789, 1074653189, 355324942, 363829390, 370015814, 378535495, 388791488, 396990987, 405657294, 413269198, 422345856, 428463817, 439326926, 446848714, 456381968, 464100043, 472014346, 481547984, 487692945, 497441868, 503961097, 512753159, 521247441, 531397632, 538155667, 548656784, 556686532, 563190353, 571070025, 581852292, 588487379, 598988368, 605028039, 615406596, 622041683, 630707861, 638582407, 648961092, 1076499463, 655596051, 664524436, 674258578, 680630801, 689690132, 697171654, 707812882, 1075201992, 1074176008, 713931405, 722982613, 730725894, 741367378, 1076023302, 747485709, 756799060, 766533330, 772651597, 781579862, 790265423, 798357142, 807042767, 1074987971, 1073964035, 815519444, 823819791, 832034389, 840597135, 848688854, 857077270, 865588757],
    [114, 100, 9, 2202753, 8772608, 17161280, 25550016, 33938560, 44145729, 51215945, 59238090, 68672585, 77700097, 1073744835, 1074285571, 1074566082, 1074850818, 84770441, 95012356, 101309444, 110747212, 119004297, 128171084, 1076696064, 135233165, 144828107, 151641732, 1075140609, 161078924, 1075420161, 170114188, 1075701760, 177176269, 186771019, 193584836, 1076506625, 203021836, 1077048321, 212057100, 219119117, 228713995, 235527748, 244965068, 254000332, 1077313540, 262268555, 269450829, 279026881, 285992655, 294485513, 303553545, 312851520, 319546959, 328040137, 337108169, 346406080, 353101327, 361987793, 371571712, 1073924037, 378005002, 387153553, 396737664, 405765780, 411821711, 421780628, 430554253, 439320276, 447604371, 455335124, 464108621, 472874516, 481289938, 488889364, 497662989, 506429012, 514844306, 522443860, 531217613, 538148433, 545777290, 556646094, 563314193, 570943050, 581811854, 588873301, 598730258, 606977550, 614039061, 623494340, 632143438, 639205077, 648930899, 656121552, 1074209735, 664370837, 673825924, 681287184, 689528534, 698991684, 706453136, 714694230, 724559442, 731618896, 1076062150, 739859990, 749594323, 756792840, 765025942, 774759955, 781958792, 790480407, 798735944, 807257815, 815513288, 824034903, 832423575],
]


def fill_table(table, me, low, high):
    if high - low == 1:
        for place, word in enumerate(STEPS[low]):
            table[place] = jnp.int32(word)
        return
    middle = (low + high) // 2
    lax.cond(
        me < middle,
        lambda: fill_table(table, me, low, middle),
        lambda: fill_table(table, me, middle, high),
    )


def neighbours(col, row):
    x = lax.rem(col, 2) * 2 + lax.rem(row // 2, 2)
    y, z, core = col // 2, row // 4, lax.rem(row, 2)
    found = [(x, y, z, 1 - core)]
    for move in (1, 3):
        for other in range(2):
            found.append((lax.rem(x + move, 4), y, z, other))
            found.append((x, lax.rem(y + move, 4), z, other))
            found.append((x, y, lax.rem(z + move, 4), other))
    return [{"col": y * 2 + x // 2, "row": z * 4 + lax.rem(x, 2) * 2 + core} for x, y, z, core in found]


def split(value):
    high = value.astype(jnp.bfloat16)
    return high, (value - high.astype(jnp.float32)).astype(jnp.bfloat16)


def spread_kernel(
    stored_ref, slots_ref, halves_ref,
    table, tile_even, tile_odd, halves_even, halves_odd, load_sem, store_sem, send_sem, recv_sem,
):
    active, half, block = stored_ref.shape[2:5]
    rows_per = active // CHUNKS
    col, row = lax.axis_index("col"), lax.axis_index("row")
    beside = neighbours(col, row)
    sibling = beside[0]
    tiles = halves_ref.shape[0]

    barrier = pltpu.get_barrier_semaphore()
    for device in beside:
        pl.semaphore_signal(barrier, inc=1, device_id=device, device_id_type=MESH)
    fill_table(table, col * lax.axis_size("row") + row, 0, len(STEPS))
    pl.semaphore_wait(barrier, len(beside))

    def hop(source, slot, chunk, place, device):
        return pltpu.make_async_remote_copy(
            src_ref=source,
            dst_ref=slots_ref.at[slot, pl.ds(chunk * rows_per, rows_per)],
            send_sem=send_sem.at[place],
            recv_sem=recv_sem.at[slot, chunk],
            device_id=device,
            device_id_type=MESH,
        )

    def arrival(slot, chunk):
        piece = slots_ref.at[slot, pl.ds(chunk * rows_per, rows_per)]
        hop(piece, slot, chunk, 0, sibling).wait_recv()

    tile = (tile_even, tile_odd)
    halves = (halves_even, halves_odd)

    def load(source, turn):
        return pltpu.make_async_copy(source, tile[turn], load_sem.at[turn])

    def store(turn, role):
        return pltpu.make_async_copy(halves[turn], halves_ref.at[role], store_sem.at[turn])

    def prepare(turn, order, role):
        load(slots_ref.at[0], turn).wait()

        @pl.when(order >= 2)
        def _():
            store(turn, 0).wait()

        for mirrored in range(2):
            @pl.when((role & 1) == mirrored)
            def _():
                @pl.loop(0, active)
                def _(line):
                    for slot in range(half):
                        value = tile[turn][line, slot]
                        high, low = split(value.T if mirrored else value)
                        halves[turn][line * half + slot, :block] = high
                        halves[turn][line * half + slot, block:] = low

        store(turn, role).start()

    steps = table[0]
    sends = table[1]

    @pl.loop(0, steps)
    def _(step):
        word = table[3 + step]
        slot = word & 63

        @pl.when((word >> 30) == 0)
        def _():
            chunk = (word >> 6) & 7
            device = {"col": (word >> 10) & 7, "row": (word >> 13) & 15}
            landing = (word >> 17) & 63
            place = (word >> 23) & 127

            @pl.when(((word >> 9) & 1) == 1)
            def _():
                arrival(slot, chunk)

            @pl.when(slot < 2)
            def _():
                piece = stored_ref.at[slot, 0, pl.ds(chunk * rows_per, rows_per)]
                hop(piece, landing, chunk, place, device).start()

            @pl.when(slot >= 2)
            def _():
                piece = slots_ref.at[slot, pl.ds(chunk * rows_per, rows_per)]
                hop(piece, landing, chunk, place, device).start()

        @pl.when((word >> 30) != 0)
        def _():
            order = (word >> 14) & 15
            for chunk in range(CHUNKS):
                @pl.when(((word >> (6 + chunk)) & 1) == 1)
                def _():
                    arrival(slot, chunk)

            for turn in range(2):
                @pl.when((order & 1) == turn)
                def _():
                    @pl.when(slot < 2)
                    def _():
                        load(stored_ref.at[slot, 0], turn).start()

                    @pl.when(slot >= 2)
                    def _():
                        load(slots_ref.at[slot], turn).start()

                    @pl.when(order >= 1)
                    def _():
                        prepare(1 - turn, order - 1, (word >> 18) & 15)

    prepare((tiles - 1) % 2, tiles - 1, table[2])

    @pl.loop(0, sends)
    def _(place):
        hop(slots_ref.at[0, pl.ds(0, rows_per)], 0, 0, place, sibling).wait_send()

    for turn in range(2):
        store(turn, 0).wait()


def spread(stored):
    most = max(entry[1] for entry in STEPS)
    active, half, block = stored.shape[2:5]
    return pl.pallas_call(
        spread_kernel,
        out_shape=(
            jax.ShapeDtypeStruct((SLOTS,) + stored.shape[2:], jnp.float32),
            jax.ShapeDtypeStruct((14, active * half, 2 * block, block), jnp.bfloat16),
        ),
        in_specs=[pl.BlockSpec(memory_space=pl.ANY)],
        out_specs=(pl.BlockSpec(memory_space=pl.ANY),) * 2,
        scratch_shapes=[
            pltpu.SMEM((max(len(entry) for entry in STEPS),), jnp.int32),
            pltpu.VMEM((active, half, block, block), jnp.float32),
            pltpu.VMEM((active, half, block, block), jnp.float32),
            pltpu.VMEM((active * half, 2 * block, block), jnp.bfloat16),
            pltpu.VMEM((active * half, 2 * block, block), jnp.bfloat16),
            pltpu.SemaphoreType.DMA((2,)),
            pltpu.SemaphoreType.DMA((2,)),
            pltpu.SemaphoreType.DMA((most,)),
            pltpu.SemaphoreType.DMA((SLOTS, CHUNKS)),
        ],
        compiler_params=pltpu.CompilerParams(
            collective_id=0, has_side_effects=True, vmem_limit_bytes=24 << 20
        ),
        name="spread",
    )(stored)[1]


def multiply_kernel(
    halves_ref, rows_ref, offs_ref, krow_ref, kcol_ref, kcnt_ref, out_ref,
    blocks, done, pairs, pair_count, bucket, bucket_count, facts, in_sem, out_sem,
):
    grid = lax.axis_size("row")
    tile_j = lax.axis_index("row")
    col_id = lax.axis_index("col")
    tiles, each = halves_ref.shape[:2]
    half = offs_ref.shape[-1]
    active = each // half
    block = halves_ref.shape[-1]
    lanes, _, kept = krow_ref.shape
    slots = 2 * half
    steps = 2
    most = steps * slots * slots

    def load(place):
        return pltpu.make_async_copy(
            halves_ref.at[place], blocks.at[pl.ds(place * each, each)], in_sem.at[place]
        )

    for place in range(tiles):
        load(place).start()

    first = rows_ref[0, 0]
    bits = [rows_ref[0, 1] ^ first, rows_ref[0, 2] ^ first, rows_ref[0, 4] ^ first]

    def rank(value):
        return sum(
            jnp.where((value & bit) != 0, jnp.int32(1 << place), jnp.int32(0))
            for place, bit in enumerate(bits)
        )

    def shifts(tile_x, tile_y):
        both = ((tile_x, tile_y), (tile_y, tile_x))
        return [rank(offs_ref[x, y, slot]) for x, y in both for slot in range(half)]

    tile_is = [col_id * lanes + lane for lane in range(lanes)]
    tile_ks = [lax.rem(tile_is[0] + tile_j + place, grid) for place in range(3)]
    right_moves = [shifts(tile_k, tile_j) for tile_k in tile_ks]

    for place in range(lanes * active):
        pair_count[place] = 0
    for lane in range(lanes):
        for step in range(steps):
            left_moves = shifts(tile_is[lane], tile_ks[lane + step])
            for slot in range(slots):
                move = left_moves[slot]
                turn = move if slot >= half else 0
                left_base = (2 * (2 * lane + step) + slot // half) * each + slot % half
                for other in range(slots):
                    apart = move ^ right_moves[lane + step][other]
                    place = lane * active + apart
                    count = pair_count[place]
                    right_base = (8 + 2 * (lane + step) + other // half) * each + other % half
                    reach = move if other < half else apart
                    pairs[place * most + count] = (
                        turn | reach << 3 | left_base << 6 | right_base << 14
                    )
                    pair_count[place] = count + 1

    widest = 4
    room = 2 * lanes * kept
    for place in range(widest + 1):
        bucket_count[place] = 0
    for place in range(lanes * active):
        pair_count[place] = place << 3 | pair_count[place] << 7

    def put(size, word):
        filled = bucket_count[size]
        bucket[size * room + filled] = word
        bucket_count[size] = filled + 1

    for lane in range(lanes):
        count = kcnt_ref[lane, 0]
        together = 8

        @pl.loop(0, kept // together)
        def _(part):
            found = []
            for offset in range(together):
                item = part * together + offset
                row = rank(krow_ref[lane, 0, item])
                place = lane * active + (row ^ rank(kcol_ref[lane, 0, item]))
                found.append(jnp.where(item < count, pair_count[place] | row, 0))
            for offset in range(together):
                item = lane * kept + part * together + offset
                products = found[offset] >> 7
                facts[item] = found[offset] & 127
                begin = jnp.where(products > 0, ((products - 1) & 7) + 1, 0)
                put((begin + 1) >> 1, item | begin << 13)

                @pl.loop(0, (products - begin) >> 3)
                def _(more):
                    put(widest, item | (begin + 8 * more) << 7 | 1 << 12 | 8 << 13)

    blocks[tiles * each] = jnp.zeros((2 * block, block), jnp.bfloat16)
    for place in range(tiles):
        load(place).wait()

    def gather(word, size):
        fact = facts[word & 127]
        row = fact & 7
        base = (fact >> 3) * most + ((word >> 7) & 31)
        products = word >> 13
        ones, twos = [], []
        for place in range(2 * size):
            inside = place < products
            code = pairs[base + jnp.where(inside, place, 0)]
            source = ((code >> 6) & 255) + (row ^ (code & 7)) * half
            ones.append(blocks[jnp.where(inside, source, tiles * each)])
            other = blocks[(code >> 14) + (row ^ ((code >> 3) & 7)) * half]
            twos.append(jnp.concatenate([other[:block], other[block:]], 1))
        total = jnp.dot(
            jnp.concatenate(ones, 1), jnp.concatenate(twos, 0), preferred_element_type=jnp.float32
        )
        total = total[:block] + total[block:]
        return total[:, :block] + total[:, block:]

    def add(word, into, total):
        again = ((word >> 12) & 1) == 1

        @pl.when(again)
        def _():
            done[into] = done[into] + total

        @pl.when(jnp.logical_not(again))
        def _():
            done[into] = total

    @pl.loop(0, bucket_count[0])
    def _(place):
        done[bucket[place] & 127] = jnp.zeros((block, block), jnp.float32)

    for size in range(1, widest + 1):
        count = bucket_count[size]

        @pl.loop(0, (count + 1) >> 1)
        def _(place):
            start = size * room + 2 * place
            one = bucket[start]
            paired = 2 * place + 1 < count
            two = bucket[jnp.where(paired, start + 1, start)]
            total_one = gather(one, size)
            total_two = gather(two, size)
            if size < widest:
                done[one & 127] = total_one
                done[jnp.where(paired, two & 127, lanes * kept)] = total_two
            else:
                add(one, one & 127, total_one)
                add(jnp.where(paired, two, 0), jnp.where(paired, two & 127, lanes * kept), total_two)

    def store(lane):
        return pltpu.make_async_copy(
            done.at[pl.ds(lane * kept, kept)], out_ref.at[lane, 0], out_sem.at[lane]
        )

    for lane in range(lanes):
        store(lane).start()
    for lane in range(lanes):
        store(lane).wait()


def multiply(halves, tile_rows, offsets, kept_rows, kept_cols, kept_count):
    block = halves.shape[-1]
    half = offsets.shape[-1]
    tiles, each = halves.shape[:2]
    active = each // half
    lanes, _, kept = kept_rows.shape
    items = lanes * kept
    products = 2 * (2 * half) ** 2
    smem = pl.BlockSpec(memory_space=pltpu.SMEM)
    return pl.pallas_call(
        multiply_kernel,
        out_shape=jax.ShapeDtypeStruct((lanes, 1, kept, block, block), jnp.float32),
        in_specs=[pl.BlockSpec(memory_space=pl.ANY)] + [smem] * 5,
        out_specs=pl.BlockSpec(memory_space=pl.ANY),
        scratch_shapes=[
            pltpu.VMEM((tiles * each + 1, 2 * block, block), jnp.bfloat16),
            pltpu.VMEM((items + 1, block, block), jnp.float32),
            pltpu.SMEM((lanes * active * products,), jnp.int32),
            pltpu.SMEM((lanes * active,), jnp.int32),
            pltpu.SMEM((10 * items,), jnp.int32),
            pltpu.SMEM((5,), jnp.int32),
            pltpu.SMEM((items,), jnp.int32),
            pltpu.SemaphoreType.DMA((tiles,)),
            pltpu.SemaphoreType.DMA((lanes,)),
        ],
        compiler_params=pltpu.CompilerParams(vmem_limit_bytes=32 << 20),
        name="multiply",
    )(halves, tile_rows, offsets, kept_rows, kept_cols, kept_count)


def local(stored, tile_rows, offsets, kept_rows, kept_cols, kept_count):
    halves = spread(stored)
    return multiply(halves, tile_rows, offsets, kept_rows, kept_cols, kept_count)


def solution(mesh):
    in_specs = (
        P("col", "row", None, None, None, None),
        P(),
        P(),
        P("col", "row", None),
        P("col", "row", None),
        P("col", "row"),
    )
    out_specs = P("col", "row", None, None, None)
    return jax.shard_map(local, mesh=mesh, in_specs=in_specs, out_specs=out_specs, check_vma=False)
```

```python
import jax
import jax.numpy as jnp
from jax import lax
from jax.experimental import pallas as pl
from jax.experimental.pallas import tpu as pltpu
from jax.sharding import PartitionSpec as P

MESH = pl.DeviceIdType.MESH
CHUNKS = 4
SLOTS = 33
STEPS = [
    [118, 104, 12, 1851393, 9576640, 17965056, 26353792, 34742336, 42213377, 50602177, 58990721, 69223106, 75767873, 84286154, 92963528, 102113929, 1073746370, 1074811906, 111558793, 1075088323, 1074326531, 119675597, 128090700, 135799499, 1076690944, 1073824768, 144720002, 1074105345, 151394826, 161645260, 169353739, 178929675, 1074651136, 1075979264, 1076258817, 187185861, 193626760, 201990341, 211165705, 220217346, 227287750, 237116045, 245531276, 252322373, 261628491, 269369484, 277619270, 287848517, 295862796, 302653957, 311829193, 321273865, 327950854, 338180101, 346718927, 352985733, 362291851, 371867787, 1076540421, 378282630, 388511877, 397050511, 404103753, 413548617, 1077337094, 419830410, 429670465, 438835728, 445284872, 455491785, 462062152, 472390288, 479084620, 488774221, 496779457, 505944784, 512664211, 521027596, 530070033, 539656783, 548552840, 554048074, 565215829, 572276865, 581048845, 588161747, 598360139, 605567569, 615547605, 624050184, 1075780548, 631773776, 640320015, 648036418, 656161490, 663659091, 674652814, 681065105, 691045013, 699547848, 707803732, 716210709, 724189387, 731396817, 739156499, 750150222, 1075540935, 756824722, 765100566, 772686028, 781990418, 790266518, 800211016, 808467092, 815432278, 825647822, 832322130, 840598230, 850813454, 858798804, 867187220],
    [106, 92, 13, 1860608, 10321984, 17039553, 25428033, 33816705, 42205185, 50725056, 59113536, 67502080, 77430912, 85746816, 92668032, 102917769, 110985216, 117713547, 1073743810, 126354052, 1074020352, 136078528, 143622794, 153365196, 159908420, 170288332, 178627213, 1073782785, 1075897345, 186919436, 194798656, 202342986, 209988107, 220358153, 229343817, 237906574, 245785612, 254517904, 262416972, 270689993, 279290445, 288238286, 296117900, 304849616, 1076169669, 313403918, 319291908, 1074354118, 1075161094, 330006537, 338715652, 346958414, 354575433, 363569680, 371468428, 380658756, 388735568, 394537675, 405824644, 412058122, 420358739, 430335052, 438673933, 445655700, 454313685, 462389962, 470682198, 480084160, 487867989, 495856339, 503841476, 514556041, 523265220, 1076482052, 1074932740, 529664658, 538199573, 547726029, 554576403, 562954823, 573276361, 580273873, 588384786, 596509383, 605308565, 614179535, 621816404, 630063751, 638994065, 647733775, 655239827, 663618055, 672548369, 681288335, 1076775943, 688925204, 698065487, 1074700232, 1075769352, 705563286, 714491473, 722340374, 1077091267, 1075540995, 730868436, 739379922, 746859083, 756157010, 764283606],
    [142, 128, 10, 2368576, 8673472, 18636929, 27025601, 35545280, 43802689, 52191233, 60710912, 69099584, 77865984, 86399554, 94265472, 103047694, 111567364, 1073744706, 119953538, 127796228, 1074287555, 136864464, 1074823168, 142893649, 153508034, 161481809, 170050130, 176579270, 185098899, 193225361, 203839490, 211944595, 218522246, 229139088, 235168273, 246176399, 253756433, 260629012, 269246997, 277111505, 288249870, 295699665, 304267794, 313025040, 321282628, 330062543, 337642641, 346211026, 353264263, 361783944, 371467456, 380786704, 388948566, 394813971, 405168772, 412115464, 422729872, 430048275, 439140373, 445407893, 455500484, 464672976, 471729348, 1073803268, 481083541, 487088723, 497834511, 505545811, 512123462, 523166422, 530866766, 539908174, 547226756, 554066438, 565109398, 570974931, 581720655, 589432019, 1076956166, 598663702, 604922439, 613442120, 621041792, 631112772, 639812242, 648307406, 656680064, 665737422, 672195096, 680419847, 688939720, 696539136, 706356232, 1074616328, 714138328, 722756249, 730093632, 739509401, 747692696, 757359246, 766400654, 773596295, 780722900, 789340757, 798631112, 806771333, 1075414725, 816627797, 823419417, 832337926, 840172569, 847831636, 858284624, 867326032, 874259527, 881910360, 890905672, 899446918, 907469463, 915694297, 924612806, 932447449, 1074132937, 941023959, 948724437, 958014600, 966154437, 1077289930, 1075995658, 976011477, 982931461, 991699975, 998826644, 1007575751, 1016887366, 1025254599, 1076272135, 1033298519, 1041523289, 1050040389, 1058276441, 1075763149, 1066852887, 1075261387, 1076849612],
    [102, 88, 9, 401537, 10076353, 17055808, 25444544, 33832960, 42221696, 50741249, 59129985, 67518529, 76030606, 85573697, 92684481, 103303888, 109584974, 119128193, 126501457, 136858128, 1073741824, 143262415, 152682497, 162024080, 168428111, 176677588, 187189840, 193593871, 201974290, 213019158, 218759823, 227271381, 237914711, 245883589, 253755923, 1073771458, 263350998, 268968462, 279437957, 287826437, 295699027, 305293910, 312476307, 321635032, 327828177, 336612057, 346030803, 355189400, 364014230, 371859458, 380355160, 1076928457, 386943577, 394912338, 405414082, 414075543, 422191170, 428982810, 1075627971, 1074076612, 439241239, 445129422, 455598661, 1075407877, 462045713, 472795863, 478798546, 489300098, 495995545, 504242257, 512483861, 1076728776, 520766097, 529549849, 537796817, 548127256, 554295954, 562962577, 571351057, 579592853, 587603969, 596370005, 605702811, 612885140, 621158593, 631139036, 637935681, 647086682, 656304732, 663216660, 673081884, 680641242, 1074908102, 1074408395, 1076525005, 689859228, 696771156, 706366043, 714195610, 1077319623, 723143387, 1075236810, 731531803, 1074734028, 1076061196],
    [110, 96, 10, 2275328, 10543105, 18677761, 27041856, 35430592, 43819008, 52207744, 60995648, 69263489, 77669058, 1073746370, 86161600, 94445570, 100983311, 1074809795, 1074298880, 111327360, 119611522, 126149327, 134912001, 144777282, 151315023, 161284161, 168343682, 176734739, 185115335, 195371207, 201900627, 210680340, 220004481, 226812559, 235838149, 243835463, 252229634, 262479943, 269009619, 277389959, 285784130, 296034439, 302563987, 1073800132, 1075913732, 311075541, 320921665, 329056449, 336894609, 1076195270, 344629909, 353015937, 363921943, 372294226, 378053127, 388030657, 396697607, 403618452, 1076729863, 411998725, 422642263, 431014418, 437172820, 445850198, 456180370, 1075430789, 1074149321, 462723665, 472957650, 479404566, 489997008, 496286283, 504013397, 514917015, 523551312, 529840779, 540082903, 546609873, 556982862, 1077302859, 563552856, 571390676, 582271504, 588718808, 596949003, 607314574, 613065237, 622107153, 632480462, 638788246, 647280843, 657646094, 664216216, 1075229640, 674546320, 680433733, 689381912, 696948929, 706396309, 714285782, 722114625, 731562005, 739942925, 1077071820, 747157698, 756728021, 765108877, 772708485, 781893717, 790274637, 798663373, 1074732045, 1075801034],
    [114, 100, 5, 1869888, 9568385, 17072193, 25460929, 33849473, 42237953, 50757632, 59146304, 67534976, 76939982, 85755904, 92700864, 103597583, 109608975, 118882830, 127699072, 137283088, 143425552, 1073741824, 152864960, 160563201, 170837712, 176980176, 185991758, 195471874, 204392080, 210534544, 219283649, 229026370, 237815503, 243826895, 253100686, 262843076, 271369807, 277381199, 286392385, 296135298, 304924303, 310935695, 321135171, 330213969, 338609744, 344752208, 354820676, 363505732, 370075156, 380534804, 387089043, 396763332, 405973650, 414246549, 422478420, 429032019, 438837250, 447916754, 456442963, 462586387, 472391810, 481471058, 489998035, 496140499, 506208320, 1073762628, 1074829826, 515025426, 523551763, 530850499, 540445206, 548464341, 556016259, 1075365955, 563643015, 573220868, 579789908, 590250644, 598089732, 606775428, 613344980, 623804628, 631513091, 640067778, 649381011, 656941122, 664306375, 674147025, 680453268, 690364548, 699828822, 706660055, 715923648, 724994710, 733013525, 741089408, 1074342854, 748192327, 758032913, 765380183, 1076453317, 774643712, 783198865, 790546071, 799547586, 808880854, 816899669, 823689735, 832488983, 1075676167, 1074130888, 1076770761, 1077310412, 1077060555, 1076028427, 1076301770, 1074747341],
    [118, 104, 5, 2401280, 10803264, 18669697, 27058369, 35446785, 43966592, 52355136, 60743680, 69001281, 77912064, 86419074, 94298304, 102711951, 111337615, 1073744578, 119855232, 128230528, 1074287555, 136266447, 144892111, 1074823168, 153409728, 161915970, 170345104, 178970768, 187081730, 196016272, 203375183, 212000847, 220636354, 227072590, 238109265, 245555727, 254059712, 260627086, 270483471, 277537284, 288023248, 296395780, 305068240, 312950992, 319480388, 329966160, 338338884, 347011152, 355549713, 363111488, 372570708, 380715729, 386589380, 397074960, 405447876, 414119952, 422002704, 428532356, 439002244, 445709011, 1073797124, 455827990, 462456339, 470874771, 1075394501, 481903125, 487651347, 495888087, 507069141, 512665175, 522666064, 529326809, 537953427, 548364505, 554492441, 562996887, 573530137, 579926611, 1077233607, 588285011, 599063252, 607208081, 613212761, 622232654, 631036506, 641286805, 647399118, 657416281, 663279822, 672827026, 682320534, 691337748, 697098905, 706381522, 1074114505, 716136601, 724892308, 731285006, 741040726, 747165710, 1076751307, 756057299, 765254170, 775504469, 781878802, 1076507592, 790420122, 798712344, 1077043148, 806266391, 815586010, 823878232, 831947918, 841704150, 848987730, 857432792, 1075749834, 1076028426, 865821336, 1076301766, 1074747341],
    [114, 100, 7, 2418752, 8691777, 18899137, 25477184, 33865856, 42254336, 50643136, 59162817, 67551233, 75939905, 86304896, 92577793, 102785025, 109494401, 117875407, 128248000, 136339585, 1073741824, 143041103, 153116737, 160090771, 168723150, 179069442, 187222740, 193241217, 204235458, 210422355, 219169424, 227443278, 238479554, 244335120, 252609166, 262720148, 269271556, 280422978, 288120898, 296264195, 305588866, 313680598, 321430083, 1073764354, 329574400, 336495118, 346841218, 353288791, 1075360515, 361808472, 369402049, 381085698, 389177942, 394699407, 403718736, 411749075, 1076941765, 420528856, 428253711, 439509526, 445563607, 453691923, 462439120, 472424579, 479117975, 489841302, 497590467, 504283671, 512901845, 523149528, 529580696, 538600017, 548315288, 555270664, 563233365, 573481048, 580436680, 589875732, 596787861, 605201106, 613991048, 623430228, 630874833, 638886039, 646759108, 656067161, 663896597, 672309778, 681233049, 689594897, 697606167, 705479236, 1074858950, 714787545, 722518552, 731538065, 741253144, 748208712, 756730393, 1074353160, 764584530, 1075163079, 773777946, 781361810, 790555226, 798269655, 807332506, 815046743, 1076754378, 822919812, 832498394, 1077281796, 1074160585, 1076012041, 1076292556, 1076563915, 1074749389],
    [86, 72, 13, 2430976, 10453056, 18686017, 27074561, 35463361, 43851905, 52762816, 61309442, 69288655, 1073744770, 77928576, 86474882, 1074287555, 94454287, 1074823168, 103094336, 111640642, 120144530, 128417986, 137443920, 145310290, 153059328, 162469953, 169951887, 178225280, 187775696, 195641874, 203391168, 212801537, 220283471, 229483022, 238107152, 246759955, 254648974, 263273104, 271925843, 279814734, 288299201, 297091795, 305076353, 313491972, 322257555, 330146510, 336534225, 346907284, 355435204, 362093142, 372072980, 380600900, 387258902, 1073797380, 396968658, 405766276, 412432920, 422404820, 428808785, 1075389381, 1075930117, 437338320, 445585937, 455959124, 462756566, 470892624, 479541912, 1076212678, 488063637, 496319192, 504446992, 512694929, 521626327, 529873496, 538395157, 546642582, 555180631, 1077008327, 563569303, 571555984, 1075195849, 580338261, 588734999, 1076776906, 1074700236, 1075759051, 1074211784, 597115605, 1076590541],
    [102, 88, 10, 2450560, 10387457, 19212353, 25493568, 33882112, 42270848, 50659520, 59179137, 67567809, 75956289, 86336512, 94709889, 102662337, 109510657, 119734863, 128279616, 136216641, 145304258, 153289231, 1073741824, 161907214, 170469890, 179135503, 186843791, 195461710, 204024450, 212690063, 220398287, 228491393, 237578818, 246244559, 1073764354, 254478992, 262570702, 271410255, 277414532, 287663296, 296125070, 304424961, 310969028, 321168003, 330524370, 338634948, 344523268, 355411972, 363111107, 372467282, 380831939, 388276803, 397633170, 405997635, 413442563, 422774787, 1075349507, 429294291, 436798020, 447686724, 1074319364, 454459987, 462636628, 472852612, 481519122, 488014483, 498272387, 504791571, 513631766, 521470537, 531302992, 538527317, 548080144, 555024905, 563693077, 573246160, 1074869189, 580470485, 589637825, 597517974, 605882897, 1076983752, 614024853, 622660177, 1077256135, 630784652, 639460950, 647826129, 655950412, 663963348, 672991889, 680854153, 689129108, 697893580, 706569942, 1075700683, 1075979275, 714294804, 722797257, 731447820, 1076252618, 1074693129, 1074189324, 1075261382, 1076849613],
    [110, 96, 7, 2447488, 10313793, 18702337, 27222080, 35610624, 43868289, 52388032, 60776576, 69556416, 77422785, 86333440, 1073744835, 1074287554, 1074823168, 94722112, 102621839, 109520592, 120412686, 127787727, 137307794, 145578574, 153477779, 160106193, 170744526, 178766484, 185271825, 195519127, 204298894, 212320852, 218572432, 226976344, 237730453, 245875220, 252380817, 262896213, 270393871, 277546577, 288061973, 295559759, 305079826, 311255578, 319250968, 328423444, 338543194, 347023058, 353198170, 361194200, 371679767, 378755220, 388874970, 395141338, 405743186, 412449371, 422429338, 428695706, 439551192, 447445717, 455467731, 464716824, 472343127, 479549980, 489537562, 498271320, 504715996, 514187859, 521348825, 531063511, 538139348, 547864788, 554116688, 563444443, 572908051, 580215496, 588711510, 596858964, 607109333, 615712408, 621240472, 630553243, 640663637, 647431830, 655712840, 1073795015, 664107547, 674218005, 679945744, 689265308, 699383957, 706552983, 714433032, 722929366, 731063961, 1074599878, 739596892, 748496087, 1075147716, 756229721, 1076987850, 765273175, 773153416, 1074124808, 781649430, 1075454924, 1075995660, 790438935, 798172697, 1076279237, 1077342155, 1076833225, 1076584397],
    [98, 84, 13, 2312384, 8724673, 17121281, 25641152, 34029632, 42418176, 50675777, 59195520, 67453057, 77809664, 84221953, 92618945, 102975552, 109387905, 118047312, 1073741824, 128141440, 134553665, 143073935, 151603919, 159982222, 168388673, 176866001, 185158159, 193536718, 203997778, 210313742, 218720385, 227197457, 235489871, 243736783, 252363345, 260513871, 269568724, 277291023, 285829121, 294306449, 302588494, 311511700, 321462352, 328288788, 336152719, 346890754, 353724949, 361832979, 370590358, 1073761222, 378104001, 386998931, 396935890, 405611138, 412174932, 420430409, 429310486, 437330515, 445596297, 456870615, 462865110, 470885075, 479150793, 490424855, 497598994, 504316425, 514376338, 523051586, 1074299913, 529973846, 539566800, 545865936, 1074061253, 1075646403, 557533783, 563405528, 573121168, 579420304, 588606101, 596959896, 607865495, 613736984, 623715010, 1074622466, 630549077, 638902872, 648618512, 654917648, 664486413, 1076998087, 672875085, 680880853, 1076745162, 1074932684, 689652429, 1076517828, 1075487691, 1076028427, 698040973, 1076302861, 1075279816],
    [106, 92, 13, 1310912, 10330177, 18849856, 27107457, 35627200, 43884545, 52273345, 60799618, 69181440, 77202114, 85958784, 92914254, 101163537, 111254211, 1073746114, 118751232, 1074809283, 128041551, 134718033, 1074298880, 144808003, 152699010, 161473168, 168403653, 178362499, 186393235, 195027472, 203661959, 211793922, 218735109, 228336147, 236970704, 243901061, 253737026, 261890771, 270525008, 279159367, 287414275, 294232645, 303300736, 1073797125, 311403028, 321511495, 329234626, 337388115, 346145423, 352821969, 363575826, 370802754, 378512020, 388620423, 394764945, 405518930, 413270097, 420455124, 430031375, 437494358, 447462034, 455213073, 463585999, 471048726, 481016530, 488898693, 495567502, 504603350, 515086871, 522715222, 529121806, 538157718, 546570304, 554672724, 565418711, 573170183, 581148679, 588906498, 596501013, 607361623, 614727749, 624138903, 631890631, 639869127, 648544278, 1075385351, 654951118, 665059525, 671998613, 681705617, 689291284, 698613765, 705553109, 715260113, 1075136457, 722845844, 732430550, 1074111432, 1075962888, 739622996, 749207702, 755884629, 764788948, 1076243398, 1076523980, 1077059531, 1075761101, 1074737092, 1076852682],
    [110, 96, 11, 370753, 10347585, 17137793, 25526465, 33914881, 42303553, 50823360, 59211904, 69272142, 75988992, 84379726, 94233729, 101154880, 111608335, 117934734, 127788225, 1073741824, 136774287, 143100622, 152953857, 161546446, 170124352, 176654862, 187105999, 193694287, 203678848, 210993810, 220266510, 228844544, 235251713, 245432462, 252414159, 262399168, 270991439, 277857796, 285977233, 1073763204, 296166032, 303023300, 311274132, 320045650, 329720528, 336570902, 344974851, 354886160, 361736854, 370140739, 1074830083, 380052048, 387434057, 395291222, 405479960, 411797519, 420463748, 429359626, 439034456, 445622998, 454026371, 462619347, 470132929, 479192259, 1075366729, 1074335687, 487817746, 497754840, 504349764, 512600596, 522920600, 530039945, 537766612, 546505299, 555205833, 562801361, 571933205, 579569807, 588760073, 596869842, 605758039, 614303762, 622297802, 630923991, 639469650, 647463498, 656114381, 663945747, 671853137, 681280013, 689373909, 698189970, 1074623432, 1077000140, 706445965, 714277523, 721791105, 731349642, 740000333, 748094037, 755870292, 1077269514, 1075184653, 764871317, 772516369, 1074159563, 1075749826, 1076028418, 781918743, 790464722, 1076308933, 1076588486, 798696087],
    [98, 84, 10, 2589760, 9691329, 18079745, 26599552, 34988096, 43245633, 51765248, 60703234, 68411521, 78087360, 85319872, 95148748, 102646338, 1073744642, 111641728, 1074287555, 120314444, 1074823168, 127811714, 134973005, 142991940, 153868940, 161211022, 169754818, 179012748, 187423244, 194765326, 1073803264, 204366416, 212304896, 220592783, 227247821, 237369871, 245097038, 254903438, 261251793, 271317650, 280069198, 286417425, 297130643, 303817422, 313230540, 319971921, 330685011, 338396236, 345137809, 355203666, 363955214, 372138640, 380369426, 388727820, 397304336, 406182419, 411797133, 422470352, 431610454, 439452878, 444981892, 456776406, 462128653, 470147588, 481942166, 488220245, 497810130, 505119830, 515496470, 521896982, 530971215, 538551957, 545645252, 557177555, 563717845, 1076960260, 571865748, 580617366, 590897879, 598080207, 605783254, 616063575, 1075665861, 622197332, 630826517, 641229335, 646963915, 655751892, 666395287, 1075419078, 1075176391, 1075979271, 672129547, 680917524, 1076260809, 688906891, 1076791242, 1074197514, 697295435, 1077349387, 1074752456],
    [106, 92, 9, 2326529, 8765440, 17154176, 25542848, 33931328, 42450945, 50839617, 59228289, 69435457, 76005569, 84640457, 1073741824, 93028873, 101051083, 109806217, 1073768448, 1076408321, 118194761, 126470798, 136945806, 143248078, 151732944, 160154116, 170098881, 178907794, 185164433, 193839813, 203653249, 210618895, 221086282, 227011283, 235627092, 246006293, 254640650, 263055381, 269443670, 279806666, 285731475, 294347412, 304972426, 311020046, 319775446, 329884238, 336062995, 346669653, 353059408, 363438094, 372107349, 380224149, 387015191, 395035204, 405381326, 414050453, 420438678, 429499021, 438954706, 445342228, 455721685, 463045196, 472770773, 479412888, 487310020, 496599564, 506063442, 512451284, 520995333, 530162381, 537389651, 545874513, 555328077, 564783634, 571687448, 579584644, 1076942786, 588882445, 595978763, 1075122180, 605119191, 613270149, 622428812, 629533323, 638673559, 646824517, 655983308, 663603855, 1074885637, 671703569, 680381007, 688874006, 696895566, 705905368, 1077251014, 1074383878, 713419339, 722158096, 730712783, 738812625, 1074666435, 1075469315, 747324048, 1075742663, 1074195463, 756236888, 764502615, 1076831176, 1076061192],
    [122, 108, 13, 1449152, 10363968, 18752704, 27272257, 35529728, 44049409, 52307072, 60826817, 68959820, 77603969, 85870285, 94125580, 102647373, 110902924, 119424525, 126363151, 136068812, 1073750016, 144590477, 1075865601, 154043984, 160179280, 169221184, 176965134, 187213457, 193864849, 203300421, 210519694, 221414996, 227288592, 236329984, 244204559, 254706704, 260843216, 269493909, 279321615, 286278805, 1076403142, 296649936, 302786192, 311827584, 321406487, 330204304, 336076499, 344737358, 355632660, 361637393, 369761814, 380126807, 388539409, 394798799, 404104857, 413539535, 420627609, 431130260, 437134929, 445654613, 454958597, 464012951, 472425553, 478684815, 487991001, 497425551, 504382549, 514369233, 521020625, 530456261, 538068185, 548570836, 554182223, 563619465, 572922959, 579618510, 588416667, 596254422, 604914831, 613713426, 621690394, 1075374018, 631785175, 638748379, 647374361, 656285317, 1076166661, 1073824773, 663635151, 672302683, 680535573, 688799450, 697320469, 705857051, 714090197, 721952339, 730875093, 1074114504, 740198104, 748168905, 755908186, 1076745155, 1074926595, 764560409, 773752472, 780672659, 789464143, 798918168, 806888969, 814358166, 1075203012, 823281241, 832472664, 840311897, 848832073, 856170003, 1074437129, 865371794, 873348762, 1075761095, 882149074, 889855574, 898926162, 1074738122, 1077114827],
    [126, 112, 12, 2327681, 9962561, 18351105, 26739841, 35259584, 43648128, 51905729, 60973647, 68813824, 78218959, 85591104, 95170132, 100927058, 109855440, 117835283, 128550415, 137113108, 142870034, 151798416, 159909378, 170099777, 179187285, 185205845, 195576337, 202114627, 212436047, 1073750017, 220999380, 227411525, 235561667, 244057283, 253985985, 262942356, 268961410, 277504643, 286000259, 296584210, 302515906, 311058947, 319554563, 328205910, 338265743, 1075859459, 344327827, 354960081, 363037697, 369757911, 379740367, 388858962, 394528466, 403456592, 412091926, 422413522, 1074831302, 430845461, 436864021, 445399568, 456632025, 462171672, 472400465, 481797657, 487219267, 495988314, 504734806, 512362197, 522346511, 531508437, 538289174, 547898001, 556928539, 563586192, 570820179, 581066895, 588000920, 599238297, 1075636169, 1076180935, 604243602, 613965843, 621416087, 630195926, 640517266, 1077235652, 646579861, 655909011, 665726101, 672507094, 680935554, 691146395, 697803856, 705562309, 714621125, 724700891, 730859158, 739615894, 746981075, 756564037, 766643803, 773301264, 781738195, 789327448, 798467280, 1074633672, 805832258, 815153218, 822742615, 1075429378, 831391365, 840450181, 848047832, 859285081, 864945669, 873873602, 881864410, 1073873925, 890650626, 898641562, 1074154443, 1074436044, 1075245005, 907558917, 915418650, 924344403, 931794455, 1076833230, 1076589514],
    [118, 104, 9, 2409664, 8944705, 18375680, 26764480, 35284033, 43541568, 51930240, 60449985, 68838529, 77907072, 84573708, 94004225, 101082754, 111461440, 118128332, 127664707, 134637122, 143156291, 153380559, 161793024, 168722126, 176947407, 186934863, 193887886, 202113103, 210298448, 220489231, 227442254, 235667471, 243852816, 254043791, 260734540, 269222031, 277399249, 286156294, 294289036, 302573200, 311322246, 319577167, 327739088, 335963650, 346578450, 1073748933, 352896529, 362545795, 369648771, 378562184, 386432001, 396100291, 403752659, 411591875, 420380174, 429654531, 436757507, 448185941, 453928518, 462183631, 1075344387, 470181570, 481740501, 487882253, 1077194754, 496551508, 505962194, 515172055, 520649921, 1076944836, 532071957, 537945672, 547905106, 557115031, 563373770, 573070994, 579871320, 590792341, 596928074, 604923590, 613703318, 1075644422, 1074359302, 621814296, 630244883, 638877261, 646980248, 657778263, 664036874, 672423638, 680534744, 689489620, 697722571, 705977942, 713606737, 722757258, 730883592, 738753665, 1076728842, 747161233, 756442763, 764438216, 773095053, 1075171336, 781239891, 789997067, 797727887, 806929940, 815029782, 823551563, 1074923463, 1074159623, 833938967, 839670799, 1076005899, 1074718731, 848873108, 856981197, 1076560841, 1073964041, 865126035],
    [114, 100, 1, 2499585, 8774785, 18367616, 26756096, 35144768, 43533504, 52052993, 60441665, 68830401, 75768832, 84272193, 93996161, 103181903, 111814220, 117819021, 126494285, 134595661, 145387205, 151537222, 160056517, 168043648, 176670224, 187330117, 193610821, 201598144, 210224784, 220622479, 227165701, 237380737, 243779280, 254438405, 262932113, 269215378, 277368532, 285886085, 296486417, 302769682, 1073745925, 1074818053, 313158789, 321529356, 328451606, 336088660, 344475270, 355206865, 361219664, 369643028, 380896910, 389006935, 396783119, 403195590, 413943320, 422192844, 428197389, 438726351, 447481425, 453764690, 1076661188, 462974549, 470304262, 481052248, 489038913, 498058903, 1074319299, 1074598918, 1075144710, 503860884, 514606744, 523503118, 529917080, 538472149, 546694232, 556410508, 563498521, 573834958, 580110038, 588926682, 596256461, 605275734, 613969557, 623658712, 630580440, 640033985, 1076462535, 647384665, 657720910, 665830935, 672812698, 679748672, 689161878, 697978458, 705307789, 716162775, 1073864649, 1075720201, 723144218, 731243544, 738862093, 1077044170, 748187157, 756418131, 763741389, 1076013000, 773213849, 781584083, 789309138, 1076288450, 1075524610, 798379737, 806749843, 814081217, 1077364683, 823526931, 830858241],
    [122, 108, 5, 302144, 10527744, 18916416, 27305152, 35693696, 44213313, 52601985, 61392400, 69379265, 75799680, 86156289, 94971522, 103335632, 111582865, 120137282, 126133972, 136890000, 145137169, 153953875, 159688340, 170444368, 176727637, 187080273, 195897043, 201631252, 212526292, 220904963, 229189122, 235185748, 246080596, 254721540, 263005843, 269002453, 280151684, 285916759, 296560147, 305316868, 313179779, 321693400, 330638982, 336111125, 346743828, 355908629, 1073746434, 363406530, 370206226, 378191383, 389490326, 395093595, 405988443, 411746007, 1074809797, 422913606, 428926610, 438738641, 447522456, 456467974, 461940373, 470869714, 480952003, 489465432, 498411206, 504145563, 515040411, 520797847, 531408408, 1074298886, 1073801347, 540485206, 546088667, 556983515, 565623893, 574039766, 579921490, 590789845, 599065816, 604808731, 615696068, 623819972, 632759830, 640869403, 649510037, 655926921, 666174616, 674416196, 682540100, 1076436996, 691340312, 699065492, 707705988, 714647241, 724894808, 733529301, 740998211, 1075928007, 748201545, 756876889, 767083669, 773495873, 781755913, 790431449, 800638037, 807050241, 1075416073, 815597081, 825803797, 830774272, 840763033, 849274522, 855940288, 1074655176, 866051802, 874159297, 882828890, 890936449, 1076758479, 899606042, 1074161611, 1076273100, 1075770317, 1077098446, 1077368778],
    [106, 92, 3, 1836032, 10403969, 18908160, 27296832, 35685504, 44074176, 52593857, 60982337, 69370881, 77333632, 85901505, 94536833, 103583250, 111198864, 117843537, 129011347, 134620881, 144621633, 153915026, 160073411, 168175249, 178176001, 187731539, 193627715, 203473616, 210118161, 221285907, 228639312, 237634689, 246853189, 252609605, 263071443, 271376579, 1073744834, 280407749, 285902467, 294552773, 304136720, 312214592, 321687250, 330311189, 338485315, 347114707, 353011203, 363988112, 372039683, 1074282499, 380407378, 388817027, 397018177, 406367892, 414319824, 420659864, 429043414, 439363221, 445956631, 456699412, 463209664, 471122647, 1073783748, 479374934, 489563283, 495903385, 507031124, 514728979, 521069145, 532197076, 540148752, 546488856, 557231749, 562988165, 573178881, 580043480, 1075895238, 588426774, 598344897, 605209176, 615951877, 621708293, 632301141, 638509593, 647530126, 1075384325, 655535766, 665723987, 672326362, 682632917, 688841433, 1074883528, 699532368, 705880602, 1076463564, 1074128842, 714392215, 723027470, 731046554, 739557975, 748193486, 756212314, 764970574, 1076240327, 1075736521, 1076794382, 1075246029, 1077098447, 1077366731],
    [106, 92, 5, 2581696, 10542272, 18907329, 27321344, 35710016, 44098688, 52618305, 61006977, 69264576, 77784065, 86467584, 94559760, 102793281, 111338689, 119725648, 127959169, 137062097, 145286677, 153148480, 161513473, 170616337, 178841173, 187204116, 195643092, 203611856, 212395733, 220758676, 229196948, 237567511, 245950101, 254313044, 262751316, 270720656, 279478484, 288056913, 296287895, 304694292, 312531968, 319481540, 328237721, 338493014, 347292885, 353403417, 363554449, 372047510, 380173911, 389235861, 394978820, 406144722, 413990614, 422012032, 430767638, 438894295, 447955989, 1073748930, 454485707, 463527040, 473121877, 1075344325, 481642130, 487907027, 497509440, 504814617, 515196498, 521461331, 529564377, 540362258, 546889242, 1076923335, 555277978, 564094488, 571507289, 580314635, 588700761, 597648984, 1074320329, 605609562, 614426264, 622371548, 630513171, 639452891, 1074856899, 646637124, 655925916, 664200843, 672718554, 681395739, 688580228, 697868892, 706010771, 714950235, 1073830916, 1075686350, 1076490186, 723034652, 731307225, 740255448, 748084377, 756893339, 1076765647, 1076000710, 764864075, 1077315533, 1074194380, 1076300811, 1074747336],
    [122, 108, 9, 287745, 8684673, 18924608, 27313152, 35832961, 44090496, 52610241, 60867776, 69387265, 75908688, 84182081, 94553153, 100986450, 109487296, 118122193, 128380418, 134652992, 143287889, 153546370, 159696387, 168453649, 176456705, 187100738, 193758864, 204104707, 210169556, 218416707, 226927744, 235562641, 243713749, 254471381, 260342977, 271213635, 1073748482, 277268053, 288025685, 294012048, 302425088, 312929474, 319473239, 327567056, 338732691, 346868823, 352732688, 361530448, 369542677, 380300309, 386582039, 395084816, 402940993, 1075339204, 412009992, 422366231, 428131971, 437028048, 447899143, 454215257, 464841817, 470468247, 478463683, 489317507, 498116307, 1075613699, 504284808, 514641623, 520799447, 531260611, 540059219, 546227912, 556584087, 565470408, 573613587, 580044441, 590671001, 599024648, 605202006, 614123226, 621987545, 632614105, 640967816, 647406810, 655279688, 663023122, 672835224, 682780231, 1074839560, 689620634, 696708756, 708076616, 714253974, 1073818569, 722650649, 733277209, 739419862, 749889223, 755297938, 764847258, 775054983, 1076453383, 781895258, 788973205, 799730837, 805594241, 815178842, 822537812, 830760129, 840607256, 1075949516, 1076753357, 847572690, 857384664, 1077021642, 864480788, 873637398, 1074419653, 882550360, 1075220430, 890676762, 899335194, 1074722758, 1077348299, 1074227151],
    [118, 104, 11, 1916097, 10560576, 18949312, 27337728, 35726464, 44246017, 52634753, 61023297, 69024833, 77800641, 86449730, 92882640, 103227010, 109659664, 119356545, 128951954, 137053779, 143205459, 153951875, 162506322, 170608275, 176759955, 185280021, 194853889, 201934480, 210446037, 220667394, 229869253, 238110340, 244000341, 254222018, 263423493, 1073745922, 271271443, 277423123, 285943445, 294338129, 305112594, 313607748, 321723971, 330532485, 338773508, 347291159, 355698245, 361841877, 1074819077, 369835729, 378504215, 388712147, 394863827, 403777240, 413998595, 422553298, 429352596, 437331544, 445333137, 454518292, 464330435, 471041753, 1076920323, 1073799684, 481379524, 487663128, 496180758, 504595993, 1075911622, 513229848, 523452055, 529499287, 538395736, 548617943, 554927705, 563168277, 571678294, 582854362, 588334229, 597108315, 604716561, 613385431, 622290516, 630662811, 640892503, 649963162, 655845076, 663824024, 672868045, 680730262, 691906074, 697779352, 706422413, 714284758, 725460570, 731333848, 739976781, 747865753, 756491803, 765412379, 773793359, 781157463, 1075410887, 790578267, 798959247, 1077254088, 807355547, 815474189, 1075169230, 823600859, 1074143180, 1075726349, 1074441162, 832521435, 840902351, 1076553673, 848381013, 857679375, 1076300815, 864634448, 1074753483],
    [118, 104, 12, 2393088, 10305664, 19344577, 27821776, 36383952, 43859968, 52496066, 61550160, 69764752, 77414592, 86181459, 94438914, 103319056, 110968896, 117911058, 128255636, 136513043, 144770626, 153650256, 162218132, 170339329, 178587220, 186713730, 193635921, 203776066, 210185874, 1073747970, 220938324, 227190481, 235351762, 245565075, 254487696, 262440064, 271147734, 279250452, 287508179, 296435732, 304557121, 313820371, 321596432, 330728513, 338256534, 344786630, 355763219, 363422230, 369569362, 1075334085, 378340998, 388269248, 396831873, 406274628, 413468372, 420283974, 431689370, 439042260, 448169089, 454241813, 464946369, 472211650, 482020954, 488932416, 497640022, 1074307908, 504169990, 515575322, 523666433, 532103364, 1075892230, 540741338, 545957521, 556097538, 564486274, 573867091, 579931739, 587900433, 599212164, 605621916, 613625557, 624198803, 632766468, 639403673, 649158867, 655953436, 664340172, 673097367, 682713235, 689508060, 698263127, 707878931, 714149403, 723060300, 731817495, 741433427, 747704027, 1074859976, 1074621379, 756614796, 764620373, 773621337, 781795864, 789786261, 798787097, 806961752, 815334924, 824092375, 832127640, 840502876, 1076466700, 849118937, 857293528, 865144475, 1075168205, 1073881035, 1075736519, 1076803530, 1077331919, 1074210766, 1076327369],
    [110, 96, 4, 2343936, 10706049, 18965504, 27354176, 35742912, 44131456, 52651009, 61039681, 69428417, 77841536, 85949968, 94594177, 103088786, 111764626, 119784640, 127893200, 136643154, 145318994, 153338944, 161447568, 170459795, 176907779, 186613328, 195421713, 203751954, 212427794, 218982085, 229080261, 237364945, 245957331, 252536325, 262792916, 270752833, 277553749, 288319062, 294479429, 304735892, 312695809, 319496853, 328033925, 338290260, 346914391, 1073743877, 354639041, 363193937, 369951384, 1074295746, 380233236, 388463621, 396952083, 406152921, 413525649, 422411927, 428671576, 438920914, 447183941, 455992537, 463798482, 473261721, 478897795, 489520855, 497935513, 504168984, 514811542, 520840899, 529786586, 539458693, 545989333, 554395203, 565140566, 573112915, 1076926467, 581821977, 590308886, 599090201, 607222867, 613098005, 623765081, 632252118, 641033305, 649026582, 655164120, 664004250, 674070039, 682720275, 689170010, 697901723, 707747030, 714335770, 723067483, 733052115, 741301398, 748233435, 758217875, 1075375052, 1076432842, 765164565, 1074624454, 773399067, 781941909, 1077249995, 790330453, 798719189, 1074127817, 1075978189, 1075734478, 1076277191, 1076811727, 1075250120, 1073959876],
    [106, 92, 11, 320513, 8717377, 17132673, 27345920, 35734656, 44123328, 52511808, 61031553, 69420097, 77808833, 86601232, 92595329, 100992129, 111363073, 120268434, 128544400, 134669841, 145321552, 151454864, 159704129, 170600018, 176647893, 185001553, 193424917, 201655297, 210035905, 220819152, 226821313, 237823638, 246097426, 252013633, 262989526, 268895312, 277179393, 288155222, 294088277, 304932374, 313460233, 1073742790, 321595090, 328298201, 335996561, 344392720, 353594368, 361162449, 369585813, 378848855, 389621466, 1073762185, 395407001, 404022416, 411501776, 420799696, 428174529, 439953050, 445990538, 454127193, 462734999, 472843401, 479545034, 488337107, 496559764, 506397897, 1074566085, 513099338, 521366592, 529843735, 540616218, 546401817, 555017296, 565782106, 571698304, 580445908, 590283849, 597388883, 605750464, 614000212, 622554771, 630916224, 639165972, 647317002, 656098831, 664497683, 672457744, 681247808, 1074840586, 689653327, 697527488, 706004695, 715064920, 723207823, 1074079691, 731842200, 739968000, 1076191181, 748619480, 1075688386, 757007896, 1077005252, 1074408392, 765150927, 1076519886, 1076007951, 1075239875, 1075525575, 1077374924],
    [118, 104, 9, 2630721, 10593408, 18981888, 27370688, 35759168, 44278977, 52667521, 60810960, 69444673, 78128129, 86221825, 92645009, 102753808, 109553170, 120071361, 128171715, 134850260, 144696912, 153724099, 162014337, 170114691, 176793108, 186640016, 195667075, 203818643, 210607685, 218474065, 229360658, 237373139, 245612035, 252290644, 260818001, 271164419, 277718677, 287704659, 293971665, 302761169, 312870419, 319659717, 328181270, 336315537, 345121941, 353484440, 361342612, 370263124, 378643608, 387196503, 397516505, 403023377, 411812881, 420587096, 429008597, 439459353, 445621846, 454149268, 462267605, 470951509, 480493123, 487565014, 496354389, 506045507, 512599125, 1073741827, 523345561, 529638936, 538559510, 546448917, 557030918, 563323910, 571589652, 579707925, 1073763266, 1074832324, 590585542, 596878534, 606848722, 612869330, 622077463, 632528518, 638821510, 648791634, 654812242, 663856856, 674471494, 680764486, 690734738, 696755346, 1075890182, 1074343237, 707894873, 714843723, 722846741, 730700805, 739223190, 748274838, 756786891, 764525592, 773564043, 781829334, 789691480, 798729739, 806470868, 1076710411, 814857432, 823510229, 831364229, 840549462, 1074634696, 848675989, 1075704781, 1077025738, 1075468239, 1075230665, 1077331911, 856958679, 1074211790, 865347223, 1076586444],
    [114, 100, 10, 2329665, 8725697, 18973888, 27362368, 35750912, 44139648, 53325328, 59057153, 68674258, 75859154, 86879952, 92611649, 102359571, 109675539, 120434320, 126166145, 135914067, 143230035, 153814032, 162377296, 170123909, 176785043, 187368656, 195267777, 203801237, 212534352, 220433409, 228966997, 237700240, 246656724, 254534168, 260908753, 270765185, 279298773, 288599700, 294463121, 1073754821, 304464405, 310740562, 322154004, 328017489, 1076906948, 337109074, 344295058, 353472017, 363923161, 1074305986, 371974744, 378768919, 389088857, 397140632, 403015186, 411666131, 422817364, 428680209, 437772306, 445877847, 456197657, 464249560, 470910538, 479432407, 487523994, 1075371974, 496623827, 504464906, 512855121, 521078362, 530833413, 538281611, 546409617, 554632730, 1075652552, 564387909, 571707031, 580200156, 1076184009, 1073849283, 588898451, 596741329, 605628125, 613933202, 621905610, 632358553, 1075957703, 639885509, 647333451, 656125662, 664348253, 672645846, 680625802, 689514141, 1074661325, 1074156554, 697811478, 706053643, 714845854, 722405082, 730981019, 739608267, 748400158, 756622877, 1075220491, 764920470, 773566046, 781526556, 1074982860, 790086230, 798303900, 806478363, 815081052, 1076836302, 823255643, 831644379, 1077373903],
    [94, 80, 7, 1432640, 10380353, 18972737, 26862784, 35251264, 43639808, 52028544, 60548097, 68936833, 77325505, 85318784, 94470273, 102516431, 110879809, 119266896, 128024577, 136070799, 144432656, 153190593, 161236559, 168420994, 177987216, 186541185, 193700436, 201975362, 1073754112, 212362961, 220593682, 229212675, 237528657, 244702400, 252813845, 262424083, 270786262, 279544451, 287860241, 295033856, 304710339, 312231439, 321117846, 1076918212, 329147393, 338034322, 344695316, 354313409, 363200082, 370516489, 379864787, 388366034, 1077187525, 1074848899, 396984387, 403826263, 413689489, 421781014, 429367383, 436856322, 446973523, 455335510, 462135956, 471588560, 480528019, 488088215, 496100503, 506479685, 512860885, 523256837, 529637973, 540034181, 1076177863, 546677449, 556811461, 563454537, 571581077, 1076454347, 580362775, 588375063, 597009033, 1075938248, 1073867785, 605528791, 613541079, 621519572, 1076758476, 629794498, 1074155469, 1074698186, 1075238914, 639100494, 1075514310, 647489038, 655877774, 664266446, 1074486286],
    [114, 100, 5, 484353, 10855617, 18859201, 27247617, 35636353, 44024897, 52544704, 60933248, 69321792, 76113612, 84378828, 94487552, 101156492, 109528589, 119918287, 126592654, 134956239, 145083919, 151733263, 159876620, 1073752064, 170249807, 1076391937, 176924238, 185287759, 193578640, 203804303, 210478798, 218842255, 227132944, 237882898, 244033038, 252929040, 260687440, 271437522, 279290945, 286483536, 294242000, 305254100, 311281285, 321234049, 328426704, 338808468, 344835589, 352814668, 361981072, 372362836, 377964173, 388342785, 397266514, 403538944, 411518669, 422694420, 428704960, 436684365, 447598226, 453870720, 463038035, 470666966, 479053381, 487425088, 496723651, 504745687, 512189505, 521635398, 529387158, 538691210, 546924243, 555189958, 1076929479, 562941462, 572245578, 579298433, 588744326, 596495958, 604595212, 613910022, 1075899398, 622325397, 631211523, 639329923, 1076704387, 647491285, 656131786, 663315532, 673154243, 680906391, 689660995, 698319939, 706072151, 714826755, 723485827, 1077234633, 1074367497, 731237911, 740271697, 748250643, 756794890, 765437457, 772367500, 1074653128, 1076233226, 781708885, 790603473, 797402305, 806874645, 814597829, 824157841, 832136851, 1074156484, 1074954245, 1073929154, 1075518466, 1075795915],
    [102, 88, 11, 1048768, 10266689, 18753536, 27142272, 35530944, 43919424, 51905100, 60598273, 69888514, 77071052, 85764225, 95054466, 101712000, 111577679, 120482510, 127402636, 136743567, 1073750016, 1075865601, 145386178, 152568332, 161261761, 1076400258, 1074844674, 170551362, 176696019, 187214349, 194904275, 204491472, 210250387, 220768845, 228458643, 237922894, 245934797, 253895313, 263211536, 269101718, 277872640, 288402071, 296766032, 302656022, 311427136, 321293007, 330197646, 336079379, 346169873, 354847247, 363751950, 371589249, 380152461, 389040784, 394799699, 405842455, 413007955, 422865496, 431008471, 438444753, 1075121092, 448031256, 1074358211, 456174167, 463864001, 473197272, 481034262, 1076206534, 487869077, 496893971, 504646357, 513157640, 522584129, 1075430341, 1073873925, 531917464, 538323656, 547749889, 555109010, 563489352, 571091670, 581697750, 588663506, 597305995, 604645974, 615252054, 622217746, 630860299, 639771217, 647383634, 656026315, 665583766, 672418325, 681192011, 1074154507, 689195605, 697707144, 1074699272, 706628308, 715016788, 723405332, 731794068, 1075770314, 1077098441, 1077374919],
    [114, 100, 9, 362561, 9963648, 18352192, 26740736, 35260481, 43518144, 52037633, 60830223, 68815041, 75860161, 85592193, 94384719, 101025793, 111282768, 119550607, 126191745, 136448528, 144716495, 154249423, 1073750017, 161614480, 170815057, 178925648, 187803663, 193333970, 204369553, 210242115, 220868624, 229746831, 235276818, 246173397, 252316374, 262811792, 271689807, 279055056, 285888212, 294128323, 304754896, 313493699, 321809937, 327682691, 335942295, 347048003, 352717394, 363753169, 369887750, 380864726, 386274007, 395333331, 403442310, 414156931, 419828247, 431255238, 436996294, 445753552, 453382743, 462442131, 470288899, 481265667, 1075855363, 486935186, 497831445, 503974550, 515082390, 1073787844, 521155096, 529157652, 537659974, 546801856, 1076940806, 554709720, 563105363, 571083350, 582191190, 588264024, 599026758, 604637718, 615745558, 622072410, 629821076, 639076416, 647238170, 657215061, 664242304, 672150168, 682912774, 689023120, 697569946, 708078726, 714188816, 722735834, 730877459, 739354704, 1074867141, 747261524, 756516864, 766267029, 773818386, 1076457415, 782134937, 790595730, 1076725709, 1074126798, 798912089, 807373010, 1075711945, 1074681803, 815689241, 824150098, 1075219402, 832466649, 1074460616, 1077353420, 1075537858],
    [106, 92, 9, 540672, 10512449, 18901185, 27420672, 35809344, 44198080, 52455425, 60844161, 69354064, 77752448, 86650385, 94519952, 103427793, 111297040, 120646356, 128454163, 136463056, 145811988, 153620179, 159924288, 170977940, 178925137, 187449938, 196004373, 204091025, 210256000, 221170389, 227159188, 235421888, 1073755074, 246475348, 252324884, 262947538, 271501909, 277614167, 288113298, 296667797, 304615059, 313278994, 1076908995, 322095641, 329780819, 338706968, 347392731, 353250904, 363872984, 1074824133, 372427353, 378154196, 389038168, 1073793988, 395758106, 403844694, 414204568, 1074340806, 422759129, 429010454, 437674001, 448055899, 453774871, 462839889, 473221787, 478940823, 487866972, 496528010, 506776091, 512495319, 521421532, 530082506, 538372243, 546451094, 555114641, 1075933128, 565365401, 571354136, 580141596, 588933771, 597084826, 604908760, 613696156, 622488267, 630646803, 638463128, 647785100, 655778001, 664431115, 672582234, 680668886, 689728076, 1076729799, 697985611, 706136794, 713698388, 723282444, 1075173387, 731408906, 739698771, 748186186, 756476115, 765225676, 1075452938, 1075727372, 1074706377, 1077331918, 1074211791, 1076586445],
    [134, 120, 9, 1960129, 10504321, 18892865, 27281601, 35670017, 44189696, 52578432, 60828240, 69355712, 77457473, 86132800, 92555795, 102771216, 109464274, 119916754, 128733716, 136595476, 142887571, 153102992, 159926978, 170125841, 179196437, 186927764, 195709635, 203827219, 210389654, 220457681, 229396628, 237259348, 246041091, 254421187, 260459154, 270911634, 277629655, 288116820, 295979732, 302271059, 312486608, 319310466, 330287234, 338580117, 344214227, 354822227, 361122386, 371574866, 380389913, 388911829, 397036099, 405416003, 411716182, 422955094, 430854741, 438979203, 447097043, 453659350, 464898262, 1073754115, 472664793, 481054932, 487344727, 495340050, 505817235, 514181138, 1076913092, 523399832, 529025602, 539633795, 548390978, 556550745, 565342936, 571099670, 581576707, 590727190, 596396695, 607547588, 612911618, 623912985, 631105537, 1075871746, 640436889, 646728215, 658010199, 665856217, 674220226, 683175959, 691021913, 698608273, 708341975, 716187801, 724945046, 733114904, 739518614, 749717506, 758673559, 764676244, 773712001, 783446616, 790112466, 799271505, 1073802181, 808873988, 815278226, 823519232, 834039940, 840173780, 1076435913, 848685120, 1075400648, 1074634694, 859205700, 865609810, 873851008, 882659866, 890513622, 899147925, 907825882, 915679254, 924182720, 932991642, 1075694538, 940845142, 949479637, 958157402, 1074409419, 966002708, 1076777933, 1074968519, 974645269, 983050258, 991422549, 999557204, 1077336012, 1075251150, 1074227151],
    [134, 120, 5, 2007040, 10946561, 18393089, 26781889, 35170369, 43559041, 52078720, 60467392, 68855808, 77636108, 86444225, 94021696, 103205571, 109357634, 119579340, 128387137, 137292292, 144745100, 153684559, 161925635, 169779392, 176753362, 185518675, 194945088, 201918994, 211077717, 220110976, 227084946, 236243477, 245408332, 254347919, 261016211, 270967441, 279513807, 286575317, 296133201, 302582354, 1073743235, 1074028547, 312920195, 321298961, 329845263, 335981125, 345295509, 354853585, 363268225, 369535685, 378456787, 387219649, 395258454, 403221126, 411478661, 420399635, 428647124, 437332695, 445032965, 455526467, 462201428, 471280345, 1075884037, 481225284, 487367188, 496052823, 1076937476, 1073816580, 507177678, 512795216, 521218711, 532343438, 538214465, 546253526, 557509198, 562342402, 571515536, 580454939, 590276804, 596683464, 604807828, 613362198, 621324998, 633006606, 637840002, 647012880, 655829593, 665774212, 672312009, 680569416, 689209345, 697248406, 1076197319, 705210950, 714918554, 722774730, 731292173, 739838555, 747153926, 756861530, 763669186, 1077255174, 773235341, 781658649, 1075693570, 1074408450, 790415898, 798140937, 806791883, 815178445, 823724699, 832490200, 840084105, 848734795, 856728272, 865151511, 874433048, 882158154, 890284680, 899064397, 907610843, 916245210, 924101258, 932620939, 940867713, 949430937, 958319192, 966044170, 974170632, 1076775944, 1074698250, 1075505160, 983485080, 991078985, 999729675, 1076563977, 1075008523],
    [106, 92, 8, 264193, 9996352, 18384896, 26773696, 35162240, 43681921, 52070465, 60994060, 68847809, 75761793, 85624833, 94276174, 102937292, 109316289, 119573199, 127830542, 136491660, 142870593, 152996494, 161657420, 168175680, 178817680, 186681935, 195735630, 204221133, 212389395, 221033170, 226896064, 237013647, 245943891, 253659854, 262844430, 268839040, 278956559, 288288276, 294302225, 302786575, 313454164, 319599190, 327952527, 338201168, 347008724, 353153750, 361507023, 371755536, 380825301, 386708118, 394668032, 405310160, 414379605, 422752920, 430713485, 438881939, 445428246, 453781583, 464449172, 473215705, 481045069, 487492101, 495906391, 506245714, 514599437, 1073745859, 520794769, 529532944, 537823813, 548581976, 554698960, 565374485, 571378373, 582267417, 588253264, 598929045, 606909074, 613812364, 623431379, 630098565, 638235345, 647366668, 1074546693, 655290071, 663401041, 672532684, 682275022, 689309772, 699183634, 705693840, 714010135, 1074304964, 1075111940, 724217998, 1076429762, 1073830854, 1075426310, 730787479, 741519896, 749908696, 1077272519, 1075720199, 758428249, 766816921, 1077040074, 1074965514, 1076807624, 1074210761, 1076323275],
    [130, 116, 8, 1884224, 10545345, 18933761, 27322433, 35711105, 44230848, 52619328, 61008000, 69526096, 77785088, 84315778, 92596354, 103080656, 110936192, 120384211, 128237779, 137531013, 142928386, 153535121, 162327059, 168726228, 179128532, 185133268, 195478033, 202041927, 212814549, 218934343, 229032657, 235727382, 246368789, 255495190, 262849098, 271534741, 280137285, 285797012, 296403466, 302705287, 311224918, 321734804, 330992726, 338608855, 344779414, 356158614, 363809365, 371901130, 380430995, 387091976, 1073743812, 397888152, 405717591, 412257928, 419752514, 431442520, 439009930, 1074029578, 445311687, 456298181, 461695682, 473385688, 481215127, 1076135938, 487254535, 495357122, 506939928, 514245201, 1074321415, 523037267, 529328854, 540184069, 547179033, 556056659, 1075392517, 565873878, 572344921, 580698304, 1076970120, 588418120, 597510873, 606388371, 1073845187, 613739020, 621186114, 631196379, 639951376, 1074911177, 647293580, 654740482, 664750747, 672972800, 680061460, 689236556, 697470152, 707610644, 715448976, 722004564, 731179724, 739150932, 749553748, 757383187, 1075186700, 765127245, 773762125, 782060185, 791593495, 798681741, 807316621, 815745563, 823714514, 832236237, 839691271, 849300059, 857268754, 865790477, 874425357, 882862746, 890823250, 1074682893, 898534548, 1075754955, 908028442, 915989138, 923577543, 933194330, 940354695, 949971674, 1077341126, 1076572110, 957254676, 966700237, 1076847567],
    [118, 104, 6, 2420737, 10774721, 18925633, 27314305, 35834048, 44222528, 52480193, 60868609, 69118672, 77777024, 84175040, 94695489, 102942720, 111315601, 120350865, 128250049, 134662803, 144616016, 153380993, 161804417, 168348372, 178424529, 184838272, 196006485, 201902740, 211724944, 218690130, 228878401, 237685464, 244369945, 253667856, 260763864, 271346257, 279628312, 286444186, 295864401, 302706712, 313288913, 321571480, 327731796, 337807889, 344649880, 354707457, 361941722, 369789012, 377776192, 388944405, 394709715, 403343572, 413952017, 422498965, 430623320, 436783636, 445041235, 453675156, 462090328, 470050816, 479251097, 487229460, 497996501, 504392406, 512403481, 520679954, 529558038, 537700435, 546239195, 554986007, 563137113, 571123801, 579793499, 588671708, 1073742786, 596691673, 604678361, 1073763269, 613347995, 622226012, 630376986, 637979155, 646883482, 655290907, 664037975, 1074836422, 1076946883, 674679517, 680708698, 688564377, 699715805, 705718870, 716622493, 722249747, 733270173, 739273366, 750176861, 755935322, 766824541, 773090007, 780970131, 789115602, 1076178887, 798386844, 808897053, 814524627, 825544733, 831810199, 839821530, 847835794, 1076711364, 1074628554, 857106972, 864987162, 1074129868, 1076500429, 1075214280, 1077316555, 1074454479, 1075782601, 1076059086],
    [102, 88, 9, 2039873, 10717377, 18950272, 27338752, 35727552, 44116032, 52775568, 60760065, 69568656, 78080657, 85926017, 94734864, 103246417, 111091905, 119900752, 128412177, 137166848, 145328723, 153438224, 162332800, 170494483, 176630468, 187132625, 195887168, 204843204, 210184708, 220547792, 229441728, 238397444, 243739268, 254101584, 260768402, 271952004, 277826132, 287672528, 294322706, 302992020, 313101011, 319750679, 327625284, 338905752, 344924312, 355838020, 1073748935, 1075334148, 363932377, 372460056, 379815937, 386867224, 397486681, 403794581, 414681177, 420151890, 431041049, 437209620, 447318675, 453706450, 462375636, 473401369, 479134359, 488327894, 497256577, 504701594, 1074566082, 514927257, 523455064, 532121753, 537862232, 547048086, 557287641, 563421914, 1074840515, 573786840, 581142593, 588194008, 596732437, 605784661, 613753370, 1073810376, 622684763, 630950613, 638517847, 1074360265, 647850523, 656115861, 663683799, 1076736970, 672877142, 681281557, 689793755, 697639514, 706431510, 1077011406, 714172501, 1075981253, 1076512715, 722561237, 1074175949, 731736731, 1075763148, 1075263439, 1077372870],
    [118, 104, 12, 297024, 10301505, 18942081, 27461632, 35719361, 44238912, 52496449, 60884993, 69693072, 77793408, 84445712, 94187521, 102959296, 109382161, 120024784, 126388432, 136909008, 142936657, 153578512, 162074768, 170043473, 176622293, 187395666, 195340501, 203239553, 210176597, 218852884, 228894805, 237974035, 243730965, 252407444, 263139923, 270706705, 277809732, 285961812, 296292368, 304916548, 311364292, 319516372, 329068737, 338471108, 344918660, 355167762, 363792918, 371790416, 380414084, 386861572, 397504214, 405735638, 414134931, 422356996, 1073745924, 428935750, 439578135, 446998549, 456339526, 462490118, 473132759, 478709904, 489893894, 1074809797, 1074300867, 496044678, 505900112, 514787926, 520652880, 531837062, 537201297, 548499094, 556730518, 565129939, 572696721, 579144401, 590573143, 596709394, 606251217, 615739031, 621875858, 629442560, 637995669, 649161814, 655429714, 665102485, 673934482, 679774336, 1074060226, 691221190, 697370822, 707882006, 714246337, 1075380230, 723340824, 731154643, 739969612, 747705042, 757820626, 763660480, 773523980, 782061272, 789743617, 798689996, 807226968, 814909569, 1073827783, 824004248, 831817811, 840206483, 849021580, 856983571, 1074631692, 865241153, 1075175368, 1075718093, 1076257737, 1076017103, 1077341131, 1076572110, 1076851658],
    [126, 112, 7, 2189377, 10709120, 18966721, 27486400, 35874816, 44263488, 53030544, 60909569, 69298305, 77589201, 84371665, 94973648, 103105170, 111143441, 117925905, 128527952, 136536787, 145476309, 151480913, 162082320, 169863825, 176646289, 185273876, 195256851, 203417681, 210439764, 220422739, 228934162, 238227158, 246245590, 254528021, 1073744834, 262365843, 269299415, 279702040, 288319512, 296043218, 302853655, 312820306, 319630999, 330033880, 338651352, 344681031, 353200840, 1074283461, 364056214, 372074646, 378268234, 386624135, 394989268, 403522201, 412207627, 420440217, 428698248, 436932244, 448514586, 453853721, 464480920, 470771737, 479423068, 487418376, 1073779651, 496447131, 506186389, 512974940, 521366172, 1074852804, 530001499, 539740757, 546529436, 554396167, 563309276, 571944667, 580083932, 590080152, 596339399, 605252124, 1076959239, 613232215, 622026780, 630450312, 638413384, 1075399688, 647441947, 655704590, 665578072, 674195544, 680487513, 689639133, 697647694, 705423882, 714804765, 725338778, 731202254, 739207897, 748382927, 1074637769, 1076483850, 755843289, 764529291, 773548687, 784058970, 789397593, 800263702, 808282134, 817613530, 825429590, 833448022, 1075185291, 840026187, 849022557, 857031310, 1074160582, 1076016142, 865331272, 874188445, 882600463, 890497032, 899377743, 1077342156, 1076832205, 1076321295, 906750154, 915663048, 923912395, 931915914],
    [106, 92, 9, 2445312, 8702080, 18958465, 27346945, 35735745, 44124225, 52898384, 59069073, 69658753, 75844162, 86452944, 92623377, 103475266, 111626962, 117787266, 128395792, 134566609, 142919680, 151472788, 161950352, 171108369, 179138770, 187124242, 193284802, 201664660, 210063953, 220915906, 229067346, 235620949, 244000853, 252662291, 262858882, 1073753027, 271010450, 277170690, 288024578, 296579218, 1076379650, 302721557, 311117845, 321212608, 329705665, 336276117, 344672405, 354766912, 363259969, 369830613, 378226901, 386880083, 397600913, 402991828, 411519188, 419743808, 430264448, 437586647, 445074004, 453298368, 464351314, 473254425, 478489108, 487016468, 495932115, 506652753, 513092248, 521097875, 531818705, 538249879, 548892697, 556197889, 562374740, 573403154, 580323990, 588869825, 1073787844, 596970007, 605646977, 1076941765, 1074868169, 613878486, 622424129, 1076709318, 632638105, 638913111, 649556121, 655978497, 666192473, 674721881, 1074116551, 682969817, 691499225, 697764374, 706538074, 1077271500, 714541654, 1075454923, 722807512, 731195992, 740092570, 747973144, 1075992525, 756869850, 1075224520, 765258266, 1075760078, 1074466762, 1074751439],
    [106, 92, 11, 2082816, 10356865, 18983104, 27371520, 35760256, 44148800, 52668545, 61057089, 69566992, 77834433, 85969088, 94242881, 103000065, 111782609, 119644738, 128174146, 136579281, 145468050, 153199298, 161622595, 170117314, 179022354, 186753538, 195177091, 203671554, 212576850, 220308098, 228731587, 237226114, 1073745922, 245867219, 253897219, 262129792, 1074817027, 271821461, 279282384, 287295552, 296618133, 304448080, 314034322, 320735425, 329613968, 339200018, 345901057, 355977298, 1076396996, 363831832, 372115989, 380872725, 388737746, 397920466, 405250643, 414059221, 422815957, 428731092, 439224917, 447981653, 454413015, 463735313, 472492049, 479062548, 489136787, 498346587, 504875670, 514826968, 521284250, 529656473, 540289563, 546941643, 555076183, 1073795015, 565158488, 572787345, 581544081, 588114516, 598712984, 607398555, 613542425, 623354387, 632564443, 639216203, 646834836, 656673361, 664382091, 673818705, 680905239, 1074602949, 689056282, 697682583, 1075929034, 705833690, 714205913, 722610778, 731368150, 739879435, 748145238, 1075682249, 1075431435, 1074403277, 756148825, 764922390, 1075213254, 1077065672, 1077331919, 1074210766, 1076326348],
    [110, 96, 11, 372737, 10692609, 18738305, 27363329, 35752001, 44140673, 52529345, 61452816, 69412929, 77458625, 86715088, 95269521, 102624257, 111880784, 120435409, 126348882, 137046032, 145338576, 152955969, 161868992, 168372822, 179540499, 185174744, 195670096, 201927382, 210235090, 218728984, 228977664, 237875793, 243870358, 252283544, 260647446, 271815379, 279703258, 285837912, 294463552, 304475200, 313758291, 319629312, 330150417, 338423450, 344795264, 355701395, 363589146, 370117127, 380220048, 388361344, 396568705, 403671687, 412324565, 421734593, 430698074, 437226055, 445876936, 456591448, 462656021, 470281746, 479562377, 489367696, 496472596, 503836306, 512723655, 523700440, 529765013, 538430614, 1073742855, 546121920, 555339289, 562409601, 571836937, 582420632, 588893849, 597136084, 605391433, 615974936, 622301844, 630705238, 639225561, 646295745, 656222871, 664111817, 671461441, 681036822, 689900059, 1074025481, 697535112, 706334297, 714576468, 723331671, 731089416, 739480149, 748145878, 757009115, 764643912, 773786267, 1075089416, 1074850756, 782051863, 1076435915, 790563419, 1075397580, 1073849282, 798829271, 1075961798, 1075711946, 1074685893, 1076267981, 1074459587, 1077098447, 1077374926],
    [102, 88, 13, 1697985, 10217600, 18475137, 26994752, 35383488, 43640833, 52029505, 60549120, 69618191, 75861007, 85967504, 94784207, 101027023, 111133200, 120164050, 128051793, 137390612, 144827091, 153848913, 161606353, 1073754112, 170945236, 178503889, 187403793, 195160081, 203811542, 212888212, 220446737, 227380438, 237103761, 245754454, 254831188, 262389841, 269323350, 279333519, 287555729, 294891096, 304474646, 312887887, 319654934, 329640598, 336480857, 347442778, 354542163, 361654997, 372608730, 378694299, 388599314, 395471387, 406162970, 412248795, 422699676, 429108888, 437250762, 445794845, 455066192, 462261398, 470706837, 480874130, 487483989, 498197212, 506826394, 512911963, 523362844, 529772056, 537913930, 546195993, 555729616, 564890769, 571361945, 581034515, 589925970, 1076908994, 596527833, 606200467, 613658328, 1074824131, 1073795015, 621955741, 632414812, 640388305, 646965770, 1074595781, 1074093001, 655256085, 664776343, 672131722, 1075420170, 680675933, 689942231, 697453277, 706719319, 1075701708, 715107863, 1076235213, 1074419652, 721783887, 730172559, 1075228619, 1076816838, 1076569038, 1076066248],
    [106, 92, 13, 354368, 10856641, 19518093, 25520256, 36022337, 42322638, 53072589, 61713036, 69822593, 75876942, 86626893, 92629184, 103656012, 112186063, 120285261, 128821964, 1073752064, 134728209, 1076391937, 145740303, 153847949, 159737856, 168282833, 178901517, 187394061, 195930636, 204460687, 212560013, 220571777, 229626447, 237725901, 245737473, 252430996, 262899725, 271149249, 279677133, 287926337, 294507029, 303024835, 313231437, 321480705, 330910291, 336693778, 344838869, 353356419, 364464787, 370248274, 378784454, 387295380, 398019283, 403032590, 412076547, 420980750, 431573523, 437504518, 445745874, 454519382, 461884049, 471574673, 479816336, 487312084, 496478286, 504850966, 512610965, 521644238, 530016982, 537250446, 546556486, 554420820, 563456084, 572091088, 579719765, 587713105, 596625987, 605792337, 614033936, 1076921347, 622449175, 630966794, 638306836, 647219846, 655730708, 664365648, 1074057222, 672909898, 681027726, 689400470, 697946775, 706464394, 714844369, 723112663, 730958482, 1074862023, 739889751, 748407498, 756394196, 1075134474, 765175825, 1073843144, 1074383880, 1074668482, 1075993547, 1075485707, 1075767236, 1076309961, 1076852677],
    [126, 112, 11, 2395137, 10626241, 18754560, 27143360, 35531904, 43920448, 52440065, 60828737, 69619404, 77606081, 86123521, 94932172, 102771841, 111554190, 120213005, 128066689, 136875596, 145116812, 153232449, 162041356, 170282060, 178521808, 184987346, 1073750016, 1075865601, 195440142, 204099213, 212076048, 218672785, 228994766, 237653581, 246975694, 254019152, 260320854, 270945292, 277229079, 288228375, 296258700, 304762573, 313525781, 321162369, 327429654, 338849411, 344338007, 355337303, 363105345, 372133391, 380634709, 388271297, 394669719, 405958339, 414057623, 423136398, 1076409282, 431124035, 439355093, 445165137, 456019535, 463734416, 470330897, 481185487, 487720595, 495365714, 506621443, 515245720, 520531602, 1076940803, 1074861059, 528887511, 538070039, 548275415, 554085906, 563359257, 572927566, 580406297, 590908494, 599131864, 604253910, 615403151, 622210695, 632851470, 641074776, 1075142596, 647376583, 656166102, 666240536, 671657681, 681331798, 689047251, 697994772, 705965721, 713305750, 1075689414, 722619543, 731549396, 741344917, 747908825, 756559498, 764955865, 772933139, 781880916, 789851737, 798371399, 806898841, 815279818, 823264851, 832212628, 840445514, 849104022, 857091591, 1077270535, 865611274, 873614423, 1075448842, 882650635, 890391767, 899427915, 907824150, 916205195, 924339289, 1074685896, 932982475, 1076265929, 1073923081, 1074202635, 1074491333],
    [114, 100, 0, 1576129, 10095616, 18484288, 26741825, 35130369, 43519105, 53063183, 61368335, 68816064, 77204608, 86259216, 94244370, 103394895, 111700623, 119541457, 128202320, 136318609, 145254479, 153587348, 161877525, 170538582, 178261521, 187198159, 195530324, 1073750017, 203820757, 212481558, 220204625, 229084692, 235432017, 245642960, 253627986, 260597777, 269462610, 279580184, 287979222, 296357464, 302540945, 311405586, 321261141, 329922198, 338275535, 344484049, 354815637, 364394010, 372616216, 380914387, 386403844, 397948634, 405409496, 414559448, 422988507, 430192272, 439725144, 448023187, 456799445, 464104591, 473188883, 481834586, 488509138, 495955154, 506874459, 512233156, 523908117, 532171351, 539463380, 548943514, 555191836, 565594779, 574239829, 580357788, 590760475, 596119108, 607794325, 614338194, 624446167, 630172818, 638062212, 1075858371, 1074304004, 647466716, 657738323, 666389015, 673025169, 682233496, 691554967, 699772056, 706229981, 714968081, 723012249, 731352668, 739789401, 1075108802, 748172893, 756911313, 764955161, 773338781, 781994004, 790465617, 1075384266, 798504477, 1074621383, 806898393, 1076466635, 1074919369, 815548628, 1077282764, 1074163654, 1076799429, 823937108, 832325780, 1076294605, 1077092296, 1075790798],
    [114, 100, 3, 279680, 10225856, 18672833, 27290688, 35810369, 44199041, 52587713, 60845184, 69233856, 77753345, 85723136, 92554304, 102682320, 111176704, 119277696, 126641745, 136236560, 142896724, 152832064, 161402512, 169886804, 178810389, 184839700, 195431123, 203222017, 211829780, 218394260, 228985491, 236776577, 245384340, 251948756, 262670465, 270454352, 278938836, 287862421, 296487061, 304934037, 310658048, 321416789, 330041365, 338488405, 344745617, 353005270, 363654165, 371591699, 379995350, 1073749955, 388525781, 397413060, 403465937, 414109381, 420769478, 428098752, 438700627, 446491713, 456133188, 464317653, 470574609, 481298948, 487509586, 497960648, 504655366, 514328577, 521299024, 529452562, 539494593, 546229970, 556680840, 562720278, 571764294, 581437505, 588172946, 598098966, 607128196, 613573840, 623824389, 1075606532, 631008778, 640420053, 647286488, 657344072, 664039046, 672951882, 682362965, 689071120, 1077188614, 1075377090, 699321989, 706506442, 714237072, 723266199, 730492502, 739560984, 748432087, 757482582, 765226634, 773597783, 1076955146, 781504152, 790374935, 799950344, 806669912, 1074356232, 816762437, 1075947525, 1076490189, 824592022, 831155350, 1076766663, 1076254667, 1075217353, 1073927118, 1074989004, 1074221007],
    [106, 92, 1, 2223232, 10628289, 18894017, 27413504, 35671105, 44059649, 52579392, 60836993, 69752400, 77745280, 86109248, 94514305, 102911168, 111695504, 119663808, 128068609, 136869522, 144829440, 153234497, 160069203, 170929680, 178515601, 184962627, 195589650, 204483664, 212069969, 218516995, 229135376, 237497876, 246688771, 252071619, 262690512, 270790161, 280243395, 1073755074, 285625987, 294286995, 304606868, 313535696, 1076909059, 321418834, 330837525, 337899217, 346584786, 354938452, 364129347, 370308694, 381169365, 388493012, 395204248, 403303506, 414461059, 420370008, 428469394, 439356561, 445281811, 456666773, 462417626, 470447827, 478800914, 489688273, 498365658, 506465361, 512880217, 521303574, 531631121, 538045977, 1075089350, 546469526, 556805264, 562687186, 1074588612, 573863514, 582627031, 588246106, 596530904, 607661653, 613543577, 1076433866, 621967062, 632958551, 638709465, 649360922, 658124439, 663743514, 674526874, 683290135, 688909466, 1074879435, 1075413966, 697194008, 706087954, 1073866701, 714476626, 722865298, 1076244428, 731795087, 1076782021, 739642578, 1076010953, 748572239, 1075771336, 756960783, 1077349319, 765349583, 1074480143],
    [126, 112, 12, 427009, 10816577, 18918400, 27307136, 35695680, 44084416, 52088464, 59278464, 69536897, 77254160, 86313985, 95061585, 103329492, 110808784, 120237589, 126387200, 136907792, 145665558, 153661012, 161795671, 170855446, 176587969, 187215380, 194694736, 203754689, 212502225, 221163158, 228904471, 237571280, 243696769, 252358297, 262844117, 269012121, 279514192, 287999505, 297053914, 302952156, 311086747, 321823957, 330632404, 338996762, 346599060, 354733719, 363766805, 372575380, 1073750978, 378580509, 389328474, 394980381, 405343376, 414360666, 420130393, 430878422, 439660186, 447393429, 455397079, 464456854, 472549009, 479243869, 487255133, 498011350, 503743553, 512798365, 523152982, 529444508, 537586845, 548736084, 556967066, 563392202, 571526300, 581897302, 590653011, 1075861448, 1075090372, 597077707, 605335178, 613076571, 623554133, 629703872, 641010708, 646622937, 655797771, 664055370, 671796763, 681258712, 691316243, 697740939, 705998346, 713608281, 723201688, 730367040, 1074846730, 738897433, 748072523, 755551257, 764743250, 775070746, 1075644427, 781233885, 789491292, 798018780, 807087704, 817145555, 1074355142, 823045660, 831573020, 840240786, 850568410, 1075417029, 856354013, 865807896, 875471957, 881512155, 892249237, 898960914, 1074655171, 906546393, 915738322, 926197395, 1076766665, 932236380, 1076259788, 1076541389, 1077331919, 1074201550, 1073968071],
    [130, 116, 10, 2536448, 10759169, 18910336, 27430017, 35818561, 44076032, 52595713, 60853312, 69373121, 78130832, 86422592, 94407872, 103344850, 109350098, 119967249, 128462416, 136754304, 145287826, 151293074, 162016784, 170308800, 176613974, 185109590, 195860180, 203697217, 210553538, 218795202, 229510675, 237803092, 245951058, 251956306, 262573713, 269258435, 279746068, 285609105, 294578371, 303074969, 313953924, 321785427, 330741272, 336652420, 344231442, 354848465, 363894295, 369495249, 380168210, 386436630, 397448855, 405671571, 414771931, 420515353, 430345809, 439129748, 444992593, 456714843, 463744193, 472946391, 478603286, 487624409, 495488726, 505949904, 515290840, 520546518, 529567321, 537431702, 545655825, 556832343, 563275801, 574000708, 581832403, 590788184, 596043926, 607555076, 614739073, 624342680, 630123075, 638356547, 646614594, 655232666, 664319516, 671926338, 680300163, 688787162, 698005085, 705620483, 713853955, 722112130, 730860567, 1073747914, 1075073027, 739948061, 747563139, 755666434, 1074827205, 764546581, 1074578379, 1073808386, 773371548, 783870619, 1074094024, 789712533, 798668445, 806414404, 817270468, 823004762, 1075678151, 1074386948, 832222941, 842590747, 848170522, 857257564, 864864258, 873467031, 1075459017, 882423516, 890431705, 898764373, 1077044173, 907077828, 915410007, 1076013006, 923854852, 932187351, 1076295628, 940361858, 949096149, 957540441, 965929113, 1077358534, 1076849615],
    [122, 108, 12, 2540544, 10570881, 18410624, 26799104, 35187776, 43576512, 52880908, 60902465, 69649536, 77679809, 86026893, 94564047, 103083600, 111627264, 119989900, 128616528, 136506895, 145026576, 153570368, 161932876, 170559504, 178450063, 186969744, 195487436, 203508737, 212502672, 220524240, 229033024, 237456576, 246057168, 254198976, 263016083, 270576205, 279113295, 286057998, 296570387, 304130573, 311215312, 319508117, 329296589, 336129669, 344674005, 353560273, 361532050, 369839637, 378725905, 389082710, 397445206, 403498574, 414010963, 422873816, 430394496, 437700311, 447802902, 456165398, 462210128, 470502997, 481593944, 487386695, 495764624, 506285779, 514911958, 523274454, 529329671, 538537039, 546498193, 556854934, 565217430, 571010629, 579661511, 588868815, 596829777, 604801746, 612953605, 621604487, 630811791, 639428313, 1073747975, 649366168, 656100884, 664192535, 671910482, 680718026, 689759897, 698305689, 705464850, 714821332, 722265742, 733252120, 739569291, 748252175, 756467351, 764603914, 773123659, 782034457, 790580249, 797503173, 806678027, 815588953, 824134873, 1075337158, 1075089413, 831712906, 840232651, 849038932, 856474640, 1074841540, 1074077700, 1075934219, 865267274, 874204820, 881649358, 1077248968, 1073865736, 1076234250, 1074424842, 1076797378, 890685015, 899632217, 1075761097, 1074735113, 1076589507],
    [126, 112, 13, 2386944, 10660865, 19199169, 26790912, 35179712, 43568256, 51956800, 61509132, 69495936, 77919297, 85773903, 94661824, 103085057, 111979599, 119721552, 128251009, 134638672, 142913229, 151309890, 161664528, 168359633, 178433153, 184970256, 195219152, 204115660, 210302481, 218524880, 228773520, 235468433, 245542081, 252079248, 261934607, 269416083, 279211072, 288140303, 294047427, 302970387, 311324306, 321039425, 328128150, 338333324, 344739540, 354209487, 361647829, 369686097, 380415183, 387763855, 395769486, 405580943, 412511439, 420269573, 428799571, 440053335, 445402644, 455773772, 462319314, 471266894, 478989893, 487904857, 495734356, 503623245, 512544389, 521860635, 532327959, 538340431, 547026651, 555380314, 562343565, 571657799, 579786454, 588009108, 595897869, 605345497, 614100634, 624602775, 630912603, 639266522, 649768663, 1073746886, 1074818054, 654626306, 664467099, 672959698, 680946703, 688311939, 697620121, 706514066, 714501263, 722652871, 731174425, 739929626, 748588696, 755289730, 764202693, 772689493, 781112854, 790531672, 1076666373, 797855381, 807177810, 815199758, 822529603, 831704583, 839798293, 848221782, 857640664, 1075898308, 1076174792, 1075671048, 864341698, 873647751, 881749074, 890697422, 899583512, 1076990978, 1075177474, 1076497354, 906415619, 1074414599, 915338963, 924618258, 932080658, 1074170883, 1074709449, 1073945547, 1075541003],
    [110, 96, 9, 2599936, 10562752, 18951232, 27339776, 35728512, 44248065, 52636865, 61285968, 69413953, 78359632, 86191233, 94588433, 103228944, 111914704, 119754449, 128386643, 134975122, 144920145, 153552531, 162245648, 170086033, 178726544, 185306706, 193416725, 201927701, 210447895, 220669136, 227249682, 235359829, 243870805, 254215699, 262909072, 269044759, 280176278, 285970130, 296701528, 304940674, 313626324, 319639258, 328150234, 338896406, 346532928, 353193626, 361704602, 371656403, 380087488, 1073750980, 389228246, 1075858371, 397512340, 1074303682, 405753368, 411774615, 422380738, 430419072, 436817047, 445329111, 455934978, 464621076, 472862360, 479145562, 489489474, 498175572, 504187994, 512437847, 1074851781, 521209564, 530157273, 539971288, 546254362, 554763804, 563842717, 572354139, 582420062, 588877465, 597520091, 607585950, 614174237, 621358741, 629623957, 639577674, 649274966, 656117341, 663301845, 671567061, 680592988, 689671901, 698183195, 706686602, 1076694982, 716637726, 722029783, 730924700, 740126363, 748629514, 1074618311, 756649497, 764234778, 773795530, 781815385, 1075681290, 792135390, 797527127, 1075440585, 1076507597, 1077035979, 1073907660, 1074190280, 1075263439, 1077372878],
    [122, 108, 12, 2165825, 10554369, 19074048, 27462720, 35720321, 44240064, 52866768, 61158608, 69560528, 77663425, 86183040, 95111891, 103101968, 111586960, 119974928, 128280592, 136656016, 143068738, 153529936, 161835088, 170989265, 176623106, 187502230, 195389584, 204516354, 212932113, 218697367, 229445334, 237718035, 246486609, 255102161, 260640279, 271388182, 280267793, 288429713, 296830999, 305204824, 313996502, 322210897, 330394243, 336137943, 346371152, 355765393, 363940055, 369561282, 378080855, 389493910, 397454530, 404047960, 411504258, 422799893, 431559891, 439397506, 1073741826, 447811096, 456988372, 464563266, 472991895, 1073767107, 481365656, 487394952, 498669203, 506153107, 513183442, 520949256, 531319379, 540874260, 546737682, 556863192, 562892360, 574428820, 580292242, 588597464, 599331923, 605458002, 613763096, 623709782, 632763478, 639151769, 649152599, 1075875781, 655298253, 666069653, 674706454, 681356308, 1074584519, 688852621, 700257876, 706260505, 714426520, 1075388358, 724789845, 733549587, 740076692, 747572813, 1075670987, 756880469, 766733013, 773369433, 780996296, 1076724744, 790434837, 798797012, 808806489, 1074121668, 814681613, 823989397, 832351316, 842098883, 1074402317, 849155285, 857255641, 867264579, 875915417, 884041731, 1075205071, 1074968522, 892692697, 1077341129, 901081113, 1076570060, 1076327374],
    [114, 100, 13, 2092224, 10830977, 18967616, 27356160, 35744896, 44133568, 52653249, 61041729, 69430273, 77589568, 86328385, 94596225, 101052048, 111625360, 117829200, 128271361, 134606544, 145179856, 153972306, 162350673, 169864320, 176778900, 187297297, 196035666, 201944660, 212692690, 218492432, 229729364, 237832853, 245361664, 254231568, 263260822, 271412882, 277834902, 287960785, 296699026, 1073755074, 305203734, 313355794, 319777814, 329903761, 337986753, 346884821, 355069009, 363807954, 372050517, 380454033, 386657879, 397216277, 403566099, 413615184, 422906503, 428830294, 437120723, 447562769, 456198230, 464340177, 471059993, 481626823, 489636882, 495709719, 504721098, 1076916165, 514919126, 521629323, 529493206, 540107924, 546041495, 557124103, 565658757, 571723353, 580462681, 589262348, 599213125, 604761815, 1076669385, 612986580, 622405657, 630681163, 638447251, 649159892, 655960793, 664235531, 674710725, 680774873, 1076416456, 688483860, 698296920, 706702924, 713944659, 724657172, 733284935, 740257484, 1074594755, 1073832967, 750208005, 756272793, 765012121, 773811852, 781544970, 1076205580, 790571672, 798453451, 806710922, 1075431435, 815737368, 1074406350, 823488074, 832514776, 1075991494, 1074961418, 1075759044, 1074206669, 1075279823],
    [106, 92, 13, 2436096, 10572801, 18803777, 27315792, 35990592, 44127297, 52481552, 60904641, 67440274, 75845140, 86847123, 94424720, 102847617, 109399700, 120026260, 128790227, 136367824, 142954068, 153580628, 162344467, 169798657, 179009219, 186985664, 195620369, 204305925, 212397777, 218435090, 226840276, 237860485, 245296321, 251989586, 262632660, 270871680, 278850689, 288192197, 296799424, 302321362, 1073750149, 313226755, 321965120, 328281751, 336678600, 346911813, 355003985, 361836055, 370363929, 381086745, 388724291, 395390551, 403918553, 414641369, 422278787, 429207256, 1075862531, 437341832, 447181844, 455945811, 464055953, 470897792, 481348736, 487927448, 1075622850, 496193113, 504450632, 513617429, 523693145, 529749072, 538136217, 548859033, 554783936, 563547734, 1076946887, 571692240, 582011904, 588328663, 596725256, 605892245, 613635088, 622251670, 1076167688, 630412432, 639028310, 647433366, 655447040, 664194582, 672476760, 1074098116, 681389781, 689001536, 697749206, 706145426, 714419736, 1076727757, 1074650060, 722930710, 731311314, 1075450831, 1074949065, 1076530126, 739708118, 748088338, 1074447307, 756887125, 764865618, 1073944522, 1075279814],
    [126, 112, 12, 1838208, 10595457, 18984001, 27372737, 35892352, 44280832, 52669632, 60926977, 69340816, 77835328, 86232657, 92646481, 103025857, 110889984, 120049155, 128689796, 134720644, 144444608, 151629459, 159894675, 170632772, 176926341, 185052228, 195825234, 202223316, 210349651, 218614867, 229353156, 235384004, 246557829, 252292627, 262655619, 271550037, 277589573, 285715972, 293973713, 304877074, 1073750659, 1075857412, 312986691, 321627140, 327921157, 335916561, 347220997, 354667729, 364095174, 372386885, 379833361, 389260870, 395030213, 403025553, 413273680, 1074305029, 421776529, 431334999, 438439440, 447204547, 456369670, 463735873, 471182938, 478661651, 490055319, 497290369, 504737498, 512478806, 523208213, 530844673, 537767444, 546294996, 557164055, 563874880, 571846170, 579448531, 587713747, 599369435, 606867154, 613920267, 622063256, 633054922, 639766224, 647474827, 655085078, 666084998, 674376901, 1075373062, 680373908, 689171992, 699141778, 708552266, 714452634, 722972363, 731115096, 739511961, 1076172745, 750495370, 755748566, 764677849, 1075145672, 775268055, 781175956, 789843545, 800826890, 806202964, 815001304, 823397913, 1076462535, 1073867786, 1076758477, 834250267, 840412747, 848023190, 1074154507, 859416219, 865061908, 876193371, 882756698, 1074697166, 892307157, 898616404, 909084309, 1074984908, 916311066, 924699802, 933088474, 1077354447, 1075803074],
    [114, 100, 10, 373825, 10587329, 18975873, 27364417, 35752961, 44157584, 53056704, 59059794, 69323280, 78362193, 84225554, 94735957, 103402006, 109546518, 120305361, 128650772, 136679125, 145345238, 151489750, 159757505, 170593876, 176656022, 187287702, 195802769, 203787797, 212453974, 218598486, 226866177, 237496855, 246396117, 254643783, 260386514, 271829063, 279688721, 1073742787, 288198151, 293940882, 304451221, 312994391, 321893525, 330510024, 338937863, 347059221, 353340954, 364064328, 371714711, 377861249, 1073763269, 1074832322, 386895578, 397872346, 405269207, 414168149, 420449882, 431173256, 439995032, 447321088, 456338952, 463587920, 472487040, 1075900424, 481136327, 490146906, 498321607, 506041408, 515706441, 523881176, 529503963, 540872329, 549046808, 554931344, 1076956100, 564858516, 572639952, 580097104, 590188167, 598413012, 607373447, 613389915, 1074354183, 624364570, 632285715, 638555803, 649924105, 658098776, 1075417034, 663721499, 672108186, 683084954, 691006099, 697537552, 706678300, 716171987, 722703568, 733810377, 741337683, 1074651078, 1075717129, 748621468, 756927001, 1076250571, 765431439, 773704281, 782175964, 790597327, 798870233, 1074182093, 807341660, 815763023, 824035993, 1077342156, 832540175, 1076827151, 1075276750],
    [86, 72, 1, 2378753, 10863617, 19376193, 26864768, 35253440, 43641856, 52030528, 61327055, 69487745, 78096577, 86492815, 94873729, 103042241, 111658575, 120039425, 128207937, 134720081, 145517649, 153601551, 1073754112, 160017106, 170772176, 179334675, 185436179, 195552852, 204326544, 212699797, 220578945, 229477077, 235957782, 245744705, 254642773, 263220883, 270910657, 279808533, 1076911042, 288386643, 297110083, 304989712, 313290449, 322275971, 330155600, 338456081, 345221784, 355233425, 361343570, 372272851, 380102356, 389384707, 397430489, 403941912, 412372503, 422045204, 429107800, 437538391, 447211156, 456493763, 1075347459, 462704343, 471050968, 481316377, 487172626, 496258711, 1073805254, 503818257, 1077223364, 514870937, 520727186, 531648089, 537757907, 546336342, 554534995, 563113686, 1075667916, 571312275, 579890838, 1075948491, 1076490185, 1076759501, 1074423754, 587704465, 1076270021, 1074974664, 596093137, 1074730951, 1075267534],
    [110, 96, 11, 2468928, 10605633, 19229825, 27249664, 35638464, 44158017, 52415616, 60935297, 69192768, 77712577, 86234764, 94743552, 103115841, 111266817, 118066832, 128177740, 136670401, 143232592, 153439308, 161600641, 168152706, 176787152, 186898124, 195390465, 1073752064, 201707074, 1076391937, 210341392, 220548300, 228709377, 235261634, 245618188, 254127296, 262885005, 270879884, 279293056, 287429825, 296734228, 303148750, 313644052, 321211404, 327536130, 336703054, 346552003, 355159757, 1076924418, 363329091, 372476994, 380325453, 389009108, 395423374, 405918932, 413879821, 422563476, 428977678, 439473300, 447827670, 456117844, 464639060, 473411151, 481382038, 487181892, 498577103, 506547734, 512347780, 521621139, 532131343, 539489795, 546426567, 557026306, 565268054, 573044355, 579456516, 588860945, 598969474, 1074847747, 605507155, 616017551, 622579337, 630672915, 640912578, 646565572, 655969873, 664382997, 1075909636, 672910857, 680644167, 689811154, 697913041, 1075144645, 706465353, 714976850, 723078801, 731754130, 739725011, 1076206536, 1075436552, 747752967, 756657877, 1075710918, 1074416646, 765185737, 772918919, 781823637, 1074692105, 1073923079, 1074214858, 790212181, 798862866, 1077374923],
    [102, 88, 9, 2510912, 10653697, 18755776, 27144256, 35532928, 43921408, 52842688, 61116940, 69208717, 78008448, 86282892, 94374605, 103174144, 111317057, 119540237, 128094337, 134640145, 1073750016, 145238608, 1075865601, 153391820, 159806033, 170404560, 178426049, 184971921, 195693203, 203723340, 210137809, 220203597, 229412941, 238572238, 245901968, 254710288, 263737870, 271190739, 279744653, 288387650, 296356435, 302789317, 313561731, 322458254, 329910803, 336343621, 346984528, 355496642, 363341840, 372126358, 380670659, 389567054, 397551766, 403452421, 414069270, 422613507, 428765775, 439494678, 445395589, 1076407427, 456167491, 462320143, 1076676613, 472813712, 479359572, 487731784, 496382601, 506236941, 514880130, 523381334, 529937097, 539897942, 548180173, 556823042, 1074335746, 1074877442, 565324502, 571880009, 581841110, 590254288, 596800148, 605983250, 613577428, 622760530, 630354452, 638726792, 647926482, 655258255, 663892488, 1075154884, 672543241, 681464341, 689869458, 697447112, 1074643915, 1073873931, 1074158601, 1075746824, 1075509194, 705589967, 715018965, 723407445, 1077359558, 1077110727, 731796117],
    [98, 84, 11, 2601089, 9965569, 18354241, 26873984, 35262464, 43520193, 52039744, 61094607, 68817088, 78098497, 85463169, 94648911, 103264257, 112088592, 119814799, 128954895, 137254480, 145101457, 153368591, 161984705, 1073750017, 170808976, 178655953, 187316369, 196186642, 204109523, 212210257, 220870865, 230265556, 237917904, 245766741, 255431252, 262829587, 270932501, 279949519, 288519876, 293868118, 304487061, 313627282, 322074116, 327684741, 338041557, 346427921, 355446927, 361387730, 369365718, 380516438, 389124306, 1075866562, 397571716, 405420049, 414167119, 420902100, 428348101, 439236822, 448369172, 455767699, 464140369, 473010770, 1076402308, 481457220, 490312340, 496399508, 506346134, 512233989, 520360086, 530034705, 1075364806, 538334808, 548289046, 553914390, 563589265, 1073820611, 571896852, 580620823, 587879442, 597143761, 605443800, 614175447, 623539795, 629674565, 639086673, 1076970501, 647386648, 1074112456, 656118423, 664171604, 672895575, 680154194, 1076219847, 1074665419, 689329816, 1075205065, 1074968522, 1077338061, 696931474, 1075776460, 1074491342],
    [114, 100, 10, 2516992, 10514433, 19034176, 27291713, 35811456, 44199936, 52457665, 61403856, 69365952, 78014592, 86012033, 94778963, 103313491, 111735440, 117861073, 128333523, 136868051, 145289744, 151415313, 161887891, 170422419, 178844240, 187066432, 195442195, 203976723, 212660885, 220620992, 229783257, 235434201, 246477394, 252078673, 263468611, 268989081, 277664278, 285633169, 296891545, 302543449, 311218774, 322062868, 330445913, 338752146, 347228756, 355743235, 361263641, 372044309, 378169488, 389166105, 395104918, 403466972, 1073746691, 1074815940, 414463107, 420270806, 428501200, 436475547, 447541845, 456280788, 462189064, 473183427, 481096405, 487221264, 498874071, 506524178, 512518748, 520909448, 528750107, 540078802, 546073116, 554463816, 565982807, 571535379, 579496016, 591148567, 597095064, 607275668, 1075884994, 612636251, 622359179, 630911582, 638347932, 646738632, 654579419, 664466142, 1076938760, 675034775, 681079371, 689369816, 1074332615, 699274906, 1073838022, 705753171, 1077249989, 716051994, 723022347, 731312728, 741217882, 748188363, 756740638, 1074126794, 1075710987, 766383834, 773255704, 781588189, 789639379, 798365277, 806416531, 1074682825, 815142429, 823849630, 1075488718, 1076287436, 831919773, 1075261391, 1076849613],
    [126, 112, 13, 1961985, 10506432, 18894976, 27283520, 35803329, 44060672, 52580481, 60822032, 69357569, 77459521, 86134849, 92558034, 102765136, 111538833, 120224340, 127931088, 136704593, 145390292, 151409365, 162017986, 171037250, 178944660, 184963669, 193483350, 203960386, 211677313, 220887572, 228594320, 237891670, 243815062, 252195029, 263188995, 268849685, 277369366, 285749269, 296743491, 305551877, 313012866, 321909443, 1073750275, 1075867714, 327570069, 336089814, 344469653, 355586050, 361386647, 371732482, 380752002, 1076931524, 386412629, 397800083, 406608537, 411848857, 420369114, 430977234, 438694417, 448551641, 453791961, 462303383, 471724225, 482237147, 486822482, 498085970, 504255002, 514969794, 524311132, 529158679, 538071623, 548418194, 553930898, 564523729, 574642716, 580014599, 590361106, 596529818, 604262418, 615510147, 624974556, 630477385, 639119578, 649458387, 658266649, 663506969, 671765079, 680407127, 690876630, 699816517, 705581658, 714616922, 724430998, 733764185, 739004505, 747262679, 756306569, 764293335, 775287315, 1076413382, 784226843, 789861065, 797847575, 808316950, 1073819397, 817781403, 823415305, 832057498, 842396243, 1076717515, 851335771, 1076204553, 856838791, 865611802, 873853592, 884365509, 890630680, 1075169228, 901142661, 907170503, 915796696, 1074139080, 926964380, 1074679815, 1074962378, 932573784, 1075760077, 1074469838, 1075541967],
    [114, 100, 8, 1904640, 8816832, 17205248, 27070656, 33870353, 44347409, 52236416, 61115074, 67564050, 78196865, 86280706, 92730002, 102568000, 111446658, 117756497, 128233553, 134645888, 145305793, 1073752194, 154194516, 161788561, 170471425, 178554946, 184864913, 193366080, 204550672, 212914708, 220508881, 229191745, 237800003, 243708501, 252113618, 263270992, 271485013, 277139665, 286175750, 296825488, 304908803, 310817493, 319222354, 330379984, 338594005, 345027272, 355521236, 361566806, 372410568, 1076381636, 381087940, 387101193, 395121302, 405572227, 411480725, 423030916, 428946007, 439257237, 1074049539, 445690504, 456716876, 462598729, 470888983, 481069251, 490271244, 496153289, 506628232, 514904724, 521177281, 529576520, 540603020, 546386583, 556959816, 562893334, 574025796, 579777094, 588286017, 596685320, 604836566, 615968772, 624068616, 1076943880, 629584405, 639423192, 647049943, 655274694, 665749525, 672977432, 681357839, 689091209, 697731280, 1075643335, 1073826825, 708375244, 714912335, 722896976, 1074637836, 731697816, 739160710, 748466895, 756058241, 1076746246, 765252184, 773632655, 781617296, 1075447823, 790549075, 798001153, 1074423749, 807326419, 815171600, 824103443, 1076270029, 832492179, 1074984907, 1077352394, 1075274702],
    [98, 84, 10, 2552896, 10786881, 18616385, 27300033, 35688577, 44077057, 52465729, 61273088, 69507073, 77336769, 86126720, 94827648, 103061633, 111292608, 119993536, 128227521, 137295569, 144846912, 153795090, 162461329, 169611265, 179092115, 187627025, 195738194, 203165825, 212792913, 220904082, 229388880, 235573974, 246847702, 254867029, 262287360, 271644181, 279624402, 288109264, 296358423, 305699333, 311752408, 321654931, 330087123, 339146310, 346821139, 355252819, 364312262, 371856023, 380418067, 389478022, 395743897, 405977241, 413938320, 420804248, 430715408, 1073753158, 439809030, 447483987, 454874842, 464951894, 470454358, 481038547, 487913048, 498637445, 504763028, 513078808, 523418201, 529961049, 538317396, 547149338, 555094548, 565615254, 571117718, 1076647880, 580260564, 590912197, 1075098563, 598348375, 607689285, 615125719, 1076945925, 1076168649, 623965909, 1074088909, 632723990, 638226454, 1074369479, 649131669, 1074913226, 1075708878, 1073898443, 657635865, 664178713, 1076009922, 1075509199, 674413273, 680956121, 1077350340, 1074752460, 689755738, 698144410],
    [114, 100, 10, 2158784, 10547328, 18935872, 27455681, 35713024, 44232769, 52742736, 61296720, 69907536, 77787265, 86175745, 95073808, 103074512, 111628496, 120016912, 128240272, 137016528, 142930434, 153405456, 161960080, 170833492, 176902803, 188017297, 195999252, 204781143, 210457107, 221039122, 226816578, 235622995, 246737617, 254719700, 260895320, 271496852, 279759442, 288313432, 293925506, 302823001, 313313938, 322261525, 328004120, 338343056, 347129986, 355422232, 364164631, 372295746, 381243911, 386200258, 397719191, 405850306, 414798471, 1073747970, 422745734, 428561107, 439404546, 445444824, 456300230, 464308946, 472862936, 1075344582, 478983833, 490007057, 498684615, 1077190791, 504149721, 515172945, 523588245, 531797062, 538495510, 549015623, 1075893187, 554889738, 565491415, 572050070, 582308565, 588575241, 1074857924, 596439704, 605352521, 613201433, 622381654, 632246424, 1074086853, 1073846216, 638907017, 649237510, 655936214, 666194517, 672330314, 681490138, 689926230, 697886740, 706015945, 1075169289, 714273418, 723433050, 731869398, 739829844, 748483278, 756987546, 765423638, 773384404, 782037518, 789770954, 798930458, 807366806, 815327380, 1074400266, 1074685901, 823980686, 1076278219, 832369230, 1077074958, 1075785676, 1076849615],
    [110, 96, 9, 2553921, 10539072, 18927744, 27316224, 35705024, 44462800, 52885697, 61256401, 69890771, 78051457, 86422033, 94819028, 103445075, 111860304, 119976593, 128373396, 136736848, 145160193, 153530961, 161927700, 171201027, 178969232, 187093588, 195719699, 204667523, 210023062, 218550422, 227070487, 237400592, 246077456, 252227607, 260756056, 271217299, 279632080, 288404165, 297029763, 305191634, 313569797, 321286288, 330357394, 338735749, 344642200, 352899671, 364139203, 372300306, 378056791, 386322966, 395334165, 406247508, 412398234, 420532378, 431247939, 1073746882, 439547971, 1074812931, 1075359877, 447787077, 454054549, 464575058, 470069846, 478597206, 487117463, 495997525, 506910868, 512274583, 520540886, 529584666, 537948827, 548600003, 555003930, 562745880, 571527770, 579392215, 588673689, 598931459, 605728792, 613077720, 621859546, 630215381, 641128660, 646230038, 655782425, 666294292, 1076944839, 672837848, 680948313, 1075651526, 689887772, 698003544, 706114265, 715053660, 723169432, 730886683, 740219548, 1075921866, 747942106, 756052699, 764719194, 772829787, 782162652, 788836566, 1073842121, 1074122700, 1074670532, 797487319, 1076522955, 1076795342, 1075247055, 1077349320, 1074489293],
    [142, 128, 9, 2426944, 10842304, 19238977, 26816641, 35205121, 43593921, 52113536, 60502016, 68759617, 77279296, 86339648, 94701760, 103256780, 110833856, 119747086, 128667662, 136644736, 145199628, 153301710, 161821265, 170199040, 178614400, 187142796, 195506899, 203764369, 212021902, 220942542, 229085772, 235604493, 245838355, 254496910, 260900945, 270897153, 279130702, 288051278, 294455441, 304451713, 310850050, 321220608, 330115074, 338006209, 346501715, 352793282, 361468564, 372058306, 380719762, 386478723, 396702417, 403507409, 414667480, 420319766, 428552708, 437105367, 445844111, 456610328, 463942291, 470233666, 478909012, 489498690, 498160210, 504050244, 512176770, 523053186, 529502809, 540103378, 1073745922, 545862211, 556085777, 563187790, 574050968, 580069523, 587936452, 596587078, 605000409, 613624019, 623989266, 629879428, 638530182, 649409243, 655069716, 663947855, 674714200, 1074813956, 680725199, 689656533, 697144022, 705901064, 714822229, 722440857, 731064403, 739455624, 747737294, 756765205, 764086989, 1075613637, 1074587653, 773009992, 781038167, 789776911, 798708373, 807105104, 815474907, 822973014, 831468038, 839463427, 848269849, 857690714, 864750221, 1076430793, 1074094089, 873411270, 881406659, 892678747, 898339540, 907749467, 916411034, 1075939334, 1074392070, 1076769795, 924005064, 934621851, 941322960, 948810263, 958081179, 1077302280, 1075223495, 966742554, 973968022, 982190669, 993341979, 1000043024, 1007784078, 1016801307, 1024561166, 1033851610, 1041442835, 1050374800, 1057862295, 1066207249, 1075508170, 1077085131, 1073964043],
    [126, 112, 3, 1799169, 10530945, 18419712, 26808512, 35197056, 43585600, 52771468, 60862465, 68908097, 77533711, 86579215, 94442062, 102986830, 111194177, 119607822, 128268812, 136541198, 144748737, 154090000, 162050701, 170349584, 178983572, 187243151, 194973839, 203993805, 212293264, 220271246, 229587664, 237548109, 245847248, 254481108, 263141968, 270759054, 279491085, 288035348, 296695952, 305230868, 311202326, 322114072, 329595468, 336499282, 345732225, 355144276, 363403983, 371134671, 379654862, 388199630, 395219602, 406000216, 413481676, 422671508, 429167315, 436933190, 447814357, 456331928, 464876696, 471110227, 481497816, 487536654, 496538201, 506557524, 1073752003, 512430790, 522787407, 530518095, 538481177, 548762840, 554373766, 565254677, 572035737, 582055124, 588190280, 598809237, 606557264, 614109914, 1076123589, 1075095557, 621482502, 632363605, 638521864, 647722177, 655135318, 1076413446, 663697550, 672043538, 682980440, 689246730, 698030737, 708146200, 713855702, 722408072, 731585041, 739595799, 747541202, 755972302, 764973785, 773150359, 782187099, 789927639, 797741718, 806294216, 814692430, 1074070471, 823481943, 832213594, 1073826756, 1074368520, 1074916360, 1076763586, 1075475458, 840241802, 849296091, 1077322697, 857379482, 866073115, 873763347, 882184778, 1076027339, 1075785739, 891239067, 899322394, 907350730, 916134609, 924095123, 1077103626, 932911697],
    [126, 112, 8, 2347008, 10580097, 19099648, 27488448, 35745857, 44265536, 52654208, 60911617, 69980880, 77689025, 84219410, 94980625, 101019666, 111636497, 120312400, 128784002, 136923729, 145190993, 153342144, 162338306, 168260117, 179032592, 187504322, 195285120, 204682899, 210203349, 220450880, 227242629, 238237267, 243757717, 254530192, 1073754242, 260796933, 271389762, 279530193, 286224903, 296186065, 302477909, 311021651, 319517253, 330512083, 336415446, 344576531, 355677203, 361974424, 369455826, 378130643, 386208978, 395790874, 403010130, 413627025, 420213460, 428151890, 438913169, 445608519, 454152921, 461706898, 471419419, 478507154, 487453207, 496448583, 504187542, 513135260, 520843973, 530002951, 538528411, 546271943, 554562135, 1076905989, 563558023, 571689496, 579825799, 588116695, 1074306055, 596996811, 605230662, 613632600, 621539924, 630527109, 639060634, 647459533, 655094292, 664212629, 672352984, 681013837, 689295964, 697659979, 705894022, 714558170, 722956813, 730976857, 739578885, 747457046, 756511373, 764146324, 1075626566, 1073813517, 773157387, 781522117, 790055514, 797560979, 1075401668, 806827207, 814565974, 823251481, 831877771, 840242245, 848906971, 857068252, 1074891787, 865539093, 874072667, 881971865, 890704981, 898495127, 1074644940, 907482325, 915788316, 923997190, 1074147279, 932385990, 1076784072, 1076537289, 1076287438, 1075263427, 1077371850],
    [106, 92, 7, 489664, 10940609, 18960576, 27348992, 35737664, 44126336, 52507280, 59209728, 69660737, 78205650, 86061584, 92756689, 103215233, 111759954, 119616080, 128380929, 134969473, 143217173, 153170640, 162197568, 168261760, 176771669, 184889429, 195646098, 201808529, 212529152, 218976919, 229577430, 238211732, 244021441, 252531287, 260509847, 271766100, 277575745, 285807128, 296932052, 302741505, 313086482, 321852054, 330494534, 336026129, 1073744835, 344527448, 352811072, 363524224, 369561687, 380826246, 386357841, 394875541, 403247832, 414372372, 422795795, 428413592, 439546374, 448092242, 456069718, 464869394, 472576192, 1074291206, 1075882946, 478490773, 489877702, 498423954, 503656469, 512938003, 523459283, 1076413381, 530141723, 538259483, 546132503, 557144274, 563270227, 1073813447, 573510166, 582178899, 588436115, 596054039, 607344787, 613601491, 621630167, 629608663, 639292057, 647723546, 654922453, 663040213, 672846425, 681278106, 689525403, 697643163, 706400985, 714832474, 1075139531, 723178009, 1074892744, 1074656204, 731198043, 739998426, 748245083, 1077032900, 756363995, 765022427, 1077299146, 1074180047, 1076812750, 1075521481, 1076322253],
    [114, 100, 12, 2215936, 10358977, 18985089, 27504704, 35893376, 44282048, 52539393, 60928065, 69316801, 77713472, 85856385, 94613504, 102879424, 111415953, 120031955, 128045184, 136187969, 145730198, 151384595, 161353729, 170895894, 178909847, 186913297, 196061910, 203690577, 212595216, 221227606, 230019733, 237245137, 246917787, 252048019, 260715154, 271682074, 279573079, 285872339, 296192595, 302649427, 310767699, 322415323, 327545043, 336212690, 347581019, 355848917, 361369619, 371689619, 380236503, 386535571, 1073753027, 397511386, 403321362, 413921936, 423078427, 431346261, 437392026, 1076388802, 447842906, 455865040, 462557402, 473008282, 479572491, 490066453, 496111706, 505907219, 514585168, 521810653, 530156244, 539619863, 545927762, 555322004, 563458763, 572371469, 580374738, 588919389, 597264916, 605401739, 613928978, 621940762, 631089752, 639480525, 647483538, 656028189, 1075881924, 664644248, 673043161, 681194141, 1076155335, 689943054, 698198552, 706064971, 714977933, 723374745, 1074858956, 1074350021, 1074105355, 731886222, 740272796, 748532301, 756535378, 1074649033, 1075189773, 765440718, 773827164, 782094937, 1075476422, 790604508, 798872089, 1077325770, 807383630, 815368788, 1076812814, 1075774408, 824158748, 832416472, 1073968079],
    [114, 100, 3, 2043904, 8755329, 18740353, 27365441, 35754177, 44142721, 52662272, 60919809, 69439680, 77828160, 86184529, 92781200, 102626369, 111382656, 119739025, 126335504, 136180929, 145592981, 151360020, 161427584, 168278608, 178123777, 187535893, 193434262, 203551936, 210221776, 221065237, 229479125, 235377366, 245741588, 253883456, 260379155, 271422037, 277189332, 287815894, 293933779, 304994002, 314020504, 321370262, 329454289, 337769472, 344298068, 354793556, 362754240, 372102802, 377983574, 388479062, 394596947, 405657106, 414683864, 421902548, 430568664, 436540051, 448238168, 455283217, 463598720, 470128641, 478646806, 489142294, 496971840, 506320466, 514702023, 523702465, 531362965, 540512792, 545624724, 556120212, 565654216, 573174808, 580098193, 589952088, 598552661, 607597064, 612735169, 623637717, 629512257, 640414805, 648884437, 655987211, 666317384, 672372817, 682357781, 1073749256, 689541771, 699251207, 707392664, 715993237, 722704593, 733417537, 739873483, 749582983, 758583425, 1075605444, 766360135, 775368840, 1076668423, 781816395, 789813265, 800526337, 1076412427, 1073816514, 806818455, 1075934153, 815207127, 1076996035, 1076217802, 823595543, 1074149317, 1077302222, 831984215, 1074961357, 1075501007, 1075252172, 1074483142],
    [118, 104, 10, 2379840, 10859648, 18477249, 26865793, 35254337, 43773952, 52162624, 60420097, 68939968, 77877440, 86619727, 94105728, 102756880, 111785487, 120214159, 128436946, 136442066, 144699984, 151491664, 162156559, 169865936, 176657616, 186929152, 195939030, 203551314, 211808912, 1073754112, 218600592, 229265487, 237881942, 246265428, 254038144, 263309912, 271995415, 279819988, 288213526, 297161431, 304723663, 313379478, 319287962, 330715799, 336040976, 346540114, 352973380, 364270167, 371831951, 378137115, 386527748, 397260308, 406090449, 414304792, 420082372, 430289920, 438980815, 447859352, 455980692, 464810513, 470282970, 482103450, 490059411, 1076912066, 498365073, 505787456, 515657946, 522564800, 531090066, 539095186, 545780314, 557600858, 565556819, 1075615685, 573688536, 581038610, 590639697, 599111187, 606586898, 612889114, 624709658, 632665811, 638184027, 647468572, 656044048, 664390237, 672634460, 681210000, 689556189, 697561803, 706188956, 714764368, 1075110851, 723110557, 1075918790, 731116043, 740144725, 748450521, 756664861, 764670603, 772403844, 782087701, 790393433, 1077233668, 797567707, 807253717, 815427792, 824030869, 832336537, 1074365385, 1073861575, 840168011, 848795356, 857502233, 1074925517, 864676507, 1074681867, 1075490760, 1076807628, 1074210762, 1076325326],
    [130, 116, 13, 2314240, 10858689, 18862145, 27250881, 35639425, 44027905, 52645952, 61584012, 69718542, 78344206, 86749708, 94370319, 103273038, 111898702, 120304332, 128055889, 137327250, 145470028, 1073752064, 153090639, 1076391937, 162493010, 171029133, 178518611, 184930818, 195252416, 203796609, 212850690, 220713614, 227005076, 238252180, 245739521, 254016211, 263442965, 271692493, 280326165, 287570579, 296858189, 304304256, 312605201, 319148674, 330002574, 338014273, 347068546, 353096408, 361222740, 372469844, 378646744, 386912921, 396622355, 403034690, 414298637, 420704791, 430954562, 436982424, 444977858, 454144152, 462639702, 1076925442, 472897730, 478925336, 487838362, 496087064, 504590935, 512741977, 522320593, 528995028, 538161233, 548368914, 555743887, 562811480, 573035214, 582210197, 590573780, 596750424, 606206609, 614051994, 624259221, 631241423, 640930517, 649032402, 656126041, 666106395, 672378897, 682324174, 691272283, 697553626, 708039253, 714715354, 724922453, 1075110851, 733215387, 738710036, 749957140, 756265105, 766769883, 773042385, 783642837, 790485712, 798741128, 806605338, 815378458, 823358103, 1075907525, 1074351109, 832428560, 840684232, 849064089, 856904342, 865063449, 874371664, 882627080, 890491482, 899395609, 907235862, 915395289, 1074627524, 924703376, 932958792, 941338841, 949187287, 1073857544, 957984858, 965956310, 1074140105, 1074948038, 1076272074, 1075502090, 1075785675, 1076852679],
    [126, 112, 12, 2397312, 10368064, 18887681, 27276481, 35664961, 43922432, 52442241, 61232780, 69088448, 78156940, 85865600, 92550670, 103568973, 111711756, 117716686, 128734861, 136614976, 142882382, 153900749, 161780928, 1073750016, 168037967, 1075865601, 176436878, 187454989, 195597900, 201592527, 212612816, 221017166, 228889600, 238431440, 243676819, 254571726, 262706892, 268971538, 277362324, 288126094, 294425793, 302255631, 310916820, 321680398, 327980033, 335810191, 346830416, 352728595, 363222092, 369768085, 378311809, 389426256, 396776460, 403322453, 411866177, 419966674, 430716560, 438719692, 445265621, 454202576, 464923792, 472659472, 479221457, 487208469, 496145552, 506866704, 512112339, 521164305, 529020500, 538220246, 545795666, 554055251, 563369044, 571356803, 580556418, 587738770, 596661841, 604911107, 613717590, 621827729, 630076995, 638751760, 646985285, 656168019, 663238164, 672830978, 680670726, 689190535, 697586900, 705574595, 714380822, 722613958, 1076403203, 730871493, 739529748, 747803728, 756168262, 764687879, 773739605, 781882946, 789722758, 797980293, 807163027, 815437506, 1075637250, 1076692998, 823145989, 832328915, 840210070, 1074358212, 1076205573, 848965271, 856962759, 866014421, 874130967, 882128455, 891180181, 1075432455, 899296855, 907957269, 916074199, 924079252, 932992019, 1074664393, 1074942985, 1075217354, 1073923082, 1074214856, 1077375947],
    [98, 84, 12, 1578113, 9966785, 18355201, 26874944, 35132481, 43652288, 52974159, 60429440, 69703184, 77206528, 86528527, 94869200, 102776401, 111964241, 120034896, 127800915, 136330769, 145773074, 153589392, 1073750017, 161355475, 169885329, 179073169, 187929811, 194909843, 204238865, 213095507, 1075858370, 220872406, 228464147, 235565589, 246650003, 253771473, 262959313, 272078553, 279868059, 288592915, 296768210, 305632921, 313146966, 321409743, 330798681, 338711122, 345093852, 355090070, 363877010, 372741657, 380640989, 388919835, 395425308, 405421590, 1074307013, 411726421, 420591196, 430972445, 438850191, 448246801, 1075633091, 456269534, 464417371, 470922908, 481304157, 487223957, 498578577, 506470045, 514749147, 523744465, 531766814, 1075384260, 537555669, 548910161, 556932702, 1074616263, 563630612, 572241626, 580538903, 589010584, 1075161030, 598875806, 605704855, 614184602, 1076216777, 622350932, 630953496, 1073877960, 639128276, 647730776, 655905428, 664508120, 1074939850, 672813655, 681293338, 1074180044, 689590999, 698070618, 1076816843, 1076574157, 1077375950],
    [94, 80, 4, 281728, 8705153, 18904128, 27292864, 35681280, 44070016, 52589697, 60978241, 69341904, 77755585, 84202561, 94916176, 102921217, 111284752, 120081424, 128504848, 136450128, 145247888, 153670864, 161616016, 168482390, 178801872, 184823894, 193648278, 201879249, 210121363, 218814166, 227044945, 235155990, 243979286, 252210833, 260321430, 271504576, 277638677, 285487318, 296277072, 303197906, 313849431, 319048896, 327946968, 339015191, 344747669, 352727635, 361026561, 370306642, 1073742787, 378828422, 386282003, 394546240, 402969793, 411832856, 420245205, 430494864, 437941960, 445002451, 456455831, 462188117, 471496200, 479474201, 487880390, 497996928, 503868945, 512496216, 523564759, 528763904, 538605128, 546583257, 556717120, 563771016, 571633298, 580154886, 590271488, 1073760264, 597612116, 606000788, 613692057, 622778068, 630469209, 638875206, 647943700, 1074302924, 1074583558, 655102616, 663907858, 1075390407, 1076192203, 1075951556, 1077275589, 1076500431, 1075208137, 1075752909, 1076807626, 1074213826, 1077105614],
    [106, 92, 3, 2094144, 10386496, 18896065, 27284545, 35673217, 44061697, 52581568, 60970048, 69350992, 77747200, 85884032, 94368960, 102913152, 111293968, 119534720, 127827136, 136992338, 144848528, 152992768, 161994371, 169875140, 178771651, 186801812, 195966609, 203937347, 212500037, 220346064, 229103107, 1073748420, 1075341315, 237133332, 246044178, 254686801, 262403154, 271351382, 277238870, 287315012, 295957522, 304905942, 310793430, 321795601, 329249792, 338460310, 344347798, 355096210, 362812548, 371455122, 380272261, 386291222, 396366852, 406050327, 1076399042, 413957142, 422319298, 429250265, 438459988, 447370962, 456013521, 463729874, 472014548, 481039426, 487970457, 496129676, 506205314, 515102423, 522878469, 531371010, 538301977, 548044485, 554849804, 562828819, 571856473, 1074326533, 581852890, 588797454, 596383443, 604771923, 615765655, 622352078, 629937811, 1076691917, 640573018, 649320023, 655906382, 663754453, 672683662, 680662680, 1073824782, 688920149, 1074112457, 699293210, 705844812, 714086037, 1076220874, 1074935751, 724459162, 730994200, 1077306315, 1076010952, 739382872, 1075770310, 747787980, 756160216, 1077089292, 764417557, 1075269583],
    [122, 108, 13, 2403520, 10949824, 18920449, 27309185, 35697857, 44086337, 52892736, 61123712, 67557010, 75805842, 86937168, 94967505, 101242516, 109491348, 120001536, 128880144, 134796820, 143045652, 151565909, 161786944, 171119701, 178967637, 184858194, 193509077, 204648083, 213062869, 218552018, 226800850, 238073558, 245672960, 255267987, 260748803, 271242453, 277263956, 288405078, 296652432, 304682513, 310957140, 319075858, 330348054, 336115221, 347254291, 355669013, 1073750978, 361412227, 369546258, 377927380, 386446997, 397315792, 406000789, 413848725, 420394694, 431140563, 439817427, 445174996, 453948934, 465245200, 473083475, 478598226, 487503494, 498120342, 506009233, 513052375, 522900501, 529446470, 540480531, 546606743, 1075861510, 1075358661, 554882584, 565646419, 571772503, 579516099, 588838038, 599463120, 605326871, 613865177, 622114315, 633017424, 639143041, 647558166, 655799949, 665392721, 672836753, 681112790, 689223243, 700126352, 706251841, 714528345, 723981440, 731557073, 738899523, 747820696, 756332235, 764851725, 773665793, 781888593, 1076415491, 1074603975, 789763672, 798275211, 807220353, 815303873, 1076195268, 1076736972, 1077004299, 823580185, 832386113, 840608785, 1074399176, 1074156489, 848884822, 857126477, 865635329, 874329281, 882038488, 890681037, 1074961421, 899077785, 1075758026, 1073944527, 1075279822],
    [114, 100, 11, 2281665, 10523776, 18912320, 27300864, 35820737, 44209217, 52466880, 60986497, 69390465, 77763585, 86154961, 94910036, 103191761, 109352530, 120246354, 128491027, 136853012, 145135121, 151295698, 162320976, 170040977, 178796180, 187077777, 195875536, 203988627, 212080149, 220632657, 229569046, 237934167, 245931731, 254817367, 260347538, 271241362, 279877143, 287874643, 296760343, 302290450, 313184274, 319329882, 329520853, 337812497, 346214401, 355374807, 362978385, 372258007, 380564054, 1073744834, 388929175, 395099226, 405812375, 413847762, 1074289603, 1075356612, 420396761, 430184021, 438489153, 445562457, 455620308, 464310800, 470324762, 478985242, 488904341, 495883997, 506393238, 512267930, 520893960, 529317018, 537826909, 548197008, 1075893191, 554178118, 563264733, 573502166, 579614408, 588168729, 596955676, 604509830, 613596701, 621712413, 630772251, 638064326, 646889113, 655938203, 1074863496, 663499848, 672710217, 680433309, 689230428, 696817370, 705442952, 713866458, 722784924, 730338822, 739819209, 1075660741, 748212827, 1074105350, 756202653, 764728028, 1074643914, 772979805, 782168664, 1073887181, 790557208, 798539401, 807334552, 1077303243, 815316489, 1075229644, 824111832, 1077077001, 1076308943, 832099035, 1076588494],
    [118, 104, 1, 357376, 10153153, 18936960, 27325504, 35714240, 44102656, 50689216, 60878416, 69636818, 75822722, 86044176, 94590082, 103191058, 109377090, 119598800, 128144450, 136902275, 145265235, 153810003, 159839764, 169930384, 178877460, 187208403, 195753171, 201782996, 212554883, 220647044, 229151251, 237696019, 243988037, 254201348, 262763732, 271225429, 277673478, 285931141, 296406149, 302740545, 313063107, 321826822, 327874245, 338384067, 346737861, 355111637, 361559750, 369817093, 380292101, 386233472, 1073743877, 395350742, 403502726, 412284631, 419787840, 430362180, 438892035, 447656070, 453441108, 464212995, 471526465, 480940693, 489344069, 497644628, 504402582, 512554566, 522636996, 529233025, 1074286596, 1074830342, 539555395, 547787410, 553973250, 564876355, 572189825, 1075625987, 581472915, 590017683, 595916482, 606295234, 614132737, 1073813506, 621843030, 629601940, 640863447, 648639636, 656839250, 665015298, 672197779, 1075402696, 680563222, 689108631, 699583639, 705918609, 715821589, 722170881, 730917971, 741257286, 747828823, 758303831, 764114113, 774811846, 781383191, 791858199, 798193233, 807318104, 814970385, 823192787, 832483864, 840136401, 848358419, 1075154892, 857649816, 1074654154, 866038488, 1076507597, 1077049295, 1077322697, 1076029387, 1076309959, 1076840398],
    [110, 96, 7, 1899649, 10769601, 19051713, 27317248, 35705920, 44094656, 52483200, 61002945, 69391489, 77780033, 86275664, 94568080, 102937601, 111334401, 119733776, 128349713, 136492161, 144899792, 153515729, 161657921, 170327699, 178681425, 184981014, 195326992, 203619408, 213038807, 220659411, 229013137, 235312790, 245825043, 254703125, 263370391, 270990931, 279213200, 288536087, 296769236, 303889409, 313701975, 321147969, 329055297, 1073742789, 336639513, 345035801, 354710736, 362609857, 370194073, 378590361, 386989714, 397432340, 1073772484, 403085014, 412286555, 422475477, 428914393, 437310681, 447894553, 454229723, 1077188550, 462599900, 472962268, 479395483, 489707092, 496023129, 504419417, 515003609, 521329884, 1075106754, 529708636, 538498573, 548459612, 554892827, 564417665, 1074863043, 570857046, 580441805, 588438620, 598636181, 605861464, 613482066, 623801941, 631019098, 640832665, 647036626, 1075405770, 656184858, 664327757, 674387033, 680590866, 689739418, 697882253, 707843612, 714267676, 724588180, 1075940297, 1074381837, 731035292, 741397660, 747822236, 757355521, 764589084, 1074139080, 1074686927, 773625562, 1076537292, 1076294606, 782022360, 790410776, 798799512, 1077096395, 1076846535],
    [138, 124, 9, 2462848, 10564673, 18953217, 27341953, 35861632, 44250112, 52507841, 61027392, 69668433, 77960192, 86193344, 92755667, 103233042, 109393107, 120000145, 128816656, 134698579, 145176274, 151336019, 161943057, 170890961, 176633346, 185161428, 195507858, 201929940, 212806802, 221091472, 227227286, 235361811, 245839442, 251999251, 263138322, 271423184, 277558806, 288306904, 294343830, 305213017, 312841408, 319502038, 330249752, 336286934, 347024594, 355578904, 363804248, 369841174, 380578898, 388994065, 397358744, 403265044, 411644948, 421989585, 430806608, 436942422, 445338710, 456207897, 464630872, 472985241, 481539674, 487536263, 498667013, 505779264, 512177858, 523458268, 529609948, 540094169, 548517016, 1073747907, 554120770, 563042014, 571684062, 579417748, 590941893, 598709329, 604976711, 612841090, 624121500, 630273180, 639184535, 649311962, 1075076098, 654922900, 663959070, 672739031, 682866202, 688871070, 697513118, 708382277, 716149905, 724784732, 730936412, 739446426, 749843672, 755971591, 764367902, 772355668, 1075613636, 781388890, 791917722, 797914823, 806712861, 815599125, 823505985, 1074579463, 1074333640, 831878813, 840119902, 847591059, 859377285, 865448961, 1074089989, 1074901958, 875779612, 881931292, 890842711, 899003521, 906581076, 916262549, 924169409, 932140126, 940772570, 949982875, 957707997, 965938202, 975148571, 1077013453, 981947539, 991759957, 1000314587, 1076495308, 1073901514, 1076796367, 1075504078, 1008039517, 1016671767, 1025480283, 1033703125, 1076049867, 1077372873],
    [126, 112, 12, 2667585, 10556480, 19076161, 27464897, 35853313, 44111040, 52499584, 60898896, 69407873, 78164993, 86053888, 94453456, 103330945, 109531842, 120012433, 128759315, 137041556, 143086146, 153173520, 162313939, 168391364, 178732625, 187479699, 193417730, 201791062, 212286993, 221034067, 227088006, 235761750, 246748888, 253836944, 263763160, 269570182, 280303128, 285941394, 297317400, 302871190, 310842518, 321339089, 329823425, 336402139, 345075931, 355800664, 361438930, 372814936, 378368534, 386339862, 394993234, 1073745861, 406501082, 411899547, 420311766, 428283094, 436936210, 448443994, 453580358, 462516379, 473241240, 479141529, 490255512, 495523334, 504713820, 512824412, 521215639, 529962517, 537490052, 546381399, 557495834, 564860436, 571822748, 579933340, 588324375, 597071445, 1074550723, 605901448, 613488156, 621747737, 632993434, 638129862, 646541828, 655302361, 664180437, 1075086342, 673912404, 680334939, 689263324, 697373916, 706296916, 714512021, 724244180, 730666523, 739340315, 748240084, 756979421, 1074059396, 764506203, 773405844, 1075381191, 782145181, 789147716, 798955022, 806297177, 815699485, 1073831881, 1075677442, 824005128, 832509582, 840514580, 849253981, 1074389640, 856772678, 866063950, 873537239, 881938438, 891229902, 1075981259, 1076514830, 899502280, 907104454, 1074964428, 916279368, 923226242, 932532252, 1076293581, 1076836303, 1077375946],
    [126, 112, 11, 390209, 10056896, 18445376, 26833920, 35222656, 42333377, 52761102, 60650510, 69170831, 75986448, 84276353, 94704270, 102593678, 111113807, 117929552, 128308940, 137048784, 145313425, 151483600, 161445583, 170251788, 178867793, 186979022, 194868430, 203781714, 210204304, 218493953, 227112644, 237310542, 245199950, 254113426, 260961408, 269315604, 280039631, 287274511, 296088720, 305098262, 313593871, 321222354, 329635468, 338652822, 347148367, 353236032, 363818582, 372576338, 379967052, 386496004, 395267733, 405868687, 413529296, 420433621, 430649488, 437122240, 1073743813, 1074028549, 447958551, 455815184, 463860752, 1075886018, 470765077, 481628370, 487453696, 496324312, 506146896, 514160146, 522581072, 529364679, 540233303, 548737042, 554825235, 565145302, 573902994, 579991251, 587822724, 598298321, 605500057, 613381768, 622581389, 630027911, 640896727, 647443161, 655455817, 664524493, 673795601, 680997465, 688879304, 697431635, 705525255, 714034773, 722564809, 730986131, 741559959, 747730441, 756512266, 765187661, 773148184, 781285001, 790066826, 798742029, 1077205958, 806826521, 1075392521, 815091352, 823096840, 832009930, 840430734, 847869508, 857034328, 865039944, 873952842, 1076973572, 882373646, 890074695, 1074891786, 1074650120, 1075718154, 898461332, 1076515847, 907539662, 915238612, 924316750, 932015700, 1075217347, 1073931267, 1076300747, 1074490379],
    [114, 100, 0, 2290688, 10574912, 18437313, 26825793, 35214465, 43734080, 52122624, 60380161, 68900032, 77692620, 86176960, 94065792, 101012994, 111246860, 119731264, 128661135, 134567618, 145063437, 153941518, 162215503, 169967180, 178451584, 185415312, 195133068, 204273294, 212547279, 220812820, 229071937, 237827790, 1073749955, 1075605507, 243995668, 254237889, 262993486, 271267343, 279533268, 286324307, 295787648, 302716116, 311252549, 322106902, 329735297, 336533138, 347272854, 354507776, 361576016, 369448578, 378599059, 388333197, 395130384, 403002946, 414381782, 421616832, 1076922370, 428807762, 439940825, 447053389, 454374929, 464082516, 473101910, 480730113, 487265364, 495801989, 507049561, 512974551, 520959696, 530380437, 538140183, 546248210, 555546197, 563568283, 571414226, 581523092, 588314131, 596860503, 604705940, 614266581, 623214285, 630929112, 641267225, 647192215, 655701713, 663574021, 674821785, 681008859, 689395210, 698037912, 705517253, 714143443, 722951707, 731338378, 1074319365, 1074867205, 740243162, 748484117, 756506203, 765408794, 1076711368, 773142161, 1074633673, 1075442697, 782186074, 1077290948, 1076254663, 1075226631, 790058698, 1076545483, 798701144, 1074209734, 807089688, 815224394, 824129178, 1076051978, 831862353],
    [118, 104, 13, 1840128, 10597568, 18985984, 27505665, 35894401, 44151872, 52540544, 61060289, 68949184, 77837377, 84399762, 92779666, 102503488, 112176659, 117954066, 126333970, 136057984, 143242901, 154119891, 160159254, 170006160, 176797269, 187674195, 195679956, 202094295, 212211345, 221359768, 227268246, 237114896, 246394515, 254793410, 263599250, 271552131, 277599958, 285718226, 296097297, 305106499, 313513538, 321001040, 330411608, 338679426, 344700439, 354555600, 361739996, 372354776, 378524695, 389428242, 1073750082, 1075868227, 394901013, 405909016, 411817558, 421926609, 430935043, 437245143, 447092305, 454014620, 462010069, 473402581, 481285122, 487044690, 498480210, 504729307, 514446868, 523646162, 532262553, 537908823, 546026583, 554308673, 565816857, 573167252, 579736728, 588232220, 597003867, 606721620, 613029057, 622169755, 630183575, 638301335, 646845464, 655341148, 665816259, 673043676, 680137857, 1076923333, 689278491, 698209436, 1074325444, 705303553, 716672021, 721933394, 731493899, 739120344, 750226581, 756929564, 765048395, 772674648, 1076168647, 783780949, 790484060, 798602891, 806622938, 1074086856, 817475289, 822596818, 831788634, 1073851337, 842640985, 848565914, 1076485068, 856954394, 1075451850, 1075212237, 865711819, 1076797390, 1075760139, 1074729935, 1075017670],
    [110, 96, 13, 638081, 10589312, 18977856, 27497537, 35755200, 44274689, 52663489, 61199056, 69309440, 77962432, 86217857, 94975634, 103019074, 111263313, 120526420, 128307792, 136429265, 145692180, 151361109, 162000981, 169983505, 176527061, 187166933, 195402880, 203682498, 212180032, 218470037, 229109909, 235518977, 246756950, 254013954, 262258321, 271922902, 280097495, 285850689, 296687316, 302355989, 312995861, 319405249, 330429079, 338009088, 347018900, 355594775, 362004115, 372586006, 379843202, 387292688, 1073750018, 395024072, 405354002, 414315095, 422558804, 431306390, 438686352, 445890259, 1075868612, 1076923331, 453744136, 463025818, 472240144, 481279188, 487298632, 497628754, 506982408, 512998931, 522794706, 532148296, 539999380, 546018952, 555292187, 565702792, 573553684, 1074315272, 580466202, 590868680, 596885075, 1073814469, 605632218, 1075400647, 613544600, 622173392, 630789723, 639211082, 647099096, 655727760, 664344283, 672765450, 680653336, 689282128, 697898651, 706320010, 714207832, 723072602, 731485898, 739766937, 748525134, 1074630666, 756913678, 764932697, 773691086, 781709849, 1074915270, 790468238, 798487257, 1076244425, 1076777998, 1075218380, 1074195407, 1076568013, 1075804107],
    [118, 104, 11, 1829952, 8680640, 18478273, 26866817, 35255361, 43643905, 52163584, 60552320, 68940864, 77327488, 84440783, 94106816, 103518800, 110881984, 117995087, 128946833, 136047616, 143160847, 154112593, 162122817, 168326799, 179016336, 185202386, 1073754112, 193229888, 204197523, 210499077, 221614085, 227145234, 235172864, 246140627, 254776017, 263222482, 271306323, 277608069, 288068112, 294647510, 305165330, 313249299, 1076911042, 321884689, 330550996, 335836288, 344716997, 355177168, 361363090, 370144918, 380497110, 389051538, 395292884, 403699222, 414051478, 420238465, 431329477, 436860498, 447605782, 456160338, 464883845, 472501441, 479753877, 487323205, 498438213, 504362582, 514714710, 520901825, 1075349509, 532386311, 539610113, 546862613, 557552327, 564776065, 572290586, 579842580, 590597140, 596399105, 607883847, 614233818, 622194201, 630174356, 640928916, 647788122, 1074321354, 655340116, 664139405, 674483284, 681342618, 691769991, 697693901, 705451073, 714469081, 1075122183, 1074883531, 723358232, 731412053, 739634841, 1076470729, 748524184, 756971140, 764800601, 773690072, 781579853, 790525636, 1075957708, 798986967, 806745613, 815298261, 1074666509, 824021592, 832468484, 1075726286, 1074181252, 840929943, 849245252, 1077330883, 857707095, 866095639, 1073948614, 1076326344],
    [102, 88, 11, 2053248, 9698369, 18863233, 27251905, 35640385, 44028929, 52934348, 60773440, 68811904, 75880002, 86742670, 94240397, 102716608, 109434562, 120297038, 128276047, 136183373, 142988930, 154244226, 161830543, 169737741, 1073752064, 1076391937, 179409986, 186602496, 194247809, 203929228, 212162255, 219806720, 226874882, 238130178, 246380037, 254409794, 1076924418, 263558790, 270401229, 279934597, 288462018, 295304256, 304846350, 311688385, 1074853827, 321877701, 329758284, 336854017, 347305683, 353621716, 363566798, 370801856, 380859987, 389387846, 397016194, 1077222340, 1075403780, 405100047, 414553798, 422181890, 430929477, 437769877, 447198732, 1075675141, 456129748, 1073865671, 465007765, 471062036, 481662470, 489683988, 1075972102, 1074416646, 496227924, 504469137, 514849876, 523466259, 530175496, 538023633, 546821845, 556399810, 565409427, 572118728, 580228690, 588764757, 599225557, 605541909, 613783058, 624391189, 632290964, 638833812, 647075345, 657945685, 664393288, 672241233, 681170568, 689280722, 1074693128, 698332816, 706721360, 714446482, 1074190282, 723498704, 731887120, 1075259337, 1076326347],
    [114, 100, 13, 292928, 8689792, 18757633, 27146305, 35665920, 43923649, 52443328, 60831808, 69220480, 75790336, 84195852, 94255233, 100940482, 109361740, 120216205, 128201231, 134494786, 142916300, 153770573, 161886915, 168065216, 176470668, 1073750016, 1075865601, 185088721, 195310223, 202275009, 210418255, 220606979, 227440769, 235583503, 245895760, 252606529, 260749455, 268974737, 279195727, 285505664, 294304463, 304361679, 311466061, 321542861, 330848465, 335845376, 344234048, 355097101, 1076408261, 363213443, 372791441, 377788608, 388502032, 395745475, 406092366, 411963925, 421042836, 428767233, 437260886, 445135441, 454441546, 465066065, 470849741, 479072853, 487996106, 496540180, 506755790, 514331280, 521583315, 531921550, 1076677572, 539497168, 546740355, 557087246, 1074340995, 564539459, 570964497, 582506513, 588692115, 596644502, 605714629, 613980884, 621810198, 630880389, 638621709, 646976214, 656046149, 664189459, 1076196295, 672010965, 680934026, 689346627, 697989125, 706490903, 713308674, 722909779, 731798034, 739119765, 748042762, 756062349, 765352594, 1076993034, 773599959, 780417666, 790141524, 798907090, 1075698630, 1075448834, 807154327, 815175683, 824072786, 1074680776, 1074959368, 832320087, 1075233737, 1073939465, 1074231243],
    [94, 80, 11, 1939456, 10255552, 18096321, 26744832, 35264577, 43653121, 52041857, 60299328, 68688000, 77076672, 85752960, 94214336, 101982337, 110762177, 119153296, 127768640, 136084544, 144473088, 152934528, 160702529, 168303107, 178887377, 186524239, 1073750017, 193468995, 203432594, 212441681, 219816528, 229612179, 235560660, 245375698, 254392981, 261258966, 271170261, 278798991, 285892180, 294394566, 304095762, 313498131, 319446548, 327948806, 337650258, 347052627, 353001108, 362029057, 372218579, 378699414, 386669190, 395977232, 405379729, 412253782, 422183511, 430545425, 437419542, 447330837, 454959823, 461904515, 472515287, 480885333, 487070403, 496640720, 1075855363, 506363404, 513679887, 1073787847, 522846871, 531235351, 1076943813, 539917900, 1075390404, 546864846, 556695180, 563633752, 571873368, 1076191176, 1075686346, 581861068, 587995718, 1076491276, 1077283789, 1074417670, 597196430, 1074960331, 1075236809, 605584910, 1074726850, 613965464, 622205080, 630750798, 1074228238, 639131352, 647370968, 655908376, 664147992],
    [118, 104, 13, 2388160, 10811584, 18905280, 27424769, 35813569, 44070976, 52590721, 60848256, 69236736, 77920384, 84177616, 94533697, 100954704, 111737040, 119684691, 126253139, 136640512, 142897680, 153370260, 159939221, 168196755, 178583616, 187847377, 195181715, 201882197, 210139859, 221401745, 229177424, 237125139, 243693587, 254956113, 262732432, 271334485, 279509008, 285503632, 295976660, 305287697, 311220241, 321666197, 330977810, 336386193, 346308180, 356143826, 361552081, 371473940, 378043093, 386980379, 398086802, 405675740, 412252380, 423252562, 428660817, 438451411, 445151765, 455372864, 464272597, 470973084, 482146974, 488927360, 497949852, 507312862, 514093056, 1073747911, 522992661, 529988319, 538211032, 548281948, 554858588, 563665504, 571888282, 1075076038, 1075348419, 579739350, 588831264, 596931096, 1073796036, 605175511, 613997280, 622219866, 1074869186, 630341143, 641530398, 647262872, 657333788, 663910428, 672193115, 680940058, 1076978632, 688791126, 700250718, 706106074, 1075939269, 714489433, 722926111, 731804253, 739122710, 748092063, 756314712, 1074122698, 764288662, 773257823, 782135837, 789724759, 798022363, 807301789, 1074667469, 1075727305, 815152857, 823188123, 832467677, 1074442188, 840318617, 848878240, 857095705, 1076815822, 1076308943, 1076590539, 865222295],
    [130, 116, 3, 2119809, 10508481, 18896897, 27416576, 35805376, 44062785, 52943568, 60971136, 69081617, 77748288, 86262338, 94656578, 103275088, 109468179, 119413393, 128606866, 136600066, 145218064, 151411283, 161356369, 170549970, 176708244, 187161232, 194910929, 203702274, 210131667, 218773652, 228868802, 235657814, 245651650, 252336214, 262945478, 271467221, 280091144, 286022343, 296499782, 1073753027, 305160391, 313776791, 319576711, 327834326, 338442886, 347103367, 355719767, 361519687, 371997190, 1076391942, 380657735, 386652374, 396647042, 403593881, 412104857, 1076922370, 422863384, 428366356, 436877332, 446972034, 453925593, 462567638, 470538774, 481583704, 487217174, 495868441, 504379417, 515138264, 521034329, 529545305, 1074322372, 540793434, 548037138, 554719322, 562584276, 571095252, 581984775, 590469704, 596400135, 604396179, 614086803, 1075384327, 623788629, 632412872, 638081620, 646592596, 658234074, 666133144, 672159962, 680679946, 689584211, 700177050, 707420754, 714102938, 722754124, 731527379, 1074880776, 741229077, 750508570, 756045850, 764697292, 772945942, 1075951557, 783172245, 791927319, 797596310, 806509194, 814889110, 823803909, 833870551, 840587981, 848583180, 856701145, 1077272521, 865747077, 875681928, 882530957, 890526348, 899299347, 1075708940, 907690181, 915134614, 924473933, 932338378, 940718166, 1074161611, 949633093, 958028301, 965892682, 1076264970, 1073927181, 1075261390, 1076842447],
    [106, 92, 12, 334016, 8714432, 17076417, 27310272, 35698816, 44087360, 52475904, 59045952, 67407873, 75962960, 86555218, 95098962, 100989056, 109351041, 120109586, 128653330, 134516801, 145545936, 153664146, 162207890, 168097792, 176591445, 187218642, 195762386, 201888339, 212654608, 218665619, 229431376, 235346128, 1073750979, 243866321, 254597776, 260477461, 1075858372, 269032017, 277534849, 285643413, 294163155, 302700609, 310843536, 322099802, 327752209, 336106003, 344529553, 353032193, 361927192, 1074305990, 369809601, 377952272, 386306773, 395500246, 403905236, 412258904, 422763226, 429070932, 437424856, 1075364802, 445970972, 454471824, 462625300, 473094682, 479402644, 488157847, 496581209, 506649242, 513191952, 521329174, 530135769, 538742912, 546495126, 555301529, 563655191, 571800220, 580467225, 588419736, 597490267, 605851712, 612702336, 622770894, 630381142, 637868032, 647409872, 656325198, 664599195, 671422528, 681095895, 1073819594, 689879694, 697629404, 706130000, 1076715469, 714406492, 723292160, 731822606, 740096731, 748204631, 1075678222, 756873755, 765235392, 1074648008, 1074932677, 1076525004, 1077315531, 1074190287, 1075259335, 1076327369],
    [106, 92, 2, 1867840, 10524737, 18913473, 27301889, 35690625, 44210368, 52598848, 60963536, 69376000, 77365248, 86153344, 94699025, 101095441, 111155794, 119308480, 128490131, 136642129, 143038545, 153238096, 159947266, 170164226, 178821651, 186973905, 193370321, 203831443, 210278978, 220495938, 229153363, 237305489, 243701905, 253901328, 260610754, 270827714, 279485139, 285776514, 296106195, 304259155, 1073741826, 313196182, 322082966, 329660435, 336370245, 346202323, 355130885, 361535493, 371603539, 380404309, 388685445, 395090053, 404896400, 413835924, 422239941, 428644549, 438075520, 1073762309, 446700050, 455793733, 464297985, 1074830275, 472521239, 480542850, 489357014, 497818200, 506632406, 514499284, 522852951, 531299926, 540186710, 548176405, 556465686, 564140690, 573741078, 581083283, 588308121, 597695186, 606248979, 615258840, 623681601, 632035992, 640458881, 648813080, 657105428, 664443468, 673848023, 682394261, 688971353, 697997964, 707402391, 715956417, 1075378120, 1077226439, 723163852, 732602964, 741114581, 748329484, 1076450316, 1075161034, 1076219849, 1074671563, 1076786126, 1077053391, 1074192333, 756080153, 1075782596, 1076054982, 764468953],
    [122, 108, 9, 2324480, 10549377, 18937857, 27457664, 35715137, 44103873, 52623424, 61133328, 69254160, 77789376, 86210624, 94566400, 103338577, 111197776, 119896720, 128504337, 136363728, 145062096, 153402963, 162058961, 170227728, 179108437, 187224721, 195608278, 201783510, 212170832, 221035605, 228905040, 237205632, 246217365, 254328342, 262459536, 268892182, 280058580, 1073742786, 285669974, 296270934, 302961239, 313358485, 321714709, 329825942, 336515607, 344389782, 354646208, 361298438, 372030485, 378458775, 388823765, 394984069, 405887572, 1073763267, 411630214, 422362325, 431288980, 437189336, 445315653, 456218772, 461961926, 473480856, 480563408, 487520408, 498162196, 504560136, 515423768, 521065175, 529463320, 537590277, 548239573, 554236486, 564968597, 573894676, 579533509, 590182485, 1074825222, 1074321413, 597736592, 607449172, 615348245, 621738584, 632863832, 641003732, 647452817, 655806994, 666549915, 672618513, 681112282, 690273939, 697916121, 706277914, 716750040, 723081817, 731443866, 740605651, 748247705, 756470418, 767213083, 773281873, 781908495, 790024786, 799325715, 806967833, 814938696, 823851599, 832107098, 842710747, 848779473, 857406095, 865522386, 876265051, 1075389385, 1075926983, 1075164100, 1077004235, 1074147277, 882571983, 1076780047, 890436296, 1075751886, 1076557770, 898824840, 1077349384, 1074751436],
    [126, 112, 11, 2152449, 10672192, 19060928, 27449472, 35707009, 44226560, 52869776, 60872769, 69261505, 78045841, 86530193, 92592850, 103201296, 111598163, 120120002, 128473809, 134535826, 145144400, 153541331, 161931857, 170416209, 176610004, 187087568, 195484307, 201777299, 212359697, 218421778, 226932948, 237926547, 245949058, 251976274, 260880402, 270981651, 277274643, 288258131, 1073744066, 294050388, 302430292, 310829139, 321936085, 327604884, 335984788, 344383699, 355752664, 361159188, 369539092, 380691030, 389044757, 395483863, 405201105, 414210709, 1074289603, 420403802, 428652626, 439411414, 447765077, 454081115, 465197146, 472309777, 481614557, 487758359, 498254045, 506362067, 515168797, 521189915, 531808285, 539916307, 546355931, 556851862, 565467800, 1075348420, 1073796037, 573889117, 580311710, 588429470, 598917213, 605452956, 613866206, 621983966, 632576600, 640212994, 1074869191, 646756562, 657742360, 665378882, 674552477, 680573595, 1076980680, 691191965, 697727580, 705616602, 714782938, 725244122, 733274243, 739948634, 748059356, 758178326, 764860958, 772978718, 781613596, 791994563, 797891098, 807057434, 817518618, 825548803, 831445658, 840358494, 848476254, 859461786, 867491907, 874166426, 1076470726, 882565721, 890411607, 899342873, 906803346, 916120281, 1075963851, 1076240330, 1075730381, 923966103, 932897433, 1075220430, 1074722764, 1077348297, 1074229199],
    [118, 104, 5, 497664, 8747008, 18550785, 27343040, 35862721, 44251201, 52639745, 60897344, 69286016, 77674496, 84244672, 94048385, 101300752, 111360129, 120011282, 126449680, 134855376, 145166544, 153565906, 161847875, 170332176, 176781520, 184891923, 193411669, 203897490, 212668435, 218462336, 227261009, 235223635, 243743253, 254229074, 263000147, 268793920, 277592721, 285817494, 294075029, 304978070, 312939088, 319388304, 327760598, 336018133, 346921174, 354095297, 361330768, 369703446, 380598482, 388340419, 396038209, 403389124, 414152722, 422680772, 430379152, 436812374, 445332036, 453849687, 464623684, 470898689, 478493331, 489492627, 497392259, 504453185, 512440836, 523204690, 529347287, 540121092, 545995396, 554513047, 565287044, 571562177, 1073743876, 579156691, 590313618, 598544595, 606444035, 1074286595, 613628617, 621621783, 632772629, 640522326, 647182921, 655560850, 665688086, 672225409, 680737289, 689115154, 699881685, 705280144, 714291849, 722669650, 733436053, 738966033, 1074829321, 747835602, 758601813, 764132049, 773675732, 780777552, 790592024, 797415616, 1075365832, 807230036, 814192768, 824007316, 830969920, 1074080711, 1076449221, 840923800, 849173012, 1074627522, 1073865674, 857701080, 866089560, 1075984332, 1077305295, 1075753934, 1077077965, 1076309963, 1076844486],
    [102, 88, 12, 2406464, 10420416, 18946113, 27334657, 35723393, 44112065, 52631744, 61020224, 69408768, 78027472, 85917696, 94574720, 103193104, 111354064, 119766674, 128358992, 136249472, 145424980, 153524880, 161709586, 169803840, 179346001, 187268758, 195240080, 204511953, 212434454, 220405840, 229677713, 237600342, 245571600, 254843409, 1073752003, 261185047, 269296215, 279230464, 286350423, 296663571, 305070682, 313097942, 1076124612, 321960023, 330236634, 337870418, 346995283, 355140244, 361437830, 371424978, 378601554, 388282496, 395673305, 405471764, 413448384, 1075348421, 420839001, 1073793986, 431012567, 439288474, 445734103, 456178327, 464192212, 470489606, 479559193, 489732119, 495788247, 504044230, 512842903, 523156179, 531563034, 538279577, 548321939, 554508311, 1074336713, 563911384, 571539666, 580688472, 588972699, 597465752, 605749851, 613096006, 1074884556, 1076724742, 622762581, 630259858, 639572494, 647797272, 656081627, 664738510, 1074132938, 673094165, 680337559, 1077284808, 1074684871, 689904270, 698260181, 705757202, 1076010957, 715070030, 1075762190, 723425941, 731578907, 1075260363, 1076589519],
    [106, 92, 11, 383104, 10582208, 18970688, 27359360, 35747840, 44252816, 50714816, 61436562, 69418704, 76012241, 86602450, 94584400, 101046336, 111768082, 120266435, 126343697, 136933970, 144915984, 151377920, 162624022, 170860245, 176675473, 187519700, 195763843, 203945985, 212955734, 221191701, 229111873, 1073746884, 238244567, 246357653, 252172881, 263287510, 271523413, 277969543, 287832257, 296841878, 304815619, 312998017, 321737364, 328432136, 338893832, 347593432, 1074807746, 355685015, 361986632, 371924547, 380762128, 1073786883, 388846164, 397614152, 405928080, 412570323, 420707016, 431168712, 439867992, 447959575, 454114841, 465033752, 473125463, 479665818, 489814224, 496456275, 504855179, 515055240, 521369736, 531757136, 1076942856, 1075382214, 539841044, 546798091, 554778329, 565697176, 571953683, 579944025, 588765204, 597521051, 605109913, 613931156, 1074097097, 1076467653, 622285459, 631077582, 639049242, 647485524, 656241179, 664238667, 672603866, 680622663, 689428692, 698184411, 706574926, 714546778, 1075177420, 723350107, 731347659, 740129422, 747731463, 1076234251, 756120263, 1074416647, 765295118, 1074706381, 1077337102, 1075782602, 1076064207],
    [114, 100, 3, 352257, 10573953, 18962625, 27482304, 35870720, 44128321, 52648064, 60905473, 69296720, 77813824, 86448657, 92624913, 102973954, 111614545, 117790801, 128139970, 137173650, 145422852, 151607442, 162224132, 170738371, 179116754, 187366084, 193550546, 204167364, 212812421, 221313734, 229448210, 235493394, 245580418, 255015045, 260659794, 269179475, 279134786, 1073743874, 288168018, 296417924, 302340753, 313219204, 322126020, 329717905, 338360900, 346773572, 353196628, 363676291, 1074288644, 372456133, 378337941, 388973061, 1075359877, 397621253, 406518487, 411392721, 420305620, 431177860, 440072727, 447158481, 453859988, 464732228, 1076947139, 473118789, 481360518, 487283219, 498024517, 507181655, 512833684, 520446081, 529610964, 540080710, 548356293, 1076440134, 555293334, 565245958, 573390915, 582679191, 588847830, 596466196, 606945283, 614128216, 621885460, 629889747, 637886529, 646773269, 656095443, 664888016, 1076712393, 672848408, 681261075, 688609939, 698442384, 705493717, 714815635, 724779012, 731568856, 739842646, 746938561, 755825237, 764491860, 773939728, 1074902986, 781900440, 790313043, 798580928, 806951446, 815357952, 823746688, 1077272525, 1075718092, 1076249547, 832135232, 1073907656, 1074190286, 1075258319, 1076056007],
    [114, 100, 12, 2480128, 8657089, 18462913, 26982528, 35371072, 43628545, 52017281, 60537024, 68794433, 75765825, 86629004, 94091264, 103387662, 109427330, 117848589, 128571980, 136942286, 145086592, 151403085, 162107982, 168434384, 178903756, 187273870, 193600080, 201971841, 210219602, 218765968, 227137537, 235508436, 244071121, 254409231, 1073745861, 1074554885, 260674132, 270915648, 277625361, 285848215, 294263312, 304470208, 311278279, 319533782, 327800897, 336345745, 344437458, 355064332, 361765068, 369734231, 378673216, 386521281, 394900183, 403028482, 411449997, 422181455, 428718663, 436712082, 445004493, 455736015, 462787096, 472783385, 480901775, 487166484, 496236685, 504371340, 1076403144, 512471638, 523115225, 529791053, 538284632, 545635010, 556669529, 563345613, 571324935, 579449367, 587577922, 598612633, 605411989, 1075368962, 612995732, 621942912, 630577685, 639089163, 646689430, 655882771, 663754764, 671988359, 680891032, 1075125255, 689174541, 696522753, 1075661766, 1074375686, 705147410, 714603091, 722221649, 1076754378, 1077285828, 730575382, 739768979, 746854529, 756388568, 764418124, 773184213, 1074938819, 1073907657, 1074192393, 1076044803, 781712083, 789714944, 798472907, 806492352, 815127125, 823638667, 832027211, 1076326411],
    [122, 108, 3, 1178688, 8757441, 18454529, 26843265, 35362944, 43620417, 52009153, 60528640, 68917440, 76676096, 84508864, 94083136, 101842048, 109937164, 120273551, 128162512, 134846980, 143366787, 152173760, 160268876, 170735747, 178494096, 185178820, 193698307, 202474189, 210493006, 221067267, 228825680, 235641411, 244178000, 252551248, 263010371, 269195971, 277715525, 286622289, 294509712, 1073742851, 304822799, 312711696, 319658629, 327524481, 336452624, 346765903, 353361553, 361603088, 372062403, 378110080, 386916049, 397097679, 404062737, 411950288, 420297363, 428972551, 438950919, 447848455, 453843541, 462527047, 472505415, 481402951, 487660242, 495821008, 504094414, 513219284, 521247431, 531225799, 540123335, 546126355, 554801799, 564780167, 573677703, 1074024455, 1074834439, 579680979, 588350093, 596368910, 605100690, 613253836, 621534862, 630266450, 638950089, 647070285, 655350865, 664214164, 672504329, 680106628, 688905233, 696623169, 705763858, 714447497, 722311685, 730956301, 1076683714, 739064403, 747477701, 755597312, 1075904517, 765278742, 773167689, 780769860, 789938385, 1073825801, 1074373636, 798833366, 1076221894, 1075193862, 1076518856, 1075752968, 806191756, 815610518, 822452225, 832387670, 839753872, 1077074890, 1075524618, 848108053, 856260672, 864885461, 873824401, 882317908, 890706452, 898439829, 1077366731],
    [130, 116, 11, 2521088, 9157760, 18479105, 26867905, 35387584, 43644993, 52164672, 60553216, 68941952, 78018624, 84655296, 93976705, 101055057, 111016578, 117963282, 126196866, 136870543, 145609427, 151386641, 161348290, 168426132, 176528578, 187070656, 195940947, 202111702, 210369108, 219019971, 227310293, 235650048, 246272531, 252443158, 1073754112, 262011458, 268958354, 277641813, 285580354, 296604307, 302774934, 311032532, 319683075, 327973525, 336698371, 345111172, 354286082, 361527829, 369466370, 1076903938, 377879185, 387054084, 395180675, 403807363, 414349457, 423088664, 428588096, 438860303, 448000665, 453376721, 461896274, 470916291, 481458385, 490328730, 495450834, 504232515, 512859203, 523401233, 1073776643, 532271706, 538049092, 548126231, 556955729, 565441113, 571079188, 581680791, 589855439, 596636379, 605158084, 614046866, 623278208, 1074321412, 632934938, 640400983, 648575567, 655096406, 665566935, 672430608, 683397725, 689290244, 697858134, 708301400, 714587156, 723024086, 733467352, 739539600, 748141716, 1075386311, 758895325, 765041874, 773355542, 1075138502, 784061085, 790084692, 798521494, 1074631624, 809226781, 815037136, 823508036, 833876505, 840202832, 848673988, 859042521, 866024156, 873839748, 884593370, 891189916, 899259410, 1074913225, 1075718091, 909628056, 916355612, 924425298, 1076262853, 932180507, 941521500, 949468372, 957346459, 1077315534, 1074195404, 965735003, 1076569037, 1076064202],
    [110, 96, 8, 1818688, 10336321, 18864193, 27252929, 35772544, 44030081, 52549696, 60938240, 69195777, 77316224, 86096588, 94492864, 102873740, 111001729, 119650892, 127778817, 136559181, 144425152, 152009231, 1073752064, 1076391937, 161593868, 169721921, 178747984, 186890893, 194756608, 202340943, 210623047, 220445389, 228442305, 237599313, 246276167, 253999629, 261053074, 269343431, 279830727, 286243347, 296319697, 303020627, 311411220, 321485457, 328194582, 338681878, 345880769, 1076934594, 354908688, 361618055, 372105351, 378518227, 1077201859, 1074334723, 389118613, 1074611142, 395303510, 405790806, 412072595, 422672981, 429766657, 437502551, 1073847236, 1075436548, 447838741, 454154776, 463321217, 471057047, 1075712968, 480868881, 487709336, 496220878, 504349396, 514292432, 521132694, 531619990, 538163726, 1074950085, 546273935, 554687190, 563337865, 573563094, 580106894, 589789840, 596498951, 605149912, 613669449, 623763463, 630569112, 640776917, 1076790279, 647224009, 655481432, 663992910, 672121428, 681531929, 689289240, 697549527, 705649234, 714455128, 722453140, 731863641, 739621080, 747880983, 755980818, 764664329, 772758226, 1074189321, 782195353, 790584025, 1075259338, 797932239, 1076323275],
    [106, 92, 13, 2259968, 8666241, 17054913, 25443393, 33831937, 42351744, 50740224, 59129024, 69368960, 75906112, 86146240, 92708428, 101481993, 109485708, 1073747969, 120094218, 1075339264, 1075881985, 126262988, 136477760, 143040012, 153622158, 162037322, 170399438, 178814666, 187743888, 193756745, 204084881, 212369034, 220862033, 227319315, 235699913, 246027985, 252755541, 260865673, 271193617, 1076416450, 280018512, 285884100, 294543051, 304617038, 311451215, 319166100, 327982803, 336485963, 344331796, 355515920, 362184205, 369497684, 380681936, 387350157, 396891662, 403750549, 411844102, 420503247, 428218068, 437689880, 446070349, 454440470, 462855896, 470703627, 479606422, 487603911, 496025109, 504790733, 513160790, 521191125, 529555087, 538588759, 546741848, 554589835, 563885650, 572178137, 579616454, 587873860, 596663823, 1074598851, 1074877443, 605697559, 613432903, 622509657, 629948038, 639383186, 646749779, 655113798, 663371396, 672806551, 1075152902, 680541703, 689348248, 697710294, 705707655, 713858707, 722091524, 1074387975, 1075719175, 731526871, 1076782084, 739950233, 748435154, 1076265928, 1073923080, 756727321, 765212178, 1074213829, 1077113861],
    [110, 96, 11, 2390145, 9575488, 17964224, 26483841, 34741376, 43129856, 51649601, 60669570, 68426753, 77887681, 85204161, 93855308, 102612546, 1073746498, 111441985, 1074809795, 119152206, 127777986, 135798412, 143292494, 152706574, 1074305025, 161332226, 169352908, 179075661, 1075372033, 187172432, 194649742, 204054031, 211295756, 219183116, 229385809, 236592846, 246128274, 251928196, 262961869, 271058576, 277093892, 287940175, 296777732, 304612880, 310779604, 321494735, 327841934, 338437649, 346299990, 352591556, 363445334, 371488769, 380773588, 386276884, 397123282, 402923076, 414218308, 422716436, 1075905540, 430186134, 438942870, 447511053, 456402515, 464232018, 472938692, 480773840, 486940308, 497786386, 504002574, 515253784, 521641557, 529561676, 540157076, 546807509, 554727628, 564930257, 572792534, 581549270, 590379140, 599140056, 605527573, 613447820, 624305816, 631512598, 640269334, 646609102, 657204881, 665427599, 674003597, 683026008, 689413781, 697850585, 706239129, 716449427, 721821268, 731404889, 741483604, 748444375, 758392531, 765221399, 773347865, 783558163, 790387351, 1074086854, 798775895, 1073846216, 1075171269, 1074670535, 1076518858, 1075749898, 1076294603, 1077097483, 1077374921],
    [98, 84, 1, 1841152, 8672384, 17071296, 25459840, 33848320, 42236992, 50756609, 59145409, 69140110, 75922497, 85727296, 92697742, 101088385, 111083214, 119281792, 126252238, 136248846, 143029838, 153360577, 1073747969, 161414222, 169613504, 176583694, 186914817, 193754639, 203692161, 210531983, 218824337, 227573330, 235828880, 245635137, 252582402, 261125651, 1075331970, 269155857, 277756420, 286291539, 294682322, 302535890, 311311044, 319749652, 328088132, 336623315, 345013906, 352867474, 362035779, 1073778948, 369382400, 378804821, 1074848709, 386823696, 395582165, 1075907395, 403373649, 411325632, 420362372, 428539601, 437532803, 445413071, 453967572, 463099414, 470685890, 479133268, 487620114, 496653910, 504641731, 512687764, 520639506, 529406082, 538631895, 546985622, 554571842, 563805848, 571373264, 580131477, 588971608, 596538960, 605304835, 614129239, 622074389, 630224531, 639303192, 646739535, 1074358215, 656080600, 663245906, 1076212680, 1077015560, 672849431, 681203414, 689626775, 696538176, 1077291978, 1076516809, 1075228614, 1076813773, 1075777483, 1074743244],
    [118, 104, 1, 1588289, 9829569, 18635904, 27024448, 35413184, 43801600, 52321409, 60710081, 69098561, 77069954, 85474433, 94264321, 102786577, 109337617, 1073744578, 119012354, 127417537, 1074287555, 136341137, 142892177, 152566850, 160971777, 169895633, 176446673, 1074829313, 186121410, 193478288, 203572943, 210132486, 220225223, 228719683, 235421200, 245515791, 252206612, 262168199, 270539911, 278264897, 288121862, 293887569, 304111175, 311819393, 319307472, 329278545, 336092756, 346160323, 352861776, 363750484, 369647316, 380370629, 388636245, 1075374533, 397035094, 403070534, 413924421, 421534791, 430589654, 436756116, 447487630, 455998994, 464413844, 470179526, 480255175, 489553618, 497698454, 503733894, 513826311, 522198023, 531496594, 1076428806, 1073830919, 539641366, 548019861, 555875459, 564946118, 573316622, 581041155, 590111814, 598482510, 605420545, 1075684297, 614614607, 623639557, 632037070, 640574484, 648683029, 657325650, 663903767, 673997958, 682359941, 690626261, 1075957704, 699294932, 705969175, 715277967, 722476563, 731012695, 739523671, 1074669515, 747642515, 756440780, 764419667, 772955799, 1076260804, 781466775, 790257165, 797974227, 806510295, 815423117, 823409879, 831938188, 840589005, 848715276, 857366093, 1076794381, 1075246026, 1077097482, 865492556, 1077363724],
    [98, 84, 13, 2405440, 8707136, 17087553, 25476225, 33864897, 42253313, 50773184, 59161664, 67550208, 77903040, 84336271, 92716160, 101113359, 111842894, 117776080, 126147584, 137008846, 145309393, 151568019, 1073747969, 161789056, 168090752, 176627346, 185122323, 195343360, 201776847, 212418193, 218676819, 226942543, 237671950, 243736274, 251976896, 262837902, 268901970, 279764115, 285906049, 1075336131, 293936784, 304929875, 311071937, 321469969, 330095635, 336237569, 346635857, 352902740, 361403457, 369958486, 378574424, 386718798, 394731026, 403496078, 411901654, 420517592, 428392147, 439147731, 445464149, 454596313, 461954708, 470621718, 479762009, 487120404, 495787670, 504927897, 513080858, 520429072, 529569432, 538230474, 546897495, 553983568, 563648025, 571784778, 1074829252, 579395284, 1075103685, 588289560, 596967066, 604847765, 614006423, 622116490, 630521434, 638402261, 647560727, 1074077639, 655670794, 1075662792, 663542990, 1074628618, 671956501, 680320014, 1074381769, 689503959, 697630426, 1073882050, 1075998667, 1076799430, 1076292557, 1076573132, 1077113868],
    [134, 120, 13, 1874945, 10394752, 18652289, 27040961, 35560512, 43949056, 52856386, 60726464, 68983873, 78174799, 86023886, 94799554, 1073746242, 102645264, 1074809795, 111729167, 119840401, 128353282, 136199760, 145676433, 153394897, 1074305025, 162301134, 169754320, 178838223, 186949137, 195462274, 203832914, 212507730, 221174353, 228891729, 238061268, 245505683, 254728209, 262184590, 270671443, 279741582, 288136790, 296671441, 304127502, 312614611, 321684494, 329833103, 337681998, 344497816, 354557459, 363627598, 372701765, 378183385, 388906201, 397444756, 406386840, 411737753, 422485531, 428777030, 439369238, 447519766, 456164948, 464976389, 470851144, 481312470, 489462998, 498107924, 506919621, 512400921, 520658520, 531512345, 537962138, 548707996, 557381720, 562994694, 573455513, 579905242, 590650908, 596957719, 1075372996, 604937862, 613459482, 623918742, 632069270, 641137285, 1075913733, 646487576, 655664284, 664682128, 674822168, 682532443, 688430808, 697607772, 707804246, 716479580, 725154008, 732864219, 738893401, 747675272, 758004825, 765240989, 773118679, 781493276, 791035538, 799710354, 806942939, 816750235, 1076195271, 823174746, 833920732, 840227415, 848338440, 856990940, 866533074, 875207890, 881761990, 890828891, 1076728838, 898670280, 907847197, 916388437, 1075168264, 925253138, 933927954, 941554325, 949790429, 958331605, 1074139081, 1074676682, 966567517, 974445207, 983103643, 1073916875, 991492123, 1076551628, 1000274453, 1075786701, 1077113869],
    [98, 84, 1, 2448513, 10802369, 17104000, 25492480, 33881280, 42269760, 50789505, 59178177, 67566657, 77430351, 86299649, 92732417, 103455298, 111213634, 119373519, 128374350, 137140944, 143195779, 153443329, 161928910, 170826243, 176749571, 1073747969, 186482191, 195483150, 204118530, 211876866, 218945043, 228425359, 237673090, 245431426, 254596820, 262495297, 271358544, 277413571, 286054099, 296049857, 305437266, 310967875, 319608467, 329866243, 1075333123, 338598083, 346095298, 355032131, 363648532, 1074298882, 371890370, 380329681, 388814484, 397187600, 403494483, 414154389, 422877906, 430931669, 438621313, 447649923, 456097365, 463918734, 473209362, 481263125, 489477716, 498375314, 506027203, 514118721, 523147331, 530240528, 539713041, 548182672, 555406480, 564878993, 572045911, 580572368, 589913219, 597211799, 606821969, 614397137, 622377687, 631174225, 1073795015, 639416854, 647951377, 1074606020, 655931927, 1076715461, 664728721, 672971350, 681235536, 689748630, 698137302, 1075681225, 1075176396, 1075975110, 1074951114, 1077064714, 1077341133, 1076570059, 1076316104],
    [98, 84, 8, 2417728, 10271937, 18668545, 27188288, 35445953, 43834433, 52223105, 60742784, 69131264, 78300674, 86163074, 94297280, 1073744514, 103466050, 111328450, 119832144, 1074287555, 128245393, 136494082, 145409218, 153411089, 1074829313, 161659970, 170574978, 178577105, 187745807, 194821249, 203718160, 212911759, 219986945, 228884112, 237297233, 246342737, 253541441, 263503571, 271631951, 280280595, 288285713, 1075364804, 295993040, 305446483, 313575119, 322223763, 330228881, 338452183, 347004119, 355638994, 363783377, 369810951, 380804626, 388293760, 397581906, 405071040, 413949463, 422501399, 428793417, 439525010, 447013888, 455892567, 464444503, 470736585, 480036437, 487890127, 495902345, 505202389, 513055823, 523001495, 531553431, 1073818565, 537583303, 546750100, 555411086, 563011081, 571915860, 580576974, 1076446217, 587914823, 597353998, 605330575, 613080711, 622370326, 630908494, 1074107399, 639420053, 647273487, 1075171270, 655924950, 664585749, 1074672584, 1077048328, 672579284, 680967700, 689479318, 697867862, 1077321677, 1075769291, 1076832204, 1076323274],
    [102, 88, 3, 351232, 10818560, 17120385, 25509057, 34028672, 42286081, 50805952, 59194432, 67451969, 77927616, 84639438, 92748800, 103093376, 109805198, 119870528, 126574287, 134848081, 1073747969, 145569363, 151748110, 160284306, 168123520, 179385537, 185179793, 196034261, 204551169, 210460239, 221093077, 229455507, 235232448, 244170322, 252665045, 263271489, 271556311, 279920277, 288175635, 294354510, 304979093, 313341651, 319512207, 330276375, 338769025, 344677903, 355442327, 364459606, 369450048, 380608087, 388972053, 395271317, 406533720, 414030869, 423179926, 430792389, 1075339717, 439721497, 447692373, 1075872707, 456734230, 462380117, 472751189, 479157269, 490419928, 1073793988, 498441817, 507066070, 514677829, 523607769, 531454981, 540751384, 546520666, 554278609, 1074341830, 565009541, 574305944, 579714770, 588977872, 597253844, 605241050, 615882393, 1076188098, 622532176, 630808212, 638164497, 647697936, 656104666, 663961242, 671989266, 681252496, 689659034, 697515546, 706436186, 1074896842, 1075703751, 714824730, 1076758476, 1074157513, 723082772, 1075227592, 1076556747, 1077097483, 1077366733, 731471444],
    [122, 108, 11, 2014273, 10822721, 18684992, 27073728, 35462144, 43850880, 52370497, 60759041, 69147777, 77511681, 86320129, 94313665, 103242446, 111221966, 119454849, 128263297, 1073746882, 136519247, 1074809795, 145038993, 153704527, 161553998, 169786561, 178595009, 186850959, 195370705, 202210000, 1074305025, 212403858, 220642449, 228794063, 237575827, 245979343, 254090833, 260637843, 270974033, 279402574, 287383182, 296822293, 304528593, 310976196, 321461843, 330258628, 337976849, 344523859, 354860049, 363404819, 371808399, 379657742, 389201622, 394855443, 403250820, 411925136, 422755990, 431040085, 438786062, 445589144, 456170575, 464068307, 472864900, 481476118, 489760405, 495811152, 506005010, 514890959, 520976912, 529073363, 540056719, 545857028, 556750852, 564725330, 571645465, 579411524, 590305348, 598279890, 1075363844, 606558350, 615589589, 624082518, 631447055, 640243727, 647169623, 657497103, 664083976, 672758484, 680854544, 689657939, 697474713, 705635864, 714808906, 723089940, 731029209, 739444247, 747970248, 756644500, 764740688, 773529098, 781524552, 790321363, 798164695, 1073816517, 806690440, 815486995, 823303769, 831465176, 1075926024, 840530516, 848626896, 857415306, 1075158985, 865818771, 873792656, 882581194, 1075695564, 1074660362, 890439319, 1074161606, 898573912, 1076276167, 1076556747, 1077097483, 1077374925],
    [102, 88, 9, 1301504, 10310657, 17136704, 25525248, 33914048, 42302592, 50822337, 59210753, 67599425, 77419649, 85720590, 92765313, 103365200, 109673552, 119633553, 127663758, 136175183, 144528577, 1073747969, 152917057, 161218126, 170743314, 177995470, 187520658, 195558546, 203284111, 213203539, 221075026, 227769427, 237362690, 1075344323, 1076933635, 245462609, 255146707, 261323987, 271048388, 279016977, 287914640, 294222992, 303291520, 313998023, 321869332, 328433299, 337501711, 347166421, 355023376, 361331728, 371711556, 1077201220, 379680465, 389363859, 397139461, 1074336645, 405355216, 414144084, 420052176, 430440146, 1074873218, 439827079, 447567058, 455859397, 464861715, 471038995, 481025093, 488061527, 498030292, 504618176, 514938389, 523713031, 530963650, 1073848455, 540104341, 548878407, 555318923, 564518018, 572332630, 581916308, 1075964872, 588504128, 598824533, 605887190, 614325967, 622664214, 631766098, 1076506569, 639056599, 647593675, 656931858, 664222359, 672759307, 682351749, 689388055, 697925195, 1076780998, 707124290, 1075743755, 714939030, 724032644, 1074710474, 732421124, 1074206669, 1075275724],
    [110, 96, 9, 353409, 10312897, 18701313, 27089985, 35478657, 43998272, 52386944, 60767810, 69164032, 75843074, 85941440, 94322306, 1073744386, 101008514, 1074287555, 111599119, 117923536, 127876290, 134831813, 142951618, 153672901, 159866384, 1074829313, 170605584, 176774789, 185558598, 193814151, 203873999, 210321102, 219243520, 229039759, 235363920, 246103120, 252272133, 260916872, 271113221, 277307024, 285818510, 293946434, 304667781, 313605780, 319120449, 329702991, 338377872, 344286209, 355401427, 363937364, 370108038, 378338902, 386489925, 397491732, 403654293, 1075363845, 413719621, 420036110, 428958784, 439287315, 445201998, 454387351, 1073811144, 464453203, 472595664, 479553239, 487390934, 496974850, 504718935, 1074617926, 1075686340, 512581319, 523173523, 531709652, 537879558, 546111126, 555293846, 563037717, 1076491209, 1077031945, 571301383, 580320856, 588725778, 596731072, 605625430, 613237832, 621608470, 630668882, 638936599, 647429656, 655834834, 1077306314, 663569608, 672734422, 680346632, 689372888, 697900054, 705644245, 713907783, 723205841, 730162369, 1076007943, 739704472, 748371601, 756114560, 765148689, 772760774, 1075234764, 781663890, 789530197, 1074212811, 798703185, 1076848589],
    [102, 88, 13, 515072, 10108032, 17153024, 25672833, 34061313, 42449985, 50707648, 59096128, 67484800, 77216768, 84541006, 92781761, 102382656, 109706894, 119160000, 126483982, 1073747969, 136060546, 143261390, 153353938, 161226434, 169991825, 178798288, 185581126, 193836564, 203685522, 211557954, 218732181, 228851282, 237518352, 247043798, 254287368, 261217871, 1075340354, 269467334, 277722708, 287432209, 296230536, 302888660, 311549583, 321404560, 1076145091, 1076417477, 330929814, 337763921, 346562248, 352949973, 363068946, 371727944, 1074867208, 378115669, 388095697, 396106754, 403543576, 414047754, 420224531, 431592982, 439500313, 445767375, 454276634, 464666329, 470933007, 481924694, 489832089, 495443072, 503944725, 514997849, 520608832, 529372760, 537386176, 547896912, 1076709319, 554679814, 563590807, 571219667, 580105818, 588889613, 596385427, 1074108363, 605271706, 615374538, 622444109, 629939795, 1075171273, 638424728, 648928906, 1074660292, 655343238, 663598740, 674094666, 1073896454, 1075748874, 680769242, 689553101, 697808471, 706330253, 1076021261, 713922264, 1074475980, 1077113868, 722974423, 731362839],
    [126, 112, 13, 2458625, 10737729, 18717888, 27106368, 35495040, 44014657, 52272128, 60791809, 69180609, 78095874, 86235137, 94346369, 103104132, 111385732, 120038978, 128834243, 1073744642, 1074287043, 136814095, 145204354, 153999363, 159882832, 1074829313, 170368719, 179152462, 187553923, 195903185, 201826000, 210476562, 219150416, 229745682, 237846161, 243768848, 252681875, 263038478, 270784641, 280042514, 285974162, 294648016, 305243282, 313597074, 321758926, 329504961, 338509329, 346267140, 353083090, 363722756, 372090510, 379927556, 386375312, 395026002, 403699856, 414295122, 422648914, 430153284, 439220292, 447194306, 1075367877, 455425092, 463707844, 472358479, 481294415, 489792722, 1074601988, 497368260, 505912975, 514848911, 522552513, 531700946, 538156681, 548264003, 556106817, 565001809, 571448915, 581826692, 589661313, 596590229, 606992580, 614040581, 624238167, 630431433, 638580752, 647857347, 655703638, 663723731, 673031764, 682621135, 691347159, 697540105, 705666579, 714703941, 724563983, 731201046, 739891337, 748520579, 758455959, 765188179, 773695188, 783621655, 789814857, 798742675, 807240707, 1075921929, 815087254, 823777481, 832144581, 840253142, 848943177, 857581204, 1074110408, 865025621, 1075701702, 874240019, 882746900, 890191381, 1076238279, 899274761, 907904067, 1075212234, 915357397, 924571859, 932807813, 1076790220, 1073933261, 1076573131, 1077113867],
    [118, 104, 9, 2070720, 10517633, 17169600, 25558144, 33946688, 42466433, 50723840, 59243521, 67632193, 77568128, 86015169, 92798145, 101307913, 1073749954, 111122432, 119569409, 128424523, 136739904, 143128076, 1075599361, 153065536, 161512513, 168294028, 178257486, 1075359744, 1076950016, 186932810, 195795022, 204198990, 210501189, 220617740, 227014220, 235798086, 245783628, 1077218244, 1074359300, 252680911, 260568780, 269352582, 279207626, 287808139, 296474254, 304086158, 311295494, 321281228, 330012814, 336451090, 346316426, 353483408, 361879251, 370146888, 380263492, 386898511, 394909321, 403570374, 413818052, 1076726790, 1074653190, 422025931, 430691854, 437255816, 446692366, 455498892, 464230414, 473290260, 480672896, 489134603, 498456148, 504102597, 514227200, 521255440, 532010708, 539254282, 546281999, 554956501, 564559040, 571587152, 582342292, 588250824, 596377093, 607149713, 613915158, 621401801, 630193672, 638320261, 648699012, 1076498440, 1074942981, 655334031, 663606994, 674258513, 680639184, 688772754, 699030532, 1075218375, 1074192391, 705951317, 716201489, 1076036547, 1073964035, 724277966, 732681422, 740293838, 749756113, 755619401, 765099533, 773298902, 781448725, 790265485, 798464662, 806614677, 815431373, 823630422, 831379026, 840597069, 848418451, 856806931, 865195603],
    [114, 100, 8, 2202817, 8772800, 17161344, 25549824, 33938496, 44022784, 51215945, 59238090, 68672585, 77577408, 1073744834, 1074285570, 1074566083, 1074850819, 84901516, 95012420, 101309508, 110747149, 119913485, 1076696064, 126975630, 136439435, 143253124, 1075140609, 152690317, 1075420161, 161987726, 1075701760, 168918606, 178382347, 185196036, 1076506625, 1077048321, 195411085, 202472974, 211936843, 218750660, 228187725, 237083649, 1077313540, 245491403, 254508753, 262134993, 270130893, 278388361, 287685837, 294512208, 302873737, 312851533, 321504260, 330006161, 337632401, 346135681, 355058820, 363560529, 371186769, 379567168, 386787024, 395411150, 404733056, 411926217, 422307475, 429382857, 439205394, 445480457, 453502538, 462937097, 472366158, 1073924038, 479166156, 489678550, 497925714, 506166801, 512222858, 522181649, 530684993, 537886220, 546170512, 556252366, 563437271, 571336208, 581417998, 588742164, 596108810, 606977682, 613768791, 623634131, 632143570, 639074004, 649062038, 656121359, 1074210759, 1076323269, 664239700, 674227798, 681287247, 688881228, 699393558, 706461384, 714432151, 724157636, 731627016, 739597847, 749463123, 756784847, 764903060, 774628883, 781950607, 790480469, 798736008, 807257621, 815513160, 824034965, 832423637],
]


def fill_table(table, me, low, high):
    if high - low == 1:
        for place, word in enumerate(STEPS[low]):
            table[place] = jnp.int32(word)
        return
    middle = (low + high) // 2
    lax.cond(
        me < middle,
        lambda: fill_table(table, me, low, middle),
        lambda: fill_table(table, me, middle, high),
    )


def neighbours(col, row):
    x = lax.rem(col, 2) * 2 + lax.rem(row // 2, 2)
    y, z, core = col // 2, row // 4, lax.rem(row, 2)
    found = [(x, y, z, 1 - core)]
    for move in (1, 3):
        for other in range(2):
            found.append((lax.rem(x + move, 4), y, z, other))
            found.append((x, lax.rem(y + move, 4), z, other))
            found.append((x, y, lax.rem(z + move, 4), other))
    return [{"col": y * 2 + x // 2, "row": z * 4 + lax.rem(x, 2) * 2 + core} for x, y, z, core in found]


def split(value):
    high = value.astype(jnp.bfloat16)
    return high, (value - high.astype(jnp.float32)).astype(jnp.bfloat16)


def spread_kernel(
    stored_ref, slots_ref, halves_ref,
    table, tile_even, tile_odd, halves_even, halves_odd, load_sem, store_sem, send_sem, recv_sem,
):
    active, half, block = stored_ref.shape[2:5]
    rows_per = active // CHUNKS
    col, row = lax.axis_index("col"), lax.axis_index("row")
    beside = neighbours(col, row)
    sibling = beside[0]
    tiles = halves_ref.shape[0]

    barrier = pltpu.get_barrier_semaphore()
    for device in beside:
        pl.semaphore_signal(barrier, inc=1, device_id=device, device_id_type=MESH)
    fill_table(table, col * lax.axis_size("row") + row, 0, len(STEPS))
    pl.semaphore_wait(barrier, len(beside))

    def hop(source, slot, chunk, place, device):
        return pltpu.make_async_remote_copy(
            src_ref=source,
            dst_ref=slots_ref.at[slot, pl.ds(chunk * rows_per, rows_per)],
            send_sem=send_sem.at[place],
            recv_sem=recv_sem.at[slot, chunk],
            device_id=device,
            device_id_type=MESH,
        )

    def arrival(slot, chunk):
        piece = slots_ref.at[slot, pl.ds(chunk * rows_per, rows_per)]
        hop(piece, slot, chunk, 0, sibling).wait_recv()

    tile = (tile_even, tile_odd)
    halves = (halves_even, halves_odd)

    def load(source, turn):
        return pltpu.make_async_copy(source, tile[turn], load_sem.at[turn])

    def store(turn, role):
        return pltpu.make_async_copy(halves[turn], halves_ref.at[role], store_sem.at[turn])

    def prepare(turn, order, role):
        load(slots_ref.at[0], turn).wait()

        @pl.when(order >= 2)
        def _():
            store(turn, 0).wait()

        for mirrored in range(2):
            @pl.when((role & 1) == mirrored)
            def _():
                @pl.loop(0, active)
                def _(line):
                    for slot in range(half):
                        value = tile[turn][line, slot]
                        high, low = split(value.T if mirrored else value)
                        halves[turn][line * half + slot, :block] = high
                        halves[turn][line * half + slot, block:] = low

        store(turn, role).start()

    steps = table[0]
    sends = table[1]

    @pl.loop(0, steps)
    def _(step):
        word = table[3 + step]
        slot = word & 63

        @pl.when((word >> 30) == 0)
        def _():
            chunk = (word >> 6) & 7
            device = {"col": (word >> 10) & 7, "row": (word >> 13) & 15}
            landing = (word >> 17) & 63
            place = (word >> 23) & 127

            @pl.when(((word >> 9) & 1) == 1)
            def _():
                arrival(slot, chunk)

            @pl.when(slot < 2)
            def _():
                piece = stored_ref.at[slot, 0, pl.ds(chunk * rows_per, rows_per)]
                hop(piece, landing, chunk, place, device).start()

            @pl.when(slot >= 2)
            def _():
                piece = slots_ref.at[slot, pl.ds(chunk * rows_per, rows_per)]
                hop(piece, landing, chunk, place, device).start()

        @pl.when((word >> 30) != 0)
        def _():
            order = (word >> 14) & 15
            for chunk in range(CHUNKS):
                @pl.when(((word >> (6 + chunk)) & 1) == 1)
                def _():
                    arrival(slot, chunk)

            for turn in range(2):
                @pl.when((order & 1) == turn)
                def _():
                    @pl.when(slot < 2)
                    def _():
                        load(stored_ref.at[slot, 0], turn).start()

                    @pl.when(slot >= 2)
                    def _():
                        load(slots_ref.at[slot], turn).start()

                    @pl.when(order >= 1)
                    def _():
                        prepare(1 - turn, order - 1, (word >> 18) & 15)

    prepare((tiles - 1) % 2, tiles - 1, table[2])

    @pl.loop(0, sends)
    def _(place):
        hop(slots_ref.at[0, pl.ds(0, rows_per)], 0, 0, place, sibling).wait_send()

    for turn in range(2):
        store(turn, 0).wait()


def spread(stored):
    most = max(entry[1] for entry in STEPS)
    active, half, block = stored.shape[2:5]
    return pl.pallas_call(
        spread_kernel,
        out_shape=(
            jax.ShapeDtypeStruct((SLOTS,) + stored.shape[2:], jnp.float32),
            jax.ShapeDtypeStruct((14, active * half, 2 * block, block), jnp.bfloat16),
        ),
        in_specs=[pl.BlockSpec(memory_space=pl.ANY)],
        out_specs=(pl.BlockSpec(memory_space=pl.ANY),) * 2,
        scratch_shapes=[
            pltpu.SMEM((max(len(entry) for entry in STEPS),), jnp.int32),
            pltpu.VMEM((active, half, block, block), jnp.float32),
            pltpu.VMEM((active, half, block, block), jnp.float32),
            pltpu.VMEM((active * half, 2 * block, block), jnp.bfloat16),
            pltpu.VMEM((active * half, 2 * block, block), jnp.bfloat16),
            pltpu.SemaphoreType.DMA((2,)),
            pltpu.SemaphoreType.DMA((2,)),
            pltpu.SemaphoreType.DMA((most,)),
            pltpu.SemaphoreType.DMA((SLOTS, CHUNKS)),
        ],
        compiler_params=pltpu.CompilerParams(
            collective_id=0, has_side_effects=True, vmem_limit_bytes=60 << 20
        ),
        name="spread",
    )(stored)[1]


def multiply_kernel(
    halves_ref, rows_ref, offs_ref, krow_ref, kcol_ref, kcnt_ref, out_ref,
    blocks, done_first, done_second, pairs, pair_count, bucket, bucket_count, facts, in_sem, out_sem,
):
    grid = lax.axis_size("row")
    tile_j = lax.axis_index("row")
    col_id = lax.axis_index("col")
    tiles, each = halves_ref.shape[:2]
    half = offs_ref.shape[1]
    active = each // half
    block = halves_ref.shape[-1]
    lanes, _, kept = krow_ref.shape
    slots = 2 * half
    steps = 2
    most = steps * slots * slots

    def load(place):
        return pltpu.make_async_copy(
            halves_ref.at[place], blocks.at[pl.ds(place * each, each)], in_sem.at[place]
        )

    waves = ([0, 1, 2, 3, 8, 9, 10, 11], [4, 5, 6, 7, 12, 13])
    for wave in waves:
        for place in wave:
            load(place).start()

    first = rows_ref[0, 0]
    bits = [rows_ref[1, 0] ^ first, rows_ref[2, 0] ^ first, rows_ref[4, 0] ^ first]

    def rank(value):
        return sum(
            jnp.where((value & bit) != 0, jnp.int32(1 << place), jnp.int32(0))
            for place, bit in enumerate(bits)
        )

    def shifts(tile_x, tile_y):
        both = ((tile_x, tile_y), (tile_y, tile_x))
        return [rank(offs_ref[x, slot, y]) for x, y in both for slot in range(half)]

    tile_is = [col_id * lanes + lane for lane in range(lanes)]
    tile_ks = [lax.rem(tile_is[0] + tile_j + place, grid) for place in range(3)]
    right_moves = [shifts(tile_k, tile_j) for tile_k in tile_ks]

    for place in range(lanes * active):
        pair_count[place] = 0
    for lane in range(lanes):
        for step in range(steps):
            left_moves = shifts(tile_is[lane], tile_ks[lane + step])
            for slot in range(slots):
                move = left_moves[slot]
                turn = move if slot >= half else 0
                left_base = (2 * (2 * lane + step) + slot // half) * each + slot % half
                for other in range(slots):
                    apart = move ^ right_moves[lane + step][other]
                    place = lane * active + apart
                    count = pair_count[place]
                    right_base = (8 + 2 * (lane + step) + other // half) * each + other % half
                    reach = move if other < half else apart
                    pairs[place * most + count] = (
                        turn | reach << 3 | left_base << 6 | right_base << 14
                    )
                    pair_count[place] = count + 1

    widest = 4
    room = 2 * kept
    for place in range(lanes * (widest + 1)):
        bucket_count[place] = 0
    for place in range(lanes * active):
        pair_count[place] = place << 3 | pair_count[place] << 7

    def put(lane, size, word):
        place = lane * (widest + 1) + size
        filled = bucket_count[place]
        bucket[place * room + filled] = word
        bucket_count[place] = filled + 1

    for lane in range(lanes):
        count = kcnt_ref[0, lane]
        together = 8

        @pl.loop(0, kept // together)
        def _(part):
            found = []
            for offset in range(together):
                item = part * together + offset
                row = rank(krow_ref[lane, 0, item])
                place = lane * active + (row ^ rank(kcol_ref[lane, 0, item]))
                found.append(jnp.where(item < count, pair_count[place] | row, 0))
            for offset in range(together):
                item = lane * kept + part * together + offset
                products = found[offset] >> 7
                facts[item] = found[offset] & 127
                begin = jnp.where(products > 0, ((products - 1) & 7) + 1, 0)
                put(lane, (begin + 1) >> 1, item | begin << 13)

                @pl.loop(0, (products - begin) >> 3)
                def _(more):
                    put(lane, widest, item | (begin + 8 * more) << 7 | 1 << 12 | 8 << 13)

    blocks[tiles * each] = jnp.zeros((2 * block, block), jnp.bfloat16)
    def gather(word, size):
        fact = facts[word & 127]
        row = fact & 7
        base = (fact >> 3) * most + ((word >> 7) & 31)
        products = word >> 13
        ones, twos = [], []
        for place in range(2 * size):
            inside = place < products
            code = pairs[base + jnp.where(inside, place, 0)]
            source = ((code >> 6) & 255) + (row ^ (code & 7)) * half
            ones.append(blocks[jnp.where(inside, source, tiles * each)])
            other = blocks[(code >> 14) + (row ^ ((code >> 3) & 7)) * half]
            twos.append(jnp.concatenate([other[:block], other[block:]], 1))
        total = jnp.dot(
            jnp.concatenate(ones, 1), jnp.concatenate(twos, 0), preferred_element_type=jnp.float32
        )
        total = total[:block] + total[block:]
        return total[:, :block] + total[:, block:]

    done = (done_first, done_second)

    def add(lane, word, into, total):
        again = ((word >> 12) & 1) == 1

        @pl.when(again)
        def _():
            done[lane][into] = done[lane][into] + total

        @pl.when(jnp.logical_not(again))
        def _():
            done[lane][into] = total

    def store(lane):
        return pltpu.make_async_copy(
            done[lane].at[pl.ds(0, kept)], out_ref.at[lane, 0], out_sem.at[lane]
        )

    for lane in range(lanes):
        for place in waves[lane]:
            load(place).wait()
        head = lane * (widest + 1)

        @pl.loop(0, bucket_count[head])
        def _(place):
            done[lane][bucket[head * room + place] & (kept - 1)] = jnp.zeros((block, block), jnp.float32)

        for size in range(1, widest + 1):
            count = bucket_count[head + size]

            @pl.loop(0, (count + 1) >> 1)
            def _(place):
                start = (head + size) * room + 2 * place
                one = bucket[start]
                paired = 2 * place + 1 < count
                two = bucket[jnp.where(paired, start + 1, start)]
                total_one = gather(one, size)
                total_two = gather(two, size)
                into_one = one & (kept - 1)
                into_two = jnp.where(paired, two & (kept - 1), kept)
                if size < widest:
                    done[lane][into_one] = total_one
                    done[lane][into_two] = total_two
                else:
                    add(lane, one, into_one, total_one)
                    add(lane, jnp.where(paired, two, 0), into_two, total_two)

        store(lane).start()

    for lane in range(lanes):
        store(lane).wait()


def multiply(halves, tile_rows, offsets, kept_rows, kept_cols, kept_count):
    block = halves.shape[-1]
    half = offsets.shape[1]
    tiles, each = halves.shape[:2]
    active = each // half
    lanes, _, kept = kept_rows.shape
    items = lanes * kept
    products = 2 * (2 * half) ** 2
    smem = pl.BlockSpec(memory_space=pltpu.SMEM)
    return pl.pallas_call(
        multiply_kernel,
        out_shape=jax.ShapeDtypeStruct((lanes, 1, kept, block, block), jnp.float32),
        in_specs=[pl.BlockSpec(memory_space=pl.ANY)] + [smem] * 5,
        out_specs=pl.BlockSpec(memory_space=pl.ANY),
        scratch_shapes=[
            pltpu.VMEM((tiles * each + 1, 2 * block, block), jnp.bfloat16),
            pltpu.VMEM((kept + 1, block, block), jnp.float32),
            pltpu.VMEM((kept + 1, block, block), jnp.float32),
            pltpu.SMEM((lanes * active * products,), jnp.int32),
            pltpu.SMEM((lanes * active,), jnp.int32),
            pltpu.SMEM((10 * items,), jnp.int32),
            pltpu.SMEM((10,), jnp.int32),
            pltpu.SMEM((items,), jnp.int32),
            pltpu.SemaphoreType.DMA((tiles,)),
            pltpu.SemaphoreType.DMA((lanes,)),
        ],
        compiler_params=pltpu.CompilerParams(vmem_limit_bytes=60 << 20),
        name="multiply",
    )(halves, tile_rows, offsets, kept_rows, kept_cols, kept_count)


def local(stored, tile_rows, offsets, kept_rows, kept_cols, kept_count):
    halves = spread(stored)
    return multiply(
        halves, tile_rows.T, jnp.swapaxes(offsets, 1, 2), kept_rows, kept_cols, kept_count.T
    )


def solution(mesh):
    in_specs = (
        P("col", "row", None, None, None, None),
        P(),
        P(),
        P("col", "row", None),
        P("col", "row", None),
        P("col", "row"),
    )
    out_specs = P("col", "row", None, None, None)
    return jax.shard_map(local, mesh=mesh, in_specs=in_specs, out_specs=out_specs, check_vma=False)
```

```python
import jax
import jax.numpy as jnp
from jax import lax
from jax.experimental import pallas as pl
from jax.experimental.pallas import tpu as pltpu
from jax.sharding import PartitionSpec as P

MESH = pl.DeviceIdType.MESH
CHUNKS = 4
SLOTS = 32
STEPS = [
    [118, 104, 12, 111, 88, 2242753, 9576576, 17965120, 26353856, 34742272, 42213505, 50601985, 60572290, 67379265, 77740033, 84156609, 92963464, 102113865, 111034441, 1073744578, 1074293762, 119683137, 1076663235, 1074844675, 126517960, 135668233, 1075118080, 144588809, 1073824768, 153237633, 1074105345, 160072264, 169222857, 178143433, 185211530, 1074651136, 1075979264, 1076258817, 193626632, 202777225, 212222152, 218766026, 228885069, 237387848, 245662221, 254165000, 262029449, 271596175, 279216781, 287719560, 296762063, 302949073, 312229954, 321927695, 330072786, 337780946, 345784322, 1076534212, 355482191, 363102925, 371335762, 379338946, 386537994, 397181010, 404890130, 1075503045, 414073484, 421796436, 430736018, 438444178, 445792846, 455350932, 464289810, 470688262, 479347214, 488127189, 496272019, 504513230, 512367178, 521052753, 531513868, 538458709, 546603731, 556679756, 564402900, 571384337, 580010638, 589568532, 596935251, 605037127, 615400140, 622344725, 630489619, 638591623, 647512592, 655899285, 663659153, 672014918, 681067088, 690625048, 697991894, 705569414, 714621584, 724179672, 731554327, 739123910, 748176080, 1075786758, 757733976, 765100630, 772809415, 781869707, 791288472, 798655126, 806363655, 815424011, 1077374983, 823829207, 832201291, 840606295, 848978635, 857383575, 865763862],
    [110, 96, 13, 109, 86, 2326721, 8650880, 17039424, 25427968, 33816768, 42336321, 50724993, 60712585, 67502081, 77824001, 84279489, 94267081, 102989953, 109587019, 1073743810, 117965316, 1074020352, 127821321, 136544321, 143141387, 153511437, 162234370, 1073782785, 1075897345, 170273422, 178677325, 187400322, 195439118, 203843213, 212566210, 220605006, 227148421, 237397709, 246514249, 254159566, 260571780, 270427209, 278921808, 288456713, 296364751, 302514884, 312755204, 321233092, 327811653, 338307663, 344457796, 354698308, 362807824, 371949634, 378143237, 1076170756, 1074883588, 388639247, 396362448, 405693648, 414285961, 420086469, 428354187, 439247952, 1076728837, 1075177477, 447062020, 455748239, 463471248, 472802320, 480879116, 487074507, 497304708, 506176138, 512756434, 522470596, 531341898, 537922066, 548299920, 1076502470, 1075736582, 556376780, 563087954, 571491985, 581673674, 588253842, 597051027, 606445636, 613689877, 621823697, 632389833, 638847574, 647382611, 656777348, 664021589, 672155153, 682336778, 689179286, 697714387, 707371660, 714344982, 722880019, 732537420, 739519189, 747652689, 756785812, 764684949, 773563092, 1077054407, 781454038, 790340180, 798728724, 1074450376, 1074731971, 1075540995],
    [134, 120, 11, 133, 110, 2259008, 10626112, 18636801, 27025473, 35414145, 43802817, 52322496, 60711040, 69099584, 77734912, 86399682, 94265344, 1073744322, 103176194, 109454915, 120087182, 1074287427, 1074823168, 128342146, 134620163, 142893647, 153507906, 160179279, 170181136, 176448015, 187324419, 193733647, 203735632, 210002639, 220362880, 227288271, 1073804228, 235463186, 243688147, 252207687, 262305984, 269354195, 1076955077, 279233168, 285631059, 294412820, 304764995, 311297107, 321700565, 330195157, 335962643, 346191872, 353240083, 363643413, 372138005, 377774735, 386687636, 397039747, 403448975, 411984470, 422363797, 430858389, 436626067, 447371459, 453903507, 1074100168, 464306773, 472801365, 480797262, 487350996, 498227342, 504497172, 514351630, 520905300, 531913425, 537273539, 547906254, 556947662, 562439299, 571523735, 581051520, 590633617, 596533910, 605315657, 612917895, 624056398, 630326356, 639943376, 647258633, 654860807, 1077254086, 664937664, 674519633, 680419862, 689201865, 696804039, 708100696, 716462609, 722601172, 730751702, 1075170311, 741655064, 749885454, 756155540, 766821080, 773224454, 781722825, 789865097, 800375448, 807172167, 815277193, 1074666505, 823182039, 832338119, 840574102, 848847372, 856736343, 865892487, 873997385, 882401868, 890290711, 899053702, 907682838, 915956364, 923329106, 933001223, 941106185, 949510860, 956883666, 966162502, 974791766, 1075730444, 982049426, 991328454, 999957718, 1075487691, 1076028427, 1076308938, 1076588493],
    [110, 96, 9, 109, 86, 401601, 8667264, 17055936, 25444416, 33832960, 42352769, 50741249, 59129921, 67641870, 75907265, 86526545, 92815888, 102375440, 109724306, 120343251, 126370384, 1073741824, 135929936, 143245972, 151667218, 162286163, 168313488, 177873040, 185221842, 195840659, 201867984, 211427536, 218776146, 229394963, 235414158, 245490326, 252723350, 260580046, 271739461, 279044694, 286277718, 294134350, 305293957, 312599254, 319832278, 329515733, 338848261, 346153494, 353386518, 363070037, 372402885, 380355287, 388235797, 1073765314, 1075360773, 396905105, 405398088, 413401749, 1077202883, 422070801, 430563848, 436994575, 447236817, 455729864, 463872649, 1074604998, 471223002, 480895624, 489038345, 1076456456, 496388634, 506446489, 514204361, 521685659, 531350167, 539370057, 1076736009, 546720410, 556515927, 562954322, 572017179, 581943897, 588120210, 1077004228, 597183067, 1074143175, 607109849, 613155407, 622750424, 632013335, 638321295, 647514843, 657441305, 663487183, 1075730378, 673082008, 680116948, 688783570, 697715290, 705282644, 713949202, 723413528, 730448404, 738598977, 1075219403, 748579416, 756531804, 763764865, 773308956, 780541953, 1074451404, 790086364, 798474908, 1074996173, 1076061197],
    [110, 96, 13, 109, 86, 1884160, 8820737, 18677953, 27041984, 35430400, 43950081, 52207744, 60596288, 69116097, 77504641, 84449472, 94159040, 102563841, 111059009, 1073744834, 119718082, 128516675, 136624836, 1074287427, 1074823168, 144883714, 153682051, 161790532, 170049666, 178061441, 186956420, 194822208, 204013763, 210549319, 220381250, 229179395, 235715271, 245153920, 253558849, 260880903, 1073792965, 271237711, 277658247, 288293585, 1074076614, 1075401735, 296403663, 304396804, 313205267, 1075159044, 1075962884, 319862915, 329958031, 338625169, 346735119, 353540229, 363790929, 371761685, 378050560, 386712208, 397345297, 405316309, 411473985, 420266512, 430645907, 438870677, 445028481, 453829198, 464200403, 472425045, 478995086, 488028758, 498401365, 504423060, 512923653, 522920531, 529588756, 538360342, 548732949, 554869386, 562469057, 571785879, 582287509, 588692182, 596951639, 607453397, 613589706, 621863636, 630241347, 639181458, 647412374, 655671831, 664347154, 672309834, 680040512, 689226455, 697901778, 705864202, 713595008, 722264590, 731456082, 1076239370, 739041998, 747804741, 1075737544, 1077055433, 756193477, 764199632, 772847619, 780976720, 1074720715, 789635668, 798013635, 1076833228, 1076590541],
    [94, 80, 3, 93, 70, 1179713, 8683584, 17072256, 25460736, 33849536, 42369153, 50757825, 59146305, 68288513, 75923457, 86280848, 93454529, 103058128, 1073741824, 110231681, 120121041, 128223760, 135037444, 144581326, 153782276, 162195026, 168592004, 178135630, 187336836, 195618449, 202146372, 211821135, 220891204, 229303826, 235700932, 245244430, 1073762308, 254445764, 262727185, 270541327, 279218768, 287893073, 295707343, 305048131, 313190098, 320742030, 1074826051, 330213571, 338355858, 346038927, 353534663, 363767811, 372164230, 379855557, 388933763, 397329926, 405021189, 1074327174, 414106694, 422742611, 430187077, 1076701445, 439272646, 447908563, 455352453, 463005204, 472951509, 480911874, 488171220, 498117205, 506208320, 1076452226, 513328790, 523405843, 531243074, 538083911, 546891348, 556837397, 564928640, 572049110, 582126227, 590094336, 596804103, 605603414, 615557781, 623517890, 630769174, 640295042, 647554708, 657203392, 663913095, 1075426250, 1077008329, 1075184647, 1074165707, 1077321676, 1075766216, 1076044808, 1076318157],
    [110, 96, 10, 109, 86, 1892544, 10280960, 18669696, 27058240, 35578049, 43966593, 52877890, 60907586, 69132289, 77520961, 86418958, 94822414, 102851074, 111598274, 1073746178, 1074809795, 119973582, 128377038, 1074298880, 136763394, 144793730, 153921233, 162062864, 170317954, 178348226, 187737104, 195617488, 204169745, 210303695, 221291728, 229335697, 235469455, 246195345, 254206542, 262889681, 271114832, 277666451, 288400464, 296444497, 303094484, 312910926, 321315470, 330260558, 1073798084, 336132687, 346858513, 355000976, 363815054, 370203156, 380675216, 388980942, 394852879, 405185678, 414146574, 420797077, 430744657, 437215890, 445700756, 453813847, 462643734, 471128597, 479241359, 487547474, 496302744, 504530585, 512975510, 521069192, 529849045, 538347224, 546530006, 554490579, 563250713, 571433490, 1075393479, 579918420, 588031511, 596599506, 1076975557, 605346389, 613582425, 622027350, 631167578, 638748377, 647944730, 655402191, 664074776, 671917719, 1075154889, 681499354, 688841416, 697345039, 1074655178, 705485395, 714007112, 722896024, 1076770763, 731183704, 739172872, 747676751, 1077304328, 756996762, 764192471, 772594195, 781616152, 1075742668, 1074193350, 1076044806, 789903576, 798393432, 1076325325],
    [126, 112, 7, 125, 102, 2418880, 8691777, 19030081, 25477185, 33865729, 42254465, 50643137, 59162624, 67551424, 75939968, 84320782, 94790350, 103082048, 109494336, 119956046, 128247936, 134783503, 144622290, 1073741824, 153510542, 161802240, 168338063, 178176658, 187064334, 193503823, 201648784, 210289282, 218669775, 229401233, 235203152, 243843778, 252092494, 262955601, 268757520, 277398018, 287752853, 294035598, 304898769, 311225044, 319341122, 329827030, 335978702, 346841617, 352643792, 1073762306, 1074836419, 362725970, 371769878, 379740289, 386179265, 398248599, 404668946, 411746840, 421683201, 431286296, 438992899, 447267414, 455237825, 464158915, 473745943, 480821910, 489971926, 497713283, 507300439, 514245333, 523526166, 531267651, 540854999, 545964760, 554615385, 562339841, 573989013, 582281432, 587907736, 596558489, 604283009, 615800982, 624224408, 631685653, 638501401, 649486357, 657236121, 663546388, 673628757, 680444633, 691429461, 699179097, 705489556, 713736792, 724852822, 733276248, 741122265, 1076948933, 747815561, 758538453, 766287897, 773507610, 781369929, 789996115, 798400722, 807062106, 814924297, 823550483, 832086168, 840616602, 848478921, 857105043, 865640664, 874171098, 1076691977, 882270931, 890675346, 898427476, 907583576, 915841106, 924229650, 1074092998, 1075419079, 932749336, 1075176395, 1075979275, 1076252612, 1074706381, 1077332936, 1074473930, 1076584396],
    [98, 84, 5, 97, 74, 2308224, 10305665, 18686081, 27074753, 35594304, 43851841, 52371648, 60628993, 69567106, 77537408, 86194240, 94191809, 102703104, 111510018, 1073744514, 119748608, 127746049, 1074287555, 1074823168, 136675394, 144914624, 152911937, 161948244, 170229954, 178993809, 185287377, 195502740, 204440210, 212550357, 220936401, 229605970, 237716053, 243874387, 254223060, 263160338, 271270549, 277813776, 287777300, 295805646, 302727761, 313210961, 320971278, 329990677, 336534096, 346137230, 353059345, 363542545, 372212434, 378092243, 386753239, 396468814, 403258003, 411918999, 422027476, 428556433, 437197456, 445850200, 455581780, 464861272, 470639191, 1073798086, 1075389384, 1075930120, 479404568, 489136276, 498415640, 504193559, 1076210628, 512959192, 522690580, 531970264, 538395353, 546513560, 557136024, 563560985, 1076479946, 571957839, 579418643, 588855834, 597254678, 604969680, 614032086, 622410458, 630669977, 1074147271, 639187546, 647586390, 1076781003, 655843983, 664353434, 672752278, 681009871, 689398287, 1075753925, 1077071820, 697778777, 1074739145, 1077368781],
    [110, 96, 13, 109, 86, 2557953, 10256577, 17105024, 25493696, 33882176, 42270720, 50790529, 59179073, 67567617, 78055553, 85753985, 92733633, 103507665, 111215312, 120138434, 128098512, 137062033, 145031811, 1073741824, 153551442, 161941697, 170172498, 179135619, 186712720, 195635778, 203595920, 212559441, 220529219, 229048850, 237439041, 245669906, 254633027, 262472195, 270598672, 279652480, 287481872, 296576003, 304153168, 313076354, 321036368, 329999889, 336396869, 346489554, 355149888, 363110610, 372335685, 380043922, 388573698, 396664978, 1073764354, 405628611, 413466819, 422085263, 430647296, 1075349507, 439445125, 445448325, 455813312, 463241281, 472999621, 479002821, 489194191, 498018894, 506553861, 512557061, 523184654, 530350081, 1074319365, 538535445, 547914319, 556739214, 563544648, 572090005, 581468687, 590293710, 597255893, 607455892, 615975443, 622265032, 630670998, 641141395, 1074868169, 647430792, 655976021, 666176212, 672613910, 682953236, 1076715466, 689784407, 699861715, 706150920, 714557142, 723059340, 733416019, 1075680264, 1075176388, 1075979268, 740116119, 748225036, 758450772, 764888662, 773391052, 782059031, 790168140, 1076249612, 798836439, 1074181063, 1077078982, 1076563917, 1074755531],
    [106, 92, 10, 105, 82, 1925248, 10313920, 18702336, 27091008, 35610817, 43999297, 52387841, 60776577, 69059214, 78055119, 84238543, 94593166, 1073744834, 1074287555, 102613710, 111370446, 1074823168, 119390734, 128779857, 136536078, 145318610, 152945230, 162465427, 170090574, 179010068, 186892498, 196019923, 201810629, 212564628, 220578384, 229574163, 235496149, 246119124, 255132885, 260661845, 271547095, 280298581, 285565455, 294216341, 304839252, 313853077, 319251013, 330267287, 338626131, 344547861, 355432983, 364184597, 369451663, 377971205, 388987479, 397215441, 405895189, 413385298, 422142034, 430376079, 1073805254, 439449813, 446939794, 455696530, 463930383, 470246021, 481392725, 488882706, 497639442, 1077221381, 505873999, 512057423, 523335829, 530956816, 1075409860, 539821585, 547734224, 557021782, 564987537, 1076987850, 572899984, 582187542, 1074126792, 588842585, 599095835, 607346715, 614139482, 624130774, 632513115, 639305370, 649427675, 657678555, 664471066, 674593435, 682844315, 689505945, 699628182, 706283033, 1075711943, 1074684873, 1076012041, 716535899, 723191514, 731871768, 739837657, 748649176, 1076287436, 757037656, 765426328, 1075261387, 1076849613],
    [110, 96, 10, 109, 86, 354304, 8724673, 17121472, 25641025, 33898624, 42418305, 50675712, 59195585, 67452992, 75965070, 84240576, 92749825, 101017728, 109387841, 117760657, 126436050, 1073741824, 134685262, 142960704, 151315153, 159851022, 170740240, 176480785, 187517520, 193273985, 201646673, 212683472, 218833487, 227205844, 237849232, 243605505, 252529301, 260514510, 269306581, 277553807, 286081622, 294208018, 302860821, 311108303, 319635990, 328026709, 336273935, 344801942, 353462337, 363922003, 1073761220, 370098821, 378356438, 387007174, 395921422, 405864979, 412435032, 420037266, 428950150, 436920916, 446253198, 456196819, 462766616, 470368850, 478864020, 487942743, 498139795, 504709848, 512836166, 520806932, 529623233, 539828370, 1074303939, 546652824, 554779142, 563440151, 573382866, 1074852802, 1076958214, 580470862, 590159890, 597248206, 607068246, 613859865, 622160599, 632234134, 1075146696, 638534341, 647414361, 655714967, 665657426, 1076727751, 672088645, 680968921, 689006721, 699343062, 1074651081, 705643013, 714523289, 722561025, 732897302, 1075708933, 739959386, 748363928, 756736666, 765141208, 773513946, 781918296, 1074165706, 1077322700, 1076028428, 790290970, 798695448, 1076304843, 1075538893],
    [106, 92, 3, 105, 82, 2070720, 10330113, 18718913, 27107393, 35627072, 44015616, 52404352, 60031618, 68796546, 77570240, 85956736, 94216321, 101032592, 110363330, 119522001, 1073744066, 127899648, 1074287555, 134718099, 1074823168, 144450194, 153076241, 161454144, 168272595, 178004498, 186630801, 195401872, 201826899, 211558994, 220185169, 228833812, 235381267, 245113554, 253616847, 262388308, 269066951, 278790291, 287171087, 296204942, 302359248, 312344787, 320725583, 329619664, 336175623, 345620482, 354287635, 363313678, 369730183, 379174978, 387842131, 396606164, 403546649, 411673159, 420741122, 429777551, 438811214, 445489753, 1073797127, 453354064, 463061186, 472383555, 480614480, 487432921, 495297040, 503964373, 514326659, 522557456, 529375897, 539623623, 546037785, 555989652, 563347522, 571073173, 581417678, 589955143, 596369561, 1075389381, 1075930117, 604627541, 614990019, 623378435, 629924057, 640286727, 646701145, 1076212681, 654959125, 665452679, 674234903, 680772118, 1077013446, 688906776, 699400919, 705684056, 716178007, 1076508616, 722461336, 732955287, 1077303243, 739492502, 1075224524, 747881174, 1075759050, 1074212804, 756269654, 764404440, 1076842445],
    [102, 88, 11, 101, 78, 2089985, 8759489, 18809025, 25526400, 33914880, 42303680, 50692160, 59211969, 67600513, 75989057, 86180558, 94364737, 101034113, 109543425, 117934735, 128123534, 136307905, 1073741824, 145425103, 151365697, 161473665, 170590799, 176932483, 185174158, 195756175, 201951438, 210757250, 218875459, 228786766, 235251713, 246088207, 252152015, 260818435, 1073760771, 269060622, 279117838, 286246596, 294094927, 304021569, 311420610, 319662800, 329187457, 336578052, 345237202, 353217040, 362741761, 369994384, 378521220, 387252881, 1074303108, 394889294, 403695170, 412418769, 420734482, 428714576, 437584465, 1074845762, 446005780, 1075388358, 454026242, 462750225, 471173140, 479691413, 1075672005, 487572548, 496216213, 504857173, 512476355, 521767507, 529892052, 538544851, 546800341, 554936533, 563340882, 572099219, 1076997065, 580487699, 588874443, 1076492232, 596895378, 605268053, 614040139, 622297621, 630433813, 639205899, 647332500, 655722644, 664371851, 672498260, 1077285899, 680888404, 689668749, 697665748, 706446029, 713525263, 723223117, 1075209162, 1076012042, 731611661, 1076285388, 1074725901, 1074229191],
    [90, 76, 9, 89, 66, 1302592, 9691264, 18079744, 26468544, 34988225, 43376705, 52790850, 60153985, 69458563, 76931073, 86345218, 94624323, 1073744642, 1074287171, 1074823168, 103122114, 111401155, 118243917, 126214863, 136676482, 144955395, 153239759, 159769103, 1073803264, 170624654, 176677508, 186793999, 193323663, 204178958, 211959951, 218489423, 229344846, 237125711, 246274769, 254510798, 262947408, 271812243, 279960276, 286016141, 295952596, 305366547, 313514580, 321938002, 329506900, 338921043, 347069076, 354672788, 364086995, 369902093, 378775052, 389011988, 397165200, 405004308, 412329612, 420233933, 430824017, 437495500, 447496720, 455989905, 462661196, 472662736, 481155601, 487958229, 498098706, 504756822, 513255063, 523264722, 529922582, 538289813, 548430482, 555088534, 563455573, 571975255, 580363991, 1076959175, 588643030, 597009941, 1075141574, 1075414981, 1074131973, 605529623, 612885188, 621273668, 1077291976, 629662212, 1076517892, 1075744714, 1074720713, 1076831179, 1076061195],
    [94, 80, 9, 93, 70, 2195585, 8765504, 17285249, 25673729, 33931456, 42319872, 50708608, 59228225, 69698185, 76005569, 86475465, 1073741824, 94863945, 103252489, 1073768448, 111921868, 1076408321, 118457034, 128698892, 136413377, 145476172, 152011274, 162253452, 170746447, 177177226, 1076943810, 1075387394, 185322190, 195912207, 202342986, 212593296, 221078159, 228687937, 237759056, 246244047, 253853697, 262925008, 269591051, 279702032, 286474834, 294879757, 302770772, 311517907, 320045645, 327936532, 336446148, 345072147, 353477195, 361491156, 370131461, 378626643, 387154573, 395045524, 403554948, 412443285, 420709069, 429247121, 437240453, 445735571, 454140619, 462146126, 470663748, 479412754, 487694987, 495700494, 504349381, 513106453, 521267734, 529515077, 538133138, 1075672069, 546433750, 554549764, 563299026, 1077252100, 571853329, 580215381, 588630609, 597017286, 605381333, 613141134, 622182918, 630319766, 638960262, 647096918, 655737414, 1074906118, 1074146310, 664128209, 1076778947, 1075219399, 1074449415, 1074734024, 1076061192],
    [110, 96, 13, 104, 81, 1448960, 10364032, 18752576, 27141312, 35529728, 44049537, 52438081, 60573324, 69215233, 76946496, 85992641, 92956238, 102112448, 111846991, 118122190, 127278208, 137012751, 143287822, 1073750016, 151395920, 1075865601, 162170385, 168436753, 176842382, 184950288, 195724945, 201991313, 211568204, 218504912, 229279441, 235545809, 245122572, 252059280, 262833745, 269100113, 277882387, 287065804, 295705619, 304785039, 311436883, 321275533, 329260115, 338339535, 344991379, 354830029, 362814611, 372418119, 378545875, 388384269, 396369107, 405972679, 413550157, 421797527, 431138311, 437143058, 1076408583, 447915143, 1076948934, 455613961, 462693385, 470697554, 1076693955, 1074355144, 479110804, 488906327, 495863506, 504399446, 514072087, 521029266, 1075417028, 529442516, 539238103, 546219604, 554976921, 564665929, 571745353, 580265113, 1074643909, 1073873925, 588285590, 596647514, 605308633, 613819609, 621840086, 630474265, 640163529, 647242953, 655762457, 1074161602, 663782934, 672417369, 682106505, 689185929, 697705561, 1076272137, 705603092, 714087962, 723158744, 730865370, 740067029, 747642522, 756844181, 1075762123, 1074992139, 1075279818, 765101656, 773621333, 782009877, 790267544, 798656024],
    [126, 112, 12, 125, 102, 369729, 9962624, 18351104, 26739776, 35128512, 43648193, 52036673, 61104783, 68813825, 75867137, 85591169, 92538449, 103047695, 109446658, 117810369, 126092817, 136602319, 143001282, 151364737, 159778370, 170156623, 178890450, 1073750017, 185075396, 193872464, 204056146, 212610630, 218760723, 227172935, 237241415, 245999250, 254553606, 260572804, 269116039, 279184519, 287942162, 294389460, 304885446, 312739335, 319447047, 330269711, 336332308, 344469141, 354682567, 361390279, 372606033, 1075863493, 378275476, 1075615751, 386412053, 395314761, 403726409, 414680643, 419966549, 428869129, 437280777, 447710351, 455880326, 461899332, 470835913, 479200457, 490178051, 495715924, 1075367880, 1074607110, 503852757, 512099970, 521167497, 529532041, 539985103, 1077231618, 1073844233, 548548247, 554305171, 562971280, 573539407, 582102615, 587728388, 596525584, 607618755, 1074906116, 615788054, 621413971, 630080208, 641173123, 1074144259, 649211607, 654575249, 664027268, 671745747, 682984465, 691154455, 697581764, 708150417, 716451414, 721684177, 731267219, 741704913, 750005974, 756432915, 765043924, 775302744, 781860994, 790209684, 800337558, 806764627, 815637584, 1076254666, 1075219403, 825634520, 831799300, 840803536, 850800152, 857358402, 865707092, 875966104, 882262227, 890872852, 898908228, 907912208, 916078786, 924689552, 1074457548, 932855810, 1076572110, 1076851661],
    [114, 100, 10, 107, 84, 285824, 9987265, 18375745, 26895488, 35284160, 43672576, 52061248, 60162764, 68707457, 76053569, 85484545, 92694146, 102105676, 109739597, 119694990, 126248642, 135660172, 143294093, 151807492, 160825868, 168451214, 176875087, 184968770, 193601678, 202014221, 210134530, 218389696, 1073754114, 227305028, 235437057, 1076911043, 243933774, 253912142, 260859588, 269384780, 1075350469, 1074326533, 277488142, 287466510, 296806032, 302668814, 311042766, 321021134, 327870159, 335830080, 1076692934, 1074094086, 344728211, 353035919, 361921683, 369894099, 378201615, 387341842, 395059731, 405858000, 412253203, 420225619, 431023632, 437419091, 445539847, 456189520, 462839378, 470705735, 479651537, 488005266, 495871687, 504817297, 512517764, 520379392, 1075944452, 529426055, 538625749, 545938510, 1075695623, 554854024, 563791509, 571762185, 579763212, 588670603, 597345813, 605316809, 613579987, 621962952, 630900309, 638871177, 646601934, 655779403, 664200721, 672425545, 680426700, 1074934793, 689071624, 697755217, 705592460, 1077298122, 1073914890, 714499787, 723314260, 730365121, 739665419, 748611222, 755530881, 1076286475, 764569160, 773645844, 780828365, 1075252232, 1074751496, 790554198, 798383826, 807331350, 815720150, 823977620, 832366292],
    [118, 104, 1, 115, 92, 271360, 8766528, 18367681, 26756097, 35144769, 43533441, 52053120, 60441600, 68830400, 75769024, 84403788, 93996096, 103050958, 109323328, 117958156, 128216718, 134629060, 142984384, 151529164, 160056901, 170421444, 176572036, 187049485, 193717840, 202000069, 212364420, 218514948, 227403409, 235415180, 244074003, 252331525, 262695940, 268846660, 279315475, 288081426, 1073745924, 1074818052, 294405715, 302663301, 313289861, 321258579, 330024530, 1076658181, 1073795011, 336348819, 346844165, 354813075, 363579090, 369903315, 380136516, 388367571, 397133458, 405564485, 411952721, 419963980, 430730437, 436479104, 445113484, 455372302, 462284305, 472262285, 480538190, 487072780, 495707792, 504262296, 514205261, 520873488, 529559252, 539371213, 546039504, 554978838, 565446159, 570803200, 580538069, 590612047, 596502225, 605703829, 615777999, 621274316, 1074599878, 1075144710, 630091480, 640943759, 646300800, 1076471751, 655257112, 664134861, 672531585, 681201173, 689300557, 697697281, 1076223944, 1075720200, 705719892, 714466317, 722863169, 731139734, 739632269, 748029121, 1077038026, 756051604, 765208279, 773317633, 781086296, 790374039, 798483585, 1074437058, 1075508226, 806637270, 815539799, 823649345, 1077355467, 831548948, 840705559, 848815297, 1076053961, 857362005, 865357398],
    [122, 108, 1, 121, 98, 302208, 10527744, 18916480, 27305024, 35693760, 44213377, 52602049, 60990465, 67411136, 77767745, 84198930, 94701122, 101236432, 109364882, 119867010, 128106001, 134530642, 145032898, 153271953, 159696594, 170198530, 178437713, 1073745922, 187491923, 193242195, 201762516, 210288144, 1074815939, 221447894, 229426179, 235447895, 243705364, 252231248, 263390742, 271508567, 277128851, 285648532, 295878353, 302843480, 313320595, 319334039, 327457792, 338888342, 347006103, 352888535, 361145940, 372022869, 378611225, 388949207, 394569427, 403226256, 1075872708, 412165721, 422372563, 428385815, 439131797, 445720217, 455927315, 461677587, 472686293, 1073802181, 479004184, 489612311, 497851925, 1076431814, 504170200, 514639043, 520395840, 531826262, 540066964, 548453588, 554772185, 564970627, 573750341, 580167240, 588580507, 598787092, 605464266, 613983836, 624082053, 630523611, 640730324, 647407242, 655926940, 665894036, 671942296, 682673236, 689350154, 697870044, 707968005, 714385032, 722798171, 732742723, 739681866, 748201500, 758299845, 764716744, 1074354186, 773129755, 782025884, 791723092, 798270984, 807191580, 1075416072, 816888852, 1074657225, 824100570, 832216257, 1077290956, 840746204, 1076256711, 848993281, 857523292, 865770561, 874432026, 882547841, 891209306, 899597978, 1075746766, 1075245003, 1076835279, 1077102541],
    [106, 92, 10, 105, 82, 1836096, 10519553, 18908289, 27427840, 35816512, 44074177, 52462657, 61006352, 69371072, 77333696, 86148224, 92702290, 102949520, 110887936, 117868242, 128115408, 136053888, 145403411, 151422610, 161669712, 168698945, 179080724, 184976914, 195747986, 202253441, 213036758, 218662615, 229433559, 235807745, 246722072, 252216855, 262987799, 269362369, 280276696, 285771351, 296804885, 303179345, 313699990, 319588037, 330096727, 336733713, 347385432, 352880279, 363651223, 370288337, 380284499, 386696837, 397074642, 403842705, 1073750979, 413961876, 420251205, 431022805, 439231621, 448048792, 453805573, 464577173, 472785989, 1075862468, 1075347461, 480947859, 489349138, 497951941, 1073793986, 506637910, 514515026, 523117573, 532327961, 540074581, 548537488, 554600071, 565882457, 571663002, 582091984, 590122708, 596828762, 607257616, 613320391, 623554259, 630383130, 640812112, 646874695, 657231444, 663937754, 672400467, 683323097, 689177747, 700100249, 706142811, 714343635, 1074336715, 1074876364, 724741654, 731308763, 739509267, 747537927, 756474395, 1074628554, 1074123783, 764863131, 1075191753, 1075734472, 1076277197, 1076818886, 1077098446, 1077373903],
    [110, 96, 9, 109, 86, 2581696, 10387521, 18932737, 27321537, 35841024, 44229760, 52487233, 60875905, 69393936, 77784256, 86467712, 94273729, 102949952, 111337104, 120022016, 127827969, 136502864, 145187904, 152993921, 159966722, 170321619, 178446032, 186991618, 195068498, 201909890, 212264467, 220782225, 228934786, 235578004, 243852866, 254207635, 262725137, 270877762, 278954514, 285796034, 296150611, 304668369, 311223939, 321209538, 329286354, 1073743874, 336389699, 346611281, 355288212, 362840722, 369944259, 378199058, 389243921, 395346454, 403498499, 411884566, 420127444, 430785748, 1074288643, 437313044, 445292564, 455951380, 462478548, 470458964, 481117268, 487644244, 498295889, 504553111, 515073233, 520805522, 531850385, 538107479, 1075348421, 548619283, 554730198, 562879702, 1073796038, 573785299, 580166296, 588577944, 1074862023, 598950995, 605061782, 613211286, 624116883, 1075145673, 630497816, 639297229, 647298072, 656369301, 664052440, 672851597, 680852696, 689923797, 1076474824, 697606744, 706405901, 714407000, 723478037, 730890838, 739960397, 747428950, 757032533, 1077009421, 1075720132, 764468372, 1076782028, 772463698, 1076017098, 781377047, 1077333963, 789241042, 798154455, 1074726862, 1074227151],
    [106, 92, 9, 105, 82, 296001, 8676481, 18664641, 27313153, 35701953, 44090497, 52479041, 60998848, 69387264, 77775936, 84436688, 94161921, 100959361, 111330432, 117991056, 127716481, 134513857, 143156752, 151290881, 161270849, 170829521, 176711248, 184872466, 195995153, 204105219, 210030291, 221161041, 229271107, 235195923, 1073744643, 243967168, 254568004, 260361875, 269141590, 1074283332, 279881361, 288681046, 296379523, 302687360, 313287812, 319082067, 327992919, 336241728, 346842116, 352644690, 361416342, 370067096, 378184704, 389344406, 397435991, 1073779654, 403490455, 414213271, 423003717, 428142290, 437044951, 447767767, 456558213, 461696658, 470468310, 481619158, 489448644, 498501317, 1074846789, 504022550, 512673496, 523562006, 531260611, 540443653, 546096663, 554616344, 565208087, 571647128, 579782232, 588399633, 597337748, 1075656649, 605472459, 613565649, 622503444, 1077238722, 630638219, 638731409, 647144472, 1075424202, 655508561, 664446548, 671376449, 681354773, 1076490184, 688153793, 698132117, 704930817, 714253528, 722912779, 1076762573, 731030616, 1075213255, 739690059, 748463701, 1077052427, 1074193356, 756721364, 765241045, 1076039631, 1074751438],
    [106, 92, 9, 103, 80, 2172032, 10560704, 18949120, 27337792, 35857473, 44246145, 52634817, 61023233, 67716688, 75834448, 84352721, 94873170, 101410515, 109651668, 119881219, 128427666, 136922820, 143072785, 153593554, 162219220, 168238673, 177030869, 187147794, 193799831, 203767363, 210585237, 221087447, 227353815, 235871832, 244262617, 252528213, 263029911, 269297175, 1073746882, 279264899, 286205465, 1074807299, 296437396, 304972823, 310977684, 321207491, 328304346, 338249220, 347020827, 352658960, 361703065, 1073781701, 370247322, 380323348, 386475028, 397352667, 402990736, 413746820, 420578906, 428680791, 439295579, 444933840, 454133274, 464078404, 472850075, 1075372036, 478757904, 489522263, 495527508, 504307416, 514540628, 523871449, 529473048, 540648601, 546653910, 554639000, 563029593, 574202969, 579561043, 588717660, 599368729, 605373974, 613883612, 622544089, 1075912647, 629612177, 638928534, 647568989, 1075662793, 655058451, 664346141, 1074628550, 1074121672, 672482902, 680992412, 688473232, 697900765, 1074403274, 705250512, 714546716, 1075213259, 1077065679, 723207193, 731455133, 739067413, 1077341134, 1076572109, 747333267, 1076848588, 756761753, 765150297],
    [118, 104, 3, 117, 94, 2393088, 10955841, 19607248, 27559040, 35734097, 42272466, 52627155, 61113408, 70069458, 77938899, 86705667, 94570003, 103493136, 111445184, 120143875, 128648835, 136513107, 142935698, 153519696, 162344082, 170475651, 178980547, 186844819, 193267282, 204375105, 212675666, 220807363, 227215045, 238093909, 246099024, 254183056, 263143621, 271255107, 280037077, 285541906, 296649857, 304950290, 1073743875, 313081923, 319489669, 330368533, 338373776, 346981569, 355418245, 361432581, 372311701, 380011728, 388443329, 397361157, 403375685, 414090241, 423046804, 1074286597, 430915653, 438731792, 448212692, 455426131, 463940609, 473203861, 479135240, 488980627, 498369557, 506932820, 512689736, 522534931, 529598025, 1074836422, 540312661, 548875796, 554632840, 1076943810, 564216337, 571672139, 581381249, 590644437, 597770961, 605095561, 1075389380, 613713105, 624504017, 631325329, 638649865, 647267473, 658058385, 666320917, 672335499, 680821777, 691612753, 697239240, 708264021, 1075929031, 714278411, 1075680264, 725167121, 731153489, 741818581, 747833035, 758451400, 1075168267, 1074149325, 766984341, 772867785, 783617096, 1077297161, 792027734, 800394376, 808805014, 817171464, 1073917898, 825582294, 833970710, 1076815820, 840647319, 849035799, 857424599, 1076308942, 865813079, 1076580303],
    [90, 76, 5, 89, 66, 2186304, 10347521, 18965504, 27354176, 35742848, 44131520, 52651009, 61039809, 69428289, 77683904, 86492816, 94594177, 102849664, 111658704, 118056515, 128435728, 136543299, 143222467, 152953921, 161709251, 168388099, 178119873, 186874883, 195633747, 202204243, 210331267, 220710480, 228818051, 1073747971, 235602644, 244147859, 252667525, 262626437, 270394497, 279519379, 286090771, 294610501, 304569413, 313073683, 319645395, 328164869, 338386514, 346628307, 354936470, 361719493, 371940882, 1075333125, 378479317, 388455621, 396879574, 403645077, 413884050, 422045206, 428941911, 439049938, 447211094, 456327896, 463952901, 473104920, 481263185, 487662295, 498040465, 504439447, 514817553, 523436632, 531359257, 539983569, 548602520, 556525273, 564222976, 571548183, 581690969, 587923988, 598468249, 604701332, 1074302920, 1074579399, 613360149, 621478484, 630137429, 1074080714, 1076454347, 1075945423, 1075704770, 1077023684, 1074948046, 1076279241, 1077330886, 1073950668, 1076844493],
    [110, 96, 8, 109, 86, 355328, 8709313, 19211457, 27345985, 35734657, 44123137, 52511937, 59172368, 67568656, 75852928, 86197971, 92726928, 101018816, 111486081, 119752339, 126281424, 134573120, 145040449, 153306643, 161958931, 168224336, 176620624, 186861139, 195513427, 201770641, 212149249, 220819094, 226952336, 235325009, 245845203, 252118224, 260490961, 1073746884, 271150678, 277267985, 288818193, 296316438, 305595601, 311486034, 321342611, 330761297, 336783060, 1074821062, 347041368, 355927185, 361948692, 1077183431, 371814102, 378741824, 387114580, 395265562, 405761688, 411362369, 420947543, 430927576, 437462144, 444916865, 456093208, 462627840, 471000724, 479282700, 488197721, 495248385, 504833687, 512837260, 521094746, 530140889, 537978386, 546776599, 554780364, 563695129, 571533010, 580331223, 588861081, 596845760, 605087378, 613369498, 622546064, 631055893, 638666316, 646923994, 656100368, 664741082, 1073792012, 673138319, 681266384, 689776213, 698304207, 706571457, 715072538, 1074076611, 723469839, 731737089, 740238426, 1075408845, 1076726730, 748635727, 756763728, 765273749, 1074385935, 1075194818, 773680193, 782051029, 1076514761, 790457473, 798958746, 1074705355, 1077075918, 1075783624, 1076323269],
    [110, 96, 13, 109, 86, 2204864, 10593280, 19113089, 27370560, 35759232, 44278849, 52553296, 61056193, 69444609, 75998865, 86107856, 94373458, 102743746, 109553233, 119662224, 127927826, 136297986, 143107793, 153216528, 161482450, 169852482, 176662033, 187286673, 195036818, 203669204, 212575748, 220841041, 1073746178, 229254805, 237616132, 246130372, 254395601, 262809109, 270515330, 279684676, 287949841, 296363605, 304725060, 313239172, 319931987, 1074806788, 329918165, 338279556, 344696343, 353616919, 361604696, 372115097, 380222660, 386901594, 395429395, 403547672, 413934616, 421772820, 428975707, 437372627, 445490840, 456001113, 464625302, 470525591, 479446167, 487433944, 497944089, 505659028, 512861723, 521651227, 531498713, 539213396, 546023127, 554943703, 564929752, 573677270, 579577431, 1073787848, 588498007, 598484056, 607231574, 613525211, 622314715, 632300616, 640785942, 647079579, 655869083, 665854984, 672114202, 681296922, 690758808, 697280154, 706462874, 1076948934, 716186824, 722446042, 731628762, 1076697034, 741352584, 748398283, 756532315, 1075136457, 765175307, 773571674, 781305491, 790341195, 1074113479, 1076487109, 1075980227, 798729867, 1076256716, 1075743755, 1074715597, 1075514318, 1074493391],
    [122, 108, 9, 121, 98, 2329601, 10552385, 18973760, 27362496, 35751040, 44139520, 50800144, 61049921, 68928066, 78087234, 84248274, 92743312, 102993089, 110747858, 120030722, 126191122, 134686416, 144936065, 152690706, 161973954, 168134226, 176524432, 185280209, 194633810, 203916930, 210077330, 218467344, 226960976, 1073747970, 236576914, 243633360, 252389009, 1075340227, 261865602, 268799056, 277554705, 287949525, 297119443, 302720593, 313115221, 322285203, 329319425, 338281109, 347450899, 354485377, 362528770, 372616787, 379651265, 388612629, 395152529, 404039319, 412860610, 420318289, 429467350, 439205891, 445875802, 454764249, 465153114, 1075884998, 472760387, 479430362, 488318617, 498707674, 506323483, 513115163, 520981713, 530130582, 539878043, 546669723, 554535953, 563815961, 1076939717, 573423747, 580093466, 588981849, 599370778, 1074342857, 606986843, 613778523, 622142999, 630959836, 1076453320, 640541403, 647333083, 655697495, 664514140, 674087107, 680756890, 689252055, 700034202, 705553108, 714704588, 723068502, 731622940, 1075679175, 739107348, 748258956, 756622870, 765177500, 772661908, 781944398, 790464015, 797827668, 807110350, 1074657226, 814867160, 823756364, 832407183, 1077293003, 840032856, 848922124, 857573071, 1076777996, 865198744, 874219022, 881975832, 890996366, 899515983, 1075218381, 1074184207, 1073942542, 1075013572],
    [86, 72, 9, 85, 62, 1432640, 10452993, 18638017, 26862656, 35382337, 43770881, 52028416, 60548225, 68805760, 77325505, 85581391, 94135425, 102727873, 110748864, 117827138, 127524495, 136078401, 144670849, 152690383, 161244161, 169836609, 177856015, 187197139, 193324738, 1073754112, 203974163, 211812050, 220751507, 228589138, 235643540, 245366290, 252420692, 262694483, 269608469, 278920850, 288587797, 294774357, 304340688, 313753685, 321406615, 328328917, 337894928, 347308245, 354960919, 361883285, 370531520, 380862613, 388515415, 397016593, 403415572, 413681367, 421781072, 428581588, 438558352, 445883030, 1076918212, 455736977, 462660118, 471194624, 479437398, 487971968, 495314434, 506068561, 1077183433, 1073802183, 512991958, 522845905, 1076437957, 530031308, 1075923910, 538419788, 545646210, 1074371523, 1075436546, 555196940, 563585676, 1075719180, 572105230, 1076778955, 580494030, 1075220426, 1074710477, 588882574, 1074205640, 597271118, 1075012622],
    [114, 100, 7, 113, 90, 484417, 10855617, 18859072, 27247744, 35636416, 44024832, 52544577, 60933249, 69321729, 75974221, 86352897, 94487745, 103271950, 109528781, 119907393, 128568912, 134727235, 143083021, 153461889, 162123472, 168281603, 176784908, 185026189, 1073752064, 193578577, 204066448, 1076391937, 210453648, 218728140, 229232144, 235619408, 243893836, 252177938, 260949638, 269173776, 277448332, 285732498, 296846927, 302728400, 312987342, 322012687, 328426577, 336064082, 347178639, 353723532, 361230034, 372344527, 378889292, 386516689, 396873294, 403555910, 414557265, 420701393, 1076930504, 428459665, 438816398, 446023369, 453494403, 462775308, 473277649, 478791185, 487583379, 495830534, 504587281, 515352068, 521137683, 529745620, 540518020, 546303699, 555075081, 563299988, 573940753, 579858003, 587686913, 599238212, 1076159431, 1075916741, 605242964, 616015556, 1076720644, 621659846, 632661137, 639460356, 1077248006, 647351829, 654821059, 663184577, 672629957, 1073860611, 680906453, 688350337, 697795589, 706072149, 714458697, 722822348, 731882496, 1074927554, 739626645, 748127301, 756900932, 764790409, 773825664, 781411473, 1075201033, 790602944, 798844036, 1074170826, 1074449418, 806569492, 815236229, 824157248, 832398532, 1074731979, 1075534859],
    [102, 88, 13, 101, 78, 1048704, 10766337, 18753536, 27142208, 35530880, 43919552, 52333132, 59769024, 69486785, 77499084, 84934720, 95054338, 102664716, 110100480, 117983950, 127830668, 136053453, 143149582, 1073750016, 1075865601, 153397970, 161219085, 168315470, 176827091, 186952338, 194773645, 201869966, 210381331, 220506706, 228328013, 237660866, 1076400067, 245672466, 253886657, 262826626, 271362769, 279052289, 287992386, 1074581506, 1074861058, 296528529, 304218177, 312756289, 321694289, 329533569, 338034899, 344861205, 352987795, 363637265, 371327105, 378686100, 386804437, 394930771, 405834447, 413532243, 420629204, 428747349, 439388815, 447086739, 454183444, 1075137476, 464554511, 472252435, 479349332, 487467669, 1074374597, 498109007, 506200277, 513042966, 521284296, 532056656, 539754581, 546597590, 554838536, 1076229062, 565611024, 573440198, 580413975, 588393032, 599165648, 606994438, 614222424, 621947528, 632720016, 1077025800, 640548934, 647776920, 657326214, 664300183, 1075731401, 673972245, 681077335, 1075479495, 1073923079, 690749589, 697854679, 706497240, 714369686, 723274264, 731146838, 1074212810, 1076852683],
    [118, 104, 11, 114, 91, 2240512, 8751105, 18352193, 26740865, 35129537, 43517953, 52037824, 60426304, 68814848, 77738176, 84248641, 93980800, 102903936, 109414593, 117836418, 128069696, 137070722, 145125059, 151390722, 162236418, 170406083, 1073750017, 179064466, 184945218, 195790914, 203960963, 210259537, 218499778, 229345474, 1075856386, 237515331, 243814033, 252020865, 260575763, 271339218, 280079055, 288109204, 296504850, 305244687, 313274900, 319311569, 327682630, 338799183, 1074042947, 344591061, 355218004, 363613778, 369625734, 380742287, 386533973, 397161172, 403197457, 411568646, 422807558, 428476949, 436736595, 447114243, 453511878, 464750790, 1075363846, 470291155, 480668803, 487459350, 498305158, 1073818565, 503974549, 514223171, 522727427, 529402518, 540248134, 546459223, 554177171, 563219144, 1076455364, 574064662, 582511816, 588122710, 599230614, 1076202439, 605179543, 613560856, 621939208, 632784982, 641231880, 647115480, 655493768, 664504848, 674786440, 680669784, 689048136, 698189888, 1074384904, 708340808, 714224280, 722340566, 1074927561, 733448406, 739397335, 748391120, 756174359, 765168208, 773606937, 782076032, 790384281, 798722704, 1075204043, 1074705357, 807161433, 815630528, 1077075918, 823938777, 1075787722, 832407552, 840927253, 1077374924, 849316053, 857704597, 866093141],
    [102, 88, 10, 101, 78, 2121728, 10512513, 18900993, 27289793, 35678273, 44197952, 52586624, 60558864, 69363712, 77619264, 86141120, 95087122, 102502032, 111173760, 120253138, 127667920, 136339648, 145803859, 152833616, 162160833, 170683094, 179358227, 184814806, 195715201, 204237398, 212912787, 218369110, 229130769, 1073746883, 237791894, 246467283, 251923606, 262824001, 271346198, 280545879, 285477910, 296239761, 1074815940, 305711639, 313003076, 321544193, 330877655, 338169028, 346571473, 1075872709, 356043415, 361369304, 371737169, 380299858, 386534936, 395468944, 405465746, 413666436, 420634640, 429058773, 437021321, 445255320, 454189264, 1073793990, 462744089, 470575817, 480775172, 487743568, 495872714, 504556053, 512518665, 520752728, 531644484, 537815690, 546499221, 554461769, 563490388, 1074337735, 573587460, 1075141641, 579758602, 588573401, 596905498, 607142084, 1075688386, 613313098, 622127705, 630599316, 640696452, 1077008394, 647653965, 655682201, 664153620, 1075460040, 672819853, 680716885, 689180250, 697985741, 705957594, 714762765, 722874068, 1077300237, 731123354, 1074694092, 1074194379, 1076309967, 1076849614],
    [118, 104, 6, 117, 94, 1960065, 10504193, 18892993, 27281473, 35670145, 44189760, 52578304, 60828304, 69355648, 77457473, 86132928, 92555859, 101067474, 109463762, 119663313, 126241298, 136587906, 144829009, 154038996, 162154708, 168184466, 176564370, 186509505, 195842581, 204098196, 210127442, 218507346, 228452353, 237924500, 246041172, 252332567, 262417090, 271566871, 1073754306, 279867924, 287983636, 294275799, 304359426, 313510103, 322204291, 327830103, 335947794, 347064407, 355758659, 361384599, 371468354, 380618903, 388780757, 395070149, 405407767, 414697669, 422335125, 428755482, 437012997, 447350999, 456640517, 464278101, 470567557, 480905303, 490195077, 1076912707, 495864474, 506753219, 512510533, 522201680, 532138053, 1075871749, 540307459, 548014231, 556657305, 562973274, 573468756, 579095059, 589310672, 598600409, 604916442, 615928534, 621038227, 631253520, 640543321, 649482774, 654592723, 665987219, 673311249, 683037334, 691152915, 699263513, 1073797062, 708473560, 716318931, 723643025, 733639256, 741484627, 1075123143, 747628544, 758805016, 765208666, 772794496, 1074883529, 783700566, 790374554, 797960384, 809136792, 815540442, 823126080, 832317466, 1076463565, 840427605, 1074121675, 848816277, 1074407374, 1076252620, 1074700232, 857204949, 865593365, 1075771332, 1077358543, 1076845514],
    [122, 108, 10, 114, 91, 557248, 10004609, 18393153, 26781697, 35170497, 43690176, 52078720, 60467200, 67665984, 77244480, 86559310, 92831872, 102673104, 111987333, 117877444, 126779983, 136227408, 145672388, 151431748, 160334543, 169781776, 179226692, 185500175, 194947728, 202050196, 210422418, 219054735, 229157397, 235448902, 246229013, 252365522, 260603904, 271100565, 279783573, 285919762, 294428752, 304654933, 313337941, 321440398, 327592580, 336371920, 346598101, 355281109, 363776132, 369926288, 378055302, 389220950, 394971730, 403480592, 414386710, 422365765, 428255748, 439255697, 1073746948, 445164230, 453708372, 464308933, 472810065, 478718470, 489884374, 497863173, 506364433, 1075082246, 1077182469, 1073800197, 512428564, 523159556, 531530449, 540215958, 546622104, 554740296, 563126924, 571943641, 580176600, 588294792, 596681420, 605497945, 613730904, 622232077, 1076168643, 1074094083, 630925978, 638896664, 647397965, 656091674, 665373390, 672180936, 681083009, 689646170, 698927630, 1075950537, 706118285, 714812122, 723184215, 731414593, 1077007303, 741935771, 748481235, 756580545, 767101659, 773646995, 781615821, 792267355, 798681623, 806398472, 1074929610, 815300609, 1075727298, 1074441218, 1076811784, 825821723, 832367187, 839950860, 1075515339, 1074751499, 848767513, 857532947, 865116748, 873933465, 882567831, 889916116, 899345111],
    [126, 112, 11, 123, 100, 2404416, 8652801, 18385089, 26904576, 35293312, 43550849, 51939393, 60459072, 68847808, 77901952, 84159116, 93882369, 103083534, 109349442, 117868558, 128233664, 134490636, 145010688, 151267916, 161909456, 168045260, 176599248, 187494033, 195463760, 203982993, 209979585, 218542160, 229437009, 237406736, 245925969, 251922561, 260485136, 271379985, 279480337, 288273043, 293865537, 304934609, 313034961, 319563840, 330216019, 336129621, 344729728, 355381971, 361295381, 369895424, 380547603, 386461333, 395061440, 403485266, 413567632, 420015829, 430713357, 437039634, 447490701, 453817042, 1073750979, 463793806, 470190222, 479210191, 487371410, 495880838, 506210893, 512791254, 1075858372, 522514126, 528910542, 537956950, 546318863, 554863303, 564457038, 570853454, 579899926, 588262031, 596806151, 605351640, 613321222, 621843094, 630205007, 638749319, 647294552, 655264326, 665594573, 671527056, 680692295, 1074301959, 691188311, 697838100, 1074585545, 1075654665, 705989194, 714403352, 722373318, 733131415, 739781204, 747932170, 1076978694, 755272386, 764840651, 773195927, 783594196, 1076206533, 1075442693, 789875338, 798289560, 805603970, 815172235, 825536532, 832055508, 840207050, 847546882, 857115211, 1077285898, 1075210250, 865470999, 875868244, 1076527106, 882280971, 890637015, 900903127, 1073923083, 907553428, 917811348, 1074205640, 1075014664, 926068759, 932579415],
    [130, 116, 10, 129, 106, 2156737, 10545217, 18933761, 27453568, 35711105, 44230720, 52749008, 61008064, 69396480, 77914768, 86461139, 92581442, 101114386, 111626835, 118001219, 126280338, 137161366, 143092245, 151555587, 159834834, 170846935, 179260121, 185002201, 193244802, 201777746, 212789847, 220678803, 227192474, 237298256, 243985029, 255150744, 260746842, 270852624, 277539525, 288705240, 294301210, 305053783, 311093765, 319769180, 327986181, 338608343, 344934940, 352882307, 361687710, 372294225, 377940569, 386878172, 397339287, 403737758, 414105751, 1073742339, 419883545, 428534341, 437209756, 445156547, 453962270, 464568977, 1073765381, 472705622, 478603929, 489637977, 496012318, 504293982, 515031190, 521202184, 1075614274, 531426006, 539969561, 546344030, 554625758, 565232337, 571533896, 581757462, 590301337, 596675806, 605088456, 615694358, 623831575, 631720467, 639142984, 647031432, 657375255, 1074843590, 1074603972, 1076185096, 664201866, 674581080, 681086088, 691191894, 697756362, 708135448, 714779850, 724746454, 1074370503, 731310666, 742083163, 748334154, 758170129, 764865034, 775637723, 781888522, 790282836, 1075173386, 800803355, 805612546, 815448724, 1075457993, 825969307, 830778562, 840614420, 847735381, 857246920, 865657373, 1076786125, 872901269, 881634501, 890823261, 1077065678, 898067157, 906800261, 915989149, 924355592, 932889300, 1077331915, 941272202, 949543645, 957131845, 965390042, 1074209740, 1076063183],
    [118, 104, 8, 117, 94, 2386113, 10537153, 18925569, 27314241, 35702913, 44222464, 52611200, 60852944, 69388352, 77883393, 86165696, 94696081, 103205586, 111184464, 117754451, 128215169, 136639185, 145148498, 153127440, 159828564, 170158145, 178582097, 187353621, 195480210, 203459216, 210160148, 221145617, 228913169, 237685461, 245811730, 252479572, 260360851, 271476945, 279761109, 288672386, 296396930, 302303763, 313419857, 321703957, 330615362, 338339906, 346974353, 353169944, 361548356, 372558338, 380282882, 386558144, 395113112, 403098260, 411863188, 420112384, 428929234, 437045892, 448056002, 455780546, 462055552, 470610648, 1073754114, 478595796, 487360724, 495609920, 504426642, 512674329, 520914964, 531908754, 537719384, 545573587, 554346579, 565463250, 571929114, 581618261, 587901075, 599017554, 1076910021, 606916693, 615172757, 621726425, 629983940, 638757081, 649349138, 1075095491, 657248405, 663538180, 672057945, 680699929, 688941783, 1076151300, 1074080711, 697758426, 705865817, 714500630, 722924186, 730778265, 739420313, 747661847, 1076446152, 756470299, 764061907, 772827799, 781636251, 789227539, 798386838, 806802011, 815164118, 823587418, 1073845195, 831941206, 1074917322, 839970898, 848325207, 1076759497, 857133787, 865136658, 1074417606, 1074700236, 1075764174, 1075525581, 1077371855],
    [106, 92, 5, 105, 82, 2468032, 10559681, 18950272, 27338944, 35727360, 44116032, 52799552, 61153872, 69421713, 78064147, 86607873, 94445697, 103507987, 111618707, 120162433, 128262672, 137062547, 144777217, 153716929, 161696273, 170339027, 178628608, 186720321, 195782867, 201796291, 212437057, 220537552, 1073746882, 228805329, 235350531, 245836371, 254126208, 262480528, 271280211, 277293699, 288327696, 294584916, 304302673, 310848067, 322013781, 328270418, 1074808835, 338659408, 345047762, 355436688, 361824914, 370109143, 380602576, 386990610, 395258457, 404179033, 414288597, 420414164, 1074305990, 428812825, 437733401, 447842837, 454370008, 465127640, 473008789, 479535640, 487533273, 496453849, 506833558, 512688660, 523848344, 531999446, 538255960, 546253465, 1075377092, 555174041, 565684230, 571809944, 582568024, 590850118, 596574868, 607733784, 616016006, 1076964296, 622684890, 632662550, 638544535, 649570502, 655321623, 666217046, 673147483, 681247388, 689793690, 1076453327, 1075687374, 698024668, 706702043, 714801756, 722430551, 1076742090, 1074149323, 731578908, 740256283, 1077307337, 748513882, 1076265927, 1073931212, 757033627, 765291034, 1076039629, 1074747333],
    [118, 104, 3, 117, 94, 305216, 10162305, 18941953, 27330625, 35719361, 44107905, 52627584, 61016064, 69404864, 76188304, 86061776, 94570560, 100993745, 111227408, 119580881, 126159441, 135991297, 144746577, 151482068, 159713809, 170592468, 178335888, 186689553, 195889794, 201656977, 212248706, 219877569, 229444162, 235368020, 246089812, 253833808, 262580290, 271387330, 279357634, 286986305, 296552962, 304967317, 312911874, 321729234, 1073743874, 328010436, 336031380, 346753172, 353011792, 363933892, 369953348, 380464725, 388016273, 397488196, 1074283459, 403507844, 411528724, 422250516, 428509392, 439431300, 445450756, 455962133, 462063632, 472985604, 1073778692, 481128149, 487368833, 497889874, 506678855, 512788562, 523055762, 531844615, 539832850, 546343058, 555175446, 563286739, 571254785, 582176455, 588452371, 596420673, 605507286, 613757527, 621840594, 630917835, 640896647, 1074846727, 647172691, 655141057, 664472139, 672616086, 680866519, 688171200, 698288781, 1075655625, 708398221, 714281619, 721725568, 1076981702, 731843085, 741952525, 747975191, 755279872, 765397581, 775507021, 781529751, 789612562, 798952141, 809061581, 1076728845, 1075181516, 1077291973, 815222358, 824135192, 1076517838, 1075487688, 832523864, 840912600, 1076029386, 849021451, 857689752, 865798795, 1076298763, 1074221007],
    [130, 116, 10, 129, 106, 2189313, 10709056, 19097792, 27486208, 35743937, 44263552, 52521025, 60909697, 69689872, 78078608, 86978193, 94988433, 103270994, 112027730, 120021584, 126168787, 137325204, 145187536, 153554453, 162490900, 170737684, 178874897, 187109013, 196045524, 204292308, 1073742787, 212806673, 221211220, 229458004, 237595345, 245829333, 254921432, 263012500, 271388374, 277441178, 288475672, 296829655, 302738054, 313092689, 321326677, 327772890, 338807384, 344678554, 353069766, 364210759, 372190289, 378137160, 386754632, 397500487, 403401222, 414542343, 422383190, 431082136, 439443463, 445344326, 456485575, 464465105, 1073765382, 472369874, 481126610, 489775303, 496200394, 1075614658, 506817159, 514657942, 521005643, 531718279, 538143306, 1074852871, 548212246, 556788379, 565264983, 571697802, 1077217225, 579153555, 588114443, 597125852, 607207959, 613640714, 621096531, 1074087946, 630442057, 640762519, 646262291, 655223499, 664234652, 671834330, 680996377, 688482906, 697166475, 707619474, 713777242, 1074369547, 722939481, 730425882, 740804754, 748120668, 755720218, 764882585, 1075180492, 774359570, 781675036, 791504914, 798572572, 807218781, 816835163, 823738524, 832384541, 842000923, 848904284, 857550557, 867166939, 873294344, 1077030853, 882458844, 891104925, 1076783053, 898230984, 906848456, 915877593, 923396744, 932014216, 1076268040, 940820489, 1074717646, 948561928, 1076042692, 957597833, 965986505, 1075538895],
    [106, 92, 9, 105, 82, 2445313, 10938433, 19212816, 27847249, 35999809, 42289810, 52767440, 61567490, 69790225, 75975315, 84224147, 94824577, 103108801, 109529683, 117778515, 128676482, 136767489, 145443349, 151472851, 159721683, 170619458, 179365909, 187386517, 1073752578, 193415699, 201664531, 212920469, 220549249, 227101187, 235481816, 246116546, 254339729, 262884053, 269036120, 280029397, 286085841, 296962649, 302590616, 311251089, 321448145, 330517145, 338381397, 344533528, 355526741, 361582673, 372460057, 377834066, 388311632, 395137041, 405203137, 414403289, 419777234, 430254736, 437307392, 447959040, 453331474, 464595546, 470861888, 481513536, 489761306, 496027840, 506679488, 1076385733, 514927322, 521193600, 531845248, 540093082, 546656852, 557247003, 563685465, 571822740, 582412955, 588851417, 596988436, 607578715, 1075086281, 614279378, 622154452, 632744667, 639445010, 647713366, 656198167, 664348825, 672879254, 681364119, 1073803204, 689514521, 698045142, 706530007, 714942546, 1076705227, 723210774, 731695703, 1077235658, 1074633676, 1075438541, 740108434, 747194947, 1075983304, 755583619, 763972291, 1077036998, 1074171907, 1074973639, 1074470863, 1075800014],
    [106, 92, 1, 105, 82, 1933312, 10733760, 18745537, 27371648, 35760128, 44148800, 52537536, 61057089, 69445825, 77834369, 85819520, 94619776, 102894160, 111388673, 120171218, 128174144, 136938001, 144967890, 153725522, 161728512, 170492625, 178522194, 187280018, 195930644, 204065346, 212435537, 220465298, 229222930, 237873812, 245203008, 252299925, 262408210, 271428308, 279055056, 285854229, 296321681, 303923392, 312609296, 319408725, 330148436, 337775248, 344574677, 354656790, 363448962, 371067009, 379822742, 1073746498, 389261847, 397002754, 404621377, 413377238, 422168770, 429787137, 438542934, 447982167, 456771796, 464259095, 473148055, 481937556, 489424983, 498313943, 507103252, 514590935, 1074807749, 523880532, 531368087, 1073785796, 540027416, 548530835, 556804824, 565307987, 1076416455, 1074601928, 573581912, 582085139, 1075673030, 590359192, 598862547, 605538905, 613821018, 622438925, 630704665, 638986970, 647998030, 655870681, 664152730, 672647833, 680929818, 1077254092, 689547981, 697690843, 706325069, 714467867, 723495566, 731245211, 739879565, 748022363, 1075179467, 1076762637, 1075475401, 757050062, 1077061578, 765438478, 1076283406, 1074471875, 1076053967],
    [110, 96, 13, 109, 86, 1961089, 8761537, 19081409, 27363392, 35752064, 44140736, 52529152, 61049025, 69437441, 77826113, 86618640, 94628880, 102967361, 111380609, 120304337, 128133121, 136178881, 144961168, 153858641, 161687681, 168233152, 179024529, 186510337, 195292752, 201787392, 212578833, 220836560, 228846800, 235341952, 246001744, 252119104, 262007873, 269420560, 279556240, 288091328, 1073750978, 296858322, 302975056, 313256960, 319523544, 330238168, 338801170, 346811520, 353077784, 363792408, 372355666, 380365888, 1075866564, 1076403141, 386894534, 395020888, 403802759, 414124120, 422687378, 428601044, 437225990, 445352600, 454134279, 464455832, 471175830, 478932628, 487557766, 496341590, 504098324, 513215063, 521243207, 529896150, 537652820, 546646613, 554666566, 563186375, 571838998, 580201109, 1075364870, 1074074631, 589009561, 596978197, 605146778, 614175321, 622660115, 630312666, 637907009, 647826003, 655871515, 663685328, 672895513, 681037403, 689672921, 698157779, 706203291, 713404545, 722930199, 730975770, 738570241, 748489363, 1075137475, 756535003, 764873431, 1074368456, 772918874, 781650583, 1074653129, 1076240330, 1075737547, 789916373, 797902992, 1077056460, 1074982862, 1076822991, 1073969101],
    [106, 92, 13, 105, 82, 1697920, 10086592, 18475072, 26863616, 35383361, 43772097, 53063375, 60549249, 68937729, 78146257, 86617679, 94923409, 103394831, 111700561, 120172175, 128477713, 1073754112, 137203346, 143157843, 153207380, 161867860, 170757714, 176548565, 187721941, 195543684, 201844868, 212700690, 218491413, 229664789, 237486596, 243787780, 254643922, 260434517, 1076908994, 271607893, 279429700, 285730884, 297111255, 302377621, 313550997, 321372868, 327674052, 339054167, 1074829316, 345000664, 354804310, 363195028, 372608535, 378554904, 388087956, 396749332, 406302352, 412109400, 421642964, 430303444, 439717527, 446808084, 454314716, 465022672, 471091868, 481026714, 490188304, 1075365830, 496257564, 505799190, 515354192, 521423452, 531358298, 538291867, 546327192, 556524058, 563457627, 570976979, 581296790, 588623387, 1074073543, 597453534, 606462678, 613789403, 622619294, 632021722, 639610397, 1074616264, 647784990, 655616587, 664637145, 1075151811, 672950878, 680782347, 689802777, 696805907, 705948363, 715107997, 721971859, 731114123, 740273885, 1073863691, 748523097, 1075710924, 1074424773, 757050973, 765300377, 1076536266, 1076029390, 1076309965, 1076852681],
    [110, 96, 11, 109, 86, 2451585, 10848449, 18860224, 27248640, 35637376, 44025920, 52914828, 61179969, 67488398, 78080588, 86345857, 92654158, 103246540, 111511553, 119796239, 126339792, 134719696, 145189388, 1073752064, 151505488, 1076391937, 159885392, 171010765, 176673489, 184928974, 193702030, 204565069, 210227857, 218483214, 227256334, 238119565, 244033742, 254896653, 262927059, 269199438, 279275585, 288092691, 296995476, 304441537, 311265428, 1076929474, 321647187, 329607169, 336702101, 344836245, 1075893187, 355201683, 362105024, 370256469, 378390613, 388231759, 397658644, 404047936, 412199637, 420333781, 430174927, 437602432, 445483028, 453888533, 464767700, 471156736, 479037652, 487574085, 498322004, 504482454, 513370706, 520980564, 529517061, 539226767, 546425558, 555313682, 563456150, 571460293, 579990167, 588368470, 597379736, 605399126, 613403269, 621267472, 1074856965, 630811346, 638035984, 647088662, 656099864, 664119318, 671599248, 681142930, 688367760, 697944583, 1074100166, 706431704, 714188821, 721932881, 731499143, 739986008, 748005590, 755487249, 765053639, 772928087, 781830727, 1077248007, 789705239, 1073862601, 798094039, 1075193800, 1076251594, 1074433034, 1074715595, 1075518475, 1075802052],
    [118, 104, 1, 117, 94, 2378752, 10660864, 18744908, 27544704, 35826880, 43910668, 52604032, 61361869, 69338638, 77769792, 86527501, 94504590, 103304845, 111979649, 1073750016, 1075865601, 119670478, 128470605, 137145537, 144836174, 151268881, 161762496, 170699841, 178128524, 184823505, 195316800, 204254209, 211683020, 218377873, 229805762, 238054540, 246023824, 254971522, 263220300, 269102610, 279709395, 286011011, 296914434, 305163276, 1076405378, 313536084, 319696597, 330040915, 338857026, 347106508, 355479252, 361639445, 371984019, 378162197, 387092111, 395194005, 405538323, 411840067, 419704401, 428494037, 439914181, 445263442, 455738896, 462433926, 470953494, 481857029, 487476305, 498085524, 503983826, 514851988, 521285206, 529542726, 538086991, 546327638, 554446339, 562966101, 573572308, 579612355, 588262918, 597183698, 607686277, 613560022, 1076156419, 623914516, 630468103, 640680980, 647114390, 655903762, 663916239, 671755922, 682231376, 689188551, 696929365, 708349509, 1075392517, 714354247, 724567124, 731024911, 739134673, 747908743, 757728976, 765242967, 772689041, 1076972551, 781201094, 790408919, 797854737, 1074634692, 1075693574, 807186071, 815287442, 823963159, 832064594, 1074411465, 839928982, 848317462, 1077302216, 1074959368, 856706262, 1075245002, 864701589, 1076822987, 1073955851],
    [106, 92, 10, 105, 82, 2469057, 9964609, 18353281, 26741953, 35130369, 43650176, 52038848, 60427328, 69577729, 77204480, 86395473, 94244560, 102764175, 111520897, 119949841, 127798800, 136318543, 145075265, 153499155, 161893009, 170626706, 1073750017, 178665043, 187058897, 195792594, 203830995, 210135183, 220958226, 229389908, 235300943, 245370383, 254512722, 262551187, 268855311, 278793872, 285839061, 296498708, 305424402, 312348240, 320868047, 327683779, 336170645, 346830548, 352741583, 361336405, 371996308, 380922002, 386502165, 397416022, 405948432, 412200148, 422581782, 431253586, 437365844, 447747734, 456419538, 462531732, 1075863490, 472913622, 481446032, 487697428, 1075621828, 498223312, 504598168, 515000400, 521505807, 1076681671, 1075385286, 529413658, 538593365, 545787459, 554929688, 1074876361, 563759253, 570953347, 580095704, 1074629573, 588925141, 596119043, 605392015, 613299802, 1074385923, 622479381, 630951639, 1075185610, 638465754, 647908057, 656117399, 1074152392, 664147547, 673073689, 681283159, 688797338, 698239641, 706448919, 714479323, 1073918924, 723405401, 731221199, 1077077963, 1076312013, 739644955, 747998287, 756422299, 764644952, 1077373902],
    [106, 92, 11, 105, 82, 1837120, 10406976, 17056896, 27290817, 35679297, 44067969, 52456449, 60738688, 67388608, 77334720, 85723136, 92816913, 103075472, 111070208, 117720128, 127666304, 136710868, 145411284, 151274496, 161876500, 170576916, 176703057, 1073755074, 184970883, 195743380, 201869009, 212347011, 218656406, 226913795, 237686356, 245901315, 253772950, 260468291, 270453952, 279455811, 287458884, 294022851, 304621763, 312790608, 321013380, 1076905987, 327708374, 338036884, 346344976, 354436310, 361262614, 371591252, 379899600, 387990550, 395053714, 404899524, 414239746, 419982934, 428608210, 438322262, 447794370, 1074309188, 453773842, 463619076, 472960066, 478965318, 487328338, 495470225, 506514562, 512519878, 521072213, 531630209, 537945232, 546074246, 556795969, 563110992, 571666067, 580021833, 588017158, 597061131, 607127553, 613442576, 621997587, 1076419590, 630615627, 638512661, 649070785, 655385808, 663907977, 672558795, 680455829, 689580759, 697724555, 706357783, 714272467, 1075648523, 723135127, 731049555, 739176149, 748300887, 756182729, 1075402695, 764571145, 1075153929, 1074643916, 1073874888, 1074160590, 1076007877, 1074984909, 1077356495, 1076326346],
    [102, 88, 11, 101, 78, 1977473, 10505409, 18893825, 27282561, 35671105, 44190720, 52579520, 61232848, 69356608, 77474881, 86133888, 94787088, 103296064, 109432401, 119953040, 128462016, 134598161, 145118800, 153627776, 159764113, 170554513, 178138113, 187297492, 195720209, 203959296, 212463252, 220886097, 228469953, 237628948, 244086418, 254151888, 263179926, 269252306, 279317584, 288345622, 296636056, 304772817, 312872080, 1073742787, 321515092, 330190424, 338711640, 346426384, 355454550, 363744792, 372266136, 378277525, 389009110, 397299416, 405820632, 411831893, 422702803, 1073767364, 430986264, 436997653, 447868435, 454448859, 462294033, 473034387, 478967378, 487460049, 498200147, 504911447, 512625745, 520473809, 529298962, 537791633, 546565852, 555112091, 562826965, 1075877830, 571862553, 580408855, 589049434, 596897308, 605574871, 613813913, 622063260, 630609499, 639381210, 1075106763, 1074859973, 647229020, 655775259, 664546842, 1074623436, 672525913, 681072279, 689310809, 1076993994, 697691865, 706490010, 1075702722, 714468505, 1076496329, 722865177, 1074154445, 731253977, 1074440135, 1076288463, 1075525576, 1077374926],
    [126, 112, 3, 125, 102, 2401344, 10685504, 18918465, 27307137, 35695809, 44084225, 52481680, 61017216, 69510336, 77901522, 86437523, 94676096, 102960320, 111455890, 119991827, 128230400, 136514560, 145157715, 153423572, 162039505, 170323667, 178589332, 187205137, 1073750978, 193375765, 203476688, 212143700, 220759697, 227061270, 237030928, 245698068, 252347585, 262196816, 269160087, 279479889, 285650645, 294178005, 302714583, 311067713, 1075856325, 319204949, 327732309, 338628313, 344622209, 352759445, 361286805, 372182681, 378176513, 386838170, 394841109, 406103575, 414256282, 1073779651, 421834322, 431148226, 439291481, 448046231, 453553814, 462597768, 471117449, 481479682, 488943122, 498011673, 506766551, 1074850758, 512667226, 523422850, 531932759, 540085338, 1076438980, 546483720, 1076196295, 555134493, 565365826, 571387418, 582518360, 590416922, 596815432, 605335113, 613338141, 621719258, 632850072, 640748762, 647147208, 655797981, 663669981, 671812631, 683181784, 1076993032, 689352349, 697224349, 705998537, 713755735, 725124632, 730377942, 739691734, 748359387, 758555730, 764849757, 772721757, 781495817, 790302299, 800498898, 805875286, 1075694538, 1074403337, 815189078, 825664530, 832507612, 1075464139, 840354838, 849022491, 859219090, 865520790, 874450588, 882804318, 891227676, 899581470, 1074182095, 908004956, 916358814, 924520091, 1077336014, 933136094, 1075261388, 1076842445],
    [142, 128, 7, 141, 118, 2370561, 10521728, 18910400, 27298816, 35687488, 44207169, 52595713, 60984449, 69479617, 77761729, 86423057, 94931985, 103033985, 111589073, 120098001, 128199745, 136754833, 145935059, 153652369, 159812819, 170536528, 178697809, 185125396, 195595345, 202017812, 212479696, 220902420, 227076695, 235703383, 246320790, 252350100, 262811280, 269011092, 279622804, 286035607, 296652502, 302681684, 313142800, 321565780, 327739543, 338595414, 344624852, 352718488, 361664026, 369674324, 380286164, 388926998, 394694227, 405679130, 411995866, 422622422, 431147091, 436637203, 447622362, 456176790, 464701459, 470585047, 478580371, 486936152, 495881818, 506508374, 515033235, 523119706, 1073748931, 531674134, 537454807, 546082327, 554044952, 563254869, 571009047, 582389339, 588549640, 595988184, 604933786, 613987993, 621332692, 630623772, 638881416, 648948890, 655529621, 663930888, 672567004, 680529618, 689485401, 697485896, 708218395, 714378312, 722603099, 731428569, 739428488, 750161627, 756715212, 764546267, 1075344327, 773232221, 781765212, 790006876, 798789278, 1076926409, 806358546, 815175197, 823315144, 834047643, 840207560, 848432155, 1075101704, 856856277, 866044108, 873893532, 882544140, 890375323, 898799125, 907986956, 915410514, 1073810379, 1074353098, 1074892740, 924227293, 932759772, 940576402, 949393053, 958327518, 966560990, 974698009, 983493150, 991726622, 1074653122, 1076241359, 1076000718, 1000270430, 1008503902, 1016645788, 1025150540, 1033816140, 1041927820, 1077314572, 1050200092, 1058982028, 1074196429, 1067378846, 1076833222, 1076584389],
    [122, 108, 11, 118, 95, 2409664, 10258497, 18410561, 26799297, 35187713, 43576449, 52096064, 60484608, 68873408, 77907072, 86149644, 94039168, 102977101, 111210063, 119850048, 128092812, 136531661, 144764559, 153667216, 161647308, 170085901, 178974354, 186958848, 194808001, 203640461, 211873295, 218678931, 228362241, 235630158, 246345429, 252233235, 261916801, 268782805, 279899669, 288419542, 294055618, 304253516, 311354900, 319114261, 330231445, 335998466, 346605264, 353062487, 363785813, 369553026, 380159504, 386617047, 396422863, 405325392, 411782807, 422480580, 428534980, 439021138, 445050434, 453560019, 1073754114, 462114327, 472812100, 478866500, 489352722, 498134614, 504685654, 512052309, 523143812, 529198212, 539684562, 546628822, 553995413, 565086724, 571141124, 582020758, 588179092, 1076908036, 596864018, 604941017, 615575062, 1074829253, 622126230, 630542040, 638495257, 647284433, 1075109827, 655707736, 663661209, 672457750, 680873624, 688826969, 697363974, 706004561, 714697871, 722774618, 730918598, 739174100, 748252239, 756328986, 764472902, 773113489, 780889806, 789883546, 798027398, 805881427, 1075655686, 814967890, 823438042, 831448660, 840527055, 848610833, 1077232583, 1073849351, 857304079, 865422872, 1076222921, 873688210, 1075449802, 1074685962, 1076529099, 1074187208, 1074470923, 1076063240, 881553038, 890465490, 898330126],
    [138, 124, 12, 130, 107, 2290752, 10783937, 18402432, 26790912, 35179712, 43568192, 52087873, 60476545, 69365324, 77253825, 86176768, 94669953, 102419457, 111308300, 119731392, 128364239, 136498705, 144862860, 153285760, 162049041, 170315411, 178441873, 184962195, 195612244, 203992209, 212530241, 220646931, 228773457, 235293715, 245944020, 254323793, 262861825, 270978643, 279105233, 285625427, 296275476, 302435842, 313044177, 321582273, 329699027, 335957203, 346748033, 354856527, 362966732, 369808919, 380022287, 389181005, 395105872, 405188239, 414346765, 420410969, 431263382, 436915780, 447901389, 453965529, 463768641, 470470148, 478596674, 489844365, 495908377, 505711617, 1073745859, 512413316, 522768020, 529288792, 537851545, 548703830, 554356420, 562482882, 571231960, 582145670, 590646806, 1074552836, 596037250, 604786328, 615700038, 624201430, 1075881925, 1076155394, 1075128322, 629952024, 640865798, 647540430, 655649940, 666031814, 675064980, 1076451334, 1075426310, 680578631, 689597457, 698021589, 708611730, 714264201, 723151953, 731575829, 739814926, 747949770, 756207113, 764701780, 772462295, 784109138, 789892682, 798019079, 806644756, 814536400, 826052114, 831573639, 840199380, 847959639, 859614420, 865390090, 1077267400, 873647817, 882535633, 889902743, 901557268, 907202121, 916090001, 924513877, 935111764, 940887690, 1074401289, 1074949129, 949014215, 1076790282, 958287386, 966456981, 974696014, 1074184199, 1073946571, 1075802123, 983453274, 990697104, 999861902, 1008619162, 1015862800, 1027378898, 1033785050],
    [122, 108, 10, 121, 98, 2599936, 10953921, 18951361, 27339905, 35728449, 44116993, 52896769, 61312592, 69674049, 78089936, 86451329, 94867088, 103108162, 111879232, 120032784, 128273922, 137045184, 145862339, 153439874, 159854290, 170599424, 179416579, 186994370, 193408658, 201928211, 212542592, 221359683, 1073750018, 229592660, 235613268, 243740242, 252259987, 263302787, 271394000, 1075855363, 277433554, 285683218, 296201280, 304948304, 310987922, 319630933, 328150661, 336146131, 346533056, 355279888, 361319442, 369962709, 378482373, 387133142, 397905489, 405611664, 411913430, 420818647, 428420691, 439848593, 448333446, 454118615, 462237205, 471150231, 480750720, 490406979, 496192533, 504573526, 515346129, 523830854, 531582676, 537603284, 546123413, 555036247, 565677585, 574292995, 581914260, 587934868, 596979223, 605236886, 616139987, 624494278, 1073777607, 632245780, 638266388, 647179798, 658082835, 666437126, 1074321352, 1075122182, 671960214, 683248787, 691733699, 697388183, 708414547, 716899459, 722685077, 730803717, 740230745, 748531288, 756108311, 764358213, 773785305, 782085656, 1074878469, 1075423177, 789400598, 1076223940, 798951065, 807374554, 814959701, 824116761, 832540250, 839732310, 849317530, 856247378, 866094618, 873680085, 882749080, 1075711950, 890326103, 899526360, 1074689999, 1077315531, 1074197453, 1077096396, 1076849610],
    [110, 96, 10, 109, 86, 2526336, 10826817, 18943041, 27331713, 35720385, 44108801, 52857856, 61158529, 69552723, 78023744, 86324225, 94980756, 103189696, 111490241, 120146452, 128792278, 137006610, 145312468, 154220245, 162573968, 170478164, 176754370, 187512470, 196128336, 204556501, 212678230, 220892882, 229722645, 238105621, 246058578, 254888533, 263009814, 271224466, 277957209, 288437909, 296791568, 1073744835, 305219733, 311365320, 321991765, 330346192, 337988307, 345050779, 356455635, 361803281, 372721819, 378605275, 386862600, 398398547, 403746449, 1074295748, 414672904, 420417160, 431953427, 440044564, 448227464, 454102619, 462360136, 471414359, 479243857, 1076920328, 490170440, 496045595, 504968919, 515542228, 1073798086, 523725000, 532616851, 540707988, 1075384266, 547702931, 1074619333, 554241666, 565917404, 571518673, 1075945417, 582436955, 587796034, 599471772, 607816788, 614811667, 621350402, 633026140, 639536794, 1075696642, 649545947, 658191900, 664702554, 674711579, 681381388, 689518103, 698256922, 1075188679, 705776153, 714935884, 723072663, 731811546, 739330777, 748490444, 756107929, 765267596, 1074938892, 773802712, 1074182093, 782191192, 1077342158, 790579864, 1076832203, 798968344, 1076325327],
    [118, 104, 9, 117, 94, 2450561, 10480769, 18967552, 27356224, 35744896, 44133568, 52423681, 61433552, 69201089, 78210640, 85978177, 94987792, 103113729, 111668432, 119891009, 128446096, 134810194, 143224339, 153611280, 162096272, 168364562, 176778835, 187000001, 195554384, 202058452, 212855827, 218696402, 227372738, 237987414, 244280406, 252276435, 263187667, 269683349, 277704194, 286355096, 296741971, 305203352, 313476677, 319909464, 327806609, 338757720, 347031237, 353464024, 361328275, 372239507, 380700888, 388974213, 395406872, 403304017, 414255128, 422528517, 428830358, 1073753093, 436858385, 445852247, 456090774, 462253634, 470773270, 478801617, 487131794, 498033686, 504196738, 1076650947, 512716502, 1075873794, 521268825, 529738455, 539976918, 546434585, 554904215, 563441163, 572081882, 580349516, 588458519, 1074326471, 596766425, 605775579, 613904076, 622004949, 630550219, 639329819, 647458316, 655043220, 663875225, 672884315, 681012876, 688597588, 1076435980, 697659019, 706438811, 713763348, 723373724, 731606670, 739853850, 747833941, 756928028, 765161166, 773794461, 782093916, 790326798, 798960157, 807259868, 815492686, 823739994, 1075664838, 1075157006, 831719957, 840265291, 1075430340, 1073887178, 1077300235, 849291997, 1074705357, 1077072841, 857680477, 865683098, 1074989000, 1074227151],
    [102, 88, 7, 101, 78, 357568, 10693824, 18803905, 27348161, 35736705, 44125249, 52513793, 59332112, 69397520, 77802624, 84498064, 94563472, 102968320, 109663824, 119729232, 126291666, 134829776, 144895184, 151457298, 159740992, 168234578, 178187329, 1073753026, 187266755, 193400466, 203353089, 210072576, 220408896, 228519041, 237719187, 243748500, 254506132, 263384130, 269291089, 279541315, 288550082, 294727381, 302468692, 313226324, 322104322, 328011409, 336023060, 346650243, 355658882, 361836053, 371946516, 378613397, 386722961, 395267671, 405370371, 412167765, 420277329, 1076387843, 1075875780, 428297940, 1074587592, 439055572, 445443601, 453840593, 462376599, 473396375, 479005713, 487386321, 495931095, 506950743, 512543762, 523439251, 531320531, 1076167622, 537873943, 1073835975, 548893719, 554486994, 565382355, 573263443, 582448343, 588041298, 598936659, 606817811, 612725888, 621595794, 632491027, 639071425, 647573016, 655848513, 664350296, 672625665, 681127640, 1076729803, 689403009, 697904792, 706686550, 715075222, 1075170252, 723463894, 1074402253, 731852310, 1074939850, 1074181070, 1077074889, 1075525583, 1077370821],
    [126, 112, 1, 125, 102, 2108609, 10595520, 18984064, 27372544, 35761216, 44280897, 52669441, 60943952, 69446785, 77605889, 86224065, 92646929, 102886928, 111553553, 120303187, 128052880, 134590033, 145108049, 153716436, 162376916, 170634963, 178384592, 184921809, 195439825, 204048020, 212708500, 220966547, 229362899, 235253393, 245771409, 254379540, 263040020, 268938901, 279694483, 288075283, 295709825, 304711252, 313371732, 319270613, 330026003, 337652801, 346924695, 352824853, 363580499, 371461650, 380610198, 386510360, 394767957, 405917378, 413797587, 422553110, 428453528, 1073750466, 436973252, 447859778, 455740435, 464758489, 470658778, 478916228, 489802882, 497683603, 503950936, 514696919, 520990298, 529247812, 540134402, 547622482, 554282712, 565028439, 571321882, 579579396, 587845211, 596618331, 606342866, 615753369, 1075861508, 621784731, 629787803, 640289875, 649307673, 1075353541, 655208090, 666094609, 674106456, 682468887, 1075114947, 688893659, 696896731, 707006098, 716416601, 722447899, 730450971, 741215448, 749709014, 758369425, 766381208, 774874710, 1076956103, 783535185, 791546904, 1074359238, 1076465608, 800312529, 807022236, 815385626, 823799388, 832293973, 840576540, 849071253, 857353948, 1074651083, 865848341, 874105946, 882869981, 890883226, 899647133, 1075722189, 907791573, 916424221, 1077309391, 924437722, 933201501, 1076794314, 1074971593, 1073948622, 1076316108],
    [114, 100, 13, 112, 89, 2436097, 10982529, 18975808, 27364480, 35752960, 44141760, 53030544, 61314113, 69200403, 77958163, 86584848, 94868481, 103362256, 111645889, 119794390, 128527952, 136951313, 144960150, 153859604, 161819841, 170773079, 178894545, 186985537, 1073750978, 195554008, 204060305, 212151425, 218599065, 229108248, 237702738, 246003281, 254274136, 262911700, 271257298, 277581530, 287828632, 297086105, 304854612, 310873625, 1075862467, 321228371, 327913114, 337635411, 346797716, 355143186, 363171539, 369856026, 379578579, 389360665, 397391381, 403410522, 414042647, 422252178, 430945941, 436702937, 1075360708, 445615816, 455985815, 464858329, 472888917, 478645849, 1076941765, 487558728, 497389203, 505407635, 515189849, 520983760, 529632905, 537890440, 548260567, 554538000, 563285723, 1074859974, 571575817, 579833352, 591251482, 596481168, 605228571, 613519049, 1074610184, 624806106, 630035536, 638783067, 647073353, 1073843143, 655855242, 1074381833, 666749082, 674215637, 680726171, 689409610, 700303450, 706186762, 715385430, 723201566, 731352778, 740551190, 748367518, 1074140170, 756795933, 765144798, 773704412, 781921886, 790350557, 1075210189, 798870108, 1076276171, 807127709, 815647260, 1076551628, 824035996, 1075785679, 1076852686, 832293469],
    [98, 84, 1, 97, 74, 2343936, 10898561, 18476224, 26864768, 35253248, 43641920, 52161729, 60550209, 68938881, 77973199, 86395969, 94104577, 103254736, 111527439, 119950529, 128420496, 136693327, 145116161, 153586192, 162156114, 170247823, 176549442, 187140688, 1073754112, 195710482, 203670656, 210103810, 218737364, 229265042, 237225152, 243658370, 252291732, 262819538, 270779456, 277457428, 288255572, 296732309, 302622804, 313420948, 321898005, 330198228, 338675285, 344959639, 355888856, 363841237, 370125335, 381054552, 388621392, 395544792, 406220440, 413787344, 420457047, 428732035, 439774744, 447341712, 454011607, 462286531, 472804372, 480896016, 490048068, 496389649, 506825348, 513166929, 521644569, 529395267, 538332881, 548768452, 555110033, 1076904004, 565544964, 570814146, 579726851, 1073780677, 1075104710, 1074337794, 589065939, 596871256, 1075403779, 605843091, 613919321, 622751446, 1075685319, 630696665, 639528534, 647473817, 656305686, 663980056, 1076230090, 672951891, 680757400, 1077284809, 689860246, 1074686923, 698117651, 1076536264, 1076031438, 1076827085, 1075005388],
    [118, 104, 3, 116, 93, 2321473, 10605697, 18861248, 27249792, 35638336, 44026880, 52784844, 60937281, 69832397, 77844111, 86339084, 94762127, 103386765, 111529552, 119787023, 128282188, 136705039, 145329677, 153472528, 161730255, 170225292, 178648271, 1073752064, 187272781, 195415696, 203673167, 1076391937, 212202575, 220425409, 229879441, 237358800, 246271699, 254268432, 262368257, 271683086, 279826067, 287823056, 296447168, 305237646, 313380371, 321377424, 329477249, 338931217, 346934867, 354931792, 363555840, 372346446, 380333184, 388093121, 397512398, 405498944, 413258753, 422817489, 430830675, 439447043, 447983185, 455996435, 464613059, 1076931971, 471051924, 481162387, 489778243, 496217620, 506328275, 514944131, 520867544, 529387143, 538160852, 546295321, 557141718, 562810392, 571330055, 580103764, 588238425, 599215826, 604753560, 1076681668, 1075387396, 1075667909, 613273287, 622309077, 632770066, 638307928, 646827591, 655993944, 663735961, 674713170, 1075937287, 681029141, 691490450, 697552585, 706317847, 714067673, 1073861570, 724913686, 1074927558, 731483799, 742083737, 747884041, 756526741, 1075210184, 767249433, 773049993, 781823192, 792022614, 798215753, 806858325, 1076265993, 817581273, 1074198475, 823766040, 834358361, 840543384, 850742934, 857312855, 1077349322, 1074482186, 865701591],
    [106, 92, 13, 105, 82, 2379776, 10653761, 18755585, 27144321, 35532865, 44052544, 52310209, 60829824, 69208780, 77606912, 86266048, 94539905, 102772928, 111424080, 119540364, 128208960, 136482817, 144978640, 153234001, 161763456, 170037441, 178532880, 186788497, 195465356, 201749140, 1073750016, 1075865601, 212087440, 220342993, 229019852, 235688654, 245508625, 254186060, 260469460, 270534732, 279351820, 285897362, 295700492, 305173133, 311185934, 321390800, 330338893, 336228946, 346556560, 355619332, 363893453, 372257302, 380110928, 389059085, 394686996, 405276688, 412250639, 420123283, 430844501, 436900563, 445018708, 456010453, 462582351, 470454867, 481176213, 489837124, 495620627, 1076406213, 506475158, 514721814, 523391684, 529699535, 539896341, 546722519, 554995860, 565195478, 573442262, 1076161796, 582111364, 588419151, 1076698051, 598608022, 605303369, 613831319, 621973519, 632304214, 640550998, 647246473, 655528591, 663384594, 1075409858, 672412169, 680824916, 688673422, 1076989895, 697578185, 705990676, 713839182, 1074645960, 1074402246, 1074942982, 1075223561, 722628751, 731156692, 739660311, 748048983, 755659474, 764571855, 1075758026, 1073939466, 1074231243],
    [110, 96, 7, 109, 86, 2504896, 10777601, 18354369, 26742849, 35131393, 43520129, 52039872, 60428416, 68816960, 78133775, 86275137, 93982720, 103256656, 111688271, 119829633, 128422416, 136722560, 144995521, 153588432, 162419712, 170276928, 1073750017, 178754192, 187585664, 195574415, 201953874, 212751424, 220740303, 229872149, 237385728, 246305984, 255038101, 260444866, 271465172, 279868610, 288592469, 296630868, 305297107, 313758421, 319164930, 330185364, 338588674, 345084566, 355612822, 364017171, 369726162, 378278553, 389167638, 397571667, 406163609, 411832921, 422722134, 431126163, 439980631, 445518343, 456276694, 462574677, 473535127, 479072839, 486937218, 497424977, 506360962, 515478231, 1075868614, 521146952, 530979473, 538072277, 548769881, 554701448, 562434626, 573454868, 581858370, 590975511, 1076924418, 596513415, 606477009, 613971031, 621908054, 630198984, 638325465, 648419857, 655914135, 666210521, 672010951, 680678421, 688493074, 1074840583, 697307656, 705434137, 714634263, 724930585, 1074069512, 1073834948, 731411671, 739348694, 747787413, 1076475849, 755602066, 1077270474, 1075187659, 764514326, 1074682821, 773820952, 1075488716, 1076284355, 782209688, 1074474958, 790598232, 798986968, 1076846541],
    [118, 104, 5, 117, 94, 2517056, 10801216, 18903105, 27291649, 35680385, 44069057, 52744192, 59009680, 69350993, 78017042, 86298816, 92564048, 102905489, 111702611, 119960274, 128610900, 136630400, 142895824, 151286339, 161625809, 170422931, 178680402, 187331284, 195743937, 201615888, 211957265, 220754451, 229012114, 237662740, 246075457, 254691411, 262813205, 271086291, 279605908, 288018433, 296634387, 304756373, 313184385, 321800403, 329922261, 336097815, 347009047, 355354771, 363476565, 369652311, 380563543, 389040338, 397022228, 403206871, 411988504, 1073746885, 422506711, 430983186, 1074820034, 438965332, 445837394, 456149138, 464131284, 470315671, 479097560, 489615511, 498092114, 504394312, 514462868, 1076921284, 521040472, 529855001, 539387904, 546337480, 557201110, 562983576, 571666642, 581331072, 587494083, 599144022, 605221010, 614885568, 621834760, 632698518, 638775314, 647129233, 655651529, 666252822, 672461401, 680683729, 1073800135, 689205769, 699937880, 706015961, 714237969, 725103768, 731435547, 739403857, 750269656, 756347545, 763654659, 775435288, 781767323, 788820611, 798373402, 806933211, 1075910659, 815150682, 1075398606, 823710299, 831550088, 840316570, 1074109448, 1075702726, 848589385, 857093850, 1076508618, 1077307340, 865366665, 1076267981, 1074449417, 1074737099, 1076844495],
    [114, 100, 11, 113, 90, 1962177, 10506241, 18894977, 27283521, 35672257, 44191808, 52580480, 60953168, 69357568, 77459457, 86134976, 92557905, 102896272, 111923281, 120093203, 126112401, 136450768, 145477777, 153647827, 161616400, 169734273, 176706070, 187202131, 193204820, 203288641, 210391704, 221141719, 226759188, 237367488, 243946200, 254311059, 260985561, 268840982, 279310400, 285889048, 296639127, 302273233, 310645460, 321638609, 327832152, 338582039, 344216081, 352989272, 363581457, 369644118, 380656282, 388903622, 396750976, 403198678, 414210650, 420368921, 430846534, 438693888, 445141654, 456012422, 464384725, 470700633, 481178118, 489681490, 1073756100, 1077178374, 498489947, 503722134, 514847378, 523655835, 528887894, 540013074, 1076927427, 1075367879, 548428314, 554586777, 562704408, 573567698, 582375963, 587870360, 598602389, 607148762, 612635284, 623768149, 630870604, 640571991, 647778908, 655765596, 666103897, 672813708, 683039451, 689721884, 697708572, 707654165, 714635997, 723276444, 731263132, 741601433, 748190301, 756830940, 764817628, 775155929, 781865484, 790133277, 797585624, 1074598850, 808710169, 814100694, 823687837, 1074883531, 1076467656, 832197324, 1075167244, 1073883086, 1076250570, 1074175951, 1075766213, 1076038601, 1074491341],
    [118, 104, 9, 117, 94, 1878016, 10293376, 18919616, 27308096, 35696768, 44085248, 50891472, 60764368, 67555921, 76057168, 85930064, 92721809, 100971154, 111096464, 119711890, 126276113, 134525522, 145297537, 153266258, 159830737, 168079890, 178065600, 186820626, 196006547, 201634514, 211759632, 220375250, 227201556, 237572161, 243828880, 254857813, 260616791, 271126721, 279742551, 288281171, 294171159, 304680961, 313296919, 321835731, 327856772, 337448960, 344492048, 355521045, 361411076, 369668823, 379392064, 388794583, 397464277, 403354180, 412919936, 422908610, 430887443, 436777623, 445452888, 455903383, 1073756099, 464573077, 470987397, 479007384, 488417472, 496562710, 504541893, 513323737, 520950488, 530360384, 537580180, 546484805, 555266713, 563417235, 573868185, 582415048, 588952199, 597209625, 605204997, 613748819, 624199705, 1077168133, 632746568, 638235332, 647541337, 655691987, 666142809, 1074301956, 674689544, 681226823, 691343938, 699697369, 708244104, 714781383, 722905281, 733287042, 1074588680, 739963610, 748335623, 756459649, 766841346, 1076697095, 1075404802, 773517850, 780997144, 790014017, 1075938249, 798552726, 806686739, 815179777, 823849562, 832107222, 1073869771, 1077023690, 839570004, 1074943949, 848884310, 1075224518, 1075768268, 856347348, 865792666, 1076561871, 1074227150],
    [94, 80, 7, 93, 70, 2398208, 10489920, 18911425, 27299841, 35688513, 44077185, 52729984, 60821696, 69531218, 77598720, 86284352, 94697106, 102764672, 111975059, 119862994, 128586260, 137140947, 145028626, 153752148, 162306579, 168047317, 179083859, 186947776, 195695252, 202045014, 1073750978, 213162499, 218378773, 227210966, 235311767, 246069399, 254546448, 260765334, 268866135, 279623767, 288502417, 294319638, 302420695, 313178327, 322056785, 327586327, 338343959, 346690260, 355661382, 363641543, 369373845, 380827142, 388807239, 397152912, 1075868612, 403477066, 414381766, 422361735, 428094037, 437031434, 447936134, 455916039, 464261840, 1076931591, 1076687878, 470586058, 481728720, 489829073, 498375363, 506204752, 1077216201, 515283088, 523383313, 1073825733, 1074113484, 530068120, 540318275, 546845208, 557095555, 1076487171, 563926617, 1076235208, 572011224, 582391824, 1074418637, 589092505, 597176920, 607557712, 614389466, 622777882, 629969546, 639555162, 1074959370, 647812825, 656332442, 1075239886, 664589849, 1075515343, 1074749387],
    [114, 100, 10, 113, 90, 2584641, 10547200, 18935872, 27324544, 35713216, 44232705, 52621441, 61126160, 69519376, 77787329, 86470657, 94564417, 103074448, 111458000, 120025281, 128234640, 136628432, 145191041, 151319107, 159969922, 170825426, 178571856, 187519699, 193262211, 204379730, 213305475, 221074067, 226816515, 237934226, 246859843, 254628371, 260371139, 272025795, 279229520, 288452690, 1073747971, 294318743, 305042962, 313968643, 322007058, 327988884, 339396759, 347435541, 353301080, 363893848, 372435473, 380727442, 386593367, 395097620, 406505559, 414011987, 420147927, 428652244, 440060119, 447836370, 453964312, 464557080, 473098961, 481653397, 487518936, 498111704, 506653265, 515207765, 520811031, 529315412, 540723223, 548762325, 554627736, 565220504, 573762193, 1075336136, 582570505, 1074829255, 589084246, 1075102660, 599347849, 1073821638, 605612697, 1077240457, 614250134, 624513097, 630639258, 639415830, 649679049, 655804954, 664581846, 672747674, 681110041, 688452290, 697913946, 706136154, 713617986, 723349713, 731441753, 738783746, 748515345, 1075939330, 1074388938, 756607705, 765292625, 773648911, 781634266, 790188250, 1075709901, 798814799, 1074164684, 1077063627, 806965274, 815592143, 824012945, 1076815822, 832369295, 1076300815, 1074752453],
    [114, 100, 9, 113, 90, 2414784, 10776705, 18927617, 27316417, 35704897, 44093569, 52974160, 61134912, 69775889, 78140112, 86300800, 94941777, 103305744, 111466496, 120107729, 128471696, 137165008, 143184595, 153662097, 162330704, 170160129, 179089987, 187496592, 195326017, 201904787, 212644547, 221050896, 228880577, 237810307, 244109845, 1073746882, 252631762, 263213588, 269013523, 279753219, 1074819075, 286186066, 294572694, 305181190, 311218773, 319740562, 330322644, 336646872, 347124358, 353161877, 361683474, 372265556, 378581139, 389478999, 397431444, 403755672, 414233286, 423033559, 428790294, 437309976, 446083094, 456718485, 462344918, 470864472, 481342022, 1076927494, 487903754, 498530967, 504287830, 512283219, 521187411, 529322709, 1075633093, 540473879, 546591321, 555135190, 1075384263, 565770325, 572019354, 579907795, 590936277, 597185050, 1074613193, 605859928, 613732938, 624490517, 630477337, 638627859, 647287498, 656202331, 664294106, 672575638, 681235164, 689756891, 697586393, 706523160, 714396298, 723178076, 731699867, 739529369, 1074369546, 748466328, 756732444, 765254171, 773345882, 782151708, 1075181515, 790287004, 1077281732, 798929052, 807186648, 815706332, 1073900488, 824094812, 831959126, 1076529102, 1074193356, 1076047823, 1076848589],
    [130, 116, 10, 125, 102, 2427008, 10850432, 18428033, 26816577, 35205121, 43593921, 52793344, 61409804, 69685902, 77924416, 86347968, 94982797, 103125056, 111741644, 120279696, 128256000, 137334849, 145314317, 153684620, 162500801, 168120980, 178991827, 187238988, 196186316, 204165648, 212546195, 220530880, 229740556, 237589197, 246100499, 254775297, 261163663, 271274576, 279654995, 288460876, 294717967, 305082966, 312955598, 321884289, 328018006, 338637462, 344273475, 352670420, 363958412, 369961110, 380580374, 386224660, 395686421, 403777747, 414134998, 420033029, 430395982, 437629589, 445720723, 453325443, 464868055, 471183957, 479529690, 486879747, 498422423, 504050246, 513127125, 521734681, 528822979, 539447822, 545993350, 555192913, 562899158, 1073755139, 571290183, 581521997, 587936454, 597537304, 605096527, 613233159, 621359685, 629494356, 638530186, 647049929, 656257688, 663816911, 671953543, 680080069, 691360343, 697250378, 705769993, 714576593, 722282518, 730411653, 741036752, 747582154, 756519441, 765004377, 1077172229, 772616903, 783634967, 789656137, 798462609, 806685274, 1075354631, 1075627976, 1074077704, 815493137, 823462554, 832418392, 840659025, 848376457, 857584344, 865150995, 1075934148, 1076990985, 874213521, 881537542, 890316883, 1075168194, 1073882114, 1076250630, 1074441222, 899379409, 906965514, 915737114, 1076809738, 924807826, 932776601, 1074991051, 1074751499, 941585106, 949553881, 958362130, 966750802],
    [118, 104, 13, 115, 92, 2061312, 10661889, 19216449, 26808384, 35196928, 43585664, 51974336, 60781632, 69679692, 77770881, 85922317, 94713857, 102936769, 111506445, 119476941, 128127695, 136647376, 145177228, 153793166, 161838285, 169808525, 178459215, 186978832, 195508940, 204124878, 212169869, 220140109, 228790927, 236942528, 245708929, 254456398, 262476432, 270874817, 279622158, 287667277, 296424084, 304051328, 311244948, 321040449, 329978580, 337842703, 346362448, 355300559, 361576660, 369660045, 380310100, 388985872, 395130964, 403214349, 413864468, 422540368, 428685332, 436768845, 445559512, 455963791, 463944204, 470356675, 481260688, 487502424, 498014866, 504279704, 514683919, 523180562, 531592400, 537834008, 548346578, 556627023, 562991767, 573512274, 580081366, 588847827, 596152525, 604574275, 613635606, 622533273, 630100567, 1073744834, 638801494, 647698969, 655266519, 663967382, 672733715, 680432151, 689377866, 697899667, 706384597, 713626243, 723196633, 731550229, 1074287556, 1074834436, 738791939, 748098250, 1076680646, 1075128326, 756619859, 765104789, 1076448259, 773624337, 781916761, 790041098, 798963919, 807047765, 1074634697, 1075703817, 1077027784, 815207050, 823956049, 832518159, 1075987397, 1073906698, 840733393, 849295439, 1074191307, 1075521479, 1076327435, 857510545, 866072719],
    [130, 116, 11, 129, 106, 2478080, 10569729, 18968705, 27357377, 35745793, 44134465, 52654080, 61042752, 69431488, 77678721, 86626960, 94597248, 103355922, 109408274, 119621697, 128570064, 136910418, 142962770, 153176257, 162124368, 168391315, 176624787, 187290128, 193688212, 204019410, 210071762, 220581952, 227232405, 235615380, 245747904, 255027799, 260796948, 269169684, 279302272, 288582295, 294613634, 302855298, 310735506, 322032209, 330525207, 338236562, 347198097, 355691223, 361460436, 369833172, 378630853, 389141009, 395528854, 406525638, 412185157, 422695633, 429083350, 436826835, 448468550, 456512152, 462385858, 471026198, 482022918, 490066648, 1073754374, 495940098, 504580694, 515576966, 521368089, 529625733, 540398168, 545878611, 554387989, 563287641, 571699289, 579957253, 590729752, 1076904900, 1073776645, 596331093, 605230105, 613642969, 1074317251, 622187226, 630396569, 638808217, 647352986, 656108059, 663319059, 1074078663, 672339161, 681013834, 689558044, 698051163, 705393236, 714544261, 722956938, 731501212, 739994331, 747598402, 756487365, 764899850, 1075927042, 773444188, 782060125, 788993107, 798454474, 806736474, 815491739, 1075418056, 1074912266, 823751371, 830936275, 839600853, 848941788, 857305739, 864892098, 873845274, 882723485, 890057730, 899500765, 907637323, 915870725, 924666397, 1075713997, 932803083, 940389442, 1075203083, 948646996, 1074702286, 957813829, 1076295628, 965153811, 1077357513, 1076588495],
    [102, 88, 9, 101, 78, 358593, 10571841, 18960513, 27348993, 35737793, 44257344, 52645888, 60633744, 69423232, 76249152, 86200512, 92590738, 102576848, 111639249, 119993044, 127742544, 136805009, 145281557, 152908304, 161970769, 170324628, 178860691, 187136529, 196039254, 204001941, 212415187, 218855552, 229593750, 237433364, 245969491, 252409856, 263148054, 271110741, 279523859, 285964480, 296702678, 302469847, 313585878, 319378008, 327618648, 335902721, 344936985, 1073755074, 354996949, 361320984, 369570007, 377845825, 389083286, 394990106, 403011713, 411521559, 422637590, 428954331, 436671128, 445206680, 453988953, 464580694, 470897243, 478613528, 487019159, 497480276, 503927512, 512168152, 521097881, 528962135, 540340377, 545730647, 557117465, 562762330, 1076913094, 571429593, 1075872712, 582283353, 587928282, 599060697, 605114907, 613094042, 1073802185, 621073106, 629616791, 1076431812, 637850194, 647058075, 654782487, 1074356165, 663015954, 672608475, 1075680199, 681366172, 689385563, 1074911179, 698143452, 706162715, 714920476, 722940059, 731697756, 1075185612, 1074158541, 1075492814, 1077342147, 1076826063, 1074751434],
    [122, 108, 0, 121, 98, 1970304, 10735681, 18985088, 27373760, 35762240, 44150784, 52670657, 61059137, 69708432, 77836289, 86380688, 94621825, 103002241, 111651536, 119787713, 128455313, 137079313, 145601107, 153490000, 161730561, 170896086, 179155475, 184939026, 195564241, 204310547, 212710099, 218493650, 228987088, 238004758, 246264467, 254153232, 262664272, 271419539, 277459524, 285602450, 295571648, 305113686, 310768210, 321392657, 1073753027, 330139859, 337514496, 346550480, 355305555, 362680384, 371716112, 380611222, 388493456, 396890705, 1076388802, 405252176, 412201608, 420205144, 428749335, 439068753, 445231812, 453915223, 462541463, 472623249, 479211608, 487314072, 496611978, 506177745, 512766104, 520868568, 1075873735, 530166346, 539469840, 546426967, 554578071, 563720906, 571968084, 579875032, 588369943, 597275146, 605522452, 613298903, 621924567, 1074060233, 1075383306, 630688468, 638595608, 646696984, 656124572, 663859784, 672395925, 681194139, 689809945, 697692762, 706359835, 714975897, 722055684, 731123794, 739635866, 1074620358, 748399196, 756281877, 765080155, 1076204491, 1074911181, 773696217, 1075196878, 781300424, 789844178, 798356186, 1077047237, 806849172, 814330500, 823390805, 831787154, 1076791300, 840674012, 848409096, 857076250, 865743579, 1074460620, 1077353480, 874359385, 882111189, 890507282, 899394076, 1075790799],
    [102, 88, 2, 101, 78, 366721, 10351809, 18976896, 27365568, 35754048, 44142592, 52662337, 61051073, 69439617, 77854352, 84252673, 94605313, 102873616, 111014977, 119747092, 128815827, 134582292, 144963152, 153204880, 161952469, 170758739, 176656597, 186759248, 195294928, 203895381, 212701715, 218599509, 228455425, 235247681, 245838485, 254644883, 260542613, 270908035, 279180304, 285545174, 294097429, 304199888, 312341633, 321720919, 327520980, 338016771, 346551507, 355275415, 361075284, 371571395, 380105747, 1073754243, 388829719, 394629780, 405271699, 411408577, 422384343, 428839640, 438679619, 447214675, 456340101, 462393880, 472627416, 481031319, 489894405, 495948376, 506181720, 514585687, 1076914821, 523448389, 529764874, 537891480, 548124824, 556528855, 565391557, 571708042, 581679128, 590083095, 598159381, 605262410, 613915281, 622196370, 631451732, 638816970, 647469649, 655750674, 1076400138, 665006228, 672635601, 680916690, 690172116, 697801233, 706082386, 1074841548, 713364118, 721752598, 730141270, 1074081734, 1076716482, 1075947470, 1076216772, 1073876937, 1074689991, 1077319624, 1075239885, 1075519439, 1075792843],
    [118, 104, 13, 117, 94, 2213888, 10088576, 18477248, 26865664, 35254336, 43774081, 52162561, 61191887, 68939841, 77711552, 85717185, 92688977, 102757072, 111523407, 119916625, 128741906, 137074324, 145083025, 154169492, 162240212, 170248913, 179335380, 1073754112, 187405908, 195414545, 204501524, 212571156, 220317824, 229666900, 236974672, 245741071, 253872192, 262959698, 270907023, 279571093, 288125650, 297113234, 305514704, 313290898, 320860688, 330667026, 339068944, 345002582, 355833042, 363457045, 370168534, 379581072, 389387346, 397789328, 403067089, 414430739, 422177493, 428888598, 436728389, 447985363, 455731797, 462025414, 470962907, 478933640, 489928339, 1076913092, 498452560, 504517147, 512225925, 523482707, 532400665, 538473048, 545780421, 555333336, 565955225, 572027544, 579596872, 588887128, 599509593, 604631622, 612782097, 621539848, 630830616, 641452761, 1075876809, 646574726, 654725265, 663483080, 672773272, 1074841538, 1074075656, 680129030, 689467416, 696775173, 706590295, 1075399686, 1074633733, 714101398, 723367575, 731009627, 740275866, 1075692487, 748187864, 757053018, 1073878987, 1075210188, 764564123, 773830362, 781709901, 1076277194, 790516380, 798865111, 1076816835, 806875789, 815682268, 824030743, 832041485, 840847964, 849327642, 857207501, 866013724, 1076561933, 1074493390],
    [122, 108, 13, 121, 98, 2453632, 10858497, 18872385, 27250880, 35639296, 44028032, 52416576, 61321932, 69824716, 77592705, 86495950, 94876236, 103379596, 111147009, 120050190, 128430604, 136933452, 144701633, 153710604, 161984652, 170392144, 1073752064, 1076391937, 178614464, 187675213, 195557904, 201708049, 212325006, 220557376, 229618317, 237501072, 245879374, 254111744, 263172621, 271055568, 279958099, 285954770, 296727245, 302774996, 311120466, 321780418, 329625793, 338557506, 347566286, 354791489, 361353941, 1076922690, 1074318338, 372232915, 381120590, 388345985, 395049492, 403296789, 414175763, 420720657, 428561042, 436992596, 445239893, 456118931, 462115346, 472774786, 478794389, 488092374, 495964374, 507080725, 512490132, 520475217, 529772625, 538169943, 549023893, 556660738, 562418385, 572239959, 580113047, 590608403, 599224334, 605794455, 613667351, 624521301, 632551571, 638824657, 647483928, 655610583, 666106067, 674721934, 679858833, 689680599, 697291414, 708407509, 716437587, 723497624, 731369624, 739234390, 748411407, 756527254, 765284953, 773313112, 781965903, 1074598853, 790081622, 797954582, 1074874308, 807131791, 1074108355, 815772376, 824005273, 832032984, 840686287, 849326104, 857559769, 865317009, 874336793, 882618391, 891269208, 899133462, 1075174346, 1075452938, 1075734472, 1076274121, 1076020171, 1073950663, 1076852678],
    [122, 108, 11, 121, 98, 2397248, 10628161, 18756672, 27145216, 35534016, 43922560, 52713100, 60959745, 69768332, 75773518, 86660685, 94514305, 103323212, 109327886, 120215245, 128068801, 136877772, 145381005, 153654796, 1073750016, 161615375, 1075865601, 170546701, 178558144, 186781391, 195318860, 203723904, 211947151, 218510865, 228873420, 237278208, 243674834, 252065425, 262427660, 269128705, 277231185, 285758478, 294294657, 302265998, 311326416, 319460417, 327693972, 336221201, 344626369, 354553423, 1076409282, 361379415, 369906775, 378574547, 388763157, 394933783, 403600976, 412128787, 422317653, 428095182, 437155472, 445953624, 455872213, 462042775, 470709776, 479507992, 489426581, 495597271, 504124439, 513062552, 520498770, 529020628, 537278161, 545805518, 554735251, 562441874, 570963540, 579614340, 589059156, 596948696, 604384786, 613168644, 622613716, 630757017, 639119062, 646460948, 655111876, 664556564, 672699929, 681061974, 688928453, 697054788, 705189006, 714643033, 723004950, 731133639, 1076942852, 738874449, 748197593, 756559510, 764425797, 773338697, 780948631, 789616211, 797980293, 806893193, 814371985, 823145989, 832058889, 1075387397, 839537873, 848574023, 857224905, 865883284, 873739783, 1075660809, 881611991, 890517127, 1074369480, 1074910216, 1075186695, 898126926, 1074689995, 1077323718, 1076282314, 1073939466, 1074229187],
    [102, 88, 11, 101, 78, 1578113, 9966593, 18355265, 26744001, 35263552, 43652224, 52843087, 60429312, 68818112, 78008975, 86488656, 93985872, 103174671, 111654608, 119151824, 128340687, 1073750017, 136820368, 144317584, 154300624, 161486355, 170374672, 177871888, 187584531, 195040851, 204094993, 212211284, 221139027, 229873173, 235148309, 245372627, 254426833, 262543060, 271470803, 280204949, 285480085, 296369745, 305295376, 314021527, 319035093, 329258643, 338312849, 346428948, 355356819, 364090581, 369366613, 380386516, 388765273, 397570128, 406426713, 413940756, 422998614, 431462103, 439106644, 448164502, 456627735, 464679056, 473405015, 481050260, 489034900, 498496022, 506696789, 1075858370, 514596571, 522983129, 532050646, 540644569, 548150875, 556537369, 565736018, 574198809, 1074302917, 581705371, 590091929, 599290386, 607753369, 1074584515, 615259675, 624456338, 630822492, 641233618, 647861848, 1075388356, 656175770, 664639192, 672952858, 681154076, 1075663814, 689730266, 697931484, 706507354, 714970648, 723359384, 1074894792, 1075181511, 731485852, 1077294027, 1077035980, 1073915849, 1076283338, 1074211789, 1076588494],
    [98, 84, 0, 97, 74, 281728, 8705025, 18616385, 27292865, 35812416, 44201152, 52589696, 60847105, 69235841, 77755392, 84167872, 94638608, 101119632, 111178817, 117722112, 127668417, 134674128, 142888000, 151451216, 161747152, 168351317, 176451153, 186912912, 195718742, 201905877, 211554305, 220884502, 227071637, 236720257, 246050518, 252237333, 262410320, 271216278, 277360661, 285668368, 296801811, 305425943, 311177938, 321967763, 330591959, 336343698, 347133523, 355757719, 361246805, 372299475, 380923479, 386675218, 394948308, 403452498, 411358273, 422449753, 428502548, 436524161, 1073755074, 447615705, 453275281, 461690049, 471103112, 481169945, 487912448, 495611476, 504657416, 514724505, 521598552, 530082832, 538211912, 545796245, 555021376, 563637392, 571930328, 579350741, 588803280, 596932296, 605353088, 613052052, 1076907016, 622130368, 630746192, 1074564042, 639382170, 647427736, 654601745, 1074322375, 664547866, 672593432, 679767761, 689713754, 1075389379, 698102490, 1075931083, 1076210633, 1076490188, 1076764621, 1075729349, 1074960334, 1075234758, 1074214863, 1077363652],
    [110, 96, 13, 109, 86, 2094144, 10386497, 18896001, 27284481, 35673281, 44061761, 52581504, 60969984, 69358656, 77608529, 86111952, 94272705, 102913216, 111163089, 119666256, 127827073, 136861203, 144717457, 153220752, 161381377, 170677844, 178271761, 187333696, 195163664, 204232212, 212350530, 220888064, 228586624, 1073744706, 237786836, 245904578, 254442624, 262141120, 1074293699, 271341204, 279852163, 287306752, 296385728, 304633427, 313013250, 321639572, 330202257, 338187923, 347223634, 355194068, 363756625, 1076403140, 372126915, 380533969, 388625427, 397292547, 405699601, 413791379, 422074067, 430847043, 439080020, 447110741, 1075377093, 455619714, 464245780, 472276693, 479090184, 489830098, 497442453, 506066131, 512644808, 523384338, 530996757, 540005910, 546592457, 556938898, 564786259, 571758217, 582096004, 590337686, 1076963271, 596923913, 607261700, 615503446, 622482955, 630085192, 640816196, 649058006, 656037451, 664032841, 674370756, 681047767, 1076195270, 1076723721, 689591947, 697194120, 1073858506, 705828440, 714602007, 1074139144, 722605720, 731379351, 739382808, 748156503, 756160216, 1074947020, 765081177, 773478091, 781858521, 1076007947, 790247065, 798635545, 1075236814, 1074733005, 1075804111],
    [110, 96, 2, 109, 86, 298176, 8729601, 18920512, 27309056, 35697856, 44086400, 52876880, 59018304, 67449985, 75806290, 86431376, 92572672, 103487121, 109491860, 117888148, 126127232, 137041489, 143046228, 151442516, 162442305, 170596049, 176600788, 184997076, 195996801, 204543555, 210155028, 218551316, 229674711, 238097923, 243840516, 251967186, 262592208, 271617623, 277165249, 285521554, 296146448, 305172119, 313595587, 1073750978, 319075858, 330224770, 338603201, 347149955, 1075865603, 353285637, 363779074, 372280855, 381097024, 386840197, 397333570, 405711873, 413865489, 420394565, 430888130, 439791192, 448205952, 453949125, 462739029, 473476627, 481900182, 1076402181, 488035410, 498642643, 507065878, 513070741, 523677208, 532231766, 538236629, 548843224, 557397718, 563532818, 574139987, 579155009, 588698834, 599174808, 607589568, 1075371974, 614266393, 624366592, 632860307, 1075648455, 639432281, 647828503, 656321553, 664598233, 672994519, 681487569, 688436868, 1075146698, 697750674, 706548823, 715041873, 721991236, 731707033, 740103319, 748596369, 755545796, 764728853, 1076726788, 1074656201, 1077023692, 1074938824, 1073919947, 773764623, 782153295, 1077331918, 1074210765, 790542031, 798930575, 1076316175],
    [114, 100, 0, 113, 90, 2281601, 10523712, 18912256, 27300992, 35689664, 44209281, 52597761, 60986433, 69390529, 77763777, 84186833, 94818513, 102931986, 111023122, 117741201, 128372881, 137008659, 144875218, 152966354, 159684113, 170315793, 178951891, 186818194, 194909330, 203608065, 212506259, 220917779, 229283411, 235181649, 245813329, 1073748931, 254817813, 262708245, 271249491, 279983765, 287874197, 296415379, 304651861, 312350290, 321048641, 1075334082, 330315477, 338205909, 344757894, 353554966, 363869269, 371366994, 378720854, 386274438, 395099863, 403478022, 412275350, 422745689, 431240281, 437042839, 445421254, 455798995, 1074303943, 464688857, 473183449, 479384278, 489854617, 498349209, 506778256, 515020313, 523514905, 529710669, 537695814, 548721168, 1074844678, 554997466, 562435270, 571915482, 582275664, 588551770, 1075127237, 596383241, 605469786, 616100564, 622106138, 630339272, 639024154, 649654868, 1075924873, 655660698, 1074639818, 663893512, 672578714, 683209236, 1077009800, 689058888, 697482893, 708375188, 1075720142, 713823433, 722255447, 733270736, 738989129, 747814605, 757002776, 763761734, 772980237, 1076774852, 782168792, 1074177037, 789722248, 797752855, 807334488, 814486665, 824111768, 1076292556, 1076574155, 830870534, 1077363663],
    [110, 96, 8, 109, 86, 349376, 10284225, 18936832, 27325504, 35714176, 44102848, 52867728, 59339841, 69004417, 75822594, 86422224, 94459473, 103345233, 111587856, 119625425, 128511185, 136753744, 145288721, 153179793, 162042386, 170708176, 178869891, 185136708, 195859029, 204393540, 212424259, 218691268, 229151442, 237948100, 245978819, 252245636, 262967829, 271502468, 279533059, 1073745923, 285799940, 296260242, 305056772, 312562705, 1074808836, 321688213, 330091600, 338515604, 344782360, 354980434, 363811864, 371780753, 378336920, 388797141, 397366424, 405589136, 411891288, 420786774, 430920792, 439143440, 445445848, 454341142, 464475352, 471657537, 478475842, 487895766, 497899092, 505211905, 515176089, 523538585, 528807554, 540331603, 548230868, 1074307017, 557119065, 565481561, 570750658, 582274579, 590173716, 1075632130, 599062041, 607424537, 1075386311, 613897875, 624217235, 632616665, 640979161, 1075136456, 647451731, 657772243, 664179351, 672617491, 680979477, 689345239, 696603776, 706145429, 714510935, 722949331, 731311317, 739676695, 746935360, 756477013, 764719766, 1074106316, 772371649, 1074643915, 780760065, 1073885125, 1076786125, 788878336, 1077061578, 797537409, 1076295622, 1077357519, 1076585422],
    [118, 104, 3, 117, 94, 2151552, 10540032, 18928704, 27317440, 35836929, 44225601, 52860432, 61135888, 69628944, 77780161, 86168705, 94926417, 103192272, 111467728, 120116867, 128480785, 136633936, 145527939, 153802387, 162035409, 170300496, 178577040, 187225795, 195745363, 201916049, 212366481, 221025859, 229168195, 237688339, 243858449, 254178384, 262575248, 271242963, 277413073, 287732880, 296522947, 305051282, 311229973, 321680595, 330217170, 336133201, 346846355, 354997763, 361561813, 371619024, 380408835, 1073742788, 1073764355, 386848471, 395359447, 403504789, 413955091, 420533912, 429053511, 437433496, 447894599, 453836373, 462345815, 1075356613, 470996679, 479245399, 489837767, 496031320, 504550919, 512930904, 523392007, 529849945, 537843351, 546494087, 556946567, 563786841, 1075900358, 1076696071, 571792921, 579917336, 588428312, 598504531, 605347545, 613340695, 621851671, 630617622, 638779034, 647026392, 655537368, 664172118, 1075139522, 672456345, 680572055, 689338006, 1074899912, 697499226, 706270860, 716461196, 723170457, 731053786, 739825164, 750015500, 758036050, 1076491209, 764608026, 773379660, 783569996, 790279385, 798545612, 808735948, 815445017, 1077019660, 1074154442, 825144850, 831944406, 840865300, 1074438094, 1075767243, 849253972, 857642708, 1076312013, 866031252, 1077366735],
    [130, 116, 13, 129, 106, 2462720, 10564800, 18953280, 27341824, 35730560, 44250177, 52638721, 60913360, 69416129, 77960256, 86193281, 92606034, 103232594, 111244816, 119903424, 126160402, 136786962, 144799376, 153982609, 162084371, 168244756, 176492178, 187118738, 195130960, 201930389, 212702801, 220804691, 226965076, 235212498, 245839058, 252531732, 260650581, 271423185, 279525011, 287903319, 294205141, 302863444, 313366033, 319239892, 330378323, 336688213, 346395776, 355675736, 361854165, 370259137, 380841496, 387019925, 395424769, 405875859, 411915476, 420590721, 428291732, 439561944, 445469844, 454145089, 464727704, 470759003, 479286363, 489796690, 1073747909, 496056029, 506007255, 512308757, 521237525, 531739666, 539571923, 546387549, 556338839, 563033755, 573789919, 580072671, 590460114, 1075078086, 596719133, 606670359, 613627487, 624120927, 632403090, 638662301, 649145555, 655570463, 666063903, 672110300, 681260617, 691088403, 697390235, 706459353, 714814985, 722800158, 731206749, 740013657, 748369545, 756485786, 764622495, 775115935, 781956761, 1075876807, 790312649, 798559894, 806303451, 815092957, 823105052, 1074846729, 1075646410, 1074617282, 831852254, 839857691, 848647325, 856659548, 865406622, 873551067, 881825436, 890834518, 898978845, 907785753, 916000470, 923882523, 1075413956, 1073859528, 1074408396, 932646426, 1076512717, 1074177998, 941035226, 949423706, 957943318, 966069854, 1076294607, 1077096395, 1076852675],
    [134, 120, 13, 133, 110, 1916097, 10556608, 18945024, 27333760, 35722304, 44241921, 52630721, 61019265, 69287632, 77796417, 84374018, 92607490, 102579201, 111720019, 117928578, 126162050, 136396304, 145274387, 153173648, 162338517, 168334868, 178076801, 187504213, 195606163, 202207958, 210441430, 220282448, 229160659, 237990616, 246748761, 252515544, 261962817, 271365209, 277705366, 288691737, 294327446, 304946834, 313308185, 319255234, 330634969, 336270934, 344265922, 355278546, 363640025, 372208152, 380966553, 386733080, 397221394, 405607957, 413971609, 420311574, 428545046, 439164498, 447551125, 456307798, 464482968, 470619288, 1073749955, 481509073, 489862358, 498037336, 504173656, 515063313, 523416726, 529363030, 540229201, 1075600324, 548582422, 555053724, 563025052, 573783697, 579933706, 590657242, 596857547, 605361355, 613357084, 622017557, 632600154, 638800459, 647304267, 655300188, 1075351496, 663960661, 674543130, 680882268, 689247883, 697243356, 705903765, 714151626, 724874906, 731074699, 739579403, 746919490, 756235477, 1074578443, 1074073602, 763926164, 773280477, 781784285, 790314519, 1074881481, 798037578, 805869140, 815223453, 823727261, 1075943373, 832257751, 839423700, 849301706, 857282141, 865812119, 1075170247, 873535114, 882677467, 890720349, 899225117, 1074407374, 907755095, 1076248586, 916231771, 924274717, 933008923, 941576266, 1073916876, 949786267, 957706268, 966742026, 973566018, 1076555718, 982732811, 1076835269, 991260892, 1000296586, 1077114831],
    [122, 108, 6, 121, 98, 390208, 10056705, 18445505, 26833985, 35222657, 43742336, 52131008, 60519488, 67499200, 77296640, 86053518, 92763842, 102986894, 109442048, 119607886, 126580228, 136541262, 142996608, 153432656, 160265296, 170096142, 176912004, 185063116, 195104782, 204033746, 210597584, 220689618, 227243588, 235394636, 245853841, 254096016, 260928656, 271021650, 277575364, 285726348, 1073754116, 294614534, 304959059, 312815824, 321353234, 327669260, 336557638, 347164308, 355406357, 361494157, 372330068, 380572373, 386659917, 397496020, 405239442, 411825677, 422661652, 430256656, 437089296, 445380301, 453998278, 464342675, 472846933, 479056897, 487552646, 497896979, 506401429, 514029262, 521393743, 1076909062, 530649294, 539840211, 546559503, 554635864, 564621009, 571331777, 579801624, 589786705, 596497473, 1075090375, 604967576, 614952465, 622057167, 630403801, 640240786, 647198409, 655217793, 663687896, 673795154, 680752649, 689165967, 697512473, 707349522, 714438283, 722695753, 731501778, 739455641, 748506775, 756381259, 764638857, 773444690, 1074842633, 1074604041, 781398617, 790449879, 798324235, 806999186, 1076453315, 815615511, 822572674, 832164882, 840781399, 848656075, 1075677195, 1074392075, 857697942, 864515650, 1076758474, 1074159626, 874475222, 1076003784, 1073931272, 882863702, 891252246, 898070018, 1076311042, 1077369797],
    [118, 104, 11, 117, 94, 2317377, 10048576, 18437248, 26825920, 35214336, 43734209, 52122753, 60511233, 67862220, 77288513, 86447630, 92755650, 101416524, 111105744, 120125073, 128390734, 134960708, 143219920, 153048592, 162068049, 170333838, 176914060, 186603152, 195622417, 204420623, 210468364, 220157520, 229430995, 238229138, 243883088, 254596691, 263395026, 268916290, 277437456, 1073745861, 288151059, 296695375, 302603408, 311383624, 321844948, 330503762, 336025090, 346250433, 353326792, 363804367, 372307605, 378633408, 386881160, 398005958, 405730900, 412187648, 422639189, 430380750, 438524929, 1074551238, 1075360774, 447674004, 456078991, 463690881, 472970773, 479540760, 487685184, 1077208007, 495932936, 506394132, 515053074, 521239680, 1075913736, 531691221, 540611654, 548503129, 555038424, 564721361, 573668889, 580449947, 590943238, 598834905, 605615643, 613758552, 622288461, 630781531, 641275014, 649166489, 655947483, 664090264, 671569538, 681008653, 1076188162, 1075161090, 689911382, 699192979, 706305756, 1076479945, 715060762, 723457687, 731471388, 740226778, 748623383, 756637340, 765392538, 773797526, 781803100, 1074136010, 1073897419, 1075752971, 790558298, 798955095, 806049476, 815226509, 824121047, 831215108, 840392397, 849294870, 857683670, 864769668, 1077070787, 1074466820, 1075014660],
    [126, 112, 0, 125, 102, 1840192, 10597568, 18985984, 27374720, 35763264, 44282881, 52671617, 61069008, 69448897, 77337600, 86225985, 92648978, 103143059, 109556883, 119813138, 126203474, 136697427, 143111251, 153367634, 162508372, 168146642, 178640403, 185054227, 195310802, 204451540, 210351765, 219002518, 228972243, 235386067, 245503505, 254774421, 260683477, 269334102, 279172688, 287446673, 296726036, 302626389, 311277270, 321115664, 329389649, 338669204, 344569365, 353220118, 363058832, 370939008, 380866263, 386905303, 394638994, 403297366, 413414546, 422546645, 428848663, 436851862, 447616600, 456100949, 462665370, 470406358, 481170968, 1073753027, 489918103, 495957143, 504608282, 512349206, 521934016, 531860503, 538162906, 546296914, 556668568, 565152789, 571717210, 579851410, 590223064, 1076386757, 598969943, 605008983, 613799002, 1075351490, 622991057, 633056795, 638964890, 646452353, 658222747, 665966278, 671618049, 683388507, 691131910, 696784065, 708554459, 716297862, 721949761, 733851164, 741463622, 747640477, 1074585606, 759017116, 765187157, 773067860, 784183004, 789959706, 797972189, 1075907528, 809348700, 815518933, 823399636, 1074356169, 834375385, 840684693, 848303645, 1075680199, 859541145, 865457370, 873469533, 884706841, 891016213, 898897044, 909872729, 915395602, 924062740, 1074911178, 1075185614, 932173010, 1074164683, 1077065676, 1077342159, 1076832196, 1076315085],
    [114, 100, 9, 113, 90, 2202817, 10604737, 18977984, 27366400, 35755136, 44143680, 52663297, 61052097, 69440641, 77722128, 86088833, 94606401, 102888016, 111254529, 120272594, 128053968, 136420417, 145438290, 153219728, 162241728, 168367699, 179018752, 186765377, 193304197, 201922259, 210212372, 220576788, 229241553, 1073750979, 235476627, 246127744, 254407249, 263534101, 268932820, 279297236, 287428609, 296433170, 302487188, 312851604, 321516049, 1075863492, 1075616710, 329987730, 336303816, 344430164, 354794580, 362926209, 1075366850, 369464837, 381105878, 386635272, 397261829, 405402257, 414529237, 420189832, 430816389, 439865480, 444962501, 456472149, 462132808, 472620096, 481808584, 1074335752, 486905413, 498415253, 506313925, 515362824, 1074873349, 523712086, 531479621, 540528712, 1074106313, 548877974, 1074656199, 556921367, 563453137, 574043670, 580361296, 590991494, 597505561, 605132299, 615641751, 622173265, 631060121, 638817996, 647075467, 657584727, 664116369, 673003097, 680760908, 689018571, 697801936, 708431878, 714946265, 722703884, 730961483, 741470935, 748002321, 1077018635, 755570195, 764647052, 773299216, 783929542, 1073894412, 790076560, 800706630, 807260760, 815649304, 1075228621, 824038040, 832426712, 1076819914, 1077357518, 1076586447],
    [110, 96, 0, 109, 86, 291840, 10603712, 18478273, 26866689, 35255425, 43643969, 52163648, 60552192, 68940928, 75789440, 86101120, 94106816, 103518864, 111266816, 117732416, 128684624, 136432704, 142898368, 151499410, 161868801, 168326735, 176665170, 1073754112, 187034817, 193492495, 201830930, 210237123, 220589121, 227047055, 235385554, 243791427, 254143617, 260601551, 269201939, 277345923, 1076918210, 288388163, 296611409, 302642900, 311145171, 319288835, 330331139, 338554385, 344585748, 1077189635, 353088147, 363885699, 372109009, 378140308, 386642515, 397440195, 405663377, 413897424, 419942037, 428897281, 436860500, 448238212, 453496533, 462451905, 473404100, 479065606, 487748817, 498331158, 1075630276, 1074865093, 506957892, 512882249, 521303185, 531885654, 540512260, 546436617, 554159701, 563246097, 573280784, 579729094, 588280897, 598994582, 604894790, 612879893, 621966417, 1075932104, 631083736, 638711497, 647001217, 657714902, 664637976, 672003718, 681045655, 689599572, 1076467718, 698192536, 705820297, 714600151, 723154068, 1075431433, 731746904, 740062338, 748154455, 756542999, 765097172, 773616834, 782005250, 1074409420, 790393922, 1076776910, 798651412, 1074694090, 1074194379, 1076303821, 1075266503],
    [102, 88, 9, 101, 78, 1922176, 9698369, 18863105, 27251905, 35640449, 44028993, 52253760, 60030081, 69834306, 77419520, 85195777, 95000258, 102979217, 110361793, 118208146, 128407120, 136175308, 1073752064, 145331714, 1076391937, 153573008, 161340940, 1076922626, 1074318338, 170497154, 178738704, 186506828, 196056782, 203904720, 211672716, 221222414, 228808273, 237370496, 244037138, 253974225, 262536192, 271554190, 277599955, 287528465, 296090688, 1074599875, 302757586, 311154195, 321256640, 329077952, 336311890, 344708755, 355563023, 363331277, 372217422, 378263123, 389248083, 396885517, 1075141573, 1075420165, 406557893, 412210837, 1075705796, 422802451, 430440013, 440112261, 445765205, 456226511, 463994509, 473666629, 479319765, 489911507, 498832389, 504485397, 514946639, 521508374, 531496586, 540243091, 546804817, 556662282, 565278351, 573439690, 580621972, 590968021, 597005910, 606993994, 616133653, 1077285830, 1074946058, 622302353, 631101131, 641299605, 1076003784, 647468049, 656266763, 666465365, 672503510, 681432715, 689280662, 698209867, 1073923083, 706188497, 1074212809, 714839572, 723228244, 731616980, 1076848583],
    [114, 100, 1, 113, 90, 2381824, 8689792, 18757824, 27146368, 35534912, 43923456, 52443137, 60831873, 69220545, 77879360, 84580876, 94386241, 103166541, 109328962, 119822464, 126270093, 136720909, 143014595, 153376960, 159824589, 170275021, 176847564, 185252367, 1073750016, 195702799, 1075865601, 202012684, 210418319, 220868751, 227179148, 235584079, 246034511, 252098637, 260733516, 271200975, 1076406212, 277264397, 286160961, 296104077, 302938113, 311081167, 319427280, 327432706, 336492673, 344627404, 352981648, 361118339, 370448388, 378435777, 386536016, 395614276, 403724933, 411701776, 420780228, 428890821, 436484738, 445290636, 454187662, 1076164552, 462445061, 470063296, 479607378, 488151122, 496392785, 504773266, 512915602, 521968211, 529666644, 537279043, 546871442, 554851022, 563221140, 572275273, 1077226629, 579885125, 587503680, 596775444, 604387843, 613833425, 622631635, 1076714439, 630330068, 638991058, 1075415043, 646200002, 655923410, 663910610, 672545298, 1074383874, 1074672582, 681089042, 689076306, 698104329, 706517523, 714234382, 722770052, 731273873, 739643925, 748436169, 755669068, 764566094, 773198549, 781990537, 789994001, 797218816, 1077042185, 806752853, 814905362, 823958163, 831918741, 1075745739, 1074975755, 1075250122, 1073955850],
    [90, 76, 7, 89, 66, 1939520, 9707521, 18356289, 26744833, 35264576, 43522241, 51910785, 60430528, 68818944, 77079247, 85825536, 93984896, 103186129, 110625491, 119380096, 128351761, 135922196, 144545984, 153517649, 161088084, 170105554, 1073750017, 178683537, 186122899, 195533397, 202900051, 212048530, 219045462, 228197012, 237476565, 244342406, 253362900, 262642325, 269359623, 278397459, 287808021, 295853783, 303571471, 312711698, 319822488, 1075868612, 330464408, 337125967, 346266194, 353376984, 364018904, 370417793, 378542616, 389184536, 397261465, 403577479, 412360769, 420485720, 431127640, 439204377, 445915329, 455237207, 464370265, 470686407, 479732367, 488791703, 497924825, 505946768, 512646806, 522724048, 1076934342, 530079436, 539501136, 547511831, 554572359, 564666896, 1077202951, 572022348, 579886278, 1074856899, 588144150, 1073825730, 1074113481, 597188108, 1076488139, 1076239306, 605576844, 1075473420, 613440582, 1076792261, 621698774, 1074450376, 630217734, 1074730958, 1075273677],
    [118, 104, 8, 117, 94, 2291712, 10645568, 18905281, 27293825, 35682369, 44070913, 52588672, 59169488, 67402258, 78270482, 84335120, 94387780, 100956754, 109476563, 117995588, 128602194, 134666896, 144981203, 151288466, 159939268, 168196627, 178933906, 185260561, 195312659, 201620178, 210270724, 218528403, 229265618, 235592273, 245644435, 252213892, 260471379, 270692544, 277535377, 1073743876, 287587411, 294418965, 304246784, 312670272, 320879620, 329447616, 336359632, 346045572, 354613376, 361525840, 371211460, 378305109, 386324560, 395079824, 404888597, 411753169, 420245520, 430054485, 437025429, 445446679, 456413908, 1074295747, 463609557, 470579413, 479263320, 489968148, 497163413, 504396424, 512555735, 523522708, 1076927430, 529415766, 537950920, 546110103, 557077076, 563232474, 572185179, 580284433, 588529305, 596670984, 605739675, 613838993, 622083673, 630258200, 639004881, 1075365829, 647249625, 656044637, 664459803, 1074070466, 1073829834, 672022230, 681210589, 688978648, 697581081, 705722952, 713882199, 723415580, 1075158024, 731004442, 739932878, 748346075, 756445265, 1075696583, 764559002, 773487118, 781253272, 790524572, 798113370, 807041678, 815428125, 823017110, 832207438, 840856284, 1074924558, 848182806, 1074689997, 857633372, 865759901, 1077324745, 1076555723, 1076832207, 1076323276],
    [114, 100, 8, 113, 90, 2119809, 10508481, 19027968, 27416704, 35674113, 44062785, 52304592, 60971072, 69359808, 75782674, 85858832, 92691025, 102777346, 111024784, 119798355, 127943234, 136190544, 144964307, 153371156, 162281553, 170514965, 178274946, 187194053, 193607698, 204200598, 1073744386, 212484293, 220748293, 229374679, 1074283460, 1073785795, 237649925, 244333208, 254302853, 260463249, 269113496, 279697942, 287981701, 296499345, 304634437, 310794961, 319052498, 330029654, 1076418565, 338313285, 346831057, 353131079, 361650778, 371841685, 380788807, 387201690, 395074055, 403593370, 411458065, 422304470, 431120391, 439105553, 445405831, 453925594, 464116437, 473063559, 479475930, 487348935, 495213202, 506714715, 1075384327, 515006663, 521418842, 531880603, 1074885574, 538984642, 546322968, 554326040, 564918935, 571759196, 582509273, 588920924, 596269784, 606861911, 613702172, 624452249, 630863900, 638212696, 648280723, 655645404, 666395225, 671758930, 679762002, 690608725, 697588380, 708338201, 714750108, 723778067, 732185236, 739260504, 749984475, 757350996, 764688922, 772691994, 783538715, 790905556, 797587666, 808188439, 1076991944, 814364818, 823146712, 832190684, 1075169229, 1074145228, 1076260814, 1076793295, 1074716617, 1075787723, 1077371850],
    [106, 92, 11, 105, 82, 325632, 8722496, 17076416, 27310145, 35698689, 44087425, 52476097, 60995712, 69384256, 77772992, 84211904, 94671504, 101128912, 111327232, 117897345, 126294544, 136614480, 142932032, 153391120, 159848592, 170310292, 176617473, 185014352, 195334352, 203864660, 212504660, 218831441, 226949185, 237419028, 243595392, 252385809, 263098967, 270973652, 277551761, 285669569, 296653335, 304779284, 313580054, 319494865, 328276690, 338746006, 346985175, 355111124, 361962072, 372300502, 380688982, 386209984, 397316759, 1073744838, 405442708, 414374418, 420551250, 1074289607, 428152832, 439670928, 447910617, 456317138, 461707392, 473076377, 479402520, 490002448, 498242073, 1075351496, 506648658, 512826002, 523407961, 529602578, 540203154, 545558592, 554900184, 562335872, 573888592, 580721371, 587501568, 599054544, 605747930, 613620376, 622366785, 1074588611, 631175893, 639441563, 647532545, 656341653, 664309953, 672856730, 681480915, 689773083, 698022490, 706646675, 1076434892, 714938971, 723188250, 731418753, 1075143620, 740227669, 748589651, 1075939274, 1074132941, 757004821, 765366803, 1077288911, 1075729349, 1074964425, 1076294603, 1077085122, 1073967054],
    [98, 84, 7, 97, 74, 2138240, 10762432, 18913409, 27302081, 35690561, 44079105, 52598784, 60987584, 69376064, 77871168, 86024384, 94541952, 103430737, 111190016, 119578688, 128202880, 136764930, 143432323, 153368576, 161915472, 170327762, 176986819, 186810563, 195705553, 203882066, 210672133, 220871313, 229015557, 237436562, 244226693, 254425617, 262570117, 271121990, 277912199, 286169669, 295705299, 304251011, 313195655, 319855303, 327981635, 337648275, 346193987, 355138759, 361536003, 371202643, 379748355, 1073741827, 1073768262, 388561926, 395221701, 404757011, 413565125, 1076137989, 421977666, 428907079, 439001812, 447143618, 455516880, 463920770, 470850055, 1074841602, 480673861, 1074332679, 489356359, 497721940, 506133511, 514333271, 1074092996, 522625552, 531562005, 539499159, 548053524, 556727957, 564664855, 572957328, 581500102, 589830871, 598385300, 607059541, 615054470, 623836885, 631701010, 639539919, 1075425227, 647691990, 656317007, 1076754378, 664469078, 673094159, 681246230, 689871503, 1077285903, 698023574, 1075211214, 1076536264, 1076032460, 1077088201, 1074749389],
    [118, 104, 13, 117, 94, 1883136, 10844225, 18937920, 27326464, 35715264, 44103808, 52214912, 61175809, 69532370, 77642962, 86341761, 92729939, 103348931, 111475282, 119848131, 128284865, 136901140, 145291779, 153418386, 161790979, 170490384, 176616147, 187234947, 195361298, 203734147, 212433616, 218559123, 227211781, 237812741, 245987984, 252113427, 260766277, 271367237, 279542352, 288158357, 294320773, 304921733, 313358464, 321450708, 329301138, 338524224, 346616404, 354466898, 361716248, 1073748932, 371782292, 379632658, 386882200, 397605385, 405598741, 413727299, 420436696, 430226499, 1075332034, 1073778691, 439548553, 447541973, 453704389, 462379608, 472693957, 1074841605, 1074344903, 481491529, 489484885, 496811200, 504715985, 515043401, 521337498, 530365504, 539850944, 548589722, 556710983, 565016576, 573763593, 580057626, 590265543, 596990481, 607320777, 615698458, 623819783, 630545041, 1076970505, 640872649, 648985735, 655710801, 1074108363, 666038409, 672332378, 1075171276, 682933785, 691099730, 699584602, 705886938, 1074668488, 716480214, 724654226, 733139162, 740096590, 1075997642, 750042777, 758208530, 765383191, 773651150, 783597273, 791763154, 798937687, 807205518, 817143318, 1076539341, 824103639, 832371214, 842309270, 1076812814, 849269399, 859086422, 867483225, 1075783631, 1076328390],
    [130, 116, 10, 129, 106, 2154625, 10541121, 18929665, 27318465, 35707009, 44226624, 52615168, 61003968, 69263425, 77781120, 84195857, 92592145, 102810114, 111198914, 120224275, 128636947, 134789844, 143186563, 153149441, 162297987, 170580563, 176732692, 186696258, 195721299, 204135059, 210287252, 221043414, 227072515, 237035713, 246183939, 254466771, 263231702, 271374934, 277404227, 288284800, 296515651, 305060439, 313563222, 321706646, 329302658, 1073743874, 338327699, 347117718, 352639569, 363649558, 369679043, 380559360, 1074286595, 388790467, 397335255, 402962513, 411359953, 422502464, 430602451, 439278231, 444905681, 453302929, 464445632, 473331799, 481221143, 486848657, 498262102, 506886295, 514889750, 523427990, 532052183, 537442900, 546757211, 1074836420, 556982294, 1076937669, 565606423, 572054151, 580041241, 588700379, 598925526, 607672917, 613997255, 622377498, 632611344, 641358407, 647551047, 655932058, 664197787, 674554576, 683301063, 689617051, 697752091, 708108880, 716724757, 723048967, 731429594, 741663376, 1073808391, 750279381, 756857368, 764985948, 775445141, 782023320, 789897746, 800741383, 806533785, 815317660, 1074093001, 825907335, 832223451, 840229458, 1075417030, 849246749, 857520728, 865395346, 874412765, 882686680, 890815004, 1074655180, 1076766664, 899578461, 907197017, 915981020, 1076254670, 924744349, 932886555, 940892882, 1075230667, 1077338061, 949533274, 957528793, 1075782607, 966441051, 1076063178],
    [114, 100, 12, 113, 90, 489472, 8886464, 18558977, 27342976, 35731520, 44120064, 52508864, 60502209, 67615312, 76118672, 84646417, 94056577, 101284560, 109812305, 119222337, 126450192, 134978193, 143226960, 153555152, 159873216, 168532689, 178720912, 185038912, 195795524, 203886608, 1073746883, 210188869, 218593408, 229349892, 237441104, 244005396, 252131845, 1074813700, 263262403, 271423508, 277567617, 285686405, 296947904, 304847044, 311121921, 319503060, 328153749, 336018117, 347279488, 355309780, 361453633, 1075349509, 369834644, 380702787, 388733060, 395008193, 403389012, 412039701, 420575827, 431034371, 439195732, 445725334, 453982933, 462641365, 472881302, 481497088, 487668310, 496195733, 506662976, 514693268, 521091669, 530020887, 539990102, 548475011, 554766866, 563575511, 570931408, 1074316226, 579932882, 588741207, 596097168, 605371084, 613487186, 622295703, 629651472, 638663382, 647445133, 655430290, 663967829, 674207958, 1073819592, 680606230, 689388045, 698309336, 707762198, 714422796, 722565779, 730306624, 739588748, 748640920, 755472512, 1076718535, 1076475849, 764885709, 773806616, 780638208, 789920332, 798063123, 1077267468, 806828621, 814840531, 1074661322, 1074158605, 824138328, 1075749835, 831739925, 1076029390, 1076303814, 1075278799],
    [106, 92, 3, 105, 82, 2302144, 10557505, 18946177, 27334849, 35723265, 44243072, 52631552, 61250192, 69408832, 77799552, 86186176, 94338642, 103094929, 111712401, 119742528, 128024147, 136649297, 145266769, 153296896, 159980098, 169836050, 178592273, 187209745, 195887700, 201923074, 211910291, 220535505, 229152977, 235479058, 243866242, 253853395, 261012117, 269025491, 277420738, 287276690, 294566613, 302588050, 1073745922, 312442578, 321435650, 327745683, 338263686, 346601666, 353567319, 363429574, 370063957, 378348118, 388595270, 396933250, 403243091, 1074807747, 413761030, 420395541, 428679702, 1073785862, 438402579, 447264834, 1076681669, 453574675, 462249047, 472823894, 481100500, 487415511, 497990294, 504561879, 512982681, 523155478, 1075388359, 529080530, 538140186, 548322006, 556597780, 563306202, 572955216, 581763732, 588471962, 598121168, 605495449, 613637722, 623286800, 629743698, 1075667908, 638811737, 647936728, 1075940296, 655827033, 663576087, 673102424, 680337622, 689143513, 698268184, 706159129, 713907863, 723434136, 731054103, 1074392009, 739474457, 747446422, 1076496330, 1074165708, 756220055, 1077319627, 764879065, 1075246030, 1077094351, 1076318157],
    [102, 88, 5, 101, 78, 2169856, 10352641, 18970688, 27359424, 35878913, 44267649, 52525056, 60913792, 69433537, 77667392, 85850177, 94599233, 102833344, 111016065, 119610496, 126474896, 137196115, 145178130, 152959169, 162362003, 168377491, 176806416, 187527699, 193543187, 201972432, 212693715, 218709203, 227138128, 238252564, 245841618, 252828241, 263279300, 1073755075, 271007314, 277994129, 288445060, 294615685, 304561810, 311548625, 1076908228, 322138708, 328169989, 336149587, 345102865, 355553348, 361724485, 372317703, 380762112, 389247636, 395279045, 405872263, 414316608, 1074829317, 422662148, 431038151, 439482496, 447967956, 454261448, 464592455, 473036992, 1075375111, 481776149, 487815816, 496335562, 506666186, 515330645, 521370184, 529866455, 540496597, 546535944, 555032215, 1076694024, 565924438, 571832842, 582163466, 1074611142, 590828181, 597391884, 605387402, 615718026, 624644758, 630553162, 640883786, 1073842186, 649810454, 656112268, 666229336, 672472663, 683365078, 689666764, 699783832, 706027031, 714832460, 724949528, 1074387980, 733338328, 1075722178, 1077299149, 1074179022, 1076553679, 1076306891, 1076058057],
    [118, 104, 11, 117, 94, 2048193, 10574017, 18962561, 27351041, 35739713, 44259456, 52648000, 61036736, 69558992, 77813760, 86563331, 92617298, 103110659, 111362641, 117783058, 128645764, 136790148, 142949010, 153811652, 159865555, 170344644, 176503506, 187365892, 193419923, 203898884, 212408852, 220920388, 227104788, 235362899, 245841988, 1073747972, 254752851, 262724291, 269048532, 279271619, 285694483, 295649281, 304683220, 313055811, 319380116, 329603139, 337994256, 346626196, 354998915, 361323092, 371546243, 379798225, 1075333123, 388569172, 395500053, 403528342, 413089921, 1074310085, 422385814, 429054613, 437082710, 446906897, 455940182, 462608981, 472212112, 1076426694, 481245395, 487520919, 497377872, 1077228482, 506673282, 512686807, 522141761, 1076974535, 531839170, 537852503, 547570321, 557004802, 563272405, 573784147, 581769942, 588077270, 596572695, 607469637, 615324182, 621631510, 633010776, 641024005, 649279554, 658176728, 664492633, 1074890697, 674578565, 682571795, 691731096, 698047001, 708001939, 1074128843, 716126355, 725285400, 733298885, 739981337, 748378841, 758333459, 1076233162, 765147353, 775110867, 782179034, 790323392, 798956186, 807099033, 1073895373, 815489024, 823867545, 832266368, 840899162, 849043520, 1075224526, 1075761096, 857676314, 865810521, 1074734031, 1076064204],
    [122, 108, 9, 117, 94, 268353, 8771649, 18462848, 26851328, 35240000, 43628736, 52148353, 60536897, 68925633, 75897548, 84269057, 94091265, 103387726, 109427330, 117971663, 126212225, 136942094, 142981634, 151526031, 161864205, 170496654, 176929285, 185080335, 195549189, 204051150, 210483781, 218634831, 229103685, 235639505, 244038277, 252459666, 262658181, 269324883, 277199426, 285981381, 296212677, 302922256, 1073743877, 1074293765, 311136913, 319805964, 327424001, 336433875, 344971852, 352721548, 1076665286, 361607701, 369900242, 377870529, 1075365831, 1074077703, 386904598, 396745293, 403585680, 411931283, 419805890, 430962690, 436476033, 1075926018, 445627080, 454013654, 463854221, 470694608, 479181320, 487567958, 495729234, 505797325, 512735880, 521255561, 529379989, 537672210, 546298060, 554809929, 562934357, 570824780, 579852428, 588878423, 598735042, 604912208, 613530121, 622432919, 630569611, 640678018, 646322188, 655342152, 663458385, 672512587, 682620994, 688134337, 1075158024, 697143827, 706067147, 714602496, 722737280, 730970825, 739095253, 748009995, 756931092, 764680256, 1075696580, 1074933769, 1077038091, 1074702347, 772510225, 781711488, 789846208, 798593559, 807262932, 815142989, 1076557770, 823759575, 832428628, 840308941, 848278166, 857594516, 865474701, 1077347267, 1073964035, 873986240, 882251789, 890509312, 899151936],
    [110, 96, 13, 107, 84, 622720, 10066112, 18585793, 26843200, 35362945, 43620352, 52140097, 60292748, 68786304, 76251660, 85694465, 93847116, 101548621, 111254030, 118069827, 127400972, 135102989, 143497732, 153557520, 160405520, 169597956, 179143247, 185440836, 195500688, 202348688, 211541060, 221086223, 227383940, 237443664, 244291664, 253484164, 263029455, 270637646, 277682705, 286785228, 296583823, 302881476, 313203346, 320593092, 327909580, 1073745924, 1074818052, 1076659141, 337746574, 346495696, 353343696, 361487438, 369852492, 379689678, 388700690, 395041998, 403538637, 413866706, 420207758, 428843022, 437590675, 445373454, 454132244, 464198226, 470802068, 478773248, 1073800130, 487922195, 495967252, 504070284, 512965270, 521133780, 529506510, 538384981, 546299476, 555065537, 563452489, 571685462, 579961044, 588585683, 596220611, 605126804, 1075912646, 1075671046, 613784265, 622017238, 629774979, 638419597, 647338505, 655825557, 663329283, 1076991943, 1075177479, 672112718, 1076503555, 680991253, 689012820, 697670281, 705903126, 713654336, 1076252616, 1074694090, 1074186249, 722803283, 731226241, 739711701, 747208896, 755833425, 764780545, 772610769, 781557825, 1074469835, 1075541003, 789387921, 797941902],
    [130, 116, 11, 129, 106, 2390016, 9026688, 18479105, 26867841, 35256513, 43644993, 52164800, 60553344, 68941888, 76135616, 84433487, 94107648, 101055042, 109599439, 120036880, 128055875, 134609410, 143153679, 153591376, 161610243, 168163970, 176708239, 187145872, 195164803, 201849362, 1073754112, 212204164, 221010513, 229481604, 237883923, 245866192, 254834819, 263049811, 270924292, 279214272, 288201732, 296604307, 304478916, 313367748, 322205776, 330551957, 338033220, 346922052, 355760272, 1076908036, 363713235, 370014727, 378534472, 386899016, 397703376, 1074825157, 406049301, 411957831, 420477576, 428842120, 438597760, 1074063302, 444988098, 456381013, 462420680, 472668817, 479173832, 1076172802, 487062098, 495833814, 504363528, 512728072, 523270147, 1075398664, 530709187, 540267221, 545897536, 556824771, 1074377731, 563214936, 570948242, 579728084, 587840512, 598767683, 605158104, 612891346, 621802073, 631535680, 638958674, 647101080, 655227591, 663605846, 673995281, 681032903, 1077268425, 689043992, 697170567, 705548950, 715938513, 722844818, 1074660298, 1073896455, 730714646, 739884034, 750024720, 756019865, 764787922, 773609688, 781054548, 789953554, 798775320, 806220436, 815250439, 823941272, 831517401, 840416327, 849107032, 857461338, 866015831, 874101826, 882627226, 891181719, 899267714, 1075746765, 907792922, 916347415, 924433602, 932958938, 941513431, 949468295, 1075241932, 1076046798, 957346329, 965603860, 1076588491],
    [110, 96, 3, 109, 86, 1564673, 10475648, 18864192, 27252928, 35641344, 44161089, 52549825, 60668428, 69326977, 77062337, 86104065, 94853711, 101300750, 110616705, 120019599, 126466638, 135782465, 145185295, 151632526, 161210960, 1073752064, 170351311, 1076391937, 178109004, 186376720, 195779140, 202103379, 210352846, 220192851, 227400404, 237852884, 244046355, 253606540, 262135827, 269343316, 279795796, 285989523, 295549644, 304078995, 311286292, 321738772, 327932627, 338279117, 346022099, 353229460, 363681940, 370399941, 380221965, 387703440, 397105796, 405387917, 413655237, 422271684, 430553677, 436978385, 447437316, 454285829, 462657683, 472375301, 1076925378, 1074848772, 481254102, 487840325, 496212051, 504748568, 514318405, 1076167623, 523197078, 529914456, 538163288, 547087056, 556751446, 563337861, 571709459, 580246168, 589815941, 1073824773, 598694422, 605412056, 613660888, 621920917, 1074109379, 1075436547, 630807065, 638826520, 646693457, 656243415, 663984339, 671859345, 1075720136, 1076778950, 681138841, 689158296, 697418453, 706304729, 714586770, 722190865, 731470425, 739752466, 747749973, 756906583, 764918482, 773683863, 781304341, 790084178, 798849559, 1075230666, 1077339081, 1076038603, 1074482187],
    [106, 92, 2, 102, 79, 2129088, 8666305, 17054785, 25443457, 33831937, 42351680, 50740224, 59128960, 69500425, 75906240, 85474827, 94666313, 101097036, 110902348, 119029323, 128220873, 135806667, 1073747969, 144998025, 1075339264, 153796173, 1075881985, 160972427, 168591050, 178962125, 186914510, 193609283, 202145290, 212516493, 218775043, 227311178, 237682189, 243941059, 252477066, 260718211, 270564416, 279451279, 1076419587, 1075653635, 285908496, 295730304, 302685776, 312507392, 1076711362, 320617996, 327588876, 338189968, 1074631621, 1074910213, 346297998, 354172620, 361406160, 371743760, 379852366, 387726988, 1075184580, 1073890308, 394697868, 405298256, 413669071, 419863756, 430464208, 438834767, 445816340, 454327889, 463738382, 470826631, 479510098, 487882449, 497554959, 504380999, 513326806, 521436689, 529143511, 537935367, 546881110, 555375691, 562960085, 571489991, 580173330, 588545681, 1074177031, 596252247, 605339346, 614095883, 621418135, 630767126, 639261835, 646583831, 655933078, 664427723, 672011861, 680697556, 688789013, 697474708, 705566357, 714251860, 1076294600, 1077097480, 723269203, 731168402, 740046547, 1077365702, 747281552, 756823571, 765212307],
    [94, 80, 9, 92, 69, 1186817, 9575617, 17964161, 26352705, 34872512, 43260992, 52700866, 60038144, 68426880, 78019139, 86255170, 1073746242, 94796483, 1074809155, 103031810, 111779343, 119961603, 126099140, 1074305025, 136586370, 1075372033, 143638096, 154040516, 159653380, 168304273, 178792146, 187276943, 195459203, 201989779, 210247377, 220734994, 229096595, 238188753, 243932755, 254289554, 262650963, 271743121, 277093956, 287835669, 296646724, 304594451, 311041043, 321390293, 330201092, 336576016, 344202884, 353115654, 1075905540, 363341394, 1074091973, 372144260, 380092115, 386538707, 394796561, 405276245, 414349329, 420462224, 428351057, 438830741, 447903825, 456113878, 465074765, 472890902, 481851917, 489668182, 498629325, 504348368, 515406477, 523222678, 529824468, 539598543, 546855566, 556375631, 563763788, 571767380, 1075154888, 580541068, 588929548, 1074654154, 597318348, 604773958, 613964302, 621551302, 630741582, 1076507593, 1077048329, 638328454, 1077325771, 647264788, 1076805638, 655653524, 1073946567, 1075799047, 664296142],
    [110, 96, 10, 109, 86, 283776, 10229953, 17071168, 25459712, 33848512, 42237056, 50756673, 59145409, 69140110, 75922561, 84309134, 94115905, 101088257, 111345231, 117864014, 127670401, 136511119, 143029774, 152836097, 1073747969, 161676815, 168565443, 176584398, 186580046, 193477188, 202011727, 212008655, 218387520, 227031748, 236911630, 243808900, 252343311, 1075335236, 262077646, 268850704, 277362692, 286407174, 294286543, 303070921, 312613065, 319452303, 328236553, 337778697, 344216576, 1074826118, 353435345, 361791113, 371333257, 377771200, 386956873, 396499017, 1074322441, 405724820, 412112530, 420624518, 1075642819, 430890516, 437278226, 445790278, 456056404, 462444114, 470554755, 481222356, 486954576, 1073825738, 496114261, 504430225, 512775890, 520886339, 529989331, 537286288, 546733782, 554440707, 1074115522, 1077015554, 563642060, 572413526, 580320915, 588676182, 596785350, 605967574, 613875283, 621943317, 630750796, 638647889, 646338256, 656047639, 664695831, 672202257, 680663765, 1077292997, 689372691, 697440917, 706248204, 715028183, 723156183, 1076783053, 731414156, 740185622, 748059670, 1076268044, 756971159, 765099159, 773740182, 781614230, 1074717639, 790525527, 798653527, 1076041672, 1075276747],
    [106, 92, 7, 105, 82, 1440769, 10247296, 18635968, 27024384, 35413056, 43932673, 52321345, 60300866, 69098689, 77200450, 85875841, 94398019, 101080784, 109592270, 1073744706, 118881409, 127813199, 1074287427, 134766098, 143146510, 152829457, 161768466, 168320594, 1074829313, 178667156, 186384017, 195322962, 201875154, 212221524, 219938385, 228877522, 235429522, 243809870, 253492945, 262431890, 269246150, 279330324, 286915778, 295585487, 302800390, 310918798, 320470146, 329139855, 336354886, 346439380, 354024450, 362694159, 369909382, 379067394, 388488726, 1075363846, 396387459, 403070544, 412622018, 422043222, 429941763, 436625040, 446176386, 454425665, 462708377, 471884995, 478567952, 489037464, 497540758, 504651481, 514475733, 522591960, 529923265, 1073813448, 538205721, 548029973, 554572953, 564649686, 571760217, 581584469, 588127321, 598473926, 606750357, 613293081, 623639622, 632047191, 638459097, 648805382, 657213079, 665198168, 673971334, 682378775, 690363928, 699399184, 707544791, 714489491, 724565200, 731266579, 741342352, 1075143626, 1075947465, 748043987, 758119504, 764821075, 1076229063, 1077031943, 1077299148, 1074180036, 1076816837, 1076563915, 1074749389],
    [106, 92, 9, 105, 82, 1899648, 10663104, 17087680, 25607297, 33995777, 42253440, 50641920, 59030592, 67550273, 77771904, 84336206, 92716225, 102973072, 111326208, 117890574, 128138832, 134648897, 143056526, 153304592, 1073747969, 159814657, 168222414, 178470608, 186823744, 193519311, 202063377, 211614720, 218535105, 227221202, 236780608, 243700865, 252395153, 260628047, 269136974, 277561041, 285793935, 294302926, 305217044, 310959631, 319723221, 330382996, 337444032, 344888917, 1075336132, 355548756, 361414230, 371907670, 378188814, 389103316, 397204994, 403609237, 412163795, 420134550, 429307479, 439016598, 445718099, 453689046, 464313986, 471250455, 479272595, 487243286, 496025287, 506125334, 512406670, 521215507, 529579655, 539811394, 546215445, 1074824131, 1073799682, 554384977, 563133959, 573365442, 579542674, 588299847, 598400214, 1075906567, 604708434, 613998296, 1074352072, 622499353, 629874194, 639286297, 647552536, 656053913, 664452249, 672718424, 680965847, 689643226, 697884312, 706385497, 714783833, 1074634700, 1075697606, 722908823, 1075185610, 731551449, 739974682, 748338393, 756752026, 765140570, 1074163657, 1076800461, 1076556747, 1077097483, 1077372869],
    [102, 88, 11, 101, 78, 1875137, 10263617, 18652289, 27040769, 35560448, 43949248, 52337728, 60726400, 69772814, 77478926, 86440463, 1073744834, 1074287555, 94938766, 102644878, 111606351, 119283408, 128383631, 136617168, 1074829313, 145524434, 153549519, 162301458, 170409556, 179239507, 185113684, 196147729, 204506709, 212352660, 218668180, 229410450, 237959891, 245906964, 252222484, 263357974, 271514259, 280135254, 288291347, 296238804, 302554324, 313850436, 322078358, 328998544, 337943696, 347142737, 354164304, 363890197, 371498064, 380959364, 387718672, 397444821, 405052432, 1075372612, 414513156, 422348370, 431028945, 439518934, 447806097, 455648974, 463355086, 470851143, 481622212, 489203278, 496909390, 504405639, 1075914693, 513211096, 523273877, 529571527, 540057175, 546866263, 555285081, 563125767, 573611735, 580427467, 1076184071, 588809751, 597228185, 607165463, 1074103240, 613981771, 622364311, 630651544, 640720023, 647536139, 655918295, 664336921, 672702091, 681114329, 689874458, 1073861643, 697760344, 706651802, 714537496, 723429082, 1075196876, 1077048332, 1077321673, 1075761101, 1074736070, 731817562, 1076588490],
    [98, 84, 10, 97, 74, 1932352, 10802369, 17103873, 25492545, 33881217, 42269889, 50789440, 59178176, 67566720, 77429888, 86299649, 92732416, 102595584, 111605391, 120232465, 127991314, 136150208, 145159759, 154049091, 161545938, 1073747969, 170221070, 178714127, 187603459, 195100242, 203775694, 212268751, 220528147, 229546627, 237043346, 245718670, 254071937, 1075335683, 263100611, 269156036, 279273038, 287626305, 296917188, 304700562, 313325072, 321559121, 330005523, 338491024, 346725009, 353041988, 363420882, 372045392, 380803140, 386596484, 396975122, 405599952, 414357636, 420150788, 428930580, 438918226, 1074825220, 447911940, 454226961, 464223827, 472185939, 480942801, 487781521, 497778387, 505740499, 1074316226, 513063509, 521205396, 531332755, 539294867, 546740758, 554759764, 563780247, 571537108, 580295318, 588444753, 596949653, 605222097, 613726741, 1073815495, 622515800, 630627030, 1075664842, 639293080, 647281365, 656070168, 664443479, 672847576, 681220631, 689609431, 1075152843, 1074128838, 1076241356, 697735766, 1075998664, 1076802501, 1077081093, 1077350349, 1074752457],
    [102, 88, 1, 101, 78, 2417664, 10525825, 18668608, 27057280, 35445760, 43834560, 52354241, 60742657, 69369346, 77519937, 86303936, 94411841, 102685825, 109371022, 119701122, 1073746562, 128370371, 136354817, 1074809283, 144866370, 153535491, 161520833, 1074305025, 170032322, 178701443, 187219537, 195853454, 203867203, 212385425, 220225042, 229295759, 237551121, 246072911, 254188672, 262962702, 268753934, 279241792, 287882961, 296517198, 302308430, 313181711, 321297600, 329959119, 338074688, 347111061, 354851840, 363127936, 372276949, 378461895, 1075375044, 388931156, 395363856, 403627591, 413957838, 419749070, 430874132, 437307024, 1076429765, 446717522, 454215318, 462331087, 1073836998, 1076999174, 471883474, 479381206, 487496847, 497049234, 504546902, 512662543, 523271765, 529712662, 537828431, 546233991, 556826133, 563519059, 571524816, 579788295, 588701207, 1077269511, 598907927, 605079120, 613867159, 624073879, 632200916, 639032919, 649239639, 657366676, 664198871, 1075191753, 674405591, 1075734474, 680959507, 1076274120, 689626829, 697736915, 1076031435, 706403917, 1076826060, 714514067, 723181069, 731569805, 1074742285],
    [110, 96, 9, 109, 86, 2430016, 8739968, 17120385, 25509057, 33897537, 42286081, 50805824, 59194560, 67583104, 77927424, 84369102, 92748800, 102612561, 111098961, 119870592, 126312014, 136167121, 144653521, 153425088, 159866382, 169721489, 178207889, 1073747969, 185032334, 196023887, 201956944, 213071428, 218455232, 227122896, 238237188, 244014159, 252288528, 263403204, 269180623, 277454480, 1075336130, 288568964, 294346383, 1074823172, 303939089, 312425489, 319512079, 330241039, 336412358, 347053589, 355286037, 361709206, 369449984, 380572879, 388996757, 397229205, 403652310, 411393088, 422515855, 430939733, 439172181, 445595158, 455957718, 465376257, 472882901, 481115349, 487538262, 497900630, 507319425, 515087896, 521615063, 531455126, 540253848, 546780759, 556620822, 563166920, 573808344, 580335255, 588209811, 596721224, 607362648, 613889559, 622296722, 630275720, 641048281, 646930003, 658314433, 663830024, 672628434, 683480129, 1073800135, 1075906568, 689641172, 697794130, 708156953, 714806932, 722427603, 733322905, 739972692, 748125714, 1074359235, 1076469705, 758488665, 765138452, 772759059, 1075703749, 781008390, 789397126, 797785670, 1076769738, 1077048330, 1077316614, 1074714571, 1075251148, 1074227149],
    [118, 104, 3, 117, 94, 2014209, 10296512, 18684928, 27073600, 35462272, 43981825, 52370625, 60759105, 69123137, 77536385, 86574798, 93157582, 103095502, 1073746882, 111066241, 1074809795, 118032080, 126179536, 136781008, 144620737, 151330449, 160266766, 170468497, 178592782, 1074305025, 187087938, 193273425, 201677328, 212411473, 220666896, 229031106, 237575698, 243605009, 254367762, 262743057, 270999184, 279362690, 285548241, 293951632, 304686289, 312811150, 321305602, 329843854, 336427150, 346496592, 355114703, 363404882, 371808338, 378078224, 388308558, 397057615, 405341198, 411924558, 422223375, 430513810, 438917266, 445187216, 455777935, 464068306, 472471762, 478741584, 487366356, 496065237, 506004558, 512532052, 1075371972, 521230997, 531572310, 537837146, 1075651527, 546396757, 556738198, 563003034, 571562517, 581904086, 588168922, 597260825, 607069718, 613334554, 622287448, 630654547, 638787081, 647274007, 656235227, 664209043, 672341577, 680304148, 689789531, 698156697, 705896073, 1075921864, 714382935, 1073850309, 722950680, 731711065, 739450569, 747937431, 1076220937, 756505240, 764872211, 772578964, 780490832, 790038227, 798269143, 807230107, 815597273, 824007195, 832373785, 1075194829, 840530137, 1076523978, 1077064714, 1077331910, 848779992, 1074212811, 857307289, 865695833, 1076842444],
    [98, 84, 5, 97, 74, 1178752, 10318849, 17136640, 25525312, 33914048, 42302592, 50822337, 59210881, 67599361, 76676288, 85816385, 92765249, 103365201, 109673553, 118619200, 127759489, 135233219, 145052867, 152173568, 160398915, 1073747969, 170218563, 178249422, 187513540, 193953283, 203772931, 211803662, 219119235, 229332498, 237240015, 1075333123, 246109906, 253746830, 263010884, 270881923, 279182991, 288438931, 296441426, 304078414, 313342468, 321125903, 329086145, 1074310404, 338507908, 344555217, 355161746, 363069007, 1076679621, 371800273, 380720661, 388619397, 397490771, 405886549, 413785285, 1074856898, 422656723, 428441105, 439441045, 447470721, 455686161, 461995665, 473265744, 481025025, 489240721, 498431632, 506191041, 514931219, 523327189, 531225605, 540089044, 548763344, 556653698, 565254740, 573430786, 582032020, 590208194, 599094800, 607197716, 615242817, 622672470, 631888965, 1073834953, 639449622, 648928322, 1076463562, 656227030, 664501964, 673004182, 681278988, 1074126792, 1075718087, 689667724, 1076257734, 698056268, 1076005900, 1074721739, 1077097483, 1077368781],
    [106, 92, 3, 105, 82, 353344, 10542208, 19078209, 27089921, 35609600, 43867329, 52255873, 60775552, 69033025, 77552832, 84231682, 94428352, 102964417, 111107136, 1073744770, 117793792, 127982656, 136518785, 1074287555, 143203918, 151340162, 161537024, 1074829313, 170346054, 176758286, 187123334, 193535694, 203900422, 210312846, 220677830, 228793345, 1075371014, 1075643335, 1073835973, 237706245, 243614786, 254483589, 261187090, 269418195, 279649349, 286745601, 294583891, 304815301, 313878037, 321715860, 330645073, 338773704, 346881748, 355810961, 363939336, 372047444, 380976849, 386229376, 397213204, 406142481, 414541397, 420413075, 429211215, 439436872, 1076736964, 1077015556, 445578771, 454376975, 464602760, 1077291016, 472964695, 479288906, 487939672, 496451088, 506816149, 514907799, 521494040, 530136088, 540370645, 548462103, 554786506, 563437272, 571817679, 579954386, 590405335, 596729482, 605633624, 613508690, 622394902, 630546072, 639057552, 647455937, 655949398, 664223312, 671442112, 681115286, 689004042, 697646735, 704988354, 1076515850, 1075226571, 714669782, 722943696, 731341889, 739851480, 748119169, 756628632, 764503698, 1076290505, 1076037581, 1074221004],
    [110, 96, 13, 109, 86, 515200, 8764480, 17153024, 25541760, 33930432, 42449985, 50838529, 59227329, 67755726, 76004481, 85606095, 93044432, 101309966, 110771727, 118210192, 126475854, 136461970, 143375888, 1073747969, 151895571, 160030350, 170016466, 176930384, 185450067, 195165200, 201954836, 211435087, 219004563, 228719696, 237876931, 244989583, 252821142, 262274256, 271685188, 278797462, 286113491, 295828624, 305239748, 311180817, 319929878, 329637589, 338793988, 1075331523, 346177042, 353484502, 363191829, 1073784068, 372348036, 379731538, 387038806, 396746389, 405648387, 413015062, 1076155330, 420338771, 430814275, 438181078, 445504531, 455980163, 463346774, 470670547, 478779028, 489299479, 497409621, 504739480, 1074868167, 514465431, 521141455, 530036249, 539892935, 546307215, 555202201, 564797143, 571472975, 580368089, 590224455, 1076715461, 596638735, 605533785, 615390343, 1075677129, 621665427, 629774036, 640556039, 646438080, 655734488, 1074124742, 665460311, 672906892, 679992320, 689288728, 1075186632, 697056849, 706461388, 713546816, 723490330, 1074424778, 730611409, 740015628, 748656282, 755777169, 765181516, 773822042, 1076530188, 1074717643, 781563480, 790599386, 797546068, 1076048845, 1077113869],
    [122, 108, 10, 121, 98, 2327681, 10329280, 18717760, 27106432, 35494912, 44014785, 52403201, 59234882, 69180481, 77825089, 85957761, 92789250, 1073744642, 102991041, 1074287555, 109566082, 119768065, 126197326, 1074829313, 134871118, 143099588, 153697999, 159751886, 168271568, 178911440, 185304258, 195640847, 201694862, 210214480, 220854352, 227124806, 235642439, 1075372997, 245972559, 252157456, 262797328, 269321287, 277683921, 285712016, 296351888, 303006723, 313212434, 319420558, 330409619, 1075912518, 338640404, 344586446, 355575379, 363544274, 369466894, 378379861, 386529294, 397518355, 403414535, 413875858, 419944642, 428573826, 1075668936, 439041618, 445488661, 456251459, 464627411, 470523527, 481771030, 487694025, 498194627, 503948486, 512990935, 523714198, 529636937, 540137603, 546145415, 554933783, 565132884, 573691907, 579699719, 588488279, 599211734, 605288533, 612861444, 621518535, 1076202884, 632766038, 638426837, 647485641, 1074648071, 655197383, 663985815, 674184852, 680631945, 689559703, 697009218, 707346063, 713924245, 722983049, 730825795, 741293780, 747740681, 756283605, 764380291, 1075183625, 772611601, 781834327, 789021764, 797777553, 807000279, 814712003, 1073902538, 1077064714, 822943313, 831780885, 839615490, 848943127, 856130692, 865589321, 873047046, 1077331917, 882112661, 889824390, 899143689, 1074212812, 1076849611],
    [106, 92, 9, 101, 78, 1866945, 8780864, 17169536, 25558016, 33946816, 42466305, 50854977, 59243649, 68975617, 76020929, 85965378, 94928521, 102742530, 109434507, 1073749762, 118095556, 128482889, 136296642, 142989003, 151649796, 1075599361, 161250369, 169851010, 176543307, 185204292, 1075359744, 1076950016, 195591689, 201709067, 212441806, 218758788, 228457678, 236747905, 1077217284, 1074359300, 246011599, 254384654, 262011918, 271089353, 279565839, 287939150, 295566414, 303193804, 313105038, 321509007, 329120910, 336748044, 344832720, 353525388, 361496133, 370252498, 380229199, 387079756, 395050693, 403806738, 414045715, 421813901, 428605061, 437361298, 447600211, 455368205, 462159365, 470661776, 479196820, 487456326, 497311309, 1076726789, 1074653189, 504216080, 514709139, 521010694, 531258436, 537770576, 546567829, 554565318, 564420301, 571578962, 581818067, 590110410, 596899349, 606887498, 1076496327, 1074159623, 613414420, 623533060, 630707862, 640572945, 647484950, 657087684, 663746260, 672005766, 682253444, 1076007880, 1074975750, 689174101, 699293393, 705951445, 715939338, 722982486, 732847761, 1075250115, 1073964035, 739759830, 749493898, 756020820, 766402129],
    [114, 100, 8, 100, 77, 2333696, 9690113, 18078913, 26467457, 34856001, 42327104, 50715776, 59104256, 69574274, 75881664, 84770377, 92923402, 102227592, 1073744578, 1074285570, 111516866, 1074566083, 1074850819, 118324873, 128181836, 135782088, 144817352, 1076696064, 151879177, 160032394, 169336392, 1075140609, 1075420161, 178371656, 1075701760, 185433801, 195421709, 202890760, 1076506625, 1077048321, 211926024, 220587661, 228703368, 237880836, 245726736, 253877264, 262511618, 1077314436, 270919245, 279412431, 287432272, 296066114, 304473805, 312966735, 320986832, 330021961, 337897164, 346390160, 354540688, 363044032, 371451532, 380075535, 388742153, 396852879, 405005836, 412335825, 421887056, 430818436, 437501521, 447053008, 453633610, 463707264, 472743444, 481150020, 488873024, 1073924037, 496336466, 503965386, 514571465, 523075220, 531481796, 538164881, 546668242, 555337429, 563207879, 573291657, 580222610, 588891733, 596762247, 605273617, 615349844, 622446101, 630316615, 639213198, 648904404, 656000661, 663870983, 672767694, 1074209799, 680885778, 689817111, 697933326, 706313939, 714983127, 723099214, 1076323270, 731479571, 740148887, 748396043, 756645523, 765314647, 773561931, 781934102, 790339211, 798711382, 807116491, 815488726, 823754323, 832265878],
]


def fill_table(table, me, low, high):
    if high - low == 1:
        for place, word in enumerate(STEPS[low]):
            table[place] = jnp.int32(word)
        return
    middle = (low + high) // 2
    lax.cond(
        me < middle,
        lambda: fill_table(table, me, low, middle),
        lambda: fill_table(table, me, middle, high),
    )


def neighbours(col, row):
    x = lax.rem(col, 2) * 2 + lax.rem(row // 2, 2)
    y, z, core = col // 2, row // 4, lax.rem(row, 2)
    found = [(x, y, z, 1 - core)]
    for move in (1, 3):
        for other in range(2):
            found.append((lax.rem(x + move, 4), y, z, other))
            found.append((x, lax.rem(y + move, 4), z, other))
            found.append((x, y, lax.rem(z + move, 4), other))
    return [{"col": y * 2 + x // 2, "row": z * 4 + lax.rem(x, 2) * 2 + core} for x, y, z, core in found]


def split(value):
    high = value.astype(jnp.bfloat16)
    return high, (value - high.astype(jnp.float32)).astype(jnp.bfloat16)


def spread_kernel(
    stored_ref, slots_ref, halves_ref,
    table, tile_even, tile_odd, halves_even, halves_odd, load_sem, store_sem, send_sem, recv_sem,
):
    active, half, block = stored_ref.shape[2:5]
    rows_per = active // CHUNKS
    col, row = lax.axis_index("col"), lax.axis_index("row")
    beside = neighbours(col, row)
    sibling = beside[0]
    tiles = halves_ref.shape[0]

    barrier = pltpu.get_barrier_semaphore()
    for device in beside:
        pl.semaphore_signal(barrier, inc=1, device_id=device, device_id_type=MESH)
    fill_table(table, col * lax.axis_size("row") + row, 0, len(STEPS))
    pl.semaphore_wait(barrier, len(beside))

    def hop(source, slot, chunk, place, device):
        return pltpu.make_async_remote_copy(
            src_ref=source,
            dst_ref=slots_ref.at[slot, pl.ds(chunk * rows_per, rows_per)],
            send_sem=send_sem.at[place],
            recv_sem=recv_sem.at[slot, chunk],
            device_id=device,
            device_id_type=MESH,
        )

    def arrival(slot, chunk):
        piece = slots_ref.at[slot, pl.ds(chunk * rows_per, rows_per)]
        hop(piece, slot, chunk, 0, sibling).wait_recv()

    tile = (tile_even, tile_odd)
    halves = (halves_even, halves_odd)

    def load(source, turn):
        return pltpu.make_async_copy(source, tile[turn], load_sem.at[turn])

    def store(turn, role):
        return pltpu.make_async_copy(halves[turn], halves_ref.at[role], store_sem.at[turn])

    def prepare(turn, order, role):
        load(slots_ref.at[0], turn).wait()

        @pl.when(order >= 2)
        def _():
            store(turn, 0).wait()

        for mirrored in range(2):
            @pl.when((role & 1) == mirrored)
            def _():
                @pl.loop(0, active)
                def _(line):
                    for slot in range(half):
                        value = tile[turn][line, slot]
                        high, low = split(value.T if mirrored else value)
                        halves[turn][line * half + slot, :block] = high
                        halves[turn][line * half + slot, block:] = low

        store(turn, role).start()

    steps = table[0]
    sends = table[1]

    def act(step):
        word = table[5 + step]
        slot = word & 63

        @pl.when((word >> 30) == 0)
        def _():
            chunk = (word >> 6) & 7
            device = {"col": (word >> 10) & 7, "row": (word >> 13) & 15}
            landing = (word >> 17) & 63
            place = (word >> 23) & 127

            @pl.when(((word >> 9) & 1) == 1)
            def _():
                arrival(slot, chunk)

            @pl.when(slot < 2)
            def _():
                piece = stored_ref.at[slot, 0, pl.ds(chunk * rows_per, rows_per)]
                hop(piece, landing, chunk, place, device).start()

            @pl.when(slot >= 2)
            def _():
                piece = slots_ref.at[slot, pl.ds(chunk * rows_per, rows_per)]
                hop(piece, landing, chunk, place, device).start()

        @pl.when((word >> 30) != 0)
        def _():
            order = (word >> 14) & 15
            for chunk in range(CHUNKS):
                @pl.when(((word >> (6 + chunk)) & 1) == 1)
                def _():
                    arrival(slot, chunk)

            for turn in range(2):
                @pl.when((order & 1) == turn)
                def _():
                    @pl.when(slot < 2)
                    def _():
                        load(stored_ref.at[slot, 0], turn).start()

                    @pl.when(slot >= 2)
                    def _():
                        load(slots_ref.at[slot], turn).start()

                    @pl.when(order >= 1)
                    def _():
                        prepare(1 - turn, order - 1, (word >> 18) & 15)

    def sent(place):
        hop(slots_ref.at[0, pl.ds(0, rows_per)], 0, 0, place, sibling).wait_send()

    pl.loop(0, table[3])(act)
    pl.loop(0, table[4])(sent)
    pl.loop(table[3], steps)(act)
    prepare((tiles - 1) % 2, tiles - 1, table[2])
    pl.loop(table[4], sends)(sent)

    for turn in range(2):
        store(turn, 0).wait()


def spread(stored):
    most = max(entry[1] for entry in STEPS)
    active, half, block = stored.shape[2:5]
    return pl.pallas_call(
        spread_kernel,
        out_shape=(
            jax.ShapeDtypeStruct((SLOTS,) + stored.shape[2:], jnp.float32),
            jax.ShapeDtypeStruct((14, active * half, 2 * block, block), jnp.bfloat16),
        ),
        in_specs=[pl.BlockSpec(memory_space=pl.ANY)],
        out_specs=(pl.BlockSpec(memory_space=pl.ANY),) * 2,
        scratch_shapes=[
            pltpu.SMEM((max(len(entry) for entry in STEPS),), jnp.int32),
            pltpu.VMEM((active, half, block, block), jnp.float32),
            pltpu.VMEM((active, half, block, block), jnp.float32),
            pltpu.VMEM((active * half, 2 * block, block), jnp.bfloat16),
            pltpu.VMEM((active * half, 2 * block, block), jnp.bfloat16),
            pltpu.SemaphoreType.DMA((2,)),
            pltpu.SemaphoreType.DMA((2,)),
            pltpu.SemaphoreType.DMA((most,)),
            pltpu.SemaphoreType.DMA((SLOTS, CHUNKS)),
        ],
        compiler_params=pltpu.CompilerParams(
            collective_id=0, has_side_effects=True, vmem_limit_bytes=60 << 20
        ),
        name="spread",
    )(stored)[1]


def multiply_kernel(
    halves_ref, rows_ref, offs_ref, krow_ref, kcol_ref, kcnt_ref, out_ref,
    blocks, done_first, done_second, pairs, pair_count, bucket, bucket_count, facts, in_sem, out_sem,
):
    grid = lax.axis_size("row")
    tile_j = lax.axis_index("row")
    col_id = lax.axis_index("col")
    tiles, each = halves_ref.shape[:2]
    half = offs_ref.shape[1]
    active = each // half
    block = halves_ref.shape[-1]
    lanes, _, kept = krow_ref.shape
    slots = 2 * half
    steps = 2
    most = steps * slots * slots

    def load(place):
        return pltpu.make_async_copy(
            halves_ref.at[place], blocks.at[pl.ds(place * each, each)], in_sem.at[place]
        )

    waves = ([0, 1, 2, 3, 8, 9, 10, 11], [4, 5, 6, 7, 12, 13])
    for wave in waves:
        for place in wave:
            load(place).start()

    first = rows_ref[0, 0]
    bits = [rows_ref[1, 0] ^ first, rows_ref[2, 0] ^ first, rows_ref[4, 0] ^ first]

    def rank(value):
        return sum(
            jnp.where((value & bit) != 0, jnp.int32(1 << place), jnp.int32(0))
            for place, bit in enumerate(bits)
        )

    def shifts(tile_x, tile_y):
        both = ((tile_x, tile_y), (tile_y, tile_x))
        return [rank(offs_ref[x, slot, y]) for x, y in both for slot in range(half)]

    tile_is = [col_id * lanes + lane for lane in range(lanes)]
    tile_ks = [lax.rem(tile_is[0] + tile_j + place, grid) for place in range(3)]
    right_moves = [shifts(tile_k, tile_j) for tile_k in tile_ks]

    for place in range(lanes * active):
        pair_count[place] = 0
    for lane in range(lanes):
        for step in range(steps):
            left_moves = shifts(tile_is[lane], tile_ks[lane + step])
            for slot in range(slots):
                move = left_moves[slot]
                turn = move if slot >= half else 0
                left_base = (2 * (2 * lane + step) + slot // half) * each + slot % half
                for other in range(slots):
                    apart = move ^ right_moves[lane + step][other]
                    place = lane * active + apart
                    count = pair_count[place]
                    right_base = (8 + 2 * (lane + step) + other // half) * each + other % half
                    reach = move if other < half else apart
                    pairs[place * most + count] = (
                        turn | reach << 3 | left_base << 6 | right_base << 14
                    )
                    pair_count[place] = count + 1

    widest = 4
    room = 2 * kept
    for place in range(lanes * (widest + 1)):
        bucket_count[place] = 0
    for place in range(lanes * active):
        pair_count[place] = place << 3 | pair_count[place] << 7

    def put(lane, size, word):
        place = lane * (widest + 1) + size
        filled = bucket_count[place]
        bucket[place * room + filled] = word
        bucket_count[place] = filled + 1

    for lane in range(lanes):
        count = kcnt_ref[0, lane]
        together = 8

        @pl.loop(0, kept // together)
        def _(part):
            found = []
            for offset in range(together):
                item = part * together + offset
                row = rank(krow_ref[lane, 0, item])
                place = lane * active + (row ^ rank(kcol_ref[lane, 0, item]))
                found.append(jnp.where(item < count, pair_count[place] | row, 0))
            for offset in range(together):
                item = lane * kept + part * together + offset
                products = found[offset] >> 7
                facts[item] = found[offset] & 127
                begin = jnp.where(products > 0, ((products - 1) & 7) + 1, 0)
                put(lane, (begin + 1) >> 1, item | begin << 13)

                @pl.loop(0, (products - begin) >> 3)
                def _(more):
                    put(lane, widest, item | (begin + 8 * more) << 7 | 1 << 12 | 8 << 13)

    blocks[tiles * each] = jnp.zeros((2 * block, block), jnp.bfloat16)
    def gather(word, size):
        fact = facts[word & 127]
        row = fact & 7
        base = (fact >> 3) * most + ((word >> 7) & 31)
        products = word >> 13
        ones, twos = [], []
        for place in range(2 * size):
            inside = place < products
            code = pairs[base + jnp.where(inside, place, 0)]
            source = ((code >> 6) & 255) + (row ^ (code & 7)) * half
            ones.append(blocks[jnp.where(inside, source, tiles * each)])
            other = blocks[(code >> 14) + (row ^ ((code >> 3) & 7)) * half]
            twos.append(jnp.concatenate([other[:block], other[block:]], 1))
        total = jnp.dot(
            jnp.concatenate(ones, 1), jnp.concatenate(twos, 0), preferred_element_type=jnp.float32
        )
        total = total[:block] + total[block:]
        return total[:, :block] + total[:, block:]

    done = (done_first, done_second)

    def add(lane, word, into, total):
        again = ((word >> 12) & 1) == 1

        @pl.when(again)
        def _():
            done[lane][into] = done[lane][into] + total

        @pl.when(jnp.logical_not(again))
        def _():
            done[lane][into] = total

    def store(lane):
        return pltpu.make_async_copy(
            done[lane].at[pl.ds(0, kept)], out_ref.at[lane, 0], out_sem.at[lane]
        )

    for lane in range(lanes):
        for place in waves[lane]:
            load(place).wait()
        head = lane * (widest + 1)

        @pl.loop(0, bucket_count[head])
        def _(place):
            done[lane][bucket[head * room + place] & (kept - 1)] = jnp.zeros((block, block), jnp.float32)

        for size in range(1, widest + 1):
            count = bucket_count[head + size]

            @pl.loop(0, (count + 1) >> 1)
            def _(place):
                start = (head + size) * room + 2 * place
                one = bucket[start]
                paired = 2 * place + 1 < count
                two = bucket[jnp.where(paired, start + 1, start)]
                total_one = gather(one, size)
                total_two = gather(two, size)
                into_one = one & (kept - 1)
                into_two = jnp.where(paired, two & (kept - 1), kept)
                if size < widest:
                    done[lane][into_one] = total_one
                    done[lane][into_two] = total_two
                else:
                    add(lane, one, into_one, total_one)
                    add(lane, jnp.where(paired, two, 0), into_two, total_two)

        store(lane).start()

    for lane in range(lanes):
        store(lane).wait()


def multiply(halves, tile_rows, offsets, kept_rows, kept_cols, kept_count):
    block = halves.shape[-1]
    half = offsets.shape[1]
    tiles, each = halves.shape[:2]
    active = each // half
    lanes, _, kept = kept_rows.shape
    items = lanes * kept
    products = 2 * (2 * half) ** 2
    smem = pl.BlockSpec(memory_space=pltpu.SMEM)
    return pl.pallas_call(
        multiply_kernel,
        out_shape=jax.ShapeDtypeStruct((lanes, 1, kept, block, block), jnp.float32),
        in_specs=[pl.BlockSpec(memory_space=pl.ANY)] + [smem] * 5,
        out_specs=pl.BlockSpec(memory_space=pl.ANY),
        scratch_shapes=[
            pltpu.VMEM((tiles * each + 1, 2 * block, block), jnp.bfloat16),
            pltpu.VMEM((kept + 1, block, block), jnp.float32),
            pltpu.VMEM((kept + 1, block, block), jnp.float32),
            pltpu.SMEM((lanes * active * products,), jnp.int32),
            pltpu.SMEM((lanes * active,), jnp.int32),
            pltpu.SMEM((10 * items,), jnp.int32),
            pltpu.SMEM((10,), jnp.int32),
            pltpu.SMEM((items,), jnp.int32),
            pltpu.SemaphoreType.DMA((tiles,)),
            pltpu.SemaphoreType.DMA((lanes,)),
        ],
        compiler_params=pltpu.CompilerParams(vmem_limit_bytes=60 << 20),
        name="multiply",
    )(halves, tile_rows, offsets, kept_rows, kept_cols, kept_count)


def local(stored, tile_rows, offsets, kept_rows, kept_cols, kept_count):
    halves = spread(stored)
    return multiply(
        halves, tile_rows.T, jnp.swapaxes(offsets, 1, 2), kept_rows, kept_cols, kept_count.T
    )


def solution(mesh):
    in_specs = (
        P("col", "row", None, None, None, None),
        P(),
        P(),
        P("col", "row", None),
        P("col", "row", None),
        P("col", "row"),
    )
    out_specs = P("col", "row", None, None, None)
    return jax.shard_map(local, mesh=mesh, in_specs=in_specs, out_specs=out_specs, check_vma=False)
```
